32 devices in a mesh: dp: 16 (over z, x, core), tensor: 2 (over y).
Axes of the slice: x: 2, y: 2, z: 4, core: 2. Of those that a mesh axis runs over, the one named last changes fastest.
Arguments:
- tokens: bfloat16 [16384, 1024], P(('dp', 'tensor')), may hold values from -6 to 6
- query_weight: bfloat16 [1024, 1024], P('dp', 'tensor'), may hold values from -0.25 to 0.25
- query_bias: bfloat16 [1024], P('tensor'), may hold values from -3 to 3
- key_weight: bfloat16 [1024, 1024], P('dp', 'tensor'), may hold values from -0.25 to 0.25
- value_weight: bfloat16 [1024, 1024], P('dp', 'tensor'), may hold values from -0.1875 to 0.1875
- value_bias: bfloat16 [1024], P('tensor'), may hold values from -3 to 3
- out_weight: bfloat16 [1024, 1024], P('tensor', 'dp'), may hold values from -1 to 1
- out_bias: bfloat16 [1024], replicated, may hold values from -2 to 2
- first_gain: bfloat16 [1024], replicated, may hold values from 0.25 to 1.75
- first_shift: bfloat16 [1024], replicated, may hold values from -3 to 3
- up_weight: bfloat16 [1024, 4096], P('dp', 'tensor'), may hold values from -0.1875 to 0.1875
- up_bias: bfloat16 [4096], P('tensor'), may hold values from -3 to 3
- down_weight: bfloat16 [4096, 1024], P('tensor', 'dp'), may hold values from -0.125 to 0.125
- down_bias: bfloat16 [1024], replicated, may hold values from -2 to 2
- second_gain: bfloat16 [1024], replicated, may hold values from 0.25 to 1.75
- second_shift: bfloat16 [1024], replicated, may hold values from -3 to 3
- cotangent: bfloat16 [16384, 1024], P(('dp', 'tensor')), may hold values from -6 to 6
- clip_limit: float32 [16], P('tensor'), may hold values from 4 to 24
Outputs:
- layer_out: bfloat16 [16384, 1024], P(('dp', 'tensor'))
- tokens_grad: bfloat16 [16384, 1024], P(('dp', 'tensor'))
- query_weight_grad: float32 [1024, 1024], P('dp', 'tensor')
- query_bias_grad: float32 [1024], P('tensor')
- key_weight_grad: float32 [1024, 1024], P('dp', 'tensor')
- value_weight_grad: float32 [1024, 1024], P('dp', 'tensor')
- value_bias_grad: float32 [1024], P('tensor')
- out_weight_grad: float32 [1024, 1024], P('tensor', 'dp')
- out_bias_grad: float32 [1024], replicated
- first_gain_grad: float32 [1024], replicated
- first_shift_grad: float32 [1024], replicated
- up_weight_grad: float32 [1024, 4096], P('dp', 'tensor')
- up_bias_grad: float32 [4096], P('tensor')
- down_weight_grad: float32 [4096, 1024], P('tensor', 'dp')
- down_bias_grad: float32 [1024], replicated
- second_gain_grad: float32 [1024], replicated
- second_shift_grad: float32 [1024], replicated
- logit_peak: float32 [16], P('tensor')
- query_clipped: bfloat16 [1024, 1024], P('dp', 'tensor')
- query_bias_clipped: bfloat16 [1024], P('tensor')
- key_clipped: bfloat16 [1024, 1024], P('dp', 'tensor')
The draws below stay inside these ranges and needn't reach their ends.
All inputs are finite; a program needn't handle non-finite values.
Results may differ from the reference program's by a relative error of at most 0.02.
Values may be sent and summed in bfloat16 or wider, within the bound.
A program may use at most 192 MiB of HBM per device.

```python
import jax
import jax.numpy as jnp
from jax import lax

D = 1024
H = 16
HD = 64
FF = 4096
LEN = 1024
TOKENS = 16384


def block_levels(stream_key, shape, cuts, least, largest):
    factor_of, own = 1.0, jax.random.fold_in(stream_key, 6)
    for position, parts in cuts:
        draws = jnp.exp(jax.random.uniform(jax.random.fold_in(own, position), (parts,), jnp.float32, least / len(cuts), largest / len(cuts)))
        factor_of = factor_of * jnp.repeat(draws, shape[position] // parts).reshape([-1 if axis == position else 1 for axis in range(len(shape))])
    return factor_of


def centred(key, dims, width, reach, pieces=(), dtype=jnp.bfloat16):
    drawn = jax.random.normal(key, dims, jnp.float32) * width
    if len(pieces) > 0:
        drawn = block_levels(key, dims, pieces, -0.22, 0.18) * drawn
    return jnp.clip(drawn, min=-reach, max=reach).astype(dtype)


def setup_inputs(seed: int = 0) -> dict:
    streams_of = jax.random.split(jax.random.key(seed), 19)
    tokens = centred(streams_of[0], (TOKENS, D), 1.0, 6.0, ((0, 32),))
    query_weight = centred(streams_of[1], (D, D), (D // 2) ** -0.5, 0.25, ((0, 16), (1, 2)))
    query_bias = centred(streams_of[2], (D,), 0.5, 3.0, ((0, 2),))
    key_weight = centred(streams_of[3], (D, D), (D // 2) ** -0.5, 0.25, ((0, 16), (1, 2)))
    value_weight = centred(streams_of[4], (D, D), D ** -0.5, 0.1875, ((0, 16), (1, 2)))
    value_bias = centred(streams_of[5], (D,), 0.5, 3.0, ((0, 2),))
    out_weight = centred(streams_of[6], (D, D), (D // 32) ** -0.5, 1.0, ((0, 2), (1, 16)))
    out_bias = centred(streams_of[7], (D,), 0.3, 2.0)
    first_gain = jnp.clip(1.0 + 0.15 * jax.random.normal(streams_of[8], (D,), jnp.float32), 0.25, 1.75).astype(jnp.bfloat16)
    first_shift = centred(streams_of[9], (D,), 0.5, 3.0)
    up_weight = centred(streams_of[10], (D, FF), D ** -0.5, 0.1875, ((0, 16), (1, 2)))
    up_bias = centred(streams_of[11], (FF,), 0.5, 3.0, ((0, 2),))
    down_weight = centred(streams_of[12], (FF, D), (FF // 2) ** -0.5, 0.125, ((0, 2), (1, 16)))
    down_bias = centred(streams_of[13], (D,), 0.3, 2.0)
    second_gain = jnp.clip(1.0 + 0.15 * jax.random.normal(streams_of[14], (D,), jnp.float32), 0.25, 1.75).astype(jnp.bfloat16)
    second_shift = centred(streams_of[15], (D,), 0.5, 3.0)
    cotangent = centred(streams_of[16], (TOKENS, D), 1.0, 6.0, ((0, 32),))
    clip_limit = jnp.clip(4.0 + 20.0 * jax.random.uniform(streams_of[17], (H,), jnp.float32) ** block_levels(streams_of[17], (H,), ((0, 2),), -0.2, 0.2), 4.0, 24.0)
    return {"tokens": tokens, "query_weight": query_weight, "query_bias": query_bias, "key_weight": key_weight, "value_weight": value_weight, "value_bias": value_bias, "out_weight": out_weight, "out_bias": out_bias, "first_gain": first_gain, "first_shift": first_shift, "up_weight": up_weight, "up_bias": up_bias, "down_weight": down_weight, "down_bias": down_bias, "second_gain": second_gain, "second_shift": second_shift, "cotangent": cotangent, "clip_limit": clip_limit}


HIGHEST = lax.Precision.HIGHEST
EPSILON = 1e-05

@jax.custom_vjp
def low(v):
    return lax.optimization_barrier(v.astype(jnp.bfloat16)).astype(jnp.float32)

@jax.custom_vjp
def low_back(v):
    return v

def low_keep(v):
    return (low(v), None)

def low_pass(kept, grad):
    return (grad,)

def back_keep(v):
    return (v, None)

def back_low(kept, grad):
    return (low(grad),)
low.defvjp(low_keep, low_pass)
low_back.defvjp(back_keep, back_low)

def product(left, right):
    return jnp.dot(left, right, precision=HIGHEST)

def layer_norm(values, gain, shift):
    center = values - lax.optimization_barrier(jnp.mean(values, axis=-1, keepdims=True))
    spread = lax.optimization_barrier(jnp.mean(center * center, axis=-1, keepdims=True))
    return center * lax.rsqrt(spread + EPSILON) * gain + shift

def forward(inputs, params):
    query_weight, query_bias, key_weight, value_weight, value_bias, out_weight, out_bias, first_gain, first_shift, up_weight, up_bias, down_weight, down_bias, second_gain, second_shift = params
    rows_low = low(inputs)
    queries = low(low_back(product(rows_low, query_weight) + query_bias))
    keyset = low(low_back(product(rows_low, key_weight)))
    valset = low(low_back(product(rows_low, value_weight) + value_bias))
    heads_query = queries.reshape(LEN, H, HD)
    heads_key = keyset.reshape(LEN, H, HD)
    heads_value = valset.reshape(LEN, H, HD)
    logits = jnp.einsum('qhd,khd->hqk', heads_query, heads_key, precision=HIGHEST) * HD ** (-0.5)
    peaks = lax.optimization_barrier(jnp.max(logits, axis=(1, 2)))
    scored = low_back(logits)
    attend_probs = low(jax.nn.softmax(scored, axis=-1))
    context = jnp.einsum('hqk,khd->qhd', attend_probs, heads_value, precision=HIGHEST).reshape(LEN, D)
    context = low(low_back(context))
    attention = low_back(product(context, out_weight) + out_bias)
    hidden = layer_norm(inputs + attention, first_gain, first_shift)
    upper = low_back(product(low(hidden), up_weight) + up_bias)
    acted = low(jax.nn.gelu(upper, approximate=False))
    branch = low_back(product(acted, down_weight) + down_bias)
    return (layer_norm(hidden + branch, second_gain, second_shift), peaks)

def reference(tokens, query_weight, query_bias, key_weight, value_weight, value_bias, out_weight, out_bias, first_gain, first_shift, up_weight, up_bias, down_weight, down_bias, second_gain, second_shift, cotangent, clip_limit):
    params = tuple((member.astype(jnp.float32) for member in (query_weight, query_bias, key_weight, value_weight, value_bias, out_weight, out_bias, first_gain, first_shift, up_weight, up_bias, down_weight, down_bias, second_gain, second_shift)))
    seq_count = tokens.shape[0] // LEN
    rows_all = tokens.astype(jnp.float32).reshape(seq_count, LEN, D)
    upstream = cotangent.astype(jnp.float32).reshape(seq_count, LEN, D)

    def one_sequence(carry, item):
        sums, peak_now = carry
        seq_rows, seq_grad = item
        outputs, pull_back, peaks = jax.vjp(forward, seq_rows, params, has_aux=True)
        input_grad, param_grads = pull_back(seq_grad)
        sums = jax.tree.map(lambda total_now, extra: total_now + extra, sums, param_grads)
        return ((sums, jnp.maximum(peak_now, peaks)), (outputs, input_grad))
    zero_grads = jax.tree.map(jnp.zeros_like, params)
    start_peak = jnp.full((H,), -jnp.inf, jnp.float32)
    (grads, peak), (outputs, input_grads) = lax.scan(one_sequence, (zero_grads, start_peak), (rows_all, upstream))
    layer_out = outputs.reshape(tokens.shape).astype(jnp.bfloat16)
    tokens_grad = input_grads.reshape(tokens.shape).astype(jnp.bfloat16)
    factor = clip_limit / jnp.maximum(peak, clip_limit)
    column_scale = jnp.repeat(jnp.sqrt(factor), HD)
    query_clipped = (params[0] * column_scale).astype(jnp.bfloat16)
    query_bias_clipped = (params[1] * column_scale).astype(jnp.bfloat16)
    key_clipped = (params[2] * column_scale).astype(jnp.bfloat16)
    return (layer_out, tokens_grad, grads[0], grads[1], grads[2], grads[3], grads[4], grads[5], grads[6], grads[7], grads[8], grads[9], grads[10], grads[11], grads[12], grads[13], grads[14], peak, query_clipped, query_bias_clipped, key_clipped)
```

```python
import functools
import math

import jax
import jax.numpy as jnp
from jax import lax
from jax.experimental import pallas as pl
from jax.experimental.pallas import tpu as pltpu
from jax.sharding import PartitionSpec as P

HD = 64
LEN = 1024
QB = 512


EPSILON = 1e-05


def layer_norm(values, gain, shift):
    center = values - jnp.mean(values, axis=-1, keepdims=True)
    spread = jnp.mean(center * center, axis=-1, keepdims=True)
    return center * lax.rsqrt(spread + EPSILON) * gain + shift


def gelu_slope(upper):
    normal_cdf = 0.5 * (1.0 + lax.erf(upper * 0.5**0.5))
    return normal_cdf + upper * jnp.exp(-0.5 * upper * upper) * (0.5 / math.pi) ** 0.5


def contract_rows(left, right):
    return lax.dot_general(
        left, right, (((0,), (0,)), ((), ())), preferred_element_type=jnp.float32
    )


def contract_cols(left, right):
    return lax.dot_general(
        left, right, (((1,), (1,)), ((), ())), preferred_element_type=jnp.float32
    )


def per_device(
    tokens,
    query_weight,
    query_bias,
    key_weight,
    value_weight,
    value_bias,
    out_weight,
    out_bias,
    first_gain,
    first_shift,
    up_weight,
    up_bias,
    down_weight,
    down_bias,
    second_gain,
    second_shift,
    cotangent,
    clip_limit,
):
    query_full, key_full, value_full, out_full, up_full, down_full = (
        lax.all_gather(query_weight, "dp", axis=0, tiled=True),
        lax.all_gather(key_weight, "dp", axis=0, tiled=True),
        lax.all_gather(value_weight, "dp", axis=0, tiled=True),
        lax.all_gather(out_weight, "dp", axis=1, tiled=True),
        lax.all_gather(up_weight, "dp", axis=0, tiled=True),
        lax.all_gather(down_weight, "dp", axis=1, tiled=True),
    )
    width = query_full.shape[1]
    hidden_width = up_full.shape[1]
    heads_here = width // HD
    score_scale = HD ** (-0.5)
    joint_weight = jnp.concatenate([query_full, key_full, value_full], axis=1)
    gathered = lax.all_gather(tokens, "tensor", axis=0, tiled=True)
    group_rows = gathered.shape[0]
    seq_count = group_rows // LEN
    block_count = LEN // QB
    projected = jnp.dot(gathered, joint_weight, preferred_element_type=jnp.float32)
    queries = (projected[:, :width] + query_bias.astype(jnp.float32)).astype(jnp.bfloat16)
    keyset = projected[:, width : 2 * width].astype(jnp.bfloat16)
    valset = (projected[:, 2 * width :] + value_bias.astype(jnp.float32)).astype(jnp.bfloat16)
    query_seq = queries.reshape(seq_count, LEN, heads_here, HD)
    key_seq = keyset.reshape(seq_count, LEN, heads_here, HD)
    value_seq = valset.reshape(seq_count, LEN, heads_here, HD)

    def attend_block(block_id):
        seq_id = block_id // block_count
        row_start = block_id % block_count * QB
        query_rows = lax.dynamic_slice_in_dim(
            lax.dynamic_index_in_dim(query_seq, seq_id, 0, False), row_start, QB, 0
        )
        key_rows = lax.dynamic_index_in_dim(key_seq, seq_id, 0, False)
        value_rows = lax.dynamic_index_in_dim(value_seq, seq_id, 0, False)
        logits = (
            jnp.einsum("qhd,khd->hqk", query_rows, key_rows, preferred_element_type=jnp.float32)
            * score_scale
        )
        row_max = jnp.max(logits, axis=2, keepdims=True)
        exponent = jnp.exp(logits - row_max)
        totals = jnp.sum(exponent, axis=2, keepdims=True)
        probs_low = (exponent / totals).astype(jnp.bfloat16)
        context_rows = jnp.einsum(
            "hqk,khd->qhd", probs_low, value_rows, preferred_element_type=jnp.float32
        )
        return (
            context_rows.reshape(QB, width).astype(jnp.bfloat16),
            (row_max + jnp.log(totals))[:, :, 0],
            jnp.max(row_max, axis=(1, 2)),
        )

    context_blocks, log_totals, block_peaks = lax.map(
        attend_block, jnp.arange(seq_count * block_count)
    )
    context = context_blocks.reshape(group_rows, width)
    logit_peak = lax.pmax(jnp.max(block_peaks, axis=0), "dp")
    attention = lax.psum_scatter(
        jnp.dot(context, out_full, preferred_element_type=jnp.float32).astype(jnp.bfloat16),
        "tensor",
        scatter_dimension=0,
        tiled=True,
    ).astype(jnp.float32) + out_bias.astype(jnp.float32)
    first_resid = tokens.astype(jnp.float32) + attention
    hidden, first_pull = jax.vjp(
        layer_norm, first_resid, first_gain.astype(jnp.float32), first_shift.astype(jnp.float32)
    )
    hidden_all = lax.all_gather(hidden.astype(jnp.bfloat16), "tensor", axis=0, tiled=True)
    upper = jnp.dot(hidden_all, up_full, preferred_element_type=jnp.float32) + up_bias.astype(
        jnp.float32
    )
    acted = jax.nn.gelu(upper, approximate=False).astype(jnp.bfloat16)
    branch = lax.psum_scatter(
        jnp.dot(acted, down_full, preferred_element_type=jnp.float32).astype(jnp.bfloat16),
        "tensor",
        scatter_dimension=0,
        tiled=True,
    ).astype(jnp.float32) + down_bias.astype(jnp.float32)
    normed, second_pull = jax.vjp(
        layer_norm,
        hidden + branch,
        second_gain.astype(jnp.float32),
        second_shift.astype(jnp.float32),
    )
    layer_out = normed.astype(jnp.bfloat16)
    grad_second, second_gain_grad, second_shift_grad = second_pull(cotangent.astype(jnp.float32))
    grad_branch = grad_second.astype(jnp.bfloat16)
    down_bias_grad = jnp.sum(grad_branch, axis=0, dtype=jnp.float32)
    branch_all = lax.all_gather(grad_branch, "tensor", axis=0, tiled=True)
    grad_acted = contract_cols(branch_all, down_full)
    down_weight_grad = contract_rows(acted, branch_all)
    grad_upper = (grad_acted * gelu_slope(upper)).astype(jnp.bfloat16)
    up_bias_grad = jnp.sum(grad_upper, axis=0, dtype=jnp.float32)
    up_weight_grad = contract_rows(hidden_all, grad_upper)
    grad_hidden = grad_second + lax.psum_scatter(
        contract_cols(grad_upper, up_full).astype(jnp.bfloat16),
        "tensor",
        scatter_dimension=0,
        tiled=True,
    ).astype(jnp.float32)
    grad_first, first_gain_grad, first_shift_grad = first_pull(grad_hidden)
    grad_attn = grad_first.astype(jnp.bfloat16)
    out_bias_grad = jnp.sum(grad_attn, axis=0, dtype=jnp.float32)
    attn_all = lax.all_gather(grad_attn, "tensor", axis=0, tiled=True)
    grad_context = contract_cols(attn_all, out_full).astype(jnp.bfloat16)
    out_weight_grad = contract_rows(context, attn_all)
    query_blocks = queries.reshape(seq_count, block_count, QB, heads_here, HD)
    grad_blocks = grad_context.reshape(seq_count, block_count, QB, heads_here, HD)
    log_blocks = log_totals.reshape(seq_count, block_count, heads_here, QB)

    def sequence_back(item):
        query_part, grad_part, log_part, key_rows, value_rows = item

        def block_back(carry, piece):
            key_acc, value_acc = carry
            query_rows, grad_rows, log_rows = piece
            logits = (
                jnp.einsum("qhd,khd->hqk", query_rows, key_rows, preferred_element_type=jnp.float32)
                * score_scale
            )
            probs = jnp.exp(logits - log_rows[:, :, None])
            probs_low = probs.astype(jnp.bfloat16)
            value_acc = value_acc + jnp.einsum(
                "hqk,qhd->khd", probs_low, grad_rows, preferred_element_type=jnp.float32
            )
            grad_probs = jnp.einsum(
                "qhd,khd->hqk", grad_rows, value_rows, preferred_element_type=jnp.float32
            )
            inner = jnp.sum(probs * grad_probs, axis=2, keepdims=True)
            grad_logits = (probs * (grad_probs - inner)).astype(jnp.bfloat16)
            grad_query = (
                jnp.einsum(
                    "hqk,khd->qhd", grad_logits, key_rows, preferred_element_type=jnp.float32
                )
                * score_scale
            )
            key_acc = (
                key_acc
                + jnp.einsum(
                    "hqk,qhd->khd", grad_logits, query_rows, preferred_element_type=jnp.float32
                )
                * score_scale
            )
            return ((key_acc, value_acc), grad_query.astype(jnp.bfloat16))

        empty = jnp.zeros((LEN, heads_here, HD), jnp.float32)
        (key_acc, value_acc), grad_query_rows = lax.scan(
            block_back, (empty, empty), (query_part, grad_part, log_part)
        )
        return (grad_query_rows, key_acc.astype(jnp.bfloat16), value_acc.astype(jnp.bfloat16))

    grad_queries_all, grad_keys_all, grad_values_all = lax.map(
        sequence_back, (query_blocks, grad_blocks, log_blocks, key_seq, value_seq)
    )
    grad_joint = jnp.concatenate(
        [
            grad_queries_all.reshape(group_rows, width),
            grad_keys_all.reshape(group_rows, width),
            grad_values_all.reshape(group_rows, width),
        ],
        axis=1,
    )
    joint_grad = contract_rows(gathered, grad_joint)
    query_weight_grad = joint_grad[:, :width]
    key_weight_grad = joint_grad[:, width : 2 * width]
    value_weight_grad = joint_grad[:, 2 * width :]
    query_bias_grad = jnp.sum(grad_joint[:, :width], axis=0, dtype=jnp.float32)
    value_bias_grad = jnp.sum(grad_joint[:, 2 * width :], axis=0, dtype=jnp.float32)
    tokens_grad = (
        grad_first
        + lax.psum_scatter(
            contract_cols(grad_joint, joint_weight).astype(jnp.bfloat16),
            "tensor",
            scatter_dimension=0,
            tiled=True,
        ).astype(jnp.float32)
    ).astype(jnp.bfloat16)
    (
        query_weight_grad,
        key_weight_grad,
        value_weight_grad,
        out_weight_grad,
        up_weight_grad,
        down_weight_grad,
    ) = (
        lax.psum_scatter(
            query_weight_grad.astype(jnp.bfloat16), "dp", scatter_dimension=0, tiled=True
        ).astype(jnp.float32),
        lax.psum_scatter(
            key_weight_grad.astype(jnp.bfloat16), "dp", scatter_dimension=0, tiled=True
        ).astype(jnp.float32),
        lax.psum_scatter(
            value_weight_grad.astype(jnp.bfloat16), "dp", scatter_dimension=0, tiled=True
        ).astype(jnp.float32),
        lax.psum_scatter(
            out_weight_grad.astype(jnp.bfloat16), "dp", scatter_dimension=1, tiled=True
        ).astype(jnp.float32),
        lax.psum_scatter(
            up_weight_grad.astype(jnp.bfloat16), "dp", scatter_dimension=0, tiled=True
        ).astype(jnp.float32),
        lax.psum_scatter(
            down_weight_grad.astype(jnp.bfloat16), "dp", scatter_dimension=1, tiled=True
        ).astype(jnp.float32),
    )
    tensor_place = lax.axis_index("tensor")
    model_width = out_bias.shape[0]
    query_spread = lax.dynamic_update_slice_in_dim(
        jnp.zeros((model_width,), jnp.float32), query_bias_grad, tensor_place * width, 0
    )
    value_spread = lax.dynamic_update_slice_in_dim(
        jnp.zeros((model_width,), jnp.float32), value_bias_grad, tensor_place * width, 0
    )
    up_spread = lax.dynamic_update_slice_in_dim(
        jnp.zeros((hidden_width * lax.axis_size("tensor"),), jnp.float32),
        up_bias_grad,
        tensor_place * hidden_width,
        0,
    )
    (
        query_spread,
        value_spread,
        up_spread,
        out_bias_grad,
        down_bias_grad,
        first_gain_grad,
        first_shift_grad,
        second_gain_grad,
        second_shift_grad,
    ) = lax.psum(
        (
            query_spread,
            value_spread,
            up_spread,
            out_bias_grad,
            down_bias_grad,
            first_gain_grad,
            first_shift_grad,
            second_gain_grad,
            second_shift_grad,
        ),
        ("dp", "tensor"),
    )
    query_bias_grad = lax.dynamic_slice_in_dim(query_spread, tensor_place * width, width, 0)
    value_bias_grad = lax.dynamic_slice_in_dim(value_spread, tensor_place * width, width, 0)
    up_bias_grad = lax.dynamic_slice_in_dim(up_spread, tensor_place * hidden_width, hidden_width, 0)
    factor = clip_limit / jnp.maximum(logit_peak, clip_limit)
    column_scale = jnp.repeat(jnp.sqrt(factor), HD)
    query_clipped = (query_weight.astype(jnp.float32) * column_scale).astype(jnp.bfloat16)
    query_bias_clipped = (query_bias.astype(jnp.float32) * column_scale).astype(jnp.bfloat16)
    key_clipped = (key_weight.astype(jnp.float32) * column_scale).astype(jnp.bfloat16)
    return (
        layer_out,
        tokens_grad,
        query_weight_grad,
        query_bias_grad,
        key_weight_grad,
        value_weight_grad,
        value_bias_grad,
        out_weight_grad,
        out_bias_grad,
        first_gain_grad,
        first_shift_grad,
        up_weight_grad,
        up_bias_grad,
        down_weight_grad,
        down_bias_grad,
        second_gain_grad,
        second_shift_grad,
        logit_peak,
        query_clipped,
        query_bias_clipped,
        key_clipped,
    )


LOG2E=1.4426950408889634
NT=(((1,),(1,)),((),()))
NN=(((1,),(0,)),((),()))
def dot(a,b,dims):
    return lax.dot_general(a,b,dims,preferred_element_type=jnp.float32)
def fwd_kernel(rb, qkv_ref, ctx_ref, lse_ref, peak_ref, vt_ref, ctxt_ref):
    rows=qkv_ref.shape[0]; width=qkv_ref.shape[1]//3; pairs=width//128
    lane=lax.broadcasted_iota(jnp.int32,(1,128),1)
    scale=jnp.bfloat16(HD**-0.5)
    @pl.loop(0,pairs)
    def _(p):
        cq=pl.multiple_of(p*128,128); ck=pl.multiple_of(width+p*128,128); cv=pl.multiple_of(2*width+p*128,128)
        vt_ref[...]=jnp.zeros_like(vt_ref)
        vT=qkv_ref[:,pl.ds(cv,128)].T
        vt_ref[0,0:64,:]=vT[0:64]; vt_ref[1,0:64,:]=vT[64:128]
        row=lax.broadcasted_iota(jnp.int32,(16,rows),0)
        ones=jnp.where(row==0,1.0,0.0).astype(jnp.bfloat16)
        vt_ref[0,64:80,:]=ones; vt_ref[1,64:80,:]=ones
        for h in (0,1):
            keep=(lane<64) if h==0 else (lane>=64)
            pk=None
            for r in range(rows//rb):
                q=qkv_ref[r*rb:(r+1)*rb,pl.ds(cq,128)]*scale
                q=jnp.where(keep,q,jnp.bfloat16(0))
                st=dot(qkv_ref[:,pl.ds(ck,128)],q,NT)
                m=jnp.max(st,axis=0,keepdims=True)
                mc=m*LOG2E
                pt=jnp.exp2(st*LOG2E-mc).astype(jnp.bfloat16)
                ot=dot(vt_ref[h],pt,NN)
                tot=ot[64:65]
                ctxt_ref[h*64:(h+1)*64,r*rb:(r+1)*rb]=ot[0:64]*(1.0/tot)
                lse_ref[pl.ds(2*p+h,1),r*rb:(r+1)*rb]=mc+jnp.log2(tot)
                mm=jnp.max(m,axis=1,keepdims=True)
                pk=mm if pk is None else jnp.maximum(pk,mm)
            peak_ref[pl.ds(2*p+h,1),:]=jnp.broadcast_to(pk,(1,128))
        ctx_ref[:,pl.ds(cq,128)]=ctxt_ref[...].T.astype(jnp.bfloat16)
def attn_fwd(qkv,rb=256):
    rows=qkv.shape[0]; width=qkv.shape[1]//3; heads=width//HD
    V=pl.BlockSpec(memory_space=pltpu.VMEM)
    return pl.pallas_call(functools.partial(fwd_kernel,rb),
      out_shape=(jax.ShapeDtypeStruct((rows,width),jnp.bfloat16),jax.ShapeDtypeStruct((heads,rows),jnp.float32),jax.ShapeDtypeStruct((heads,128),jnp.float32)),
      in_specs=[V],out_specs=(V,V,V),
      scratch_shapes=[pltpu.VMEM((2,80,rows),jnp.bfloat16),pltpu.VMEM((128,rows),jnp.float32)],
      compiler_params=pltpu.CompilerParams(vmem_limit_bytes=56*2**20),name="attn_fwd")(qkv)
def bwd_kernel(rb, qkv_ref, ctx_ref, dctx_ref, lse_ref, dqkv_ref, kt_ref, dqt_ref, dk_ref, dv_ref, dl_ref):
    rows=qkv_ref.shape[0]; width=qkv_ref.shape[1]//3; pairs=width//128
    lane=lax.broadcasted_iota(jnp.int32,(1,128),1)
    scale=jnp.bfloat16(HD**-0.5)
    zero=jnp.bfloat16(0)
    @pl.loop(0,pairs)
    def _(p):
        cq=pl.multiple_of(p*128,128); ck=pl.multiple_of(width+p*128,128); cv=pl.multiple_of(2*width+p*128,128)
        kt_ref[...]=qkv_ref[:,pl.ds(ck,128)].T
        prod=(ctx_ref[:,pl.ds(cq,128)].astype(jnp.float32)*dctx_ref[:,pl.ds(cq,128)].astype(jnp.float32)).T
        dl_ref[0:1]=jnp.sum(prod[0:64],axis=0,keepdims=True)
        dl_ref[1:2]=jnp.sum(prod[64:128],axis=0,keepdims=True)
        dk_ref[...]=jnp.zeros_like(dk_ref); dv_ref[...]=jnp.zeros_like(dv_ref)
        for r in range(rows//rb):
            rs=slice(r*rb,(r+1)*rb)
            for h in (0,1):
                keep=(lane<64) if h==0 else (lane>=64)
                q=jnp.where(keep,qkv_ref[rs,pl.ds(cq,128)]*scale,zero)
                do=jnp.where(keep,dctx_ref[rs,pl.ds(cq,128)],zero)
                st=dot(qkv_ref[:,pl.ds(ck,128)],q,NT)
                pt=jnp.exp2(st*LOG2E-lse_ref[pl.ds(2*p+h,1),rs])
                dpt=dot(qkv_ref[:,pl.ds(cv,128)],do,NT)
                ds=(pt*(dpt-dl_ref[h:h+1,rs])).astype(jnp.bfloat16)
                dv_ref[...]+=dot(pt.astype(jnp.bfloat16),do,NN)
                dk_ref[...]+=dot(ds,q,NN)
                dqt_ref[h*64:(h+1)*64,rs]=dot(kt_ref[h*64:(h+1)*64,:],ds,NN)
        dqkv_ref[:,pl.ds(cq,128)]=(dqt_ref[...].T*(HD**-0.5)).astype(jnp.bfloat16)
        dqkv_ref[:,pl.ds(ck,128)]=dk_ref[...].astype(jnp.bfloat16)
        dqkv_ref[:,pl.ds(cv,128)]=dv_ref[...].astype(jnp.bfloat16)
def attn_bwd(qkv,ctx,dctx,lse,rb=256):
    rows=qkv.shape[0]; width=qkv.shape[1]//3; heads=width//HD
    V=pl.BlockSpec(memory_space=pltpu.VMEM)
    return pl.pallas_call(functools.partial(bwd_kernel,rb),
      out_shape=jax.ShapeDtypeStruct((rows,3*width),jnp.bfloat16),
      in_specs=[V]*4,out_specs=V,
      scratch_shapes=[pltpu.VMEM((128,rows),jnp.bfloat16),pltpu.VMEM((128,rows),jnp.float32),pltpu.VMEM((rows,128),jnp.float32),pltpu.VMEM((rows,128),jnp.float32),pltpu.VMEM((8,rows),jnp.float32)],
      compiler_params=pltpu.CompilerParams(vmem_limit_bytes=56*2**20),name="attn_bwd")(qkv,ctx,dctx,lse)

MESH=pl.DeviceIdType.MESH
TN=(((0,),(0,)),((),()))
F32=jnp.float32; BF=jnp.bfloat16

def greet(partner):
    barrier=pltpu.get_barrier_semaphore()
    pl.semaphore_signal(barrier,inc=1,device_id=partner,device_id_type=MESH)
    pl.semaphore_wait(barrier,1)

def qkv_kernel(tok_ref,w_ref,bias_ref,qkv_ref,xall_ref,ssem,rsem):
    d=lax.axis_index("dp"); t=lax.axis_index("tensor")
    partner=(d,1-t)
    own=tok_ref.shape[0]
    greet(partner)
    mine=pl.ds(pl.multiple_of(t*own,own),own); other=pl.ds(pl.multiple_of((1-t)*own,own),own)
    copy=pltpu.make_async_remote_copy(tok_ref,xall_ref.at[mine],ssem,rsem,device_id=partner,device_id_type=MESH)
    copy.start()
    xall_ref[mine]=tok_ref[...]
    n=w_ref.shape[1]
    def rows(which):
        @pl.loop(0,n//256)
        def _(j):
            cs=pl.ds(pl.multiple_of(j*256,256),256)
            qkv_ref[which,cs]=(dot(xall_ref[which],w_ref[:,cs],NN)+bias_ref[:,cs]).astype(BF)
    rows(mine)
    copy.wait_recv()
    rows(other)
    copy.wait_send()

def qkv_call(tok,w,bias,cid):
    V=pl.BlockSpec(memory_space=pltpu.VMEM)
    rows=2*tok.shape[0]
    return pl.pallas_call(qkv_kernel,
      out_shape=(jax.ShapeDtypeStruct((rows,w.shape[1]),BF),jax.ShapeDtypeStruct((rows,tok.shape[1]),BF)),
      in_specs=[V]*3,out_specs=(V,V),scratch_shapes=[pltpu.SemaphoreType.DMA,pltpu.SemaphoreType.DMA],
      compiler_params=pltpu.CompilerParams(collective_id=cid,has_side_effects=True,vmem_limit_bytes=56*2**20),
      cost_estimate=pl.CostEstimate(flops=2*rows*w.shape[0]*w.shape[1],bytes_accessed=8*2**20,transcendentals=0),
      name="qkv")(tok,w,bias)

NC=4
def ffn_kernel(ctx,w_hbm,tok,cot,vec,upb,
               lo,gf,dctx,dw_hbm,vg,ubg,
               wo,wup,wdn,xh,hid,rst,hall,act,slp,ball,aall,part,sbuf,rbuf,tb,th,stage,
               wsem,osem,ssem,rsem):
    d=lax.axis_index("dp"); t=lax.axis_index("tensor")
    partner=(d,1-t)
    own=tok.shape[0]; cr=own//NC; width=ctx.shape[1]; ff=wup.shape[1]; dm=tok.shape[1]
    cws=[pltpu.make_async_copy(w_hbm.at[:,0:width],wo,wsem.at[0]),
         pltpu.make_async_copy(w_hbm.at[:,width:width+ff],wup,wsem.at[1]),
         pltpu.make_async_copy(w_hbm.at[:,width+ff:width+2*ff],wdn,wsem.at[2])]
    for c in cws: c.start()
    greet(partner)
    def rows(rank,c): return pl.ds(pl.multiple_of(rank*own+c*cr,cr),cr)
    def loc(c): return pl.ds(pl.multiple_of(c*cr,cr),cr)
    def rs_copy(k,c):
        return pltpu.make_async_remote_copy(sbuf.at[k,loc(c)],rbuf.at[k,loc(c)],ssem.at[k,c],rsem.at[k,c],device_id=partner,device_id_type=MESH)
    def ag_copy(k,buf,c,rank):
        return pltpu.make_async_remote_copy(buf.at[rows(rank,c)],buf.at[rows(rank,c)],ssem.at[k,c],rsem.at[k,c],device_id=partner,device_id_type=MESH)
    vg[...]=jnp.zeros_like(vg); ubg[...]=jnp.zeros_like(ubg)
    cws[0].wait()
    @pl.loop(0,NC)
    def _(c):
        sbuf[0,loc(c)]=dot(ctx[rows(1-t,c)],wo[...],NT).astype(BF)
        rs_copy(0,c).start()
        part[loc(c)]=dot(ctx[rows(t,c)],wo[...],NT)
    @pl.loop(0,NC)
    def _(c):
        rs_copy(0,c).wait_recv()
        v=tok[loc(c)].astype(F32)+part[loc(c)]+rbuf[0,loc(c)].astype(F32)+vec[0:1]
        cen=v-jnp.mean(v,axis=1,keepdims=True)
        r=lax.rsqrt(jnp.mean(cen*cen,axis=1,keepdims=True)+EPSILON)
        x=cen*r
        h=x*vec[1:2]+vec[2:3]
        xh[loc(c)]=x; hid[loc(c)]=h
        rst[loc(c)]=jnp.broadcast_to(r,(cr,128))
        hall[rows(t,c)]=h.astype(BF)
        ag_copy(3,hall,c,t).start()
    cws[1].wait(); cws[2].wait()
    TF=512
    @pl.loop(0,NC)
    def _(c):
        ag_copy(3,hall,c,1-t).wait_recv()
        for who in (0,1):
            rr=rows(1-t if who==0 else t,c)
            @pl.loop(0,ff//TF)
            def _(j):
                cs=pl.ds(pl.multiple_of(j*TF,TF),TF)
                u=dot(hall[rr],wup[:,cs],NN)+upb[:,cs]
                cdf=0.5*(1.0+lax.erf(u*0.5**0.5))
                act[rr,cs]=(u*cdf).astype(BF)
                slp[rr,cs]=(cdf+u*jnp.exp(-0.5*u*u)*(0.5/math.pi)**0.5).astype(BF)
            p=dot(act[rr],wdn[...],NT)
            if who==0:
                sbuf[1,loc(c)]=p.astype(BF)
                rs_copy(1,c).start()
            else:
                part[loc(c)]=p
    @pl.loop(0,NC)
    def _(c):
        rs_copy(1,c).wait_recv()
        v=hid[loc(c)]+part[loc(c)]+rbuf[1,loc(c)].astype(F32)+vec[3:4]
        cen=v-jnp.mean(v,axis=1,keepdims=True)
        r=lax.rsqrt(jnp.mean(cen*cen,axis=1,keepdims=True)+EPSILON)
        x=cen*r
        lo[loc(c)]=(x*vec[4:5]+vec[5:6]).astype(BF)
        dy=cot[loc(c)].astype(F32)
        vg[4:5]+=jnp.sum(dy*x,axis=0,keepdims=True)
        vg[5:6]+=jnp.sum(dy,axis=0,keepdims=True)
        dx=dy*vec[4:5]
        g=r*(dx-jnp.mean(dx,axis=1,keepdims=True)-x*jnp.mean(dx*x,axis=1,keepdims=True))
        gf[loc(c)]=g
        gb=g.astype(BF)
        vg[3:4]+=jnp.sum(gb.astype(F32),axis=0,keepdims=True)
        ball[rows(t,c)]=gb
        ag_copy(4,ball,c,t).start()
        th[:,pl.ds(pl.multiple_of(c*256,256),256)]=hall[pl.ds(pl.multiple_of(c*256,256),256)].T
    @pl.loop(0,NC)
    def _(c):
        ag_copy(4,ball,c,1-t).wait_recv()
        for who in (0,1):
            rr=rows(1-t if who==0 else t,c)
            @pl.loop(0,ff//TF)
            def _(j):
                cs=pl.ds(pl.multiple_of(j*TF,TF),TF)
                gu=(dot(ball[rr],wdn[:,cs],NN)*slp[rr,cs].astype(F32)).astype(BF)
                slp[rr,cs]=gu
                ubg[0:1,cs]+=jnp.sum(gu.astype(F32),axis=0,keepdims=True)
            p=dot(slp[rr],wup[...],NT)
            if who==0:
                sbuf[2,loc(c)]=p.astype(BF)
                rs_copy(2,c).start()
            else:
                part[loc(c)]=p
    def out_copy(slot,col):
        return pltpu.make_async_copy(stage.at[slot],dw_hbm.at[:,pl.ds(pl.multiple_of(col,512),512)],osem.at[slot])
    def wgrad(slot,left,right_ref,rcol,ocol):
        @pl.loop(0,dm//256)
        def _(i):
            ms=pl.ds(pl.multiple_of(i*256,256),256)
            stage[slot,ms]=dot(left[ms],right_ref[:,pl.ds(pl.multiple_of(rcol,512),512)],NN).astype(BF)
        out_copy(slot,ocol).start()
    nt=ff//512
    @pl.loop(0,NC)
    def _(c):
        tb[:,pl.ds(pl.multiple_of(c*256,256),256)]=ball[pl.ds(pl.multiple_of(c*256,256),256)].T
        rs_copy(2,c).wait_recv()
        dy=gf[loc(c)]+part[loc(c)]+rbuf[2,loc(c)].astype(F32)
        x=xh[loc(c)]; r=rst[loc(c)][:,0:1]
        vg[1:2]+=jnp.sum(dy*x,axis=0,keepdims=True)
        vg[2:3]+=jnp.sum(dy,axis=0,keepdims=True)
        dx=dy*vec[1:2]
        g=r*(dx-jnp.mean(dx,axis=1,keepdims=True)-x*jnp.mean(dx*x,axis=1,keepdims=True))
        gf[loc(c)]=g
        gb=g.astype(BF)
        vg[0:1]+=jnp.sum(gb.astype(F32),axis=0,keepdims=True)
        aall[rows(t,c)]=gb
        ag_copy(5,aall,c,t).start()
    @pl.loop(0,NC)
    def _(c):
        slot=c%2
        @pl.when(c>=2)
        def _(): out_copy(slot,0).wait()
        wgrad(slot,th,slp,c*512,width+c*512)
        ag_copy(5,aall,c,1-t).wait_recv()
        for who in (0,1):
            rr=rows(1-t if who==0 else t,c)
            dctx[rr]=dot(aall[rr],wo[...],NN).astype(BF)
    @pl.loop(0,nt)
    def _(c):
        slot=c%2
        out_copy(slot,0).wait()
        wgrad(slot,tb,act,c*512,width+ff+c*512)
    @pl.loop(0,NC)
    def _(c):
        tb[:,pl.ds(pl.multiple_of(c*256,256),256)]=aall[pl.ds(pl.multiple_of(c*256,256),256)].T
    out_copy(0,0).wait()
    wgrad(0,tb,ctx,0,0)
    out_copy(1,0).wait()
    out_copy(0,0).wait()
    for k in range(3):
        @pl.loop(0,NC)
        def _(c): rs_copy(k,c).wait_send()
    for k,buf in ((3,hall),(4,ball),(5,aall)):
        @pl.loop(0,NC)
        def _(c): ag_copy(k,buf,c,t).wait_send()

def ffn_call(ctx,w,tok,cot,vec,upb,cid):
    V=pl.BlockSpec(memory_space=pltpu.VMEM); A=pl.BlockSpec(memory_space=pl.ANY)
    rows,width=ctx.shape; own,dm=tok.shape; ff=upb.shape[1]
    S=jax.ShapeDtypeStruct
    return pl.pallas_call(ffn_kernel,
      out_shape=(S((own,dm),BF),S((own,dm),F32),S((rows,width),BF),S((dm,width+2*ff),BF),S((8,dm),F32),S((8,ff),F32)),
      in_specs=[V,A,V,V,V,V],out_specs=(V,V,V,A,V,V),
      scratch_shapes=[pltpu.VMEM((dm,width),BF),pltpu.VMEM((dm,ff),BF),pltpu.VMEM((dm,ff),BF),
        pltpu.VMEM((own,dm),F32),pltpu.VMEM((own,dm),F32),pltpu.VMEM((own,128),F32),
        pltpu.VMEM((rows,dm),BF),pltpu.VMEM((rows,ff),BF),pltpu.VMEM((rows,ff),BF),pltpu.VMEM((rows,dm),BF),pltpu.VMEM((rows,dm),BF),
        pltpu.VMEM((own,dm),F32),pltpu.VMEM((3,own,dm),BF),pltpu.VMEM((3,own,dm),BF),
        pltpu.VMEM((dm,rows),BF),pltpu.VMEM((dm,rows),BF),pltpu.VMEM((2,dm,512),BF),
        pltpu.SemaphoreType.DMA((3,)),pltpu.SemaphoreType.DMA((2,)),pltpu.SemaphoreType.DMA((6,NC)),pltpu.SemaphoreType.DMA((6,NC))],
      compiler_params=pltpu.CompilerParams(collective_id=cid,has_side_effects=True,vmem_limit_bytes=60*2**20),
      cost_estimate=pl.CostEstimate(flops=2*rows*dm*(6*ff+3*width),bytes_accessed=40*2**20,transcendentals=2*rows*ff),
      name="ffn")(ctx,w,tok,cot,vec,upb)

def tail_kernel(dqkv,w,xall,gf,tg,dw,xt,part,sbuf,rbuf,ssem,rsem):
    d=lax.axis_index("dp"); t=lax.axis_index("tensor")
    partner=(d,1-t)
    own,dm=gf.shape; n=w.shape[1]; rows=xall.shape[0]; half=own//2
    greet(partner)
    def rs_copy(c):
        return pltpu.make_async_remote_copy(sbuf.at[c],rbuf.at[c],ssem.at[c],rsem.at[c],device_id=partner,device_id_type=MESH)
    def rr(rank,c): return pl.ds(pl.multiple_of(rank*own+c*half,half),half)
    for c in (0,1):
        sbuf[c]=dot(dqkv[rr(1-t,c)],w[...],NT).astype(BF)
        rs_copy(c).start()
    for c in (0,1):
        part[c]=dot(dqkv[rr(t,c)],w[...],NT)
    @pl.loop(0,rows//256)
    def _(c):
        xt[:,pl.ds(pl.multiple_of(c*256,256),256)]=xall[pl.ds(pl.multiple_of(c*256,256),256)].T
    @pl.loop(0,n//512)
    def _(j):
        cs=pl.ds(pl.multiple_of(j*512,512),512)
        @pl.loop(0,dm//256)
        def _(i):
            ms=pl.ds(pl.multiple_of(i*256,256),256)
            dw[ms,cs]=dot(xt[ms],dqkv[:,cs],NN).astype(BF)
    for c in (0,1):
        rs_copy(c).wait_recv()
        ls=slice(c*half,(c+1)*half)
        tg[ls]=(gf[ls]+part[c]+rbuf[c].astype(F32)).astype(BF)
    for c in (0,1): rs_copy(c).wait_send()

def tail_call(dqkv,w,xall,gf,cid):
    V=pl.BlockSpec(memory_space=pltpu.VMEM)
    own,dm=gf.shape; n=w.shape[1]; rows=xall.shape[0]
    S=jax.ShapeDtypeStruct
    return pl.pallas_call(tail_kernel,out_shape=(S((own,dm),BF),S((dm,n),BF)),in_specs=[V]*4,out_specs=(V,V),
      scratch_shapes=[pltpu.VMEM((dm,rows),BF),pltpu.VMEM((2,own//2,dm),F32),pltpu.VMEM((2,own//2,dm),BF),pltpu.VMEM((2,own//2,dm),BF),
        pltpu.SemaphoreType.DMA((2,)),pltpu.SemaphoreType.DMA((2,))],
      compiler_params=pltpu.CompilerParams(collective_id=cid,has_side_effects=True,vmem_limit_bytes=56*2**20),
      name="tail")(dqkv,w,xall,gf)

def per_device_pair(tokens,query_weight,query_bias,key_weight,value_weight,value_bias,out_weight,out_bias,first_gain,first_shift,
    up_weight,up_bias,down_weight,down_bias,second_gain,second_shift,cotangent,clip_limit):
    width=query_weight.shape[1]; ff=up_weight.shape[1]; dm=tokens.shape[1]
    f=lambda a:a.astype(F32)
    head_shard=jnp.concatenate([query_weight,key_weight,value_weight],axis=1)
    rest_shard=jnp.concatenate([out_weight.T,up_weight,down_weight.T],axis=1)
    head_w=lax.all_gather(head_shard,"dp",axis=0,tiled=True)
    rest_shard,_=lax.optimization_barrier((rest_shard,head_w))
    rest_w=lax.all_gather(rest_shard,"dp",axis=0,tiled=True)
    bias=jnp.concatenate([f(query_bias),jnp.zeros((width,),F32),f(value_bias)])[None]
    qkv,xall=qkv_call(tokens,head_w,bias,0)
    ctx,lse,peak=attn_fwd(qkv,512)
    z=jnp.zeros((dm,),F32)
    vec=jnp.stack([f(out_bias),f(first_gain),f(first_shift),f(down_bias),f(second_gain),f(second_shift),z,z])
    lo,gf,dctx,dw,vg,ubg=ffn_call(ctx,rest_w,tokens,cotangent,vec,f(up_bias)[None],1)
    rest_g=lax.psum_scatter(dw,"dp",scatter_dimension=0,tiled=True)
    dqkv=attn_bwd(qkv,ctx,dctx,lse,256)
    tg,dwh=tail_call(dqkv,head_w,xall,gf,2)
    head_g=lax.psum_scatter(dwh,"dp",scatter_dimension=0,tiled=True)
    qb=jnp.sum(dqkv[:,:width],axis=0,dtype=F32); vb=jnp.sum(dqkv[:,2*width:],axis=0,dtype=F32)
    small=jnp.concatenate([qb,vb,ubg[0]])
    small=lax.psum(small,"dp")
    vgs=lax.psum(vg,("dp","tensor"))
    logit_peak=lax.pmax(peak[:,0],"dp")
    factor=clip_limit/jnp.maximum(logit_peak,clip_limit)
    cs=jnp.repeat(jnp.sqrt(factor),HD)
    qc=(f(query_weight)*cs).astype(BF); qbc=(f(query_bias)*cs).astype(BF); kc=(f(key_weight)*cs).astype(BF)
    hg=f(head_g); rg=f(rest_g)
    return (lo,tg,hg[:,:width],small[:width],hg[:,width:2*width],hg[:,2*width:],small[width:2*width],
      rg[:,:width].T,vgs[0],vgs[1],vgs[2],rg[:,width:width+ff],small[2*width:],rg[:,width+ff:].T,vgs[3],vgs[4],vgs[5],
      logit_peak,qc,qbc,kc)


def layer(*args):
    paired = lax.axis_size("tensor") == 2 and 2 * args[0].shape[0] == LEN
    return per_device_pair(*args) if paired else per_device(*args)


def solution(mesh):
    in_specs = (
        P(("dp", "tensor"), None),
        P("dp", "tensor"),
        P("tensor"),
        P("dp", "tensor"),
        P("dp", "tensor"),
        P("tensor"),
        P("tensor", "dp"),
        P(),
        P(),
        P(),
        P("dp", "tensor"),
        P("tensor"),
        P("tensor", "dp"),
        P(),
        P(),
        P(),
        P(("dp", "tensor"), None),
        P("tensor"),
    )
    out_specs = (
        P(("dp", "tensor"), None),
        P(("dp", "tensor"), None),
        P("dp", "tensor"),
        P("tensor"),
        P("dp", "tensor"),
        P("dp", "tensor"),
        P("tensor"),
        P("tensor", "dp"),
        P(),
        P(),
        P(),
        P("dp", "tensor"),
        P("tensor"),
        P("tensor", "dp"),
        P(),
        P(),
        P(),
        P("tensor"),
        P("dp", "tensor"),
        P("tensor"),
        P("dp", "tensor"),
    )
    return jax.shard_map(
        layer, mesh=mesh, in_specs=in_specs, out_specs=out_specs, check_vma=False
    )
```

```python
import functools
import math

import jax
import jax.numpy as jnp
from jax import lax
from jax.experimental import pallas as pl
from jax.experimental.pallas import tpu as pltpu
from jax.sharding import PartitionSpec as P

HD = 64
LEN = 1024
QB = 512


EPSILON = 1e-05


def layer_norm(values, gain, shift):
    center = values - jnp.mean(values, axis=-1, keepdims=True)
    spread = jnp.mean(center * center, axis=-1, keepdims=True)
    return center * lax.rsqrt(spread + EPSILON) * gain + shift


def gelu_slope(upper):
    normal_cdf = 0.5 * (1.0 + lax.erf(upper * 0.5**0.5))
    return normal_cdf + upper * jnp.exp(-0.5 * upper * upper) * (0.5 / math.pi) ** 0.5


def contract_rows(left, right):
    return lax.dot_general(
        left, right, (((0,), (0,)), ((), ())), preferred_element_type=jnp.float32
    )


def contract_cols(left, right):
    return lax.dot_general(
        left, right, (((1,), (1,)), ((), ())), preferred_element_type=jnp.float32
    )


def per_device(
    tokens,
    query_weight,
    query_bias,
    key_weight,
    value_weight,
    value_bias,
    out_weight,
    out_bias,
    first_gain,
    first_shift,
    up_weight,
    up_bias,
    down_weight,
    down_bias,
    second_gain,
    second_shift,
    cotangent,
    clip_limit,
):
    query_full, key_full, value_full, out_full, up_full, down_full = (
        lax.all_gather(query_weight, "dp", axis=0, tiled=True),
        lax.all_gather(key_weight, "dp", axis=0, tiled=True),
        lax.all_gather(value_weight, "dp", axis=0, tiled=True),
        lax.all_gather(out_weight, "dp", axis=1, tiled=True),
        lax.all_gather(up_weight, "dp", axis=0, tiled=True),
        lax.all_gather(down_weight, "dp", axis=1, tiled=True),
    )
    width = query_full.shape[1]
    hidden_width = up_full.shape[1]
    heads_here = width // HD
    score_scale = HD ** (-0.5)
    joint_weight = jnp.concatenate([query_full, key_full, value_full], axis=1)
    gathered = lax.all_gather(tokens, "tensor", axis=0, tiled=True)
    group_rows = gathered.shape[0]
    seq_count = group_rows // LEN
    block_count = LEN // QB
    projected = jnp.dot(gathered, joint_weight, preferred_element_type=jnp.float32)
    queries = (projected[:, :width] + query_bias.astype(jnp.float32)).astype(jnp.bfloat16)
    keyset = projected[:, width : 2 * width].astype(jnp.bfloat16)
    valset = (projected[:, 2 * width :] + value_bias.astype(jnp.float32)).astype(jnp.bfloat16)
    query_seq = queries.reshape(seq_count, LEN, heads_here, HD)
    key_seq = keyset.reshape(seq_count, LEN, heads_here, HD)
    value_seq = valset.reshape(seq_count, LEN, heads_here, HD)

    def attend_block(block_id):
        seq_id = block_id // block_count
        row_start = block_id % block_count * QB
        query_rows = lax.dynamic_slice_in_dim(
            lax.dynamic_index_in_dim(query_seq, seq_id, 0, False), row_start, QB, 0
        )
        key_rows = lax.dynamic_index_in_dim(key_seq, seq_id, 0, False)
        value_rows = lax.dynamic_index_in_dim(value_seq, seq_id, 0, False)
        logits = (
            jnp.einsum("qhd,khd->hqk", query_rows, key_rows, preferred_element_type=jnp.float32)
            * score_scale
        )
        row_max = jnp.max(logits, axis=2, keepdims=True)
        exponent = jnp.exp(logits - row_max)
        totals = jnp.sum(exponent, axis=2, keepdims=True)
        probs_low = (exponent / totals).astype(jnp.bfloat16)
        context_rows = jnp.einsum(
            "hqk,khd->qhd", probs_low, value_rows, preferred_element_type=jnp.float32
        )
        return (
            context_rows.reshape(QB, width).astype(jnp.bfloat16),
            (row_max + jnp.log(totals))[:, :, 0],
            jnp.max(row_max, axis=(1, 2)),
        )

    context_blocks, log_totals, block_peaks = lax.map(
        attend_block, jnp.arange(seq_count * block_count)
    )
    context = context_blocks.reshape(group_rows, width)
    logit_peak = lax.pmax(jnp.max(block_peaks, axis=0), "dp")
    attention = lax.psum_scatter(
        jnp.dot(context, out_full, preferred_element_type=jnp.float32).astype(jnp.bfloat16),
        "tensor",
        scatter_dimension=0,
        tiled=True,
    ).astype(jnp.float32) + out_bias.astype(jnp.float32)
    first_resid = tokens.astype(jnp.float32) + attention
    hidden, first_pull = jax.vjp(
        layer_norm, first_resid, first_gain.astype(jnp.float32), first_shift.astype(jnp.float32)
    )
    hidden_all = lax.all_gather(hidden.astype(jnp.bfloat16), "tensor", axis=0, tiled=True)
    upper = jnp.dot(hidden_all, up_full, preferred_element_type=jnp.float32) + up_bias.astype(
        jnp.float32
    )
    acted = jax.nn.gelu(upper, approximate=False).astype(jnp.bfloat16)
    branch = lax.psum_scatter(
        jnp.dot(acted, down_full, preferred_element_type=jnp.float32).astype(jnp.bfloat16),
        "tensor",
        scatter_dimension=0,
        tiled=True,
    ).astype(jnp.float32) + down_bias.astype(jnp.float32)
    normed, second_pull = jax.vjp(
        layer_norm,
        hidden + branch,
        second_gain.astype(jnp.float32),
        second_shift.astype(jnp.float32),
    )
    layer_out = normed.astype(jnp.bfloat16)
    grad_second, second_gain_grad, second_shift_grad = second_pull(cotangent.astype(jnp.float32))
    grad_branch = grad_second.astype(jnp.bfloat16)
    down_bias_grad = jnp.sum(grad_branch, axis=0, dtype=jnp.float32)
    branch_all = lax.all_gather(grad_branch, "tensor", axis=0, tiled=True)
    grad_acted = contract_cols(branch_all, down_full)
    down_weight_grad = contract_rows(acted, branch_all)
    grad_upper = (grad_acted * gelu_slope(upper)).astype(jnp.bfloat16)
    up_bias_grad = jnp.sum(grad_upper, axis=0, dtype=jnp.float32)
    up_weight_grad = contract_rows(hidden_all, grad_upper)
    grad_hidden = grad_second + lax.psum_scatter(
        contract_cols(grad_upper, up_full).astype(jnp.bfloat16),
        "tensor",
        scatter_dimension=0,
        tiled=True,
    ).astype(jnp.float32)
    grad_first, first_gain_grad, first_shift_grad = first_pull(grad_hidden)
    grad_attn = grad_first.astype(jnp.bfloat16)
    out_bias_grad = jnp.sum(grad_attn, axis=0, dtype=jnp.float32)
    attn_all = lax.all_gather(grad_attn, "tensor", axis=0, tiled=True)
    grad_context = contract_cols(attn_all, out_full).astype(jnp.bfloat16)
    out_weight_grad = contract_rows(context, attn_all)
    query_blocks = queries.reshape(seq_count, block_count, QB, heads_here, HD)
    grad_blocks = grad_context.reshape(seq_count, block_count, QB, heads_here, HD)
    log_blocks = log_totals.reshape(seq_count, block_count, heads_here, QB)

    def sequence_back(item):
        query_part, grad_part, log_part, key_rows, value_rows = item

        def block_back(carry, piece):
            key_acc, value_acc = carry
            query_rows, grad_rows, log_rows = piece
            logits = (
                jnp.einsum("qhd,khd->hqk", query_rows, key_rows, preferred_element_type=jnp.float32)
                * score_scale
            )
            probs = jnp.exp(logits - log_rows[:, :, None])
            probs_low = probs.astype(jnp.bfloat16)
            value_acc = value_acc + jnp.einsum(
                "hqk,qhd->khd", probs_low, grad_rows, preferred_element_type=jnp.float32
            )
            grad_probs = jnp.einsum(
                "qhd,khd->hqk", grad_rows, value_rows, preferred_element_type=jnp.float32
            )
            inner = jnp.sum(probs * grad_probs, axis=2, keepdims=True)
            grad_logits = (probs * (grad_probs - inner)).astype(jnp.bfloat16)
            grad_query = (
                jnp.einsum(
                    "hqk,khd->qhd", grad_logits, key_rows, preferred_element_type=jnp.float32
                )
                * score_scale
            )
            key_acc = (
                key_acc
                + jnp.einsum(
                    "hqk,qhd->khd", grad_logits, query_rows, preferred_element_type=jnp.float32
                )
                * score_scale
            )
            return ((key_acc, value_acc), grad_query.astype(jnp.bfloat16))

        empty = jnp.zeros((LEN, heads_here, HD), jnp.float32)
        (key_acc, value_acc), grad_query_rows = lax.scan(
            block_back, (empty, empty), (query_part, grad_part, log_part)
        )
        return (grad_query_rows, key_acc.astype(jnp.bfloat16), value_acc.astype(jnp.bfloat16))

    grad_queries_all, grad_keys_all, grad_values_all = lax.map(
        sequence_back, (query_blocks, grad_blocks, log_blocks, key_seq, value_seq)
    )
    grad_joint = jnp.concatenate(
        [
            grad_queries_all.reshape(group_rows, width),
            grad_keys_all.reshape(group_rows, width),
            grad_values_all.reshape(group_rows, width),
        ],
        axis=1,
    )
    joint_grad = contract_rows(gathered, grad_joint)
    query_weight_grad = joint_grad[:, :width]
    key_weight_grad = joint_grad[:, width : 2 * width]
    value_weight_grad = joint_grad[:, 2 * width :]
    query_bias_grad = jnp.sum(grad_joint[:, :width], axis=0, dtype=jnp.float32)
    value_bias_grad = jnp.sum(grad_joint[:, 2 * width :], axis=0, dtype=jnp.float32)
    tokens_grad = (
        grad_first
        + lax.psum_scatter(
            contract_cols(grad_joint, joint_weight).astype(jnp.bfloat16),
            "tensor",
            scatter_dimension=0,
            tiled=True,
        ).astype(jnp.float32)
    ).astype(jnp.bfloat16)
    (
        query_weight_grad,
        key_weight_grad,
        value_weight_grad,
        out_weight_grad,
        up_weight_grad,
        down_weight_grad,
    ) = (
        lax.psum_scatter(
            query_weight_grad.astype(jnp.bfloat16), "dp", scatter_dimension=0, tiled=True
        ).astype(jnp.float32),
        lax.psum_scatter(
            key_weight_grad.astype(jnp.bfloat16), "dp", scatter_dimension=0, tiled=True
        ).astype(jnp.float32),
        lax.psum_scatter(
            value_weight_grad.astype(jnp.bfloat16), "dp", scatter_dimension=0, tiled=True
        ).astype(jnp.float32),
        lax.psum_scatter(
            out_weight_grad.astype(jnp.bfloat16), "dp", scatter_dimension=1, tiled=True
        ).astype(jnp.float32),
        lax.psum_scatter(
            up_weight_grad.astype(jnp.bfloat16), "dp", scatter_dimension=0, tiled=True
        ).astype(jnp.float32),
        lax.psum_scatter(
            down_weight_grad.astype(jnp.bfloat16), "dp", scatter_dimension=1, tiled=True
        ).astype(jnp.float32),
    )
    tensor_place = lax.axis_index("tensor")
    model_width = out_bias.shape[0]
    query_spread = lax.dynamic_update_slice_in_dim(
        jnp.zeros((model_width,), jnp.float32), query_bias_grad, tensor_place * width, 0
    )
    value_spread = lax.dynamic_update_slice_in_dim(
        jnp.zeros((model_width,), jnp.float32), value_bias_grad, tensor_place * width, 0
    )
    up_spread = lax.dynamic_update_slice_in_dim(
        jnp.zeros((hidden_width * lax.axis_size("tensor"),), jnp.float32),
        up_bias_grad,
        tensor_place * hidden_width,
        0,
    )
    (
        query_spread,
        value_spread,
        up_spread,
        out_bias_grad,
        down_bias_grad,
        first_gain_grad,
        first_shift_grad,
        second_gain_grad,
        second_shift_grad,
    ) = lax.psum(
        (
            query_spread,
            value_spread,
            up_spread,
            out_bias_grad,
            down_bias_grad,
            first_gain_grad,
            first_shift_grad,
            second_gain_grad,
            second_shift_grad,
        ),
        ("dp", "tensor"),
    )
    query_bias_grad = lax.dynamic_slice_in_dim(query_spread, tensor_place * width, width, 0)
    value_bias_grad = lax.dynamic_slice_in_dim(value_spread, tensor_place * width, width, 0)
    up_bias_grad = lax.dynamic_slice_in_dim(up_spread, tensor_place * hidden_width, hidden_width, 0)
    factor = clip_limit / jnp.maximum(logit_peak, clip_limit)
    column_scale = jnp.repeat(jnp.sqrt(factor), HD)
    query_clipped = (query_weight.astype(jnp.float32) * column_scale).astype(jnp.bfloat16)
    query_bias_clipped = (query_bias.astype(jnp.float32) * column_scale).astype(jnp.bfloat16)
    key_clipped = (key_weight.astype(jnp.float32) * column_scale).astype(jnp.bfloat16)
    return (
        layer_out,
        tokens_grad,
        query_weight_grad,
        query_bias_grad,
        key_weight_grad,
        value_weight_grad,
        value_bias_grad,
        out_weight_grad,
        out_bias_grad,
        first_gain_grad,
        first_shift_grad,
        up_weight_grad,
        up_bias_grad,
        down_weight_grad,
        down_bias_grad,
        second_gain_grad,
        second_shift_grad,
        logit_peak,
        query_clipped,
        query_bias_clipped,
        key_clipped,
    )


LOG2E=1.4426950408889634
NT=(((1,),(1,)),((),()))
NN=(((1,),(0,)),((),()))
def dot(a,b,dims):
    return lax.dot_general(a,b,dims,preferred_element_type=jnp.float32)
def fwd_kernel(rb, qkv_ref, ctx_ref, lse_ref, peak_ref, vt_ref, ctxt_ref):
    rows=qkv_ref.shape[0]; width=qkv_ref.shape[1]//3; pairs=width//128
    lane=lax.broadcasted_iota(jnp.int32,(1,128),1)
    scale=jnp.bfloat16(HD**-0.5)
    @pl.loop(0,pairs)
    def _(p):
        cq=pl.multiple_of(p*128,128); ck=pl.multiple_of(width+p*128,128); cv=pl.multiple_of(2*width+p*128,128)
        vt_ref[...]=jnp.zeros_like(vt_ref)
        vT=qkv_ref[:,pl.ds(cv,128)].T
        vt_ref[0,0:64,:]=vT[0:64]; vt_ref[1,0:64,:]=vT[64:128]
        row=lax.broadcasted_iota(jnp.int32,(16,rows),0)
        ones=jnp.where(row==0,1.0,0.0).astype(jnp.bfloat16)
        vt_ref[0,64:80,:]=ones; vt_ref[1,64:80,:]=ones
        pks=[]
        for h in (0,1):
            keep=(lane<64) if h==0 else (lane>=64)
            pk=None
            for r in range(rows//rb):
                q=qkv_ref[r*rb:(r+1)*rb,pl.ds(cq,128)]*scale
                q=jnp.where(keep,q,jnp.bfloat16(0))
                st=dot(qkv_ref[:,pl.ds(ck,128)],q,NT)
                m=jnp.max(st,axis=0,keepdims=True)
                mc=m*LOG2E
                pt=jnp.exp2(st*LOG2E-mc).astype(jnp.bfloat16)
                ot=dot(vt_ref[h],pt,NN)
                tot=ot[64:65]
                ctxt_ref[h*64:(h+1)*64,r*rb:(r+1)*rb]=ot[0:64]*(1.0/tot)
                lse_ref[pl.ds(2*p+h,1),r*rb:(r+1)*rb]=mc+jnp.log2(tot)
                mm=jnp.max(m,axis=1,keepdims=True)
                pk=mm if pk is None else jnp.maximum(pk,mm)
            pks.append(pk)
        peak_ref[:,pl.ds(cq,128)]=jnp.where(lane<64,pks[0],pks[1])
        ctx_ref[:,pl.ds(cq,128)]=ctxt_ref[...].T.astype(jnp.bfloat16)
def attn_fwd(qkv,rb=256):
    rows=qkv.shape[0]; width=qkv.shape[1]//3; heads=width//HD
    V=pl.BlockSpec(memory_space=pltpu.VMEM)
    return pl.pallas_call(functools.partial(fwd_kernel,rb),
      out_shape=(jax.ShapeDtypeStruct((rows,width),jnp.bfloat16),jax.ShapeDtypeStruct((heads,rows),jnp.float32),jax.ShapeDtypeStruct((1,width),jnp.float32)),
      in_specs=[V],out_specs=(V,V,V),
      scratch_shapes=[pltpu.VMEM((2,80,rows),jnp.bfloat16),pltpu.VMEM((128,rows),jnp.float32)],
      compiler_params=pltpu.CompilerParams(vmem_limit_bytes=56*2**20),name="attn_fwd")(qkv)
def bwd_kernel(rb, qkv_ref, ctx_ref, dctx_ref, lse_ref, dqkv_ref, kt_ref, dqt_ref, dk_ref, dv_ref, dl_ref):
    rows=qkv_ref.shape[0]; width=qkv_ref.shape[1]//3; pairs=width//128
    lane=lax.broadcasted_iota(jnp.int32,(1,128),1)
    scale=jnp.bfloat16(HD**-0.5)
    zero=jnp.bfloat16(0)
    @pl.loop(0,pairs)
    def _(p):
        cq=pl.multiple_of(p*128,128); ck=pl.multiple_of(width+p*128,128); cv=pl.multiple_of(2*width+p*128,128)
        kt_ref[...]=qkv_ref[:,pl.ds(ck,128)].T
        prod=(ctx_ref[:,pl.ds(cq,128)].astype(jnp.float32)*dctx_ref[:,pl.ds(cq,128)].astype(jnp.float32)).T
        dl_ref[0:1]=jnp.sum(prod[0:64],axis=0,keepdims=True)
        dl_ref[1:2]=jnp.sum(prod[64:128],axis=0,keepdims=True)
        dk_ref[...]=jnp.zeros_like(dk_ref); dv_ref[...]=jnp.zeros_like(dv_ref)
        for r in range(rows//rb):
            rs=slice(r*rb,(r+1)*rb)
            for h in (0,1):
                keep=(lane<64) if h==0 else (lane>=64)
                q=jnp.where(keep,qkv_ref[rs,pl.ds(cq,128)]*scale,zero)
                do=jnp.where(keep,dctx_ref[rs,pl.ds(cq,128)],zero)
                st=dot(qkv_ref[:,pl.ds(ck,128)],q,NT)
                pt=jnp.exp2(st*LOG2E-lse_ref[pl.ds(2*p+h,1),rs])
                dpt=dot(qkv_ref[:,pl.ds(cv,128)],do,NT)
                ds=(pt*(dpt-dl_ref[h:h+1,rs])).astype(jnp.bfloat16)
                dv_ref[...]+=dot(pt.astype(jnp.bfloat16),do,NN)
                dk_ref[...]+=dot(ds,q,NN)
                dqt_ref[h*64:(h+1)*64,rs]=dot(kt_ref[h*64:(h+1)*64,:],ds,NN)
        dqkv_ref[:,pl.ds(cq,128)]=(dqt_ref[...].T*(HD**-0.5)).astype(jnp.bfloat16)
        dqkv_ref[:,pl.ds(ck,128)]=dk_ref[...].astype(jnp.bfloat16)
        dqkv_ref[:,pl.ds(cv,128)]=dv_ref[...].astype(jnp.bfloat16)
def attn_bwd(qkv,ctx,dctx,lse,rb=256):
    rows=qkv.shape[0]; width=qkv.shape[1]//3; heads=width//HD
    V=pl.BlockSpec(memory_space=pltpu.VMEM)
    return pl.pallas_call(functools.partial(bwd_kernel,rb),
      out_shape=jax.ShapeDtypeStruct((rows,3*width),jnp.bfloat16),
      in_specs=[V]*4,out_specs=V,
      scratch_shapes=[pltpu.VMEM((128,rows),jnp.bfloat16),pltpu.VMEM((128,rows),jnp.float32),pltpu.VMEM((rows,128),jnp.float32),pltpu.VMEM((rows,128),jnp.float32),pltpu.VMEM((8,rows),jnp.float32)],
      compiler_params=pltpu.CompilerParams(vmem_limit_bytes=56*2**20),name="attn_bwd")(qkv,ctx,dctx,lse)

MESH=pl.DeviceIdType.MESH
TN=(((0,),(0,)),((),()))
F32=jnp.float32; BF=jnp.bfloat16

def greet(partner):
    barrier=pltpu.get_barrier_semaphore()
    pl.semaphore_signal(barrier,inc=1,device_id=partner,device_id_type=MESH)
    pl.semaphore_wait(barrier,1)

def qkv_kernel(tok_ref,w_ref,bias_ref,qkv_ref,xall_ref,ssem,rsem):
    d=lax.axis_index("dp"); t=lax.axis_index("tensor")
    partner=(d,1-t)
    own=tok_ref.shape[0]
    greet(partner)
    mine=pl.ds(pl.multiple_of(t*own,own),own); other=pl.ds(pl.multiple_of((1-t)*own,own),own)
    copy=pltpu.make_async_remote_copy(tok_ref,xall_ref.at[mine],ssem,rsem,device_id=partner,device_id_type=MESH)
    copy.start()
    xall_ref[mine]=tok_ref[...]
    n=w_ref.shape[1]
    def rows(which):
        @pl.loop(0,n//256)
        def _(j):
            cs=pl.ds(pl.multiple_of(j*256,256),256)
            qkv_ref[which,cs]=(dot(xall_ref[which],w_ref[:,cs],NN)+bias_ref[:,cs]).astype(BF)
    rows(mine)
    copy.wait_recv()
    rows(other)
    copy.wait_send()

def qkv_call(tok,w,bias,cid):
    V=pl.BlockSpec(memory_space=pltpu.VMEM)
    rows=2*tok.shape[0]
    return pl.pallas_call(qkv_kernel,
      out_shape=(jax.ShapeDtypeStruct((rows,w.shape[1]),BF),jax.ShapeDtypeStruct((rows,tok.shape[1]),BF)),
      in_specs=[V]*3,out_specs=(V,V),scratch_shapes=[pltpu.SemaphoreType.DMA,pltpu.SemaphoreType.DMA],
      compiler_params=pltpu.CompilerParams(collective_id=cid,has_side_effects=True,vmem_limit_bytes=56*2**20),
      cost_estimate=pl.CostEstimate(flops=2*rows*w.shape[0]*w.shape[1],bytes_accessed=8*2**20,transcendentals=0),
      name="qkv")(tok,w,bias)

NC=4
def ffn_kernel(ctx,w_hbm,tok,cot,vec,upb,
               lo,gf,dctx,dw_hbm,vg,ubg,
               wo,wup,wdn,xh,hid,rst,hall,act,slp,ball,aall,part,sbuf,rbuf,tb,th,stage,
               wsem,osem,ssem,rsem):
    d=lax.axis_index("dp"); t=lax.axis_index("tensor")
    partner=(d,1-t)
    own=tok.shape[0]; cr=own//NC; width=ctx.shape[1]; ff=wup.shape[1]; dm=tok.shape[1]
    cws=[pltpu.make_async_copy(w_hbm.at[:,0:width],wo,wsem.at[0]),
         pltpu.make_async_copy(w_hbm.at[:,width:width+ff],wup,wsem.at[1]),
         pltpu.make_async_copy(w_hbm.at[:,width+ff:width+2*ff],wdn,wsem.at[2])]
    for c in cws: c.start()
    greet(partner)
    def rows(rank,c): return pl.ds(pl.multiple_of(rank*own+c*cr,cr),cr)
    def loc(c): return pl.ds(pl.multiple_of(c*cr,cr),cr)
    def rs_copy(k,c):
        return pltpu.make_async_remote_copy(sbuf.at[k,loc(c)],rbuf.at[k,loc(c)],ssem.at[k,c],rsem.at[k,c],device_id=partner,device_id_type=MESH)
    def ag_copy(k,buf,c,rank):
        return pltpu.make_async_remote_copy(buf.at[rows(rank,c)],buf.at[rows(rank,c)],ssem.at[k,c],rsem.at[k,c],device_id=partner,device_id_type=MESH)
    vg[...]=jnp.zeros_like(vg); ubg[...]=jnp.zeros_like(ubg)
    cws[0].wait()
    @pl.loop(0,NC)
    def _(c):
        sbuf[0,loc(c)]=dot(ctx[rows(1-t,c)],wo[...],NT).astype(BF)
        rs_copy(0,c).start()
        part[loc(c)]=dot(ctx[rows(t,c)],wo[...],NT)
    @pl.loop(0,NC)
    def _(c):
        rs_copy(0,c).wait_recv()
        v=tok[loc(c)].astype(F32)+part[loc(c)]+rbuf[0,loc(c)].astype(F32)+vec[0:1]
        cen=v-jnp.mean(v,axis=1,keepdims=True)
        r=lax.rsqrt(jnp.mean(cen*cen,axis=1,keepdims=True)+EPSILON)
        x=cen*r
        h=x*vec[1:2]+vec[2:3]
        xh[loc(c)]=x; hid[loc(c)]=h
        rst[loc(c)]=jnp.broadcast_to(r,(cr,128))
        hall[rows(t,c)]=h.astype(BF)
        ag_copy(3,hall,c,t).start()
    cws[1].wait(); cws[2].wait()
    TF=512
    @pl.loop(0,NC)
    def _(c):
        ag_copy(3,hall,c,1-t).wait_recv()
        for who in (0,1):
            rr=rows(1-t if who==0 else t,c)
            @pl.loop(0,ff//TF)
            def _(j):
                cs=pl.ds(pl.multiple_of(j*TF,TF),TF)
                u=dot(hall[rr],wup[:,cs],NN)+upb[:,cs]
                cdf=0.5*(1.0+lax.erf(u*0.5**0.5))
                act[rr,cs]=(u*cdf).astype(BF)
                slp[rr,cs]=(cdf+u*jnp.exp(-0.5*u*u)*(0.5/math.pi)**0.5).astype(BF)
            p=dot(act[rr],wdn[...],NT)
            if who==0:
                sbuf[1,loc(c)]=p.astype(BF)
                rs_copy(1,c).start()
            else:
                part[loc(c)]=p
    @pl.loop(0,NC)
    def _(c):
        rs_copy(1,c).wait_recv()
        v=hid[loc(c)]+part[loc(c)]+rbuf[1,loc(c)].astype(F32)+vec[3:4]
        cen=v-jnp.mean(v,axis=1,keepdims=True)
        r=lax.rsqrt(jnp.mean(cen*cen,axis=1,keepdims=True)+EPSILON)
        x=cen*r
        lo[loc(c)]=(x*vec[4:5]+vec[5:6]).astype(BF)
        dy=cot[loc(c)].astype(F32)
        vg[4:5]+=jnp.sum(dy*x,axis=0,keepdims=True)
        vg[5:6]+=jnp.sum(dy,axis=0,keepdims=True)
        dx=dy*vec[4:5]
        g=r*(dx-jnp.mean(dx,axis=1,keepdims=True)-x*jnp.mean(dx*x,axis=1,keepdims=True))
        gf[loc(c)]=g
        gb=g.astype(BF)
        vg[3:4]+=jnp.sum(gb.astype(F32),axis=0,keepdims=True)
        ball[rows(t,c)]=gb
        ag_copy(4,ball,c,t).start()
        th[:,pl.ds(pl.multiple_of(c*256,256),256)]=hall[pl.ds(pl.multiple_of(c*256,256),256)].T
    @pl.loop(0,NC)
    def _(c):
        ag_copy(4,ball,c,1-t).wait_recv()
        for who in (0,1):
            rr=rows(1-t if who==0 else t,c)
            @pl.loop(0,ff//TF)
            def _(j):
                cs=pl.ds(pl.multiple_of(j*TF,TF),TF)
                gu=(dot(ball[rr],wdn[:,cs],NN)*slp[rr,cs].astype(F32)).astype(BF)
                slp[rr,cs]=gu
                ubg[0:1,cs]+=jnp.sum(gu.astype(F32),axis=0,keepdims=True)
            p=dot(slp[rr],wup[...],NT)
            if who==0:
                sbuf[2,loc(c)]=p.astype(BF)
                rs_copy(2,c).start()
            else:
                part[loc(c)]=p
    def out_copy(slot,col):
        return pltpu.make_async_copy(stage.at[slot],dw_hbm.at[:,pl.ds(pl.multiple_of(col,512),512)],osem.at[slot])
    def wgrad(slot,left,right_ref,rcol,ocol):
        @pl.loop(0,dm//256)
        def _(i):
            ms=pl.ds(pl.multiple_of(i*256,256),256)
            stage[slot,ms]=dot(left[ms],right_ref[:,pl.ds(pl.multiple_of(rcol,512),512)],NN).astype(BF)
        out_copy(slot,ocol).start()
    nt=ff//512
    @pl.loop(0,NC)
    def _(c):
        tb[:,pl.ds(pl.multiple_of(c*256,256),256)]=ball[pl.ds(pl.multiple_of(c*256,256),256)].T
        rs_copy(2,c).wait_recv()
        dy=gf[loc(c)]+part[loc(c)]+rbuf[2,loc(c)].astype(F32)
        x=xh[loc(c)]; r=rst[loc(c)][:,0:1]
        vg[1:2]+=jnp.sum(dy*x,axis=0,keepdims=True)
        vg[2:3]+=jnp.sum(dy,axis=0,keepdims=True)
        dx=dy*vec[1:2]
        g=r*(dx-jnp.mean(dx,axis=1,keepdims=True)-x*jnp.mean(dx*x,axis=1,keepdims=True))
        gf[loc(c)]=g
        gb=g.astype(BF)
        vg[0:1]+=jnp.sum(gb.astype(F32),axis=0,keepdims=True)
        aall[rows(t,c)]=gb
        ag_copy(5,aall,c,t).start()
    @pl.loop(0,NC)
    def _(c):
        slot=c%2
        @pl.when(c>=2)
        def _(): out_copy(slot,0).wait()
        wgrad(slot,th,slp,c*512,width+c*512)
        ag_copy(5,aall,c,1-t).wait_recv()
        for who in (0,1):
            rr=rows(1-t if who==0 else t,c)
            dctx[rr]=dot(aall[rr],wo[...],NN).astype(BF)
    @pl.loop(0,nt)
    def _(c):
        slot=c%2
        out_copy(slot,0).wait()
        wgrad(slot,tb,act,c*512,width+ff+c*512)
    @pl.loop(0,NC)
    def _(c):
        tb[:,pl.ds(pl.multiple_of(c*256,256),256)]=aall[pl.ds(pl.multiple_of(c*256,256),256)].T
    out_copy(0,0).wait()
    wgrad(0,tb,ctx,0,0)
    out_copy(1,0).wait()
    out_copy(0,0).wait()
    for k in range(3):
        @pl.loop(0,NC)
        def _(c): rs_copy(k,c).wait_send()
    for k,buf in ((3,hall),(4,ball),(5,aall)):
        @pl.loop(0,NC)
        def _(c): ag_copy(k,buf,c,t).wait_send()

def ffn_call(ctx,w,tok,cot,vec,upb,cid):
    V=pl.BlockSpec(memory_space=pltpu.VMEM); A=pl.BlockSpec(memory_space=pl.ANY)
    rows,width=ctx.shape; own,dm=tok.shape; ff=upb.shape[1]
    S=jax.ShapeDtypeStruct
    return pl.pallas_call(ffn_kernel,
      out_shape=(S((own,dm),BF),S((own,dm),F32),S((rows,width),BF),S((dm,width+2*ff),BF),S((8,dm),F32),S((8,ff),F32)),
      in_specs=[V,A,V,V,V,V],out_specs=(V,V,V,A,V,V),
      scratch_shapes=[pltpu.VMEM((dm,width),BF),pltpu.VMEM((dm,ff),BF),pltpu.VMEM((dm,ff),BF),
        pltpu.VMEM((own,dm),F32),pltpu.VMEM((own,dm),F32),pltpu.VMEM((own,128),F32),
        pltpu.VMEM((rows,dm),BF),pltpu.VMEM((rows,ff),BF),pltpu.VMEM((rows,ff),BF),pltpu.VMEM((rows,dm),BF),pltpu.VMEM((rows,dm),BF),
        pltpu.VMEM((own,dm),F32),pltpu.VMEM((3,own,dm),BF),pltpu.VMEM((3,own,dm),BF),
        pltpu.VMEM((dm,rows),BF),pltpu.VMEM((dm,rows),BF),pltpu.VMEM((2,dm,512),BF),
        pltpu.SemaphoreType.DMA((3,)),pltpu.SemaphoreType.DMA((2,)),pltpu.SemaphoreType.DMA((6,NC)),pltpu.SemaphoreType.DMA((6,NC))],
      compiler_params=pltpu.CompilerParams(collective_id=cid,has_side_effects=True,vmem_limit_bytes=60*2**20),
      cost_estimate=pl.CostEstimate(flops=2*rows*dm*(6*ff+3*width),bytes_accessed=40*2**20,transcendentals=2*rows*ff),
      name="ffn")(ctx,w,tok,cot,vec,upb)


def back_kernel(qkv_ref,ctx_ref,dctx_ref,lse_ref,dw_hbm,w_hbm,x_hbm,gf,early,wqk,bq,lim,
                tg,gq,gk,gv,go,gu,gd,sums,late,qc,kc,qbc,
                kt_ref,dqt_ref,dk_ref,dv_ref,dl_ref,dqkv_ref,
                xv,xt,wv,part,dwh,ysb,yrb,
                o1,r1,s2,r2,s3,r3,eb,er,lb,lr,
                lsem,s1s,s1r,s2s,s2r,s3s,s3r,ysend,yrecv,es,erc,ls,lrc):
    d=lax.axis_index("dp"); t=lax.axis_index("tensor")
    core=d%2; x=(d//2)%2; z=d//4
    def dev(z_,x_,c_): return ((z_*2+x_)*2+c_,t)
    sib=dev(z,x,1-core); xp=dev(z,1-x,core); yp=(d,1-t)
    zp=[dev((z+k)%4,x,core) for k in (1,2,3)]
    zb=[dev(z+1-2*(z%2),x,core),dev((z+2)%4,x,core)]
    barrier=pltpu.get_barrier_semaphore()
    everyone=[sib,xp,yp]+zp
    for p in everyone: pl.semaphore_signal(barrier,inc=1,device_id=p,device_id_type=MESH)
    rows=qkv_ref.shape[0]; width=qkv_ref.shape[1]//3; pairs=width//128
    own,dm=gf.shape; n=3*width; half=own//2
    def remote(src,dst,a,b,p): return pltpu.make_async_remote_copy(src,dst,a,b,device_id=p,device_id_type=MESH)
    loads=[pltpu.make_async_copy(w_hbm,wv,lsem.at[0]),pltpu.make_async_copy(x_hbm,xv,lsem.at[1])]
    own_loads=[pltpu.make_async_copy(dw_hbm.at[:,core,:,g*n:(g+1)*n],o1.at[g],lsem.at[2+g]) for g in range(3)]
    for c in own_loads+loads: c.start()
    eb[0]=early[...]
    pl.semaphore_wait(barrier,len(everyone))
    def s1(g):
        src=dw_hbm.at[:,1-core,:,g*n:(g+1)*n] if g<3 else dwh.at[:,1-core]
        return remote(src,r1.at[g],s1s.at[g],s1r.at[g],sib)
    def s2c(g): return remote(s2.at[g],r2.at[g],s2s.at[g],s2r.at[g],xp)
    def s3c(g,k): return remote(s3.at[g,(z+k)%4],r3.at[g,3-k],s3s.at[g,k-1],s3r.at[g,k-1],zp[k-1])
    for g in range(3): s1(g).start()
    f32=lambda a:a.astype(F32)
    def mine(g,k):
        return f32(o1[g,k] if g<3 else dwh[k,core])+f32(r1[g,k])
    def step2(g):
        s1(g).wait_recv()
        if g<3: own_loads[g].wait()
        @pl.loop(0,4)
        def _(i): s2[g,i]=mine(g,2*i+1-x).astype(BF)
        s2c(g).start()
    def step3(g):
        s2c(g).wait_recv()
        @pl.loop(0,4)
        def _(i): s3[g,i]=(mine(g,2*i+x)+f32(r2[g,i])).astype(BF)
        for k in (1,2,3): s3c(g,k).start()
    def step4(g):
        for k in (1,2,3): s3c(g,k).wait_recv()
        v=mine(g,2*z+x)+f32(r2[g,z])
        return v+f32(r3[g,0])+f32(r3[g,1])+f32(r3[g,2])
    hops=[sib,xp,zb[0],zb[1],yp]
    def ecopy(i):
        return remote(eb.at[i],er.at[i],es.at[i],erc.at[i],hops[i])
    def eadd(i):
        ecopy(i).wait_recv()
        nr=8 if i==4 else 16
        a=eb[i,0:8]+er[i,0:8]
        b=eb[i,8:16]; c=er[i,8:16]
        if i<4:
            r=lax.broadcasted_iota(jnp.int32,b.shape,0)
            b=jnp.where(r==2,jnp.maximum(b,c),b+c)
        eb[i+1,0:8]=a; eb[i+1,8:16]=b
    def lcopy(i): return remote(lb.at[i],lr.at[i],ls.at[i],lrc.at[i],hops[i])
    def ladd(i):
        lcopy(i).wait_recv()
        lb[i+1]=lb[i]+lr[i]
    ecopy(0).start()
    lane=lax.broadcasted_iota(jnp.int32,(1,128),1)
    scale=jnp.bfloat16(HD**-0.5)
    zero=jnp.bfloat16(0)
    rb=256
    @pl.loop(0,pairs)
    def _(p):
        cq=pl.multiple_of(p*128,128); ck=pl.multiple_of(width+p*128,128); cv=pl.multiple_of(2*width+p*128,128)
        kt_ref[...]=qkv_ref[:,pl.ds(ck,128)].T
        prod=(ctx_ref[:,pl.ds(cq,128)].astype(F32)*dctx_ref[:,pl.ds(cq,128)].astype(F32)).T
        dl_ref[0:1]=jnp.sum(prod[0:64],axis=0,keepdims=True)
        dl_ref[1:2]=jnp.sum(prod[64:128],axis=0,keepdims=True)
        dk_ref[...]=jnp.zeros_like(dk_ref); dv_ref[...]=jnp.zeros_like(dv_ref)
        @pl.loop(0,rows//rb)
        def _(r):
            rs=pl.ds(pl.multiple_of(r*rb,rb),rb)
            for h in (0,1):
                keep=(lane<64) if h==0 else (lane>=64)
                q=jnp.where(keep,qkv_ref[rs,pl.ds(cq,128)]*scale,zero)
                do=jnp.where(keep,dctx_ref[rs,pl.ds(cq,128)],zero)
                st=dot(qkv_ref[:,pl.ds(ck,128)],q,NT)
                pt=jnp.exp2(st*LOG2E-lse_ref[pl.ds(2*p+h,1),rs])
                dpt=dot(qkv_ref[:,pl.ds(cv,128)],do,NT)
                ds=(pt*(dpt-dl_ref[h:h+1,rs])).astype(BF)
                dv_ref[...]+=dot(pt.astype(BF),do,NN)
                dk_ref[...]+=dot(ds,q,NN)
                dqt_ref[h*64:(h+1)*64,rs]=dot(kt_ref[h*64:(h+1)*64,:],ds,NN)
        dqkv_ref[:,pl.ds(cq,128)]=(dqt_ref[...].T*(HD**-0.5)).astype(BF)
        dqkv_ref[:,pl.ds(ck,128)]=dk_ref[...].astype(BF)
        dqkv_ref[:,pl.ds(cv,128)]=dv_ref[...].astype(BF)
        @pl.when(p==0)
        def _():
            step2(0); step2(1); step2(2)
            eadd(0); ecopy(1).start()
        @pl.when(p==1)
        def _():
            eadd(1); ecopy(2).start()
        @pl.when(p==2)
        def _():
            step3(0)
            eadd(2); ecopy(3).start()
    loads[0].wait()
    def rr(rank,c): return pl.ds(pl.multiple_of(rank*own+c*half,half),half)
    def ycopy(c): return remote(ysb.at[c],yrb.at[c],ysend.at[c],yrecv.at[c],yp)
    for c in (0,1):
        ysb[c]=dot(dqkv_ref[rr(1-t,c)],wv[...],NT).astype(BF)
        ycopy(c).start()
    lb[0]=jnp.zeros_like(lb[0])
    lb[0,0:1,0:width]=jnp.sum(f32(dqkv_ref[:,0:width]),axis=0,keepdims=True)
    lb[0,0:1,width:2*width]=jnp.sum(f32(dqkv_ref[:,2*width:]),axis=0,keepdims=True)
    lcopy(0).start()
    loads[1].wait()
    @pl.loop(0,rows//256)
    def _(c):
        cs=pl.ds(pl.multiple_of(c*256,256),256)
        xt[:,cs]=xv[cs].T
    @pl.loop(0,dm//128)
    def _(i):
        ms=pl.ds(pl.multiple_of(i*128,128),128)
        for j in range(n//512):
            v=dot(xt[ms],dqkv_ref[:,j*512:(j+1)*512],NN).astype(BF)
            dwh[i,0,:,j*512:(j+1)*512]=v[0:64]
            dwh[i,1,:,j*512:(j+1)*512]=v[64:128]
    s1(3).start()
    eadd(3); ecopy(4).start()
    ladd(0); lcopy(1).start()
    step3(1)
    step2(3)
    ladd(1); lcopy(2).start()
    for c in (0,1):
        part[c]=dot(dqkv_ref[rr(t,c)],wv[...],NT)
    ladd(2); lcopy(3).start()
    v=step4(0)
    go[...]=v[:,0:512].T
    gu[:,0:1024]=v[:,512:1536]
    eadd(4)
    sums[...]=eb[5]
    pk=eb[4,10:11,0:width]
    sc=jnp.sqrt(lim[...]/jnp.maximum(pk,lim[...]))
    qc[...]=(f32(wqk[0])*sc).astype(BF); kc[...]=(f32(wqk[1])*sc).astype(BF)
    qbc[...]=(bq[...]*sc).astype(BF)
    step3(2)
    ladd(3)
    late[...]=lb[4]
    v=step4(1)
    gu[:,1024:2048]=v[:,0:1024]
    gd[0:512]=v[:,1024:1536].T
    for c in (0,1):
        ycopy(c).wait_recv()
        lo_=slice(c*half,(c+1)*half)
        tg[lo_]=(gf[lo_]+part[c]+f32(yrb[c])).astype(BF)
    step3(3)
    v=step4(2)
    gd[512:2048]=v.T
    v=step4(3)
    gq[...]=v[:,0:width]; gk[...]=v[:,width:2*width]; gv[...]=v[:,2*width:]
    for g in range(4):
        s1(g).wait_send(); s2c(g).wait_send()
        for k in (1,2,3): s3c(g,k).wait_send()
    for i in range(5): ecopy(i).wait_send()
    for i in range(4): lcopy(i).wait_send()
    for c in (0,1): ycopy(c).wait_send()

def back_call(qkv,ctx,dctx,lse,dw,w,xall,gf,early,wqk,bq,lim,cid):
    V=pl.BlockSpec(memory_space=pltpu.VMEM); A=pl.BlockSpec(memory_space=pl.ANY)
    S=jax.ShapeDtypeStruct
    own,dm=gf.shape; rows,n=qkv.shape; width=n//3; half=own//2
    nr=dw.shape[1]; ff=(nr-width)//2
    dw4=dw.reshape(8,2,64,nr)
    D=pltpu.SemaphoreType.DMA; M=pltpu.VMEM
    return pl.pallas_call(back_kernel,
      out_shape=(S((own,dm),BF),S((64,width),F32),S((64,width),F32),S((64,width),F32),S((width,64),F32),S((64,ff),F32),S((ff,64),F32),
                 S((16,1024),F32),S((8,1024),F32),S((64,width),BF),S((64,width),BF),S((1,width),BF)),
      in_specs=[V]*4+[A]*3+[V]*5,out_specs=(V,)*12,
      scratch_shapes=[M((128,rows),BF),M((128,rows),F32),M((rows,128),F32),M((rows,128),F32),M((8,rows),F32),M((rows,n),BF),
        M((rows,dm),BF),M((dm,rows),BF),M((dm,n),BF),M((2,half,dm),F32),M((8,2,64,n),BF),M((2,half,dm),BF),M((2,half,dm),BF),
        M((3,8,64,n),BF),M((4,8,64,n),BF),M((4,4,64,n),BF),M((4,4,64,n),BF),M((4,4,64,n),BF),M((4,3,64,n),BF),
        M((6,16,1024),F32),M((5,16,1024),F32),M((5,8,1024),F32),M((4,8,1024),F32),
        D((5,)),D((4,)),D((4,)),D((4,)),D((4,)),D((4,3)),D((4,3)),D((2,)),D((2,)),D((5,)),D((5,)),D((4,)),D((4,))],
      compiler_params=pltpu.CompilerParams(collective_id=cid,has_side_effects=True,vmem_limit_bytes=61*2**20),
      name="back")(qkv,ctx,dctx,lse,dw4,w,xall,gf,early,wqk,bq,lim)

def per_device_pair(tokens,query_weight,query_bias,key_weight,value_weight,value_bias,out_weight,out_bias,first_gain,first_shift,
    up_weight,up_bias,down_weight,down_bias,second_gain,second_shift,cotangent,clip_limit):
    width=query_weight.shape[1]; ff=up_weight.shape[1]; dm=tokens.shape[1]
    f=lambda a:a.astype(F32)
    head_shard=jnp.concatenate([query_weight,key_weight,value_weight],axis=1)
    rest_shard=jnp.concatenate([out_weight.T,up_weight,down_weight.T],axis=1)
    head_w=lax.all_gather(head_shard,"dp",axis=0,tiled=True)
    rest_shard,_=lax.optimization_barrier((rest_shard,head_w))
    rest_w=lax.all_gather(rest_shard,"dp",axis=0,tiled=True)
    bias=jnp.concatenate([f(query_bias),jnp.zeros((width,),F32),f(value_bias)])[None]
    qkv,xall=qkv_call(tokens,head_w,bias,0)
    ctx,lse,peak=attn_fwd(qkv,512)
    z=jnp.zeros((dm,),F32)
    vec=jnp.stack([f(out_bias),f(first_gain),f(first_shift),f(down_bias),f(second_gain),f(second_shift),z,z])
    lo,gf,dctx,dw,vg,ubg=ffn_call(ctx,rest_w,tokens,cotangent,vec,f(up_bias)[None],1)
    early=jnp.concatenate([vg,ubg[0].reshape(2,dm),jnp.pad(peak,((0,0),(0,dm-width))),jnp.zeros((5,dm),F32)])
    wqk=jnp.stack([query_weight,key_weight])
    lim=jnp.repeat(clip_limit,HD)[None]
    tg,gq,gk,gv,go,gu,gd,sums,late,qc,kc,qbc=back_call(qkv,ctx,dctx,lse,dw,head_w,xall,gf,early,wqk,f(query_bias)[None],lim,2)
    return (lo,tg,gq,late[0,:width],gk,gv,late[0,width:2*width],go,sums[0],sums[1],sums[2],gu,sums[8:10].reshape(ff),gd,
      sums[3],sums[4],sums[5],sums[10,:width:HD],qc,qbc[0],kc)


def layer(*args):
    paired = lax.axis_size("dp") == 16 and lax.axis_size("tensor") == 2 and 2 * args[0].shape[0] == LEN
    return per_device_pair(*args) if paired else per_device(*args)


def solution(mesh):
    in_specs = (
        P(("dp", "tensor"), None),
        P("dp", "tensor"),
        P("tensor"),
        P("dp", "tensor"),
        P("dp", "tensor"),
        P("tensor"),
        P("tensor", "dp"),
        P(),
        P(),
        P(),
        P("dp", "tensor"),
        P("tensor"),
        P("tensor", "dp"),
        P(),
        P(),
        P(),
        P(("dp", "tensor"), None),
        P("tensor"),
    )
    out_specs = (
        P(("dp", "tensor"), None),
        P(("dp", "tensor"), None),
        P("dp", "tensor"),
        P("tensor"),
        P("dp", "tensor"),
        P("dp", "tensor"),
        P("tensor"),
        P("tensor", "dp"),
        P(),
        P(),
        P(),
        P("dp", "tensor"),
        P("tensor"),
        P("tensor", "dp"),
        P(),
        P(),
        P(),
        P("tensor"),
        P("dp", "tensor"),
        P("tensor"),
        P("dp", "tensor"),
    )
    return jax.shard_map(
        layer, mesh=mesh, in_specs=in_specs, out_specs=out_specs, check_vma=False
    )
```

```python
import functools
import math

import jax
import jax.numpy as jnp
from jax import lax
from jax.experimental import pallas as pl
from jax.experimental.pallas import tpu as pltpu
from jax.sharding import PartitionSpec as P

HD = 64
LEN = 1024
QB = 512


def layer_norm(values, gain, shift):
    center = values - jnp.mean(values, axis=-1, keepdims=True)
    spread = jnp.mean(center * center, axis=-1, keepdims=True)
    return center * lax.rsqrt(spread + EPSILON) * gain + shift


def gelu_slope(upper):
    normal_cdf = 0.5 * (1.0 + lax.erf(upper * 0.5**0.5))
    return normal_cdf + upper * jnp.exp(-0.5 * upper * upper) * (0.5 / math.pi) ** 0.5


def contract_rows(left, right):
    return lax.dot_general(
        left, right, (((0,), (0,)), ((), ())), preferred_element_type=jnp.float32
    )


def contract_cols(left, right):
    return lax.dot_general(
        left, right, (((1,), (1,)), ((), ())), preferred_element_type=jnp.float32
    )


def per_device(
    tokens,
    query_weight,
    query_bias,
    key_weight,
    value_weight,
    value_bias,
    out_weight,
    out_bias,
    first_gain,
    first_shift,
    up_weight,
    up_bias,
    down_weight,
    down_bias,
    second_gain,
    second_shift,
    cotangent,
    clip_limit,
):
    query_full, key_full, value_full, out_full, up_full, down_full = (
        lax.all_gather(query_weight, "dp", axis=0, tiled=True),
        lax.all_gather(key_weight, "dp", axis=0, tiled=True),
        lax.all_gather(value_weight, "dp", axis=0, tiled=True),
        lax.all_gather(out_weight, "dp", axis=1, tiled=True),
        lax.all_gather(up_weight, "dp", axis=0, tiled=True),
        lax.all_gather(down_weight, "dp", axis=1, tiled=True),
    )
    width = query_full.shape[1]
    hidden_width = up_full.shape[1]
    heads_here = width // HD
    score_scale = HD ** (-0.5)
    joint_weight = jnp.concatenate([query_full, key_full, value_full], axis=1)
    gathered = lax.all_gather(tokens, "tensor", axis=0, tiled=True)
    group_rows = gathered.shape[0]
    seq_count = group_rows // LEN
    block_count = LEN // QB
    projected = jnp.dot(gathered, joint_weight, preferred_element_type=jnp.float32)
    queries = (projected[:, :width] + query_bias.astype(jnp.float32)).astype(jnp.bfloat16)
    keyset = projected[:, width : 2 * width].astype(jnp.bfloat16)
    valset = (projected[:, 2 * width :] + value_bias.astype(jnp.float32)).astype(jnp.bfloat16)
    query_seq = queries.reshape(seq_count, LEN, heads_here, HD)
    key_seq = keyset.reshape(seq_count, LEN, heads_here, HD)
    value_seq = valset.reshape(seq_count, LEN, heads_here, HD)

    def attend_block(block_id):
        seq_id = block_id // block_count
        row_start = block_id % block_count * QB
        query_rows = lax.dynamic_slice_in_dim(
            lax.dynamic_index_in_dim(query_seq, seq_id, 0, False), row_start, QB, 0
        )
        key_rows = lax.dynamic_index_in_dim(key_seq, seq_id, 0, False)
        value_rows = lax.dynamic_index_in_dim(value_seq, seq_id, 0, False)
        logits = (
            jnp.einsum("qhd,khd->hqk", query_rows, key_rows, preferred_element_type=jnp.float32)
            * score_scale
        )
        row_max = jnp.max(logits, axis=2, keepdims=True)
        exponent = jnp.exp(logits - row_max)
        totals = jnp.sum(exponent, axis=2, keepdims=True)
        probs_low = (exponent / totals).astype(jnp.bfloat16)
        context_rows = jnp.einsum(
            "hqk,khd->qhd", probs_low, value_rows, preferred_element_type=jnp.float32
        )
        return (
            context_rows.reshape(QB, width).astype(jnp.bfloat16),
            (row_max + jnp.log(totals))[:, :, 0],
            jnp.max(row_max, axis=(1, 2)),
        )

    context_blocks, log_totals, block_peaks = lax.map(
        attend_block, jnp.arange(seq_count * block_count)
    )
    context = context_blocks.reshape(group_rows, width)
    logit_peak = lax.pmax(jnp.max(block_peaks, axis=0), "dp")
    attention = lax.psum_scatter(
        jnp.dot(context, out_full, preferred_element_type=jnp.float32).astype(jnp.bfloat16),
        "tensor",
        scatter_dimension=0,
        tiled=True,
    ).astype(jnp.float32) + out_bias.astype(jnp.float32)
    first_resid = tokens.astype(jnp.float32) + attention
    hidden, first_pull = jax.vjp(
        layer_norm, first_resid, first_gain.astype(jnp.float32), first_shift.astype(jnp.float32)
    )
    hidden_all = lax.all_gather(hidden.astype(jnp.bfloat16), "tensor", axis=0, tiled=True)
    upper = jnp.dot(hidden_all, up_full, preferred_element_type=jnp.float32) + up_bias.astype(
        jnp.float32
    )
    acted = jax.nn.gelu(upper, approximate=False).astype(jnp.bfloat16)
    branch = lax.psum_scatter(
        jnp.dot(acted, down_full, preferred_element_type=jnp.float32).astype(jnp.bfloat16),
        "tensor",
        scatter_dimension=0,
        tiled=True,
    ).astype(jnp.float32) + down_bias.astype(jnp.float32)
    normed, second_pull = jax.vjp(
        layer_norm,
        hidden + branch,
        second_gain.astype(jnp.float32),
        second_shift.astype(jnp.float32),
    )
    layer_out = normed.astype(jnp.bfloat16)
    grad_second, second_gain_grad, second_shift_grad = second_pull(cotangent.astype(jnp.float32))
    grad_branch = grad_second.astype(jnp.bfloat16)
    down_bias_grad = jnp.sum(grad_branch, axis=0, dtype=jnp.float32)
    branch_all = lax.all_gather(grad_branch, "tensor", axis=0, tiled=True)
    grad_acted = contract_cols(branch_all, down_full)
    down_weight_grad = contract_rows(acted, branch_all)
    grad_upper = (grad_acted * gelu_slope(upper)).astype(jnp.bfloat16)
    up_bias_grad = jnp.sum(grad_upper, axis=0, dtype=jnp.float32)
    up_weight_grad = contract_rows(hidden_all, grad_upper)
    grad_hidden = grad_second + lax.psum_scatter(
        contract_cols(grad_upper, up_full).astype(jnp.bfloat16),
        "tensor",
        scatter_dimension=0,
        tiled=True,
    ).astype(jnp.float32)
    grad_first, first_gain_grad, first_shift_grad = first_pull(grad_hidden)
    grad_attn = grad_first.astype(jnp.bfloat16)
    out_bias_grad = jnp.sum(grad_attn, axis=0, dtype=jnp.float32)
    attn_all = lax.all_gather(grad_attn, "tensor", axis=0, tiled=True)
    grad_context = contract_cols(attn_all, out_full).astype(jnp.bfloat16)
    out_weight_grad = contract_rows(context, attn_all)
    query_blocks = queries.reshape(seq_count, block_count, QB, heads_here, HD)
    grad_blocks = grad_context.reshape(seq_count, block_count, QB, heads_here, HD)
    log_blocks = log_totals.reshape(seq_count, block_count, heads_here, QB)

    def sequence_back(item):
        query_part, grad_part, log_part, key_rows, value_rows = item

        def block_back(carry, piece):
            key_acc, value_acc = carry
            query_rows, grad_rows, log_rows = piece
            logits = (
                jnp.einsum("qhd,khd->hqk", query_rows, key_rows, preferred_element_type=jnp.float32)
                * score_scale
            )
            probs = jnp.exp(logits - log_rows[:, :, None])
            probs_low = probs.astype(jnp.bfloat16)
            value_acc = value_acc + jnp.einsum(
                "hqk,qhd->khd", probs_low, grad_rows, preferred_element_type=jnp.float32
            )
            grad_probs = jnp.einsum(
                "qhd,khd->hqk", grad_rows, value_rows, preferred_element_type=jnp.float32
            )
            inner = jnp.sum(probs * grad_probs, axis=2, keepdims=True)
            grad_logits = (probs * (grad_probs - inner)).astype(jnp.bfloat16)
            grad_query = (
                jnp.einsum(
                    "hqk,khd->qhd", grad_logits, key_rows, preferred_element_type=jnp.float32
                )
                * score_scale
            )
            key_acc = (
                key_acc
                + jnp.einsum(
                    "hqk,qhd->khd", grad_logits, query_rows, preferred_element_type=jnp.float32
                )
                * score_scale
            )
            return ((key_acc, value_acc), grad_query.astype(jnp.bfloat16))

        empty = jnp.zeros((LEN, heads_here, HD), jnp.float32)
        (key_acc, value_acc), grad_query_rows = lax.scan(
            block_back, (empty, empty), (query_part, grad_part, log_part)
        )
        return (grad_query_rows, key_acc.astype(jnp.bfloat16), value_acc.astype(jnp.bfloat16))

    grad_queries_all, grad_keys_all, grad_values_all = lax.map(
        sequence_back, (query_blocks, grad_blocks, log_blocks, key_seq, value_seq)
    )
    grad_joint = jnp.concatenate(
        [
            grad_queries_all.reshape(group_rows, width),
            grad_keys_all.reshape(group_rows, width),
            grad_values_all.reshape(group_rows, width),
        ],
        axis=1,
    )
    joint_grad = contract_rows(gathered, grad_joint)
    query_weight_grad = joint_grad[:, :width]
    key_weight_grad = joint_grad[:, width : 2 * width]
    value_weight_grad = joint_grad[:, 2 * width :]
    query_bias_grad = jnp.sum(grad_joint[:, :width], axis=0, dtype=jnp.float32)
    value_bias_grad = jnp.sum(grad_joint[:, 2 * width :], axis=0, dtype=jnp.float32)
    tokens_grad = (
        grad_first
        + lax.psum_scatter(
            contract_cols(grad_joint, joint_weight).astype(jnp.bfloat16),
            "tensor",
            scatter_dimension=0,
            tiled=True,
        ).astype(jnp.float32)
    ).astype(jnp.bfloat16)
    (
        query_weight_grad,
        key_weight_grad,
        value_weight_grad,
        out_weight_grad,
        up_weight_grad,
        down_weight_grad,
    ) = (
        lax.psum_scatter(
            query_weight_grad.astype(jnp.bfloat16), "dp", scatter_dimension=0, tiled=True
        ).astype(jnp.float32),
        lax.psum_scatter(
            key_weight_grad.astype(jnp.bfloat16), "dp", scatter_dimension=0, tiled=True
        ).astype(jnp.float32),
        lax.psum_scatter(
            value_weight_grad.astype(jnp.bfloat16), "dp", scatter_dimension=0, tiled=True
        ).astype(jnp.float32),
        lax.psum_scatter(
            out_weight_grad.astype(jnp.bfloat16), "dp", scatter_dimension=1, tiled=True
        ).astype(jnp.float32),
        lax.psum_scatter(
            up_weight_grad.astype(jnp.bfloat16), "dp", scatter_dimension=0, tiled=True
        ).astype(jnp.float32),
        lax.psum_scatter(
            down_weight_grad.astype(jnp.bfloat16), "dp", scatter_dimension=1, tiled=True
        ).astype(jnp.float32),
    )
    tensor_place = lax.axis_index("tensor")
    model_width = out_bias.shape[0]
    query_spread = lax.dynamic_update_slice_in_dim(
        jnp.zeros((model_width,), jnp.float32), query_bias_grad, tensor_place * width, 0
    )
    value_spread = lax.dynamic_update_slice_in_dim(
        jnp.zeros((model_width,), jnp.float32), value_bias_grad, tensor_place * width, 0
    )
    up_spread = lax.dynamic_update_slice_in_dim(
        jnp.zeros((hidden_width * lax.axis_size("tensor"),), jnp.float32),
        up_bias_grad,
        tensor_place * hidden_width,
        0,
    )
    (
        query_spread,
        value_spread,
        up_spread,
        out_bias_grad,
        down_bias_grad,
        first_gain_grad,
        first_shift_grad,
        second_gain_grad,
        second_shift_grad,
    ) = lax.psum(
        (
            query_spread,
            value_spread,
            up_spread,
            out_bias_grad,
            down_bias_grad,
            first_gain_grad,
            first_shift_grad,
            second_gain_grad,
            second_shift_grad,
        ),
        ("dp", "tensor"),
    )
    query_bias_grad = lax.dynamic_slice_in_dim(query_spread, tensor_place * width, width, 0)
    value_bias_grad = lax.dynamic_slice_in_dim(value_spread, tensor_place * width, width, 0)
    up_bias_grad = lax.dynamic_slice_in_dim(up_spread, tensor_place * hidden_width, hidden_width, 0)
    factor = clip_limit / jnp.maximum(logit_peak, clip_limit)
    column_scale = jnp.repeat(jnp.sqrt(factor), HD)
    query_clipped = (query_weight.astype(jnp.float32) * column_scale).astype(jnp.bfloat16)
    query_bias_clipped = (query_bias.astype(jnp.float32) * column_scale).astype(jnp.bfloat16)
    key_clipped = (key_weight.astype(jnp.float32) * column_scale).astype(jnp.bfloat16)
    return (
        layer_out,
        tokens_grad,
        query_weight_grad,
        query_bias_grad,
        key_weight_grad,
        value_weight_grad,
        value_bias_grad,
        out_weight_grad,
        out_bias_grad,
        first_gain_grad,
        first_shift_grad,
        up_weight_grad,
        up_bias_grad,
        down_weight_grad,
        down_bias_grad,
        second_gain_grad,
        second_shift_grad,
        logit_peak,
        query_clipped,
        query_bias_clipped,
        key_clipped,
    )


LOG2E=1.4426950408889634
NT=(((1,),(1,)),((),()))
NN=(((1,),(0,)),((),()))
F32=jnp.float32
BF=jnp.bfloat16
MESH=pl.DeviceIdType.MESH
EPSILON=1e-5
NC=4


def dot(a,b,dims):
    return lax.dot_general(a,b,dims,preferred_element_type=jnp.float32)


def greet(partner):
    barrier=pltpu.get_barrier_semaphore()
    pl.semaphore_signal(barrier,inc=1,device_id=partner,device_id_type=MESH)
    pl.semaphore_wait(barrier,1)


def qkv_kernel(tok_ref,w_ref,bias_ref,qkv_ref,xall_ref,ssem,rsem):
    d=lax.axis_index("dp"); t=lax.axis_index("tensor")
    partner=(d,1-t)
    own=tok_ref.shape[0]; cr=own//NC
    greet(partner)
    def rows(rank,c): return pl.ds(pl.multiple_of(2*c*cr+rank*cr,cr),cr)
    def copy(c): return pltpu.make_async_remote_copy(tok_ref.at[c*cr:(c+1)*cr],xall_ref.at[rows(t,c)],ssem.at[c],rsem.at[c],device_id=partner,device_id_type=MESH)
    for c in range(NC):
        copy(c).start()
    for c in range(NC):
        xall_ref[rows(t,c)]=tok_ref[c*cr:(c+1)*cr]
    n=w_ref.shape[1]
    for c in range(NC):
        copy(c).wait_recv()
        @pl.loop(0,n//512)
        def _(j):
            cs=pl.ds(pl.multiple_of(j*512,512),512)
            rr=slice(2*c*cr,2*(c+1)*cr)
            qkv_ref[rr,cs]=(dot(xall_ref[rr],w_ref[:,cs],NN)+bias_ref[:,cs]).astype(BF)
    for c in range(NC): copy(c).wait_send()

def qkv_call(tok,w,bias,cid):
    V=pl.BlockSpec(memory_space=pltpu.VMEM)
    rows=2*tok.shape[0]
    return pl.pallas_call(qkv_kernel,
      out_shape=(jax.ShapeDtypeStruct((rows,w.shape[1]),BF),jax.ShapeDtypeStruct((rows,tok.shape[1]),BF)),
      in_specs=[V]*3,out_specs=(V,V),scratch_shapes=[pltpu.SemaphoreType.DMA((NC,)),pltpu.SemaphoreType.DMA((NC,))],
      compiler_params=pltpu.CompilerParams(collective_id=cid,has_side_effects=True,vmem_limit_bytes=56*2**20),
      cost_estimate=pl.CostEstimate(flops=2*rows*w.shape[0]*w.shape[1],bytes_accessed=8*2**20,transcendentals=0),
      name="qkv")(tok,w,bias)

def mid_kernel(qkv_hbm,w_hbm,tok,cot_hbm,vec,upb,
               lo_hbm,gf,dqkv_hbm,dw,r1,r2,r3,early,
               qkv,vt,kt,ctx,ctxo,lse,cl,wo,wup,wdn,xh,rst,hall,act,slp,ball,ga,dcs,dcall,part,pch,ctt,dqt,dl,dkv,sbuf,rbuf,tb,th,stage,
               lsem,losem,dsem,osem,ssem,rsem,rl,g1s,g1r,g2s,g2r,g3s,g3r):
    d=lax.axis_index("dp"); t=lax.axis_index("tensor")
    partner=(d,1-t)
    core=d%2; x_=(d//2)%2; z=d//4
    def dev(z_,xx,c_): return ((z_*2+xx)*2+c_,t)
    sib=dev(z,x_,1-core); xp=dev(z,1-x_,core); zp=[dev((z+k)%4,x_,core) for k in (1,2,3)]
    own,dm=tok.shape; cr=own//NC; cg=2*cr; rows_all=2*own; width=ctx.shape[1]; ff=wup.shape[2]; wide=wo.shape[2]; pairs=width//128
    loads=[pltpu.make_async_copy(qkv_hbm,qkv,lsem.at[0]),
         pltpu.make_async_copy(w_hbm.at[:,:,0:wide],wo,lsem.at[1]),
         pltpu.make_async_copy(w_hbm.at[:,:,wide:wide+ff],wup,lsem.at[2]),
         pltpu.make_async_copy(w_hbm.at[:,:,wide+ff:wide+2*ff],wdn,lsem.at[3]),
         pltpu.make_async_copy(cot_hbm,cl,lsem.at[4])]
    for c in loads: c.start()
    barrier=pltpu.get_barrier_semaphore()
    everyone=[partner,sib,xp]+zp
    for p in everyone: pl.semaphore_signal(barrier,inc=1,device_id=p,device_id_type=MESH)
    def chunk(c): return pl.ds(pl.multiple_of(c*cg,cg),cg)
    def rows(rank,c): return pl.ds(pl.multiple_of(c*cg+rank*cr,cr),cr)
    def half(rank): return pl.ds(pl.multiple_of(rank*cr,cr),cr)
    def loc(c): return pl.ds(pl.multiple_of(c*cr,cr),cr)
    def rs_copy(k,c):
        return pltpu.make_async_remote_copy(sbuf.at[k-1,loc(c)],rbuf.at[k-1,loc(c)],ssem.at[k,c],rsem.at[k,c],device_id=partner,device_id_type=MESH)
    def ag_copy(k,buf,c,rank):
        return pltpu.make_async_remote_copy(buf.at[rows(rank,c)],buf.at[rows(rank,c)],ssem.at[k,c],rsem.at[k,c],device_id=partner,device_id_type=MESH)
    def cols(rank): return pl.ds(pl.multiple_of(rank*width,128),width)
    def ctx_copy(c,rank):
        return pltpu.make_async_remote_copy(ctx.at[rows(1-rank,c)],ctxo.at[loc(c),cols(rank)],ssem.at[0,c],rsem.at[0,c],device_id=partner,device_id_type=MESH)
    def dctx_copy(c,rank):
        return pltpu.make_async_remote_copy(dcs.at[loc(c),cols(1-rank)],dcall.at[rows(rank,c)],ssem.at[5,c],rsem.at[5,c],device_id=partner,device_id_type=MESH)
    early[...]=jnp.zeros_like(early)
    early[10:11]=jnp.full_like(early[10:11],-jnp.inf)
    def whole(w): return w[...].reshape(dm,w.shape[2])
    def strip(w,cs): return w[:,:,cs].reshape(dm,TF)
    dkv[...]=jnp.zeros_like(dkv)
    lane=lax.broadcasted_iota(jnp.int32,(1,128),1)
    scale=jnp.bfloat16(HD**-0.5); zero=jnp.bfloat16(0)
    loads[0].wait()
    ones=jnp.where(lax.broadcasted_iota(jnp.int32,(16,rows_all),0)==0,1.0,0.0).astype(BF)
    @pl.loop(0,pairs)
    def _(p):
        ck=pl.multiple_of(width+p*128,128); cv=pl.multiple_of(2*width+p*128,128)
        kt[p]=qkv[:,pl.ds(ck,128)].T
        v=qkv[:,pl.ds(cv,128)].T
        vt[2*p,0:64]=v[0:64]; vt[2*p,64:80]=ones
        vt[2*p+1,0:64]=v[64:128]; vt[2*p+1,64:80]=ones
    loads[1].wait()
    pl.semaphore_wait(barrier,len(everyone))
    def split(k,c):
        sbuf[k-1,loc(c)]=pch[half(1-t)].astype(BF)
        rs_copy(k,c).start()
        part[loc(c)]=pch[half(t)]
    def stats(v):
        cen=v-jnp.mean(v,axis=1,keepdims=True)
        r=lax.rsqrt(jnp.mean(cen*cen,axis=1,keepdims=True)+EPSILON)
        return cen*r,r
    def lo_copy(c): return pltpu.make_async_copy(cl.at[loc(c)],lo_hbm.at[loc(c)],losem.at[c])
    TF=512
    def out_copy(slot,col):
        return pltpu.make_async_copy(stage.at[slot],dw.at[:,:,:,:,pl.ds(pl.multiple_of(col,512),512)],osem.at[slot])
    def wgrad(slot,left,right_ref,rcol,ocol):
        @pl.loop(0,dm//256)
        def _(i):
            ms=pl.ds(pl.multiple_of(i*256,256),256)
            stage[slot,i]=dot(left[ms],right_ref[:,pl.ds(pl.multiple_of(rcol,512),512)],NN).astype(BF).reshape(2,2,64,512)
        out_copy(slot,ocol).start()
    def stage_a(c):
        rs=chunk(c)
        @pl.loop(0,pairs)
        def _(p):
            cq=pl.ds(pl.multiple_of(p*128,128),128); ck=pl.ds(pl.multiple_of(width+p*128,128),128)
            pks=[]
            for h in (0,1):
                keep=(lane<64) if h==0 else (lane>=64)
                q=jnp.where(keep,qkv[rs,cq]*scale,zero)
                st=dot(qkv[:,ck],q,NT)
                m=jnp.max(st,axis=0,keepdims=True)
                mc=m*LOG2E
                pt=jnp.exp2(st*LOG2E-mc).astype(BF)
                ot=dot(vt[2*p+h],pt,NN)
                tot=ot[64:65]
                ctt[h*64:(h+1)*64,:]=ot[0:64]*(1.0/tot)
                lse[pl.ds(2*p+h,1),rs]=mc+jnp.log2(tot)
                pks.append(jnp.max(m,axis=1,keepdims=True))
            early[10:11,cq]=jnp.maximum(early[10:11,cq],jnp.where(lane<64,pks[0],pks[1]))
            ctx[rs,cq]=ctt[...].T.astype(BF)
        ctx_copy(c,t).start()
        ctxo[loc(c),cols(t)]=ctx[rows(t,c)]
    def stage_b(c):
        ctx_copy(c,1-t).wait_recv()
        x,r=stats(tok[loc(c)].astype(F32)+dot(ctxo[loc(c)],whole(wo),NT)+vec[0:1])
        xh[loc(c)]=x
        rst[loc(c)]=jnp.broadcast_to(r,(cr,128))
        hall[rows(t,c)]=(x*vec[1:2]+vec[2:3]).astype(BF)
        ag_copy(3,hall,c,t).start()
    def stage_c(c):
        rs=chunk(c)
        ag_copy(3,hall,c,1-t).wait_recv()
        @pl.loop(0,ff//TF)
        def _(j):
            cs=pl.ds(pl.multiple_of(j*TF,TF),TF)
            u=dot(hall[rs],strip(wup,cs),NN)+upb[:,cs]
            cdf=0.5*(1.0+lax.erf(u*0.5**0.5))
            act[rs,cs]=(u*cdf).astype(BF)
            slp[rs,cs]=(cdf+u*jnp.exp(-0.5*u*u)*(0.5/math.pi)**0.5).astype(BF)
        pch[...]=dot(act[rs],whole(wdn),NT)
        split(1,c)
    def stage_d(c):
        rs_copy(1,c).wait_recv()
        x,r=stats(xh[loc(c)]*vec[1:2]+vec[2:3]+part[loc(c)]+rbuf[0,loc(c)].astype(F32)+vec[3:4])
        dy=cl[loc(c)].astype(F32)
        cl[loc(c)]=(x*vec[4:5]+vec[5:6]).astype(BF)
        lo_copy(c).start()
        early[4:5]+=jnp.sum(dy*x,axis=0,keepdims=True)
        early[5:6]+=jnp.sum(dy,axis=0,keepdims=True)
        dx=dy*vec[4:5]
        g=r*(dx-jnp.mean(dx,axis=1,keepdims=True)-x*jnp.mean(dx*x,axis=1,keepdims=True))
        gf[loc(c)]=g
        gb=g.astype(BF)
        early[3:4]+=jnp.sum(gb.astype(F32),axis=0,keepdims=True)
        ball[rows(t,c)]=gb
        ag_copy(4,ball,c,t).start()
        tb[:,rows(t,c)]=gb.T
    def stage_e(c):
        rs=chunk(c)
        ag_copy(4,ball,c,1-t).wait_recv()
        @pl.loop(0,ff//TF)
        def _(j):
            cs=pl.ds(pl.multiple_of(j*TF,TF),TF)
            gu=(dot(ball[rs],strip(wdn,cs),NN)*slp[rs,cs].astype(F32)).astype(BF)
            slp[rs,cs]=gu
            row=pl.ds(8+j*TF//dm,1); cc=pl.ds(pl.multiple_of(j*TF%dm,TF),TF)
            early[row,cc]+=jnp.sum(gu.astype(F32),axis=0,keepdims=True)
        pch[...]=dot(slp[rs],whole(wup),NT)
        split(2,c)
        tb[:,rows(1-t,c)]=ball[rows(1-t,c)].T
        th[:,chunk(c)]=hall[chunk(c)].T
    def stage_f(c):
        rs_copy(2,c).wait_recv()
        dy=gf[loc(c)]+part[loc(c)]+rbuf[1,loc(c)].astype(F32)
        x=xh[loc(c)]; r=rst[loc(c)][:,0:1]
        early[1:2]+=jnp.sum(dy*x,axis=0,keepdims=True)
        early[2:3]+=jnp.sum(dy,axis=0,keepdims=True)
        dx=dy*vec[1:2]
        g=r*(dx-jnp.mean(dx,axis=1,keepdims=True)-x*jnp.mean(dx*x,axis=1,keepdims=True))
        gf[loc(c)]=g
        gb=g.astype(BF)
        early[0:1]+=jnp.sum(gb.astype(F32),axis=0,keepdims=True)
        ga[loc(c)]=gb
        dcs[loc(c)]=dot(gb,whole(wo),NN).astype(BF)
        dctx_copy(c,t).start()
        dcall[rows(t,c)]=dcs[loc(c),cols(t)]
    def stage_g(c):
        rs=chunk(c)
        dctx_copy(c,1-t).wait_recv()
        @pl.loop(0,pairs)
        def _(p):
            cq=pl.ds(pl.multiple_of(p*128,128),128); ck=pl.ds(pl.multiple_of(width+p*128,128),128); cv=pl.ds(pl.multiple_of(2*width+p*128,128),128)
            prod=(ctx[rs,cq].astype(F32)*dcall[rs,cq].astype(F32)).T
            dl[0:1]=jnp.sum(prod[0:64],axis=0,keepdims=True)
            dl[1:2]=jnp.sum(prod[64:128],axis=0,keepdims=True)
            for h in (0,1):
                keep=(lane<64) if h==0 else (lane>=64)
                q=jnp.where(keep,qkv[rs,cq]*scale,zero)
                do=jnp.where(keep,dcall[rs,cq],zero)
                st=dot(qkv[:,ck],q,NT)
                pt=jnp.exp2(st*LOG2E-lse[pl.ds(2*p+h,1),rs])
                dpt=dot(qkv[:,cv],do,NT)
                ds=(pt*(dpt-dl[h:h+1])).astype(BF)
                dkv[1,:,cq]+=dot(pt.astype(BF),do,NN)
                dkv[0,:,cq]+=dot(ds,q,NN)
                dqt[h*64:(h+1)*64,:]=dot(kt[p,h*64:(h+1)*64,:],ds,NN)
            qkv[rs,cq]=(dqt[...].T*(HD**-0.5)).astype(BF)
    def grad_down(c):
        slot=c%2
        @pl.when(c>=2)
        def _(): out_copy(slot,0).wait()
        wgrad(slot,tb,act,c*512,wide+ff+c*512)
    def grad_up(c):
        slot=c%2
        @pl.when(c>=2)
        def _(): out_copy(slot,0).wait()
        wgrad(slot,th,slp,c*512,wide+c*512)
    def grad_out():
        @pl.loop(0,NC)
        def _(c): tb[:,loc(c)]=ga[loc(c)].T
        for j in range(wide//512):
            @pl.loop(0,dm//256)
            def _(i):
                ms=pl.ds(pl.multiple_of(i*256,256),256)
                stage[j%2,i]=dot(tb[ms,0:own],ctxo[:,j*512:(j+1)*512],NN).astype(BF).reshape(2,2,64,512)
            out_copy(j%2,j*512).start()
    @pl.loop(0,NC)
    def _(c):
        stage_a(c)
        @pl.when(c>0)
        def _(): stage_b(c-1)
    loads[2].wait(); loads[3].wait(); loads[4].wait()
    @pl.loop(0,NC)
    def _(c):
        stage_c(c)
        @pl.when(c==0)
        def _(): stage_b(NC-1)
        @pl.when(c>=2)
        def _(): stage_d(c-2)
    @pl.loop(NC-2,NC)
    def _(c): stage_d(c)
    @pl.loop(0,NC)
    def _(c): stage_e(c)
    def remote(src,dst,a,b,p): return pltpu.make_async_remote_copy(src,dst,a,b,device_id=p,device_id_type=MESH)
    base=(wide+ff,wide)
    def s1(g): return remote(dw.at[:,:,1-core,:,base[g]:base[g]+ff],r1.at[g],g1s.at[g],g1r.at[g],sib)
    def s2(g): return remote(wup.at[8+4*g:12+4*g],r2.at[g],g2s.at[g],g2r.at[g],xp)
    def s3(k): return remote(wdn.at[12+(z+k)%4],r3.at[3-k],g3s.at[k-1],g3r.at[k-1],zp[k-1])
    def load2(g): return [pltpu.make_async_copy(dw.at[:,1-x_,core,:,base[g]:base[g]+ff],wup.at[0:4],rl.at[0]),
                          pltpu.make_async_copy(r1.at[g,:,1-x_],wup.at[4:8],rl.at[1])]
    def load3(): return [pltpu.make_async_copy(dw.at[:,x_,core,:,base[0]:base[0]+ff],wdn.at[0:4],rl.at[2]),
                         pltpu.make_async_copy(r1.at[0,:,x_],wdn.at[4:8],rl.at[3]),
                         pltpu.make_async_copy(r2.at[0],wdn.at[8:12],rl.at[4])]
    def add2(g):
        for c in load2(g): c.wait()
        @pl.loop(0,4)
        def _(i): wup[8+4*g+i]=(wup[i].astype(F32)+wup[4+i].astype(F32)).astype(BF)
    @pl.loop(0,NC)
    def _(c): grad_down(c)
    out_copy(0,0).wait()
    out_copy(1,0).wait()
    s1(0).start()
    @pl.loop(0,NC)
    def _(c):
        stage_f(c)
        grad_up(c)
        @pl.when(c==1)
        def _():
            s1(0).wait_recv()
            for l in load2(0): l.start()
        @pl.when(c==2)
        def _():
            add2(0)
            s2(0).start()
    out_copy(0,0).wait()
    out_copy(1,0).wait()
    s1(1).start()
    grad_out()
    @pl.loop(0,NC)
    def _(c):
        stage_g(c)
        @pl.when(c==0)
        def _():
            s1(1).wait_recv()
            for l in load2(1): l.start()
        @pl.when(c==1)
        def _():
            add2(1)
            s2(0).wait_send()
            s2(1).start()
            s2(0).wait_recv()
            for l in load3(): l.start()
        @pl.when(c==2)
        def _():
            for l in load3(): l.wait()
            @pl.loop(0,4)
            def _(i): wdn[12+i]=(wdn[i].astype(F32)+wdn[4+i].astype(F32)+wdn[8+i].astype(F32)).astype(BF)
            for k in (1,2,3): s3(k).start()
    @pl.loop(0,pairs)
    def _(p):
        cq=pl.ds(pl.multiple_of(p*128,128),128); ck=pl.ds(pl.multiple_of(width+p*128,128),128); cv=pl.ds(pl.multiple_of(2*width+p*128,128),128)
        qkv[:,ck]=dkv[0,:,cq].astype(BF)
        qkv[:,cv]=dkv[1,:,cq].astype(BF)
    dq_out=pltpu.make_async_copy(qkv,dqkv_hbm,dsem.at[0])
    dq_out.start()
    out_copy(0,0).wait()
    out_copy(1,0).wait()
    dq_out.wait()
    for g in (0,1): s1(g).wait_send()
    s2(1).wait()
    for k in (1,2,3): s3(k).wait()
    @pl.loop(0,NC)
    def _(c):
        lo_copy(c).wait()
        ctx_copy(c,t).wait_send(); dctx_copy(c,t).wait_send()
        for k in (1,2): rs_copy(k,c).wait_send()
        for k,buf in ((3,hall),(4,ball)): ag_copy(k,buf,c,t).wait_send()

def mid_call(qkv,w,tok,cot,vec,upb,cid):
    V=pl.BlockSpec(memory_space=pltpu.VMEM); A=pl.BlockSpec(memory_space=pl.ANY)
    rows,n=qkv.shape; width=n//3; own,dm=tok.shape; ff=upb.shape[1]; cr=own//NC
    S=jax.ShapeDtypeStruct; M=pltpu.VMEM; D=pltpu.SemaphoreType.DMA
    return pl.pallas_call(mid_kernel,
      out_shape=(S((own,dm),BF),S((own,dm),F32),S((rows,n),BF),S((4,2,2,64,2*width+2*ff),BF),S((2,4,2,64,ff),BF),S((2,4,64,ff),BF),S((3,64,ff),BF),S((16,dm),F32)),
      in_specs=[A,A,V,A,V,V],out_specs=(A,V,A,A,A,A,A,V),
      scratch_shapes=[M((rows,n),BF),M((width//HD,80,rows),BF),M((width//128,128,rows),BF),M((rows,width),BF),M((own,2*width),BF),M((width//HD,rows),F32),M((own,dm),BF),
        M((16,64,2*width),BF),M((16,64,ff),BF),M((16,64,ff),BF),
        M((own,dm),F32),M((own,128),F32),
        M((rows,dm),BF),M((rows,ff),BF),M((rows,ff),BF),M((rows,dm),BF),M((own,dm),BF),M((own,2*width),BF),M((rows,width),BF),
        M((own,dm),F32),M((2*cr,dm),F32),M((128,2*cr),F32),M((128,2*cr),F32),M((8,2*cr),F32),M((2,rows,width),F32),
        M((2,own,dm),BF),M((2,own,dm),BF),
        M((dm,rows),BF),M((dm,rows),BF),M((2,4,2,2,64,512),BF),
        D((5,)),D((NC,)),D((1,)),D((2,)),D((6,NC)),D((6,NC)),D((5,)),D((2,)),D((2,)),D((2,)),D((2,)),D((3,)),D((3,))],
      compiler_params=pltpu.CompilerParams(collective_id=cid,has_side_effects=True,vmem_limit_bytes=61*2**20),
      cost_estimate=pl.CostEstimate(flops=2*rows*dm*(6*ff+3*width),bytes_accessed=40*2**20,transcendentals=2*rows*ff),
      name="mid")(qkv,w,tok,cot,vec,upb)

def tail_kernel(dqkv_ref,dw,r1w,r2w,r3w,w_hbm,x_hbm,gf,early,wqk,bq,lim,
                tg,gq,gk,gv,go,gu,gd,sums,late,qc,kc,qbc,
                xv,xt,wv,part,pc,dwh,ysb,yrb,fw,zu,su,ru,oo,o1,o2s,o2,o3s,o3,h1,h2s,h2,h3s,h3,osb,orb,eb,er,lb,lr,
                lsem,s1s,s1r,s2s,s2r,s3s,s3r,ysend,yrecv,es,erc,ls,lrc,os_,or_):
    d=lax.axis_index("dp"); t=lax.axis_index("tensor")
    core=d%2; x=(d//2)%2; z=d//4
    def dev(z_,x_,c_): return ((z_*2+x_)*2+c_,t)
    sib=dev(z,x,1-core); xp=dev(z,1-x,core); yp=(d,1-t)
    zp=[dev((z+k)%4,x,core) for k in (1,2,3)]
    zb=[dev(z+1-2*(z%2),x,core),dev((z+2)%4,x,core)]
    barrier=pltpu.get_barrier_semaphore()
    everyone=[sib,xp,yp]+zp
    for p in everyone: pl.semaphore_signal(barrier,inc=1,device_id=p,device_id_type=MESH)
    own,dm=gf.shape; rows,n=dqkv_ref.shape; width=n//3; cr=own//NC; ff=fw.shape[2]; wide=2*width
    def remote(src,dst,a,b,p): return pltpu.make_async_remote_copy(src,dst,a,b,device_id=p,device_id_type=MESH)
    def local(src,dst,i): return pltpu.make_async_copy(src,dst,lsem.at[i])
    f32=lambda a:a.astype(F32)
    wcols=slice(wide+ff,wide+2*ff); ucols=slice(wide,wide+ff)
    loads=[local(dw.at[:,x,core,:,ucols],zu.at[0],0),local(r1w.at[1,:,x],zu.at[1],1),local(r2w.at[1],zu.at[2],2),
           local(dw.at[:,:,core,:,0:wide],oo,3),local(w_hbm.at[:,:,:],wv,4),local(x_hbm,xv,5),
           local(dw.at[z,x,core,:,wcols],fw.at[0],6),local(r1w.at[0,z,x],fw.at[1],7),local(r2w.at[0,z],fw.at[2],8),
           local(r3w.at[0],fw.at[3],9),local(r3w.at[1],fw.at[4],10),local(r3w.at[2],fw.at[5],11)]
    for c in loads: c.start()
    eb[0]=early[...]
    lb[0]=jnp.zeros_like(lb[0])
    pl.semaphore_wait(barrier,len(everyone))
    o_s1=remote(dw.at[:,:,1-core,:,0:wide],o1,s1s.at[0],s1r.at[0],sib); o_s1.start()
    h_s1=remote(dwh.at[:,:,1-core],h1,s1s.at[1],s1r.at[1],sib)
    o_s2=remote(o2s,o2,s2s.at[0],s2r.at[0],xp)
    h_s2=remote(h2s,h2,s2s.at[1],s2r.at[1],xp)
    def z3(g,src,dst): return [remote(src.at[(z+k)%4],dst.at[3-k],s3s.at[g,k-1],s3r.at[g,k-1],zp[k-1]) for k in (1,2,3)]
    u_s3=z3(0,su,ru); o_s3=z3(1,o3s,o3); h_s3=z3(2,h3s,h3)
    hops=[sib,xp,zb[0],zb[1],yp]
    def ecopy(i): return remote(eb.at[i],er.at[i],es.at[i],erc.at[i],hops[i])
    def eadd(i):
        ecopy(i).wait_recv()
        b=eb[i,8:16]; c=er[i,8:16]
        if i<4:
            r=lax.broadcasted_iota(jnp.int32,b.shape,0)
            b=jnp.where(r==2,jnp.maximum(b,c),b+c)
        eb[i+1,0:8]=eb[i,0:8]+er[i,0:8]; eb[i+1,8:16]=b
    def lcopy(i): return remote(lb.at[i],lr.at[i],ls.at[i],lrc.at[i],hops[i])
    def ladd(i):
        lcopy(i).wait_recv()
        lb[i+1]=lb[i]+lr[i]
    ecopy(0).start()
    for i in (0,1,2): loads[i].wait()
    @pl.loop(0,4)
    def _(i): su[i]=(f32(zu[0,i])+f32(zu[1,i])+f32(zu[2,i])).astype(BF)
    for c in u_s3: c.start()
    loads[4].wait()
    def ycopy(c): return remote(ysb.at[c],yrb.at[c],ysend.at[c],yrecv.at[c],yp)
    @pl.loop(0,NC)
    def _(c):
        pc[...]=dot(dqkv_ref[pl.ds(pl.multiple_of(2*c*cr,2*cr),2*cr)],wv[...].reshape(dm,n),NT)
        ysb[c]=pc[pl.ds(pl.multiple_of((1-t)*cr,cr),cr)].astype(BF)
        ycopy(c).start()
        part[c]=pc[pl.ds(pl.multiple_of(t*cr,cr),cr)]
    lb[0,0:1,0:width]=jnp.sum(f32(dqkv_ref[:,0:width]),axis=0,keepdims=True)
    lb[0,0:1,width:2*width]=jnp.sum(f32(dqkv_ref[:,2*width:]),axis=0,keepdims=True)
    lcopy(0).start()
    eadd(0); ecopy(1).start()
    o_s1.wait_recv(); loads[3].wait()
    @pl.loop(0,4)
    def _(i): o2s[i]=(f32(oo[i,1-x])+f32(o1[i,1-x])).astype(BF)
    o_s2.start()
    loads[5].wait()
    @pl.loop(0,rows//256)
    def _(c):
        cs=pl.ds(pl.multiple_of(c*256,256),256)
        xt[:,cs]=xv[cs].T
    eadd(1); ecopy(2).start()
    @pl.loop(0,4)
    def _(i):
        ms=pl.ds(pl.multiple_of(i*256,256),256)
        for j in range(n//512):
            dwh[i,:,:,:,j*512:(j+1)*512]=dot(xt[ms],dqkv_ref[:,j*512:(j+1)*512],NN).astype(BF).reshape(2,2,64,512)
    h_s1.start()
    ladd(0); lcopy(1).start()
    eadd(2); ecopy(3).start()
    h_s1.wait_recv()
    @pl.loop(0,4)
    def _(i): h2s[i]=(f32(dwh[i,1-x,core])+f32(h1[i,1-x])).astype(BF)
    o_s2.wait_recv()
    @pl.loop(0,4)
    def _(i): o3s[i]=(f32(oo[i,x])+f32(o1[i,x])+f32(o2[i])).astype(BF)
    o_s2.wait_send()
    h_s2.start()
    ladd(1); lcopy(2).start()
    eadd(3); ecopy(4).start()
    for i in range(6,12): loads[i].wait()
    v=f32(fw[0])+f32(fw[1])+f32(fw[2])
    v=v+f32(fw[3])+f32(fw[4])+f32(fw[5])
    gd[...]=v.T
    ladd(2); lcopy(3).start()
    eadd(4)
    sums[...]=eb[5]
    pk=eb[4,10:11,0:width]
    sc=jnp.sqrt(lim[...]/jnp.maximum(pk,lim[...]))
    qc[...]=(f32(wqk[0])*sc).astype(BF); kc[...]=(f32(wqk[1])*sc).astype(BF)
    qbc[...]=(bq[...]*sc).astype(BF)
    for c in u_s3: c.wait_send()
    for c in o_s3: c.start()
    for c in u_s3: c.wait_recv()
    v=f32(zu[0,z])+f32(zu[1,z])+f32(zu[2,z])
    gu[...]=v+f32(ru[0])+f32(ru[1])+f32(ru[2])
    for c in range(NC):
        ycopy(c).wait_recv()
        lo_=slice(c*cr,(c+1)*cr)
        tg[lo_]=(gf[lo_]+part[c]+f32(yrb[c])).astype(BF)
    ladd(3)
    late[...]=lb[4]
    h_s2.wait_recv()
    @pl.loop(0,4)
    def _(i): h3s[i]=(f32(dwh[i,x,core])+f32(h1[i,x])+f32(h2[i])).astype(BF)
    for c in o_s3: c.wait_send()
    for c in h_s3: c.start()
    for c in o_s3: c.wait_recv()
    v=f32(oo[z,x])+f32(o1[z,x])+f32(o2[z])
    v=v+f32(o3[0])+f32(o3[1])+f32(o3[2])
    osb[0]=v[:,0:width]; osb[1]=v[:,width:]
    ocopy=remote(osb.at[1-t],orb,os_,or_,yp)
    ocopy.start()
    ocopy.wait_recv()
    go[...]=(osb[t]+orb[...]).T
    for c in h_s3: c.wait_recv()
    v=f32(dwh[z,x,core])+f32(h1[z,x])+f32(h2[z])
    v=v+f32(h3[0])+f32(h3[1])+f32(h3[2])
    gq[...]=v[:,0:width]; gk[...]=v[:,width:2*width]; gv[...]=v[:,2*width:]
    for c in [o_s1,h_s1,h_s2,ocopy]+h_s3: c.wait_send()
    for i in range(5): ecopy(i).wait_send()
    for i in range(4): lcopy(i).wait_send()
    for c in range(NC): ycopy(c).wait_send()

def tail_call(dqkv,dw,r1,r2,r3,w,xall,gf,early,wqk,bq,lim,cid):
    V=pl.BlockSpec(memory_space=pltpu.VMEM); A=pl.BlockSpec(memory_space=pl.ANY)
    S=jax.ShapeDtypeStruct; D=pltpu.SemaphoreType.DMA; M=pltpu.VMEM
    own,dm=gf.shape; rows,n=dqkv.shape; width=n//3; cr=own//NC
    ff=r3.shape[2]; wide=2*width
    return pl.pallas_call(tail_kernel,
      out_shape=(S((own,dm),BF),S((64,width),F32),S((64,width),F32),S((64,width),F32),S((width,64),F32),S((64,ff),F32),S((ff,64),F32),
                 S((16,1024),F32),S((8,1024),F32),S((64,width),BF),S((64,width),BF),S((1,width),BF)),
      in_specs=[V]+[A]*6+[V]*5,out_specs=(V,)*12,
      scratch_shapes=[M((rows,dm),BF),M((dm,rows),BF),M((16,64,n),BF),M((NC,cr,dm),F32),M((2*cr,dm),F32),M((4,2,2,64,n),BF),M((NC,cr,dm),BF),M((NC,cr,dm),BF),
        M((6,64,ff),BF),M((3,4,64,ff),BF),M((4,64,ff),BF),M((3,64,ff),BF),
        M((4,2,64,wide),BF),M((4,2,64,wide),BF),M((4,64,wide),BF),M((4,64,wide),BF),M((4,64,wide),BF),M((3,64,wide),BF),
        M((4,2,64,n),BF),M((4,64,n),BF),M((4,64,n),BF),M((4,64,n),BF),M((3,64,n),BF),M((2,64,width),F32),M((64,width),F32),
        M((6,16,1024),F32),M((5,16,1024),F32),M((5,8,1024),F32),M((4,8,1024),F32),
        D((12,)),D((2,)),D((2,)),D((2,)),D((2,)),D((3,3)),D((3,3)),D((NC,)),D((NC,)),D((5,)),D((5,)),D((4,)),D((4,)),D,D],
      compiler_params=pltpu.CompilerParams(collective_id=cid,has_side_effects=True,vmem_limit_bytes=61*2**20),
      name="tail")(dqkv,dw,r1,r2,r3,w,xall,gf,early,wqk,bq,lim)

def per_device_pair(tokens,query_weight,query_bias,key_weight,value_weight,value_bias,out_weight,out_bias,first_gain,first_shift,
    up_weight,up_bias,down_weight,down_bias,second_gain,second_shift,cotangent,clip_limit):
    width=query_weight.shape[1]; ff=up_weight.shape[1]; dm=tokens.shape[1]
    f=lambda a:a.astype(F32)
    t=lax.axis_index("tensor")
    head_shard=jnp.concatenate([query_weight,key_weight,value_weight],axis=1)
    out_t=out_weight.T
    out_o=lax.ppermute(out_t,"tensor",[(0,1),(1,0)])
    out_both=jnp.where(t==0,jnp.concatenate([out_t,out_o],axis=1),jnp.concatenate([out_o,out_t],axis=1))
    rest_shard=jnp.concatenate([out_both,up_weight,down_weight.T],axis=1)
    head_w=lax.all_gather(head_shard,"dp",axis=0,tiled=True)
    rest_shard,_=lax.optimization_barrier((rest_shard,head_w))
    rest_w=lax.all_gather(rest_shard,"dp",axis=0,tiled=True)
    bias=jnp.concatenate([f(query_bias),jnp.zeros((width,),F32),f(value_bias)])[None]
    qkv,xall=qkv_call(tokens,head_w,bias,0)
    z=jnp.zeros((dm,),F32)
    vec=jnp.stack([f(out_bias),f(first_gain),f(first_shift),f(down_bias),f(second_gain),f(second_shift),z,z])
    lo,gf,dqkv,dw,r1,r2,r3,early=mid_call(qkv,rest_w.reshape(16,64,-1),tokens,cotangent,vec,f(up_bias)[None],1)
    wqk=jnp.stack([query_weight,key_weight])
    lim=jnp.repeat(clip_limit,HD)[None]
    tg,gq,gk,gv,go,gu,gd,sums,late,qc,kc,qbc=tail_call(dqkv,dw,r1,r2,r3,head_w.reshape(16,64,-1),xall,gf,early,wqk,f(query_bias)[None],lim,2)
    return (lo,tg,gq,late[0,:width],gk,gv,late[0,width:2*width],go,sums[0],sums[1],sums[2],gu,sums[8:10].reshape(ff),gd,
      sums[3],sums[4],sums[5],sums[10,:width:HD],qc,qbc[0],kc)


def layer(*args):
    paired = lax.axis_size("dp") == 16 and lax.axis_size("tensor") == 2 and 2 * args[0].shape[0] == LEN
    return per_device_pair(*args) if paired else per_device(*args)


def solution(mesh):
    in_specs = (
        P(("dp", "tensor"), None),
        P("dp", "tensor"),
        P("tensor"),
        P("dp", "tensor"),
        P("dp", "tensor"),
        P("tensor"),
        P("tensor", "dp"),
        P(),
        P(),
        P(),
        P("dp", "tensor"),
        P("tensor"),
        P("tensor", "dp"),
        P(),
        P(),
        P(),
        P(("dp", "tensor"), None),
        P("tensor"),
    )
    out_specs = (
        P(("dp", "tensor"), None),
        P(("dp", "tensor"), None),
        P("dp", "tensor"),
        P("tensor"),
        P("dp", "tensor"),
        P("dp", "tensor"),
        P("tensor"),
        P("tensor", "dp"),
        P(),
        P(),
        P(),
        P("dp", "tensor"),
        P("tensor"),
        P("tensor", "dp"),
        P(),
        P(),
        P(),
        P("tensor"),
        P("dp", "tensor"),
        P("tensor"),
        P("dp", "tensor"),
    )
    return jax.shard_map(
        layer, mesh=mesh, in_specs=in_specs, out_specs=out_specs, check_vma=False
    )
```

```python
import functools
import math

import jax
import jax.numpy as jnp
from jax import lax
from jax.experimental import pallas as pl
from jax.experimental.pallas import tpu as pltpu
from jax.sharding import PartitionSpec as P

HD = 64
LEN = 1024
QB = 512


def layer_norm(values, gain, shift):
    center = values - jnp.mean(values, axis=-1, keepdims=True)
    spread = jnp.mean(center * center, axis=-1, keepdims=True)
    return center * lax.rsqrt(spread + EPSILON) * gain + shift


def gelu_slope(upper):
    normal_cdf = 0.5 * (1.0 + lax.erf(upper * 0.5**0.5))
    return normal_cdf + upper * jnp.exp(-0.5 * upper * upper) * (0.5 / math.pi) ** 0.5


def contract_rows(left, right):
    return lax.dot_general(
        left, right, (((0,), (0,)), ((), ())), preferred_element_type=jnp.float32
    )


def contract_cols(left, right):
    return lax.dot_general(
        left, right, (((1,), (1,)), ((), ())), preferred_element_type=jnp.float32
    )


def per_device(
    tokens,
    query_weight,
    query_bias,
    key_weight,
    value_weight,
    value_bias,
    out_weight,
    out_bias,
    first_gain,
    first_shift,
    up_weight,
    up_bias,
    down_weight,
    down_bias,
    second_gain,
    second_shift,
    cotangent,
    clip_limit,
):
    query_full, key_full, value_full, out_full, up_full, down_full = (
        lax.all_gather(query_weight, "dp", axis=0, tiled=True),
        lax.all_gather(key_weight, "dp", axis=0, tiled=True),
        lax.all_gather(value_weight, "dp", axis=0, tiled=True),
        lax.all_gather(out_weight, "dp", axis=1, tiled=True),
        lax.all_gather(up_weight, "dp", axis=0, tiled=True),
        lax.all_gather(down_weight, "dp", axis=1, tiled=True),
    )
    width = query_full.shape[1]
    hidden_width = up_full.shape[1]
    heads_here = width // HD
    score_scale = HD ** (-0.5)
    joint_weight = jnp.concatenate([query_full, key_full, value_full], axis=1)
    gathered = lax.all_gather(tokens, "tensor", axis=0, tiled=True)
    group_rows = gathered.shape[0]
    seq_count = group_rows // LEN
    block_count = LEN // QB
    projected = jnp.dot(gathered, joint_weight, preferred_element_type=jnp.float32)
    queries = (projected[:, :width] + query_bias.astype(jnp.float32)).astype(jnp.bfloat16)
    keyset = projected[:, width : 2 * width].astype(jnp.bfloat16)
    valset = (projected[:, 2 * width :] + value_bias.astype(jnp.float32)).astype(jnp.bfloat16)
    query_seq = queries.reshape(seq_count, LEN, heads_here, HD)
    key_seq = keyset.reshape(seq_count, LEN, heads_here, HD)
    value_seq = valset.reshape(seq_count, LEN, heads_here, HD)

    def attend_block(block_id):
        seq_id = block_id // block_count
        row_start = block_id % block_count * QB
        query_rows = lax.dynamic_slice_in_dim(
            lax.dynamic_index_in_dim(query_seq, seq_id, 0, False), row_start, QB, 0
        )
        key_rows = lax.dynamic_index_in_dim(key_seq, seq_id, 0, False)
        value_rows = lax.dynamic_index_in_dim(value_seq, seq_id, 0, False)
        logits = (
            jnp.einsum("qhd,khd->hqk", query_rows, key_rows, preferred_element_type=jnp.float32)
            * score_scale
        )
        row_max = jnp.max(logits, axis=2, keepdims=True)
        exponent = jnp.exp(logits - row_max)
        totals = jnp.sum(exponent, axis=2, keepdims=True)
        probs_low = (exponent / totals).astype(jnp.bfloat16)
        context_rows = jnp.einsum(
            "hqk,khd->qhd", probs_low, value_rows, preferred_element_type=jnp.float32
        )
        return (
            context_rows.reshape(QB, width).astype(jnp.bfloat16),
            (row_max + jnp.log(totals))[:, :, 0],
            jnp.max(row_max, axis=(1, 2)),
        )

    context_blocks, log_totals, block_peaks = lax.map(
        attend_block, jnp.arange(seq_count * block_count)
    )
    context = context_blocks.reshape(group_rows, width)
    logit_peak = lax.pmax(jnp.max(block_peaks, axis=0), "dp")
    attention = lax.psum_scatter(
        jnp.dot(context, out_full, preferred_element_type=jnp.float32).astype(jnp.bfloat16),
        "tensor",
        scatter_dimension=0,
        tiled=True,
    ).astype(jnp.float32) + out_bias.astype(jnp.float32)
    first_resid = tokens.astype(jnp.float32) + attention
    hidden, first_pull = jax.vjp(
        layer_norm, first_resid, first_gain.astype(jnp.float32), first_shift.astype(jnp.float32)
    )
    hidden_all = lax.all_gather(hidden.astype(jnp.bfloat16), "tensor", axis=0, tiled=True)
    upper = jnp.dot(hidden_all, up_full, preferred_element_type=jnp.float32) + up_bias.astype(
        jnp.float32
    )
    acted = jax.nn.gelu(upper, approximate=False).astype(jnp.bfloat16)
    branch = lax.psum_scatter(
        jnp.dot(acted, down_full, preferred_element_type=jnp.float32).astype(jnp.bfloat16),
        "tensor",
        scatter_dimension=0,
        tiled=True,
    ).astype(jnp.float32) + down_bias.astype(jnp.float32)
    normed, second_pull = jax.vjp(
        layer_norm,
        hidden + branch,
        second_gain.astype(jnp.float32),
        second_shift.astype(jnp.float32),
    )
    layer_out = normed.astype(jnp.bfloat16)
    grad_second, second_gain_grad, second_shift_grad = second_pull(cotangent.astype(jnp.float32))
    grad_branch = grad_second.astype(jnp.bfloat16)
    down_bias_grad = jnp.sum(grad_branch, axis=0, dtype=jnp.float32)
    branch_all = lax.all_gather(grad_branch, "tensor", axis=0, tiled=True)
    grad_acted = contract_cols(branch_all, down_full)
    down_weight_grad = contract_rows(acted, branch_all)
    grad_upper = (grad_acted * gelu_slope(upper)).astype(jnp.bfloat16)
    up_bias_grad = jnp.sum(grad_upper, axis=0, dtype=jnp.float32)
    up_weight_grad = contract_rows(hidden_all, grad_upper)
    grad_hidden = grad_second + lax.psum_scatter(
        contract_cols(grad_upper, up_full).astype(jnp.bfloat16),
        "tensor",
        scatter_dimension=0,
        tiled=True,
    ).astype(jnp.float32)
    grad_first, first_gain_grad, first_shift_grad = first_pull(grad_hidden)
    grad_attn = grad_first.astype(jnp.bfloat16)
    out_bias_grad = jnp.sum(grad_attn, axis=0, dtype=jnp.float32)
    attn_all = lax.all_gather(grad_attn, "tensor", axis=0, tiled=True)
    grad_context = contract_cols(attn_all, out_full).astype(jnp.bfloat16)
    out_weight_grad = contract_rows(context, attn_all)
    query_blocks = queries.reshape(seq_count, block_count, QB, heads_here, HD)
    grad_blocks = grad_context.reshape(seq_count, block_count, QB, heads_here, HD)
    log_blocks = log_totals.reshape(seq_count, block_count, heads_here, QB)

    def sequence_back(item):
        query_part, grad_part, log_part, key_rows, value_rows = item

        def block_back(carry, piece):
            key_acc, value_acc = carry
            query_rows, grad_rows, log_rows = piece
            logits = (
                jnp.einsum("qhd,khd->hqk", query_rows, key_rows, preferred_element_type=jnp.float32)
                * score_scale
            )
            probs = jnp.exp(logits - log_rows[:, :, None])
            probs_low = probs.astype(jnp.bfloat16)
            value_acc = value_acc + jnp.einsum(
                "hqk,qhd->khd", probs_low, grad_rows, preferred_element_type=jnp.float32
            )
            grad_probs = jnp.einsum(
                "qhd,khd->hqk", grad_rows, value_rows, preferred_element_type=jnp.float32
            )
            inner = jnp.sum(probs * grad_probs, axis=2, keepdims=True)
            grad_logits = (probs * (grad_probs - inner)).astype(jnp.bfloat16)
            grad_query = (
                jnp.einsum(
                    "hqk,khd->qhd", grad_logits, key_rows, preferred_element_type=jnp.float32
                )
                * score_scale
            )
            key_acc = (
                key_acc
                + jnp.einsum(
                    "hqk,qhd->khd", grad_logits, query_rows, preferred_element_type=jnp.float32
                )
                * score_scale
            )
            return ((key_acc, value_acc), grad_query.astype(jnp.bfloat16))

        empty = jnp.zeros((LEN, heads_here, HD), jnp.float32)
        (key_acc, value_acc), grad_query_rows = lax.scan(
            block_back, (empty, empty), (query_part, grad_part, log_part)
        )
        return (grad_query_rows, key_acc.astype(jnp.bfloat16), value_acc.astype(jnp.bfloat16))

    grad_queries_all, grad_keys_all, grad_values_all = lax.map(
        sequence_back, (query_blocks, grad_blocks, log_blocks, key_seq, value_seq)
    )
    grad_joint = jnp.concatenate(
        [
            grad_queries_all.reshape(group_rows, width),
            grad_keys_all.reshape(group_rows, width),
            grad_values_all.reshape(group_rows, width),
        ],
        axis=1,
    )
    joint_grad = contract_rows(gathered, grad_joint)
    query_weight_grad = joint_grad[:, :width]
    key_weight_grad = joint_grad[:, width : 2 * width]
    value_weight_grad = joint_grad[:, 2 * width :]
    query_bias_grad = jnp.sum(grad_joint[:, :width], axis=0, dtype=jnp.float32)
    value_bias_grad = jnp.sum(grad_joint[:, 2 * width :], axis=0, dtype=jnp.float32)
    tokens_grad = (
        grad_first
        + lax.psum_scatter(
            contract_cols(grad_joint, joint_weight).astype(jnp.bfloat16),
            "tensor",
            scatter_dimension=0,
            tiled=True,
        ).astype(jnp.float32)
    ).astype(jnp.bfloat16)
    (
        query_weight_grad,
        key_weight_grad,
        value_weight_grad,
        out_weight_grad,
        up_weight_grad,
        down_weight_grad,
    ) = (
        lax.psum_scatter(
            query_weight_grad.astype(jnp.bfloat16), "dp", scatter_dimension=0, tiled=True
        ).astype(jnp.float32),
        lax.psum_scatter(
            key_weight_grad.astype(jnp.bfloat16), "dp", scatter_dimension=0, tiled=True
        ).astype(jnp.float32),
        lax.psum_scatter(
            value_weight_grad.astype(jnp.bfloat16), "dp", scatter_dimension=0, tiled=True
        ).astype(jnp.float32),
        lax.psum_scatter(
            out_weight_grad.astype(jnp.bfloat16), "dp", scatter_dimension=1, tiled=True
        ).astype(jnp.float32),
        lax.psum_scatter(
            up_weight_grad.astype(jnp.bfloat16), "dp", scatter_dimension=0, tiled=True
        ).astype(jnp.float32),
        lax.psum_scatter(
            down_weight_grad.astype(jnp.bfloat16), "dp", scatter_dimension=1, tiled=True
        ).astype(jnp.float32),
    )
    tensor_place = lax.axis_index("tensor")
    model_width = out_bias.shape[0]
    query_spread = lax.dynamic_update_slice_in_dim(
        jnp.zeros((model_width,), jnp.float32), query_bias_grad, tensor_place * width, 0
    )
    value_spread = lax.dynamic_update_slice_in_dim(
        jnp.zeros((model_width,), jnp.float32), value_bias_grad, tensor_place * width, 0
    )
    up_spread = lax.dynamic_update_slice_in_dim(
        jnp.zeros((hidden_width * lax.axis_size("tensor"),), jnp.float32),
        up_bias_grad,
        tensor_place * hidden_width,
        0,
    )
    (
        query_spread,
        value_spread,
        up_spread,
        out_bias_grad,
        down_bias_grad,
        first_gain_grad,
        first_shift_grad,
        second_gain_grad,
        second_shift_grad,
    ) = lax.psum(
        (
            query_spread,
            value_spread,
            up_spread,
            out_bias_grad,
            down_bias_grad,
            first_gain_grad,
            first_shift_grad,
            second_gain_grad,
            second_shift_grad,
        ),
        ("dp", "tensor"),
    )
    query_bias_grad = lax.dynamic_slice_in_dim(query_spread, tensor_place * width, width, 0)
    value_bias_grad = lax.dynamic_slice_in_dim(value_spread, tensor_place * width, width, 0)
    up_bias_grad = lax.dynamic_slice_in_dim(up_spread, tensor_place * hidden_width, hidden_width, 0)
    factor = clip_limit / jnp.maximum(logit_peak, clip_limit)
    column_scale = jnp.repeat(jnp.sqrt(factor), HD)
    query_clipped = (query_weight.astype(jnp.float32) * column_scale).astype(jnp.bfloat16)
    query_bias_clipped = (query_bias.astype(jnp.float32) * column_scale).astype(jnp.bfloat16)
    key_clipped = (key_weight.astype(jnp.float32) * column_scale).astype(jnp.bfloat16)
    return (
        layer_out,
        tokens_grad,
        query_weight_grad,
        query_bias_grad,
        key_weight_grad,
        value_weight_grad,
        value_bias_grad,
        out_weight_grad,
        out_bias_grad,
        first_gain_grad,
        first_shift_grad,
        up_weight_grad,
        up_bias_grad,
        down_weight_grad,
        down_bias_grad,
        second_gain_grad,
        second_shift_grad,
        logit_peak,
        query_clipped,
        query_bias_clipped,
        key_clipped,
    )


LOG2E=1.4426950408889634
NT=(((1,),(1,)),((),()))
NN=(((1,),(0,)),((),()))
F32=jnp.float32
BF=jnp.bfloat16
MESH=pl.DeviceIdType.MESH
EPSILON=1e-5
NC=4


def dot(a,b,dims):
    return lax.dot_general(a,b,dims,preferred_element_type=jnp.float32)


def greet(partner):
    barrier=pltpu.get_barrier_semaphore()
    pl.semaphore_signal(barrier,inc=1,device_id=partner,device_id_type=MESH)
    pl.semaphore_wait(barrier,1)


def main_kernel(wq,wk,wv,wos,wu,wds,tok,cot_hbm,bias,vec,upb,
               lo_hbm,gf,dqkv_hbm,dw,r1,r2,r3,early,x_hbm,wh_hbm,
               sh,qkv,vt,kt,ctx,ctxo,lse,cl,wo,wup,wdn,xh,rst,hall,act,slp,ball,ga,dcs,dcall,part,pch,ctt,dqt,dl,dkv,sbuf,rbuf,tb,th,stage,
               lsem,losem,dsem,osem,ssem,rsem,rl,g1s,g1r,g2s,g2r,g3s,g3r,ts,tr,azs,azr,axs,axr,acs,acr):
    d=lax.axis_index("dp"); t=lax.axis_index("tensor")
    partner=(d,1-t)
    core=d%2; x_=(d//2)%2; z=d//4
    def dev(z_,xx,c_): return ((z_*2+xx)*2+c_,t)
    sib=dev(z,x_,1-core); xp=dev(z,1-x_,core); zp=[dev((z+k)%4,x_,core) for k in (1,2,3)]
    own,dm=tok.shape; cr=own//NC; cg=2*cr; rows_all=2*own; width=ctx.shape[1]; ff=wup.shape[2]; wide=wo.shape[2]; pairs=width//128
    def local(src,dst,i): return pltpu.make_async_copy(src,dst,lsem.at[i])
    def remote(src,dst,a,b,p): return pltpu.make_async_remote_copy(src,dst,a,b,device_id=p,device_id_type=MESH)
    cot_load=local(cot_hbm,cl,0)
    cot_load.start()
    barrier=pltpu.get_barrier_semaphore()
    n=3*width
    sh[:,0:width]=wq[...]; sh[:,width:2*width]=wk[...]; sh[:,2*width:n]=wv[...]
    everyone=[partner,sib,xp]+zp
    for p in everyone: pl.semaphore_signal(barrier,inc=1,device_id=p,device_id_type=MESH)
    def chunk(c): return pl.ds(pl.multiple_of(c*cg,cg),cg)
    def rows(rank,c): return pl.ds(pl.multiple_of(c*cg+rank*cr,cr),cr)
    def half(rank): return pl.ds(pl.multiple_of(rank*cr,cr),cr)
    def loc(c): return pl.ds(pl.multiple_of(c*cr,cr),cr)
    def rs_copy(k,c):
        return pltpu.make_async_remote_copy(sbuf.at[k-1,loc(c)],rbuf.at[k-1,loc(c)],ssem.at[k,c],rsem.at[k,c],device_id=partner,device_id_type=MESH)
    def ag_copy(k,buf,c,rank):
        return pltpu.make_async_remote_copy(buf.at[rows(rank,c)],buf.at[rows(rank,c)],ssem.at[k,c],rsem.at[k,c],device_id=partner,device_id_type=MESH)
    def cols(rank): return pl.ds(pl.multiple_of(rank*width,128),width)
    def ctx_copy(c,rank):
        return pltpu.make_async_remote_copy(ctx.at[rows(1-rank,c)],ctxo.at[loc(c),cols(rank)],ssem.at[0,c],rsem.at[0,c],device_id=partner,device_id_type=MESH)
    def dctx_copy(c,rank):
        return pltpu.make_async_remote_copy(dcs.at[loc(c),cols(1-rank)],dcall.at[rows(rank,c)],ssem.at[5,c],rsem.at[5,c],device_id=partner,device_id_type=MESH)
    early[...]=jnp.zeros_like(early)
    early[10:11]=jnp.full_like(early[10:11],-jnp.inf)
    def whole(w): return w[...].reshape(dm,w.shape[2])
    def strip(w,cs): return w[:,:,cs].reshape(dm,TF)
    dkv[...]=jnp.zeros_like(dkv)
    lane=lax.broadcasted_iota(jnp.int32,(1,128),1)
    scale=jnp.bfloat16(HD**-0.5); zero=jnp.bfloat16(0)
    q4=ff//2
    groups=[(act,0,0,width),(act,width,width,width),(act,2*width,2*width,width),(wo,0,n,wide),
            (wup,0,n+wide,q4),(wup,q4,n+wide+q4,q4),(wdn,0,n+wide+ff,q4),(wdn,q4,n+wide+ff+q4,q4)]
    def block(z_,xx): return (z_*2+xx)*2+core
    me=block(z,x_)
    def place(g,b):
        buf,c0,_,nc=groups[g]
        return buf.at[b,:,c0:c0+nc]
    def z_hop(g,k,b): return remote(sh.at[:,groups[g][2]:groups[g][2]+groups[g][3]],place(g,b),azs.at[g,k-1],azr.at[g,k-1],zp[k-1])
    def x_hop(g,k,b): return remote(sh.at[:,groups[g][2]:groups[g][2]+groups[g][3]] if k==0 else place(g,b),place(g,b),axs.at[g,k],axr.at[g,k],xp)
    def c_hop(g,k,b): return remote(sh.at[:,groups[g][2]:groups[g][2]+groups[g][3]] if k==0 else place(g,b),place(g,b),acs.at[g,k],acr.at[g,k],sib)
    def back(k): return (z-k)%4
    def gather_start(g):
        buf,c0,s0,nc=groups[g]
        for k in (1,2,3): z_hop(g,k,me).start()
        x_hop(g,0,me).start()
        c_hop(g,0,me).start()
        buf[me,:,c0:c0+nc]=sh[:,s0:s0+nc]
    def gather_sent(g):
        for k in (1,2,3): z_hop(g,k,me).wait_send()
    def gather_x(g):
        for k in (1,2,3):
            b=block(back(k),x_)
            z_hop(g,k,b).wait_recv()
            x_hop(g,k,b).start()
            c_hop(g,k,b).start()
    def gather_core(g):
        for k in (0,1,2,3):
            b=block(back(k),1-x_)
            x_hop(g,k,b).wait_recv()
            c_hop(g,4+k,b).start()
    def gather_done(g):
        for k in range(8): c_hop(g,k,me).wait_recv()
        for k in range(4): x_hop(g,k,me).wait_send()
        for k in range(8): c_hop(g,k,me).wait_send()
    own_copies=[local(tok.at[c*cr:(c+1)*cr],hall.at[rows(t,c)],1+c) for c in range(NC)]
    for c in own_copies: c.start()
    pl.semaphore_wait(barrier,len(everyone))
    gather_start(0)
    def tok_copy(c): return remote(tok.at[loc(c)],hall.at[rows(t,c)],ts.at[c],tr.at[c],partner)
    def mine_o(rank): return sh.at[:,pl.ds(pl.multiple_of(n+rank*width,128),width)]
    o_swap=remote(mine_o(t),mine_o(t),ts.at[NC],tr.at[NC],partner)
    sh[:,pl.ds(pl.multiple_of(n+t*width,128),width)]=wos[...].T
    o_swap.start()
    @pl.loop(0,NC)
    def _(c): tok_copy(c).start()
    sh[:,n+wide:n+wide+ff]=wu[...]
    sh[:,n+wide+ff:]=wds[...].T
    gather_sent(0); gather_start(1)
    gather_x(0)
    gather_sent(1); gather_start(2)
    gather_x(1)
    gather_core(0)
    o_swap.wait_recv()
    gather_sent(2); gather_start(3)
    gather_x(2)
    gather_core(1); gather_core(2)
    for g in range(3): gather_done(g)
    for c in own_copies: c.wait()
    TF=512
    @pl.loop(0,NC)
    def _(c):
        tok_copy(c).wait_recv()
        @pl.loop(0,n//TF)
        def _(j):
            cs=pl.ds(pl.multiple_of(j*TF,TF),TF)
            qkv[chunk(c),cs]=(dot(hall[chunk(c)],strip(act,cs),NN)+bias[:,cs]).astype(BF)
    x_out=local(hall,x_hbm,5); w_out=local(act.at[:,:,0:n],wh_hbm,6)
    x_out.start(); w_out.start()
    gather_sent(3); gather_start(4)
    gather_x(3)
    ones=jnp.where(lax.broadcasted_iota(jnp.int32,(16,rows_all),0)==0,1.0,0.0).astype(BF)
    @pl.loop(0,pairs)
    def _(p):
        ck=pl.multiple_of(width+p*128,128); cv=pl.multiple_of(2*width+p*128,128)
        kt[p]=qkv[:,pl.ds(ck,128)].T
        v=qkv[:,pl.ds(cv,128)].T
        vt[2*p,0:64]=v[0:64]; vt[2*p,64:80]=ones
        vt[2*p+1,0:64]=v[64:128]; vt[2*p+1,64:80]=ones
    x_out.wait()
    def split(k,c):
        sbuf[k-1,loc(c)]=pch[half(1-t)].astype(BF)
        rs_copy(k,c).start()
        part[loc(c)]=pch[half(t)]
    def stats(v):
        cen=v-jnp.mean(v,axis=1,keepdims=True)
        r=lax.rsqrt(jnp.mean(cen*cen,axis=1,keepdims=True)+EPSILON)
        return cen*r,r
    def lo_copy(c): return pltpu.make_async_copy(cl.at[loc(c)],lo_hbm.at[loc(c)],losem.at[c])
    def out_copy(slot,col):
        return pltpu.make_async_copy(stage.at[slot],dw.at[:,:,:,:,pl.ds(pl.multiple_of(col,512),512)],osem.at[slot])
    def wgrad(slot,left,right_ref,rcol,ocol):
        @pl.loop(0,dm//256)
        def _(i):
            ms=pl.ds(pl.multiple_of(i*256,256),256)
            right=right_ref[:,pl.ds(pl.multiple_of(rcol,512),512)] if len(right_ref.shape)==2 else strip(right_ref,pl.ds(pl.multiple_of(rcol,512),512))
            stage[slot,i]=dot(left[ms],right,NN).astype(BF).reshape(2,2,64,512)
        out_copy(slot,ocol).start()
    def stage_a(c):
        rs=chunk(c)
        @pl.loop(0,pairs)
        def _(p):
            cq=pl.ds(pl.multiple_of(p*128,128),128); ck=pl.ds(pl.multiple_of(width+p*128,128),128)
            pks=[]
            for h in (0,1):
                keep=(lane<64) if h==0 else (lane>=64)
                q=jnp.where(keep,qkv[rs,cq]*scale,zero)
                st=dot(qkv[:,ck],q,NT)
                m=jnp.max(st,axis=0,keepdims=True)
                mc=m*LOG2E
                pt=jnp.exp2(st*LOG2E-mc).astype(BF)
                ot=dot(vt[2*p+h],pt,NN)
                tot=ot[64:65]
                ctt[h*64:(h+1)*64,:]=ot[0:64]*(1.0/tot)
                lse[pl.ds(2*p+h,1),rs]=mc+jnp.log2(tot)
                pks.append(jnp.max(m,axis=1,keepdims=True))
            early[10:11,cq]=jnp.maximum(early[10:11,cq],jnp.where(lane<64,pks[0],pks[1]))
            ctx[rs,cq]=ctt[...].T.astype(BF)
            step=c*pairs+p
            @pl.when(step==4)
            def _():
                gather_core(3)
                gather_done(3)
            @pl.when(step==5)
            def _():
                gather_sent(4); gather_start(5)
                gather_x(4)
            @pl.when(step==11)
            def _():
                gather_sent(5); gather_start(6)
                gather_x(5)
                gather_core(4)
        ctx_copy(c,t).start()
        ctxo[loc(c),cols(t)]=ctx[rows(t,c)]
    def stage_b(c):
        ctx_copy(c,1-t).wait_recv()
        x,r=stats(hall[rows(t,c)].astype(F32)+dot(ctxo[loc(c)],whole(wo),NT)+vec[0:1])
        xh[loc(c)]=x
        rst[loc(c)]=jnp.broadcast_to(r,(cr,128))
        hall[rows(t,c)]=(x*vec[1:2]+vec[2:3]).astype(BF)
        ag_copy(3,hall,c,t).start()
    def stage_c(c):
        rs=chunk(c)
        ag_copy(3,hall,c,1-t).wait_recv()
        @pl.loop(0,ff//TF)
        def _(j):
            cs=pl.ds(pl.multiple_of(j*TF,TF),TF)
            u=dot(hall[rs],strip(wup,cs),NN)+upb[:,cs]
            cdf=0.5*(1.0+lax.erf(u*0.5**0.5))
            act[pl.ds(4*c,4),:,cs]=(u*cdf).astype(BF).reshape(4,64,TF)
            slp[rs,cs]=(cdf+u*jnp.exp(-0.5*u*u)*(0.5/math.pi)**0.5).astype(BF)
        @pl.when(c==0)
        def _():
            gather_sent(6); gather_start(7)
            gather_x(6)
            gather_core(6)
            gather_sent(7); gather_x(7)
            gather_core(7)
            gather_done(6); gather_done(7)
        pch[...]=dot(act[pl.ds(4*c,4)].reshape(cg,ff),whole(wdn),NT)
        split(1,c)
    def stage_d(c):
        rs_copy(1,c).wait_recv()
        x,r=stats(xh[loc(c)]*vec[1:2]+vec[2:3]+part[loc(c)]+rbuf[0,loc(c)].astype(F32)+vec[3:4])
        dy=cl[loc(c)].astype(F32)
        cl[loc(c)]=(x*vec[4:5]+vec[5:6]).astype(BF)
        lo_copy(c).start()
        early[4:5]+=jnp.sum(dy*x,axis=0,keepdims=True)
        early[5:6]+=jnp.sum(dy,axis=0,keepdims=True)
        dx=dy*vec[4:5]
        g=r*(dx-jnp.mean(dx,axis=1,keepdims=True)-x*jnp.mean(dx*x,axis=1,keepdims=True))
        gf[loc(c)]=g
        gb=g.astype(BF)
        early[3:4]+=jnp.sum(gb.astype(F32),axis=0,keepdims=True)
        ball[rows(t,c)]=gb
        ag_copy(4,ball,c,t).start()
        tb[:,rows(t,c)]=gb.T
    def stage_e(c):
        rs=chunk(c)
        ag_copy(4,ball,c,1-t).wait_recv()
        @pl.loop(0,ff//TF)
        def _(j):
            cs=pl.ds(pl.multiple_of(j*TF,TF),TF)
            gu=(dot(ball[rs],strip(wdn,cs),NN)*slp[rs,cs].astype(F32)).astype(BF)
            slp[rs,cs]=gu
            row=pl.ds(8+j*TF//dm,1); cc=pl.ds(pl.multiple_of(j*TF%dm,TF),TF)
            early[row,cc]+=jnp.sum(gu.astype(F32),axis=0,keepdims=True)
        pch[...]=dot(slp[rs],whole(wup),NT)
        split(2,c)
        tb[:,rows(1-t,c)]=ball[rows(1-t,c)].T
        th[:,chunk(c)]=hall[chunk(c)].T
    def stage_f(c):
        rs_copy(2,c).wait_recv()
        dy=gf[loc(c)]+part[loc(c)]+rbuf[1,loc(c)].astype(F32)
        x=xh[loc(c)]; r=rst[loc(c)][:,0:1]
        early[1:2]+=jnp.sum(dy*x,axis=0,keepdims=True)
        early[2:3]+=jnp.sum(dy,axis=0,keepdims=True)
        dx=dy*vec[1:2]
        g=r*(dx-jnp.mean(dx,axis=1,keepdims=True)-x*jnp.mean(dx*x,axis=1,keepdims=True))
        gf[loc(c)]=g
        gb=g.astype(BF)
        early[0:1]+=jnp.sum(gb.astype(F32),axis=0,keepdims=True)
        ga[loc(c)]=gb
        dcs[loc(c)]=dot(gb,whole(wo),NN).astype(BF)
        dctx_copy(c,t).start()
        dcall[rows(t,c)]=dcs[loc(c),cols(t)]
    def stage_g(c):
        rs=chunk(c)
        dctx_copy(c,1-t).wait_recv()
        @pl.loop(0,pairs)
        def _(p):
            cq=pl.ds(pl.multiple_of(p*128,128),128); ck=pl.ds(pl.multiple_of(width+p*128,128),128); cv=pl.ds(pl.multiple_of(2*width+p*128,128),128)
            prod=(ctx[rs,cq].astype(F32)*dcall[rs,cq].astype(F32)).T
            dl[0:1]=jnp.sum(prod[0:64],axis=0,keepdims=True)
            dl[1:2]=jnp.sum(prod[64:128],axis=0,keepdims=True)
            for h in (0,1):
                keep=(lane<64) if h==0 else (lane>=64)
                q=jnp.where(keep,qkv[rs,cq]*scale,zero)
                do=jnp.where(keep,dcall[rs,cq],zero)
                st=dot(qkv[:,ck],q,NT)
                pt=jnp.exp2(st*LOG2E-lse[pl.ds(2*p+h,1),rs])
                dpt=dot(qkv[:,cv],do,NT)
                ds=(pt*(dpt-dl[h:h+1])).astype(BF)
                dkv[1,:,cq]+=dot(pt.astype(BF),do,NN)
                dkv[0,:,cq]+=dot(ds,q,NN)
                dqt[h*64:(h+1)*64,:]=dot(kt[p,h*64:(h+1)*64,:],ds,NN)
            qkv[rs,cq]=(dqt[...].T*(HD**-0.5)).astype(BF)
    def grad_down(c):
        slot=c%2
        @pl.when(c>=2)
        def _(): out_copy(slot,0).wait()
        wgrad(slot,tb,act,c*512,wide+ff+c*512)
    def grad_up(c):
        slot=c%2
        @pl.when(c>=2)
        def _(): out_copy(slot,0).wait()
        wgrad(slot,th,slp,c*512,wide+c*512)
    def grad_out():
        @pl.loop(0,NC)
        def _(c): tb[:,loc(c)]=ga[loc(c)].T
        for j in range(wide//512):
            @pl.loop(0,dm//256)
            def _(i):
                ms=pl.ds(pl.multiple_of(i*256,256),256)
                stage[j%2,i]=dot(tb[ms,0:own],ctxo[:,j*512:(j+1)*512],NN).astype(BF).reshape(2,2,64,512)
            out_copy(j%2,j*512).start()
    @pl.loop(0,NC)
    def _(c):
        stage_a(c)
        @pl.when(c>0)
        def _(): stage_b(c-1)
    cot_load.wait(); w_out.wait()
    gather_core(5)
    gather_done(4); gather_done(5)
    @pl.loop(0,NC)
    def _(c):
        stage_c(c)
        @pl.when(c==0)
        def _(): stage_b(NC-1)
        @pl.when(c>=2)
        def _(): stage_d(c-2)
    @pl.loop(NC-2,NC)
    def _(c): stage_d(c)
    @pl.loop(0,NC)
    def _(c): stage_e(c)
    base=(wide+ff,wide)
    def s1(g): return remote(dw.at[:,:,1-core,:,base[g]:base[g]+ff],r1.at[g],g1s.at[g],g1r.at[g],sib)
    def s2(g): return remote(wup.at[8+4*g:12+4*g],r2.at[g],g2s.at[g],g2r.at[g],xp)
    def s3(k): return remote(wdn.at[12+(z+k)%4],r3.at[3-k],g3s.at[k-1],g3r.at[k-1],zp[k-1])
    def load2(g): return [pltpu.make_async_copy(dw.at[:,1-x_,core,:,base[g]:base[g]+ff],wup.at[0:4],rl.at[0]),
                          pltpu.make_async_copy(r1.at[g,:,1-x_],wup.at[4:8],rl.at[1])]
    def load3(): return [pltpu.make_async_copy(dw.at[:,x_,core,:,base[0]:base[0]+ff],wdn.at[0:4],rl.at[2]),
                         pltpu.make_async_copy(r1.at[0,:,x_],wdn.at[4:8],rl.at[3]),
                         pltpu.make_async_copy(r2.at[0],wdn.at[8:12],rl.at[4])]
    def add2(g):
        for c in load2(g): c.wait()
        @pl.loop(0,4)
        def _(i): wup[8+4*g+i]=(wup[i].astype(F32)+wup[4+i].astype(F32)).astype(BF)
    @pl.loop(0,NC)
    def _(c): grad_down(c)
    out_copy(0,0).wait()
    out_copy(1,0).wait()
    s1(0).start()
    @pl.loop(0,NC)
    def _(c):
        stage_f(c)
        grad_up(c)
        @pl.when(c==1)
        def _():
            s1(0).wait_recv()
            for l in load2(0): l.start()
        @pl.when(c==2)
        def _():
            add2(0)
            s2(0).start()
    out_copy(0,0).wait()
    out_copy(1,0).wait()
    s1(1).start()
    grad_out()
    @pl.loop(0,NC)
    def _(c):
        stage_g(c)
        @pl.when(c==0)
        def _():
            s1(1).wait_recv()
            for l in load2(1): l.start()
        @pl.when(c==1)
        def _():
            add2(1)
            s2(0).wait_send()
            s2(1).start()
            s2(0).wait_recv()
            for l in load3(): l.start()
        @pl.when(c==2)
        def _():
            for l in load3(): l.wait()
            @pl.loop(0,4)
            def _(i): wdn[12+i]=(wdn[i].astype(F32)+wdn[4+i].astype(F32)+wdn[8+i].astype(F32)).astype(BF)
            for k in (1,2,3): s3(k).start()
    @pl.loop(0,pairs)
    def _(p):
        cq=pl.ds(pl.multiple_of(p*128,128),128); ck=pl.ds(pl.multiple_of(width+p*128,128),128); cv=pl.ds(pl.multiple_of(2*width+p*128,128),128)
        qkv[:,ck]=dkv[0,:,cq].astype(BF)
        qkv[:,cv]=dkv[1,:,cq].astype(BF)
    dq_out=pltpu.make_async_copy(qkv,dqkv_hbm,dsem.at[0])
    dq_out.start()
    out_copy(0,0).wait()
    out_copy(1,0).wait()
    dq_out.wait()
    o_swap.wait_send()
    for g in (0,1): s1(g).wait_send()
    s2(1).wait()
    for k in (1,2,3): s3(k).wait()
    @pl.loop(0,NC)
    def _(c):
        lo_copy(c).wait()
        ctx_copy(c,t).wait_send(); dctx_copy(c,t).wait_send(); tok_copy(c).wait_send()
        for k in (1,2): rs_copy(k,c).wait_send()
        for k,buf in ((3,hall),(4,ball)): ag_copy(k,buf,c,t).wait_send()

def main_call(shards,tok,cot,bias,vec,upb,cid):
    V=pl.BlockSpec(memory_space=pltpu.VMEM); A=pl.BlockSpec(memory_space=pl.ANY)
    width=shards[0].shape[1]; ff=shards[4].shape[1]; own,dm=tok.shape; rows=2*own; n=3*width; cr=own//NC; wide=2*width
    S=jax.ShapeDtypeStruct; M=pltpu.VMEM; D=pltpu.SemaphoreType.DMA
    return pl.pallas_call(main_kernel,
      out_shape=(S((own,dm),BF),S((own,dm),F32),S((rows,n),BF),S((4,2,2,64,wide+2*ff),BF),S((2,4,2,64,ff),BF),S((2,4,64,ff),BF),S((3,64,ff),BF),S((16,dm),F32),S((rows,dm),BF),S((16,64,n),BF)),
      in_specs=[V]*6+[A,A,V,V,V],out_specs=(A,V,A,A,A,A,A,V,A,A),
      scratch_shapes=[M((64,n+wide+2*ff),BF),M((rows,n),BF),M((width//HD,80,rows),BF),M((width//128,128,rows),BF),M((rows,width),BF),M((own,wide),BF),M((width//HD,rows),F32),M((own,dm),BF),
        M((16,64,wide),BF),M((16,64,ff),BF),M((16,64,ff),BF),
        M((own,dm),F32),M((own,128),F32),
        M((rows,dm),BF),M((16,64,ff),BF),M((rows,ff),BF),M((rows,dm),BF),M((own,dm),BF),M((own,wide),BF),M((rows,width),BF),
        M((own,dm),F32),M((2*cr,dm),F32),M((128,2*cr),F32),M((128,2*cr),F32),M((8,2*cr),F32),M((2,rows,width),F32),
        M((2,own,dm),BF),M((2,own,dm),BF),
        M((dm,rows),BF),M((dm,rows),BF),M((2,4,2,2,64,512),BF),
        D((7,)),D((NC,)),D((1,)),D((2,)),D((6,NC)),D((6,NC)),D((5,)),D((2,)),D((2,)),D((2,)),D((2,)),D((3,)),D((3,)),
        D((NC+1,)),D((NC+1,)),D((8,3)),D((8,3)),D((8,4)),D((8,4)),D((8,8)),D((8,8))],
      compiler_params=pltpu.CompilerParams(collective_id=cid,has_side_effects=True,vmem_limit_bytes=61*2**20),
      name="main")(*shards,tok,cot,bias,vec,upb)

def tail_kernel(dqkv_ref,dw,r1w,r2w,r3w,w_hbm,x_hbm,gf,early,wqk,bq,lim,
                tg,gq,gk,gv,go,gu,gd,sums,late,qc,kc,qbc,
                xv,xt,wv,part,pc,dwh,ysb,yrb,fw,zu,su,ru,oo,o1,o2s,o2,o3s,o3,h1,h2s,h2,h3s,h3,osb,orb,eb,er,lb,lr,
                lsem,s1s,s1r,s2s,s2r,s3s,s3r,ysend,yrecv,es,erc,ls,lrc,os_,or_):
    d=lax.axis_index("dp"); t=lax.axis_index("tensor")
    core=d%2; x=(d//2)%2; z=d//4
    def dev(z_,x_,c_): return ((z_*2+x_)*2+c_,t)
    sib=dev(z,x,1-core); xp=dev(z,1-x,core); yp=(d,1-t)
    zp=[dev((z+k)%4,x,core) for k in (1,2,3)]
    zb=[dev(z+1-2*(z%2),x,core),dev((z+2)%4,x,core)]
    barrier=pltpu.get_barrier_semaphore()
    everyone=[sib,xp,yp]+zp
    for p in everyone: pl.semaphore_signal(barrier,inc=1,device_id=p,device_id_type=MESH)
    own,dm=gf.shape; rows,n=dqkv_ref.shape; width=n//3; cr=own//NC; ff=fw.shape[2]; wide=2*width
    def remote(src,dst,a,b,p): return pltpu.make_async_remote_copy(src,dst,a,b,device_id=p,device_id_type=MESH)
    def local(src,dst,i): return pltpu.make_async_copy(src,dst,lsem.at[i])
    f32=lambda a:a.astype(F32)
    wcols=slice(wide+ff,wide+2*ff); ucols=slice(wide,wide+ff)
    loads=[local(dw.at[:,x,core,:,ucols],zu.at[0],0),local(r1w.at[1,:,x],zu.at[1],1),local(r2w.at[1],zu.at[2],2),
           local(dw.at[:,:,core,:,0:wide],oo,3),local(w_hbm.at[:,:,:],wv,4),local(x_hbm,xv,5),
           local(dw.at[z,x,core,:,wcols],fw.at[0],6),local(r1w.at[0,z,x],fw.at[1],7),local(r2w.at[0,z],fw.at[2],8),
           local(r3w.at[0],fw.at[3],9),local(r3w.at[1],fw.at[4],10),local(r3w.at[2],fw.at[5],11)]
    for c in loads: c.start()
    eb[0]=early[...]
    lb[0]=jnp.zeros_like(lb[0])
    pl.semaphore_wait(barrier,len(everyone))
    o_s1=remote(dw.at[:,:,1-core,:,0:wide],o1,s1s.at[0],s1r.at[0],sib); o_s1.start()
    h_s1=remote(dwh.at[:,:,1-core],h1,s1s.at[1],s1r.at[1],sib)
    o_s2=remote(o2s,o2,s2s.at[0],s2r.at[0],xp)
    h_s2=remote(h2s,h2,s2s.at[1],s2r.at[1],xp)
    def z3(g,src,dst): return [remote(src.at[(z+k)%4],dst.at[3-k],s3s.at[g,k-1],s3r.at[g,k-1],zp[k-1]) for k in (1,2,3)]
    u_s3=z3(0,su,ru); o_s3=z3(1,o3s,o3); h_s3=z3(2,h3s,h3)
    hops=[sib,xp,zb[0],zb[1],yp]
    def ecopy(i): return remote(eb.at[i],er.at[i],es.at[i],erc.at[i],hops[i])
    def eadd(i):
        ecopy(i).wait_recv()
        b=eb[i,8:16]; c=er[i,8:16]
        if i<4:
            r=lax.broadcasted_iota(jnp.int32,b.shape,0)
            b=jnp.where(r==2,jnp.maximum(b,c),b+c)
        eb[i+1,0:8]=eb[i,0:8]+er[i,0:8]; eb[i+1,8:16]=b
    def lcopy(i): return remote(lb.at[i],lr.at[i],ls.at[i],lrc.at[i],hops[i])
    def ladd(i):
        lcopy(i).wait_recv()
        lb[i+1]=lb[i]+lr[i]
    ecopy(0).start()
    for i in (0,1,2): loads[i].wait()
    @pl.loop(0,4)
    def _(i): su[i]=(f32(zu[0,i])+f32(zu[1,i])+f32(zu[2,i])).astype(BF)
    for c in u_s3: c.start()
    loads[4].wait()
    def ycopy(c): return remote(ysb.at[c],yrb.at[c],ysend.at[c],yrecv.at[c],yp)
    @pl.loop(0,NC)
    def _(c):
        pc[...]=dot(dqkv_ref[pl.ds(pl.multiple_of(2*c*cr,2*cr),2*cr)],wv[...].reshape(dm,n),NT)
        ysb[c]=pc[pl.ds(pl.multiple_of((1-t)*cr,cr),cr)].astype(BF)
        ycopy(c).start()
        part[c]=pc[pl.ds(pl.multiple_of(t*cr,cr),cr)]
    lb[0,0:1,0:width]=jnp.sum(f32(dqkv_ref[:,0:width]),axis=0,keepdims=True)
    lb[0,0:1,width:2*width]=jnp.sum(f32(dqkv_ref[:,2*width:]),axis=0,keepdims=True)
    lcopy(0).start()
    eadd(0); ecopy(1).start()
    o_s1.wait_recv(); loads[3].wait()
    @pl.loop(0,4)
    def _(i): o2s[i]=(f32(oo[i,1-x])+f32(o1[i,1-x])).astype(BF)
    o_s2.start()
    loads[5].wait()
    @pl.loop(0,rows//256)
    def _(c):
        cs=pl.ds(pl.multiple_of(c*256,256),256)
        xt[:,cs]=xv[cs].T
    eadd(1); ecopy(2).start()
    @pl.loop(0,4)
    def _(i):
        ms=pl.ds(pl.multiple_of(i*256,256),256)
        for j in range(n//512):
            dwh[i,:,:,:,j*512:(j+1)*512]=dot(xt[ms],dqkv_ref[:,j*512:(j+1)*512],NN).astype(BF).reshape(2,2,64,512)
    h_s1.start()
    ladd(0); lcopy(1).start()
    eadd(2); ecopy(3).start()
    h_s1.wait_recv()
    @pl.loop(0,4)
    def _(i): h2s[i]=(f32(dwh[i,1-x,core])+f32(h1[i,1-x])).astype(BF)
    o_s2.wait_recv()
    @pl.loop(0,4)
    def _(i): o3s[i]=(f32(oo[i,x])+f32(o1[i,x])+f32(o2[i])).astype(BF)
    o_s2.wait_send()
    h_s2.start()
    ladd(1); lcopy(2).start()
    eadd(3); ecopy(4).start()
    for i in range(6,12): loads[i].wait()
    v=f32(fw[0])+f32(fw[1])+f32(fw[2])
    v=v+f32(fw[3])+f32(fw[4])+f32(fw[5])
    gd[...]=v.T
    ladd(2); lcopy(3).start()
    eadd(4)
    sums[...]=eb[5]
    pk=eb[4,10:11,0:width]
    sc=jnp.sqrt(lim[...]/jnp.maximum(pk,lim[...]))
    qc[...]=(f32(wqk[0])*sc).astype(BF); kc[...]=(f32(wqk[1])*sc).astype(BF)
    qbc[...]=(bq[...]*sc).astype(BF)
    for c in u_s3: c.wait_send()
    for c in o_s3: c.start()
    for c in u_s3: c.wait_recv()
    v=f32(zu[0,z])+f32(zu[1,z])+f32(zu[2,z])
    gu[...]=v+f32(ru[0])+f32(ru[1])+f32(ru[2])
    for c in range(NC):
        ycopy(c).wait_recv()
        lo_=slice(c*cr,(c+1)*cr)
        tg[lo_]=(gf[lo_]+part[c]+f32(yrb[c])).astype(BF)
    ladd(3)
    late[...]=lb[4]
    h_s2.wait_recv()
    @pl.loop(0,4)
    def _(i): h3s[i]=(f32(dwh[i,x,core])+f32(h1[i,x])+f32(h2[i])).astype(BF)
    for c in o_s3: c.wait_send()
    for c in h_s3: c.start()
    for c in o_s3: c.wait_recv()
    v=f32(oo[z,x])+f32(o1[z,x])+f32(o2[z])
    v=v+f32(o3[0])+f32(o3[1])+f32(o3[2])
    osb[0]=v[:,0:width]; osb[1]=v[:,width:]
    ocopy=remote(osb.at[1-t],orb,os_,or_,yp)
    ocopy.start()
    ocopy.wait_recv()
    go[...]=(osb[t]+orb[...]).T
    for c in h_s3: c.wait_recv()
    v=f32(dwh[z,x,core])+f32(h1[z,x])+f32(h2[z])
    v=v+f32(h3[0])+f32(h3[1])+f32(h3[2])
    gq[...]=v[:,0:width]; gk[...]=v[:,width:2*width]; gv[...]=v[:,2*width:]
    for c in [o_s1,h_s1,h_s2,ocopy]+h_s3: c.wait_send()
    for i in range(5): ecopy(i).wait_send()
    for i in range(4): lcopy(i).wait_send()
    for c in range(NC): ycopy(c).wait_send()

def tail_call(dqkv,dw,r1,r2,r3,w,xall,gf,early,wqk,bq,lim,cid):
    V=pl.BlockSpec(memory_space=pltpu.VMEM); A=pl.BlockSpec(memory_space=pl.ANY)
    S=jax.ShapeDtypeStruct; D=pltpu.SemaphoreType.DMA; M=pltpu.VMEM
    own,dm=gf.shape; rows,n=dqkv.shape; width=n//3; cr=own//NC
    ff=r3.shape[2]; wide=2*width
    return pl.pallas_call(tail_kernel,
      out_shape=(S((own,dm),BF),S((64,width),F32),S((64,width),F32),S((64,width),F32),S((width,64),F32),S((64,ff),F32),S((ff,64),F32),
                 S((16,1024),F32),S((8,1024),F32),S((64,width),BF),S((64,width),BF),S((1,width),BF)),
      in_specs=[V]+[A]*6+[V]*5,out_specs=(V,)*12,
      scratch_shapes=[M((rows,dm),BF),M((dm,rows),BF),M((16,64,n),BF),M((NC,cr,dm),F32),M((2*cr,dm),F32),M((4,2,2,64,n),BF),M((NC,cr,dm),BF),M((NC,cr,dm),BF),
        M((6,64,ff),BF),M((3,4,64,ff),BF),M((4,64,ff),BF),M((3,64,ff),BF),
        M((4,2,64,wide),BF),M((4,2,64,wide),BF),M((4,64,wide),BF),M((4,64,wide),BF),M((4,64,wide),BF),M((3,64,wide),BF),
        M((4,2,64,n),BF),M((4,64,n),BF),M((4,64,n),BF),M((4,64,n),BF),M((3,64,n),BF),M((2,64,width),F32),M((64,width),F32),
        M((6,16,1024),F32),M((5,16,1024),F32),M((5,8,1024),F32),M((4,8,1024),F32),
        D((12,)),D((2,)),D((2,)),D((2,)),D((2,)),D((3,3)),D((3,3)),D((NC,)),D((NC,)),D((5,)),D((5,)),D((4,)),D((4,)),D,D],
      compiler_params=pltpu.CompilerParams(collective_id=cid,has_side_effects=True,vmem_limit_bytes=61*2**20),
      name="tail")(dqkv,dw,r1,r2,r3,w,xall,gf,early,wqk,bq,lim)

def per_device_pair(tokens,query_weight,query_bias,key_weight,value_weight,value_bias,out_weight,out_bias,first_gain,first_shift,
    up_weight,up_bias,down_weight,down_bias,second_gain,second_shift,cotangent,clip_limit):
    width=query_weight.shape[1]; ff=up_weight.shape[1]; dm=tokens.shape[1]
    f=lambda a:a.astype(F32)
    bias=jnp.concatenate([f(query_bias),jnp.zeros((width,),F32),f(value_bias)])[None]
    z=jnp.zeros((dm,),F32)
    vec=jnp.stack([f(out_bias),f(first_gain),f(first_shift),f(down_bias),f(second_gain),f(second_shift),z,z])
    shards=(query_weight,key_weight,value_weight,out_weight,up_weight,down_weight)
    lo,gf,dqkv,dw,r1,r2,r3,early,xall,wh=main_call(shards,tokens,cotangent,bias,vec,f(up_bias)[None],1)
    wqk=jnp.stack([query_weight,key_weight])
    lim=jnp.repeat(clip_limit,HD)[None]
    tg,gq,gk,gv,go,gu,gd,sums,late,qc,kc,qbc=tail_call(dqkv,dw,r1,r2,r3,wh,xall,gf,early,wqk,f(query_bias)[None],lim,2)
    return (lo,tg,gq,late[0,:width],gk,gv,late[0,width:2*width],go,sums[0],sums[1],sums[2],gu,sums[8:10].reshape(ff),gd,
      sums[3],sums[4],sums[5],sums[10,:width:HD],qc,qbc[0],kc)


def layer(*args):
    paired = lax.axis_size("dp") == 16 and lax.axis_size("tensor") == 2 and 2 * args[0].shape[0] == LEN
    return per_device_pair(*args) if paired else per_device(*args)


def solution(mesh):
    in_specs = (
        P(("dp", "tensor"), None),
        P("dp", "tensor"),
        P("tensor"),
        P("dp", "tensor"),
        P("dp", "tensor"),
        P("tensor"),
        P("tensor", "dp"),
        P(),
        P(),
        P(),
        P("dp", "tensor"),
        P("tensor"),
        P("tensor", "dp"),
        P(),
        P(),
        P(),
        P(("dp", "tensor"), None),
        P("tensor"),
    )
    out_specs = (
        P(("dp", "tensor"), None),
        P(("dp", "tensor"), None),
        P("dp", "tensor"),
        P("tensor"),
        P("dp", "tensor"),
        P("dp", "tensor"),
        P("tensor"),
        P("tensor", "dp"),
        P(),
        P(),
        P(),
        P("dp", "tensor"),
        P("tensor"),
        P("tensor", "dp"),
        P(),
        P(),
        P(),
        P("tensor"),
        P("dp", "tensor"),
        P("tensor"),
        P("dp", "tensor"),
    )
    return jax.shard_map(
        layer, mesh=mesh, in_specs=in_specs, out_specs=out_specs, check_vma=False
    )
```

```python
import functools
import math

import jax
import jax.numpy as jnp
from jax import lax
from jax.experimental import pallas as pl
from jax.experimental.pallas import tpu as pltpu
from jax.sharding import PartitionSpec as P

HD = 64
LEN = 1024
QB = 512


def layer_norm(values, gain, shift):
    center = values - jnp.mean(values, axis=-1, keepdims=True)
    spread = jnp.mean(center * center, axis=-1, keepdims=True)
    return center * lax.rsqrt(spread + EPSILON) * gain + shift


def gelu_slope(upper):
    normal_cdf = 0.5 * (1.0 + lax.erf(upper * 0.5**0.5))
    return normal_cdf + upper * jnp.exp(-0.5 * upper * upper) * (0.5 / math.pi) ** 0.5


def contract_rows(left, right):
    return lax.dot_general(
        left, right, (((0,), (0,)), ((), ())), preferred_element_type=jnp.float32
    )


def contract_cols(left, right):
    return lax.dot_general(
        left, right, (((1,), (1,)), ((), ())), preferred_element_type=jnp.float32
    )


def per_device(
    tokens,
    query_weight,
    query_bias,
    key_weight,
    value_weight,
    value_bias,
    out_weight,
    out_bias,
    first_gain,
    first_shift,
    up_weight,
    up_bias,
    down_weight,
    down_bias,
    second_gain,
    second_shift,
    cotangent,
    clip_limit,
):
    query_full, key_full, value_full, out_full, up_full, down_full = (
        lax.all_gather(query_weight, "dp", axis=0, tiled=True),
        lax.all_gather(key_weight, "dp", axis=0, tiled=True),
        lax.all_gather(value_weight, "dp", axis=0, tiled=True),
        lax.all_gather(out_weight, "dp", axis=1, tiled=True),
        lax.all_gather(up_weight, "dp", axis=0, tiled=True),
        lax.all_gather(down_weight, "dp", axis=1, tiled=True),
    )
    width = query_full.shape[1]
    hidden_width = up_full.shape[1]
    heads_here = width // HD
    score_scale = HD ** (-0.5)
    joint_weight = jnp.concatenate([query_full, key_full, value_full], axis=1)
    gathered = lax.all_gather(tokens, "tensor", axis=0, tiled=True)
    group_rows = gathered.shape[0]
    seq_count = group_rows // LEN
    block_count = LEN // QB
    projected = jnp.dot(gathered, joint_weight, preferred_element_type=jnp.float32)
    queries = (projected[:, :width] + query_bias.astype(jnp.float32)).astype(jnp.bfloat16)
    keyset = projected[:, width : 2 * width].astype(jnp.bfloat16)
    valset = (projected[:, 2 * width :] + value_bias.astype(jnp.float32)).astype(jnp.bfloat16)
    query_seq = queries.reshape(seq_count, LEN, heads_here, HD)
    key_seq = keyset.reshape(seq_count, LEN, heads_here, HD)
    value_seq = valset.reshape(seq_count, LEN, heads_here, HD)

    def attend_block(block_id):
        seq_id = block_id // block_count
        row_start = block_id % block_count * QB
        query_rows = lax.dynamic_slice_in_dim(
            lax.dynamic_index_in_dim(query_seq, seq_id, 0, False), row_start, QB, 0
        )
        key_rows = lax.dynamic_index_in_dim(key_seq, seq_id, 0, False)
        value_rows = lax.dynamic_index_in_dim(value_seq, seq_id, 0, False)
        logits = (
            jnp.einsum("qhd,khd->hqk", query_rows, key_rows, preferred_element_type=jnp.float32)
            * score_scale
        )
        row_max = jnp.max(logits, axis=2, keepdims=True)
        exponent = jnp.exp(logits - row_max)
        totals = jnp.sum(exponent, axis=2, keepdims=True)
        probs_low = (exponent / totals).astype(jnp.bfloat16)
        context_rows = jnp.einsum(
            "hqk,khd->qhd", probs_low, value_rows, preferred_element_type=jnp.float32
        )
        return (
            context_rows.reshape(QB, width).astype(jnp.bfloat16),
            (row_max + jnp.log(totals))[:, :, 0],
            jnp.max(row_max, axis=(1, 2)),
        )

    context_blocks, log_totals, block_peaks = lax.map(
        attend_block, jnp.arange(seq_count * block_count)
    )
    context = context_blocks.reshape(group_rows, width)
    logit_peak = lax.pmax(jnp.max(block_peaks, axis=0), "dp")
    attention = lax.psum_scatter(
        jnp.dot(context, out_full, preferred_element_type=jnp.float32).astype(jnp.bfloat16),
        "tensor",
        scatter_dimension=0,
        tiled=True,
    ).astype(jnp.float32) + out_bias.astype(jnp.float32)
    first_resid = tokens.astype(jnp.float32) + attention
    hidden, first_pull = jax.vjp(
        layer_norm, first_resid, first_gain.astype(jnp.float32), first_shift.astype(jnp.float32)
    )
    hidden_all = lax.all_gather(hidden.astype(jnp.bfloat16), "tensor", axis=0, tiled=True)
    upper = jnp.dot(hidden_all, up_full, preferred_element_type=jnp.float32) + up_bias.astype(
        jnp.float32
    )
    acted = jax.nn.gelu(upper, approximate=False).astype(jnp.bfloat16)
    branch = lax.psum_scatter(
        jnp.dot(acted, down_full, preferred_element_type=jnp.float32).astype(jnp.bfloat16),
        "tensor",
        scatter_dimension=0,
        tiled=True,
    ).astype(jnp.float32) + down_bias.astype(jnp.float32)
    normed, second_pull = jax.vjp(
        layer_norm,
        hidden + branch,
        second_gain.astype(jnp.float32),
        second_shift.astype(jnp.float32),
    )
    layer_out = normed.astype(jnp.bfloat16)
    grad_second, second_gain_grad, second_shift_grad = second_pull(cotangent.astype(jnp.float32))
    grad_branch = grad_second.astype(jnp.bfloat16)
    down_bias_grad = jnp.sum(grad_branch, axis=0, dtype=jnp.float32)
    branch_all = lax.all_gather(grad_branch, "tensor", axis=0, tiled=True)
    grad_acted = contract_cols(branch_all, down_full)
    down_weight_grad = contract_rows(acted, branch_all)
    grad_upper = (grad_acted * gelu_slope(upper)).astype(jnp.bfloat16)
    up_bias_grad = jnp.sum(grad_upper, axis=0, dtype=jnp.float32)
    up_weight_grad = contract_rows(hidden_all, grad_upper)
    grad_hidden = grad_second + lax.psum_scatter(
        contract_cols(grad_upper, up_full).astype(jnp.bfloat16),
        "tensor",
        scatter_dimension=0,
        tiled=True,
    ).astype(jnp.float32)
    grad_first, first_gain_grad, first_shift_grad = first_pull(grad_hidden)
    grad_attn = grad_first.astype(jnp.bfloat16)
    out_bias_grad = jnp.sum(grad_attn, axis=0, dtype=jnp.float32)
    attn_all = lax.all_gather(grad_attn, "tensor", axis=0, tiled=True)
    grad_context = contract_cols(attn_all, out_full).astype(jnp.bfloat16)
    out_weight_grad = contract_rows(context, attn_all)
    query_blocks = queries.reshape(seq_count, block_count, QB, heads_here, HD)
    grad_blocks = grad_context.reshape(seq_count, block_count, QB, heads_here, HD)
    log_blocks = log_totals.reshape(seq_count, block_count, heads_here, QB)

    def sequence_back(item):
        query_part, grad_part, log_part, key_rows, value_rows = item

        def block_back(carry, piece):
            key_acc, value_acc = carry
            query_rows, grad_rows, log_rows = piece
            logits = (
                jnp.einsum("qhd,khd->hqk", query_rows, key_rows, preferred_element_type=jnp.float32)
                * score_scale
            )
            probs = jnp.exp(logits - log_rows[:, :, None])
            probs_low = probs.astype(jnp.bfloat16)
            value_acc = value_acc + jnp.einsum(
                "hqk,qhd->khd", probs_low, grad_rows, preferred_element_type=jnp.float32
            )
            grad_probs = jnp.einsum(
                "qhd,khd->hqk", grad_rows, value_rows, preferred_element_type=jnp.float32
            )
            inner = jnp.sum(probs * grad_probs, axis=2, keepdims=True)
            grad_logits = (probs * (grad_probs - inner)).astype(jnp.bfloat16)
            grad_query = (
                jnp.einsum(
                    "hqk,khd->qhd", grad_logits, key_rows, preferred_element_type=jnp.float32
                )
                * score_scale
            )
            key_acc = (
                key_acc
                + jnp.einsum(
                    "hqk,qhd->khd", grad_logits, query_rows, preferred_element_type=jnp.float32
                )
                * score_scale
            )
            return ((key_acc, value_acc), grad_query.astype(jnp.bfloat16))

        empty = jnp.zeros((LEN, heads_here, HD), jnp.float32)
        (key_acc, value_acc), grad_query_rows = lax.scan(
            block_back, (empty, empty), (query_part, grad_part, log_part)
        )
        return (grad_query_rows, key_acc.astype(jnp.bfloat16), value_acc.astype(jnp.bfloat16))

    grad_queries_all, grad_keys_all, grad_values_all = lax.map(
        sequence_back, (query_blocks, grad_blocks, log_blocks, key_seq, value_seq)
    )
    grad_joint = jnp.concatenate(
        [
            grad_queries_all.reshape(group_rows, width),
            grad_keys_all.reshape(group_rows, width),
            grad_values_all.reshape(group_rows, width),
        ],
        axis=1,
    )
    joint_grad = contract_rows(gathered, grad_joint)
    query_weight_grad = joint_grad[:, :width]
    key_weight_grad = joint_grad[:, width : 2 * width]
    value_weight_grad = joint_grad[:, 2 * width :]
    query_bias_grad = jnp.sum(grad_joint[:, :width], axis=0, dtype=jnp.float32)
    value_bias_grad = jnp.sum(grad_joint[:, 2 * width :], axis=0, dtype=jnp.float32)
    tokens_grad = (
        grad_first
        + lax.psum_scatter(
            contract_cols(grad_joint, joint_weight).astype(jnp.bfloat16),
            "tensor",
            scatter_dimension=0,
            tiled=True,
        ).astype(jnp.float32)
    ).astype(jnp.bfloat16)
    (
        query_weight_grad,
        key_weight_grad,
        value_weight_grad,
        out_weight_grad,
        up_weight_grad,
        down_weight_grad,
    ) = (
        lax.psum_scatter(
            query_weight_grad.astype(jnp.bfloat16), "dp", scatter_dimension=0, tiled=True
        ).astype(jnp.float32),
        lax.psum_scatter(
            key_weight_grad.astype(jnp.bfloat16), "dp", scatter_dimension=0, tiled=True
        ).astype(jnp.float32),
        lax.psum_scatter(
            value_weight_grad.astype(jnp.bfloat16), "dp", scatter_dimension=0, tiled=True
        ).astype(jnp.float32),
        lax.psum_scatter(
            out_weight_grad.astype(jnp.bfloat16), "dp", scatter_dimension=1, tiled=True
        ).astype(jnp.float32),
        lax.psum_scatter(
            up_weight_grad.astype(jnp.bfloat16), "dp", scatter_dimension=0, tiled=True
        ).astype(jnp.float32),
        lax.psum_scatter(
            down_weight_grad.astype(jnp.bfloat16), "dp", scatter_dimension=1, tiled=True
        ).astype(jnp.float32),
    )
    tensor_place = lax.axis_index("tensor")
    model_width = out_bias.shape[0]
    query_spread = lax.dynamic_update_slice_in_dim(
        jnp.zeros((model_width,), jnp.float32), query_bias_grad, tensor_place * width, 0
    )
    value_spread = lax.dynamic_update_slice_in_dim(
        jnp.zeros((model_width,), jnp.float32), value_bias_grad, tensor_place * width, 0
    )
    up_spread = lax.dynamic_update_slice_in_dim(
        jnp.zeros((hidden_width * lax.axis_size("tensor"),), jnp.float32),
        up_bias_grad,
        tensor_place * hidden_width,
        0,
    )
    (
        query_spread,
        value_spread,
        up_spread,
        out_bias_grad,
        down_bias_grad,
        first_gain_grad,
        first_shift_grad,
        second_gain_grad,
        second_shift_grad,
    ) = lax.psum(
        (
            query_spread,
            value_spread,
            up_spread,
            out_bias_grad,
            down_bias_grad,
            first_gain_grad,
            first_shift_grad,
            second_gain_grad,
            second_shift_grad,
        ),
        ("dp", "tensor"),
    )
    query_bias_grad = lax.dynamic_slice_in_dim(query_spread, tensor_place * width, width, 0)
    value_bias_grad = lax.dynamic_slice_in_dim(value_spread, tensor_place * width, width, 0)
    up_bias_grad = lax.dynamic_slice_in_dim(up_spread, tensor_place * hidden_width, hidden_width, 0)
    factor = clip_limit / jnp.maximum(logit_peak, clip_limit)
    column_scale = jnp.repeat(jnp.sqrt(factor), HD)
    query_clipped = (query_weight.astype(jnp.float32) * column_scale).astype(jnp.bfloat16)
    query_bias_clipped = (query_bias.astype(jnp.float32) * column_scale).astype(jnp.bfloat16)
    key_clipped = (key_weight.astype(jnp.float32) * column_scale).astype(jnp.bfloat16)
    return (
        layer_out,
        tokens_grad,
        query_weight_grad,
        query_bias_grad,
        key_weight_grad,
        value_weight_grad,
        value_bias_grad,
        out_weight_grad,
        out_bias_grad,
        first_gain_grad,
        first_shift_grad,
        up_weight_grad,
        up_bias_grad,
        down_weight_grad,
        down_bias_grad,
        second_gain_grad,
        second_shift_grad,
        logit_peak,
        query_clipped,
        query_bias_clipped,
        key_clipped,
    )


LOG2E=1.4426950408889634
NT=(((1,),(1,)),((),()))
NN=(((1,),(0,)),((),()))
F32=jnp.float32
BF=jnp.bfloat16
MESH=pl.DeviceIdType.MESH
EPSILON=1e-5
NC=4


def dot(a,b,dims):
    return lax.dot_general(a,b,dims,preferred_element_type=jnp.float32)


def greet(partner):
    barrier=pltpu.get_barrier_semaphore()
    pl.semaphore_signal(barrier,inc=1,device_id=partner,device_id_type=MESH)
    pl.semaphore_wait(barrier,1)


def main_kernel(wq,wk,wv,wos,wu,wds,tok,cot_hbm,v_ob,v_g1,v_b1,v_db,v_g2,v_b2,v_ub,v_qb,v_vb,
               lo_hbm,gf,dqkv_hbm,dw,r1,r2,r3,early,x_hbm,wh_hbm,
               bias,vec,upb,sh,qkv,vt,kt,ctx,ctxo,lse,cl,wo,wup,wdn,xh,rst,hall,act,slp,ball,ga,dcs,dcall,part,pch,ctt,dqt,dl,dkv,sbuf,rbuf,tb,th,stage,
               lsem,losem,dsem,osem,ssem,rsem,rl,g1s,g1r,g2s,g2r,g3s,g3r,ts,tr,azs,azr,axs,axr,acs,acr):
    d=lax.axis_index("dp"); t=lax.axis_index("tensor")
    partner=(d,1-t)
    core=d%2; x_=(d//2)%2; z=d//4
    def dev(z_,xx,c_): return ((z_*2+xx)*2+c_,t)
    sib=dev(z,x_,1-core); xp=dev(z,1-x_,core); zp=[dev((z+k)%4,x_,core) for k in (1,2,3)]
    own,dm=tok.shape; cr=own//NC; cg=2*cr; rows_all=2*own; width=ctx.shape[1]; ff=wup.shape[2]; wide=wo.shape[2]; pairs=width//128
    def local(src,dst,i): return pltpu.make_async_copy(src,dst,lsem.at[i])
    def remote(src,dst,a,b,p): return pltpu.make_async_remote_copy(src,dst,a,b,device_id=p,device_id_type=MESH)
    cot_load=local(cot_hbm,cl,0)
    cot_load.start()
    barrier=pltpu.get_barrier_semaphore()
    n=3*width
    def row(v): return v[...].astype(F32).reshape(1,v.shape[0])
    sh[:,0:width]=wq[...]; sh[:,width:2*width]=wk[...]; sh[:,2*width:n]=wv[...]
    everyone=[partner,sib,xp]+zp
    for p in everyone: pl.semaphore_signal(barrier,inc=1,device_id=p,device_id_type=MESH)
    def chunk(c): return pl.ds(pl.multiple_of(c*cg,cg),cg)
    def rows(rank,c): return pl.ds(pl.multiple_of(c*cg+rank*cr,cr),cr)
    def half(rank): return pl.ds(pl.multiple_of(rank*cr,cr),cr)
    def loc(c): return pl.ds(pl.multiple_of(c*cr,cr),cr)
    def rs_copy(k,c):
        return pltpu.make_async_remote_copy(sbuf.at[k-1,loc(c)],rbuf.at[k-1,loc(c)],ssem.at[k,c],rsem.at[k,c],device_id=partner,device_id_type=MESH)
    def ag_copy(k,buf,c,rank):
        return pltpu.make_async_remote_copy(buf.at[rows(rank,c)],buf.at[rows(rank,c)],ssem.at[k,c],rsem.at[k,c],device_id=partner,device_id_type=MESH)
    def cols(rank): return pl.ds(pl.multiple_of(rank*width,128),width)
    def ctx_copy(c,rank):
        return pltpu.make_async_remote_copy(ctx.at[rows(1-rank,c)],ctxo.at[loc(c),cols(rank)],ssem.at[0,c],rsem.at[0,c],device_id=partner,device_id_type=MESH)
    def dctx_copy(c,rank):
        return pltpu.make_async_remote_copy(dcs.at[loc(c),cols(1-rank)],dcall.at[rows(rank,c)],ssem.at[5,c],rsem.at[5,c],device_id=partner,device_id_type=MESH)
    early[...]=jnp.zeros_like(early)
    early[10:11]=jnp.full_like(early[10:11],-jnp.inf)
    def whole(w): return w[...].reshape(dm,w.shape[2])
    def strip(w,cs): return w[:,:,cs].reshape(dm,TF)
    dkv[...]=jnp.zeros_like(dkv)
    lane=lax.broadcasted_iota(jnp.int32,(1,128),1)
    scale=jnp.bfloat16(HD**-0.5); zero=jnp.bfloat16(0)
    q4=ff//2
    groups=[(act,0,0,width),(act,width,width,width),(act,2*width,2*width,width),(wo,0,n,wide),
            (wup,0,n+wide,q4),(wup,q4,n+wide+q4,q4),(wdn,0,n+wide+ff,q4),(wdn,q4,n+wide+ff+q4,q4)]
    def block(z_,xx): return (z_*2+xx)*2+core
    me=block(z,x_)
    def place(g,b):
        buf,c0,_,nc=groups[g]
        return buf.at[b,:,c0:c0+nc]
    def z_hop(g,k,b): return remote(sh.at[:,groups[g][2]:groups[g][2]+groups[g][3]],place(g,b),azs.at[g,k-1],azr.at[g,k-1],zp[k-1])
    def x_hop(g,k,b): return remote(sh.at[:,groups[g][2]:groups[g][2]+groups[g][3]] if k==0 else place(g,b),place(g,b),axs.at[g,k],axr.at[g,k],xp)
    def c_hop(g,k,b): return remote(sh.at[:,groups[g][2]:groups[g][2]+groups[g][3]] if k==0 else place(g,b),place(g,b),acs.at[g,k],acr.at[g,k],sib)
    def back(k): return (z-k)%4
    def gather_start(g):
        buf,c0,s0,nc=groups[g]
        for k in (1,2,3): z_hop(g,k,me).start()
        x_hop(g,0,me).start()
        c_hop(g,0,me).start()
        buf[me,:,c0:c0+nc]=sh[:,s0:s0+nc]
    def gather_sent(g):
        for k in (1,2,3): z_hop(g,k,me).wait_send()
    def gather_x(g):
        for k in (1,2,3):
            b=block(back(k),x_)
            z_hop(g,k,b).wait_recv()
            x_hop(g,k,b).start()
            c_hop(g,k,b).start()
    def gather_core(g):
        for k in (0,1,2,3):
            b=block(back(k),1-x_)
            x_hop(g,k,b).wait_recv()
            c_hop(g,4+k,b).start()
    def gather_done(g):
        for k in range(8): c_hop(g,k,me).wait_recv()
        for k in range(4): x_hop(g,k,me).wait_send()
        for k in range(8): c_hop(g,k,me).wait_send()
    own_copies=[local(tok.at[c*cr:(c+1)*cr],hall.at[rows(t,c)],1+c) for c in range(NC)]
    for c in own_copies: c.start()
    pl.semaphore_wait(barrier,len(everyone))
    gather_start(0)
    def tok_copy(c): return remote(tok.at[loc(c)],hall.at[rows(t,c)],ts.at[c],tr.at[c],partner)
    def mine_o(rank): return sh.at[:,pl.ds(pl.multiple_of(n+rank*width,128),width)]
    o_swap=remote(mine_o(t),mine_o(t),ts.at[NC],tr.at[NC],partner)
    sh[:,pl.ds(pl.multiple_of(n+t*width,128),width)]=wos[...]
    o_swap.start()
    @pl.loop(0,NC)
    def _(c): tok_copy(c).start()
    sh[:,n+wide:n+wide+ff]=wu[...]
    sh[:,n+wide+ff:]=wds[...]
    for i,v in enumerate((v_ob,v_g1,v_b1,v_db,v_g2,v_b2)): vec[i:i+1]=row(v)
    upb[...]=row(v_ub)
    bias[...]=jnp.zeros_like(bias)
    bias[:,0:width]=row(v_qb); bias[:,2*width:]=row(v_vb)
    gather_sent(0); gather_start(1)
    gather_x(0)
    gather_sent(1); gather_start(2)
    gather_x(1)
    gather_core(0)
    o_swap.wait_recv()
    gather_sent(2); gather_start(3)
    gather_x(2)
    gather_core(1); gather_core(2)
    for g in range(3): gather_done(g)
    gather_sent(3); gather_start(4)
    gather_x(3)
    for c in own_copies: c.wait()
    TF=512
    @pl.loop(0,NC)
    def _(c):
        tok_copy(c).wait_recv()
        @pl.loop(0,n//TF)
        def _(j):
            cs=pl.ds(pl.multiple_of(j*TF,TF),TF)
            qkv[chunk(c),cs]=(dot(hall[chunk(c)],strip(act,cs),NN)+bias[:,cs]).astype(BF)
    x_out=local(hall,x_hbm,5); w_out=local(act.at[:,:,0:n],wh_hbm,6)
    x_out.start(); w_out.start()
    gather_core(3)
    ones=jnp.where(lax.broadcasted_iota(jnp.int32,(16,rows_all),0)==0,1.0,0.0).astype(BF)
    @pl.loop(0,pairs)
    def _(p):
        ck=pl.multiple_of(width+p*128,128); cv=pl.multiple_of(2*width+p*128,128)
        kt[p]=qkv[:,pl.ds(ck,128)].T
        v=qkv[:,pl.ds(cv,128)].T
        vt[2*p,0:64]=v[0:64]; vt[2*p,64:80]=ones
        vt[2*p+1,0:64]=v[64:128]; vt[2*p+1,64:80]=ones
    x_out.wait()
    def split(k,c):
        sbuf[k-1,loc(c)]=pch[half(1-t)].astype(BF)
        rs_copy(k,c).start()
        part[loc(c)]=pch[half(t)]
    def stats(v):
        cen=v-jnp.mean(v,axis=1,keepdims=True)
        r=lax.rsqrt(jnp.mean(cen*cen,axis=1,keepdims=True)+EPSILON)
        return cen*r,r
    def lo_copy(c): return pltpu.make_async_copy(cl.at[loc(c)],lo_hbm.at[loc(c)],losem.at[c])
    def out_copy(slot,col):
        return pltpu.make_async_copy(stage.at[slot],dw.at[:,:,:,:,pl.ds(pl.multiple_of(col,512),512)],osem.at[slot])
    def wgrad(slot,left,right_ref,rcol,ocol):
        @pl.loop(0,dm//256)
        def _(i):
            ms=pl.ds(pl.multiple_of(i*256,256),256)
            right=right_ref[:,pl.ds(pl.multiple_of(rcol,512),512)] if len(right_ref.shape)==2 else strip(right_ref,pl.ds(pl.multiple_of(rcol,512),512))
            stage[slot,i]=dot(left[ms],right,NN).astype(BF).reshape(2,2,64,512)
        out_copy(slot,ocol).start()
    def stage_a(c):
        rs=chunk(c)
        @pl.loop(0,pairs)
        def _(p):
            cq=pl.ds(pl.multiple_of(p*128,128),128); ck=pl.ds(pl.multiple_of(width+p*128,128),128)
            pks=[]
            for h in (0,1):
                keep=(lane<64) if h==0 else (lane>=64)
                q=jnp.where(keep,qkv[rs,cq]*scale,zero)
                st=dot(qkv[:,ck],q,NT)
                m=jnp.max(st,axis=0,keepdims=True)
                mc=m*LOG2E
                pt=jnp.exp2(st*LOG2E-mc).astype(BF)
                ot=dot(vt[2*p+h],pt,NN)
                tot=ot[64:65]
                ctt[h*64:(h+1)*64,:]=ot[0:64]*(1.0/tot)
                lse[pl.ds(2*p+h,1),rs]=mc+jnp.log2(tot)
                pks.append(jnp.max(m,axis=1,keepdims=True))
            early[10:11,cq]=jnp.maximum(early[10:11,cq],jnp.where(lane<64,pks[0],pks[1]))
            ctx[rs,cq]=ctt[...].T.astype(BF)
            step=c*pairs+p
            @pl.when(step==2)
            def _():
                gather_sent(4); gather_start(5)
                gather_x(4)
                gather_done(3)
            @pl.when(step==8)
            def _():
                gather_sent(5); gather_start(6)
                gather_x(5)
                gather_core(4)
            @pl.when(step==14)
            def _():
                gather_sent(6); gather_start(7)
                gather_x(6)
                gather_core(5)
        ctx_copy(c,t).start()
        ctxo[loc(c),cols(t)]=ctx[rows(t,c)]
    def stage_b(c):
        ctx_copy(c,1-t).wait_recv()
        x,r=stats(hall[rows(t,c)].astype(F32)+dot(ctxo[loc(c)],whole(wo),NT)+vec[0:1])
        xh[loc(c)]=x
        rst[loc(c)]=jnp.broadcast_to(r,(cr,128))
        hall[rows(t,c)]=(x*vec[1:2]+vec[2:3]).astype(BF)
        ag_copy(3,hall,c,t).start()
    def stage_c(c):
        rs=chunk(c)
        ag_copy(3,hall,c,1-t).wait_recv()
        @pl.loop(0,ff//TF)
        def _(j):
            cs=pl.ds(pl.multiple_of(j*TF,TF),TF)
            u=dot(hall[rs],strip(wup,cs),NN)+upb[:,cs]
            cdf=0.5*(1.0+lax.erf(u*0.5**0.5))
            act[pl.ds(4*c,4),:,cs]=(u*cdf).astype(BF).reshape(4,64,TF)
            slp[rs,cs]=(cdf+u*jnp.exp(-0.5*u*u)*(0.5/math.pi)**0.5).astype(BF)
        @pl.when(c==0)
        def _():
            gather_core(6)
            gather_sent(7); gather_x(7)
            gather_core(7)
            gather_done(6); gather_done(7)
        pch[...]=dot(act[pl.ds(4*c,4)].reshape(cg,ff),whole(wdn),NT)
        split(1,c)
    def stage_d(c):
        rs_copy(1,c).wait_recv()
        x,r=stats(xh[loc(c)]*vec[1:2]+vec[2:3]+part[loc(c)]+rbuf[0,loc(c)].astype(F32)+vec[3:4])
        dy=cl[loc(c)].astype(F32)
        cl[loc(c)]=(x*vec[4:5]+vec[5:6]).astype(BF)
        lo_copy(c).start()
        early[4:5]+=jnp.sum(dy*x,axis=0,keepdims=True)
        early[5:6]+=jnp.sum(dy,axis=0,keepdims=True)
        dx=dy*vec[4:5]
        g=r*(dx-jnp.mean(dx,axis=1,keepdims=True)-x*jnp.mean(dx*x,axis=1,keepdims=True))
        gf[loc(c)]=g
        gb=g.astype(BF)
        early[3:4]+=jnp.sum(gb.astype(F32),axis=0,keepdims=True)
        ball[rows(t,c)]=gb
        ag_copy(4,ball,c,t).start()
        tb[:,rows(t,c)]=gb.T
    def stage_e(c):
        rs=chunk(c)
        ag_copy(4,ball,c,1-t).wait_recv()
        @pl.loop(0,ff//TF)
        def _(j):
            cs=pl.ds(pl.multiple_of(j*TF,TF),TF)
            gu=(dot(ball[rs],strip(wdn,cs),NN)*slp[rs,cs].astype(F32)).astype(BF)
            slp[rs,cs]=gu
            row=pl.ds(8+j*TF//dm,1); cc=pl.ds(pl.multiple_of(j*TF%dm,TF),TF)
            early[row,cc]+=jnp.sum(gu.astype(F32),axis=0,keepdims=True)
        pch[...]=dot(slp[rs],whole(wup),NT)
        split(2,c)
        tb[:,rows(1-t,c)]=ball[rows(1-t,c)].T
        th[:,chunk(c)]=hall[chunk(c)].T
    def stage_f(c):
        rs_copy(2,c).wait_recv()
        dy=gf[loc(c)]+part[loc(c)]+rbuf[1,loc(c)].astype(F32)
        x=xh[loc(c)]; r=rst[loc(c)][:,0:1]
        early[1:2]+=jnp.sum(dy*x,axis=0,keepdims=True)
        early[2:3]+=jnp.sum(dy,axis=0,keepdims=True)
        dx=dy*vec[1:2]
        g=r*(dx-jnp.mean(dx,axis=1,keepdims=True)-x*jnp.mean(dx*x,axis=1,keepdims=True))
        gf[loc(c)]=g
        gb=g.astype(BF)
        early[0:1]+=jnp.sum(gb.astype(F32),axis=0,keepdims=True)
        ga[loc(c)]=gb
        dcs[loc(c)]=dot(gb,whole(wo),NN).astype(BF)
        dctx_copy(c,t).start()
        dcall[rows(t,c)]=dcs[loc(c),cols(t)]
    def stage_g(c):
        rs=chunk(c)
        dctx_copy(c,1-t).wait_recv()
        @pl.loop(0,pairs)
        def _(p):
            cq=pl.ds(pl.multiple_of(p*128,128),128); ck=pl.ds(pl.multiple_of(width+p*128,128),128); cv=pl.ds(pl.multiple_of(2*width+p*128,128),128)
            prod=(ctx[rs,cq].astype(F32)*dcall[rs,cq].astype(F32)).T
            dl[0:1]=jnp.sum(prod[0:64],axis=0,keepdims=True)
            dl[1:2]=jnp.sum(prod[64:128],axis=0,keepdims=True)
            for h in (0,1):
                keep=(lane<64) if h==0 else (lane>=64)
                q=jnp.where(keep,qkv[rs,cq]*scale,zero)
                do=jnp.where(keep,dcall[rs,cq],zero)
                st=dot(qkv[:,ck],q,NT)
                pt=jnp.exp2(st*LOG2E-lse[pl.ds(2*p+h,1),rs])
                dpt=dot(qkv[:,cv],do,NT)
                ds=(pt*(dpt-dl[h:h+1])).astype(BF)
                dkv[1,:,cq]+=dot(pt.astype(BF),do,NN)
                dkv[0,:,cq]+=dot(ds,q,NN)
                dqt[h*64:(h+1)*64,:]=dot(kt[p,h*64:(h+1)*64,:],ds,NN)
            qkv[rs,cq]=(dqt[...].T*(HD**-0.5)).astype(BF)
    def grad_down(c):
        slot=c%2
        @pl.when(c>=2)
        def _(): out_copy(slot,0).wait()
        wgrad(slot,tb,act,c*512,wide+ff+c*512)
    def grad_up(c):
        slot=c%2
        @pl.when(c>=2)
        def _(): out_copy(slot,0).wait()
        wgrad(slot,th,slp,c*512,wide+c*512)
    def grad_out():
        @pl.loop(0,NC)
        def _(c): tb[:,loc(c)]=ga[loc(c)].T
        for j in range(wide//512):
            @pl.loop(0,dm//256)
            def _(i):
                ms=pl.ds(pl.multiple_of(i*256,256),256)
                stage[j%2,i]=dot(tb[ms,0:own],ctxo[:,j*512:(j+1)*512],NN).astype(BF).reshape(2,2,64,512)
            out_copy(j%2,j*512).start()
    @pl.loop(0,NC)
    def _(c):
        stage_a(c)
        @pl.when(c>0)
        def _(): stage_b(c-1)
    cot_load.wait(); w_out.wait()
    gather_done(4); gather_done(5)
    @pl.loop(0,NC)
    def _(c):
        stage_c(c)
        @pl.when(c==0)
        def _(): stage_b(NC-1)
        @pl.when(c>=2)
        def _(): stage_d(c-2)
    @pl.loop(NC-2,NC)
    def _(c): stage_d(c)
    @pl.loop(0,NC)
    def _(c): stage_e(c)
    base=(wide+ff,wide)
    def s1(g): return remote(dw.at[:,:,1-core,:,base[g]:base[g]+ff],r1.at[g],g1s.at[g],g1r.at[g],sib)
    def s2(g): return remote(wup.at[8+4*g:12+4*g],r2.at[g],g2s.at[g],g2r.at[g],xp)
    def s3(k): return remote(wdn.at[12+(z+k)%4],r3.at[3-k],g3s.at[k-1],g3r.at[k-1],zp[k-1])
    def load2(g): return [pltpu.make_async_copy(dw.at[:,1-x_,core,:,base[g]:base[g]+ff],wup.at[0:4],rl.at[0]),
                          pltpu.make_async_copy(r1.at[g,:,1-x_],wup.at[4:8],rl.at[1])]
    def load3(): return [pltpu.make_async_copy(dw.at[:,x_,core,:,base[0]:base[0]+ff],wdn.at[0:4],rl.at[2]),
                         pltpu.make_async_copy(r1.at[0,:,x_],wdn.at[4:8],rl.at[3]),
                         pltpu.make_async_copy(r2.at[0],wdn.at[8:12],rl.at[4])]
    def add2(g):
        for c in load2(g): c.wait()
        @pl.loop(0,4)
        def _(i): wup[8+4*g+i]=(wup[i].astype(F32)+wup[4+i].astype(F32)).astype(BF)
    @pl.loop(0,NC)
    def _(c): grad_down(c)
    out_copy(0,0).wait()
    out_copy(1,0).wait()
    s1(0).start()
    @pl.loop(0,NC)
    def _(c):
        stage_f(c)
        grad_up(c)
        @pl.when(c==1)
        def _():
            s1(0).wait_recv()
            for l in load2(0): l.start()
        @pl.when(c==2)
        def _():
            add2(0)
            s2(0).start()
    out_copy(0,0).wait()
    out_copy(1,0).wait()
    s1(1).start()
    grad_out()
    @pl.loop(0,NC)
    def _(c):
        stage_g(c)
        @pl.when(c==0)
        def _():
            s1(1).wait_recv()
            for l in load2(1): l.start()
        @pl.when(c==1)
        def _():
            add2(1)
            s2(0).wait_send()
            s2(1).start()
            s2(0).wait_recv()
            for l in load3(): l.start()
        @pl.when(c==2)
        def _():
            for l in load3(): l.wait()
            @pl.loop(0,4)
            def _(i): wdn[12+i]=(wdn[i].astype(F32)+wdn[4+i].astype(F32)+wdn[8+i].astype(F32)).astype(BF)
            for k in (1,2,3): s3(k).start()
    @pl.loop(0,pairs)
    def _(p):
        cq=pl.ds(pl.multiple_of(p*128,128),128); ck=pl.ds(pl.multiple_of(width+p*128,128),128); cv=pl.ds(pl.multiple_of(2*width+p*128,128),128)
        qkv[:,ck]=dkv[0,:,cq].astype(BF)
        qkv[:,cv]=dkv[1,:,cq].astype(BF)
    dq_out=pltpu.make_async_copy(qkv,dqkv_hbm,dsem.at[0])
    dq_out.start()
    out_copy(0,0).wait()
    out_copy(1,0).wait()
    dq_out.wait()
    o_swap.wait_send()
    for g in (0,1): s1(g).wait_send()
    s2(1).wait()
    for k in (1,2,3): s3(k).wait()
    @pl.loop(0,NC)
    def _(c):
        lo_copy(c).wait()
        ctx_copy(c,t).wait_send(); dctx_copy(c,t).wait_send(); tok_copy(c).wait_send()
        for k in (1,2): rs_copy(k,c).wait_send()
        for k,buf in ((3,hall),(4,ball)): ag_copy(k,buf,c,t).wait_send()

def main_call(shards,tok,cot,vectors,cid):
    V=pl.BlockSpec(memory_space=pltpu.VMEM); A=pl.BlockSpec(memory_space=pl.ANY)
    width=shards[0].shape[1]; ff=shards[4].shape[1]; own,dm=tok.shape; rows=2*own; n=3*width; cr=own//NC; wide=2*width
    S=jax.ShapeDtypeStruct; M=pltpu.VMEM; D=pltpu.SemaphoreType.DMA
    return pl.pallas_call(main_kernel,
      out_shape=(S((own,dm),BF),S((own,dm),F32),S((rows,n),BF),S((4,2,2,64,wide+2*ff),BF),S((2,4,2,64,ff),BF),S((2,4,64,ff),BF),S((3,64,ff),BF),S((16,dm),F32),S((rows,dm),BF),S((16,64,n),BF)),
      in_specs=[V]*6+[A,A]+[V]*9,out_specs=(A,V,A,A,A,A,A,V,A,A),
      scratch_shapes=[M((1,n),F32),M((8,dm),F32),M((1,ff),F32),M((64,n+wide+2*ff),BF),M((rows,n),BF),M((width//HD,80,rows),BF),M((width//128,128,rows),BF),M((rows,width),BF),M((own,wide),BF),M((width//HD,rows),F32),M((own,dm),BF),
        M((16,64,wide),BF),M((16,64,ff),BF),M((16,64,ff),BF),
        M((own,dm),F32),M((own,128),F32),
        M((rows,dm),BF),M((16,64,ff),BF),M((rows,ff),BF),M((rows,dm),BF),M((own,dm),BF),M((own,wide),BF),M((rows,width),BF),
        M((own,dm),F32),M((2*cr,dm),F32),M((128,2*cr),F32),M((128,2*cr),F32),M((8,2*cr),F32),M((2,rows,width),F32),
        M((2,own,dm),BF),M((2,own,dm),BF),
        M((dm,rows),BF),M((dm,rows),BF),M((2,4,2,2,64,512),BF),
        D((7,)),D((NC,)),D((1,)),D((2,)),D((6,NC)),D((6,NC)),D((5,)),D((2,)),D((2,)),D((2,)),D((2,)),D((3,)),D((3,)),
        D((NC+1,)),D((NC+1,)),D((8,3)),D((8,3)),D((8,4)),D((8,4)),D((8,8)),D((8,8))],
      compiler_params=pltpu.CompilerParams(collective_id=cid,has_side_effects=True,vmem_limit_bytes=61*2**20),
      name="main")(*shards,tok,cot,*vectors)

def tail_kernel(dqkv_ref,dw,r1w,r2w,r3w,w_hbm,x_hbm,gf,early,wq,wk,bq,lim,
                tg,gq,gk,gv,go,gu,gd,sums,late,qc,kc,qbc,
                xv,xt,wv,part,pc,dwh,ysb,yrb,fw,zu,su,ru,oo,o1,o2s,o2,o3s,o3,h1,h2s,h2,h3s,h3,osb,orb,eb,er,lb,lr,
                lsem,s1s,s1r,s2s,s2r,s3s,s3r,ysend,yrecv,es,erc,ls,lrc,os_,or_):
    d=lax.axis_index("dp"); t=lax.axis_index("tensor")
    core=d%2; x=(d//2)%2; z=d//4
    def dev(z_,x_,c_): return ((z_*2+x_)*2+c_,t)
    sib=dev(z,x,1-core); xp=dev(z,1-x,core); yp=(d,1-t)
    zp=[dev((z+k)%4,x,core) for k in (1,2,3)]
    zb=[dev(z+1-2*(z%2),x,core),dev((z+2)%4,x,core)]
    barrier=pltpu.get_barrier_semaphore()
    everyone=[sib,xp,yp]+zp
    for p in everyone: pl.semaphore_signal(barrier,inc=1,device_id=p,device_id_type=MESH)
    own,dm=gf.shape; rows,n=dqkv_ref.shape; width=n//3; cr=own//NC; ff=fw.shape[2]; wide=2*width
    def remote(src,dst,a,b,p): return pltpu.make_async_remote_copy(src,dst,a,b,device_id=p,device_id_type=MESH)
    def local(src,dst,i): return pltpu.make_async_copy(src,dst,lsem.at[i])
    f32=lambda a:a.astype(F32)
    wcols=slice(wide+ff,wide+2*ff); ucols=slice(wide,wide+ff)
    loads=[local(dw.at[:,x,core,:,ucols],zu.at[0],0),local(r1w.at[1,:,x],zu.at[1],1),local(r2w.at[1],zu.at[2],2),
           local(dw.at[:,:,core,:,0:wide],oo,3),local(w_hbm.at[:,:,:],wv,4),local(x_hbm,xv,5),
           local(dw.at[z,x,core,:,wcols],fw.at[0],6),local(r1w.at[0,z,x],fw.at[1],7),local(r2w.at[0,z],fw.at[2],8),
           local(r3w.at[0],fw.at[3],9),local(r3w.at[1],fw.at[4],10),local(r3w.at[2],fw.at[5],11)]
    for c in loads: c.start()
    eb[0]=early[...]
    lb[0]=jnp.zeros_like(lb[0])
    pl.semaphore_wait(barrier,len(everyone))
    o_s1=remote(dw.at[:,:,1-core,:,0:wide],o1,s1s.at[0],s1r.at[0],sib); o_s1.start()
    h_s1=remote(dwh.at[:,:,1-core],h1,s1s.at[1],s1r.at[1],sib)
    o_s2=remote(o2s,o2,s2s.at[0],s2r.at[0],xp)
    h_s2=remote(h2s,h2,s2s.at[1],s2r.at[1],xp)
    def z3(g,src,dst): return [remote(src.at[(z+k)%4],dst.at[3-k],s3s.at[g,k-1],s3r.at[g,k-1],zp[k-1]) for k in (1,2,3)]
    u_s3=z3(0,su,ru); o_s3=z3(1,o3s,o3); h_s3=z3(2,h3s,h3)
    hops=[sib,xp,zb[0],zb[1],yp]
    def ecopy(i): return remote(eb.at[i],er.at[i],es.at[i],erc.at[i],hops[i])
    def eadd(i):
        ecopy(i).wait_recv()
        b=eb[i,8:16]; c=er[i,8:16]
        if i<4:
            r=lax.broadcasted_iota(jnp.int32,b.shape,0)
            b=jnp.where(r==2,jnp.maximum(b,c),b+c)
        eb[i+1,0:8]=eb[i,0:8]+er[i,0:8]; eb[i+1,8:16]=b
    def lcopy(i): return remote(lb.at[i],lr.at[i],ls.at[i],lrc.at[i],hops[i])
    def ladd(i):
        lcopy(i).wait_recv()
        lb[i+1]=lb[i]+lr[i]
    ecopy(0).start()
    for i in (0,1,2): loads[i].wait()
    @pl.loop(0,4)
    def _(i): su[i]=(f32(zu[0,i])+f32(zu[1,i])+f32(zu[2,i])).astype(BF)
    for c in u_s3: c.start()
    loads[4].wait()
    def ycopy(c): return remote(ysb.at[c],yrb.at[c],ysend.at[c],yrecv.at[c],yp)
    @pl.loop(0,NC)
    def _(c):
        pc[...]=dot(dqkv_ref[pl.ds(pl.multiple_of(2*c*cr,2*cr),2*cr)],wv[...].reshape(dm,n),NT)
        ysb[c]=pc[pl.ds(pl.multiple_of((1-t)*cr,cr),cr)].astype(BF)
        ycopy(c).start()
        part[c]=pc[pl.ds(pl.multiple_of(t*cr,cr),cr)]
    lb[0,0:1,0:width]=jnp.sum(f32(dqkv_ref[:,0:width]),axis=0,keepdims=True)
    lb[0,0:1,width:2*width]=jnp.sum(f32(dqkv_ref[:,2*width:]),axis=0,keepdims=True)
    lcopy(0).start()
    eadd(0); ecopy(1).start()
    o_s1.wait_recv(); loads[3].wait()
    @pl.loop(0,4)
    def _(i): o2s[i]=(f32(oo[i,1-x])+f32(o1[i,1-x])).astype(BF)
    o_s2.start()
    loads[5].wait()
    @pl.loop(0,rows//256)
    def _(c):
        cs=pl.ds(pl.multiple_of(c*256,256),256)
        xt[:,cs]=xv[cs].T
    eadd(1); ecopy(2).start()
    @pl.loop(0,4)
    def _(i):
        ms=pl.ds(pl.multiple_of(i*256,256),256)
        for j in range(n//512):
            dwh[i,:,:,:,j*512:(j+1)*512]=dot(xt[ms],dqkv_ref[:,j*512:(j+1)*512],NN).astype(BF).reshape(2,2,64,512)
    h_s1.start()
    ladd(0); lcopy(1).start()
    eadd(2); ecopy(3).start()
    h_s1.wait_recv()
    @pl.loop(0,4)
    def _(i): h2s[i]=(f32(dwh[i,1-x,core])+f32(h1[i,1-x])).astype(BF)
    o_s2.wait_recv()
    @pl.loop(0,4)
    def _(i): o3s[i]=(f32(oo[i,x])+f32(o1[i,x])+f32(o2[i])).astype(BF)
    o_s2.wait_send()
    h_s2.start()
    ladd(1); lcopy(2).start()
    eadd(3); ecopy(4).start()
    for i in range(6,12): loads[i].wait()
    v=f32(fw[0])+f32(fw[1])+f32(fw[2])
    v=v+f32(fw[3])+f32(fw[4])+f32(fw[5])
    gd[...]=v
    ladd(2); lcopy(3).start()
    eadd(4)
    sums[...]=eb[5]
    pk=eb[4,10:11,0:width]
    head=lax.broadcasted_iota(jnp.int32,(1,width),1)//HD
    limit=jnp.zeros((1,width),F32)
    for h in range(width//HD): limit=jnp.where(head==h,lim[h],limit)
    sc=jnp.sqrt(limit/jnp.maximum(pk,limit))
    qc[...]=(f32(wq[...])*sc).astype(BF); kc[...]=(f32(wk[...])*sc).astype(BF)
    qbc[...]=f32(bq[...]).reshape(1,width)*sc
    for c in u_s3: c.wait_send()
    for c in o_s3: c.start()
    for c in u_s3: c.wait_recv()
    v=f32(zu[0,z])+f32(zu[1,z])+f32(zu[2,z])
    gu[...]=v+f32(ru[0])+f32(ru[1])+f32(ru[2])
    for c in range(NC):
        ycopy(c).wait_recv()
        lo_=slice(c*cr,(c+1)*cr)
        tg[lo_]=(gf[lo_]+part[c]+f32(yrb[c])).astype(BF)
    ladd(3)
    late[...]=lb[4]
    h_s2.wait_recv()
    @pl.loop(0,4)
    def _(i): h3s[i]=(f32(dwh[i,x,core])+f32(h1[i,x])+f32(h2[i])).astype(BF)
    for c in o_s3: c.wait_send()
    for c in h_s3: c.start()
    for c in o_s3: c.wait_recv()
    v=f32(oo[z,x])+f32(o1[z,x])+f32(o2[z])
    v=v+f32(o3[0])+f32(o3[1])+f32(o3[2])
    osb[0]=v[:,0:width]; osb[1]=v[:,width:]
    ocopy=remote(osb.at[1-t],orb,os_,or_,yp)
    ocopy.start()
    ocopy.wait_recv()
    go[...]=osb[t]+orb[...]
    for c in h_s3: c.wait_recv()
    v=f32(dwh[z,x,core])+f32(h1[z,x])+f32(h2[z])
    v=v+f32(h3[0])+f32(h3[1])+f32(h3[2])
    gq[...]=v[:,0:width]; gk[...]=v[:,width:2*width]; gv[...]=v[:,2*width:]
    for c in [o_s1,h_s1,h_s2,ocopy]+h_s3: c.wait_send()
    for i in range(5): ecopy(i).wait_send()
    for i in range(4): lcopy(i).wait_send()
    for c in range(NC): ycopy(c).wait_send()

def tail_call(dqkv,dw,r1,r2,r3,w,xall,gf,early,wq,wk,bq,lim,cid):
    V=pl.BlockSpec(memory_space=pltpu.VMEM); A=pl.BlockSpec(memory_space=pl.ANY)
    S=jax.ShapeDtypeStruct; D=pltpu.SemaphoreType.DMA; M=pltpu.VMEM
    own,dm=gf.shape; rows,n=dqkv.shape; width=n//3; cr=own//NC
    ff=r3.shape[2]; wide=2*width
    return pl.pallas_call(tail_kernel,
      out_shape=(S((own,dm),BF),S((64,width),F32),S((64,width),F32),S((64,width),F32),S((64,width),F32),S((64,ff),F32),S((64,ff),F32),
                 S((16,1024),F32),S((8,1024),F32),S((64,width),BF),S((64,width),BF),S((1,width),F32)),
      in_specs=[V]+[A]*6+[V]*5+[pl.BlockSpec(memory_space=pltpu.SMEM)],out_specs=(V,)*12,
      scratch_shapes=[M((rows,dm),BF),M((dm,rows),BF),M((16,64,n),BF),M((NC,cr,dm),F32),M((2*cr,dm),F32),M((4,2,2,64,n),BF),M((NC,cr,dm),BF),M((NC,cr,dm),BF),
        M((6,64,ff),BF),M((3,4,64,ff),BF),M((4,64,ff),BF),M((3,64,ff),BF),
        M((4,2,64,wide),BF),M((4,2,64,wide),BF),M((4,64,wide),BF),M((4,64,wide),BF),M((4,64,wide),BF),M((3,64,wide),BF),
        M((4,2,64,n),BF),M((4,64,n),BF),M((4,64,n),BF),M((4,64,n),BF),M((3,64,n),BF),M((2,64,width),F32),M((64,width),F32),
        M((6,16,1024),F32),M((5,16,1024),F32),M((5,8,1024),F32),M((4,8,1024),F32),
        D((12,)),D((2,)),D((2,)),D((2,)),D((2,)),D((3,3)),D((3,3)),D((NC,)),D((NC,)),D((5,)),D((5,)),D((4,)),D((4,)),D,D],
      compiler_params=pltpu.CompilerParams(collective_id=cid,has_side_effects=True,vmem_limit_bytes=61*2**20),
      name="tail")(dqkv,dw,r1,r2,r3,w,xall,gf,early,wq,wk,bq,lim)

def finish_kernel(lo,tg,gq,gk,gv,go,gu,gd,qc,kc,sums,late,qbc,
                  lo_,tg_,gq_,gk_,gv_,go_,gu_,gd_,qc_,kc_,qb_,vb_,ob_,g1_,b1_,ub_,db_,g2_,b2_,pk_,qbc_,sem):
    moves=[pltpu.make_async_copy(a,b,sem.at[i]) for i,(a,b) in enumerate(zip((lo,tg,gq,gk,gv,go,gu,gd,qc,kc),(lo_,tg_,gq_,gk_,gv_,go_,gu_,gd_,qc_,kc_)))]
    for c in moves: c.start()
    width=qb_.shape[0]; dm=ob_.shape[0]
    def line(v): return v.reshape(v.shape[1])
    qb_[...]=line(late[0:1,0:width]); vb_[...]=line(late[0:1,width:2*width])
    for i,o in enumerate((ob_,g1_,b1_,db_,g2_,b2_)): o[...]=line(sums[i:i+1])
    ub_[0:dm]=line(sums[8:9]); ub_[dm:2*dm]=line(sums[9:10])
    for h in range(pk_.shape[0]): pk_[h]=jnp.max(sums[10:11,h*HD:(h+1)*HD])
    qbc_[...]=line(qbc[...]).astype(BF)
    for c in moves: c.wait()

def finish_call(lo,tg,gq,gk,gv,go,gu,gd,qc,kc,sums,late,qbc):
    V=pl.BlockSpec(memory_space=pltpu.VMEM); A=pl.BlockSpec(memory_space=pl.ANY); S=jax.ShapeDtypeStruct
    big=(lo,tg,gq,gk,gv,go,gu,gd,qc,kc)
    width=gq.shape[1]; ff=gu.shape[1]; dm=tg.shape[1]
    return pl.pallas_call(finish_kernel,
      out_shape=tuple(S(a.shape,a.dtype) for a in big)+tuple(S((k,),F32) for k in (width,width,dm,dm,dm,ff,dm,dm,dm,width//HD))+(S((width,),BF),),
      in_specs=[A]*10+[V]*3,out_specs=(A,)*10+(V,)*9+(pl.BlockSpec(memory_space=pltpu.SMEM),V),
      scratch_shapes=[pltpu.SemaphoreType.DMA((10,))],name="finish")(*big,sums,late,qbc)

def per_device_pair(tokens,query_weight,query_bias,key_weight,value_weight,value_bias,out_weight,out_bias,first_gain,first_shift,
    up_weight,up_bias,down_weight,down_bias,second_gain,second_shift,cotangent,clip_limit):
    shards=(query_weight,key_weight,value_weight,out_weight.T,up_weight,down_weight.T)
    vectors=(out_bias,first_gain,first_shift,down_bias,second_gain,second_shift,up_bias,query_bias,value_bias)
    lo,gf,dqkv,dw,r1,r2,r3,early,xall,wh=main_call(shards,tokens,cotangent,vectors,1)
    tg,gq,gk,gv,go,gu,gd,sums,late,qc,kc,qbc=tail_call(dqkv,dw,r1,r2,r3,wh,xall,gf,early,query_weight,key_weight,query_bias,clip_limit,2)
    lo,tg,gq,gk,gv,go,gu,gd,qc,kc,qb,vb,ob,g1,b1,ub,db,g2,b2,pk,qbc=finish_call(lo,tg,gq,gk,gv,go,gu,gd,qc,kc,sums,late,qbc)
    return (lo,tg,gq,qb,gk,gv,vb,go.T,ob,g1,b1,gu,ub,gd.T,db,g2,b2,pk,qc,qbc,kc)


def layer(*args):
    paired = lax.axis_size("dp") == 16 and lax.axis_size("tensor") == 2 and 2 * args[0].shape[0] == LEN
    return per_device_pair(*args) if paired else per_device(*args)


def solution(mesh):
    in_specs = (
        P(("dp", "tensor"), None),
        P("dp", "tensor"),
        P("tensor"),
        P("dp", "tensor"),
        P("dp", "tensor"),
        P("tensor"),
        P("tensor", "dp"),
        P(),
        P(),
        P(),
        P("dp", "tensor"),
        P("tensor"),
        P("tensor", "dp"),
        P(),
        P(),
        P(),
        P(("dp", "tensor"), None),
        P("tensor"),
    )
    out_specs = (
        P(("dp", "tensor"), None),
        P(("dp", "tensor"), None),
        P("dp", "tensor"),
        P("tensor"),
        P("dp", "tensor"),
        P("dp", "tensor"),
        P("tensor"),
        P("tensor", "dp"),
        P(),
        P(),
        P(),
        P("dp", "tensor"),
        P("tensor"),
        P("tensor", "dp"),
        P(),
        P(),
        P(),
        P("tensor"),
        P("dp", "tensor"),
        P("tensor"),
        P("dp", "tensor"),
    )
    return jax.shard_map(
        layer, mesh=mesh, in_specs=in_specs, out_specs=out_specs, check_vma=False
    )
```

```python
import functools
import math

import jax
import jax.numpy as jnp
from jax import lax
from jax.experimental import pallas as pl
from jax.experimental.pallas import tpu as pltpu
from jax.sharding import PartitionSpec as P

HD = 64
LEN = 1024
QB = 512


def layer_norm(values, gain, shift):
    center = values - jnp.mean(values, axis=-1, keepdims=True)
    spread = jnp.mean(center * center, axis=-1, keepdims=True)
    return center * lax.rsqrt(spread + EPSILON) * gain + shift


def gelu_slope(upper):
    normal_cdf = 0.5 * (1.0 + lax.erf(upper * 0.5**0.5))
    return normal_cdf + upper * jnp.exp(-0.5 * upper * upper) * (0.5 / math.pi) ** 0.5


def contract_rows(left, right):
    return lax.dot_general(
        left, right, (((0,), (0,)), ((), ())), preferred_element_type=jnp.float32
    )


def contract_cols(left, right):
    return lax.dot_general(
        left, right, (((1,), (1,)), ((), ())), preferred_element_type=jnp.float32
    )


def per_device(
    tokens,
    query_weight,
    query_bias,
    key_weight,
    value_weight,
    value_bias,
    out_weight,
    out_bias,
    first_gain,
    first_shift,
    up_weight,
    up_bias,
    down_weight,
    down_bias,
    second_gain,
    second_shift,
    cotangent,
    clip_limit,
):
    query_full, key_full, value_full, out_full, up_full, down_full = (
        lax.all_gather(query_weight, "dp", axis=0, tiled=True),
        lax.all_gather(key_weight, "dp", axis=0, tiled=True),
        lax.all_gather(value_weight, "dp", axis=0, tiled=True),
        lax.all_gather(out_weight, "dp", axis=1, tiled=True),
        lax.all_gather(up_weight, "dp", axis=0, tiled=True),
        lax.all_gather(down_weight, "dp", axis=1, tiled=True),
    )
    width = query_full.shape[1]
    hidden_width = up_full.shape[1]
    heads_here = width // HD
    score_scale = HD ** (-0.5)
    joint_weight = jnp.concatenate([query_full, key_full, value_full], axis=1)
    gathered = lax.all_gather(tokens, "tensor", axis=0, tiled=True)
    group_rows = gathered.shape[0]
    seq_count = group_rows // LEN
    block_count = LEN // QB
    projected = jnp.dot(gathered, joint_weight, preferred_element_type=jnp.float32)
    queries = (projected[:, :width] + query_bias.astype(jnp.float32)).astype(jnp.bfloat16)
    keyset = projected[:, width : 2 * width].astype(jnp.bfloat16)
    valset = (projected[:, 2 * width :] + value_bias.astype(jnp.float32)).astype(jnp.bfloat16)
    query_seq = queries.reshape(seq_count, LEN, heads_here, HD)
    key_seq = keyset.reshape(seq_count, LEN, heads_here, HD)
    value_seq = valset.reshape(seq_count, LEN, heads_here, HD)

    def attend_block(block_id):
        seq_id = block_id // block_count
        row_start = block_id % block_count * QB
        query_rows = lax.dynamic_slice_in_dim(
            lax.dynamic_index_in_dim(query_seq, seq_id, 0, False), row_start, QB, 0
        )
        key_rows = lax.dynamic_index_in_dim(key_seq, seq_id, 0, False)
        value_rows = lax.dynamic_index_in_dim(value_seq, seq_id, 0, False)
        logits = (
            jnp.einsum("qhd,khd->hqk", query_rows, key_rows, preferred_element_type=jnp.float32)
            * score_scale
        )
        row_max = jnp.max(logits, axis=2, keepdims=True)
        exponent = jnp.exp(logits - row_max)
        totals = jnp.sum(exponent, axis=2, keepdims=True)
        probs_low = (exponent / totals).astype(jnp.bfloat16)
        context_rows = jnp.einsum(
            "hqk,khd->qhd", probs_low, value_rows, preferred_element_type=jnp.float32
        )
        return (
            context_rows.reshape(QB, width).astype(jnp.bfloat16),
            (row_max + jnp.log(totals))[:, :, 0],
            jnp.max(row_max, axis=(1, 2)),
        )

    context_blocks, log_totals, block_peaks = lax.map(
        attend_block, jnp.arange(seq_count * block_count)
    )
    context = context_blocks.reshape(group_rows, width)
    logit_peak = lax.pmax(jnp.max(block_peaks, axis=0), "dp")
    attention = lax.psum_scatter(
        jnp.dot(context, out_full, preferred_element_type=jnp.float32).astype(jnp.bfloat16),
        "tensor",
        scatter_dimension=0,
        tiled=True,
    ).astype(jnp.float32) + out_bias.astype(jnp.float32)
    first_resid = tokens.astype(jnp.float32) + attention
    hidden, first_pull = jax.vjp(
        layer_norm, first_resid, first_gain.astype(jnp.float32), first_shift.astype(jnp.float32)
    )
    hidden_all = lax.all_gather(hidden.astype(jnp.bfloat16), "tensor", axis=0, tiled=True)
    upper = jnp.dot(hidden_all, up_full, preferred_element_type=jnp.float32) + up_bias.astype(
        jnp.float32
    )
    acted = jax.nn.gelu(upper, approximate=False).astype(jnp.bfloat16)
    branch = lax.psum_scatter(
        jnp.dot(acted, down_full, preferred_element_type=jnp.float32).astype(jnp.bfloat16),
        "tensor",
        scatter_dimension=0,
        tiled=True,
    ).astype(jnp.float32) + down_bias.astype(jnp.float32)
    normed, second_pull = jax.vjp(
        layer_norm,
        hidden + branch,
        second_gain.astype(jnp.float32),
        second_shift.astype(jnp.float32),
    )
    layer_out = normed.astype(jnp.bfloat16)
    grad_second, second_gain_grad, second_shift_grad = second_pull(cotangent.astype(jnp.float32))
    grad_branch = grad_second.astype(jnp.bfloat16)
    down_bias_grad = jnp.sum(grad_branch, axis=0, dtype=jnp.float32)
    branch_all = lax.all_gather(grad_branch, "tensor", axis=0, tiled=True)
    grad_acted = contract_cols(branch_all, down_full)
    down_weight_grad = contract_rows(acted, branch_all)
    grad_upper = (grad_acted * gelu_slope(upper)).astype(jnp.bfloat16)
    up_bias_grad = jnp.sum(grad_upper, axis=0, dtype=jnp.float32)
    up_weight_grad = contract_rows(hidden_all, grad_upper)
    grad_hidden = grad_second + lax.psum_scatter(
        contract_cols(grad_upper, up_full).astype(jnp.bfloat16),
        "tensor",
        scatter_dimension=0,
        tiled=True,
    ).astype(jnp.float32)
    grad_first, first_gain_grad, first_shift_grad = first_pull(grad_hidden)
    grad_attn = grad_first.astype(jnp.bfloat16)
    out_bias_grad = jnp.sum(grad_attn, axis=0, dtype=jnp.float32)
    attn_all = lax.all_gather(grad_attn, "tensor", axis=0, tiled=True)
    grad_context = contract_cols(attn_all, out_full).astype(jnp.bfloat16)
    out_weight_grad = contract_rows(context, attn_all)
    query_blocks = queries.reshape(seq_count, block_count, QB, heads_here, HD)
    grad_blocks = grad_context.reshape(seq_count, block_count, QB, heads_here, HD)
    log_blocks = log_totals.reshape(seq_count, block_count, heads_here, QB)

    def sequence_back(item):
        query_part, grad_part, log_part, key_rows, value_rows = item

        def block_back(carry, piece):
            key_acc, value_acc = carry
            query_rows, grad_rows, log_rows = piece
            logits = (
                jnp.einsum("qhd,khd->hqk", query_rows, key_rows, preferred_element_type=jnp.float32)
                * score_scale
            )
            probs = jnp.exp(logits - log_rows[:, :, None])
            probs_low = probs.astype(jnp.bfloat16)
            value_acc = value_acc + jnp.einsum(
                "hqk,qhd->khd", probs_low, grad_rows, preferred_element_type=jnp.float32
            )
            grad_probs = jnp.einsum(
                "qhd,khd->hqk", grad_rows, value_rows, preferred_element_type=jnp.float32
            )
            inner = jnp.sum(probs * grad_probs, axis=2, keepdims=True)
            grad_logits = (probs * (grad_probs - inner)).astype(jnp.bfloat16)
            grad_query = (
                jnp.einsum(
                    "hqk,khd->qhd", grad_logits, key_rows, preferred_element_type=jnp.float32
                )
                * score_scale
            )
            key_acc = (
                key_acc
                + jnp.einsum(
                    "hqk,qhd->khd", grad_logits, query_rows, preferred_element_type=jnp.float32
                )
                * score_scale
            )
            return ((key_acc, value_acc), grad_query.astype(jnp.bfloat16))

        empty = jnp.zeros((LEN, heads_here, HD), jnp.float32)
        (key_acc, value_acc), grad_query_rows = lax.scan(
            block_back, (empty, empty), (query_part, grad_part, log_part)
        )
        return (grad_query_rows, key_acc.astype(jnp.bfloat16), value_acc.astype(jnp.bfloat16))

    grad_queries_all, grad_keys_all, grad_values_all = lax.map(
        sequence_back, (query_blocks, grad_blocks, log_blocks, key_seq, value_seq)
    )
    grad_joint = jnp.concatenate(
        [
            grad_queries_all.reshape(group_rows, width),
            grad_keys_all.reshape(group_rows, width),
            grad_values_all.reshape(group_rows, width),
        ],
        axis=1,
    )
    joint_grad = contract_rows(gathered, grad_joint)
    query_weight_grad = joint_grad[:, :width]
    key_weight_grad = joint_grad[:, width : 2 * width]
    value_weight_grad = joint_grad[:, 2 * width :]
    query_bias_grad = jnp.sum(grad_joint[:, :width], axis=0, dtype=jnp.float32)
    value_bias_grad = jnp.sum(grad_joint[:, 2 * width :], axis=0, dtype=jnp.float32)
    tokens_grad = (
        grad_first
        + lax.psum_scatter(
            contract_cols(grad_joint, joint_weight).astype(jnp.bfloat16),
            "tensor",
            scatter_dimension=0,
            tiled=True,
        ).astype(jnp.float32)
    ).astype(jnp.bfloat16)
    (
        query_weight_grad,
        key_weight_grad,
        value_weight_grad,
        out_weight_grad,
        up_weight_grad,
        down_weight_grad,
    ) = (
        lax.psum_scatter(
            query_weight_grad.astype(jnp.bfloat16), "dp", scatter_dimension=0, tiled=True
        ).astype(jnp.float32),
        lax.psum_scatter(
            key_weight_grad.astype(jnp.bfloat16), "dp", scatter_dimension=0, tiled=True
        ).astype(jnp.float32),
        lax.psum_scatter(
            value_weight_grad.astype(jnp.bfloat16), "dp", scatter_dimension=0, tiled=True
        ).astype(jnp.float32),
        lax.psum_scatter(
            out_weight_grad.astype(jnp.bfloat16), "dp", scatter_dimension=1, tiled=True
        ).astype(jnp.float32),
        lax.psum_scatter(
            up_weight_grad.astype(jnp.bfloat16), "dp", scatter_dimension=0, tiled=True
        ).astype(jnp.float32),
        lax.psum_scatter(
            down_weight_grad.astype(jnp.bfloat16), "dp", scatter_dimension=1, tiled=True
        ).astype(jnp.float32),
    )
    tensor_place = lax.axis_index("tensor")
    model_width = out_bias.shape[0]
    query_spread = lax.dynamic_update_slice_in_dim(
        jnp.zeros((model_width,), jnp.float32), query_bias_grad, tensor_place * width, 0
    )
    value_spread = lax.dynamic_update_slice_in_dim(
        jnp.zeros((model_width,), jnp.float32), value_bias_grad, tensor_place * width, 0
    )
    up_spread = lax.dynamic_update_slice_in_dim(
        jnp.zeros((hidden_width * lax.axis_size("tensor"),), jnp.float32),
        up_bias_grad,
        tensor_place * hidden_width,
        0,
    )
    (
        query_spread,
        value_spread,
        up_spread,
        out_bias_grad,
        down_bias_grad,
        first_gain_grad,
        first_shift_grad,
        second_gain_grad,
        second_shift_grad,
    ) = lax.psum(
        (
            query_spread,
            value_spread,
            up_spread,
            out_bias_grad,
            down_bias_grad,
            first_gain_grad,
            first_shift_grad,
            second_gain_grad,
            second_shift_grad,
        ),
        ("dp", "tensor"),
    )
    query_bias_grad = lax.dynamic_slice_in_dim(query_spread, tensor_place * width, width, 0)
    value_bias_grad = lax.dynamic_slice_in_dim(value_spread, tensor_place * width, width, 0)
    up_bias_grad = lax.dynamic_slice_in_dim(up_spread, tensor_place * hidden_width, hidden_width, 0)
    factor = clip_limit / jnp.maximum(logit_peak, clip_limit)
    column_scale = jnp.repeat(jnp.sqrt(factor), HD)
    query_clipped = (query_weight.astype(jnp.float32) * column_scale).astype(jnp.bfloat16)
    query_bias_clipped = (query_bias.astype(jnp.float32) * column_scale).astype(jnp.bfloat16)
    key_clipped = (key_weight.astype(jnp.float32) * column_scale).astype(jnp.bfloat16)
    return (
        layer_out,
        tokens_grad,
        query_weight_grad,
        query_bias_grad,
        key_weight_grad,
        value_weight_grad,
        value_bias_grad,
        out_weight_grad,
        out_bias_grad,
        first_gain_grad,
        first_shift_grad,
        up_weight_grad,
        up_bias_grad,
        down_weight_grad,
        down_bias_grad,
        second_gain_grad,
        second_shift_grad,
        logit_peak,
        query_clipped,
        query_bias_clipped,
        key_clipped,
    )


LOG2E=1.4426950408889634
NT=(((1,),(1,)),((),()))
NN=(((1,),(0,)),((),()))
F32=jnp.float32
BF=jnp.bfloat16
MESH=pl.DeviceIdType.MESH
EPSILON=1e-5
NC=4


def dot(a,b,dims):
    return lax.dot_general(a,b,dims,preferred_element_type=jnp.float32)


def greet(partner):
    barrier=pltpu.get_barrier_semaphore()
    pl.semaphore_signal(barrier,inc=1,device_id=partner,device_id_type=MESH)
    pl.semaphore_wait(barrier,1)


def main_kernel(wq,wk,wv,wos,wu,wds,tok,cot_hbm,v_ob,v_g1,v_b1,v_db,v_g2,v_b2,v_ub,v_qb,v_vb,
               lo_hbm,gf,dqkv_hbm,dw,r1,r2,r3,early,x_hbm,wh_hbm,
               bias,vec,upb,sh,qkv,vt,kt,ctx,ctxo,lse,cl,wo,wup,wdn,xh,rst,hall,act,slp,ball,ga,dcs,dcall,part,pch,ctt,dqt,dl,dkv,sbuf,rbuf,tb,th,stage,
               lsem,losem,dsem,osem,ssem,rsem,rl,g1s,g1r,g2s,g2r,g3s,g3r,ts,tr,azs,azr,axs,axr,acs,acr):
    d=lax.axis_index("dp"); t=lax.axis_index("tensor")
    partner=(d,1-t)
    core=d%2; x_=(d//2)%2; z=d//4
    def dev(z_,xx,c_): return ((z_*2+xx)*2+c_,t)
    sib=dev(z,x_,1-core); xp=dev(z,1-x_,core); zp=[dev((z+k)%4,x_,core) for k in (1,2,3)]
    own,dm=tok.shape; cr=own//NC; cg=2*cr; rows_all=2*own; width=ctx.shape[1]; ff=wup.shape[2]; wide=wo.shape[2]; pairs=width//128
    def local(src,dst,i): return pltpu.make_async_copy(src,dst,lsem.at[i])
    def remote(src,dst,a,b,p): return pltpu.make_async_remote_copy(src,dst,a,b,device_id=p,device_id_type=MESH)
    cot_load=local(cot_hbm,cl,0)
    cot_load.start()
    barrier=pltpu.get_barrier_semaphore()
    n=3*width
    def row(v): return v[...].astype(F32).reshape(1,v.shape[0])
    sh[:,0:width]=wq[...]; sh[:,width:2*width]=wk[...]; sh[:,2*width:n]=wv[...]
    everyone=[partner,sib,xp]+zp
    for p in everyone: pl.semaphore_signal(barrier,inc=1,device_id=p,device_id_type=MESH)
    def chunk(c): return pl.ds(pl.multiple_of(c*cg,cg),cg)
    def rows(rank,c): return pl.ds(pl.multiple_of(c*cg+rank*cr,cr),cr)
    def half(rank): return pl.ds(pl.multiple_of(rank*cr,cr),cr)
    def loc(c): return pl.ds(pl.multiple_of(c*cr,cr),cr)
    def rs_copy(k,c):
        return pltpu.make_async_remote_copy(sbuf.at[k-1,loc(c)],rbuf.at[k-1,loc(c)],ssem.at[k,c],rsem.at[k,c],device_id=partner,device_id_type=MESH)
    def ag_copy(k,buf,c,rank):
        return pltpu.make_async_remote_copy(buf.at[rows(rank,c)],buf.at[rows(rank,c)],ssem.at[k,c],rsem.at[k,c],device_id=partner,device_id_type=MESH)
    def cols(rank): return pl.ds(pl.multiple_of(rank*width,128),width)
    def ctx_copy(c,rank):
        return pltpu.make_async_remote_copy(ctx.at[rows(1-rank,c)],ctxo.at[loc(c),cols(rank)],ssem.at[0,c],rsem.at[0,c],device_id=partner,device_id_type=MESH)
    def dctx_copy(c,rank):
        return pltpu.make_async_remote_copy(dcs.at[loc(c),cols(1-rank)],dcall.at[rows(rank,c)],ssem.at[5,c],rsem.at[5,c],device_id=partner,device_id_type=MESH)
    early[...]=jnp.zeros_like(early)
    early[10:11]=jnp.full_like(early[10:11],-jnp.inf)
    def whole(w): return w[...].reshape(dm,w.shape[2])
    def strip(w,cs): return w[:,:,cs].reshape(dm,TF)
    dkv[...]=jnp.zeros_like(dkv)
    lane=lax.broadcasted_iota(jnp.int32,(1,128),1)
    scale=jnp.bfloat16(HD**-0.5); zero=jnp.bfloat16(0)
    q4=ff//2
    groups=[(act,0,0,width),(act,width,width,width),(act,2*width,2*width,width),(wo,0,n,wide),
            (wup,0,n+wide,q4),(wup,q4,n+wide+q4,q4),(wdn,0,n+wide+ff,q4),(wdn,q4,n+wide+ff+q4,q4)]
    def block(z_,xx): return (z_*2+xx)*2+core
    me=block(z,x_)
    def place(g,b):
        buf,c0,_,nc=groups[g]
        return buf.at[b,:,c0:c0+nc]
    def z_hop(g,k,b): return remote(sh.at[:,groups[g][2]:groups[g][2]+groups[g][3]],place(g,b),azs.at[g,k-1],azr.at[g,k-1],zp[k-1])
    def x_hop(g,k,b): return remote(sh.at[:,groups[g][2]:groups[g][2]+groups[g][3]] if k==0 else place(g,b),place(g,b),axs.at[g,k],axr.at[g,k],xp)
    def c_hop(g,k,b): return remote(sh.at[:,groups[g][2]:groups[g][2]+groups[g][3]] if k==0 else place(g,b),place(g,b),acs.at[g,k],acr.at[g,k],sib)
    def back(k): return (z-k)%4
    def gather_start(g):
        buf,c0,s0,nc=groups[g]
        for k in (1,2,3): z_hop(g,k,me).start()
        x_hop(g,0,me).start()
        c_hop(g,0,me).start()
        buf[me,:,c0:c0+nc]=sh[:,s0:s0+nc]
    def gather_sent(g):
        for k in (1,2,3): z_hop(g,k,me).wait_send()
    def gather_x(g):
        for k in (1,2,3):
            b=block(back(k),x_)
            z_hop(g,k,b).wait_recv()
            x_hop(g,k,b).start()
            c_hop(g,k,b).start()
    def gather_core(g):
        for k in (0,1,2,3):
            b=block(back(k),1-x_)
            x_hop(g,k,b).wait_recv()
            c_hop(g,4+k,b).start()
    def gather_done(g):
        for k in range(8): c_hop(g,k,me).wait_recv()
        for k in range(4): x_hop(g,k,me).wait_send()
        for k in range(8): c_hop(g,k,me).wait_send()
    own_copies=[local(tok.at[c*cr:(c+1)*cr],hall.at[rows(t,c)],1+c) for c in range(NC)]
    for c in own_copies: c.start()
    pl.semaphore_wait(barrier,len(everyone))
    gather_start(0)
    def tok_copy(c): return remote(tok.at[loc(c)],hall.at[rows(t,c)],ts.at[c],tr.at[c],partner)
    def mine_o(rank): return sh.at[:,pl.ds(pl.multiple_of(n+rank*width,128),width)]
    o_swap=remote(mine_o(t),mine_o(t),ts.at[NC],tr.at[NC],partner)
    sh[:,pl.ds(pl.multiple_of(n+t*width,128),width)]=wos[...]
    o_swap.start()
    @pl.loop(0,NC)
    def _(c): tok_copy(c).start()
    sh[:,n+wide:n+wide+ff]=wu[...]
    sh[:,n+wide+ff:]=wds[...]
    for i,v in enumerate((v_ob,v_g1,v_b1,v_db,v_g2,v_b2)): vec[i:i+1]=row(v)
    upb[...]=row(v_ub)
    bias[...]=jnp.zeros_like(bias)
    bias[:,0:width]=row(v_qb); bias[:,2*width:]=row(v_vb)
    gather_sent(0); gather_start(1)
    gather_x(0)
    gather_sent(1); gather_start(2)
    gather_x(1)
    gather_core(0)
    o_swap.wait_recv()
    gather_sent(2); gather_start(3)
    gather_x(2)
    gather_core(1); gather_core(2)
    for g in range(3): gather_done(g)
    gather_sent(3); gather_start(4)
    gather_x(3)
    for c in own_copies: c.wait()
    TF=512
    @pl.loop(0,NC)
    def _(c):
        tok_copy(c).wait_recv()
        @pl.loop(0,n//TF)
        def _(j):
            cs=pl.ds(pl.multiple_of(j*TF,TF),TF)
            qkv[chunk(c),cs]=(dot(hall[chunk(c)],strip(act,cs),NN)+bias[:,cs]).astype(BF)
    x_out=local(hall,x_hbm,5); w_out=local(act.at[:,:,0:n],wh_hbm,6)
    x_out.start(); w_out.start()
    gather_core(3)
    ones=jnp.where(lax.broadcasted_iota(jnp.int32,(16,rows_all),0)==0,1.0,0.0).astype(BF)
    @pl.loop(0,pairs)
    def _(p):
        ck=pl.multiple_of(width+p*128,128); cv=pl.multiple_of(2*width+p*128,128)
        kt[p]=qkv[:,pl.ds(ck,128)].T
        v=qkv[:,pl.ds(cv,128)].T
        vt[2*p,0:64]=v[0:64]; vt[2*p,64:80]=ones
        vt[2*p+1,0:64]=v[64:128]; vt[2*p+1,64:80]=ones
    x_out.wait()
    def split(k,c):
        sbuf[k-1,loc(c)]=pch[half(1-t)].astype(BF)
        rs_copy(k,c).start()
        part[loc(c)]=pch[half(t)]
    def stats(v):
        cen=v-jnp.mean(v,axis=1,keepdims=True)
        r=lax.rsqrt(jnp.mean(cen*cen,axis=1,keepdims=True)+EPSILON)
        return cen*r,r
    def lo_copy(c): return pltpu.make_async_copy(cl.at[loc(c)],lo_hbm.at[loc(c)],losem.at[c])
    def out_copy(slot,col):
        return pltpu.make_async_copy(stage.at[slot],dw.at[:,:,:,:,pl.ds(pl.multiple_of(col,512),512)],osem.at[slot])
    def wgrad(slot,left,right_ref,rcol,ocol):
        @pl.loop(0,dm//256)
        def _(i):
            ms=pl.ds(pl.multiple_of(i*256,256),256)
            right=right_ref[:,pl.ds(pl.multiple_of(rcol,512),512)] if len(right_ref.shape)==2 else strip(right_ref,pl.ds(pl.multiple_of(rcol,512),512))
            stage[slot,i]=dot(left[ms],right,NN).astype(BF).reshape(2,2,64,512)
        out_copy(slot,ocol).start()
    def stage_a(c):
        rs=chunk(c)
        @pl.loop(0,pairs)
        def _(p):
            cq=pl.ds(pl.multiple_of(p*128,128),128); ck=pl.ds(pl.multiple_of(width+p*128,128),128)
            pks=[]
            for h in (0,1):
                keep=(lane<64) if h==0 else (lane>=64)
                q=jnp.where(keep,qkv[rs,cq]*scale,zero)
                st=dot(qkv[:,ck],q,NT)
                m=jnp.max(st,axis=0,keepdims=True)
                mc=m*LOG2E
                pt=jnp.exp2(st*LOG2E-mc).astype(BF)
                ot=dot(vt[2*p+h],pt,NN)
                tot=ot[64:65]
                ctt[h*64:(h+1)*64,:]=ot[0:64]*(1.0/tot)
                lse[pl.ds(2*p+h,1),rs]=mc+jnp.log2(tot)
                pks.append(jnp.max(m,axis=1,keepdims=True))
            early[10:11,cq]=jnp.maximum(early[10:11,cq],jnp.where(lane<64,pks[0],pks[1]))
            ctx[rs,cq]=ctt[...].T.astype(BF)
            step=c*pairs+p
            @pl.when(step==2)
            def _():
                gather_sent(4); gather_start(5)
                gather_x(4)
                gather_done(3)
            @pl.when(step==8)
            def _():
                gather_sent(5); gather_start(6)
                gather_x(5)
                gather_core(4)
            @pl.when(step==14)
            def _():
                gather_sent(6); gather_start(7)
                gather_x(6)
                gather_core(5)
        ctx_copy(c,t).start()
        ctxo[loc(c),cols(t)]=ctx[rows(t,c)]
    def stage_b(c):
        ctx_copy(c,1-t).wait_recv()
        x,r=stats(hall[rows(t,c)].astype(F32)+dot(ctxo[loc(c)],whole(wo),NT)+vec[0:1])
        xh[loc(c)]=x
        rst[loc(c)]=jnp.broadcast_to(r,(cr,128))
        hall[rows(t,c)]=(x*vec[1:2]+vec[2:3]).astype(BF)
        ag_copy(3,hall,c,t).start()
    def stage_c(c):
        rs=chunk(c)
        ag_copy(3,hall,c,1-t).wait_recv()
        @pl.loop(0,ff//TF)
        def _(j):
            cs=pl.ds(pl.multiple_of(j*TF,TF),TF)
            u=dot(hall[rs],strip(wup,cs),NN)+upb[:,cs]
            cdf=0.5*(1.0+lax.erf(u*0.5**0.5))
            act[pl.ds(4*c,4),:,cs]=(u*cdf).astype(BF).reshape(4,64,TF)
            slp[rs,cs]=(cdf+u*jnp.exp(-0.5*u*u)*(0.5/math.pi)**0.5).astype(BF)
        @pl.when(c==0)
        def _():
            gather_core(6)
            gather_sent(7); gather_x(7)
            gather_core(7)
            gather_done(6); gather_done(7)
        pch[...]=dot(act[pl.ds(4*c,4)].reshape(cg,ff),whole(wdn),NT)
        split(1,c)
    def stage_d(c):
        rs_copy(1,c).wait_recv()
        x,r=stats(xh[loc(c)]*vec[1:2]+vec[2:3]+part[loc(c)]+rbuf[0,loc(c)].astype(F32)+vec[3:4])
        dy=cl[loc(c)].astype(F32)
        cl[loc(c)]=(x*vec[4:5]+vec[5:6]).astype(BF)
        lo_copy(c).start()
        early[4:5]+=jnp.sum(dy*x,axis=0,keepdims=True)
        early[5:6]+=jnp.sum(dy,axis=0,keepdims=True)
        dx=dy*vec[4:5]
        g=r*(dx-jnp.mean(dx,axis=1,keepdims=True)-x*jnp.mean(dx*x,axis=1,keepdims=True))
        gf[loc(c)]=g
        gb=g.astype(BF)
        early[3:4]+=jnp.sum(gb.astype(F32),axis=0,keepdims=True)
        ball[rows(t,c)]=gb
        ag_copy(4,ball,c,t).start()
        tb[:,rows(t,c)]=gb.T
    def stage_e(c):
        rs=chunk(c)
        ag_copy(4,ball,c,1-t).wait_recv()
        @pl.loop(0,ff//TF)
        def _(j):
            cs=pl.ds(pl.multiple_of(j*TF,TF),TF)
            gu=(dot(ball[rs],strip(wdn,cs),NN)*slp[rs,cs].astype(F32)).astype(BF)
            slp[rs,cs]=gu
            row=pl.ds(8+j*TF//dm,1); cc=pl.ds(pl.multiple_of(j*TF%dm,TF),TF)
            early[row,cc]+=jnp.sum(gu.astype(F32),axis=0,keepdims=True)
        pch[...]=dot(slp[rs],whole(wup),NT)
        split(2,c)
        tb[:,rows(1-t,c)]=ball[rows(1-t,c)].T
        th[:,chunk(c)]=hall[chunk(c)].T
    def stage_f(c):
        rs_copy(2,c).wait_recv()
        dy=gf[loc(c)]+part[loc(c)]+rbuf[1,loc(c)].astype(F32)
        x=xh[loc(c)]; r=rst[loc(c)][:,0:1]
        early[1:2]+=jnp.sum(dy*x,axis=0,keepdims=True)
        early[2:3]+=jnp.sum(dy,axis=0,keepdims=True)
        dx=dy*vec[1:2]
        g=r*(dx-jnp.mean(dx,axis=1,keepdims=True)-x*jnp.mean(dx*x,axis=1,keepdims=True))
        gf[loc(c)]=g
        gb=g.astype(BF)
        early[0:1]+=jnp.sum(gb.astype(F32),axis=0,keepdims=True)
        ga[loc(c)]=gb
        dcs[loc(c)]=dot(gb,whole(wo),NN).astype(BF)
        dctx_copy(c,t).start()
        dcall[rows(t,c)]=dcs[loc(c),cols(t)]
    def stage_g(c):
        rs=chunk(c)
        dctx_copy(c,1-t).wait_recv()
        @pl.loop(0,pairs)
        def _(p):
            cq=pl.ds(pl.multiple_of(p*128,128),128); ck=pl.ds(pl.multiple_of(width+p*128,128),128); cv=pl.ds(pl.multiple_of(2*width+p*128,128),128)
            prod=(ctx[rs,cq].astype(F32)*dcall[rs,cq].astype(F32)).T
            dl[0:1]=jnp.sum(prod[0:64],axis=0,keepdims=True)
            dl[1:2]=jnp.sum(prod[64:128],axis=0,keepdims=True)
            for h in (0,1):
                keep=(lane<64) if h==0 else (lane>=64)
                q=jnp.where(keep,qkv[rs,cq]*scale,zero)
                do=jnp.where(keep,dcall[rs,cq],zero)
                st=dot(qkv[:,ck],q,NT)
                pt=jnp.exp2(st*LOG2E-lse[pl.ds(2*p+h,1),rs])
                dpt=dot(qkv[:,cv],do,NT)
                ds=(pt*(dpt-dl[h:h+1])).astype(BF)
                dkv[1,:,cq]+=dot(pt.astype(BF),do,NN)
                dkv[0,:,cq]+=dot(ds,q,NN)
                dqt[h*64:(h+1)*64,:]=dot(kt[p,h*64:(h+1)*64,:],ds,NN)
            qkv[rs,cq]=(dqt[...].T*(HD**-0.5)).astype(BF)
    def grad_down(c):
        slot=c%2
        @pl.when(c>=2)
        def _(): out_copy(slot,0).wait()
        wgrad(slot,tb,act,c*512,wide+ff+c*512)
    def grad_up(c):
        slot=c%2
        @pl.when(c>=2)
        def _(): out_copy(slot,0).wait()
        wgrad(slot,th,slp,c*512,wide+c*512)
    def grad_out():
        @pl.loop(0,NC)
        def _(c): tb[:,loc(c)]=ga[loc(c)].T
        for j in range(wide//512):
            @pl.loop(0,dm//256)
            def _(i):
                ms=pl.ds(pl.multiple_of(i*256,256),256)
                stage[j%2,i]=dot(tb[ms,0:own],ctxo[:,j*512:(j+1)*512],NN).astype(BF).reshape(2,2,64,512)
            out_copy(j%2,j*512).start()
    @pl.loop(0,NC)
    def _(c):
        stage_a(c)
        @pl.when(c>0)
        def _(): stage_b(c-1)
    cot_load.wait(); w_out.wait()
    gather_done(4); gather_done(5)
    @pl.loop(0,NC)
    def _(c):
        stage_c(c)
        @pl.when(c==0)
        def _(): stage_b(NC-1)
        @pl.when(c>=2)
        def _(): stage_d(c-2)
    @pl.loop(NC-2,NC)
    def _(c): stage_d(c)
    @pl.loop(0,NC)
    def _(c): stage_e(c)
    base=(wide+ff,wide)
    def s1(g): return remote(dw.at[:,:,1-core,:,base[g]:base[g]+ff],r1.at[g],g1s.at[g],g1r.at[g],sib)
    def s2(g): return remote(wup.at[8+4*g:12+4*g],r2.at[g],g2s.at[g],g2r.at[g],xp)
    def s3(k): return remote(wdn.at[12+(z+k)%4],r3.at[3-k],g3s.at[k-1],g3r.at[k-1],zp[k-1])
    def load2(g): return [pltpu.make_async_copy(dw.at[:,1-x_,core,:,base[g]:base[g]+ff],wup.at[0:4],rl.at[0]),
                          pltpu.make_async_copy(r1.at[g,:,1-x_],wup.at[4:8],rl.at[1])]
    def load3(): return [pltpu.make_async_copy(dw.at[:,x_,core,:,base[0]:base[0]+ff],wdn.at[0:4],rl.at[2]),
                         pltpu.make_async_copy(r1.at[0,:,x_],wdn.at[4:8],rl.at[3]),
                         pltpu.make_async_copy(r2.at[0],wdn.at[8:12],rl.at[4])]
    def add2(g):
        for c in load2(g): c.wait()
        @pl.loop(0,4)
        def _(i): wup[8+4*g+i]=(wup[i].astype(F32)+wup[4+i].astype(F32)).astype(BF)
    @pl.loop(0,NC)
    def _(c): grad_down(c)
    out_copy(0,0).wait()
    out_copy(1,0).wait()
    s1(0).start()
    @pl.loop(0,NC)
    def _(c):
        stage_f(c)
        grad_up(c)
        @pl.when(c==1)
        def _():
            s1(0).wait_recv()
            for l in load2(0): l.start()
        @pl.when(c==2)
        def _():
            add2(0)
            s2(0).start()
    out_copy(0,0).wait()
    out_copy(1,0).wait()
    s1(1).start()
    grad_out()
    @pl.loop(0,NC)
    def _(c):
        stage_g(c)
        @pl.when(c==0)
        def _():
            s1(1).wait_recv()
            for l in load2(1): l.start()
        @pl.when(c==1)
        def _():
            add2(1)
            s2(0).wait_send()
            s2(1).start()
            s2(0).wait_recv()
            for l in load3(): l.start()
        @pl.when(c==2)
        def _():
            for l in load3(): l.wait()
            @pl.loop(0,4)
            def _(i): wdn[12+i]=(wdn[i].astype(F32)+wdn[4+i].astype(F32)+wdn[8+i].astype(F32)).astype(BF)
            for k in (1,2,3): s3(k).start()
    @pl.loop(0,pairs)
    def _(p):
        cq=pl.ds(pl.multiple_of(p*128,128),128); ck=pl.ds(pl.multiple_of(width+p*128,128),128); cv=pl.ds(pl.multiple_of(2*width+p*128,128),128)
        qkv[:,ck]=dkv[0,:,cq].astype(BF)
        qkv[:,cv]=dkv[1,:,cq].astype(BF)
    dq_out=pltpu.make_async_copy(qkv,dqkv_hbm,dsem.at[0])
    dq_out.start()
    out_copy(0,0).wait()
    out_copy(1,0).wait()
    dq_out.wait()
    o_swap.wait_send()
    for g in (0,1): s1(g).wait_send()
    s2(1).wait()
    for k in (1,2,3): s3(k).wait()
    @pl.loop(0,NC)
    def _(c):
        lo_copy(c).wait()
        ctx_copy(c,t).wait_send(); dctx_copy(c,t).wait_send(); tok_copy(c).wait_send()
        for k in (1,2): rs_copy(k,c).wait_send()
        for k,buf in ((3,hall),(4,ball)): ag_copy(k,buf,c,t).wait_send()

def main_call(shards,tok,cot,vectors,cid):
    V=pl.BlockSpec(memory_space=pltpu.VMEM); A=pl.BlockSpec(memory_space=pl.ANY)
    width=shards[0].shape[1]; ff=shards[4].shape[1]; own,dm=tok.shape; rows=2*own; n=3*width; cr=own//NC; wide=2*width
    S=jax.ShapeDtypeStruct; M=pltpu.VMEM; D=pltpu.SemaphoreType.DMA
    return pl.pallas_call(main_kernel,
      out_shape=(S((own,dm),BF),S((own,dm),F32),S((rows,n),BF),S((4,2,2,64,wide+2*ff),BF),S((2,4,2,64,ff),BF),S((2,4,64,ff),BF),S((3,64,ff),BF),S((16,dm),F32),S((rows,dm),BF),S((16,64,n),BF)),
      in_specs=[V]*6+[A,A]+[V]*9,out_specs=(A,V,A,A,A,A,A,V,A,A),
      scratch_shapes=[M((1,n),F32),M((8,dm),F32),M((1,ff),F32),M((64,n+wide+2*ff),BF),M((rows,n),BF),M((width//HD,80,rows),BF),M((width//128,128,rows),BF),M((rows,width),BF),M((own,wide),BF),M((width//HD,rows),F32),M((own,dm),BF),
        M((16,64,wide),BF),M((16,64,ff),BF),M((16,64,ff),BF),
        M((own,dm),F32),M((own,128),F32),
        M((rows,dm),BF),M((16,64,ff),BF),M((rows,ff),BF),M((rows,dm),BF),M((own,dm),BF),M((own,wide),BF),M((rows,width),BF),
        M((own,dm),F32),M((2*cr,dm),F32),M((128,2*cr),F32),M((128,2*cr),F32),M((8,2*cr),F32),M((2,rows,width),F32),
        M((2,own,dm),BF),M((2,own,dm),BF),
        M((dm,rows),BF),M((dm,rows),BF),M((2,4,2,2,64,512),BF),
        D((7,)),D((NC,)),D((1,)),D((2,)),D((6,NC)),D((6,NC)),D((5,)),D((2,)),D((2,)),D((2,)),D((2,)),D((3,)),D((3,)),
        D((NC+1,)),D((NC+1,)),D((8,3)),D((8,3)),D((8,4)),D((8,4)),D((8,8)),D((8,8))],
      compiler_params=pltpu.CompilerParams(collective_id=cid,has_side_effects=True,vmem_limit_bytes=61*2**20),
      name="main")(*shards,tok,cot,*vectors)

def tail_kernel(dqkv_ref,dw,r1w,r2w,r3w,w_hbm,x_hbm,gf,early,wq,wk,bq,lim,
                tg,gq,gk,gv,go,gu,gd,sums,late,qc,kc,qbc,
                xv,xt,wv,part,pc,dwh,ysb,yrb,fw,zu,su,ru,oo,o1,o2s,o2,o3s,o3,h1,h2s,h2,h3s,h3,osb,orb,eb,er,lb,lr,
                lsem,s1s,s1r,s2s,s2r,s3s,s3r,ysend,yrecv,es,erc,ls,lrc,os_,or_):
    d=lax.axis_index("dp"); t=lax.axis_index("tensor")
    core=d%2; x=(d//2)%2; z=d//4
    def dev(z_,x_,c_): return ((z_*2+x_)*2+c_,t)
    sib=dev(z,x,1-core); xp=dev(z,1-x,core); yp=(d,1-t)
    zp=[dev((z+k)%4,x,core) for k in (1,2,3)]
    zb=[dev(z+1-2*(z%2),x,core),dev((z+2)%4,x,core)]
    barrier=pltpu.get_barrier_semaphore()
    everyone=[sib,xp,yp]+zp
    for p in everyone: pl.semaphore_signal(barrier,inc=1,device_id=p,device_id_type=MESH)
    own,dm=gf.shape; rows,n=dqkv_ref.shape; width=n//3; cr=own//NC; ff=fw.shape[2]; wide=2*width
    def remote(src,dst,a,b,p): return pltpu.make_async_remote_copy(src,dst,a,b,device_id=p,device_id_type=MESH)
    def local(src,dst,i): return pltpu.make_async_copy(src,dst,lsem.at[i])
    f32=lambda a:a.astype(F32)
    wcols=slice(wide+ff,wide+2*ff); ucols=slice(wide,wide+ff)
    loads=[local(dw.at[:,x,core,:,ucols],zu.at[0],0),local(r1w.at[1,:,x],zu.at[1],1),local(r2w.at[1],zu.at[2],2),
           local(dw.at[:,:,core,:,0:wide],oo,3),local(w_hbm.at[:,:,:],wv,4),local(x_hbm,xv,5),
           local(dw.at[z,x,core,:,wcols],fw.at[0],6),local(r1w.at[0,z,x],fw.at[1],7),local(r2w.at[0,z],fw.at[2],8),
           local(r3w.at[0],fw.at[3],9),local(r3w.at[1],fw.at[4],10),local(r3w.at[2],fw.at[5],11)]
    for c in loads: c.start()
    eb[0]=early[...]
    lb[0]=jnp.zeros_like(lb[0])
    pl.semaphore_wait(barrier,len(everyone))
    o_s1=remote(dw.at[:,:,1-core,:,0:wide],o1,s1s.at[0],s1r.at[0],sib); o_s1.start()
    h_s1=remote(dwh.at[:,:,1-core],h1,s1s.at[1],s1r.at[1],sib)
    o_s2=remote(o2s,o2,s2s.at[0],s2r.at[0],xp)
    h_s2=remote(h2s,h2,s2s.at[1],s2r.at[1],xp)
    def z3(g,src,dst): return [remote(src.at[(z+k)%4],dst.at[3-k],s3s.at[g,k-1],s3r.at[g,k-1],zp[k-1]) for k in (1,2,3)]
    u_s3=z3(0,su,ru); o_s3=z3(1,o3s,o3); h_s3=z3(2,h3s,h3)
    hops=[sib,xp,zb[0],zb[1],yp]
    def ecopy(i): return remote(eb.at[i],er.at[i],es.at[i],erc.at[i],hops[i])
    def eadd(i):
        ecopy(i).wait_recv()
        b=eb[i,8:16]; c=er[i,8:16]
        if i<4:
            r=lax.broadcasted_iota(jnp.int32,b.shape,0)
            b=jnp.where(r==2,jnp.maximum(b,c),b+c)
        eb[i+1,0:8]=eb[i,0:8]+er[i,0:8]; eb[i+1,8:16]=b
    def lcopy(i): return remote(lb.at[i],lr.at[i],ls.at[i],lrc.at[i],hops[i])
    def ladd(i):
        lcopy(i).wait_recv()
        lb[i+1]=lb[i]+lr[i]
    ecopy(0).start()
    for i in (0,1,2): loads[i].wait()
    @pl.loop(0,4)
    def _(i): su[i]=(f32(zu[0,i])+f32(zu[1,i])+f32(zu[2,i])).astype(BF)
    for c in u_s3: c.start()
    loads[4].wait()
    def ycopy(c): return remote(ysb.at[c],yrb.at[c],ysend.at[c],yrecv.at[c],yp)
    @pl.loop(0,NC)
    def _(c):
        pc[...]=dot(dqkv_ref[pl.ds(pl.multiple_of(2*c*cr,2*cr),2*cr)],wv[...].reshape(dm,n),NT)
        ysb[c]=pc[pl.ds(pl.multiple_of((1-t)*cr,cr),cr)].astype(BF)
        ycopy(c).start()
        part[c]=pc[pl.ds(pl.multiple_of(t*cr,cr),cr)]
    lb[0,0:1,0:width]=jnp.sum(f32(dqkv_ref[:,0:width]),axis=0,keepdims=True)
    lb[0,0:1,width:2*width]=jnp.sum(f32(dqkv_ref[:,2*width:]),axis=0,keepdims=True)
    lcopy(0).start()
    eadd(0); ecopy(1).start()
    o_s1.wait_recv(); loads[3].wait()
    @pl.loop(0,4)
    def _(i): o2s[i]=(f32(oo[i,1-x])+f32(o1[i,1-x])).astype(BF)
    o_s2.start()
    loads[5].wait()
    @pl.loop(0,rows//256)
    def _(c):
        cs=pl.ds(pl.multiple_of(c*256,256),256)
        xt[:,cs]=xv[cs].T
    eadd(1); ecopy(2).start()
    @pl.loop(0,4)
    def _(i):
        ms=pl.ds(pl.multiple_of(i*256,256),256)
        for j in range(n//512):
            dwh[i,:,:,:,j*512:(j+1)*512]=dot(xt[ms],dqkv_ref[:,j*512:(j+1)*512],NN).astype(BF).reshape(2,2,64,512)
    h_s1.start()
    ladd(0); lcopy(1).start()
    eadd(2); ecopy(3).start()
    h_s1.wait_recv()
    @pl.loop(0,4)
    def _(i): h2s[i]=(f32(dwh[i,1-x,core])+f32(h1[i,1-x])).astype(BF)
    o_s2.wait_recv()
    @pl.loop(0,4)
    def _(i): o3s[i]=(f32(oo[i,x])+f32(o1[i,x])+f32(o2[i])).astype(BF)
    o_s2.wait_send()
    h_s2.start()
    ladd(1); lcopy(2).start()
    eadd(3); ecopy(4).start()
    for i in range(6,12): loads[i].wait()
    v=f32(fw[0])+f32(fw[1])+f32(fw[2])
    v=v+f32(fw[3])+f32(fw[4])+f32(fw[5])
    gd[...]=v
    ladd(2); lcopy(3).start()
    eadd(4)
    sums[...]=eb[5]
    pk=eb[4,10:11,0:width]
    head=lax.broadcasted_iota(jnp.int32,(1,width),1)//HD
    limit=jnp.zeros((1,width),F32)
    for h in range(width//HD): limit=jnp.where(head==h,lim[h],limit)
    sc=jnp.sqrt(limit/jnp.maximum(pk,limit))
    qc[...]=(f32(wq[...])*sc).astype(BF); kc[...]=(f32(wk[...])*sc).astype(BF)
    qbc[...]=f32(bq[...]).reshape(1,width)*sc
    for c in u_s3: c.wait_send()
    for c in o_s3: c.start()
    for c in u_s3: c.wait_recv()
    v=f32(zu[0,z])+f32(zu[1,z])+f32(zu[2,z])
    gu[...]=v+f32(ru[0])+f32(ru[1])+f32(ru[2])
    for c in range(NC):
        ycopy(c).wait_recv()
        lo_=slice(c*cr,(c+1)*cr)
        tg[lo_]=(gf[lo_]+part[c]+f32(yrb[c])).astype(BF)
    ladd(3)
    late[...]=lb[4]
    h_s2.wait_recv()
    @pl.loop(0,4)
    def _(i): h3s[i]=(f32(dwh[i,x,core])+f32(h1[i,x])+f32(h2[i])).astype(BF)
    for c in o_s3: c.wait_send()
    for c in h_s3: c.start()
    for c in o_s3: c.wait_recv()
    v=f32(oo[z,x])+f32(o1[z,x])+f32(o2[z])
    v=v+f32(o3[0])+f32(o3[1])+f32(o3[2])
    osb[0]=v[:,0:width]; osb[1]=v[:,width:]
    ocopy=remote(osb.at[1-t],orb,os_,or_,yp)
    ocopy.start()
    ocopy.wait_recv()
    go[...]=osb[t]+orb[...]
    for c in h_s3: c.wait_recv()
    v=f32(dwh[z,x,core])+f32(h1[z,x])+f32(h2[z])
    v=v+f32(h3[0])+f32(h3[1])+f32(h3[2])
    gq[...]=v[:,0:width]; gk[...]=v[:,width:2*width]; gv[...]=v[:,2*width:]
    for c in [o_s1,h_s1,h_s2,ocopy]+h_s3: c.wait_send()
    for i in range(5): ecopy(i).wait_send()
    for i in range(4): lcopy(i).wait_send()
    for c in range(NC): ycopy(c).wait_send()

def tail_call(dqkv,dw,r1,r2,r3,w,xall,gf,early,wq,wk,bq,lim,cid):
    V=pl.BlockSpec(memory_space=pltpu.VMEM); A=pl.BlockSpec(memory_space=pl.ANY)
    S=jax.ShapeDtypeStruct; D=pltpu.SemaphoreType.DMA; M=pltpu.VMEM
    own,dm=gf.shape; rows,n=dqkv.shape; width=n//3; cr=own//NC
    ff=r3.shape[2]; wide=2*width
    return pl.pallas_call(tail_kernel,
      out_shape=(S((own,dm),BF),S((64,width),F32),S((64,width),F32),S((64,width),F32),S((64,width),F32),S((64,ff),F32),S((64,ff),F32),
                 S((16,1024),F32),S((8,1024),F32),S((64,width),BF),S((64,width),BF),S((1,width),F32)),
      in_specs=[V]+[A]*6+[V]*5+[pl.BlockSpec(memory_space=pltpu.SMEM)],out_specs=(V,)*12,
      scratch_shapes=[M((rows,dm),BF),M((dm,rows),BF),M((16,64,n),BF),M((NC,cr,dm),F32),M((2*cr,dm),F32),M((4,2,2,64,n),BF),M((NC,cr,dm),BF),M((NC,cr,dm),BF),
        M((6,64,ff),BF),M((3,4,64,ff),BF),M((4,64,ff),BF),M((3,64,ff),BF),
        M((4,2,64,wide),BF),M((4,2,64,wide),BF),M((4,64,wide),BF),M((4,64,wide),BF),M((4,64,wide),BF),M((3,64,wide),BF),
        M((4,2,64,n),BF),M((4,64,n),BF),M((4,64,n),BF),M((4,64,n),BF),M((3,64,n),BF),M((2,64,width),F32),M((64,width),F32),
        M((6,16,1024),F32),M((5,16,1024),F32),M((5,8,1024),F32),M((4,8,1024),F32),
        D((12,)),D((2,)),D((2,)),D((2,)),D((2,)),D((3,3)),D((3,3)),D((NC,)),D((NC,)),D((5,)),D((5,)),D((4,)),D((4,)),D,D],
      compiler_params=pltpu.CompilerParams(collective_id=cid,has_side_effects=True,vmem_limit_bytes=61*2**20),
      name="tail")(dqkv,dw,r1,r2,r3,w,xall,gf,early,wq,wk,bq,lim)

def finish_kernel(lo,tg,gq,gk,gv,go,gu,gd,qc,kc,sums,late,qbc,
                  lo_,tg_,gq_,gk_,gv_,go_,gu_,gd_,qc_,kc_,qb_,vb_,ob_,g1_,b1_,ub_,db_,g2_,b2_,pk_,qbc_,*rest):
    held=rest[:10]; sem=rest[10]
    given=(lo,tg,gq,gk,gv,go,gu,gd,qc,kc)
    ins=[pltpu.make_async_copy(a,b,sem.at[0,i]) for i,(a,b) in enumerate(zip(given,held))]
    outs=[pltpu.make_async_copy(a,b,sem.at[1,i]) for i,(a,b) in enumerate(zip(held,(lo_,tg_,gq_,gk_,gv_,go_,gu_,gd_,qc_,kc_)))]
    for c in ins: c.start()
    width=qb_.shape[0]; dm=ob_.shape[0]
    def line(v): return v.reshape(v.shape[1])
    qb_[...]=line(late[0:1,0:width]); vb_[...]=line(late[0:1,width:2*width])
    for i,o in enumerate((ob_,g1_,b1_,db_,g2_,b2_)): o[...]=line(sums[i:i+1])
    ub_[0:dm]=line(sums[8:9]); ub_[dm:2*dm]=line(sums[9:10])
    for h in range(pk_.shape[0]): pk_[h]=jnp.max(sums[10:11,h*HD:(h+1)*HD])
    qbc_[...]=line(qbc[...]).astype(BF)
    for a,b in zip(ins,outs):
        a.wait()
        b.start()
    for c in outs: c.wait()

def finish_call(lo,tg,gq,gk,gv,go,gu,gd,qc,kc,sums,late,qbc):
    V=pl.BlockSpec(memory_space=pltpu.VMEM); A=pl.BlockSpec(memory_space=pl.ANY); S=jax.ShapeDtypeStruct
    big=(lo,tg,gq,gk,gv,go,gu,gd,qc,kc)
    width=gq.shape[1]; ff=gu.shape[1]; dm=tg.shape[1]
    return pl.pallas_call(finish_kernel,
      out_shape=tuple(S(a.shape,a.dtype) for a in big)+tuple(S((k,),F32) for k in (width,width,dm,dm,dm,ff,dm,dm,dm,width//HD))+(S((width,),BF),),
      in_specs=[A]*10+[V]*3,out_specs=(A,)*10+(V,)*9+(pl.BlockSpec(memory_space=pltpu.SMEM),V),
      scratch_shapes=[pltpu.VMEM(a.shape,a.dtype) for a in big]+[pltpu.SemaphoreType.DMA((2,10))],
      compiler_params=pltpu.CompilerParams(vmem_limit_bytes=40*2**20),name="finish")(*big,sums,late,qbc)

def per_device_pair(tokens,query_weight,query_bias,key_weight,value_weight,value_bias,out_weight,out_bias,first_gain,first_shift,
    up_weight,up_bias,down_weight,down_bias,second_gain,second_shift,cotangent,clip_limit):
    shards=(query_weight,key_weight,value_weight,out_weight.T,up_weight,down_weight.T)
    vectors=(out_bias,first_gain,first_shift,down_bias,second_gain,second_shift,up_bias,query_bias,value_bias)
    lo,gf,dqkv,dw,r1,r2,r3,early,xall,wh=main_call(shards,tokens,cotangent,vectors,1)
    tg,gq,gk,gv,go,gu,gd,sums,late,qc,kc,qbc=tail_call(dqkv,dw,r1,r2,r3,wh,xall,gf,early,query_weight,key_weight,query_bias,clip_limit,2)
    lo,tg,gq,gk,gv,go,gu,gd,qc,kc,qb,vb,ob,g1,b1,ub,db,g2,b2,pk,qbc=finish_call(lo,tg,gq,gk,gv,go,gu,gd,qc,kc,sums,late,qbc)
    return (lo,tg,gq,qb,gk,gv,vb,go.T,ob,g1,b1,gu,ub,gd.T,db,g2,b2,pk,qc,qbc,kc)


def layer(*args):
    paired = lax.axis_size("dp") == 16 and lax.axis_size("tensor") == 2 and 2 * args[0].shape[0] == LEN
    return per_device_pair(*args) if paired else per_device(*args)


def solution(mesh):
    in_specs = (
        P(("dp", "tensor"), None),
        P("dp", "tensor"),
        P("tensor"),
        P("dp", "tensor"),
        P("dp", "tensor"),
        P("tensor"),
        P("tensor", "dp"),
        P(),
        P(),
        P(),
        P("dp", "tensor"),
        P("tensor"),
        P("tensor", "dp"),
        P(),
        P(),
        P(),
        P(("dp", "tensor"), None),
        P("tensor"),
    )
    out_specs = (
        P(("dp", "tensor"), None),
        P(("dp", "tensor"), None),
        P("dp", "tensor"),
        P("tensor"),
        P("dp", "tensor"),
        P("dp", "tensor"),
        P("tensor"),
        P("tensor", "dp"),
        P(),
        P(),
        P(),
        P("dp", "tensor"),
        P("tensor"),
        P("tensor", "dp"),
        P(),
        P(),
        P(),
        P("tensor"),
        P("dp", "tensor"),
        P("tensor"),
        P("dp", "tensor"),
    )
    return jax.shard_map(
        layer, mesh=mesh, in_specs=in_specs, out_specs=out_specs, check_vma=False
    )
```

```python
import functools
import math

import jax
import jax.numpy as jnp
from jax import lax
from jax.experimental import pallas as pl
from jax.experimental.pallas import tpu as pltpu
from jax.sharding import PartitionSpec as P

HD = 64
LEN = 1024
QB = 512


def layer_norm(values, gain, shift):
    center = values - jnp.mean(values, axis=-1, keepdims=True)
    spread = jnp.mean(center * center, axis=-1, keepdims=True)
    return center * lax.rsqrt(spread + EPSILON) * gain + shift


def gelu_slope(upper):
    normal_cdf = 0.5 * (1.0 + lax.erf(upper * 0.5**0.5))
    return normal_cdf + upper * jnp.exp(-0.5 * upper * upper) * (0.5 / math.pi) ** 0.5


def contract_rows(left, right):
    return lax.dot_general(
        left, right, (((0,), (0,)), ((), ())), preferred_element_type=jnp.float32
    )


def contract_cols(left, right):
    return lax.dot_general(
        left, right, (((1,), (1,)), ((), ())), preferred_element_type=jnp.float32
    )


def per_device(
    tokens,
    query_weight,
    query_bias,
    key_weight,
    value_weight,
    value_bias,
    out_weight,
    out_bias,
    first_gain,
    first_shift,
    up_weight,
    up_bias,
    down_weight,
    down_bias,
    second_gain,
    second_shift,
    cotangent,
    clip_limit,
):
    query_full, key_full, value_full, out_full, up_full, down_full = (
        lax.all_gather(query_weight, "dp", axis=0, tiled=True),
        lax.all_gather(key_weight, "dp", axis=0, tiled=True),
        lax.all_gather(value_weight, "dp", axis=0, tiled=True),
        lax.all_gather(out_weight, "dp", axis=1, tiled=True),
        lax.all_gather(up_weight, "dp", axis=0, tiled=True),
        lax.all_gather(down_weight, "dp", axis=1, tiled=True),
    )
    width = query_full.shape[1]
    hidden_width = up_full.shape[1]
    heads_here = width // HD
    score_scale = HD ** (-0.5)
    joint_weight = jnp.concatenate([query_full, key_full, value_full], axis=1)
    gathered = lax.all_gather(tokens, "tensor", axis=0, tiled=True)
    group_rows = gathered.shape[0]
    seq_count = group_rows // LEN
    block_count = LEN // QB
    projected = jnp.dot(gathered, joint_weight, preferred_element_type=jnp.float32)
    queries = (projected[:, :width] + query_bias.astype(jnp.float32)).astype(jnp.bfloat16)
    keyset = projected[:, width : 2 * width].astype(jnp.bfloat16)
    valset = (projected[:, 2 * width :] + value_bias.astype(jnp.float32)).astype(jnp.bfloat16)
    query_seq = queries.reshape(seq_count, LEN, heads_here, HD)
    key_seq = keyset.reshape(seq_count, LEN, heads_here, HD)
    value_seq = valset.reshape(seq_count, LEN, heads_here, HD)

    def attend_block(block_id):
        seq_id = block_id // block_count
        row_start = block_id % block_count * QB
        query_rows = lax.dynamic_slice_in_dim(
            lax.dynamic_index_in_dim(query_seq, seq_id, 0, False), row_start, QB, 0
        )
        key_rows = lax.dynamic_index_in_dim(key_seq, seq_id, 0, False)
        value_rows = lax.dynamic_index_in_dim(value_seq, seq_id, 0, False)
        logits = (
            jnp.einsum("qhd,khd->hqk", query_rows, key_rows, preferred_element_type=jnp.float32)
            * score_scale
        )
        row_max = jnp.max(logits, axis=2, keepdims=True)
        exponent = jnp.exp(logits - row_max)
        totals = jnp.sum(exponent, axis=2, keepdims=True)
        probs_low = (exponent / totals).astype(jnp.bfloat16)
        context_rows = jnp.einsum(
            "hqk,khd->qhd", probs_low, value_rows, preferred_element_type=jnp.float32
        )
        return (
            context_rows.reshape(QB, width).astype(jnp.bfloat16),
            (row_max + jnp.log(totals))[:, :, 0],
            jnp.max(row_max, axis=(1, 2)),
        )

    context_blocks, log_totals, block_peaks = lax.map(
        attend_block, jnp.arange(seq_count * block_count)
    )
    context = context_blocks.reshape(group_rows, width)
    logit_peak = lax.pmax(jnp.max(block_peaks, axis=0), "dp")
    attention = lax.psum_scatter(
        jnp.dot(context, out_full, preferred_element_type=jnp.float32).astype(jnp.bfloat16),
        "tensor",
        scatter_dimension=0,
        tiled=True,
    ).astype(jnp.float32) + out_bias.astype(jnp.float32)
    first_resid = tokens.astype(jnp.float32) + attention
    hidden, first_pull = jax.vjp(
        layer_norm, first_resid, first_gain.astype(jnp.float32), first_shift.astype(jnp.float32)
    )
    hidden_all = lax.all_gather(hidden.astype(jnp.bfloat16), "tensor", axis=0, tiled=True)
    upper = jnp.dot(hidden_all, up_full, preferred_element_type=jnp.float32) + up_bias.astype(
        jnp.float32
    )
    acted = jax.nn.gelu(upper, approximate=False).astype(jnp.bfloat16)
    branch = lax.psum_scatter(
        jnp.dot(acted, down_full, preferred_element_type=jnp.float32).astype(jnp.bfloat16),
        "tensor",
        scatter_dimension=0,
        tiled=True,
    ).astype(jnp.float32) + down_bias.astype(jnp.float32)
    normed, second_pull = jax.vjp(
        layer_norm,
        hidden + branch,
        second_gain.astype(jnp.float32),
        second_shift.astype(jnp.float32),
    )
    layer_out = normed.astype(jnp.bfloat16)
    grad_second, second_gain_grad, second_shift_grad = second_pull(cotangent.astype(jnp.float32))
    grad_branch = grad_second.astype(jnp.bfloat16)
    down_bias_grad = jnp.sum(grad_branch, axis=0, dtype=jnp.float32)
    branch_all = lax.all_gather(grad_branch, "tensor", axis=0, tiled=True)
    grad_acted = contract_cols(branch_all, down_full)
    down_weight_grad = contract_rows(acted, branch_all)
    grad_upper = (grad_acted * gelu_slope(upper)).astype(jnp.bfloat16)
    up_bias_grad = jnp.sum(grad_upper, axis=0, dtype=jnp.float32)
    up_weight_grad = contract_rows(hidden_all, grad_upper)
    grad_hidden = grad_second + lax.psum_scatter(
        contract_cols(grad_upper, up_full).astype(jnp.bfloat16),
        "tensor",
        scatter_dimension=0,
        tiled=True,
    ).astype(jnp.float32)
    grad_first, first_gain_grad, first_shift_grad = first_pull(grad_hidden)
    grad_attn = grad_first.astype(jnp.bfloat16)
    out_bias_grad = jnp.sum(grad_attn, axis=0, dtype=jnp.float32)
    attn_all = lax.all_gather(grad_attn, "tensor", axis=0, tiled=True)
    grad_context = contract_cols(attn_all, out_full).astype(jnp.bfloat16)
    out_weight_grad = contract_rows(context, attn_all)
    query_blocks = queries.reshape(seq_count, block_count, QB, heads_here, HD)
    grad_blocks = grad_context.reshape(seq_count, block_count, QB, heads_here, HD)
    log_blocks = log_totals.reshape(seq_count, block_count, heads_here, QB)

    def sequence_back(item):
        query_part, grad_part, log_part, key_rows, value_rows = item

        def block_back(carry, piece):
            key_acc, value_acc = carry
            query_rows, grad_rows, log_rows = piece
            logits = (
                jnp.einsum("qhd,khd->hqk", query_rows, key_rows, preferred_element_type=jnp.float32)
                * score_scale
            )
            probs = jnp.exp(logits - log_rows[:, :, None])
            probs_low = probs.astype(jnp.bfloat16)
            value_acc = value_acc + jnp.einsum(
                "hqk,qhd->khd", probs_low, grad_rows, preferred_element_type=jnp.float32
            )
            grad_probs = jnp.einsum(
                "qhd,khd->hqk", grad_rows, value_rows, preferred_element_type=jnp.float32
            )
            inner = jnp.sum(probs * grad_probs, axis=2, keepdims=True)
            grad_logits = (probs * (grad_probs - inner)).astype(jnp.bfloat16)
            grad_query = (
                jnp.einsum(
                    "hqk,khd->qhd", grad_logits, key_rows, preferred_element_type=jnp.float32
                )
                * score_scale
            )
            key_acc = (
                key_acc
                + jnp.einsum(
                    "hqk,qhd->khd", grad_logits, query_rows, preferred_element_type=jnp.float32
                )
                * score_scale
            )
            return ((key_acc, value_acc), grad_query.astype(jnp.bfloat16))

        empty = jnp.zeros((LEN, heads_here, HD), jnp.float32)
        (key_acc, value_acc), grad_query_rows = lax.scan(
            block_back, (empty, empty), (query_part, grad_part, log_part)
        )
        return (grad_query_rows, key_acc.astype(jnp.bfloat16), value_acc.astype(jnp.bfloat16))

    grad_queries_all, grad_keys_all, grad_values_all = lax.map(
        sequence_back, (query_blocks, grad_blocks, log_blocks, key_seq, value_seq)
    )
    grad_joint = jnp.concatenate(
        [
            grad_queries_all.reshape(group_rows, width),
            grad_keys_all.reshape(group_rows, width),
            grad_values_all.reshape(group_rows, width),
        ],
        axis=1,
    )
    joint_grad = contract_rows(gathered, grad_joint)
    query_weight_grad = joint_grad[:, :width]
    key_weight_grad = joint_grad[:, width : 2 * width]
    value_weight_grad = joint_grad[:, 2 * width :]
    query_bias_grad = jnp.sum(grad_joint[:, :width], axis=0, dtype=jnp.float32)
    value_bias_grad = jnp.sum(grad_joint[:, 2 * width :], axis=0, dtype=jnp.float32)
    tokens_grad = (
        grad_first
        + lax.psum_scatter(
            contract_cols(grad_joint, joint_weight).astype(jnp.bfloat16),
            "tensor",
            scatter_dimension=0,
            tiled=True,
        ).astype(jnp.float32)
    ).astype(jnp.bfloat16)
    (
        query_weight_grad,
        key_weight_grad,
        value_weight_grad,
        out_weight_grad,
        up_weight_grad,
        down_weight_grad,
    ) = (
        lax.psum_scatter(
            query_weight_grad.astype(jnp.bfloat16), "dp", scatter_dimension=0, tiled=True
        ).astype(jnp.float32),
        lax.psum_scatter(
            key_weight_grad.astype(jnp.bfloat16), "dp", scatter_dimension=0, tiled=True
        ).astype(jnp.float32),
        lax.psum_scatter(
            value_weight_grad.astype(jnp.bfloat16), "dp", scatter_dimension=0, tiled=True
        ).astype(jnp.float32),
        lax.psum_scatter(
            out_weight_grad.astype(jnp.bfloat16), "dp", scatter_dimension=1, tiled=True
        ).astype(jnp.float32),
        lax.psum_scatter(
            up_weight_grad.astype(jnp.bfloat16), "dp", scatter_dimension=0, tiled=True
        ).astype(jnp.float32),
        lax.psum_scatter(
            down_weight_grad.astype(jnp.bfloat16), "dp", scatter_dimension=1, tiled=True
        ).astype(jnp.float32),
    )
    tensor_place = lax.axis_index("tensor")
    model_width = out_bias.shape[0]
    query_spread = lax.dynamic_update_slice_in_dim(
        jnp.zeros((model_width,), jnp.float32), query_bias_grad, tensor_place * width, 0
    )
    value_spread = lax.dynamic_update_slice_in_dim(
        jnp.zeros((model_width,), jnp.float32), value_bias_grad, tensor_place * width, 0
    )
    up_spread = lax.dynamic_update_slice_in_dim(
        jnp.zeros((hidden_width * lax.axis_size("tensor"),), jnp.float32),
        up_bias_grad,
        tensor_place * hidden_width,
        0,
    )
    (
        query_spread,
        value_spread,
        up_spread,
        out_bias_grad,
        down_bias_grad,
        first_gain_grad,
        first_shift_grad,
        second_gain_grad,
        second_shift_grad,
    ) = lax.psum(
        (
            query_spread,
            value_spread,
            up_spread,
            out_bias_grad,
            down_bias_grad,
            first_gain_grad,
            first_shift_grad,
            second_gain_grad,
            second_shift_grad,
        ),
        ("dp", "tensor"),
    )
    query_bias_grad = lax.dynamic_slice_in_dim(query_spread, tensor_place * width, width, 0)
    value_bias_grad = lax.dynamic_slice_in_dim(value_spread, tensor_place * width, width, 0)
    up_bias_grad = lax.dynamic_slice_in_dim(up_spread, tensor_place * hidden_width, hidden_width, 0)
    factor = clip_limit / jnp.maximum(logit_peak, clip_limit)
    column_scale = jnp.repeat(jnp.sqrt(factor), HD)
    query_clipped = (query_weight.astype(jnp.float32) * column_scale).astype(jnp.bfloat16)
    query_bias_clipped = (query_bias.astype(jnp.float32) * column_scale).astype(jnp.bfloat16)
    key_clipped = (key_weight.astype(jnp.float32) * column_scale).astype(jnp.bfloat16)
    return (
        layer_out,
        tokens_grad,
        query_weight_grad,
        query_bias_grad,
        key_weight_grad,
        value_weight_grad,
        value_bias_grad,
        out_weight_grad,
        out_bias_grad,
        first_gain_grad,
        first_shift_grad,
        up_weight_grad,
        up_bias_grad,
        down_weight_grad,
        down_bias_grad,
        second_gain_grad,
        second_shift_grad,
        logit_peak,
        query_clipped,
        query_bias_clipped,
        key_clipped,
    )


LOG2E=1.4426950408889634
NT=(((1,),(1,)),((),()))
NN=(((1,),(0,)),((),()))
F32=jnp.float32
BF=jnp.bfloat16
MESH=pl.DeviceIdType.MESH
EPSILON=1e-5
NC=4


def dot(a,b,dims):
    return lax.dot_general(a,b,dims,preferred_element_type=jnp.float32)


def greet(partner):
    barrier=pltpu.get_barrier_semaphore()
    pl.semaphore_signal(barrier,inc=1,device_id=partner,device_id_type=MESH)
    pl.semaphore_wait(barrier,1)


def main_kernel(wq,wk,wv,wos,wu,wds,tok,cot_hbm,v_ob,v_g1,v_b1,v_db,v_g2,v_b2,v_ub,v_qb,v_vb,
               lo_hbm,gf,dqkv_hbm,dw,r1,r2,r3,early,x_hbm,wh_hbm,
               bias,vec,upb,sh,qkv,vt,kt,ctx,ctxo,lse,cl,wo,wup,wdn,xh,rst,hall,act,slp,ball,ga,dcs,dcall,part,pch,ctt,dqt,dl,dkv,sbuf,rbuf,tb,th,stage,
               lsem,losem,dsem,osem,ssem,rsem,rl,g1s,g1r,g2s,g2r,g3s,g3r,ts,tr,azs,azr,axs,axr,acs,acr):
    d=lax.axis_index("dp"); t=lax.axis_index("tensor")
    partner=(d,1-t)
    core=d%2; x_=(d//2)%2; z=d//4
    def dev(z_,xx,c_): return ((z_*2+xx)*2+c_,t)
    sib=dev(z,x_,1-core); xp=dev(z,1-x_,core); zp=[dev((z+k)%4,x_,core) for k in (1,2,3)]
    own,dm=tok.shape; cr=own//NC; cg=2*cr; rows_all=2*own; width=ctx.shape[1]; ff=wup.shape[2]; wide=wo.shape[2]; pairs=width//128
    def local(src,dst,i): return pltpu.make_async_copy(src,dst,lsem.at[i])
    def remote(src,dst,a,b,p): return pltpu.make_async_remote_copy(src,dst,a,b,device_id=p,device_id_type=MESH)
    cot_load=local(cot_hbm,cl,0)
    cot_load.start()
    barrier=pltpu.get_barrier_semaphore()
    n=3*width
    def row(v): return v[...].astype(F32).reshape(1,v.shape[0])
    sh[:,0:width]=wq[...]; sh[:,width:2*width]=wk[...]; sh[:,2*width:n]=wv[...]
    everyone=[partner,sib,xp]+zp
    for p in everyone: pl.semaphore_signal(barrier,inc=1,device_id=p,device_id_type=MESH)
    def chunk(c): return pl.ds(pl.multiple_of(c*cg,cg),cg)
    def rows(rank,c): return pl.ds(pl.multiple_of(c*cg+rank*cr,cr),cr)
    def half(rank): return pl.ds(pl.multiple_of(rank*cr,cr),cr)
    def loc(c): return pl.ds(pl.multiple_of(c*cr,cr),cr)
    def rs_copy(k,c):
        return pltpu.make_async_remote_copy(sbuf.at[k-1,loc(c)],rbuf.at[k-1,loc(c)],ssem.at[k,c],rsem.at[k,c],device_id=partner,device_id_type=MESH)
    def ag_copy(k,buf,c,rank):
        return pltpu.make_async_remote_copy(buf.at[rows(rank,c)],buf.at[rows(rank,c)],ssem.at[k,c],rsem.at[k,c],device_id=partner,device_id_type=MESH)
    def cols(rank): return pl.ds(pl.multiple_of(rank*width,128),width)
    def ctx_copy(c,rank):
        return pltpu.make_async_remote_copy(ctx.at[rows(1-rank,c)],ctxo.at[loc(c),cols(rank)],ssem.at[0,c],rsem.at[0,c],device_id=partner,device_id_type=MESH)
    def dctx_copy(c,rank):
        return pltpu.make_async_remote_copy(dcs.at[loc(c),cols(1-rank)],dcall.at[rows(rank,c)],ssem.at[5,c],rsem.at[5,c],device_id=partner,device_id_type=MESH)
    early[...]=jnp.zeros_like(early)
    early[10:11]=jnp.full_like(early[10:11],-jnp.inf)
    def whole(w): return w[...].reshape(dm,w.shape[2])
    def strip(w,cs): return w[:,:,cs].reshape(dm,TF)
    dkv[...]=jnp.zeros_like(dkv)
    lane=lax.broadcasted_iota(jnp.int32,(1,128),1)
    scale=jnp.bfloat16(HD**-0.5); zero=jnp.bfloat16(0)
    q4=ff//2
    groups=[(act,0,0,width),(act,width,width,width),(act,2*width,2*width,width),(wo,0,n,wide),
            (wup,0,n+wide,q4),(wup,q4,n+wide+q4,q4),(wdn,0,n+wide+ff,q4),(wdn,q4,n+wide+ff+q4,q4)]
    def block(z_,xx): return (z_*2+xx)*2+core
    me=block(z,x_)
    def place(g,b):
        buf,c0,_,nc=groups[g]
        return buf.at[b,:,c0:c0+nc]
    def shard(g): return sh.at[:,groups[g][2]:groups[g][2]+groups[g][3]]
    up=dev(jnp.minimum(z+1,3),x_,core); down=dev(jnp.maximum(z-1,0),x_,core)
    def z_hop(g,way,j,b): return remote(shard(g) if j==1 else place(g,b),place(g,b),azs.at[g,way,j-1],azr.at[g,way,j-1],up if way==0 else down)
    def x_hop(g,zz,own_): return remote(shard(g) if own_ else place(g,block(zz,x_)),place(g,block(zz,x_)),axs.at[g,zz],axr.at[g,zz],xp)
    def x_land(g,zz): return remote(place(g,block(zz,1-x_)),place(g,block(zz,1-x_)),axs.at[g,zz],axr.at[g,zz],xp)
    def c_hop(g,xx,zz,b,own_): return remote(shard(g) if own_ else place(g,b),place(g,b),acs.at[g,4*xx+zz],acr.at[g,4*xx+zz],sib)
    def gather_start(g):
        buf,c0,s0,nc=groups[g]
        @pl.when(z<3)
        def _(): z_hop(g,0,1,me).start()
        @pl.when(z>0)
        def _(): z_hop(g,1,1,me).start()
        x_hop(g,z,True).start()
        c_hop(g,0,z,me,True).start()
        buf[me,:,c0:c0+nc]=sh[:,s0:s0+nc]
    def gather_z(g,j):
        for way in (0,1):
            here=(z>=j) if way==0 else (z+j<=3)
            zz=jnp.maximum(z-j,0) if way==0 else jnp.minimum(z+j,3)
            @pl.when(here)
            def _():
                b=block(zz,x_)
                z_hop(g,way,j,b).wait_recv()
                x_hop(g,zz,False).start()
                c_hop(g,0,zz,b,False).start()
            if j<3:
                @pl.when(here & ((z<3) if way==0 else (z>0)))
                def _(): z_hop(g,way,j+1,block(zz,x_)).start()
    def gather_x(g):
        for zz in range(4):
            x_land(g,zz).wait_recv()
            c_hop(g,1,zz,block(zz,1-x_),False).start()
    def gather_done(g):
        for xx in (0,1):
            for zz in range(4):
                b=block(zz,x_)
                c_hop(g,xx,zz,b,False).wait_recv()
                c_hop(g,xx,zz,b,False).wait_send()
        for zz in range(4): x_land(g,zz).wait_send()
        for j in (1,2,3):
            @pl.when((z>=j-1) & (z<3))
            def _(): z_hop(g,0,j,me).wait_send()
            @pl.when((z+j-1<=3) & (z>0))
            def _(): z_hop(g,1,j,me).wait_send()
    own_copies=[local(tok.at[c*cr:(c+1)*cr],hall.at[rows(t,c)],1+c) for c in range(NC)]
    for c in own_copies: c.start()
    pl.semaphore_wait(barrier,len(everyone))
    gather_start(0); gather_start(1)
    def tok_copy(c): return remote(tok.at[loc(c)],hall.at[rows(t,c)],ts.at[c],tr.at[c],partner)
    def mine_o(rank): return sh.at[:,pl.ds(pl.multiple_of(n+rank*width,128),width)]
    o_swap=remote(mine_o(t),mine_o(t),ts.at[NC],tr.at[NC],partner)
    sh[:,pl.ds(pl.multiple_of(n+t*width,128),width)]=wos[...]
    o_swap.start()
    @pl.loop(0,NC)
    def _(c): tok_copy(c).start()
    sh[:,n+wide:n+wide+ff]=wu[...]
    sh[:,n+wide+ff:]=wds[...]
    for i,v in enumerate((v_ob,v_g1,v_b1,v_db,v_g2,v_b2)): vec[i:i+1]=row(v)
    upb[...]=row(v_ub)
    bias[...]=jnp.zeros_like(bias)
    bias[:,0:width]=row(v_qb); bias[:,2*width:]=row(v_vb)
    gather_z(0,1); gather_start(2)
    gather_z(1,1); gather_z(0,2)
    gather_z(2,1); o_swap.wait_recv(); gather_start(3)
    gather_z(1,2); gather_z(0,3); gather_z(2,2); gather_z(1,3)
    gather_x(0); gather_z(3,1); gather_z(2,3)
    gather_x(1); gather_z(3,2)
    gather_start(4)
    gather_x(2); gather_z(3,3); gather_z(4,1)
    for g in range(3): gather_done(g)
    for c in own_copies: c.wait()
    TF=512
    @pl.loop(0,NC)
    def _(c):
        tok_copy(c).wait_recv()
        @pl.loop(0,n//TF)
        def _(j):
            cs=pl.ds(pl.multiple_of(j*TF,TF),TF)
            qkv[chunk(c),cs]=(dot(hall[chunk(c)],strip(act,cs),NN)+bias[:,cs]).astype(BF)
        @pl.when(c==0)
        def _(): gather_z(4,2)
        @pl.when(c==1)
        def _():
            gather_x(3); gather_z(4,3)
        @pl.when(c==2)
        def _(): gather_start(5)
        @pl.when(c==3)
        def _():
            gather_z(5,1); gather_done(3)
    x_out=local(hall,x_hbm,5); w_out=local(act.at[:,:,0:n],wh_hbm,6)
    x_out.start(); w_out.start()
    ones=jnp.where(lax.broadcasted_iota(jnp.int32,(16,rows_all),0)==0,1.0,0.0).astype(BF)
    @pl.loop(0,pairs)
    def _(p):
        ck=pl.multiple_of(width+p*128,128); cv=pl.multiple_of(2*width+p*128,128)
        kt[p]=qkv[:,pl.ds(ck,128)].T
        v=qkv[:,pl.ds(cv,128)].T
        vt[2*p,0:64]=v[0:64]; vt[2*p,64:80]=ones
        vt[2*p+1,0:64]=v[64:128]; vt[2*p+1,64:80]=ones
    x_out.wait()
    def split(k,c):
        sbuf[k-1,loc(c)]=pch[half(1-t)].astype(BF)
        rs_copy(k,c).start()
        part[loc(c)]=pch[half(t)]
    def stats(v):
        cen=v-jnp.mean(v,axis=1,keepdims=True)
        r=lax.rsqrt(jnp.mean(cen*cen,axis=1,keepdims=True)+EPSILON)
        return cen*r,r
    def lo_copy(c): return pltpu.make_async_copy(cl.at[loc(c)],lo_hbm.at[loc(c)],losem.at[c])
    def out_copy(slot,col):
        return pltpu.make_async_copy(stage.at[slot],dw.at[:,:,:,:,pl.ds(pl.multiple_of(col,512),512)],osem.at[slot])
    def wgrad(slot,left,right_ref,rcol,ocol):
        @pl.loop(0,dm//256)
        def _(i):
            ms=pl.ds(pl.multiple_of(i*256,256),256)
            right=right_ref[:,pl.ds(pl.multiple_of(rcol,512),512)] if len(right_ref.shape)==2 else strip(right_ref,pl.ds(pl.multiple_of(rcol,512),512))
            stage[slot,i]=dot(left[ms],right,NN).astype(BF).reshape(2,2,64,512)
        out_copy(slot,ocol).start()
    def stage_a(c):
        rs=chunk(c)
        @pl.loop(0,pairs)
        def _(p):
            cq=pl.ds(pl.multiple_of(p*128,128),128); ck=pl.ds(pl.multiple_of(width+p*128,128),128)
            pks=[]
            for h in (0,1):
                keep=(lane<64) if h==0 else (lane>=64)
                q=jnp.where(keep,qkv[rs,cq]*scale,zero)
                st=dot(qkv[:,ck],q,NT)
                m=jnp.max(st,axis=0,keepdims=True)
                mc=m*LOG2E
                pt=jnp.exp2(st*LOG2E-mc).astype(BF)
                ot=dot(vt[2*p+h],pt,NN)
                tot=ot[64:65]
                ctt[h*64:(h+1)*64,:]=ot[0:64]*(1.0/tot)
                lse[pl.ds(2*p+h,1),rs]=mc+jnp.log2(tot)
                pks.append(jnp.max(m,axis=1,keepdims=True))
            early[10:11,cq]=jnp.maximum(early[10:11,cq],jnp.where(lane<64,pks[0],pks[1]))
            ctx[rs,cq]=ctt[...].T.astype(BF)
            step=c*pairs+p
            @pl.when(step==0)
            def _():
                gather_z(5,2)
            @pl.when(step==2)
            def _():
                gather_z(5,3)
                gather_start(6)
            @pl.when(step==4)
            def _():
                gather_z(6,1)
                gather_x(4)
            @pl.when(step==6)
            def _():
                gather_z(6,2)
                gather_start(7)
            @pl.when(step==8)
            def _():
                gather_z(6,3)
                gather_z(7,1)
            @pl.when(step==10)
            def _():
                gather_z(7,2)
                gather_x(5)
            @pl.when(step==12)
            def _():
                gather_z(7,3)
            @pl.when(step==14)
            def _():
                gather_x(6)
        ctx_copy(c,t).start()
        ctxo[loc(c),cols(t)]=ctx[rows(t,c)]
    def stage_b(c):
        ctx_copy(c,1-t).wait_recv()
        x,r=stats(hall[rows(t,c)].astype(F32)+dot(ctxo[loc(c)],whole(wo),NT)+vec[0:1])
        xh[loc(c)]=x
        rst[loc(c)]=jnp.broadcast_to(r,(cr,128))
        hall[rows(t,c)]=(x*vec[1:2]+vec[2:3]).astype(BF)
        ag_copy(3,hall,c,t).start()
    def stage_c(c):
        rs=chunk(c)
        ag_copy(3,hall,c,1-t).wait_recv()
        @pl.loop(0,ff//TF)
        def _(j):
            cs=pl.ds(pl.multiple_of(j*TF,TF),TF)
            u=dot(hall[rs],strip(wup,cs),NN)+upb[:,cs]
            cdf=0.5*(1.0+lax.erf(u*0.5**0.5))
            act[pl.ds(4*c,4),:,cs]=(u*cdf).astype(BF).reshape(4,64,TF)
            slp[rs,cs]=(cdf+u*jnp.exp(-0.5*u*u)*(0.5/math.pi)**0.5).astype(BF)
        @pl.when(c==0)
        def _():
            gather_x(7)
            gather_done(6); gather_done(7)
        pch[...]=dot(act[pl.ds(4*c,4)].reshape(cg,ff),whole(wdn),NT)
        split(1,c)
    def stage_d(c):
        rs_copy(1,c).wait_recv()
        x,r=stats(xh[loc(c)]*vec[1:2]+vec[2:3]+part[loc(c)]+rbuf[0,loc(c)].astype(F32)+vec[3:4])
        dy=cl[loc(c)].astype(F32)
        cl[loc(c)]=(x*vec[4:5]+vec[5:6]).astype(BF)
        lo_copy(c).start()
        early[4:5]+=jnp.sum(dy*x,axis=0,keepdims=True)
        early[5:6]+=jnp.sum(dy,axis=0,keepdims=True)
        dx=dy*vec[4:5]
        g=r*(dx-jnp.mean(dx,axis=1,keepdims=True)-x*jnp.mean(dx*x,axis=1,keepdims=True))
        gf[loc(c)]=g
        gb=g.astype(BF)
        early[3:4]+=jnp.sum(gb.astype(F32),axis=0,keepdims=True)
        ball[rows(t,c)]=gb
        ag_copy(4,ball,c,t).start()
        tb[:,rows(t,c)]=gb.T
    def stage_e(c):
        rs=chunk(c)
        ag_copy(4,ball,c,1-t).wait_recv()
        @pl.loop(0,ff//TF)
        def _(j):
            cs=pl.ds(pl.multiple_of(j*TF,TF),TF)
            gu=(dot(ball[rs],strip(wdn,cs),NN)*slp[rs,cs].astype(F32)).astype(BF)
            slp[rs,cs]=gu
            row=pl.ds(8+j*TF//dm,1); cc=pl.ds(pl.multiple_of(j*TF%dm,TF),TF)
            early[row,cc]+=jnp.sum(gu.astype(F32),axis=0,keepdims=True)
        pch[...]=dot(slp[rs],whole(wup),NT)
        split(2,c)
        tb[:,rows(1-t,c)]=ball[rows(1-t,c)].T
        th[:,chunk(c)]=hall[chunk(c)].T
    def stage_f(c):
        rs_copy(2,c).wait_recv()
        dy=gf[loc(c)]+part[loc(c)]+rbuf[1,loc(c)].astype(F32)
        x=xh[loc(c)]; r=rst[loc(c)][:,0:1]
        early[1:2]+=jnp.sum(dy*x,axis=0,keepdims=True)
        early[2:3]+=jnp.sum(dy,axis=0,keepdims=True)
        dx=dy*vec[1:2]
        g=r*(dx-jnp.mean(dx,axis=1,keepdims=True)-x*jnp.mean(dx*x,axis=1,keepdims=True))
        gf[loc(c)]=g
        gb=g.astype(BF)
        early[0:1]+=jnp.sum(gb.astype(F32),axis=0,keepdims=True)
        ga[loc(c)]=gb
        dcs[loc(c)]=dot(gb,whole(wo),NN).astype(BF)
        dctx_copy(c,t).start()
        dcall[rows(t,c)]=dcs[loc(c),cols(t)]
    def stage_g(c):
        rs=chunk(c)
        dctx_copy(c,1-t).wait_recv()
        @pl.loop(0,pairs)
        def _(p):
            cq=pl.ds(pl.multiple_of(p*128,128),128); ck=pl.ds(pl.multiple_of(width+p*128,128),128); cv=pl.ds(pl.multiple_of(2*width+p*128,128),128)
            prod=(ctx[rs,cq].astype(F32)*dcall[rs,cq].astype(F32)).T
            dl[0:1]=jnp.sum(prod[0:64],axis=0,keepdims=True)
            dl[1:2]=jnp.sum(prod[64:128],axis=0,keepdims=True)
            for h in (0,1):
                keep=(lane<64) if h==0 else (lane>=64)
                q=jnp.where(keep,qkv[rs,cq]*scale,zero)
                do=jnp.where(keep,dcall[rs,cq],zero)
                st=dot(qkv[:,ck],q,NT)
                pt=jnp.exp2(st*LOG2E-lse[pl.ds(2*p+h,1),rs])
                dpt=dot(qkv[:,cv],do,NT)
                ds=(pt*(dpt-dl[h:h+1])).astype(BF)
                dkv[1,:,cq]+=dot(pt.astype(BF),do,NN)
                dkv[0,:,cq]+=dot(ds,q,NN)
                dqt[h*64:(h+1)*64,:]=dot(kt[p,h*64:(h+1)*64,:],ds,NN)
            qkv[rs,cq]=(dqt[...].T*(HD**-0.5)).astype(BF)
            step=c*pairs+p
            @pl.when(step==0)
            def _():
                s2(0).wait_send(); s2(1).start()
                fetch3(0)
            @pl.when(step==1)
            def _():
                add3(0)
                fetch2(2)
            @pl.when(step==2)
            def _():
                add2(2)
                fetch2(3)
            @pl.when(step==3)
            def _():
                add2(3)
            @pl.when(step==6)
            def _():
                s2(1).wait_send(); s2(2).start()
                fetch3(1)
            @pl.when(step==8)
            def _():
                sent3(0); add3(1)
            @pl.when(step==12)
            def _():
                s2(2).wait_send(); s2(3).start()
                fetch3(2)
            @pl.when(step==14)
            def _():
                sent3(1); add3(2)
    def grad_down(c):
        slot=c%2
        wgrad(slot,tb,act,c*512,wide+ff+c*512)
    def grad_up(c):
        slot=c%2
        wgrad(slot,th,slp,c*512,wide+c*512)
    def grad_out():
        @pl.loop(0,NC)
        def _(c): tb[:,loc(c)]=ga[loc(c)].T
        for j in range(wide//512):
            @pl.loop(0,dm//256)
            def _(i):
                ms=pl.ds(pl.multiple_of(i*256,256),256)
                stage[j%2,i]=dot(tb[ms,0:own],ctxo[:,j*512:(j+1)*512],NN).astype(BF).reshape(2,2,64,512)
            out_copy(j%2,j*512).start()
    @pl.loop(0,NC)
    def _(c):
        stage_a(c)
        @pl.when(c>0)
        def _(): stage_b(c-1)
    cot_load.wait(); w_out.wait()
    gather_done(4); gather_done(5)
    @pl.loop(0,NC)
    def _(c):
        stage_c(c)
        @pl.when(c==0)
        def _(): stage_b(NC-1)
        @pl.when(c>=2)
        def _(): stage_d(c-2)
    @pl.loop(NC-2,NC)
    def _(c): stage_d(c)
    @pl.loop(0,NC)
    def _(c): stage_e(c)
    piece=ff//2
    base=(wide+ff,wide+ff+piece,wide,wide+piece)
    def s1(g): return remote(dw.at[:,:,1-core,:,base[g]:base[g]+piece],r1.at[g],g1s.at[g],g1r.at[g],sib)
    sum2=[wup.at[8+4*(g%2):12+4*(g%2),:,g//2*piece:(g//2+1)*piece] for g in range(4)]
    sum3=[wdn.at[12:16,:,0:piece],wdn.at[12:16,:,piece:],wdn.at[0:4,:,piece:]]
    def s2(g): return remote(sum2[g],r2.at[g],g2s.at[g],g2r.at[g],xp)
    def s3(g,k): return remote(sum3[g].at[(z+k)%4],r3.at[g,3-k],g3s.at[g,k-1],g3r.at[g,k-1],zp[k-1])
    def load2(g): return [pltpu.make_async_copy(dw.at[:,1-x_,core,:,base[g]:base[g]+piece],wup.at[0:4,:,0:piece],rl.at[0]),
                          pltpu.make_async_copy(r1.at[g,:,1-x_],wup.at[4:8,:,0:piece],rl.at[1])]
    def load3(g): return [pltpu.make_async_copy(dw.at[:,x_,core,:,base[g]:base[g]+piece],wdn.at[0:4,:,0:piece],rl.at[2]),
                         pltpu.make_async_copy(r1.at[g,:,x_],wdn.at[4:8,:,0:piece],rl.at[3]),
                         pltpu.make_async_copy(r2.at[g],wdn.at[8:12,:,0:piece],rl.at[4])]
    def fetch2(g):
        s1(g).wait_recv()
        for l in load2(g): l.start()
    def add2(g):
        for l in load2(g): l.wait()
        @pl.loop(0,4)
        def _(i): sum2[g][i]=(wup[i,:,0:piece].astype(F32)+wup[4+i,:,0:piece].astype(F32)).astype(BF)
    def fetch3(g):
        s2(g).wait_recv()
        for l in load3(g): l.start()
    def add3(g):
        for l in load3(g): l.wait()
        @pl.loop(0,4)
        def _(i): sum3[g][i]=(wdn[i,:,0:piece].astype(F32)+wdn[4+i,:,0:piece].astype(F32)+wdn[8+i,:,0:piece].astype(F32)).astype(BF)
        for k in (1,2,3): s3(g,k).start()
    def sent3(g):
        for k in (1,2,3): s3(g,k).wait_send()
    def drain():
        out_copy(0,0).wait()
        out_copy(1,0).wait()
    grad_down(0); grad_down(1)
    drain(); s1(0).start()
    grad_down(2); grad_down(3)
    drain(); s1(1).start()
    @pl.loop(0,NC)
    def _(c):
        stage_f(c)
        grad_up(c)
        @pl.when(c==0)
        def _(): fetch2(0)
        @pl.when(c==1)
        def _():
            add2(0); s2(0).start()
            fetch2(1)
            drain(); s1(2).start()
        @pl.when(c==2)
        def _(): add2(1)
        @pl.when(c==3)
        def _():
            drain(); s1(3).start()
    grad_out()
    @pl.loop(0,NC)
    def _(c): stage_g(c)
    @pl.loop(0,pairs)
    def _(p):
        cq=pl.ds(pl.multiple_of(p*128,128),128); ck=pl.ds(pl.multiple_of(width+p*128,128),128); cv=pl.ds(pl.multiple_of(2*width+p*128,128),128)
        qkv[:,ck]=dkv[0,:,cq].astype(BF)
        qkv[:,cv]=dkv[1,:,cq].astype(BF)
    dq_out=pltpu.make_async_copy(qkv,dqkv_hbm,dsem.at[0])
    dq_out.start()
    out_copy(0,0).wait()
    out_copy(1,0).wait()
    dq_out.wait()
    o_swap.wait_send()
    for g in range(4): s1(g).wait_send()
    s2(3).wait()
    sent3(2)
    for g in range(3):
        for k in (1,2,3): s3(g,k).wait_recv()
    @pl.loop(0,NC)
    def _(c):
        lo_copy(c).wait()
        ctx_copy(c,t).wait_send(); dctx_copy(c,t).wait_send(); tok_copy(c).wait_send()
        for k in (1,2): rs_copy(k,c).wait_send()
        for k,buf in ((3,hall),(4,ball)): ag_copy(k,buf,c,t).wait_send()

def main_call(shards,tok,cot,vectors,cid):
    V=pl.BlockSpec(memory_space=pltpu.VMEM); A=pl.BlockSpec(memory_space=pl.ANY)
    width=shards[0].shape[1]; ff=shards[4].shape[1]; own,dm=tok.shape; rows=2*own; n=3*width; cr=own//NC; wide=2*width
    S=jax.ShapeDtypeStruct; M=pltpu.VMEM; D=pltpu.SemaphoreType.DMA
    return pl.pallas_call(main_kernel,
      out_shape=(S((own,dm),BF),S((own,dm),F32),S((rows,n),BF),S((4,2,2,64,wide+2*ff),BF),S((4,4,2,64,ff//2),BF),S((4,4,64,ff//2),BF),S((3,3,64,ff//2),BF),S((16,dm),F32),S((rows,dm),BF),S((16,64,n),BF)),
      in_specs=[V]*6+[A,A]+[V]*9,out_specs=(A,V,A,A,A,A,A,V,A,A),
      scratch_shapes=[M((1,n),F32),M((8,dm),F32),M((1,ff),F32),M((64,n+wide+2*ff),BF),M((rows,n),BF),M((width//HD,80,rows),BF),M((width//128,128,rows),BF),M((rows,width),BF),M((own,wide),BF),M((width//HD,rows),F32),M((own,dm),BF),
        M((16,64,wide),BF),M((16,64,ff),BF),M((16,64,ff),BF),
        M((own,dm),F32),M((own,128),F32),
        M((rows,dm),BF),M((16,64,ff),BF),M((rows,ff),BF),M((rows,dm),BF),M((own,dm),BF),M((own,wide),BF),M((rows,width),BF),
        M((own,dm),F32),M((2*cr,dm),F32),M((128,2*cr),F32),M((128,2*cr),F32),M((8,2*cr),F32),M((2,rows,width),F32),
        M((2,own,dm),BF),M((2,own,dm),BF),
        M((dm,rows),BF),M((dm,rows),BF),M((2,4,2,2,64,512),BF),
        D((7,)),D((NC,)),D((1,)),D((2,)),D((6,NC)),D((6,NC)),D((5,)),D((4,)),D((4,)),D((4,)),D((4,)),D((3,3)),D((3,3)),
        D((NC+1,)),D((NC+1,)),D((8,2,3)),D((8,2,3)),D((8,4)),D((8,4)),D((8,8)),D((8,8))],
      compiler_params=pltpu.CompilerParams(collective_id=cid,has_side_effects=True,vmem_limit_bytes=61*2**20),
      name="main")(*shards,tok,cot,*vectors)

def tail_kernel(dqkv_ref,dw,r1w,r2w,r3w,w_hbm,x_hbm,gf,early,wq,wk,bq,lim,
                tg,gq,gk,gv,go,gu,gd,sums,late,qc,kc,qbc,
                xv,xt,wv,part,pc,dwh,ysb,yrb,fw,zu,su,ru,oo,o1,o2s,o2,o3s,o3,h1,h2s,h2,h3s,h3,osb,orb,eb,er,lb,lr,
                lsem,s1s,s1r,s2s,s2r,s3s,s3r,ysend,yrecv,es,erc,ls,lrc,os_,or_):
    d=lax.axis_index("dp"); t=lax.axis_index("tensor")
    core=d%2; x=(d//2)%2; z=d//4
    def dev(z_,x_,c_): return ((z_*2+x_)*2+c_,t)
    sib=dev(z,x,1-core); xp=dev(z,1-x,core); yp=(d,1-t)
    zp=[dev((z+k)%4,x,core) for k in (1,2,3)]
    zb=[dev(z+1-2*(z%2),x,core),dev((z+2)%4,x,core)]
    barrier=pltpu.get_barrier_semaphore()
    everyone=[sib,xp,yp]+zp
    for p in everyone: pl.semaphore_signal(barrier,inc=1,device_id=p,device_id_type=MESH)
    own,dm=gf.shape; rows,n=dqkv_ref.shape; width=n//3; cr=own//NC; piece=ru.shape[2]; wide=2*width
    def remote(src,dst,a,b,p): return pltpu.make_async_remote_copy(src,dst,a,b,device_id=p,device_id_type=MESH)
    def local(src,dst,i): return pltpu.make_async_copy(src,dst,lsem.at[i])
    f32=lambda a:a.astype(F32)
    first=(wide+2*piece,wide+3*piece,wide,wide+piece)
    def part_of(g): return slice(first[g],first[g]+piece)
    loads=[local(dw.at[:,x,core,:,part_of(3)],zu.at[0],0),local(r1w.at[3,:,x],zu.at[1],1),local(r2w.at[3],zu.at[2],2),
           local(dw.at[:,:,core,:,0:wide],oo,3),local(w_hbm,wv,4),local(x_hbm,xv,5)]
    finals=[[local(dw.at[z,x,core,:,part_of(g)],fw.at[g,0],6+4*g),local(r1w.at[g,z,x],fw.at[g,1],7+4*g),local(r2w.at[g,z],fw.at[g,2],8+4*g),
             local(r3w.at[g],fw.at[g,3:6],9+4*g)] for g in range(3)]
    for c in loads: c.start()
    for f in finals:
        for c in f: c.start()
    eb[0]=early[...]
    lb[0]=jnp.zeros_like(lb[0])
    pl.semaphore_wait(barrier,len(everyone))
    o_s1=remote(dw.at[:,:,1-core,:,0:wide],o1,s1s.at[3],s1r.at[3],sib); o_s1.start()
    def cols(p): return slice(p*width,(p+1)*width)
    h_s1=[remote(dwh.at[:,:,1-core,:,cols(p)],h1.at[:,:,:,cols(p)],s1s.at[p],s1r.at[p],sib) for p in range(3)]
    o_s2=remote(o2s,o2,s2s.at[3],s2r.at[3],xp)
    h_s2=[remote(h2s.at[p],h2.at[p],s2s.at[p],s2r.at[p],xp) for p in range(3)]
    def z3(g,src,dst): return [remote(src.at[(z+k)%4],dst.at[3-k],s3s.at[g,k-1],s3r.at[g,k-1],zp[k-1]) for k in (1,2,3)]
    u_s3=z3(0,su,ru); o_s3=z3(1,o3s,o3); h_s3=[z3(2+p,h3s.at[p],h3.at[p]) for p in range(3)]
    def begin(cs):
        for c in cs: c.start()
    def sent(cs):
        for c in cs: c.wait_send()
    def landed(cs):
        for c in cs: c.wait_recv()
    hops=[sib,xp,zb[0],zb[1],yp]
    def ecopy(i): return remote(eb.at[i],er.at[i],es.at[i],erc.at[i],hops[i])
    def eadd(i):
        ecopy(i).wait_recv()
        b=eb[i,8:16]; c=er[i,8:16]
        if i<4:
            r=lax.broadcasted_iota(jnp.int32,b.shape,0)
            b=jnp.where(r==2,jnp.maximum(b,c),b+c)
        eb[i+1,0:8]=eb[i,0:8]+er[i,0:8]; eb[i+1,8:16]=b
    def lcopy(i): return remote(lb.at[i],lr.at[i],ls.at[i],lrc.at[i],hops[i])
    def ladd(i):
        lcopy(i).wait_recv()
        lb[i+1]=lb[i]+lr[i]
    def pair_sum(p):
        h_s1[p].wait_recv()
        @pl.loop(0,4)
        def _(i): h2s[p,i]=(f32(dwh[i,1-x,core,:,cols(p)])+f32(h1[i,1-x,:,cols(p)])).astype(BF)
    def quad_sum(p):
        h_s2[p].wait_recv()
        @pl.loop(0,4)
        def _(i): h3s[p,i]=(f32(dwh[i,x,core,:,cols(p)])+f32(h1[i,x,:,cols(p)])+f32(h2[p,i])).astype(BF)
    def head_sum(p,out):
        landed(h_s3[p])
        v=f32(dwh[z,x,core,:,cols(p)])+f32(h1[z,x,:,cols(p)])+f32(h2[p,z])
        out[...]=v+f32(h3[p,0])+f32(h3[p,1])+f32(h3[p,2])
    ecopy(0).start()
    for i in (0,1,2): loads[i].wait()
    @pl.loop(0,4)
    def _(i): su[i]=(f32(zu[0,i])+f32(zu[1,i])+f32(zu[2,i])).astype(BF)
    begin(u_s3)
    o_s1.wait_recv(); loads[3].wait()
    @pl.loop(0,4)
    def _(i): o2s[i]=(f32(oo[i,1-x])+f32(o1[i,1-x])).astype(BF)
    o_s2.start()
    eadd(0); ecopy(1).start()
    loads[5].wait()
    @pl.loop(0,rows//256)
    def _(c):
        cs=pl.ds(pl.multiple_of(c*256,256),256)
        xt[:,cs]=xv[cs].T
    def head_grad(j):
        @pl.loop(0,4)
        def _(i):
            ms=pl.ds(pl.multiple_of(i*256,256),256)
            dwh[i,:,:,:,cols(j)]=dot(xt[ms],dqkv_ref[:,cols(j)],NN).astype(BF).reshape(2,2,64,width)
        h_s1[j].start()
    head_grad(0)
    loads[4].wait()
    def ycopy(c): return remote(ysb.at[c],yrb.at[c],ysend.at[c],yrecv.at[c],yp)
    @pl.loop(0,NC)
    def _(c):
        pc[...]=dot(dqkv_ref[pl.ds(pl.multiple_of(2*c*cr,2*cr),2*cr)],wv[...].reshape(dm,n),NT)
        ysb[c]=pc[pl.ds(pl.multiple_of((1-t)*cr,cr),cr)].astype(BF)
        ycopy(c).start()
        part[c]=pc[pl.ds(pl.multiple_of(t*cr,cr),cr)]
    pair_sum(0)
    eadd(1); ecopy(2).start()
    lb[0,0:1,0:width]=jnp.sum(f32(dqkv_ref[:,0:width]),axis=0,keepdims=True)
    lb[0,0:1,width:2*width]=jnp.sum(f32(dqkv_ref[:,2*width:]),axis=0,keepdims=True)
    lcopy(0).start()
    head_grad(1)
    head_grad(2)
    eadd(2); ecopy(3).start()
    ladd(0); lcopy(1).start()
    sent([o_s2]); h_s2[0].start()
    landed([o_s2])
    @pl.loop(0,4)
    def _(i): o3s[i]=(f32(oo[i,x])+f32(o1[i,x])+f32(o2[i])).astype(BF)
    sent(u_s3); begin(o_s3)
    pair_sum(1); pair_sum(2)
    eadd(3); ecopy(4).start()
    ladd(1); lcopy(2).start()
    sent([h_s2[0]]); h_s2[1].start()
    quad_sum(0)
    for g,out,c0 in ((0,gd,0),(1,gd,piece),(2,gu,0)):
        for c in finals[g]: c.wait()
        v=f32(fw[g,0])+f32(fw[g,1])+f32(fw[g,2])
        out[:,c0:c0+piece]=v+f32(fw[g,3])+f32(fw[g,4])+f32(fw[g,5])
    sent([h_s2[1]]); h_s2[2].start()
    sent(o_s3); begin(h_s3[0])
    eadd(4)
    ladd(2); lcopy(3).start()
    sums[...]=eb[5]
    pk=eb[4,10:11,0:width]
    head=lax.broadcasted_iota(jnp.int32,(1,width),1)//HD
    limit=jnp.zeros((1,width),F32)
    for h in range(width//HD): limit=jnp.where(head==h,lim[h],limit)
    sc=jnp.sqrt(limit/jnp.maximum(pk,limit))
    qc[...]=(f32(wq[...])*sc).astype(BF); kc[...]=(f32(wk[...])*sc).astype(BF)
    qbc[...]=f32(bq[...]).reshape(1,width)*sc
    landed(u_s3)
    v=f32(zu[0,z])+f32(zu[1,z])+f32(zu[2,z])
    gu[:,piece:]=v+f32(ru[0])+f32(ru[1])+f32(ru[2])
    quad_sum(1)
    sent(h_s3[0]); begin(h_s3[1])
    landed(o_s3)
    v=f32(oo[z,x])+f32(o1[z,x])+f32(o2[z])
    v=v+f32(o3[0])+f32(o3[1])+f32(o3[2])
    osb[0]=v[:,0:width]; osb[1]=v[:,width:]
    ocopy=remote(osb.at[1-t],orb,os_,or_,yp)
    ocopy.start()
    quad_sum(2)
    sent(h_s3[1]); begin(h_s3[2])
    ladd(3)
    late[...]=lb[4]
    for c in range(NC):
        ycopy(c).wait_recv()
        lo_=slice(c*cr,(c+1)*cr)
        tg[lo_]=(gf[lo_]+part[c]+f32(yrb[c])).astype(BF)
    ocopy.wait_recv()
    go[...]=osb[t]+orb[...]
    head_sum(0,gq); head_sum(1,gk); head_sum(2,gv)
    sent([o_s1,h_s2[2],ocopy]+h_s1+h_s3[2])
    for i in range(5): ecopy(i).wait_send()
    for i in range(4): lcopy(i).wait_send()
    for c in range(NC): ycopy(c).wait_send()

def tail_call(dqkv,dw,r1,r2,r3,w,xall,gf,early,wq,wk,bq,lim,cid):
    V=pl.BlockSpec(memory_space=pltpu.VMEM); A=pl.BlockSpec(memory_space=pl.ANY)
    S=jax.ShapeDtypeStruct; D=pltpu.SemaphoreType.DMA; M=pltpu.VMEM
    own,dm=gf.shape; rows,n=dqkv.shape; width=n//3; cr=own//NC
    piece=r3.shape[3]; ff=2*piece; wide=2*width
    return pl.pallas_call(tail_kernel,
      out_shape=(S((own,dm),BF),S((64,width),F32),S((64,width),F32),S((64,width),F32),S((64,width),F32),S((64,ff),F32),S((64,ff),F32),
                 S((16,1024),F32),S((8,1024),F32),S((64,width),BF),S((64,width),BF),S((1,width),F32)),
      in_specs=[V]+[A]*6+[V]*5+[pl.BlockSpec(memory_space=pltpu.SMEM)],out_specs=(V,)*12,
      scratch_shapes=[M((rows,dm),BF),M((dm,rows),BF),M((16,64,n),BF),M((NC,cr,dm),F32),M((2*cr,dm),F32),M((4,2,2,64,n),BF),M((NC,cr,dm),BF),M((NC,cr,dm),BF),
        M((3,6,64,piece),BF),M((3,4,64,piece),BF),M((4,64,piece),BF),M((3,64,piece),BF),
        M((4,2,64,wide),BF),M((4,2,64,wide),BF),M((4,64,wide),BF),M((4,64,wide),BF),M((4,64,wide),BF),M((3,64,wide),BF),
        M((4,2,64,n),BF),M((3,4,64,width),BF),M((3,4,64,width),BF),M((3,4,64,width),BF),M((3,3,64,width),BF),M((2,64,width),F32),M((64,width),F32),
        M((6,16,1024),F32),M((5,16,1024),F32),M((5,8,1024),F32),M((4,8,1024),F32),
        D((18,)),D((4,)),D((4,)),D((4,)),D((4,)),D((5,3)),D((5,3)),D((NC,)),D((NC,)),D((5,)),D((5,)),D((4,)),D((4,)),D,D],
      compiler_params=pltpu.CompilerParams(collective_id=cid,has_side_effects=True,vmem_limit_bytes=61*2**20),
      name="tail")(dqkv,dw,r1,r2,r3,w,xall,gf,early,wq,wk,bq,lim)

def finish_kernel(lo,tg,gq,gk,gv,go,gu,gd,qc,kc,sums,late,qbc,
                  lo_,tg_,gq_,gk_,gv_,go_,gu_,gd_,qc_,kc_,qb_,vb_,ob_,g1_,b1_,ub_,db_,g2_,b2_,pk_,qbc_,*rest):
    held=rest[:10]; sem=rest[10]
    given=(lo,tg,gq,gk,gv,go,gu,gd,qc,kc)
    ins=[pltpu.make_async_copy(a,b,sem.at[0,i]) for i,(a,b) in enumerate(zip(given,held))]
    outs=[pltpu.make_async_copy(a,b,sem.at[1,i]) for i,(a,b) in enumerate(zip(held,(lo_,tg_,gq_,gk_,gv_,go_,gu_,gd_,qc_,kc_)))]
    for c in ins: c.start()
    width=qb_.shape[0]; dm=ob_.shape[0]
    def line(v): return v.reshape(v.shape[1])
    qb_[...]=line(late[0:1,0:width]); vb_[...]=line(late[0:1,width:2*width])
    for i,o in enumerate((ob_,g1_,b1_,db_,g2_,b2_)): o[...]=line(sums[i:i+1])
    ub_[0:dm]=line(sums[8:9]); ub_[dm:2*dm]=line(sums[9:10])
    for h in range(pk_.shape[0]): pk_[h]=jnp.max(sums[10:11,h*HD:(h+1)*HD])
    qbc_[...]=line(qbc[...]).astype(BF)
    for a,b in zip(ins,outs):
        a.wait()
        b.start()
    for c in outs: c.wait()

def finish_call(lo,tg,gq,gk,gv,go,gu,gd,qc,kc,sums,late,qbc):
    V=pl.BlockSpec(memory_space=pltpu.VMEM); A=pl.BlockSpec(memory_space=pl.ANY); S=jax.ShapeDtypeStruct
    big=(lo,tg,gq,gk,gv,go,gu,gd,qc,kc)
    width=gq.shape[1]; ff=gu.shape[1]; dm=tg.shape[1]
    return pl.pallas_call(finish_kernel,
      out_shape=tuple(S(a.shape,a.dtype) for a in big)+tuple(S((k,),F32) for k in (width,width,dm,dm,dm,ff,dm,dm,dm,width//HD))+(S((width,),BF),),
      in_specs=[A]*10+[V]*3,out_specs=(A,)*10+(V,)*9+(pl.BlockSpec(memory_space=pltpu.SMEM),V),
      scratch_shapes=[pltpu.VMEM(a.shape,a.dtype) for a in big]+[pltpu.SemaphoreType.DMA((2,10))],
      compiler_params=pltpu.CompilerParams(vmem_limit_bytes=61*2**20),name="finish")(*big,sums,late,qbc)

def per_device_pair(tokens,query_weight,query_bias,key_weight,value_weight,value_bias,out_weight,out_bias,first_gain,first_shift,
    up_weight,up_bias,down_weight,down_bias,second_gain,second_shift,cotangent,clip_limit):
    shards=(query_weight,key_weight,value_weight,out_weight.T,up_weight,down_weight.T)
    vectors=(out_bias,first_gain,first_shift,down_bias,second_gain,second_shift,up_bias,query_bias,value_bias)
    lo,gf,dqkv,dw,r1,r2,r3,early,xall,wh=main_call(shards,tokens,cotangent,vectors,1)
    tg,gq,gk,gv,go,gu,gd,sums,late,qc,kc,qbc=tail_call(dqkv,dw,r1,r2,r3,wh,xall,gf,early,query_weight,key_weight,query_bias,clip_limit,2)
    lo,tg,gq,gk,gv,go,gu,gd,qc,kc,qb,vb,ob,g1,b1,ub,db,g2,b2,pk,qbc=finish_call(lo,tg,gq,gk,gv,go,gu,gd,qc,kc,sums,late,qbc)
    return (lo,tg,gq,qb,gk,gv,vb,go.T,ob,g1,b1,gu,ub,gd.T,db,g2,b2,pk,qc,qbc,kc)


def layer(*args):
    paired = lax.axis_size("dp") == 16 and lax.axis_size("tensor") == 2 and 2 * args[0].shape[0] == LEN
    return per_device_pair(*args) if paired else per_device(*args)


def solution(mesh):
    in_specs = (
        P(("dp", "tensor"), None),
        P("dp", "tensor"),
        P("tensor"),
        P("dp", "tensor"),
        P("dp", "tensor"),
        P("tensor"),
        P("tensor", "dp"),
        P(),
        P(),
        P(),
        P("dp", "tensor"),
        P("tensor"),
        P("tensor", "dp"),
        P(),
        P(),
        P(),
        P(("dp", "tensor"), None),
        P("tensor"),
    )
    out_specs = (
        P(("dp", "tensor"), None),
        P(("dp", "tensor"), None),
        P("dp", "tensor"),
        P("tensor"),
        P("dp", "tensor"),
        P("dp", "tensor"),
        P("tensor"),
        P("tensor", "dp"),
        P(),
        P(),
        P(),
        P("dp", "tensor"),
        P("tensor"),
        P("tensor", "dp"),
        P(),
        P(),
        P(),
        P("tensor"),
        P("dp", "tensor"),
        P("tensor"),
        P("dp", "tensor"),
    )
    return jax.shard_map(
        layer, mesh=mesh, in_specs=in_specs, out_specs=out_specs, check_vma=False
    )
```

```python
import functools
import math

import jax
import jax.numpy as jnp
from jax import lax
from jax.experimental import pallas as pl
from jax.experimental.pallas import tpu as pltpu
from jax.sharding import PartitionSpec as P

HD = 64
LEN = 1024
QB = 512


def layer_norm(values, gain, shift):
    center = values - jnp.mean(values, axis=-1, keepdims=True)
    spread = jnp.mean(center * center, axis=-1, keepdims=True)
    return center * lax.rsqrt(spread + EPSILON) * gain + shift


def gelu_slope(upper):
    normal_cdf = 0.5 * (1.0 + lax.erf(upper * 0.5**0.5))
    return normal_cdf + upper * jnp.exp(-0.5 * upper * upper) * (0.5 / math.pi) ** 0.5


def contract_rows(left, right):
    return lax.dot_general(
        left, right, (((0,), (0,)), ((), ())), preferred_element_type=jnp.float32
    )


def contract_cols(left, right):
    return lax.dot_general(
        left, right, (((1,), (1,)), ((), ())), preferred_element_type=jnp.float32
    )


def per_device(
    tokens,
    query_weight,
    query_bias,
    key_weight,
    value_weight,
    value_bias,
    out_weight,
    out_bias,
    first_gain,
    first_shift,
    up_weight,
    up_bias,
    down_weight,
    down_bias,
    second_gain,
    second_shift,
    cotangent,
    clip_limit,
):
    query_full, key_full, value_full, out_full, up_full, down_full = (
        lax.all_gather(query_weight, "dp", axis=0, tiled=True),
        lax.all_gather(key_weight, "dp", axis=0, tiled=True),
        lax.all_gather(value_weight, "dp", axis=0, tiled=True),
        lax.all_gather(out_weight, "dp", axis=1, tiled=True),
        lax.all_gather(up_weight, "dp", axis=0, tiled=True),
        lax.all_gather(down_weight, "dp", axis=1, tiled=True),
    )
    width = query_full.shape[1]
    hidden_width = up_full.shape[1]
    heads_here = width // HD
    score_scale = HD ** (-0.5)
    joint_weight = jnp.concatenate([query_full, key_full, value_full], axis=1)
    gathered = lax.all_gather(tokens, "tensor", axis=0, tiled=True)
    group_rows = gathered.shape[0]
    seq_count = group_rows // LEN
    block_count = LEN // QB
    projected = jnp.dot(gathered, joint_weight, preferred_element_type=jnp.float32)
    queries = (projected[:, :width] + query_bias.astype(jnp.float32)).astype(jnp.bfloat16)
    keyset = projected[:, width : 2 * width].astype(jnp.bfloat16)
    valset = (projected[:, 2 * width :] + value_bias.astype(jnp.float32)).astype(jnp.bfloat16)
    query_seq = queries.reshape(seq_count, LEN, heads_here, HD)
    key_seq = keyset.reshape(seq_count, LEN, heads_here, HD)
    value_seq = valset.reshape(seq_count, LEN, heads_here, HD)

    def attend_block(block_id):
        seq_id = block_id // block_count
        row_start = block_id % block_count * QB
        query_rows = lax.dynamic_slice_in_dim(
            lax.dynamic_index_in_dim(query_seq, seq_id, 0, False), row_start, QB, 0
        )
        key_rows = lax.dynamic_index_in_dim(key_seq, seq_id, 0, False)
        value_rows = lax.dynamic_index_in_dim(value_seq, seq_id, 0, False)
        logits = (
            jnp.einsum("qhd,khd->hqk", query_rows, key_rows, preferred_element_type=jnp.float32)
            * score_scale
        )
        row_max = jnp.max(logits, axis=2, keepdims=True)
        exponent = jnp.exp(logits - row_max)
        totals = jnp.sum(exponent, axis=2, keepdims=True)
        probs_low = (exponent / totals).astype(jnp.bfloat16)
        context_rows = jnp.einsum(
            "hqk,khd->qhd", probs_low, value_rows, preferred_element_type=jnp.float32
        )
        return (
            context_rows.reshape(QB, width).astype(jnp.bfloat16),
            (row_max + jnp.log(totals))[:, :, 0],
            jnp.max(row_max, axis=(1, 2)),
        )

    context_blocks, log_totals, block_peaks = lax.map(
        attend_block, jnp.arange(seq_count * block_count)
    )
    context = context_blocks.reshape(group_rows, width)
    logit_peak = lax.pmax(jnp.max(block_peaks, axis=0), "dp")
    attention = lax.psum_scatter(
        jnp.dot(context, out_full, preferred_element_type=jnp.float32).astype(jnp.bfloat16),
        "tensor",
        scatter_dimension=0,
        tiled=True,
    ).astype(jnp.float32) + out_bias.astype(jnp.float32)
    first_resid = tokens.astype(jnp.float32) + attention
    hidden, first_pull = jax.vjp(
        layer_norm, first_resid, first_gain.astype(jnp.float32), first_shift.astype(jnp.float32)
    )
    hidden_all = lax.all_gather(hidden.astype(jnp.bfloat16), "tensor", axis=0, tiled=True)
    upper = jnp.dot(hidden_all, up_full, preferred_element_type=jnp.float32) + up_bias.astype(
        jnp.float32
    )
    acted = jax.nn.gelu(upper, approximate=False).astype(jnp.bfloat16)
    branch = lax.psum_scatter(
        jnp.dot(acted, down_full, preferred_element_type=jnp.float32).astype(jnp.bfloat16),
        "tensor",
        scatter_dimension=0,
        tiled=True,
    ).astype(jnp.float32) + down_bias.astype(jnp.float32)
    normed, second_pull = jax.vjp(
        layer_norm,
        hidden + branch,
        second_gain.astype(jnp.float32),
        second_shift.astype(jnp.float32),
    )
    layer_out = normed.astype(jnp.bfloat16)
    grad_second, second_gain_grad, second_shift_grad = second_pull(cotangent.astype(jnp.float32))
    grad_branch = grad_second.astype(jnp.bfloat16)
    down_bias_grad = jnp.sum(grad_branch, axis=0, dtype=jnp.float32)
    branch_all = lax.all_gather(grad_branch, "tensor", axis=0, tiled=True)
    grad_acted = contract_cols(branch_all, down_full)
    down_weight_grad = contract_rows(acted, branch_all)
    grad_upper = (grad_acted * gelu_slope(upper)).astype(jnp.bfloat16)
    up_bias_grad = jnp.sum(grad_upper, axis=0, dtype=jnp.float32)
    up_weight_grad = contract_rows(hidden_all, grad_upper)
    grad_hidden = grad_second + lax.psum_scatter(
        contract_cols(grad_upper, up_full).astype(jnp.bfloat16),
        "tensor",
        scatter_dimension=0,
        tiled=True,
    ).astype(jnp.float32)
    grad_first, first_gain_grad, first_shift_grad = first_pull(grad_hidden)
    grad_attn = grad_first.astype(jnp.bfloat16)
    out_bias_grad = jnp.sum(grad_attn, axis=0, dtype=jnp.float32)
    attn_all = lax.all_gather(grad_attn, "tensor", axis=0, tiled=True)
    grad_context = contract_cols(attn_all, out_full).astype(jnp.bfloat16)
    out_weight_grad = contract_rows(context, attn_all)
    query_blocks = queries.reshape(seq_count, block_count, QB, heads_here, HD)
    grad_blocks = grad_context.reshape(seq_count, block_count, QB, heads_here, HD)
    log_blocks = log_totals.reshape(seq_count, block_count, heads_here, QB)

    def sequence_back(item):
        query_part, grad_part, log_part, key_rows, value_rows = item

        def block_back(carry, piece):
            key_acc, value_acc = carry
            query_rows, grad_rows, log_rows = piece
            logits = (
                jnp.einsum("qhd,khd->hqk", query_rows, key_rows, preferred_element_type=jnp.float32)
                * score_scale
            )
            probs = jnp.exp(logits - log_rows[:, :, None])
            probs_low = probs.astype(jnp.bfloat16)
            value_acc = value_acc + jnp.einsum(
                "hqk,qhd->khd", probs_low, grad_rows, preferred_element_type=jnp.float32
            )
            grad_probs = jnp.einsum(
                "qhd,khd->hqk", grad_rows, value_rows, preferred_element_type=jnp.float32
            )
            inner = jnp.sum(probs * grad_probs, axis=2, keepdims=True)
            grad_logits = (probs * (grad_probs - inner)).astype(jnp.bfloat16)
            grad_query = (
                jnp.einsum(
                    "hqk,khd->qhd", grad_logits, key_rows, preferred_element_type=jnp.float32
                )
                * score_scale
            )
            key_acc = (
                key_acc
                + jnp.einsum(
                    "hqk,qhd->khd", grad_logits, query_rows, preferred_element_type=jnp.float32
                )
                * score_scale
            )
            return ((key_acc, value_acc), grad_query.astype(jnp.bfloat16))

        empty = jnp.zeros((LEN, heads_here, HD), jnp.float32)
        (key_acc, value_acc), grad_query_rows = lax.scan(
            block_back, (empty, empty), (query_part, grad_part, log_part)
        )
        return (grad_query_rows, key_acc.astype(jnp.bfloat16), value_acc.astype(jnp.bfloat16))

    grad_queries_all, grad_keys_all, grad_values_all = lax.map(
        sequence_back, (query_blocks, grad_blocks, log_blocks, key_seq, value_seq)
    )
    grad_joint = jnp.concatenate(
        [
            grad_queries_all.reshape(group_rows, width),
            grad_keys_all.reshape(group_rows, width),
            grad_values_all.reshape(group_rows, width),
        ],
        axis=1,
    )
    joint_grad = contract_rows(gathered, grad_joint)
    query_weight_grad = joint_grad[:, :width]
    key_weight_grad = joint_grad[:, width : 2 * width]
    value_weight_grad = joint_grad[:, 2 * width :]
    query_bias_grad = jnp.sum(grad_joint[:, :width], axis=0, dtype=jnp.float32)
    value_bias_grad = jnp.sum(grad_joint[:, 2 * width :], axis=0, dtype=jnp.float32)
    tokens_grad = (
        grad_first
        + lax.psum_scatter(
            contract_cols(grad_joint, joint_weight).astype(jnp.bfloat16),
            "tensor",
            scatter_dimension=0,
            tiled=True,
        ).astype(jnp.float32)
    ).astype(jnp.bfloat16)
    (
        query_weight_grad,
        key_weight_grad,
        value_weight_grad,
        out_weight_grad,
        up_weight_grad,
        down_weight_grad,
    ) = (
        lax.psum_scatter(
            query_weight_grad.astype(jnp.bfloat16), "dp", scatter_dimension=0, tiled=True
        ).astype(jnp.float32),
        lax.psum_scatter(
            key_weight_grad.astype(jnp.bfloat16), "dp", scatter_dimension=0, tiled=True
        ).astype(jnp.float32),
        lax.psum_scatter(
            value_weight_grad.astype(jnp.bfloat16), "dp", scatter_dimension=0, tiled=True
        ).astype(jnp.float32),
        lax.psum_scatter(
            out_weight_grad.astype(jnp.bfloat16), "dp", scatter_dimension=1, tiled=True
        ).astype(jnp.float32),
        lax.psum_scatter(
            up_weight_grad.astype(jnp.bfloat16), "dp", scatter_dimension=0, tiled=True
        ).astype(jnp.float32),
        lax.psum_scatter(
            down_weight_grad.astype(jnp.bfloat16), "dp", scatter_dimension=1, tiled=True
        ).astype(jnp.float32),
    )
    tensor_place = lax.axis_index("tensor")
    model_width = out_bias.shape[0]
    query_spread = lax.dynamic_update_slice_in_dim(
        jnp.zeros((model_width,), jnp.float32), query_bias_grad, tensor_place * width, 0
    )
    value_spread = lax.dynamic_update_slice_in_dim(
        jnp.zeros((model_width,), jnp.float32), value_bias_grad, tensor_place * width, 0
    )
    up_spread = lax.dynamic_update_slice_in_dim(
        jnp.zeros((hidden_width * lax.axis_size("tensor"),), jnp.float32),
        up_bias_grad,
        tensor_place * hidden_width,
        0,
    )
    (
        query_spread,
        value_spread,
        up_spread,
        out_bias_grad,
        down_bias_grad,
        first_gain_grad,
        first_shift_grad,
        second_gain_grad,
        second_shift_grad,
    ) = lax.psum(
        (
            query_spread,
            value_spread,
            up_spread,
            out_bias_grad,
            down_bias_grad,
            first_gain_grad,
            first_shift_grad,
            second_gain_grad,
            second_shift_grad,
        ),
        ("dp", "tensor"),
    )
    query_bias_grad = lax.dynamic_slice_in_dim(query_spread, tensor_place * width, width, 0)
    value_bias_grad = lax.dynamic_slice_in_dim(value_spread, tensor_place * width, width, 0)
    up_bias_grad = lax.dynamic_slice_in_dim(up_spread, tensor_place * hidden_width, hidden_width, 0)
    factor = clip_limit / jnp.maximum(logit_peak, clip_limit)
    column_scale = jnp.repeat(jnp.sqrt(factor), HD)
    query_clipped = (query_weight.astype(jnp.float32) * column_scale).astype(jnp.bfloat16)
    query_bias_clipped = (query_bias.astype(jnp.float32) * column_scale).astype(jnp.bfloat16)
    key_clipped = (key_weight.astype(jnp.float32) * column_scale).astype(jnp.bfloat16)
    return (
        layer_out,
        tokens_grad,
        query_weight_grad,
        query_bias_grad,
        key_weight_grad,
        value_weight_grad,
        value_bias_grad,
        out_weight_grad,
        out_bias_grad,
        first_gain_grad,
        first_shift_grad,
        up_weight_grad,
        up_bias_grad,
        down_weight_grad,
        down_bias_grad,
        second_gain_grad,
        second_shift_grad,
        logit_peak,
        query_clipped,
        query_bias_clipped,
        key_clipped,
    )


LOG2E=1.4426950408889634
NT=(((1,),(1,)),((),()))
NN=(((1,),(0,)),((),()))
F32=jnp.float32
BF=jnp.bfloat16
MESH=pl.DeviceIdType.MESH
EPSILON=1e-5
NC=4


def dot(a,b,dims):
    return lax.dot_general(a,b,dims,preferred_element_type=jnp.float32)


def greet(partner):
    barrier=pltpu.get_barrier_semaphore()
    pl.semaphore_signal(barrier,inc=1,device_id=partner,device_id_type=MESH)
    pl.semaphore_wait(barrier,1)


def main_kernel(wq,wk,wv,wos,wu,wds,tok,cot_hbm,v_ob,v_g1,v_b1,v_db,v_g2,v_b2,v_ub,v_qb,v_vb,lim,
               lo_hbm,tg_hbm,fin,fin_head,go_hbm,qc_hbm,kc_hbm,smalls,dw,r1,r2,r3,x_hbm,wh_hbm,
               bias,vec,upb,gf,eb,er,lb,lr,osb,orb,sh,qkv,vt,kt,ctx,ctxo,lse,cl,wo,wup,wdn,xh,rst,hall,act,slp,ball,ga,dcs,dcall,part,pch,ctt,dqt,dl,dkv,sbuf,rbuf,tb,th,stage,
               lsem,losem,dsem,osem,ssem,rsem,rl,g1s,g1r,g2s,g2r,g3s,g3r,ts,tr,azs,azr,axs,axr,acs,acr,es,erc,ls,lrc,os_,or_,fl,fs):
    d=lax.axis_index("dp"); t=lax.axis_index("tensor")
    partner=(d,1-t)
    core=d%2; x_=(d//2)%2; z=d//4
    def dev(z_,xx,c_): return ((z_*2+xx)*2+c_,t)
    sib=dev(z,x_,1-core); xp=dev(z,1-x_,core); zp=[dev((z+k)%4,x_,core) for k in (1,2,3)]
    own,dm=tok.shape; cr=own//NC; cg=2*cr; rows_all=2*own; width=ctx.shape[1]; ff=wup.shape[2]; wide=wo.shape[2]; pairs=width//128
    def local(src,dst,i): return pltpu.make_async_copy(src,dst,lsem.at[i])
    def remote(src,dst,a,b,p): return pltpu.make_async_remote_copy(src,dst,a,b,device_id=p,device_id_type=MESH)
    cot_load=local(cot_hbm,cl,0)
    cot_load.start()
    barrier=pltpu.get_barrier_semaphore()
    n=3*width
    def row(v): return v[...].astype(F32).reshape(1,v.shape[0])
    sh[:,0:width]=wq[...]; sh[:,width:2*width]=wk[...]; sh[:,2*width:n]=wv[...]
    everyone=[partner,sib,xp]+zp
    for p in everyone: pl.semaphore_signal(barrier,inc=1,device_id=p,device_id_type=MESH)
    def chunk(c): return pl.ds(pl.multiple_of(c*cg,cg),cg)
    def rows(rank,c): return pl.ds(pl.multiple_of(c*cg+rank*cr,cr),cr)
    def half(rank): return pl.ds(pl.multiple_of(rank*cr,cr),cr)
    def loc(c): return pl.ds(pl.multiple_of(c*cr,cr),cr)
    def rs_copy(k,c):
        return pltpu.make_async_remote_copy(sbuf.at[k-1,loc(c)],rbuf.at[k-1,loc(c)],ssem.at[k,c],rsem.at[k,c],device_id=partner,device_id_type=MESH)
    def ag_copy(k,buf,c,rank):
        return pltpu.make_async_remote_copy(buf.at[rows(rank,c)],buf.at[rows(rank,c)],ssem.at[k,c],rsem.at[k,c],device_id=partner,device_id_type=MESH)
    def cols(rank): return pl.ds(pl.multiple_of(rank*width,128),width)
    def ctx_copy(c,rank):
        return pltpu.make_async_remote_copy(ctx.at[rows(1-rank,c)],ctxo.at[loc(c),cols(rank)],ssem.at[0,c],rsem.at[0,c],device_id=partner,device_id_type=MESH)
    def dctx_copy(c,rank):
        return pltpu.make_async_remote_copy(dcs.at[loc(c),cols(1-rank)],dcall.at[rows(rank,c)],ssem.at[5,c],rsem.at[5,c],device_id=partner,device_id_type=MESH)
    early=eb.at[0]
    early[...]=jnp.zeros((16,dm),F32)
    early[10:11]=jnp.full((1,dm),-jnp.inf,F32)
    lb[0]=jnp.zeros((8,dm),F32)
    def whole(w): return w[...].reshape(dm,w.shape[2])
    def strip(w,cs): return w[:,:,cs].reshape(dm,TF)
    dkv[...]=jnp.zeros_like(dkv)
    lane=lax.broadcasted_iota(jnp.int32,(1,128),1)
    scale=jnp.bfloat16(HD**-0.5); zero=jnp.bfloat16(0)
    q4=ff//2
    groups=[(act,0,0,width),(act,width,width,width),(act,2*width,2*width,width),(wo,0,n,wide),
            (wup,0,n+wide,q4),(wup,q4,n+wide+q4,q4),(wdn,0,n+wide+ff,q4),(wdn,q4,n+wide+ff+q4,q4)]
    def block(z_,xx): return (z_*2+xx)*2+core
    me=block(z,x_)
    def place(g,b):
        buf,c0,_,nc=groups[g]
        return buf.at[b,:,c0:c0+nc]
    def shard(g): return sh.at[:,groups[g][2]:groups[g][2]+groups[g][3]]
    up=dev(jnp.minimum(z+1,3),x_,core); down=dev(jnp.maximum(z-1,0),x_,core)
    def z_hop(g,way,j,b): return remote(shard(g) if j==1 else place(g,b),place(g,b),azs.at[g,way,j-1],azr.at[g,way,j-1],up if way==0 else down)
    def x_hop(g,zz,own_): return remote(shard(g) if own_ else place(g,block(zz,x_)),place(g,block(zz,x_)),axs.at[g,zz],axr.at[g,zz],xp)
    def x_land(g,zz): return remote(place(g,block(zz,1-x_)),place(g,block(zz,1-x_)),axs.at[g,zz],axr.at[g,zz],xp)
    def c_hop(g,xx,zz,b,own_): return remote(shard(g) if own_ else place(g,b),place(g,b),acs.at[g,4*xx+zz],acr.at[g,4*xx+zz],sib)
    def gather_start(g):
        buf,c0,s0,nc=groups[g]
        @pl.when(z<3)
        def _(): z_hop(g,0,1,me).start()
        @pl.when(z>0)
        def _(): z_hop(g,1,1,me).start()
        x_hop(g,z,True).start()
        c_hop(g,0,z,me,True).start()
        buf[me,:,c0:c0+nc]=sh[:,s0:s0+nc]
    def gather_z(g,j):
        for way in (0,1):
            here=(z>=j) if way==0 else (z+j<=3)
            zz=jnp.maximum(z-j,0) if way==0 else jnp.minimum(z+j,3)
            @pl.when(here)
            def _():
                b=block(zz,x_)
                z_hop(g,way,j,b).wait_recv()
                x_hop(g,zz,False).start()
                c_hop(g,0,zz,b,False).start()
            if j<3:
                @pl.when(here & ((z<3) if way==0 else (z>0)))
                def _(): z_hop(g,way,j+1,block(zz,x_)).start()
    def gather_x(g):
        for zz in range(4):
            x_land(g,zz).wait_recv()
            c_hop(g,1,zz,block(zz,1-x_),False).start()
    def gather_done(g):
        for xx in (0,1):
            for zz in range(4):
                b=block(zz,x_)
                c_hop(g,xx,zz,b,False).wait_recv()
                c_hop(g,xx,zz,b,False).wait_send()
        for zz in range(4): x_land(g,zz).wait_send()
        for j in (1,2,3):
            @pl.when((z>=j-1) & (z<3))
            def _(): z_hop(g,0,j,me).wait_send()
            @pl.when((z+j-1<=3) & (z>0))
            def _(): z_hop(g,1,j,me).wait_send()
    own_copies=[local(tok.at[c*cr:(c+1)*cr],hall.at[rows(t,c)],1+c) for c in range(NC)]
    for c in own_copies: c.start()
    pl.semaphore_wait(barrier,len(everyone))
    gather_start(0); gather_start(1)
    def tok_copy(c): return remote(tok.at[loc(c)],hall.at[rows(t,c)],ts.at[c],tr.at[c],partner)
    def mine_o(rank): return sh.at[:,pl.ds(pl.multiple_of(n+rank*width,128),width)]
    o_swap=remote(mine_o(t),mine_o(t),ts.at[NC],tr.at[NC],partner)
    sh[:,pl.ds(pl.multiple_of(n+t*width,128),width)]=wos[...]
    o_swap.start()
    @pl.loop(0,NC)
    def _(c): tok_copy(c).start()
    sh[:,n+wide:n+wide+ff]=wu[...]
    sh[:,n+wide+ff:]=wds[...]
    for i,v in enumerate((v_ob,v_g1,v_b1,v_db,v_g2,v_b2)): vec[i:i+1]=row(v)
    upb[...]=row(v_ub)
    bias[...]=jnp.zeros_like(bias)
    bias[:,0:width]=row(v_qb); bias[:,2*width:]=row(v_vb)
    gather_z(0,1); gather_start(2)
    gather_z(1,1); gather_z(0,2)
    gather_z(2,1); o_swap.wait_recv(); gather_start(3)
    gather_z(1,2); gather_z(0,3); gather_z(2,2); gather_z(1,3)
    gather_x(0); gather_z(3,1); gather_z(2,3)
    gather_x(1); gather_z(3,2)
    gather_start(4)
    gather_x(2); gather_z(3,3); gather_z(4,1)
    for g in range(3): gather_done(g)
    for c in own_copies: c.wait()
    TF=512
    @pl.loop(0,NC)
    def _(c):
        tok_copy(c).wait_recv()
        @pl.loop(0,n//TF)
        def _(j):
            cs=pl.ds(pl.multiple_of(j*TF,TF),TF)
            qkv[chunk(c),cs]=(dot(hall[chunk(c)],strip(act,cs),NN)+bias[:,cs]).astype(BF)
        @pl.when(c==0)
        def _(): gather_z(4,2)
        @pl.when(c==1)
        def _():
            gather_x(3); gather_z(4,3)
        @pl.when(c==2)
        def _(): gather_start(5)
        @pl.when(c==3)
        def _():
            gather_z(5,1); gather_done(3)
    x_out=local(hall,x_hbm,5); w_out=local(act.at[:,:,0:n],wh_hbm,6)
    x_out.start(); w_out.start()
    ones=jnp.where(lax.broadcasted_iota(jnp.int32,(16,rows_all),0)==0,1.0,0.0).astype(BF)
    @pl.loop(0,pairs)
    def _(p):
        ck=pl.multiple_of(width+p*128,128); cv=pl.multiple_of(2*width+p*128,128)
        kt[p]=qkv[:,pl.ds(ck,128)].T
        v=qkv[:,pl.ds(cv,128)].T
        vt[2*p,0:64]=v[0:64]; vt[2*p,64:80]=ones
        vt[2*p+1,0:64]=v[64:128]; vt[2*p+1,64:80]=ones
    x_out.wait()
    def split(k,c):
        sbuf[k-1,loc(c)]=pch[half(1-t)].astype(BF)
        rs_copy(k,c).start()
        part[loc(c)]=pch[half(t)]
    def stats(v):
        cen=v-jnp.mean(v,axis=1,keepdims=True)
        r=lax.rsqrt(jnp.mean(cen*cen,axis=1,keepdims=True)+EPSILON)
        return cen*r,r
    def lo_copy(c): return pltpu.make_async_copy(cl.at[loc(c)],lo_hbm.at[loc(c)],losem.at[c])
    def out_copy(slot,col):
        return pltpu.make_async_copy(stage.at[slot],dw.at[:,:,:,:,pl.ds(pl.multiple_of(col,512),512)],osem.at[slot])
    def wgrad(slot,left,right_ref,rcol,ocol):
        @pl.loop(0,dm//256)
        def _(i):
            ms=pl.ds(pl.multiple_of(i*256,256),256)
            right=right_ref[:,pl.ds(pl.multiple_of(rcol,512),512)] if len(right_ref.shape)==2 else strip(right_ref,pl.ds(pl.multiple_of(rcol,512),512))
            stage[slot,i]=dot(left[ms],right,NN).astype(BF).reshape(2,2,64,512)
        out_copy(slot,ocol).start()
    def stage_a(c):
        rs=chunk(c)
        @pl.loop(0,pairs)
        def _(p):
            cq=pl.ds(pl.multiple_of(p*128,128),128); ck=pl.ds(pl.multiple_of(width+p*128,128),128)
            pks=[]
            for h in (0,1):
                keep=(lane<64) if h==0 else (lane>=64)
                q=jnp.where(keep,qkv[rs,cq]*scale,zero)
                st=dot(qkv[:,ck],q,NT)
                m=jnp.max(st,axis=0,keepdims=True)
                mc=m*LOG2E
                pt=jnp.exp2(st*LOG2E-mc).astype(BF)
                ot=dot(vt[2*p+h],pt,NN)
                tot=ot[64:65]
                ctt[h*64:(h+1)*64,:]=ot[0:64]*(1.0/tot)
                lse[pl.ds(2*p+h,1),rs]=mc+jnp.log2(tot)
                pks.append(jnp.max(m,axis=1,keepdims=True))
            early[10:11,cq]=jnp.maximum(early[10:11,cq],jnp.where(lane<64,pks[0],pks[1]))
            ctx[rs,cq]=ctt[...].T.astype(BF)
            step=c*pairs+p
            @pl.when(step==0)
            def _():
                gather_z(5,2)
            @pl.when(step==2)
            def _():
                gather_z(5,3)
                gather_start(6)
            @pl.when(step==4)
            def _():
                gather_z(6,1)
                gather_x(4)
            @pl.when(step==6)
            def _():
                gather_z(6,2)
                gather_start(7)
            @pl.when(step==8)
            def _():
                gather_z(6,3)
                gather_z(7,1)
            @pl.when(step==10)
            def _():
                gather_z(7,2)
                gather_x(5)
            @pl.when(step==12)
            def _():
                gather_z(7,3)
            @pl.when(step==14)
            def _():
                gather_x(6)
        ctx_copy(c,t).start()
        ctxo[loc(c),cols(t)]=ctx[rows(t,c)]
    def stage_b(c):
        ctx_copy(c,1-t).wait_recv()
        x,r=stats(hall[rows(t,c)].astype(F32)+dot(ctxo[loc(c)],whole(wo),NT)+vec[0:1])
        xh[loc(c)]=x
        rst[loc(c)]=jnp.broadcast_to(r,(cr,128))
        hall[rows(t,c)]=(x*vec[1:2]+vec[2:3]).astype(BF)
        ag_copy(3,hall,c,t).start()
    def stage_c(c):
        rs=chunk(c)
        ag_copy(3,hall,c,1-t).wait_recv()
        @pl.loop(0,ff//TF)
        def _(j):
            cs=pl.ds(pl.multiple_of(j*TF,TF),TF)
            u=dot(hall[rs],strip(wup,cs),NN)+upb[:,cs]
            cdf=0.5*(1.0+lax.erf(u*0.5**0.5))
            act[pl.ds(4*c,4),:,cs]=(u*cdf).astype(BF).reshape(4,64,TF)
            slp[rs,cs]=(cdf+u*jnp.exp(-0.5*u*u)*(0.5/math.pi)**0.5).astype(BF)
        @pl.when(c==0)
        def _():
            gather_x(7)
            gather_done(6); gather_done(7)
        pch[...]=dot(act[pl.ds(4*c,4)].reshape(cg,ff),whole(wdn),NT)
        split(1,c)
    def stage_d(c):
        rs_copy(1,c).wait_recv()
        x,r=stats(xh[loc(c)]*vec[1:2]+vec[2:3]+part[loc(c)]+rbuf[0,loc(c)].astype(F32)+vec[3:4])
        dy=cl[loc(c)].astype(F32)
        cl[loc(c)]=(x*vec[4:5]+vec[5:6]).astype(BF)
        lo_copy(c).start()
        early[4:5]+=jnp.sum(dy*x,axis=0,keepdims=True)
        early[5:6]+=jnp.sum(dy,axis=0,keepdims=True)
        dx=dy*vec[4:5]
        g=r*(dx-jnp.mean(dx,axis=1,keepdims=True)-x*jnp.mean(dx*x,axis=1,keepdims=True))
        gf[loc(c)]=g
        gb=g.astype(BF)
        early[3:4]+=jnp.sum(gb.astype(F32),axis=0,keepdims=True)
        ball[rows(t,c)]=gb
        ag_copy(4,ball,c,t).start()
        tb[:,rows(t,c)]=gb.T
    def stage_e(c):
        rs=chunk(c)
        ag_copy(4,ball,c,1-t).wait_recv()
        @pl.loop(0,ff//TF)
        def _(j):
            cs=pl.ds(pl.multiple_of(j*TF,TF),TF)
            gu=(dot(ball[rs],strip(wdn,cs),NN)*slp[rs,cs].astype(F32)).astype(BF)
            slp[rs,cs]=gu
            row=pl.ds(8+j*TF//dm,1); cc=pl.ds(pl.multiple_of(j*TF%dm,TF),TF)
            early[row,cc]+=jnp.sum(gu.astype(F32),axis=0,keepdims=True)
        pch[...]=dot(slp[rs],whole(wup),NT)
        split(2,c)
        tb[:,rows(1-t,c)]=ball[rows(1-t,c)].T
        th[:,chunk(c)]=hall[chunk(c)].T
    def stage_f(c):
        rs_copy(2,c).wait_recv()
        dy=gf[loc(c)]+part[loc(c)]+rbuf[1,loc(c)].astype(F32)
        x=xh[loc(c)]; r=rst[loc(c)][:,0:1]
        early[1:2]+=jnp.sum(dy*x,axis=0,keepdims=True)
        early[2:3]+=jnp.sum(dy,axis=0,keepdims=True)
        dx=dy*vec[1:2]
        g=r*(dx-jnp.mean(dx,axis=1,keepdims=True)-x*jnp.mean(dx*x,axis=1,keepdims=True))
        gf[loc(c)]=g
        gb=g.astype(BF)
        early[0:1]+=jnp.sum(gb.astype(F32),axis=0,keepdims=True)
        ga[loc(c)]=gb
        dcs[loc(c)]=dot(gb,whole(wo),NN).astype(BF)
        dctx_copy(c,t).start()
        dcall[rows(t,c)]=dcs[loc(c),cols(t)]
    def stage_g(c):
        rs=chunk(c)
        dctx_copy(c,1-t).wait_recv()
        @pl.loop(0,pairs)
        def _(p):
            cq=pl.ds(pl.multiple_of(p*128,128),128); ck=pl.ds(pl.multiple_of(width+p*128,128),128); cv=pl.ds(pl.multiple_of(2*width+p*128,128),128)
            prod=(ctx[rs,cq].astype(F32)*dcall[rs,cq].astype(F32)).T
            dl[0:1]=jnp.sum(prod[0:64],axis=0,keepdims=True)
            dl[1:2]=jnp.sum(prod[64:128],axis=0,keepdims=True)
            for h in (0,1):
                keep=(lane<64) if h==0 else (lane>=64)
                q=jnp.where(keep,qkv[rs,cq]*scale,zero)
                do=jnp.where(keep,dcall[rs,cq],zero)
                st=dot(qkv[:,ck],q,NT)
                pt=jnp.exp2(st*LOG2E-lse[pl.ds(2*p+h,1),rs])
                dpt=dot(qkv[:,cv],do,NT)
                ds=(pt*(dpt-dl[h:h+1])).astype(BF)
                dkv[1,:,cq]+=dot(pt.astype(BF),do,NN)
                dkv[0,:,cq]+=dot(ds,q,NN)
                dqt[h*64:(h+1)*64,:]=dot(kt[p,h*64:(h+1)*64,:],ds,NN)
            qkv[rs,cq]=(dqt[...].T*(HD**-0.5)).astype(BF)
            step=c*pairs+p
            @pl.when(step==0)
            def _():
                s2(0).wait_send(); s2(1).start()
                fetch3(0)
                ecopy(0).start()
            @pl.when(step==1)
            def _():
                add3(0)
                fetch2(2)
            @pl.when(step==2)
            def _():
                add2(2)
                fetch2(3)
            @pl.when(step==3)
            def _():
                add2(3)
                drain(); s1(4).start()
            @pl.when(step==4)
            def _():
                eadd(0); ecopy(1).start()
            @pl.when(step==5)
            def _():
                fetch2(4)
            @pl.when(step==6)
            def _():
                s2(1).wait_send(); s2(2).start()
                fetch3(1)
                add2(4)
            @pl.when(step==7)
            def _():
                eadd(1); ecopy(2).start()
            @pl.when(step==8)
            def _():
                sent3(0); add3(1)
            @pl.when(step==10)
            def _():
                eadd(2); ecopy(3).start()
            @pl.when(step==11)
            def _():
                fetchf(0)
            @pl.when(step==12)
            def _():
                s2(2).wait_send(); s2(3).start()
                fetch3(2)
            @pl.when(step==13)
            def _():
                finish(0)
                eadd(3); ecopy(4).start()
            @pl.when(step==14)
            def _():
                sent3(1); add3(2)
    def grad_down(c):
        slot=c%2
        wgrad(slot,tb,act,c*512,wide+ff+c*512)
    def grad_up(c):
        slot=c%2
        wgrad(slot,th,slp,c*512,wide+c*512)
    def grad_out():
        @pl.loop(0,NC)
        def _(c): tb[:,loc(c)]=ga[loc(c)].T
        for j in range(wide//512):
            @pl.loop(0,dm//256)
            def _(i):
                ms=pl.ds(pl.multiple_of(i*256,256),256)
                stage[j%2,i]=dot(tb[ms,0:own],ctxo[:,j*512:(j+1)*512],NN).astype(BF).reshape(2,2,64,512)
            out_copy(j%2,j*512).start()
    @pl.loop(0,NC)
    def _(c):
        stage_a(c)
        @pl.when(c>0)
        def _(): stage_b(c-1)
    cot_load.wait(); w_out.wait()
    gather_done(4); gather_done(5)
    @pl.loop(0,NC)
    def _(c):
        stage_c(c)
        @pl.when(c==0)
        def _(): stage_b(NC-1)
        @pl.when(c>=2)
        def _(): stage_d(c-2)
    @pl.loop(NC-2,NC)
    def _(c): stage_d(c)
    @pl.loop(0,NC)
    def _(c): stage_e(c)
    piece=ff//2
    base=(wide+ff,wide+ff+piece,wide,wide+piece,0,wide+2*ff,wide+2*ff+width,wide+2*ff+2*width)
    span=(piece,)*5+(width,)*3
    def s1(g): return remote(dw.at[:,:,1-core,:,base[g]:base[g]+span[g]],r1.at[g,:,:,:,0:span[g]],g1s.at[g],g1r.at[g],sib)
    slots2=[wup.at[8:12,:,0:piece],wup.at[12:16,:,0:piece],wup.at[8:12,:,piece:],wup.at[12:16,:,piece:],wup.at[0:4,:,piece:],wup.at[4:8,:,piece:]]
    slots3=[wdn.at[12:16,:,0:piece],wdn.at[12:16,:,piece:],wdn.at[0:4,:,piece:],wdn.at[4:8,:,piece:],wdn.at[8:12,:,piece:]]
    sum2=[slots2[g%6] for g in range(8)]
    sum3=[slots3[g%5] for g in range(8)]
    def s2(g): return remote(sum2[g].at[:,:,0:span[g]],r2.at[g,:,:,0:span[g]],g2s.at[g],g2r.at[g],xp)
    def s3(g,k): return remote(sum3[g].at[(z+k)%4,:,0:span[g]],r3.at[g,3-k,:,0:span[g]],g3s.at[g,k-1],g3r.at[g,k-1],zp[k-1])
    def load2(g): return [pltpu.make_async_copy(dw.at[:,1-x_,core,:,base[g]:base[g]+span[g]],wup.at[0:4,:,0:span[g]],rl.at[0]),
                          pltpu.make_async_copy(r1.at[g,:,1-x_,:,0:span[g]],wup.at[4:8,:,0:span[g]],rl.at[1])]
    def load3(g): return [pltpu.make_async_copy(dw.at[:,x_,core,:,base[g]:base[g]+span[g]],wdn.at[0:4,:,0:span[g]],rl.at[2]),
                         pltpu.make_async_copy(r1.at[g,:,x_,:,0:span[g]],wdn.at[4:8,:,0:span[g]],rl.at[3]),
                         pltpu.make_async_copy(r2.at[g,:,:,0:span[g]],wdn.at[8:12,:,0:span[g]],rl.at[4])]
    def fetch2(g):
        s1(g).wait_recv()
        for l in load2(g): l.start()
    def add2(g):
        for l in load2(g): l.wait()
        @pl.loop(0,4)
        def _(i): sum2[g][i,:,0:span[g]]=(wup[i,:,0:span[g]].astype(F32)+wup[4+i,:,0:span[g]].astype(F32)).astype(BF)
    def fetch3(g):
        s2(g).wait_recv()
        for l in load3(g): l.start()
    def add3(g):
        for l in load3(g): l.wait()
        @pl.loop(0,4)
        def _(i): sum3[g][i,:,0:span[g]]=(wdn[i,:,0:span[g]].astype(F32)+wdn[4+i,:,0:span[g]].astype(F32)+wdn[8+i,:,0:span[g]].astype(F32)).astype(BF)
        for k in (1,2,3): s3(g,k).start()
    def sent3(g):
        for k in (1,2,3): s3(g,k).wait_send()
    def fslot(g,i):
        r=64*(6*(g%2)+i)
        return tb.at[r:r+64,0:span[g]]
    def loadf(g): return [pltpu.make_async_copy(src,fslot(g,i),fl.at[g%2,i]) for i,src in enumerate(
        [dw.at[z,x_,core,:,base[g]:base[g]+span[g]],r1.at[g,z,x_,:,0:span[g]],r2.at[g,z,:,0:span[g]]]+[r3.at[g,k,:,0:span[g]] for k in range(3)])]
    def fetchf(g):
        for k in (1,2,3): s3(g,k).wait_recv()
        for l in loadf(g): l.start()
    def final(g):
        for l in loadf(g): l.wait()
        v=[fslot(g,i)[...].astype(F32) for i in range(6)]
        return v[0]+v[1]+v[2]+v[3]+v[4]+v[5]
    def fin_copy(g):
        src=xh.at[64*g:64*g+64,0:span[g]]
        return pltpu.make_async_copy(src,fin.at[g] if g<4 else go_hbm if g==4 else fin_head.at[g-5],fs.at[g]) if g!=4 else pltpu.make_async_copy(xh.at[256:320,0:width],go_hbm,fs.at[4])
    def finish(g):
        xh[64*g:64*g+64,0:span[g]]=final(g)
        fin_copy(g).start()
    zb=[dev(z+1-2*(z%2),x_,core),dev((z+2)%4,x_,core)]
    hops=[sib,xp,zb[0],zb[1],partner]
    def ecopy(i): return remote(eb.at[i],er.at[i],es.at[i],erc.at[i],hops[i])
    def eadd(i):
        ecopy(i).wait_recv()
        b=eb[i,8:16]; c=er[i,8:16]
        if i<4:
            r=lax.broadcasted_iota(jnp.int32,b.shape,0)
            b=jnp.where(r==2,jnp.maximum(b,c),b+c)
        eb[i+1,0:8]=eb[i,0:8]+er[i,0:8]; eb[i+1,8:16]=b
    def lcopy(i): return remote(lb.at[i],lr.at[i],ls.at[i],lrc.at[i],hops[i])
    def ladd(i):
        lcopy(i).wait_recv()
        lb[i+1]=lb[i]+lr[i]
    def drain():
        out_copy(0,0).wait()
        out_copy(1,0).wait()
    @pl.loop(0,NC)
    def _(c): ag_copy(3,hall,c,t).wait_send()
    x_in=pltpu.make_async_copy(x_hbm,hall,dsem.at[0])
    x_in.start()
    grad_down(0); grad_down(1)
    drain(); s1(0).start()
    grad_down(2); grad_down(3)
    drain(); s1(1).start()
    wh_in=pltpu.make_async_copy(wh_hbm,act.at[:,:,0:n],dsem.at[1])
    wh_in.start()
    @pl.loop(0,NC)
    def _(c):
        stage_f(c)
        grad_up(c)
        @pl.when(c==0)
        def _(): fetch2(0)
        @pl.when(c==1)
        def _():
            add2(0); s2(0).start()
            fetch2(1)
            drain(); s1(2).start()
        @pl.when(c==2)
        def _(): add2(1)
        @pl.when(c==3)
        def _():
            drain(); s1(3).start()
    grad_out()
    @pl.loop(0,NC)
    def _(c): stage_g(c)
    @pl.loop(0,pairs)
    def _(p):
        cq=pl.ds(pl.multiple_of(p*128,128),128); ck=pl.ds(pl.multiple_of(width+p*128,128),128); cv=pl.ds(pl.multiple_of(2*width+p*128,128),128)
        qkv[:,ck]=dkv[0,:,cq].astype(BF)
        qkv[:,cv]=dkv[1,:,cq].astype(BF)
    def ycopy(c): return remote(sbuf.at[0,loc(c)],rbuf.at[0,loc(c)],ssem.at[6,c],rsem.at[6,c],partner)
    wh_in.wait()
    @pl.loop(0,NC)
    def _(c):
        pch[...]=dot(qkv[chunk(c)],act[:,:,0:n].reshape(dm,n),NT)
        rs_copy(1,c).wait_send()
        sbuf[0,loc(c)]=pch[half(1-t)].astype(BF)
        ycopy(c).start()
        part[loc(c)]=pch[half(t)]
    s2(3).wait_send(); s2(4).start()
    fetch3(3)
    lb[0,0:1,0:width]=jnp.sum(qkv[:,0:width].astype(F32),axis=0,keepdims=True)
    lb[0,0:1,width:2*width]=jnp.sum(qkv[:,2*width:].astype(F32),axis=0,keepdims=True)
    lcopy(0).start()
    x_in.wait()
    @pl.loop(0,NC)
    def _(c): th[:,chunk(c)]=hall[chunk(c)].T
    sent3(2); add3(3)
    wgrad(0,th,qkv,0,base[5])
    wgrad(1,th,qkv,width,base[6])
    out_copy(0,0).wait(); s1(5).start()
    fetchf(1)
    out_copy(1,0).wait(); s1(6).start()
    wgrad(0,th,qkv,2*width,base[7])
    finish(1)
    out_copy(0,0).wait(); s1(7).start()
    fetch2(5)
    ladd(0); lcopy(1).start()
    eadd(4)
    add2(5)
    fetch2(6)
    s2(4).wait_send(); s2(5).start()
    fetch3(4)
    add2(6)
    fetch2(7)
    fetchf(2)
    sent3(3); add3(4)
    ladd(1); lcopy(2).start()
    add2(7)
    s2(5).wait_send(); s2(6).start()
    fetch3(5)
    finish(2)
    smalls[...]=eb[5]
    pk=eb[4,10:11,0:width]
    head=lax.broadcasted_iota(jnp.int32,(1,width),1)//HD
    limit=jnp.zeros((1,width),F32)
    for h in range(width//HD): limit=jnp.where(head==h,lim[h],limit)
    sc=jnp.sqrt(limit/jnp.maximum(pk,limit))
    ga[0:64,0:width]=(wq[...].astype(F32)*sc).astype(BF)
    ga[64:128,0:width]=(wk[...].astype(F32)*sc).astype(BF)
    clips=[pltpu.make_async_copy(ga.at[0:64,0:width],qc_hbm,fs.at[8]),pltpu.make_async_copy(ga.at[64:128,0:width],kc_hbm,fs.at[9])]
    for c in clips: c.start()
    smalls[11:12,0:width]=row(v_qb)*sc
    ladd(2); lcopy(3).start()
    fetchf(3)
    sent3(4); add3(5)
    s2(6).wait_send(); s2(7).start()
    fetch3(6)
    finish(3)
    @pl.loop(0,NC)
    def _(c): lo_copy(c).wait()
    def tg_copy(c): return pltpu.make_async_copy(cl.at[loc(c)],tg_hbm.at[loc(c)],losem.at[c])
    @pl.loop(0,NC)
    def _(c):
        ycopy(c).wait_recv()
        cl[loc(c)]=(gf[loc(c)]+part[loc(c)]+rbuf[0,loc(c)].astype(F32)).astype(BF)
        tg_copy(c).start()
    fetchf(4)
    ladd(3)
    smalls[12:13]=lb[4,0:1]
    sent3(5); add3(6)
    v=final(4)
    osb[0]=v[:,0:width]; osb[1]=v[:,width:]
    ocopy=remote(osb.at[1-t],orb,os_.at[0],or_.at[0],partner)
    ocopy.start()
    fetch3(7)
    fetchf(5)
    s2(7).wait_send()
    sent3(6); add3(7)
    finish(5)
    ocopy.wait_recv()
    xh[256:320,0:width]=osb[t]+orb[...]
    fin_copy(4).start()
    fetchf(6)
    finish(6)
    fetchf(7)
    finish(7)
    o_swap.wait_send()
    ocopy.wait_send()
    for g in range(8):
        s1(g).wait_send()
        fin_copy(g).wait()
    sent3(7)
    for c in clips: c.wait()
    for i in range(5): ecopy(i).wait_send()
    for i in range(4): lcopy(i).wait_send()
    @pl.loop(0,NC)
    def _(c):
        tg_copy(c).wait()
        ctx_copy(c,t).wait_send(); dctx_copy(c,t).wait_send(); tok_copy(c).wait_send()
        rs_copy(2,c).wait_send(); ycopy(c).wait_send()
        ag_copy(4,ball,c,t).wait_send()

def main_call(shards,tok,cot,vectors,lim,cid):
    V=pl.BlockSpec(memory_space=pltpu.VMEM); A=pl.BlockSpec(memory_space=pl.ANY)
    width=shards[0].shape[1]; ff=shards[4].shape[1]; own,dm=tok.shape; rows=2*own; n=3*width; cr=own//NC; wide=2*width; piece=ff//2
    S=jax.ShapeDtypeStruct; M=pltpu.VMEM; D=pltpu.SemaphoreType.DMA
    return pl.pallas_call(main_kernel,
      out_shape=(S((own,dm),BF),S((own,dm),BF),S((4,64,piece),F32),S((3,64,width),F32),S((64,width),F32),S((64,width),BF),S((64,width),BF),S((16,dm),F32),
        S((4,2,2,64,wide+2*ff+n),BF),S((8,4,2,64,piece),BF),S((8,4,64,piece),BF),S((8,3,64,piece),BF),S((rows,dm),BF),S((16,64,n),BF)),
      in_specs=[V]*6+[A,A]+[V]*9+[pl.BlockSpec(memory_space=pltpu.SMEM)],out_specs=(A,)*7+(V,)+(A,)*6,
      scratch_shapes=[M((1,n),F32),M((8,dm),F32),M((1,ff),F32),M((own,dm),F32),M((6,16,dm),F32),M((5,16,dm),F32),M((5,8,dm),F32),M((4,8,dm),F32),M((2,64,width),F32),M((64,width),F32),
        M((64,n+wide+2*ff),BF),M((rows,n),BF),M((width//HD,80,rows),BF),M((width//128,128,rows),BF),M((rows,width),BF),M((own,wide),BF),M((width//HD,rows),F32),M((own,dm),BF),
        M((16,64,wide),BF),M((16,64,ff),BF),M((16,64,ff),BF),
        M((own,dm),F32),M((own,128),F32),
        M((rows,dm),BF),M((16,64,ff),BF),M((rows,ff),BF),M((rows,dm),BF),M((own,dm),BF),M((own,wide),BF),M((rows,width),BF),
        M((own,dm),F32),M((2*cr,dm),F32),M((128,2*cr),F32),M((128,2*cr),F32),M((8,2*cr),F32),M((2,rows,width),F32),
        M((2,own,dm),BF),M((2,own,dm),BF),
        M((dm,rows),BF),M((dm,rows),BF),M((2,4,2,2,64,512),BF),
        D((7,)),D((NC,)),D((2,)),D((2,)),D((7,NC)),D((7,NC)),D((5,)),D((8,)),D((8,)),D((8,)),D((8,)),D((8,3)),D((8,3)),
        D((NC+1,)),D((NC+1,)),D((8,2,3)),D((8,2,3)),D((8,4)),D((8,4)),D((8,8)),D((8,8)),
        D((5,)),D((5,)),D((4,)),D((4,)),D((1,)),D((1,)),D((2,6)),D((10,))],
      compiler_params=pltpu.CompilerParams(collective_id=cid,has_side_effects=True,vmem_limit_bytes=61*2**20),
      name="main")(*shards,tok,cot,*vectors,lim)

def finish_kernel(lo,tg,fin,fin_head,go,qc,kc,smalls,
                  lo_,tg_,gq_,gk_,gv_,go_,gu_,gd_,qc_,kc_,qb_,vb_,ob_,g1_,b1_,ub_,db_,g2_,b2_,pk_,qbc_,h_lo,h_tg,h_fin,h_head,h_go,h_qc,h_kc,isem,sem):
    piece=fin.shape[2]
    ins=[pltpu.make_async_copy(a,b,isem.at[i]) for i,(a,b) in enumerate(((lo,h_lo),(tg,h_tg),(fin,h_fin),(fin_head,h_head),(go,h_go),(qc,h_qc),(kc,h_kc)))]
    outs=[[(h_lo,lo_)],[(h_tg,tg_)],[(h_fin.at[0],gd_.at[:,0:piece]),(h_fin.at[1],gd_.at[:,piece:]),(h_fin.at[2],gu_.at[:,0:piece]),(h_fin.at[3],gu_.at[:,piece:])],
          [(h_head.at[0],gq_),(h_head.at[1],gk_),(h_head.at[2],gv_)],[(h_go,go_)],[(h_qc,qc_)],[(h_kc,kc_)]]
    for c in ins: c.start()
    width=qb_.shape[0]; dm=ob_.shape[0]
    def line(v): return v.reshape(v.shape[1])
    qb_[...]=line(smalls[12:13,0:width]); vb_[...]=line(smalls[12:13,width:2*width])
    for i,o in enumerate((ob_,g1_,b1_,db_,g2_,b2_)): o[...]=line(smalls[i:i+1])
    ub_[0:dm]=line(smalls[8:9]); ub_[dm:2*dm]=line(smalls[9:10])
    for h in range(pk_.shape[0]): pk_[h]=jnp.max(smalls[10:11,h*HD:(h+1)*HD])
    qbc_[...]=line(smalls[11:12,0:width]).astype(BF)
    moved=[]
    for a,group in zip(ins,outs):
        a.wait()
        for src,dst in group:
            c=pltpu.make_async_copy(src,dst,sem.at[len(moved)])
            c.start()
            moved.append(c)
    for c in moved: c.wait()

def finish_call(big,smalls,heads):
    V=pl.BlockSpec(memory_space=pltpu.VMEM); A=pl.BlockSpec(memory_space=pl.ANY); S=jax.ShapeDtypeStruct
    lo,tg,fin,fin_head,go,qc,kc=big
    width=go.shape[1]; piece=fin.shape[2]; ff=2*piece; dm=tg.shape[1]
    return pl.pallas_call(finish_kernel,
      out_shape=(S(lo.shape,BF),S(tg.shape,BF))+(S((64,width),F32),)*4+(S((64,ff),F32),)*2+(S((64,width),BF),)*2
        +tuple(S((k,),F32) for k in (width,width,dm,dm,dm,ff,dm,dm,dm,heads))+(S((width,),BF),),
      in_specs=[A]*7+[V],out_specs=(A,)*10+(V,)*9+(pl.BlockSpec(memory_space=pltpu.SMEM),V),
      scratch_shapes=[pltpu.VMEM(a.shape,a.dtype) for a in big]+[pltpu.SemaphoreType.DMA((7,)),pltpu.SemaphoreType.DMA((12,))],
      compiler_params=pltpu.CompilerParams(vmem_limit_bytes=61*2**20),name="finish")(*big,smalls)

def per_device_pair(tokens,query_weight,query_bias,key_weight,value_weight,value_bias,out_weight,out_bias,first_gain,first_shift,
    up_weight,up_bias,down_weight,down_bias,second_gain,second_shift,cotangent,clip_limit):
    shards=(query_weight,key_weight,value_weight,out_weight.T,up_weight,down_weight.T)
    vectors=(out_bias,first_gain,first_shift,down_bias,second_gain,second_shift,up_bias,query_bias,value_bias)
    res=main_call(shards,tokens,cotangent,vectors,clip_limit,1)
    lo,tg,gq,gk,gv,go,gu,gd,qc,kc,qb,vb,ob,g1,b1,ub,db,g2,b2,pk,qbc=finish_call(res[:7],res[7],clip_limit.shape[0])
    return (lo,tg,gq,qb,gk,gv,vb,go.T,ob,g1,b1,gu,ub,gd.T,db,g2,b2,pk,qc,qbc,kc)


def layer(*args):
    paired = lax.axis_size("dp") == 16 and lax.axis_size("tensor") == 2 and 2 * args[0].shape[0] == LEN
    return per_device_pair(*args) if paired else per_device(*args)


def solution(mesh):
    in_specs = (
        P(("dp", "tensor"), None),
        P("dp", "tensor"),
        P("tensor"),
        P("dp", "tensor"),
        P("dp", "tensor"),
        P("tensor"),
        P("tensor", "dp"),
        P(),
        P(),
        P(),
        P("dp", "tensor"),
        P("tensor"),
        P("tensor", "dp"),
        P(),
        P(),
        P(),
        P(("dp", "tensor"), None),
        P("tensor"),
    )
    out_specs = (
        P(("dp", "tensor"), None),
        P(("dp", "tensor"), None),
        P("dp", "tensor"),
        P("tensor"),
        P("dp", "tensor"),
        P("dp", "tensor"),
        P("tensor"),
        P("tensor", "dp"),
        P(),
        P(),
        P(),
        P("dp", "tensor"),
        P("tensor"),
        P("tensor", "dp"),
        P(),
        P(),
        P(),
        P("tensor"),
        P("dp", "tensor"),
        P("tensor"),
        P("dp", "tensor"),
    )
    return jax.shard_map(
        layer, mesh=mesh, in_specs=in_specs, out_specs=out_specs, check_vma=False
    )
```

```python
import functools
import math

import jax
import jax.numpy as jnp
from jax import lax
from jax.experimental import pallas as pl
from jax.experimental.pallas import tpu as pltpu
from jax.sharding import PartitionSpec as P

HD = 64
LEN = 1024
QB = 512


def layer_norm(values, gain, shift):
    center = values - jnp.mean(values, axis=-1, keepdims=True)
    spread = jnp.mean(center * center, axis=-1, keepdims=True)
    return center * lax.rsqrt(spread + EPSILON) * gain + shift


def gelu_slope(upper):
    normal_cdf = 0.5 * (1.0 + lax.erf(upper * 0.5**0.5))
    return normal_cdf + upper * jnp.exp(-0.5 * upper * upper) * (0.5 / math.pi) ** 0.5


def contract_rows(left, right):
    return lax.dot_general(
        left, right, (((0,), (0,)), ((), ())), preferred_element_type=jnp.float32
    )


def contract_cols(left, right):
    return lax.dot_general(
        left, right, (((1,), (1,)), ((), ())), preferred_element_type=jnp.float32
    )


def per_device(
    tokens,
    query_weight,
    query_bias,
    key_weight,
    value_weight,
    value_bias,
    out_weight,
    out_bias,
    first_gain,
    first_shift,
    up_weight,
    up_bias,
    down_weight,
    down_bias,
    second_gain,
    second_shift,
    cotangent,
    clip_limit,
):
    query_full, key_full, value_full, out_full, up_full, down_full = (
        lax.all_gather(query_weight, "dp", axis=0, tiled=True),
        lax.all_gather(key_weight, "dp", axis=0, tiled=True),
        lax.all_gather(value_weight, "dp", axis=0, tiled=True),
        lax.all_gather(out_weight, "dp", axis=1, tiled=True),
        lax.all_gather(up_weight, "dp", axis=0, tiled=True),
        lax.all_gather(down_weight, "dp", axis=1, tiled=True),
    )
    width = query_full.shape[1]
    hidden_width = up_full.shape[1]
    heads_here = width // HD
    score_scale = HD ** (-0.5)
    joint_weight = jnp.concatenate([query_full, key_full, value_full], axis=1)
    gathered = lax.all_gather(tokens, "tensor", axis=0, tiled=True)
    group_rows = gathered.shape[0]
    seq_count = group_rows // LEN
    block_count = LEN // QB
    projected = jnp.dot(gathered, joint_weight, preferred_element_type=jnp.float32)
    queries = (projected[:, :width] + query_bias.astype(jnp.float32)).astype(jnp.bfloat16)
    keyset = projected[:, width : 2 * width].astype(jnp.bfloat16)
    valset = (projected[:, 2 * width :] + value_bias.astype(jnp.float32)).astype(jnp.bfloat16)
    query_seq = queries.reshape(seq_count, LEN, heads_here, HD)
    key_seq = keyset.reshape(seq_count, LEN, heads_here, HD)
    value_seq = valset.reshape(seq_count, LEN, heads_here, HD)

    def attend_block(block_id):
        seq_id = block_id // block_count
        row_start = block_id % block_count * QB
        query_rows = lax.dynamic_slice_in_dim(
            lax.dynamic_index_in_dim(query_seq, seq_id, 0, False), row_start, QB, 0
        )
        key_rows = lax.dynamic_index_in_dim(key_seq, seq_id, 0, False)
        value_rows = lax.dynamic_index_in_dim(value_seq, seq_id, 0, False)
        logits = (
            jnp.einsum("qhd,khd->hqk", query_rows, key_rows, preferred_element_type=jnp.float32)
            * score_scale
        )
        row_max = jnp.max(logits, axis=2, keepdims=True)
        exponent = jnp.exp(logits - row_max)
        totals = jnp.sum(exponent, axis=2, keepdims=True)
        probs_low = (exponent / totals).astype(jnp.bfloat16)
        context_rows = jnp.einsum(
            "hqk,khd->qhd", probs_low, value_rows, preferred_element_type=jnp.float32
        )
        return (
            context_rows.reshape(QB, width).astype(jnp.bfloat16),
            (row_max + jnp.log(totals))[:, :, 0],
            jnp.max(row_max, axis=(1, 2)),
        )

    context_blocks, log_totals, block_peaks = lax.map(
        attend_block, jnp.arange(seq_count * block_count)
    )
    context = context_blocks.reshape(group_rows, width)
    logit_peak = lax.pmax(jnp.max(block_peaks, axis=0), "dp")
    attention = lax.psum_scatter(
        jnp.dot(context, out_full, preferred_element_type=jnp.float32).astype(jnp.bfloat16),
        "tensor",
        scatter_dimension=0,
        tiled=True,
    ).astype(jnp.float32) + out_bias.astype(jnp.float32)
    first_resid = tokens.astype(jnp.float32) + attention
    hidden, first_pull = jax.vjp(
        layer_norm, first_resid, first_gain.astype(jnp.float32), first_shift.astype(jnp.float32)
    )
    hidden_all = lax.all_gather(hidden.astype(jnp.bfloat16), "tensor", axis=0, tiled=True)
    upper = jnp.dot(hidden_all, up_full, preferred_element_type=jnp.float32) + up_bias.astype(
        jnp.float32
    )
    acted = jax.nn.gelu(upper, approximate=False).astype(jnp.bfloat16)
    branch = lax.psum_scatter(
        jnp.dot(acted, down_full, preferred_element_type=jnp.float32).astype(jnp.bfloat16),
        "tensor",
        scatter_dimension=0,
        tiled=True,
    ).astype(jnp.float32) + down_bias.astype(jnp.float32)
    normed, second_pull = jax.vjp(
        layer_norm,
        hidden + branch,
        second_gain.astype(jnp.float32),
        second_shift.astype(jnp.float32),
    )
    layer_out = normed.astype(jnp.bfloat16)
    grad_second, second_gain_grad, second_shift_grad = second_pull(cotangent.astype(jnp.float32))
    grad_branch = grad_second.astype(jnp.bfloat16)
    down_bias_grad = jnp.sum(grad_branch, axis=0, dtype=jnp.float32)
    branch_all = lax.all_gather(grad_branch, "tensor", axis=0, tiled=True)
    grad_acted = contract_cols(branch_all, down_full)
    down_weight_grad = contract_rows(acted, branch_all)
    grad_upper = (grad_acted * gelu_slope(upper)).astype(jnp.bfloat16)
    up_bias_grad = jnp.sum(grad_upper, axis=0, dtype=jnp.float32)
    up_weight_grad = contract_rows(hidden_all, grad_upper)
    grad_hidden = grad_second + lax.psum_scatter(
        contract_cols(grad_upper, up_full).astype(jnp.bfloat16),
        "tensor",
        scatter_dimension=0,
        tiled=True,
    ).astype(jnp.float32)
    grad_first, first_gain_grad, first_shift_grad = first_pull(grad_hidden)
    grad_attn = grad_first.astype(jnp.bfloat16)
    out_bias_grad = jnp.sum(grad_attn, axis=0, dtype=jnp.float32)
    attn_all = lax.all_gather(grad_attn, "tensor", axis=0, tiled=True)
    grad_context = contract_cols(attn_all, out_full).astype(jnp.bfloat16)
    out_weight_grad = contract_rows(context, attn_all)
    query_blocks = queries.reshape(seq_count, block_count, QB, heads_here, HD)
    grad_blocks = grad_context.reshape(seq_count, block_count, QB, heads_here, HD)
    log_blocks = log_totals.reshape(seq_count, block_count, heads_here, QB)

    def sequence_back(item):
        query_part, grad_part, log_part, key_rows, value_rows = item

        def block_back(carry, piece):
            key_acc, value_acc = carry
            query_rows, grad_rows, log_rows = piece
            logits = (
                jnp.einsum("qhd,khd->hqk", query_rows, key_rows, preferred_element_type=jnp.float32)
                * score_scale
            )
            probs = jnp.exp(logits - log_rows[:, :, None])
            probs_low = probs.astype(jnp.bfloat16)
            value_acc = value_acc + jnp.einsum(
                "hqk,qhd->khd", probs_low, grad_rows, preferred_element_type=jnp.float32
            )
            grad_probs = jnp.einsum(
                "qhd,khd->hqk", grad_rows, value_rows, preferred_element_type=jnp.float32
            )
            inner = jnp.sum(probs * grad_probs, axis=2, keepdims=True)
            grad_logits = (probs * (grad_probs - inner)).astype(jnp.bfloat16)
            grad_query = (
                jnp.einsum(
                    "hqk,khd->qhd", grad_logits, key_rows, preferred_element_type=jnp.float32
                )
                * score_scale
            )
            key_acc = (
                key_acc
                + jnp.einsum(
                    "hqk,qhd->khd", grad_logits, query_rows, preferred_element_type=jnp.float32
                )
                * score_scale
            )
            return ((key_acc, value_acc), grad_query.astype(jnp.bfloat16))

        empty = jnp.zeros((LEN, heads_here, HD), jnp.float32)
        (key_acc, value_acc), grad_query_rows = lax.scan(
            block_back, (empty, empty), (query_part, grad_part, log_part)
        )
        return (grad_query_rows, key_acc.astype(jnp.bfloat16), value_acc.astype(jnp.bfloat16))

    grad_queries_all, grad_keys_all, grad_values_all = lax.map(
        sequence_back, (query_blocks, grad_blocks, log_blocks, key_seq, value_seq)
    )
    grad_joint = jnp.concatenate(
        [
            grad_queries_all.reshape(group_rows, width),
            grad_keys_all.reshape(group_rows, width),
            grad_values_all.reshape(group_rows, width),
        ],
        axis=1,
    )
    joint_grad = contract_rows(gathered, grad_joint)
    query_weight_grad = joint_grad[:, :width]
    key_weight_grad = joint_grad[:, width : 2 * width]
    value_weight_grad = joint_grad[:, 2 * width :]
    query_bias_grad = jnp.sum(grad_joint[:, :width], axis=0, dtype=jnp.float32)
    value_bias_grad = jnp.sum(grad_joint[:, 2 * width :], axis=0, dtype=jnp.float32)
    tokens_grad = (
        grad_first
        + lax.psum_scatter(
            contract_cols(grad_joint, joint_weight).astype(jnp.bfloat16),
            "tensor",
            scatter_dimension=0,
            tiled=True,
        ).astype(jnp.float32)
    ).astype(jnp.bfloat16)
    (
        query_weight_grad,
        key_weight_grad,
        value_weight_grad,
        out_weight_grad,
        up_weight_grad,
        down_weight_grad,
    ) = (
        lax.psum_scatter(
            query_weight_grad.astype(jnp.bfloat16), "dp", scatter_dimension=0, tiled=True
        ).astype(jnp.float32),
        lax.psum_scatter(
            key_weight_grad.astype(jnp.bfloat16), "dp", scatter_dimension=0, tiled=True
        ).astype(jnp.float32),
        lax.psum_scatter(
            value_weight_grad.astype(jnp.bfloat16), "dp", scatter_dimension=0, tiled=True
        ).astype(jnp.float32),
        lax.psum_scatter(
            out_weight_grad.astype(jnp.bfloat16), "dp", scatter_dimension=1, tiled=True
        ).astype(jnp.float32),
        lax.psum_scatter(
            up_weight_grad.astype(jnp.bfloat16), "dp", scatter_dimension=0, tiled=True
        ).astype(jnp.float32),
        lax.psum_scatter(
            down_weight_grad.astype(jnp.bfloat16), "dp", scatter_dimension=1, tiled=True
        ).astype(jnp.float32),
    )
    tensor_place = lax.axis_index("tensor")
    model_width = out_bias.shape[0]
    query_spread = lax.dynamic_update_slice_in_dim(
        jnp.zeros((model_width,), jnp.float32), query_bias_grad, tensor_place * width, 0
    )
    value_spread = lax.dynamic_update_slice_in_dim(
        jnp.zeros((model_width,), jnp.float32), value_bias_grad, tensor_place * width, 0
    )
    up_spread = lax.dynamic_update_slice_in_dim(
        jnp.zeros((hidden_width * lax.axis_size("tensor"),), jnp.float32),
        up_bias_grad,
        tensor_place * hidden_width,
        0,
    )
    (
        query_spread,
        value_spread,
        up_spread,
        out_bias_grad,
        down_bias_grad,
        first_gain_grad,
        first_shift_grad,
        second_gain_grad,
        second_shift_grad,
    ) = lax.psum(
        (
            query_spread,
            value_spread,
            up_spread,
            out_bias_grad,
            down_bias_grad,
            first_gain_grad,
            first_shift_grad,
            second_gain_grad,
            second_shift_grad,
        ),
        ("dp", "tensor"),
    )
    query_bias_grad = lax.dynamic_slice_in_dim(query_spread, tensor_place * width, width, 0)
    value_bias_grad = lax.dynamic_slice_in_dim(value_spread, tensor_place * width, width, 0)
    up_bias_grad = lax.dynamic_slice_in_dim(up_spread, tensor_place * hidden_width, hidden_width, 0)
    factor = clip_limit / jnp.maximum(logit_peak, clip_limit)
    column_scale = jnp.repeat(jnp.sqrt(factor), HD)
    query_clipped = (query_weight.astype(jnp.float32) * column_scale).astype(jnp.bfloat16)
    query_bias_clipped = (query_bias.astype(jnp.float32) * column_scale).astype(jnp.bfloat16)
    key_clipped = (key_weight.astype(jnp.float32) * column_scale).astype(jnp.bfloat16)
    return (
        layer_out,
        tokens_grad,
        query_weight_grad,
        query_bias_grad,
        key_weight_grad,
        value_weight_grad,
        value_bias_grad,
        out_weight_grad,
        out_bias_grad,
        first_gain_grad,
        first_shift_grad,
        up_weight_grad,
        up_bias_grad,
        down_weight_grad,
        down_bias_grad,
        second_gain_grad,
        second_shift_grad,
        logit_peak,
        query_clipped,
        query_bias_clipped,
        key_clipped,
    )


LOG2E=1.4426950408889634
NT=(((1,),(1,)),((),()))
NN=(((1,),(0,)),((),()))
F32=jnp.float32
BF=jnp.bfloat16
MESH=pl.DeviceIdType.MESH
EPSILON=1e-5
NC=4


def dot(a,b,dims):
    return lax.dot_general(a,b,dims,preferred_element_type=jnp.float32)


def greet(partner):
    barrier=pltpu.get_barrier_semaphore()
    pl.semaphore_signal(barrier,inc=1,device_id=partner,device_id_type=MESH)
    pl.semaphore_wait(barrier,1)


def main_kernel(wq,wk,wv,wos,wu,wds,tok,cot_hbm,v_ob,v_g1,v_b1,v_db,v_g2,v_b2,v_ub,v_qb,v_vb,lim,
               lo_hbm,tg_hbm,fin,fin_head,go_hbm,qc_hbm,kc_hbm,smalls,dw,r1,r2,r3,x_hbm,wh_hbm,
               bias,vec,upb,gf,eb,er,lb,lr,sh,qkv,vt,kt,ctx,ctxo,lse,cl,wo,wup,wdn,xh,rst,hall,act,slp,ball,ga,dcs,dcall,part,pch,ctt,dqt,dl,dkv,sbuf,rbuf,tb,th,stage,
               lsem,losem,dsem,osem,ssem,rsem,rl,g1s,g1r,g2s,g2r,g3s,g3r,ts,tr,azs,azr,axs,axr,acs,acr,es,erc,ls,lrc,fl,fs):
    d=lax.axis_index("dp"); t=lax.axis_index("tensor")
    partner=(d,1-t)
    core=d%2; x_=(d//2)%2; z=d//4
    def dev(z_,xx,c_): return ((z_*2+xx)*2+c_,t)
    sib=dev(z,x_,1-core); xp=dev(z,1-x_,core); zp=[dev((z+k)%4,x_,core) for k in (1,2,3)]
    own,dm=tok.shape; cr=own//NC; cg=2*cr; rows_all=2*own; width=ctx.shape[1]; ff=wup.shape[2]; wide=wo.shape[2]; pairs=width//128
    def local(src,dst,i): return pltpu.make_async_copy(src,dst,lsem.at[i])
    def remote(src,dst,a,b,p): return pltpu.make_async_remote_copy(src,dst,a,b,device_id=p,device_id_type=MESH)
    cot_load=local(cot_hbm,cl,0)
    cot_load.start()
    barrier=pltpu.get_barrier_semaphore()
    n=3*width
    def row(v): return v[...].astype(F32).reshape(1,v.shape[0])
    sh[:,0:width]=wq[...]; sh[:,width:2*width]=wk[...]; sh[:,2*width:n]=wv[...]
    everyone=[partner,sib,xp]+zp
    for p in everyone: pl.semaphore_signal(barrier,inc=1,device_id=p,device_id_type=MESH)
    def chunk(c): return pl.ds(pl.multiple_of(c*cg,cg),cg)
    def rows(rank,c): return pl.ds(pl.multiple_of(c*cg+rank*cr,cr),cr)
    def half(rank): return pl.ds(pl.multiple_of(rank*cr,cr),cr)
    def loc(c): return pl.ds(pl.multiple_of(c*cr,cr),cr)
    def rs_copy(k,c):
        return pltpu.make_async_remote_copy(sbuf.at[k-1,loc(c)],rbuf.at[k-1,loc(c)],ssem.at[k,c],rsem.at[k,c],device_id=partner,device_id_type=MESH)
    def ag_copy(k,buf,c,rank):
        return pltpu.make_async_remote_copy(buf.at[rows(rank,c)],buf.at[rows(rank,c)],ssem.at[k,c],rsem.at[k,c],device_id=partner,device_id_type=MESH)
    def cols(rank): return pl.ds(pl.multiple_of(rank*width,128),width)
    def ctx_copy(c,rank):
        return pltpu.make_async_remote_copy(ctx.at[rows(1-rank,c)],ctxo.at[loc(c),cols(rank)],ssem.at[0,c],rsem.at[0,c],device_id=partner,device_id_type=MESH)
    def dctx_copy(c,rank):
        return pltpu.make_async_remote_copy(dcs.at[loc(c),cols(1-rank)],dcall.at[rows(rank,c)],ssem.at[5,c],rsem.at[5,c],device_id=partner,device_id_type=MESH)
    early=eb.at[0]
    early[...]=jnp.zeros((16,dm),F32)
    early[10:11]=jnp.full((1,dm),-jnp.inf,F32)
    lb[0]=jnp.zeros((8,dm),F32)
    def whole(w): return w[...].reshape(dm,w.shape[2])
    def strip(w,cs): return w[:,:,cs].reshape(dm,TF)
    dkv[...]=jnp.zeros_like(dkv)
    lane=lax.broadcasted_iota(jnp.int32,(1,128),1)
    scale=jnp.bfloat16(HD**-0.5); zero=jnp.bfloat16(0)
    q4=ff//2
    groups=[(act,0,0,width),(act,width,width,width),(act,2*width,2*width,width),(wo,0,n,wide),
            (wup,0,n+wide,q4),(wup,q4,n+wide+q4,q4),(wdn,0,n+wide+ff,q4),(wdn,q4,n+wide+ff+q4,q4)]
    def block(z_,xx): return (z_*2+xx)*2+core
    me=block(z,x_)
    def place(g,b):
        buf,c0,_,nc=groups[g]
        return buf.at[b,:,c0:c0+nc]
    def shard(g): return sh.at[:,groups[g][2]:groups[g][2]+groups[g][3]]
    up=dev(jnp.minimum(z+1,3),x_,core); down=dev(jnp.maximum(z-1,0),x_,core)
    def z_hop(g,way,j,b): return remote(shard(g) if j==1 else place(g,b),place(g,b),azs.at[g,way,j-1],azr.at[g,way,j-1],up if way==0 else down)
    def x_hop(g,zz,own_): return remote(shard(g) if own_ else place(g,block(zz,x_)),place(g,block(zz,x_)),axs.at[g,zz],axr.at[g,zz],xp)
    def x_land(g,zz): return remote(place(g,block(zz,1-x_)),place(g,block(zz,1-x_)),axs.at[g,zz],axr.at[g,zz],xp)
    def c_hop(g,xx,zz,b,own_): return remote(shard(g) if own_ else place(g,b),place(g,b),acs.at[g,4*xx+zz],acr.at[g,4*xx+zz],sib)
    def gather_start(g):
        buf,c0,s0,nc=groups[g]
        @pl.when(z<3)
        def _(): z_hop(g,0,1,me).start()
        @pl.when(z>0)
        def _(): z_hop(g,1,1,me).start()
        x_hop(g,z,True).start()
        c_hop(g,0,z,me,True).start()
        buf[me,:,c0:c0+nc]=sh[:,s0:s0+nc]
    def gather_z(g,j):
        for way in (0,1):
            here=(z>=j) if way==0 else (z+j<=3)
            zz=jnp.maximum(z-j,0) if way==0 else jnp.minimum(z+j,3)
            @pl.when(here)
            def _():
                b=block(zz,x_)
                z_hop(g,way,j,b).wait_recv()
                x_hop(g,zz,False).start()
                c_hop(g,0,zz,b,False).start()
            if j<3:
                @pl.when(here & ((z<3) if way==0 else (z>0)))
                def _(): z_hop(g,way,j+1,block(zz,x_)).start()
    def gather_x(g):
        for zz in range(4):
            x_land(g,zz).wait_recv()
            c_hop(g,1,zz,block(zz,1-x_),False).start()
    def gather_done(g):
        for xx in (0,1):
            for zz in range(4):
                b=block(zz,x_)
                c_hop(g,xx,zz,b,False).wait_recv()
                c_hop(g,xx,zz,b,False).wait_send()
        for zz in range(4): x_land(g,zz).wait_send()
        for j in (1,2,3):
            @pl.when((z>=j-1) & (z<3))
            def _(): z_hop(g,0,j,me).wait_send()
            @pl.when((z+j-1<=3) & (z>0))
            def _(): z_hop(g,1,j,me).wait_send()
    own_copies=[local(tok.at[c*cr:(c+1)*cr],hall.at[rows(t,c)],1+c) for c in range(NC)]
    for c in own_copies: c.start()
    pl.semaphore_wait(barrier,len(everyone))
    gather_start(0); gather_start(1)
    def tok_copy(c): return remote(tok.at[loc(c)],hall.at[rows(t,c)],ts.at[c],tr.at[c],partner)
    def mine_o(rank): return sh.at[:,pl.ds(pl.multiple_of(n+rank*width,128),width)]
    o_swap=remote(mine_o(t),mine_o(t),ts.at[NC],tr.at[NC],partner)
    sh[:,pl.ds(pl.multiple_of(n+t*width,128),width)]=wos[...]
    o_swap.start()
    @pl.loop(0,NC)
    def _(c): tok_copy(c).start()
    sh[:,n+wide:n+wide+ff]=wu[...]
    sh[:,n+wide+ff:]=wds[...]
    for i,v in enumerate((v_ob,v_g1,v_b1,v_db,v_g2,v_b2)): vec[i:i+1]=row(v)
    upb[...]=row(v_ub)
    bias[...]=jnp.zeros_like(bias)
    bias[:,0:width]=row(v_qb); bias[:,2*width:]=row(v_vb)
    gather_z(0,1); gather_start(2)
    gather_z(1,1); gather_z(0,2)
    gather_z(2,1); o_swap.wait_recv(); gather_start(3)
    gather_z(1,2); gather_z(0,3); gather_z(2,2); gather_z(1,3)
    gather_x(0); gather_z(3,1); gather_z(2,3)
    gather_x(1); gather_z(3,2)
    gather_start(4)
    gather_x(2); gather_z(3,3); gather_z(4,1)
    for g in range(3): gather_done(g)
    for c in own_copies: c.wait()
    TF=512
    @pl.loop(0,NC)
    def _(c):
        tok_copy(c).wait_recv()
        @pl.loop(0,n//TF)
        def _(j):
            cs=pl.ds(pl.multiple_of(j*TF,TF),TF)
            qkv[chunk(c),cs]=(dot(hall[chunk(c)],strip(act,cs),NN)+bias[:,cs]).astype(BF)
        @pl.when(c==0)
        def _(): gather_z(4,2)
        @pl.when(c==1)
        def _():
            gather_x(3); gather_z(4,3)
        @pl.when(c==2)
        def _(): gather_start(5)
        @pl.when(c==3)
        def _():
            gather_z(5,1); gather_done(3)
    x_out=local(hall,x_hbm,5); w_out=local(act.at[:,:,0:n],wh_hbm,6)
    x_out.start(); w_out.start()
    ones=jnp.where(lax.broadcasted_iota(jnp.int32,(16,rows_all),0)==0,1.0,0.0).astype(BF)
    @pl.loop(0,pairs)
    def _(p):
        ck=pl.multiple_of(width+p*128,128); cv=pl.multiple_of(2*width+p*128,128)
        kt[p]=qkv[:,pl.ds(ck,128)].T
        v=qkv[:,pl.ds(cv,128)].T
        vt[2*p,0:64]=v[0:64]; vt[2*p,64:80]=ones
        vt[2*p+1,0:64]=v[64:128]; vt[2*p+1,64:80]=ones
    x_out.wait()
    def split(k,c):
        sbuf[k-1,loc(c)]=pch[half(1-t)].astype(BF)
        rs_copy(k,c).start()
        part[loc(c)]=pch[half(t)]
    def stats(v):
        cen=v-jnp.mean(v,axis=1,keepdims=True)
        r=lax.rsqrt(jnp.mean(cen*cen,axis=1,keepdims=True)+EPSILON)
        return cen*r,r
    def lo_copy(c): return pltpu.make_async_copy(cl.at[loc(c)],lo_hbm.at[loc(c)],losem.at[c])
    def out_copy(slot,col):
        return pltpu.make_async_copy(stage.at[slot],dw.at[:,:,:,:,pl.ds(pl.multiple_of(col,512),512)],osem.at[slot])
    def wgrad(slot,left,right_ref,rcol,ocol):
        @pl.loop(0,dm//256)
        def _(i):
            ms=pl.ds(pl.multiple_of(i*256,256),256)
            right=right_ref[:,pl.ds(pl.multiple_of(rcol,512),512)] if len(right_ref.shape)==2 else strip(right_ref,pl.ds(pl.multiple_of(rcol,512),512))
            stage[slot,i]=dot(left[ms],right,NN).astype(BF).reshape(2,2,64,512)
        out_copy(slot,ocol).start()
    def stage_a(c):
        rs=chunk(c)
        @pl.loop(0,pairs)
        def _(p):
            cq=pl.ds(pl.multiple_of(p*128,128),128); ck=pl.ds(pl.multiple_of(width+p*128,128),128)
            pks=[]
            for h in (0,1):
                keep=(lane<64) if h==0 else (lane>=64)
                q=jnp.where(keep,qkv[rs,cq]*scale,zero)
                st=dot(qkv[:,ck],q,NT)
                m=jnp.max(st,axis=0,keepdims=True)
                mc=m*LOG2E
                pt=jnp.exp2(st*LOG2E-mc).astype(BF)
                ot=dot(vt[2*p+h],pt,NN)
                tot=ot[64:65]
                ctt[h*64:(h+1)*64,:]=ot[0:64]*(1.0/tot)
                lse[pl.ds(2*p+h,1),rs]=mc+jnp.log2(tot)
                pks.append(jnp.max(m,axis=1,keepdims=True))
            early[10:11,cq]=jnp.maximum(early[10:11,cq],jnp.where(lane<64,pks[0],pks[1]))
            ctx[rs,cq]=ctt[...].T.astype(BF)
            step=c*pairs+p
            @pl.when(step==0)
            def _():
                gather_z(5,2)
            @pl.when(step==2)
            def _():
                gather_z(5,3)
                gather_start(6)
            @pl.when(step==4)
            def _():
                gather_z(6,1)
                gather_x(4)
            @pl.when(step==6)
            def _():
                gather_z(6,2)
                gather_start(7)
            @pl.when(step==8)
            def _():
                gather_z(6,3)
                gather_z(7,1)
            @pl.when(step==10)
            def _():
                gather_z(7,2)
                gather_x(5)
            @pl.when(step==12)
            def _():
                gather_z(7,3)
            @pl.when(step==14)
            def _():
                gather_x(6)
        ctx_copy(c,t).start()
        ctxo[loc(c),cols(t)]=ctx[rows(t,c)]
    def stage_b(c):
        ctx_copy(c,1-t).wait_recv()
        x,r=stats(hall[rows(t,c)].astype(F32)+dot(ctxo[loc(c)],whole(wo),NT)+vec[0:1])
        xh[loc(c)]=x
        rst[loc(c)]=jnp.broadcast_to(r,(cr,128))
        hall[rows(t,c)]=(x*vec[1:2]+vec[2:3]).astype(BF)
        ag_copy(3,hall,c,t).start()
    def stage_c(c):
        rs=chunk(c)
        ag_copy(3,hall,c,1-t).wait_recv()
        @pl.loop(0,ff//TF)
        def _(j):
            cs=pl.ds(pl.multiple_of(j*TF,TF),TF)
            u=dot(hall[rs],strip(wup,cs),NN)+upb[:,cs]
            cdf=0.5*(1.0+lax.erf(u*0.5**0.5))
            act[pl.ds(4*c,4),:,cs]=(u*cdf).astype(BF).reshape(4,64,TF)
            slp[rs,cs]=(cdf+u*jnp.exp(-0.5*u*u)*(0.5/math.pi)**0.5).astype(BF)
    def stage_c2(c):
        pch[...]=dot(act[pl.ds(4*c,4)].reshape(cg,ff),whole(wdn),NT)
        split(1,c)
    def stage_d(c):
        rs_copy(1,c).wait_recv()
        x,r=stats(xh[loc(c)]*vec[1:2]+vec[2:3]+part[loc(c)]+rbuf[0,loc(c)].astype(F32)+vec[3:4])
        dy=cl[loc(c)].astype(F32)
        cl[loc(c)]=(x*vec[4:5]+vec[5:6]).astype(BF)
        lo_copy(c).start()
        early[4:5]+=jnp.sum(dy*x,axis=0,keepdims=True)
        early[5:6]+=jnp.sum(dy,axis=0,keepdims=True)
        dx=dy*vec[4:5]
        g=r*(dx-jnp.mean(dx,axis=1,keepdims=True)-x*jnp.mean(dx*x,axis=1,keepdims=True))
        gf[loc(c)]=g
        gb=g.astype(BF)
        early[3:4]+=jnp.sum(gb.astype(F32),axis=0,keepdims=True)
        ball[rows(t,c)]=gb
        ag_copy(4,ball,c,t).start()
        tb[:,rows(t,c)]=gb.T
    def stage_e(c):
        rs=chunk(c)
        ag_copy(4,ball,c,1-t).wait_recv()
        @pl.loop(0,ff//TF)
        def _(j):
            cs=pl.ds(pl.multiple_of(j*TF,TF),TF)
            gu=(dot(ball[rs],strip(wdn,cs),NN)*slp[rs,cs].astype(F32)).astype(BF)
            slp[rs,cs]=gu
            row=pl.ds(8+j*TF//dm,1); cc=pl.ds(pl.multiple_of(j*TF%dm,TF),TF)
            early[row,cc]+=jnp.sum(gu.astype(F32),axis=0,keepdims=True)
        pch[...]=dot(slp[rs],whole(wup),NT)
        split(2,c)
        tb[:,rows(1-t,c)]=ball[rows(1-t,c)].T
        th[:,chunk(c)]=hall[chunk(c)].T
    def stage_f(c):
        rs_copy(2,c).wait_recv()
        dy=gf[loc(c)]+part[loc(c)]+rbuf[1,loc(c)].astype(F32)
        x=xh[loc(c)]; r=rst[loc(c)][:,0:1]
        early[1:2]+=jnp.sum(dy*x,axis=0,keepdims=True)
        early[2:3]+=jnp.sum(dy,axis=0,keepdims=True)
        dx=dy*vec[1:2]
        g=r*(dx-jnp.mean(dx,axis=1,keepdims=True)-x*jnp.mean(dx*x,axis=1,keepdims=True))
        gf[loc(c)]=g
        gb=g.astype(BF)
        early[0:1]+=jnp.sum(gb.astype(F32),axis=0,keepdims=True)
        ga[loc(c)]=gb
        ball[rows(t,c)]=gb
        dcs[loc(c)]=dot(gb,whole(wo),NN).astype(BF)
        dctx_copy(c,t).start()
        dcall[rows(t,c)]=dcs[loc(c),cols(t)]
    def stage_g(c):
        rs=chunk(c)
        dctx_copy(c,1-t).wait_recv()
        @pl.when(c==0)
        def _():
            for i in range(NC): ga_copy(i).start()
        @pl.loop(0,pairs)
        def _(p):
            cq=pl.ds(pl.multiple_of(p*128,128),128); ck=pl.ds(pl.multiple_of(width+p*128,128),128); cv=pl.ds(pl.multiple_of(2*width+p*128,128),128)
            prod=(ctx[rs,cq].astype(F32)*dcall[rs,cq].astype(F32)).T
            dl[0:1]=jnp.sum(prod[0:64],axis=0,keepdims=True)
            dl[1:2]=jnp.sum(prod[64:128],axis=0,keepdims=True)
            for h in (0,1):
                keep=(lane<64) if h==0 else (lane>=64)
                q=jnp.where(keep,qkv[rs,cq]*scale,zero)
                do=jnp.where(keep,dcall[rs,cq],zero)
                st=dot(qkv[:,ck],q,NT)
                pt=jnp.exp2(st*LOG2E-lse[pl.ds(2*p+h,1),rs])
                dpt=dot(qkv[:,cv],do,NT)
                ds=(pt*(dpt-dl[h:h+1])).astype(BF)
                dkv[1,:,cq]+=dot(pt.astype(BF),do,NN)
                dkv[0,:,cq]+=dot(ds,q,NN)
                dqt[h*64:(h+1)*64,:]=dot(kt[p,h*64:(h+1)*64,:],ds,NN)
            qkv[rs,cq]=(dqt[...].T*(HD**-0.5)).astype(BF)
            step=c*pairs+p
            @pl.when(step==0)
            def _():
                add3(0)
                add2(2)
                fetch2(3)
            @pl.when(step==1)
            def _():
                add2(3)
                ecopy(0).start()
            @pl.when(step==4)
            def _():
                eadd(0); ecopy(1).start()
            @pl.when(step==5)
            def _():
                s2(1).wait_send(); s2(2).start()
                fetch3(1)
            @pl.when(step==6)
            def _():
                eadd(1); ecopy(2).start()
            @pl.when(step==7)
            def _():
                sent3(0); add3(1)
            @pl.when(step==8)
            def _():
                eadd(2); ecopy(3).start()
            @pl.when(step==9)
            def _():
                fetchf(0)
            @pl.when(step==10)
            def _():
                finish(0)
                eadd(3); ecopy(4).start()
            @pl.when(step==11)
            def _():
                s2(2).wait_send(); s2(3).start()
                fetch3(2)
            @pl.when(step==12)
            def _():
                for i in range(NC): ga_copy(i).wait_recv()
                for i in range(NC): th[:,i*cg:(i+1)*cg]=ball[i*cg:(i+1)*cg].T
            @pl.when(step==13)
            def _():
                sent3(1); add3(2)
                wgrad(0,th,ctx,0,base[4])
            @pl.when(step==14)
            def _():
                out_copy(0,0).wait(); s1(4).start()
            @pl.when(step==15)
            def _():
                fetch2(4)
    def grad_down(c):
        slot=c%2
        wgrad(slot,tb,act,c*512,width+ff+c*512)
    def grad_up(c):
        slot=c%2
        wgrad(slot,th,slp,c*512,width+c*512)
    def ga_copy(c):
        return pltpu.make_async_remote_copy(ga.at[loc(c)],ball.at[rows(t,c)],ssem.at[7,c],rsem.at[7,c],device_id=partner,device_id_type=MESH)
    @pl.loop(0,NC)
    def _(c):
        stage_a(c)
        @pl.when(c>0)
        def _(): stage_b(c-1)
    cot_load.wait(); w_out.wait()
    gather_done(4); gather_done(5)
    @pl.loop(0,NC)
    def _(c):
        stage_c(c)
        @pl.when(c==0)
        def _(): stage_b(NC-1)
    gather_x(7)
    gather_done(6); gather_done(7)
    @pl.loop(0,NC)
    def _(c): stage_c2(c)
    @pl.loop(0,NC)
    def _(c): stage_d(c)
    @pl.loop(0,NC)
    def _(c): stage_e(c)
    piece=ff//2
    base=(width+ff,width+ff+piece,width,width+piece,0,width+2*ff,2*width+2*ff,3*width+2*ff)
    span=(piece,)*4+(width,)*4
    def s1(g): return remote(dw.at[:,:,1-core,:,base[g]:base[g]+span[g]],r1.at[g,:,:,:,0:span[g]],g1s.at[g],g1r.at[g],sib)
    slots2=[wup.at[8:12,:,0:piece],wup.at[12:16,:,0:piece],wup.at[8:12,:,piece:],wup.at[12:16,:,piece:],wup.at[0:4,:,piece:],wup.at[4:8,:,piece:]]
    slots3=[wdn.at[12:16,:,0:piece],wdn.at[12:16,:,piece:],wdn.at[0:4,:,piece:],wdn.at[4:8,:,piece:],wdn.at[8:12,:,piece:]]
    sum2=[slots2[g%6] for g in range(8)]
    sum3=[slots3[g%5] for g in range(8)]
    def s2(g): return remote(sum2[g].at[:,:,0:span[g]],r2.at[g,:,:,0:span[g]],g2s.at[g],g2r.at[g],xp)
    def s3(g,k): return remote(sum3[g].at[(z+k)%4,:,0:span[g]],r3.at[g,3-k,:,0:span[g]],g3s.at[g,k-1],g3r.at[g,k-1],zp[k-1])
    def load2(g): return [pltpu.make_async_copy(dw.at[:,1-x_,core,:,base[g]:base[g]+span[g]],wup.at[0:4,:,0:span[g]],rl.at[0]),
                          pltpu.make_async_copy(r1.at[g,:,1-x_,:,0:span[g]],wup.at[4:8,:,0:span[g]],rl.at[1])]
    def load3(g): return [pltpu.make_async_copy(dw.at[:,x_,core,:,base[g]:base[g]+span[g]],wdn.at[0:4,:,0:span[g]],rl.at[2]),
                         pltpu.make_async_copy(r1.at[g,:,x_,:,0:span[g]],wdn.at[4:8,:,0:span[g]],rl.at[3]),
                         pltpu.make_async_copy(r2.at[g,:,:,0:span[g]],wdn.at[8:12,:,0:span[g]],rl.at[4])]
    def fetch2(g):
        s1(g).wait_recv()
        for l in load2(g): l.start()
    def add2(g):
        for l in load2(g): l.wait()
        @pl.loop(0,4)
        def _(i): sum2[g][i,:,0:span[g]]=(wup[i,:,0:span[g]].astype(F32)+wup[4+i,:,0:span[g]].astype(F32)).astype(BF)
    def fetch3(g):
        s2(g).wait_recv()
        for l in load3(g): l.start()
    def add3(g):
        for l in load3(g): l.wait()
        @pl.loop(0,4)
        def _(i): sum3[g][i,:,0:span[g]]=(wdn[i,:,0:span[g]].astype(F32)+wdn[4+i,:,0:span[g]].astype(F32)+wdn[8+i,:,0:span[g]].astype(F32)).astype(BF)
        for k in (1,2,3): s3(g,k).start()
    def sent3(g):
        for k in (1,2,3): s3(g,k).wait_send()
    def fslot(g,i):
        r=64*(6*(g%2)+i)
        return tb.at[r:r+64,0:span[g]]
    def loadf(g): return [pltpu.make_async_copy(src,fslot(g,i),fl.at[g%2,i]) for i,src in enumerate(
        [dw.at[z,x_,core,:,base[g]:base[g]+span[g]],r1.at[g,z,x_,:,0:span[g]],r2.at[g,z,:,0:span[g]]]+[r3.at[g,k,:,0:span[g]] for k in range(3)])]
    def fetchf(g):
        for k in (1,2,3): s3(g,k).wait_recv()
        for l in loadf(g): l.start()
    def final(g):
        for l in loadf(g): l.wait()
        v=[fslot(g,i)[...].astype(F32) for i in range(6)]
        return v[0]+v[1]+v[2]+v[3]+v[4]+v[5]
    def fin_copy(g):
        return pltpu.make_async_copy(xh.at[64*g:64*g+64,0:span[g]],fin.at[g] if g<4 else go_hbm if g==4 else fin_head.at[g-5],fs.at[g])
    def finish(g):
        xh[64*g:64*g+64,0:span[g]]=final(g)
        fin_copy(g).start()
    zb=[dev(z+1-2*(z%2),x_,core),dev((z+2)%4,x_,core)]
    hops=[sib,xp,zb[0],zb[1],partner]
    def ecopy(i): return remote(eb.at[i],er.at[i],es.at[i],erc.at[i],hops[i])
    def eadd(i):
        ecopy(i).wait_recv()
        b=eb[i,8:16]; c=er[i,8:16]
        if i<4:
            r=lax.broadcasted_iota(jnp.int32,b.shape,0)
            b=jnp.where(r==2,jnp.maximum(b,c),b+c)
        eb[i+1,0:8]=eb[i,0:8]+er[i,0:8]; eb[i+1,8:16]=b
    def lcopy(i): return remote(lb.at[i],lr.at[i],ls.at[i],lrc.at[i],hops[i])
    def ladd(i):
        lcopy(i).wait_recv()
        lb[i+1]=lb[i]+lr[i]
    def drain():
        out_copy(0,0).wait()
        out_copy(1,0).wait()
    @pl.loop(0,NC)
    def _(c):
        ag_copy(3,hall,c,t).wait_send()
        ag_copy(4,ball,c,t).wait_send()
    x_in=pltpu.make_async_copy(x_hbm,hall,dsem.at[0])
    x_in.start()
    grad_down(0); grad_down(1)
    drain(); s1(0).start()
    grad_down(2); grad_down(3)
    drain(); s1(1).start()
    wh_in=pltpu.make_async_copy(wh_hbm,act.at[:,:,0:n],dsem.at[1])
    wh_in.start()
    fetch2(0)
    @pl.loop(0,NC)
    def _(c):
        stage_f(c)
        @pl.when(c==0)
        def _():
            add2(0); s2(0).start()
            fetch2(1)
        grad_up(c)
        @pl.when(c==1)
        def _():
            drain(); s1(2).start()
            add2(1)
        @pl.when(c==3)
        def _():
            drain(); s1(3).start()
            fetch2(2)
            s2(0).wait_send(); s2(1).start()
            fetch3(0)
    @pl.loop(0,NC)
    def _(c): stage_g(c)
    add2(4)
    s2(3).wait_send(); s2(4).start()
    fetch3(3)
    x_in.wait()
    @pl.loop(0,NC)
    def _(c): th[:,chunk(c)]=hall[chunk(c)].T
    wgrad(0,th,qkv,0,base[5])
    sent3(2); add3(3)
    out_copy(0,0).wait(); s1(5).start()
    fetchf(1)
    @pl.loop(0,pairs)
    def _(p):
        cq=pl.ds(pl.multiple_of(p*128,128),128); ck=pl.ds(pl.multiple_of(width+p*128,128),128); cv=pl.ds(pl.multiple_of(2*width+p*128,128),128)
        qkv[:,ck]=dkv[0,:,cq].astype(BF)
        qkv[:,cv]=dkv[1,:,cq].astype(BF)
    fetch2(5)
    def ycopy(c): return remote(sbuf.at[0,loc(c)],rbuf.at[0,loc(c)],ssem.at[6,c],rsem.at[6,c],partner)
    wh_in.wait()
    def token_grad(c):
        pch[...]=dot(qkv[chunk(c)],act[:,:,0:n].reshape(dm,n),NT)
        rs_copy(1,c).wait_send()
        sbuf[0,loc(c)]=pch[half(1-t)].astype(BF)
        ycopy(c).start()
        part[loc(c)]=pch[half(t)]
    @pl.loop(0,2)
    def _(c): token_grad(c)
    add2(5)
    s2(4).wait_send(); s2(5).start()
    wgrad(1,th,qkv,width,base[6])
    fetch3(4)
    out_copy(1,0).wait(); s1(6).start()
    wgrad(0,th,qkv,2*width,base[7])
    fetch2(6)
    out_copy(0,0).wait(); s1(7).start()
    @pl.loop(2,NC)
    def _(c): token_grad(c)
    add2(6)
    s2(5).wait_send(); s2(6).start()
    fetch2(7)
    sent3(3); add3(4)
    fetch3(5)
    lb[0,0:1,0:width]=jnp.sum(qkv[:,0:width].astype(F32),axis=0,keepdims=True)
    lb[0,0:1,width:2*width]=jnp.sum(qkv[:,2*width:].astype(F32),axis=0,keepdims=True)
    lcopy(0).start()
    finish(1)
    add2(7)
    eadd(4)
    sent3(4); add3(5)
    s2(6).wait_send(); s2(7).start()
    fetch3(6)
    ladd(0); lcopy(1).start()
    fetchf(2)
    smalls[...]=eb[5]
    pk=eb[4,10:11,0:width]
    head=lax.broadcasted_iota(jnp.int32,(1,width),1)//HD
    limit=jnp.zeros((1,width),F32)
    for h in range(width//HD): limit=jnp.where(head==h,lim[h],limit)
    sc=jnp.sqrt(limit/jnp.maximum(pk,limit))
    ctxo[0:64,0:width]=(wq[...].astype(F32)*sc).astype(BF)
    ctxo[64:128,0:width]=(wk[...].astype(F32)*sc).astype(BF)
    clips=[pltpu.make_async_copy(ctxo.at[0:64,0:width],qc_hbm,fs.at[8]),pltpu.make_async_copy(ctxo.at[64:128,0:width],kc_hbm,fs.at[9])]
    for c in clips: c.start()
    smalls[11:12,0:width]=row(v_qb)*sc
    finish(2)
    ladd(1); lcopy(2).start()
    fetchf(3)
    sent3(5); add3(6)
    fetch3(7)
    finish(3)
    fetchf(4)
    ladd(2); lcopy(3).start()
    @pl.loop(0,NC)
    def _(c): lo_copy(c).wait()
    finish(4)
    sent3(6); add3(7)
    fetchf(5)
    def tg_copy(c): return pltpu.make_async_copy(cl.at[loc(c)],tg_hbm.at[loc(c)],losem.at[c])
    @pl.loop(0,NC)
    def _(c):
        ycopy(c).wait_recv()
        cl[loc(c)]=(gf[loc(c)]+part[loc(c)]+rbuf[0,loc(c)].astype(F32)).astype(BF)
        tg_copy(c).start()
    ladd(3)
    smalls[12:13]=lb[4,0:1]
    finish(5)
    fetchf(6)
    finish(6)
    fetchf(7)
    finish(7)
    o_swap.wait_send()
    for g in range(8):
        s1(g).wait_send()
        fin_copy(g).wait()
    s2(7).wait_send()
    sent3(7)
    for c in clips: c.wait()
    for i in range(5): ecopy(i).wait_send()
    for i in range(4): lcopy(i).wait_send()
    @pl.loop(0,NC)
    def _(c):
        tg_copy(c).wait()
        ctx_copy(c,t).wait_send(); dctx_copy(c,t).wait_send(); tok_copy(c).wait_send()
        rs_copy(2,c).wait_send(); ycopy(c).wait_send()
        ga_copy(c).wait_send()

def main_call(shards,tok,cot,vectors,lim,cid):
    V=pl.BlockSpec(memory_space=pltpu.VMEM); A=pl.BlockSpec(memory_space=pl.ANY)
    width=shards[0].shape[1]; ff=shards[4].shape[1]; own,dm=tok.shape; rows=2*own; n=3*width; cr=own//NC; wide=2*width; piece=ff//2
    S=jax.ShapeDtypeStruct; M=pltpu.VMEM; D=pltpu.SemaphoreType.DMA
    return pl.pallas_call(main_kernel,
      out_shape=(S((own,dm),BF),S((own,dm),BF),S((4,64,piece),F32),S((3,64,width),F32),S((64,width),F32),S((64,width),BF),S((64,width),BF),S((16,dm),F32),
        S((4,2,2,64,width+2*ff+n),BF),S((8,4,2,64,piece),BF),S((8,4,64,piece),BF),S((8,3,64,piece),BF),S((rows,dm),BF),S((16,64,n),BF)),
      in_specs=[V]*6+[A,A]+[V]*9+[pl.BlockSpec(memory_space=pltpu.SMEM)],out_specs=(A,)*7+(V,)+(A,)*6,
      scratch_shapes=[M((1,n),F32),M((8,dm),F32),M((1,ff),F32),M((own,dm),F32),M((6,16,dm),F32),M((5,16,dm),F32),M((5,8,dm),F32),M((4,8,dm),F32),
        M((64,n+wide+2*ff),BF),M((rows,n),BF),M((width//HD,80,rows),BF),M((width//128,128,rows),BF),M((rows,width),BF),M((own,wide),BF),M((width//HD,rows),F32),M((own,dm),BF),
        M((16,64,wide),BF),M((16,64,ff),BF),M((16,64,ff),BF),
        M((own,dm),F32),M((own,128),F32),
        M((rows,dm),BF),M((16,64,ff),BF),M((rows,ff),BF),M((rows,dm),BF),M((own,dm),BF),M((own,wide),BF),M((rows,width),BF),
        M((own,dm),F32),M((2*cr,dm),F32),M((128,2*cr),F32),M((128,2*cr),F32),M((8,2*cr),F32),M((2,rows,width),F32),
        M((2,own,dm),BF),M((2,own,dm),BF),
        M((dm,rows),BF),M((dm,rows),BF),M((2,4,2,2,64,512),BF),
        D((7,)),D((NC,)),D((2,)),D((2,)),D((8,NC)),D((8,NC)),D((5,)),D((8,)),D((8,)),D((8,)),D((8,)),D((8,3)),D((8,3)),
        D((NC+1,)),D((NC+1,)),D((8,2,3)),D((8,2,3)),D((8,4)),D((8,4)),D((8,8)),D((8,8)),
        D((5,)),D((5,)),D((4,)),D((4,)),D((2,6)),D((10,))],
      compiler_params=pltpu.CompilerParams(collective_id=cid,has_side_effects=True,vmem_limit_bytes=61*2**20),
      name="main")(*shards,tok,cot,*vectors,lim)

def finish_kernel(lo,tg,fin,fin_head,go,qc,kc,smalls,
                  lo_,tg_,gq_,gk_,gv_,go_,gu_,gd_,qc_,kc_,qb_,vb_,ob_,g1_,b1_,ub_,db_,g2_,b2_,pk_,qbc_,h_lo,h_tg,h_fin,h_head,h_go,h_qc,h_kc,isem,sem):
    piece=fin.shape[2]
    ins=[pltpu.make_async_copy(a,b,isem.at[i]) for i,(a,b) in enumerate(((lo,h_lo),(tg,h_tg),(fin,h_fin),(fin_head,h_head),(go,h_go),(qc,h_qc),(kc,h_kc)))]
    outs=[[(h_lo,lo_)],[(h_tg,tg_)],[(h_fin.at[0],gd_.at[:,0:piece]),(h_fin.at[1],gd_.at[:,piece:]),(h_fin.at[2],gu_.at[:,0:piece]),(h_fin.at[3],gu_.at[:,piece:])],
          [(h_head.at[0],gq_),(h_head.at[1],gk_),(h_head.at[2],gv_)],[(h_go,go_)],[(h_qc,qc_)],[(h_kc,kc_)]]
    for c in ins: c.start()
    width=qb_.shape[0]; dm=ob_.shape[0]
    def line(v): return v.reshape(v.shape[1])
    qb_[...]=line(smalls[12:13,0:width]); vb_[...]=line(smalls[12:13,width:2*width])
    for i,o in enumerate((ob_,g1_,b1_,db_,g2_,b2_)): o[...]=line(smalls[i:i+1])
    ub_[0:dm]=line(smalls[8:9]); ub_[dm:2*dm]=line(smalls[9:10])
    for h in range(pk_.shape[0]): pk_[h]=jnp.max(smalls[10:11,h*HD:(h+1)*HD])
    qbc_[...]=line(smalls[11:12,0:width]).astype(BF)
    moved=[]
    for a,group in zip(ins,outs):
        a.wait()
        for src,dst in group:
            c=pltpu.make_async_copy(src,dst,sem.at[len(moved)])
            c.start()
            moved.append(c)
    for c in moved: c.wait()

def finish_call(big,smalls,heads):
    V=pl.BlockSpec(memory_space=pltpu.VMEM); A=pl.BlockSpec(memory_space=pl.ANY); S=jax.ShapeDtypeStruct
    lo,tg,fin,fin_head,go,qc,kc=big
    width=go.shape[1]; piece=fin.shape[2]; ff=2*piece; dm=tg.shape[1]
    return pl.pallas_call(finish_kernel,
      out_shape=(S(lo.shape,BF),S(tg.shape,BF))+(S((64,width),F32),)*4+(S((64,ff),F32),)*2+(S((64,width),BF),)*2
        +tuple(S((k,),F32) for k in (width,width,dm,dm,dm,ff,dm,dm,dm,heads))+(S((width,),BF),),
      in_specs=[A]*7+[V],out_specs=(A,)*10+(V,)*9+(pl.BlockSpec(memory_space=pltpu.SMEM),V),
      scratch_shapes=[pltpu.VMEM(a.shape,a.dtype) for a in big]+[pltpu.SemaphoreType.DMA((7,)),pltpu.SemaphoreType.DMA((12,))],
      compiler_params=pltpu.CompilerParams(vmem_limit_bytes=61*2**20),name="finish")(*big,smalls)

def per_device_pair(tokens,query_weight,query_bias,key_weight,value_weight,value_bias,out_weight,out_bias,first_gain,first_shift,
    up_weight,up_bias,down_weight,down_bias,second_gain,second_shift,cotangent,clip_limit):
    shards=(query_weight,key_weight,value_weight,out_weight.T,up_weight,down_weight.T)
    vectors=(out_bias,first_gain,first_shift,down_bias,second_gain,second_shift,up_bias,query_bias,value_bias)
    res=main_call(shards,tokens,cotangent,vectors,clip_limit,1)
    lo,tg,gq,gk,gv,go,gu,gd,qc,kc,qb,vb,ob,g1,b1,ub,db,g2,b2,pk,qbc=finish_call(res[:7],res[7],clip_limit.shape[0])
    return (lo,tg,gq,qb,gk,gv,vb,go.T,ob,g1,b1,gu,ub,gd.T,db,g2,b2,pk,qc,qbc,kc)


def layer(*args):
    paired = lax.axis_size("dp") == 16 and lax.axis_size("tensor") == 2 and 2 * args[0].shape[0] == LEN
    return per_device_pair(*args) if paired else per_device(*args)


def solution(mesh):
    in_specs = (
        P(("dp", "tensor"), None),
        P("dp", "tensor"),
        P("tensor"),
        P("dp", "tensor"),
        P("dp", "tensor"),
        P("tensor"),
        P("tensor", "dp"),
        P(),
        P(),
        P(),
        P("dp", "tensor"),
        P("tensor"),
        P("tensor", "dp"),
        P(),
        P(),
        P(),
        P(("dp", "tensor"), None),
        P("tensor"),
    )
    out_specs = (
        P(("dp", "tensor"), None),
        P(("dp", "tensor"), None),
        P("dp", "tensor"),
        P("tensor"),
        P("dp", "tensor"),
        P("dp", "tensor"),
        P("tensor"),
        P("tensor", "dp"),
        P(),
        P(),
        P(),
        P("dp", "tensor"),
        P("tensor"),
        P("tensor", "dp"),
        P(),
        P(),
        P(),
        P("tensor"),
        P("dp", "tensor"),
        P("tensor"),
        P("dp", "tensor"),
    )
    return jax.shard_map(
        layer, mesh=mesh, in_specs=in_specs, out_specs=out_specs, check_vma=False
    )
```

```python
import functools
import math

import jax
import jax.numpy as jnp
from jax import lax
from jax.experimental import pallas as pl
from jax.experimental.pallas import tpu as pltpu
from jax.sharding import PartitionSpec as P

HD = 64
LEN = 1024
QB = 512


def layer_norm(values, gain, shift):
    center = values - jnp.mean(values, axis=-1, keepdims=True)
    spread = jnp.mean(center * center, axis=-1, keepdims=True)
    return center * lax.rsqrt(spread + EPSILON) * gain + shift


def gelu_slope(upper):
    normal_cdf = 0.5 * (1.0 + lax.erf(upper * 0.5**0.5))
    return normal_cdf + upper * jnp.exp(-0.5 * upper * upper) * (0.5 / math.pi) ** 0.5


def contract_rows(left, right):
    return lax.dot_general(
        left, right, (((0,), (0,)), ((), ())), preferred_element_type=jnp.float32
    )


def contract_cols(left, right):
    return lax.dot_general(
        left, right, (((1,), (1,)), ((), ())), preferred_element_type=jnp.float32
    )


def per_device(
    tokens,
    query_weight,
    query_bias,
    key_weight,
    value_weight,
    value_bias,
    out_weight,
    out_bias,
    first_gain,
    first_shift,
    up_weight,
    up_bias,
    down_weight,
    down_bias,
    second_gain,
    second_shift,
    cotangent,
    clip_limit,
):
    query_full, key_full, value_full, out_full, up_full, down_full = (
        lax.all_gather(query_weight, "dp", axis=0, tiled=True),
        lax.all_gather(key_weight, "dp", axis=0, tiled=True),
        lax.all_gather(value_weight, "dp", axis=0, tiled=True),
        lax.all_gather(out_weight, "dp", axis=1, tiled=True),
        lax.all_gather(up_weight, "dp", axis=0, tiled=True),
        lax.all_gather(down_weight, "dp", axis=1, tiled=True),
    )
    width = query_full.shape[1]
    hidden_width = up_full.shape[1]
    heads_here = width // HD
    score_scale = HD ** (-0.5)
    joint_weight = jnp.concatenate([query_full, key_full, value_full], axis=1)
    gathered = lax.all_gather(tokens, "tensor", axis=0, tiled=True)
    group_rows = gathered.shape[0]
    seq_count = group_rows // LEN
    block_count = LEN // QB
    projected = jnp.dot(gathered, joint_weight, preferred_element_type=jnp.float32)
    queries = (projected[:, :width] + query_bias.astype(jnp.float32)).astype(jnp.bfloat16)
    keyset = projected[:, width : 2 * width].astype(jnp.bfloat16)
    valset = (projected[:, 2 * width :] + value_bias.astype(jnp.float32)).astype(jnp.bfloat16)
    query_seq = queries.reshape(seq_count, LEN, heads_here, HD)
    key_seq = keyset.reshape(seq_count, LEN, heads_here, HD)
    value_seq = valset.reshape(seq_count, LEN, heads_here, HD)

    def attend_block(block_id):
        seq_id = block_id // block_count
        row_start = block_id % block_count * QB
        query_rows = lax.dynamic_slice_in_dim(
            lax.dynamic_index_in_dim(query_seq, seq_id, 0, False), row_start, QB, 0
        )
        key_rows = lax.dynamic_index_in_dim(key_seq, seq_id, 0, False)
        value_rows = lax.dynamic_index_in_dim(value_seq, seq_id, 0, False)
        logits = (
            jnp.einsum("qhd,khd->hqk", query_rows, key_rows, preferred_element_type=jnp.float32)
            * score_scale
        )
        row_max = jnp.max(logits, axis=2, keepdims=True)
        exponent = jnp.exp(logits - row_max)
        totals = jnp.sum(exponent, axis=2, keepdims=True)
        probs_low = (exponent / totals).astype(jnp.bfloat16)
        context_rows = jnp.einsum(
            "hqk,khd->qhd", probs_low, value_rows, preferred_element_type=jnp.float32
        )
        return (
            context_rows.reshape(QB, width).astype(jnp.bfloat16),
            (row_max + jnp.log(totals))[:, :, 0],
            jnp.max(row_max, axis=(1, 2)),
        )

    context_blocks, log_totals, block_peaks = lax.map(
        attend_block, jnp.arange(seq_count * block_count)
    )
    context = context_blocks.reshape(group_rows, width)
    logit_peak = lax.pmax(jnp.max(block_peaks, axis=0), "dp")
    attention = lax.psum_scatter(
        jnp.dot(context, out_full, preferred_element_type=jnp.float32).astype(jnp.bfloat16),
        "tensor",
        scatter_dimension=0,
        tiled=True,
    ).astype(jnp.float32) + out_bias.astype(jnp.float32)
    first_resid = tokens.astype(jnp.float32) + attention
    hidden, first_pull = jax.vjp(
        layer_norm, first_resid, first_gain.astype(jnp.float32), first_shift.astype(jnp.float32)
    )
    hidden_all = lax.all_gather(hidden.astype(jnp.bfloat16), "tensor", axis=0, tiled=True)
    upper = jnp.dot(hidden_all, up_full, preferred_element_type=jnp.float32) + up_bias.astype(
        jnp.float32
    )
    acted = jax.nn.gelu(upper, approximate=False).astype(jnp.bfloat16)
    branch = lax.psum_scatter(
        jnp.dot(acted, down_full, preferred_element_type=jnp.float32).astype(jnp.bfloat16),
        "tensor",
        scatter_dimension=0,
        tiled=True,
    ).astype(jnp.float32) + down_bias.astype(jnp.float32)
    normed, second_pull = jax.vjp(
        layer_norm,
        hidden + branch,
        second_gain.astype(jnp.float32),
        second_shift.astype(jnp.float32),
    )
    layer_out = normed.astype(jnp.bfloat16)
    grad_second, second_gain_grad, second_shift_grad = second_pull(cotangent.astype(jnp.float32))
    grad_branch = grad_second.astype(jnp.bfloat16)
    down_bias_grad = jnp.sum(grad_branch, axis=0, dtype=jnp.float32)
    branch_all = lax.all_gather(grad_branch, "tensor", axis=0, tiled=True)
    grad_acted = contract_cols(branch_all, down_full)
    down_weight_grad = contract_rows(acted, branch_all)
    grad_upper = (grad_acted * gelu_slope(upper)).astype(jnp.bfloat16)
    up_bias_grad = jnp.sum(grad_upper, axis=0, dtype=jnp.float32)
    up_weight_grad = contract_rows(hidden_all, grad_upper)
    grad_hidden = grad_second + lax.psum_scatter(
        contract_cols(grad_upper, up_full).astype(jnp.bfloat16),
        "tensor",
        scatter_dimension=0,
        tiled=True,
    ).astype(jnp.float32)
    grad_first, first_gain_grad, first_shift_grad = first_pull(grad_hidden)
    grad_attn = grad_first.astype(jnp.bfloat16)
    out_bias_grad = jnp.sum(grad_attn, axis=0, dtype=jnp.float32)
    attn_all = lax.all_gather(grad_attn, "tensor", axis=0, tiled=True)
    grad_context = contract_cols(attn_all, out_full).astype(jnp.bfloat16)
    out_weight_grad = contract_rows(context, attn_all)
    query_blocks = queries.reshape(seq_count, block_count, QB, heads_here, HD)
    grad_blocks = grad_context.reshape(seq_count, block_count, QB, heads_here, HD)
    log_blocks = log_totals.reshape(seq_count, block_count, heads_here, QB)

    def sequence_back(item):
        query_part, grad_part, log_part, key_rows, value_rows = item

        def block_back(carry, piece):
            key_acc, value_acc = carry
            query_rows, grad_rows, log_rows = piece
            logits = (
                jnp.einsum("qhd,khd->hqk", query_rows, key_rows, preferred_element_type=jnp.float32)
                * score_scale
            )
            probs = jnp.exp(logits - log_rows[:, :, None])
            probs_low = probs.astype(jnp.bfloat16)
            value_acc = value_acc + jnp.einsum(
                "hqk,qhd->khd", probs_low, grad_rows, preferred_element_type=jnp.float32
            )
            grad_probs = jnp.einsum(
                "qhd,khd->hqk", grad_rows, value_rows, preferred_element_type=jnp.float32
            )
            inner = jnp.sum(probs * grad_probs, axis=2, keepdims=True)
            grad_logits = (probs * (grad_probs - inner)).astype(jnp.bfloat16)
            grad_query = (
                jnp.einsum(
                    "hqk,khd->qhd", grad_logits, key_rows, preferred_element_type=jnp.float32
                )
                * score_scale
            )
            key_acc = (
                key_acc
                + jnp.einsum(
                    "hqk,qhd->khd", grad_logits, query_rows, preferred_element_type=jnp.float32
                )
                * score_scale
            )
            return ((key_acc, value_acc), grad_query.astype(jnp.bfloat16))

        empty = jnp.zeros((LEN, heads_here, HD), jnp.float32)
        (key_acc, value_acc), grad_query_rows = lax.scan(
            block_back, (empty, empty), (query_part, grad_part, log_part)
        )
        return (grad_query_rows, key_acc.astype(jnp.bfloat16), value_acc.astype(jnp.bfloat16))

    grad_queries_all, grad_keys_all, grad_values_all = lax.map(
        sequence_back, (query_blocks, grad_blocks, log_blocks, key_seq, value_seq)
    )
    grad_joint = jnp.concatenate(
        [
            grad_queries_all.reshape(group_rows, width),
            grad_keys_all.reshape(group_rows, width),
            grad_values_all.reshape(group_rows, width),
        ],
        axis=1,
    )
    joint_grad = contract_rows(gathered, grad_joint)
    query_weight_grad = joint_grad[:, :width]
    key_weight_grad = joint_grad[:, width : 2 * width]
    value_weight_grad = joint_grad[:, 2 * width :]
    query_bias_grad = jnp.sum(grad_joint[:, :width], axis=0, dtype=jnp.float32)
    value_bias_grad = jnp.sum(grad_joint[:, 2 * width :], axis=0, dtype=jnp.float32)
    tokens_grad = (
        grad_first
        + lax.psum_scatter(
            contract_cols(grad_joint, joint_weight).astype(jnp.bfloat16),
            "tensor",
            scatter_dimension=0,
            tiled=True,
        ).astype(jnp.float32)
    ).astype(jnp.bfloat16)
    (
        query_weight_grad,
        key_weight_grad,
        value_weight_grad,
        out_weight_grad,
        up_weight_grad,
        down_weight_grad,
    ) = (
        lax.psum_scatter(
            query_weight_grad.astype(jnp.bfloat16), "dp", scatter_dimension=0, tiled=True
        ).astype(jnp.float32),
        lax.psum_scatter(
            key_weight_grad.astype(jnp.bfloat16), "dp", scatter_dimension=0, tiled=True
        ).astype(jnp.float32),
        lax.psum_scatter(
            value_weight_grad.astype(jnp.bfloat16), "dp", scatter_dimension=0, tiled=True
        ).astype(jnp.float32),
        lax.psum_scatter(
            out_weight_grad.astype(jnp.bfloat16), "dp", scatter_dimension=1, tiled=True
        ).astype(jnp.float32),
        lax.psum_scatter(
            up_weight_grad.astype(jnp.bfloat16), "dp", scatter_dimension=0, tiled=True
        ).astype(jnp.float32),
        lax.psum_scatter(
            down_weight_grad.astype(jnp.bfloat16), "dp", scatter_dimension=1, tiled=True
        ).astype(jnp.float32),
    )
    tensor_place = lax.axis_index("tensor")
    model_width = out_bias.shape[0]
    query_spread = lax.dynamic_update_slice_in_dim(
        jnp.zeros((model_width,), jnp.float32), query_bias_grad, tensor_place * width, 0
    )
    value_spread = lax.dynamic_update_slice_in_dim(
        jnp.zeros((model_width,), jnp.float32), value_bias_grad, tensor_place * width, 0
    )
    up_spread = lax.dynamic_update_slice_in_dim(
        jnp.zeros((hidden_width * lax.axis_size("tensor"),), jnp.float32),
        up_bias_grad,
        tensor_place * hidden_width,
        0,
    )
    (
        query_spread,
        value_spread,
        up_spread,
        out_bias_grad,
        down_bias_grad,
        first_gain_grad,
        first_shift_grad,
        second_gain_grad,
        second_shift_grad,
    ) = lax.psum(
        (
            query_spread,
            value_spread,
            up_spread,
            out_bias_grad,
            down_bias_grad,
            first_gain_grad,
            first_shift_grad,
            second_gain_grad,
            second_shift_grad,
        ),
        ("dp", "tensor"),
    )
    query_bias_grad = lax.dynamic_slice_in_dim(query_spread, tensor_place * width, width, 0)
    value_bias_grad = lax.dynamic_slice_in_dim(value_spread, tensor_place * width, width, 0)
    up_bias_grad = lax.dynamic_slice_in_dim(up_spread, tensor_place * hidden_width, hidden_width, 0)
    factor = clip_limit / jnp.maximum(logit_peak, clip_limit)
    column_scale = jnp.repeat(jnp.sqrt(factor), HD)
    query_clipped = (query_weight.astype(jnp.float32) * column_scale).astype(jnp.bfloat16)
    query_bias_clipped = (query_bias.astype(jnp.float32) * column_scale).astype(jnp.bfloat16)
    key_clipped = (key_weight.astype(jnp.float32) * column_scale).astype(jnp.bfloat16)
    return (
        layer_out,
        tokens_grad,
        query_weight_grad,
        query_bias_grad,
        key_weight_grad,
        value_weight_grad,
        value_bias_grad,
        out_weight_grad,
        out_bias_grad,
        first_gain_grad,
        first_shift_grad,
        up_weight_grad,
        up_bias_grad,
        down_weight_grad,
        down_bias_grad,
        second_gain_grad,
        second_shift_grad,
        logit_peak,
        query_clipped,
        query_bias_clipped,
        key_clipped,
    )


LOG2E=1.4426950408889634
NT=(((1,),(1,)),((),()))
NN=(((1,),(0,)),((),()))
F32=jnp.float32
BF=jnp.bfloat16
MESH=pl.DeviceIdType.MESH
EPSILON=1e-5
NC=4


def dot(a,b,dims):
    return lax.dot_general(a,b,dims,preferred_element_type=jnp.float32)


def greet(partner):
    barrier=pltpu.get_barrier_semaphore()
    pl.semaphore_signal(barrier,inc=1,device_id=partner,device_id_type=MESH)
    pl.semaphore_wait(barrier,1)


def main_kernel(wq,wk,wv,wos,wu,wds,tok,cot_hbm,v_ob,v_g1,v_b1,v_db,v_g2,v_b2,v_ub,v_qb,v_vb,lim,
               lo_hbm,tg_hbm,fin,fin_head,go_hbm,qc_hbm,kc_hbm,smalls,dw,r1,r2,r3,x_hbm,wh_hbm,
               bias,vec,upb,gf,eb,er,lb,lr,sh,qkv,vt,kt,ctx,ctxo,lse,cl,wo,wup,wdn,xh,rst,hall,act,slp,ball,ga,dcs,dcall,part,pch,ctt,dqt,dl,dkv,sbuf,rbuf,tb,th,stage,
               lsem,losem,dsem,osem,ssem,rsem,rl,g1s,g1r,g2s,g2r,g3s,g3r,ts,tr,azs,azr,bzs,bzr,axs,axr,acs,acr,es,erc,ls,lrc,fl,fs):
    d=lax.axis_index("dp"); t=lax.axis_index("tensor")
    partner=(d,1-t)
    core=d%2; x_=(d//2)%2; z=d//4
    def dev(z_,xx,c_): return ((z_*2+xx)*2+c_,t)
    sib=dev(z,x_,1-core); xp=dev(z,1-x_,core); zp=[dev((z+k)%4,x_,core) for k in (1,2,3)]
    own,dm=tok.shape; cr=own//NC; cg=2*cr; rows_all=2*own; width=ctx.shape[1]; ff=wup.shape[2]; wide=wo.shape[2]; pairs=width//128
    def local(src,dst,i): return pltpu.make_async_copy(src,dst,lsem.at[i])
    def remote(src,dst,a,b,p): return pltpu.make_async_remote_copy(src,dst,a,b,device_id=p,device_id_type=MESH)
    cot_load=local(cot_hbm,cl,0)
    cot_load.start()
    barrier=pltpu.get_barrier_semaphore()
    n=3*width
    def row(v): return v[...].astype(F32).reshape(1,v.shape[0])
    sh[:,0:width]=wq[...]; sh[:,width:2*width]=wk[...]; sh[:,2*width:n]=wv[...]
    everyone=[partner,sib,xp]+zp
    for p in everyone: pl.semaphore_signal(barrier,inc=1,device_id=p,device_id_type=MESH)
    def chunk(c): return pl.ds(pl.multiple_of(c*cg,cg),cg)
    def rows(rank,c): return pl.ds(pl.multiple_of(c*cg+rank*cr,cr),cr)
    def half(rank): return pl.ds(pl.multiple_of(rank*cr,cr),cr)
    def loc(c): return pl.ds(pl.multiple_of(c*cr,cr),cr)
    def rs_copy(k,c):
        return pltpu.make_async_remote_copy(sbuf.at[k-1,loc(c)],rbuf.at[k-1,loc(c)],ssem.at[k,c],rsem.at[k,c],device_id=partner,device_id_type=MESH)
    def ag_copy(k,buf,c,rank):
        return pltpu.make_async_remote_copy(buf.at[rows(rank,c)],buf.at[rows(rank,c)],ssem.at[k,c],rsem.at[k,c],device_id=partner,device_id_type=MESH)
    def cols(rank): return pl.ds(pl.multiple_of(rank*width,128),width)
    def ctx_copy(c,rank):
        return pltpu.make_async_remote_copy(ctx.at[rows(1-rank,c)],ctxo.at[loc(c),cols(rank)],ssem.at[0,c],rsem.at[0,c],device_id=partner,device_id_type=MESH)
    def dctx_copy(c,rank):
        return pltpu.make_async_remote_copy(dcs.at[loc(c),cols(1-rank)],dcall.at[rows(rank,c)],ssem.at[5,c],rsem.at[5,c],device_id=partner,device_id_type=MESH)
    early=eb.at[0]
    early[...]=jnp.zeros((16,dm),F32)
    early[10:11]=jnp.full((1,dm),-jnp.inf,F32)
    lb[0]=jnp.zeros((8,dm),F32)
    def whole(w): return w[...].reshape(dm,w.shape[2])
    def strip(w,cs): return w[:,:,cs].reshape(dm,TF)
    dkv[...]=jnp.zeros_like(dkv)
    lane=lax.broadcasted_iota(jnp.int32,(1,128),1)
    scale=jnp.bfloat16(HD**-0.5); zero=jnp.bfloat16(0)
    q4=ff//2
    groups=[(act,0,0,width),(act,width,width,width),(act,2*width,2*width,width),(wo,0,n,wide),
            (wup,0,n+wide,q4),(wup,q4,n+wide+q4,q4),(wdn,0,n+wide+ff,q4),(wdn,q4,n+wide+ff+q4,q4)]
    def block(z_,xx): return (z_*2+xx)*2+core
    me=block(z,x_)
    def place(g,b):
        buf,c0,_,nc=groups[g]
        return buf.at[b,:,c0:c0+nc]
    def shard(g): return sh.at[:,groups[g][2]:groups[g][2]+groups[g][3]]
    up=dev(jnp.minimum(z+1,3),x_,core); down=dev(jnp.maximum(z-1,0),x_,core)
    def z_hop(g,way,j,b): return remote(shard(g) if j==1 else place(g,b),place(g,b),azs.at[g,way,j-1],azr.at[g,way,j-1],up if way==0 else down)
    def x_hop(g,zz,own_): return remote(shard(g) if own_ else place(g,block(zz,x_)),place(g,block(zz,x_)),axs.at[g,zz],axr.at[g,zz],xp)
    def x_land(g,zz): return remote(place(g,block(zz,1-x_)),place(g,block(zz,1-x_)),axs.at[g,zz],axr.at[g,zz],xp)
    def c_hop(g,xx,zz,b,own_): return remote(shard(g) if own_ else place(g,b),place(g,b),acs.at[g,4*xx+zz],acr.at[g,4*xx+zz],sib)
    def gather_start(g):
        buf,c0,s0,nc=groups[g]
        @pl.when(z<3)
        def _(): z_hop(g,0,1,me).start()
        @pl.when(z>0)
        def _(): z_hop(g,1,1,me).start()
        x_hop(g,z,True).start()
        c_hop(g,0,z,me,True).start()
        buf[me,:,c0:c0+nc]=sh[:,s0:s0+nc]
    last=7
    def z_other(way,j,b): return remote(place(last,b),place(last,b),bzs.at[way,j-1],bzr.at[way,j-1],up if way==0 else down)
    def gather_cross():
        b=block(z,1-x_)
        x_land(last,z).wait_recv()
        @pl.when(z<3)
        def _(): z_other(0,1,b).start()
        @pl.when(z>0)
        def _(): z_other(1,1,b).start()
        c_hop(last,1,z,b,False).start()
    def gather_z(g,j):
        for way in (0,1):
            here=(z>=j) if way==0 else (z+j<=3)
            zz=jnp.maximum(z-j,0) if way==0 else jnp.minimum(z+j,3)
            b=block(zz,x_); b2=block(zz,1-x_)
            onward=here & ((z<3) if way==0 else (z>0))
            @pl.when(here)
            def _():
                z_hop(g,way,j,b).wait_recv()
                if g!=last: x_hop(g,zz,False).start()
                c_hop(g,0,zz,b,False).start()
                if g==last:
                    z_other(way,j,b2).wait_recv()
                    c_hop(g,1,zz,b2,False).start()
            if j<3:
                @pl.when(onward)
                def _():
                    z_hop(g,way,j+1,b).start()
                    if g==last: z_other(way,j+1,b2).start()
    def gather_x(g):
        for zz in range(4):
            x_land(g,zz).wait_recv()
            c_hop(g,1,zz,block(zz,1-x_),False).start()
    def gather_done(g):
        for xx in (0,1):
            for zz in range(4):
                b=block(zz,x_)
                c_hop(g,xx,zz,b,False).wait_recv()
                c_hop(g,xx,zz,b,False).wait_send()
        if g==last: x_land(g,z).wait_send()
        else:
            for zz in range(4): x_land(g,zz).wait_send()
        for j in (1,2,3):
            @pl.when((z>=j-1) & (z<3))
            def _():
                z_hop(g,0,j,me).wait_send()
                if g==last: z_other(0,j,me).wait_send()
            @pl.when((z+j-1<=3) & (z>0))
            def _():
                z_hop(g,1,j,me).wait_send()
                if g==last: z_other(1,j,me).wait_send()
    own_copies=[local(tok.at[c*cr:(c+1)*cr],hall.at[rows(t,c)],1+c) for c in range(NC)]
    for c in own_copies: c.start()
    pl.semaphore_wait(barrier,len(everyone))
    gather_start(0); gather_start(1)
    def tok_copy(c): return remote(tok.at[loc(c)],hall.at[rows(t,c)],ts.at[c],tr.at[c],partner)
    def mine_o(rank): return sh.at[:,pl.ds(pl.multiple_of(n+rank*width,128),width)]
    o_swap=remote(mine_o(t),mine_o(t),ts.at[NC],tr.at[NC],partner)
    sh[:,pl.ds(pl.multiple_of(n+t*width,128),width)]=wos[...]
    o_swap.start()
    @pl.loop(0,NC)
    def _(c): tok_copy(c).start()
    sh[:,n+wide:n+wide+ff]=wu[...]
    sh[:,n+wide+ff:]=wds[...]
    for i,v in enumerate((v_ob,v_g1,v_b1,v_db,v_g2,v_b2)): vec[i:i+1]=row(v)
    upb[...]=row(v_ub)
    bias[...]=jnp.zeros_like(bias)
    bias[:,0:width]=row(v_qb); bias[:,2*width:]=row(v_vb)
    gather_z(0,1); gather_start(2)
    gather_z(1,1); gather_z(0,2)
    gather_z(2,1); o_swap.wait_recv(); gather_start(3)
    gather_z(1,2); gather_z(0,3); gather_z(2,2); gather_z(1,3)
    gather_x(0); gather_z(3,1); gather_z(2,3)
    gather_x(1); gather_z(3,2)
    gather_start(4)
    gather_x(2); gather_z(3,3); gather_z(4,1)
    for g in range(3): gather_done(g)
    for c in own_copies: c.wait()
    TF=512
    @pl.loop(0,NC)
    def _(c):
        tok_copy(c).wait_recv()
        @pl.loop(0,n//TF)
        def _(j):
            cs=pl.ds(pl.multiple_of(j*TF,TF),TF)
            qkv[chunk(c),cs]=(dot(hall[chunk(c)],strip(act,cs),NN)+bias[:,cs]).astype(BF)
        @pl.when(c==0)
        def _(): gather_z(4,2)
        @pl.when(c==1)
        def _():
            gather_x(3); gather_z(4,3)
            gather_start(5)
        @pl.when(c==3)
        def _(): gather_done(3)
    x_out=local(hall,x_hbm,5); w_out=local(act.at[:,:,0:n],wh_hbm,6)
    x_out.start(); w_out.start()
    ones=jnp.where(lax.broadcasted_iota(jnp.int32,(16,rows_all),0)==0,1.0,0.0).astype(BF)
    @pl.loop(0,pairs)
    def _(p):
        ck=pl.multiple_of(width+p*128,128); cv=pl.multiple_of(2*width+p*128,128)
        kt[p]=qkv[:,pl.ds(ck,128)].T
        v=qkv[:,pl.ds(cv,128)].T
        vt[2*p,0:64]=v[0:64]; vt[2*p,64:80]=ones
        vt[2*p+1,0:64]=v[64:128]; vt[2*p+1,64:80]=ones
    gather_z(5,1)
    x_out.wait()
    def split(k,c):
        sbuf[k-1,loc(c)]=pch[half(1-t)].astype(BF)
        rs_copy(k,c).start()
        part[loc(c)]=pch[half(t)]
    def stats(v):
        cen=v-jnp.mean(v,axis=1,keepdims=True)
        r=lax.rsqrt(jnp.mean(cen*cen,axis=1,keepdims=True)+EPSILON)
        return cen*r,r
    def lo_copy(c): return pltpu.make_async_copy(cl.at[loc(c)],lo_hbm.at[loc(c)],losem.at[c])
    def out_copy(slot,col):
        return pltpu.make_async_copy(stage.at[slot],dw.at[:,:,:,:,pl.ds(pl.multiple_of(col,512),512)],osem.at[slot])
    def wgrad(slot,left,right_ref,rcol,ocol):
        @pl.loop(0,dm//256)
        def _(i):
            ms=pl.ds(pl.multiple_of(i*256,256),256)
            right=right_ref[:,pl.ds(pl.multiple_of(rcol,512),512)] if len(right_ref.shape)==2 else strip(right_ref,pl.ds(pl.multiple_of(rcol,512),512))
            stage[slot,i]=dot(left[ms],right,NN).astype(BF).reshape(2,2,64,512)
        out_copy(slot,ocol).start()
    def stage_a(c):
        rs=chunk(c)
        @pl.loop(0,pairs//2)
        def _(pp):
            todo=[]
            for i in (0,1):
                p=2*pp+i
                cq=pl.ds(pl.multiple_of(p*128,128),128); ck=pl.ds(pl.multiple_of(width+p*128,128),128)
                for h in (0,1): todo.append((i,2*p+h,h,cq,ck,(lane<64) if h==0 else (lane>=64)))
            sts=[dot(qkv[:,ck],jnp.where(keep,qkv[rs,cq]*scale,zero),NT) for _,_,_,cq,ck,keep in todo]
            ms=[jnp.max(st,axis=0,keepdims=True) for st in sts]
            mcs=[v*LOG2E for v in ms]
            pts=[jnp.exp2(st*LOG2E-mc).astype(BF) for st,mc in zip(sts,mcs)]
            ots=[dot(vt[e[1]],pt,NN) for e,pt in zip(todo,pts)]
            for (i,hd,h,_,_,_),ot,mc in zip(todo,ots,mcs):
                tot=ot[64:65]
                ctt[i,h*64:(h+1)*64,:]=ot[0:64]*(1.0/tot)
                lse[pl.ds(hd,1),rs]=mc+jnp.log2(tot)
            tops=[jnp.max(v,axis=1,keepdims=True) for v in ms]
            for i in (0,1):
                cq=todo[2*i][3]
                early[10:11,cq]=jnp.maximum(early[10:11,cq],jnp.where(lane<64,tops[2*i],tops[2*i+1]))
                ctx[rs,cq]=ctt[i].T.astype(BF)
            step=c*(pairs//2)+pp
            @pl.when(step==0)
            def _():
                gather_z(5,2); gather_start(6)
            @pl.when(step==2)
            def _():
                gather_z(5,3); gather_z(6,1)
                gather_x(4)
            @pl.when(step==3)
            def _():
                gather_start(7); gather_z(6,2)
            @pl.when(step==4)
            def _():
                gather_z(6,3)
                gather_cross()
            @pl.when(step==5)
            def _():
                gather_z(7,1)
            @pl.when(step==6)
            def _():
                gather_z(7,2)
            @pl.when(step==7)
            def _():
                gather_z(7,3)
                gather_x(5)
        ctx_copy(c,t).start()
        ctxo[loc(c),cols(t)]=ctx[rows(t,c)]
    def stage_b(c):
        ctx_copy(c,1-t).wait_recv()
        x,r=stats(hall[rows(t,c)].astype(F32)+dot(ctxo[loc(c)],whole(wo),NT)+vec[0:1])
        xh[loc(c)]=x
        rst[loc(c)]=jnp.broadcast_to(r,(cr,128))
        hall[rows(t,c)]=(x*vec[1:2]+vec[2:3]).astype(BF)
        ag_copy(3,hall,c,t).start()
    def stage_c(c):
        rs=chunk(c)
        ag_copy(3,hall,c,1-t).wait_recv()
        @pl.loop(0,ff//TF)
        def _(j):
            cs=pl.ds(pl.multiple_of(j*TF,TF),TF)
            u=dot(hall[rs],strip(wup,cs),NN)+upb[:,cs]
            cdf=0.5*(1.0+lax.erf(u*0.5**0.5))
            act[pl.ds(4*c,4),:,cs]=(u*cdf).astype(BF).reshape(4,64,TF)
            slp[rs,cs]=(cdf+u*jnp.exp(-0.5*u*u)*(0.5/math.pi)**0.5).astype(BF)
    def stage_c2(c):
        pch[...]=dot(act[pl.ds(4*c,4)].reshape(cg,ff),whole(wdn),NT)
        split(1,c)
    def stage_d(c):
        rs_copy(1,c).wait_recv()
        x,r=stats(xh[loc(c)]*vec[1:2]+vec[2:3]+part[loc(c)]+rbuf[0,loc(c)].astype(F32)+vec[3:4])
        dy=cl[loc(c)].astype(F32)
        cl[loc(c)]=(x*vec[4:5]+vec[5:6]).astype(BF)
        lo_copy(c).start()
        early[4:5]+=jnp.sum(dy*x,axis=0,keepdims=True)
        early[5:6]+=jnp.sum(dy,axis=0,keepdims=True)
        dx=dy*vec[4:5]
        g=r*(dx-jnp.mean(dx,axis=1,keepdims=True)-x*jnp.mean(dx*x,axis=1,keepdims=True))
        gf[loc(c)]=g
        gb=g.astype(BF)
        early[3:4]+=jnp.sum(gb.astype(F32),axis=0,keepdims=True)
        ball[rows(t,c)]=gb
        ag_copy(4,ball,c,t).start()
        tb[:,rows(t,c)]=gb.T
    def stage_e(c):
        rs=chunk(c)
        ag_copy(4,ball,c,1-t).wait_recv()
        @pl.loop(0,ff//TF)
        def _(j):
            cs=pl.ds(pl.multiple_of(j*TF,TF),TF)
            gu=(dot(ball[rs],strip(wdn,cs),NN)*slp[rs,cs].astype(F32)).astype(BF)
            slp[rs,cs]=gu
            row=pl.ds(8+j*TF//dm,1); cc=pl.ds(pl.multiple_of(j*TF%dm,TF),TF)
            early[row,cc]+=jnp.sum(gu.astype(F32),axis=0,keepdims=True)
        pch[...]=dot(slp[rs],whole(wup),NT)
        split(2,c)
        tb[:,rows(1-t,c)]=ball[rows(1-t,c)].T
        th[:,chunk(c)]=hall[chunk(c)].T
    def stage_f(c):
        rs_copy(2,c).wait_recv()
        dy=gf[loc(c)]+part[loc(c)]+rbuf[1,loc(c)].astype(F32)
        x=xh[loc(c)]; r=rst[loc(c)][:,0:1]
        early[1:2]+=jnp.sum(dy*x,axis=0,keepdims=True)
        early[2:3]+=jnp.sum(dy,axis=0,keepdims=True)
        dx=dy*vec[1:2]
        g=r*(dx-jnp.mean(dx,axis=1,keepdims=True)-x*jnp.mean(dx*x,axis=1,keepdims=True))
        gf[loc(c)]=g
        gb=g.astype(BF)
        early[0:1]+=jnp.sum(gb.astype(F32),axis=0,keepdims=True)
        ga[loc(c)]=gb
        ball[rows(t,c)]=gb
        dcs[loc(c)]=dot(gb,whole(wo),NN).astype(BF)
        dctx_copy(c,t).start()
        dcall[rows(t,c)]=dcs[loc(c),cols(t)]
    def stage_g(c):
        rs=chunk(c)
        dctx_copy(c,1-t).wait_recv()
        @pl.when(c==0)
        def _():
            for i in range(NC): ga_copy(i).start()
        @pl.loop(0,pairs)
        def _(p):
            cq=pl.ds(pl.multiple_of(p*128,128),128); ck=pl.ds(pl.multiple_of(width+p*128,128),128); cv=pl.ds(pl.multiple_of(2*width+p*128,128),128)
            prod=(ctx[rs,cq].astype(F32)*dcall[rs,cq].astype(F32)).T
            dl[0:1]=jnp.sum(prod[0:64],axis=0,keepdims=True)
            dl[1:2]=jnp.sum(prod[64:128],axis=0,keepdims=True)
            for h in (0,1):
                keep=(lane<64) if h==0 else (lane>=64)
                q=jnp.where(keep,qkv[rs,cq]*scale,zero)
                do=jnp.where(keep,dcall[rs,cq],zero)
                st=dot(qkv[:,ck],q,NT)
                pt=jnp.exp2(st*LOG2E-lse[pl.ds(2*p+h,1),rs])
                dpt=dot(qkv[:,cv],do,NT)
                ds=(pt*(dpt-dl[h:h+1])).astype(BF)
                dkv[1,:,cq]+=dot(pt.astype(BF),do,NN)
                dkv[0,:,cq]+=dot(ds,q,NN)
                dqt[h*64:(h+1)*64,:]=dot(kt[p,h*64:(h+1)*64,:],ds,NN)
            qkv[rs,cq]=(dqt[...].T*(HD**-0.5)).astype(BF)
            step=c*pairs+p
            @pl.when(step==0)
            def _():
                add3(0)
                add2(2)
                fetch2(3)
            @pl.when(step==1)
            def _():
                add2(3)
                ecopy(0).start()
            @pl.when(step==4)
            def _():
                eadd(0); ecopy(1).start()
            @pl.when(step==5)
            def _():
                s2(1).wait_send(); s2(2).start()
                fetch3(1)
            @pl.when(step==6)
            def _():
                eadd(1); ecopy(2).start()
            @pl.when(step==7)
            def _():
                sent3(0); add3(1)
            @pl.when(step==8)
            def _():
                eadd(2); ecopy(3).start()
            @pl.when(step==9)
            def _():
                fetchf(0)
            @pl.when(step==10)
            def _():
                finish(0)
                eadd(3); ecopy(4).start()
            @pl.when(step==11)
            def _():
                s2(2).wait_send(); s2(3).start()
                fetch3(2)
            @pl.when(step==12)
            def _():
                for i in range(NC): ga_copy(i).wait_recv()
                for i in range(NC): th[:,i*cg:(i+1)*cg]=ball[i*cg:(i+1)*cg].T
            @pl.when(step==13)
            def _():
                sent3(1); add3(2)
                wgrad(0,th,ctx,0,base[4])
            @pl.when(step==14)
            def _():
                out_copy(0,0).wait(); s1(4).start()
            @pl.when(step==15)
            def _():
                fetch2(4)
    def grad_down(c):
        slot=c%2
        wgrad(slot,tb,act,c*512,width+ff+c*512)
    def grad_up(c):
        slot=c%2
        wgrad(slot,th,slp,c*512,width+c*512)
    def ga_copy(c):
        return pltpu.make_async_remote_copy(ga.at[loc(c)],ball.at[rows(t,c)],ssem.at[7,c],rsem.at[7,c],device_id=partner,device_id_type=MESH)
    @pl.loop(0,NC)
    def _(c):
        stage_a(c)
        @pl.when(c>0)
        def _(): stage_b(c-1)
    cot_load.wait(); w_out.wait()
    gather_done(4); gather_done(5)
    @pl.loop(0,NC-1)
    def _(c):
        stage_c(c)
        @pl.when(c==0)
        def _(): stage_b(NC-1)
    gather_x(6)
    gather_done(6); gather_done(7)
    @pl.loop(0,NC)
    def _(c):
        stage_c2(c)
        @pl.when(c==1)
        def _(): stage_c(NC-1)
    @pl.loop(0,NC)
    def _(c): stage_d(c)
    @pl.loop(0,NC)
    def _(c): stage_e(c)
    piece=ff//2
    base=(width+ff,width+ff+piece,width,width+piece,0,width+2*ff,2*width+2*ff,3*width+2*ff)
    span=(piece,)*4+(width,)*4
    def s1(g): return remote(dw.at[:,:,1-core,:,base[g]:base[g]+span[g]],r1.at[g,:,:,:,0:span[g]],g1s.at[g],g1r.at[g],sib)
    slots2=[wup.at[8:12,:,0:piece],wup.at[12:16,:,0:piece],wup.at[8:12,:,piece:],wup.at[12:16,:,piece:],wup.at[0:4,:,piece:],wup.at[4:8,:,piece:]]
    slots3=[wdn.at[12:16,:,0:piece],wdn.at[12:16,:,piece:],wdn.at[0:4,:,piece:],wdn.at[4:8,:,piece:],wdn.at[8:12,:,piece:]]
    sum2=[slots2[g%6] for g in range(8)]
    sum3=[slots3[g%5] for g in range(8)]
    def s2(g): return remote(sum2[g].at[:,:,0:span[g]],r2.at[g,:,:,0:span[g]],g2s.at[g],g2r.at[g],xp)
    def s3(g,k): return remote(sum3[g].at[(z+k)%4,:,0:span[g]],r3.at[g,3-k,:,0:span[g]],g3s.at[g,k-1],g3r.at[g,k-1],zp[k-1])
    def load2(g): return [pltpu.make_async_copy(dw.at[:,1-x_,core,:,base[g]:base[g]+span[g]],wup.at[0:4,:,0:span[g]],rl.at[0]),
                          pltpu.make_async_copy(r1.at[g,:,1-x_,:,0:span[g]],wup.at[4:8,:,0:span[g]],rl.at[1])]
    def load3(g): return [pltpu.make_async_copy(dw.at[:,x_,core,:,base[g]:base[g]+span[g]],wdn.at[0:4,:,0:span[g]],rl.at[2]),
                         pltpu.make_async_copy(r1.at[g,:,x_,:,0:span[g]],wdn.at[4:8,:,0:span[g]],rl.at[3]),
                         pltpu.make_async_copy(r2.at[g,:,:,0:span[g]],wdn.at[8:12,:,0:span[g]],rl.at[4])]
    def fetch2(g):
        s1(g).wait_recv()
        for l in load2(g): l.start()
    def add2(g):
        for l in load2(g): l.wait()
        @pl.loop(0,4)
        def _(i): sum2[g][i,:,0:span[g]]=(wup[i,:,0:span[g]].astype(F32)+wup[4+i,:,0:span[g]].astype(F32)).astype(BF)
    def fetch3(g):
        s2(g).wait_recv()
        for l in load3(g): l.start()
    def add3(g):
        for l in load3(g): l.wait()
        @pl.loop(0,4)
        def _(i): sum3[g][i,:,0:span[g]]=(wdn[i,:,0:span[g]].astype(F32)+wdn[4+i,:,0:span[g]].astype(F32)+wdn[8+i,:,0:span[g]].astype(F32)).astype(BF)
        for k in (1,2,3): s3(g,k).start()
    def sent3(g):
        for k in (1,2,3): s3(g,k).wait_send()
    def fslot(g,i):
        r=64*(6*(g%2)+i)
        return tb.at[r:r+64,0:span[g]]
    def loadf(g): return [pltpu.make_async_copy(src,fslot(g,i),fl.at[g%2,i]) for i,src in enumerate(
        [dw.at[z,x_,core,:,base[g]:base[g]+span[g]],r1.at[g,z,x_,:,0:span[g]],r2.at[g,z,:,0:span[g]]]+[r3.at[g,k,:,0:span[g]] for k in range(3)])]
    def fetchf(g):
        for k in (1,2,3): s3(g,k).wait_recv()
        for l in loadf(g): l.start()
    def final(g):
        for l in loadf(g): l.wait()
        v=[fslot(g,i)[...].astype(F32) for i in range(6)]
        return v[0]+v[1]+v[2]+v[3]+v[4]+v[5]
    def fin_copy(g):
        return pltpu.make_async_copy(xh.at[64*g:64*g+64,0:span[g]],fin.at[g] if g<4 else go_hbm if g==4 else fin_head.at[g-5],fs.at[g])
    def finish(g):
        xh[64*g:64*g+64,0:span[g]]=final(g)
        fin_copy(g).start()
    zb=[dev(z+1-2*(z%2),x_,core),dev((z+2)%4,x_,core)]
    hops=[sib,xp,zb[0],zb[1],partner]
    def ecopy(i): return remote(eb.at[i],er.at[i],es.at[i],erc.at[i],hops[i])
    def eadd(i):
        ecopy(i).wait_recv()
        b=eb[i,8:16]; c=er[i,8:16]
        if i<4:
            r=lax.broadcasted_iota(jnp.int32,b.shape,0)
            b=jnp.where(r==2,jnp.maximum(b,c),b+c)
        eb[i+1,0:8]=eb[i,0:8]+er[i,0:8]; eb[i+1,8:16]=b
    def lcopy(i): return remote(lb.at[i],lr.at[i],ls.at[i],lrc.at[i],hops[i])
    def ladd(i):
        lcopy(i).wait_recv()
        lb[i+1]=lb[i]+lr[i]
    def drain():
        out_copy(0,0).wait()
        out_copy(1,0).wait()
    @pl.loop(0,NC)
    def _(c):
        ag_copy(3,hall,c,t).wait_send()
        ag_copy(4,ball,c,t).wait_send()
    x_in=pltpu.make_async_copy(x_hbm,hall,dsem.at[0])
    x_in.start()
    grad_down(0); grad_down(1)
    drain(); s1(0).start()
    grad_down(2); grad_down(3)
    drain(); s1(1).start()
    wh_in=pltpu.make_async_copy(wh_hbm,act.at[:,:,0:n],dsem.at[1])
    wh_in.start()
    fetch2(0)
    @pl.loop(0,NC)
    def _(c):
        stage_f(c)
        @pl.when(c==0)
        def _():
            add2(0); s2(0).start()
            fetch2(1)
        grad_up(c)
        @pl.when(c==1)
        def _():
            drain(); s1(2).start()
            add2(1)
        @pl.when(c==3)
        def _():
            drain(); s1(3).start()
            fetch2(2)
            s2(0).wait_send(); s2(1).start()
            fetch3(0)
    @pl.loop(0,NC)
    def _(c): stage_g(c)
    add2(4)
    s2(3).wait_send(); s2(4).start()
    fetch3(3)
    x_in.wait()
    @pl.loop(0,NC)
    def _(c): th[:,chunk(c)]=hall[chunk(c)].T
    wgrad(0,th,qkv,0,base[5])
    sent3(2); add3(3)
    out_copy(0,0).wait(); s1(5).start()
    fetchf(1)
    @pl.loop(0,pairs)
    def _(p):
        cq=pl.ds(pl.multiple_of(p*128,128),128); ck=pl.ds(pl.multiple_of(width+p*128,128),128); cv=pl.ds(pl.multiple_of(2*width+p*128,128),128)
        qkv[:,ck]=dkv[0,:,cq].astype(BF)
        qkv[:,cv]=dkv[1,:,cq].astype(BF)
    fetch2(5)
    def ycopy(c): return remote(sbuf.at[0,loc(c)],rbuf.at[0,loc(c)],ssem.at[6,c],rsem.at[6,c],partner)
    wh_in.wait()
    def token_grad(c):
        pch[...]=dot(qkv[chunk(c)],act[:,:,0:n].reshape(dm,n),NT)
        rs_copy(1,c).wait_send()
        sbuf[0,loc(c)]=pch[half(1-t)].astype(BF)
        ycopy(c).start()
        part[loc(c)]=pch[half(t)]
    @pl.loop(0,2)
    def _(c): token_grad(c)
    add2(5)
    s2(4).wait_send(); s2(5).start()
    wgrad(1,th,qkv,width,base[6])
    fetch3(4)
    out_copy(1,0).wait(); s1(6).start()
    wgrad(0,th,qkv,2*width,base[7])
    fetch2(6)
    out_copy(0,0).wait(); s1(7).start()
    @pl.loop(2,NC)
    def _(c): token_grad(c)
    add2(6)
    s2(5).wait_send(); s2(6).start()
    fetch2(7)
    sent3(3); add3(4)
    fetch3(5)
    lb[0,0:1,0:width]=jnp.sum(qkv[:,0:width].astype(F32),axis=0,keepdims=True)
    lb[0,0:1,width:2*width]=jnp.sum(qkv[:,2*width:].astype(F32),axis=0,keepdims=True)
    lcopy(0).start()
    finish(1)
    add2(7)
    eadd(4)
    sent3(4); add3(5)
    s2(6).wait_send(); s2(7).start()
    fetch3(6)
    ladd(0); lcopy(1).start()
    fetchf(2)
    smalls[...]=eb[5]
    pk=eb[4,10:11,0:width]
    head=lax.broadcasted_iota(jnp.int32,(1,width),1)//HD
    limit=jnp.zeros((1,width),F32)
    for h in range(width//HD): limit=jnp.where(head==h,lim[h],limit)
    sc=jnp.sqrt(limit/jnp.maximum(pk,limit))
    ctxo[0:64,0:width]=(wq[...].astype(F32)*sc).astype(BF)
    ctxo[64:128,0:width]=(wk[...].astype(F32)*sc).astype(BF)
    clips=[pltpu.make_async_copy(ctxo.at[0:64,0:width],qc_hbm,fs.at[8]),pltpu.make_async_copy(ctxo.at[64:128,0:width],kc_hbm,fs.at[9])]
    for c in clips: c.start()
    smalls[11:12,0:width]=row(v_qb)*sc
    finish(2)
    ladd(1); lcopy(2).start()
    fetchf(3)
    sent3(5); add3(6)
    fetch3(7)
    finish(3)
    fetchf(4)
    ladd(2); lcopy(3).start()
    @pl.loop(0,NC)
    def _(c): lo_copy(c).wait()
    finish(4)
    sent3(6); add3(7)
    fetchf(5)
    def tg_copy(c): return pltpu.make_async_copy(cl.at[loc(c)],tg_hbm.at[loc(c)],losem.at[c])
    @pl.loop(0,NC)
    def _(c):
        ycopy(c).wait_recv()
        cl[loc(c)]=(gf[loc(c)]+part[loc(c)]+rbuf[0,loc(c)].astype(F32)).astype(BF)
        tg_copy(c).start()
    ladd(3)
    smalls[12:13]=lb[4,0:1]
    finish(5)
    fetchf(6)
    finish(6)
    fetchf(7)
    finish(7)
    o_swap.wait_send()
    for g in range(8):
        s1(g).wait_send()
        fin_copy(g).wait()
    s2(7).wait_send()
    sent3(7)
    for c in clips: c.wait()
    for i in range(5): ecopy(i).wait_send()
    for i in range(4): lcopy(i).wait_send()
    @pl.loop(0,NC)
    def _(c):
        tg_copy(c).wait()
        ctx_copy(c,t).wait_send(); dctx_copy(c,t).wait_send(); tok_copy(c).wait_send()
        rs_copy(2,c).wait_send(); ycopy(c).wait_send()
        ga_copy(c).wait_send()

def main_call(shards,tok,cot,vectors,lim,cid):
    V=pl.BlockSpec(memory_space=pltpu.VMEM); A=pl.BlockSpec(memory_space=pl.ANY)
    width=shards[0].shape[1]; ff=shards[4].shape[1]; own,dm=tok.shape; rows=2*own; n=3*width; cr=own//NC; wide=2*width; piece=ff//2
    S=jax.ShapeDtypeStruct; M=pltpu.VMEM; D=pltpu.SemaphoreType.DMA
    return pl.pallas_call(main_kernel,
      out_shape=(S((own,dm),BF),S((own,dm),BF),S((4,64,piece),F32),S((3,64,width),F32),S((64,width),F32),S((64,width),BF),S((64,width),BF),S((16,dm),F32),
        S((4,2,2,64,width+2*ff+n),BF),S((8,4,2,64,piece),BF),S((8,4,64,piece),BF),S((8,3,64,piece),BF),S((rows,dm),BF),S((16,64,n),BF)),
      in_specs=[V]*6+[A,A]+[V]*9+[pl.BlockSpec(memory_space=pltpu.SMEM)],out_specs=(A,)*7+(V,)+(A,)*6,
      scratch_shapes=[M((1,n),F32),M((8,dm),F32),M((1,ff),F32),M((own,dm),F32),M((6,16,dm),F32),M((5,16,dm),F32),M((5,8,dm),F32),M((4,8,dm),F32),
        M((64,n+wide+2*ff),BF),M((rows,n),BF),M((width//HD,80,rows),BF),M((width//128,128,rows),BF),M((rows,width),BF),M((own,wide),BF),M((width//HD,rows),F32),M((own,dm),BF),
        M((16,64,wide),BF),M((16,64,ff),BF),M((16,64,ff),BF),
        M((own,dm),F32),M((own,128),F32),
        M((rows,dm),BF),M((16,64,ff),BF),M((rows,ff),BF),M((rows,dm),BF),M((own,dm),BF),M((own,wide),BF),M((rows,width),BF),
        M((own,dm),F32),M((2*cr,dm),F32),M((2,128,2*cr),F32),M((128,2*cr),F32),M((8,2*cr),F32),M((2,rows,width),F32),
        M((2,own,dm),BF),M((2,own,dm),BF),
        M((dm,rows),BF),M((dm,rows),BF),M((2,4,2,2,64,512),BF),
        D((7,)),D((NC,)),D((2,)),D((2,)),D((8,NC)),D((8,NC)),D((5,)),D((8,)),D((8,)),D((8,)),D((8,)),D((8,3)),D((8,3)),
        D((NC+1,)),D((NC+1,)),D((8,2,3)),D((8,2,3)),D((2,3)),D((2,3)),D((8,4)),D((8,4)),D((8,8)),D((8,8)),
        D((5,)),D((5,)),D((4,)),D((4,)),D((2,6)),D((10,))],
      compiler_params=pltpu.CompilerParams(collective_id=cid,has_side_effects=True,vmem_limit_bytes=61*2**20),
      name="main")(*shards,tok,cot,*vectors,lim)

def finish_kernel(lo,tg,fin,fin_head,go,qc,kc,smalls,
                  lo_,tg_,gq_,gk_,gv_,go_,gu_,gd_,qc_,kc_,qb_,vb_,ob_,g1_,b1_,ub_,db_,g2_,b2_,pk_,qbc_,h_lo,h_tg,h_fin,h_head,h_go,h_qc,h_kc,isem,sem):
    piece=fin.shape[2]
    ins=[pltpu.make_async_copy(a,b,isem.at[i]) for i,(a,b) in enumerate(((lo,h_lo),(tg,h_tg),(fin,h_fin),(fin_head,h_head),(go,h_go),(qc,h_qc),(kc,h_kc)))]
    outs=[[(h_lo,lo_)],[(h_tg,tg_)],[(h_fin.at[0],gd_.at[:,0:piece]),(h_fin.at[1],gd_.at[:,piece:]),(h_fin.at[2],gu_.at[:,0:piece]),(h_fin.at[3],gu_.at[:,piece:])],
          [(h_head.at[0],gq_),(h_head.at[1],gk_),(h_head.at[2],gv_)],[(h_go,go_)],[(h_qc,qc_)],[(h_kc,kc_)]]
    for c in ins: c.start()
    width=qb_.shape[0]; dm=ob_.shape[0]
    def line(v): return v.reshape(v.shape[1])
    qb_[...]=line(smalls[12:13,0:width]); vb_[...]=line(smalls[12:13,width:2*width])
    for i,o in enumerate((ob_,g1_,b1_,db_,g2_,b2_)): o[...]=line(smalls[i:i+1])
    ub_[0:dm]=line(smalls[8:9]); ub_[dm:2*dm]=line(smalls[9:10])
    for h in range(pk_.shape[0]): pk_[h]=jnp.max(smalls[10:11,h*HD:(h+1)*HD])
    qbc_[...]=line(smalls[11:12,0:width]).astype(BF)
    moved=[]
    for a,group in zip(ins,outs):
        a.wait()
        for src,dst in group:
            c=pltpu.make_async_copy(src,dst,sem.at[len(moved)])
            c.start()
            moved.append(c)
    for c in moved: c.wait()

def finish_call(big,smalls,heads):
    V=pl.BlockSpec(memory_space=pltpu.VMEM); A=pl.BlockSpec(memory_space=pl.ANY); S=jax.ShapeDtypeStruct
    lo,tg,fin,fin_head,go,qc,kc=big
    width=go.shape[1]; piece=fin.shape[2]; ff=2*piece; dm=tg.shape[1]
    return pl.pallas_call(finish_kernel,
      out_shape=(S(lo.shape,BF),S(tg.shape,BF))+(S((64,width),F32),)*4+(S((64,ff),F32),)*2+(S((64,width),BF),)*2
        +tuple(S((k,),F32) for k in (width,width,dm,dm,dm,ff,dm,dm,dm,heads))+(S((width,),BF),),
      in_specs=[A]*7+[V],out_specs=(A,)*10+(V,)*9+(pl.BlockSpec(memory_space=pltpu.SMEM),V),
      scratch_shapes=[pltpu.VMEM(a.shape,a.dtype) for a in big]+[pltpu.SemaphoreType.DMA((7,)),pltpu.SemaphoreType.DMA((12,))],
      compiler_params=pltpu.CompilerParams(vmem_limit_bytes=61*2**20),name="finish")(*big,smalls)

def per_device_pair(tokens,query_weight,query_bias,key_weight,value_weight,value_bias,out_weight,out_bias,first_gain,first_shift,
    up_weight,up_bias,down_weight,down_bias,second_gain,second_shift,cotangent,clip_limit):
    shards=(query_weight,key_weight,value_weight,out_weight.T,up_weight,down_weight.T)
    vectors=(out_bias,first_gain,first_shift,down_bias,second_gain,second_shift,up_bias,query_bias,value_bias)
    res=main_call(shards,tokens,cotangent,vectors,clip_limit,1)
    lo,tg,gq,gk,gv,go,gu,gd,qc,kc,qb,vb,ob,g1,b1,ub,db,g2,b2,pk,qbc=finish_call(res[:7],res[7],clip_limit.shape[0])
    return (lo,tg,gq,qb,gk,gv,vb,go.T,ob,g1,b1,gu,ub,gd.T,db,g2,b2,pk,qc,qbc,kc)


def layer(*args):
    paired = lax.axis_size("dp") == 16 and lax.axis_size("tensor") == 2 and 2 * args[0].shape[0] == LEN
    return per_device_pair(*args) if paired else per_device(*args)


def solution(mesh):
    in_specs = (
        P(("dp", "tensor"), None),
        P("dp", "tensor"),
        P("tensor"),
        P("dp", "tensor"),
        P("dp", "tensor"),
        P("tensor"),
        P("tensor", "dp"),
        P(),
        P(),
        P(),
        P("dp", "tensor"),
        P("tensor"),
        P("tensor", "dp"),
        P(),
        P(),
        P(),
        P(("dp", "tensor"), None),
        P("tensor"),
    )
    out_specs = (
        P(("dp", "tensor"), None),
        P(("dp", "tensor"), None),
        P("dp", "tensor"),
        P("tensor"),
        P("dp", "tensor"),
        P("dp", "tensor"),
        P("tensor"),
        P("tensor", "dp"),
        P(),
        P(),
        P(),
        P("dp", "tensor"),
        P("tensor"),
        P("tensor", "dp"),
        P(),
        P(),
        P(),
        P("tensor"),
        P("dp", "tensor"),
        P("tensor"),
        P("dp", "tensor"),
    )
    return jax.shard_map(
        layer, mesh=mesh, in_specs=in_specs, out_specs=out_specs, check_vma=False
    )
```

```python
import functools
import math

import jax
import jax.numpy as jnp
from jax import lax
from jax.experimental import pallas as pl
from jax.experimental.pallas import tpu as pltpu
from jax.sharding import PartitionSpec as P

HD = 64
LEN = 1024
QB = 512


def layer_norm(values, gain, shift):
    center = values - jnp.mean(values, axis=-1, keepdims=True)
    spread = jnp.mean(center * center, axis=-1, keepdims=True)
    return center * lax.rsqrt(spread + EPSILON) * gain + shift


def gelu_slope(upper):
    normal_cdf = 0.5 * (1.0 + lax.erf(upper * 0.5**0.5))
    return normal_cdf + upper * jnp.exp(-0.5 * upper * upper) * (0.5 / math.pi) ** 0.5


def contract_rows(left, right):
    return lax.dot_general(
        left, right, (((0,), (0,)), ((), ())), preferred_element_type=jnp.float32
    )


def contract_cols(left, right):
    return lax.dot_general(
        left, right, (((1,), (1,)), ((), ())), preferred_element_type=jnp.float32
    )


def per_device(
    tokens,
    query_weight,
    query_bias,
    key_weight,
    value_weight,
    value_bias,
    out_weight,
    out_bias,
    first_gain,
    first_shift,
    up_weight,
    up_bias,
    down_weight,
    down_bias,
    second_gain,
    second_shift,
    cotangent,
    clip_limit,
):
    query_full, key_full, value_full, out_full, up_full, down_full = (
        lax.all_gather(query_weight, "dp", axis=0, tiled=True),
        lax.all_gather(key_weight, "dp", axis=0, tiled=True),
        lax.all_gather(value_weight, "dp", axis=0, tiled=True),
        lax.all_gather(out_weight, "dp", axis=1, tiled=True),
        lax.all_gather(up_weight, "dp", axis=0, tiled=True),
        lax.all_gather(down_weight, "dp", axis=1, tiled=True),
    )
    width = query_full.shape[1]
    hidden_width = up_full.shape[1]
    heads_here = width // HD
    score_scale = HD ** (-0.5)
    joint_weight = jnp.concatenate([query_full, key_full, value_full], axis=1)
    gathered = lax.all_gather(tokens, "tensor", axis=0, tiled=True)
    group_rows = gathered.shape[0]
    seq_count = group_rows // LEN
    block_count = LEN // QB
    projected = jnp.dot(gathered, joint_weight, preferred_element_type=jnp.float32)
    queries = (projected[:, :width] + query_bias.astype(jnp.float32)).astype(jnp.bfloat16)
    keyset = projected[:, width : 2 * width].astype(jnp.bfloat16)
    valset = (projected[:, 2 * width :] + value_bias.astype(jnp.float32)).astype(jnp.bfloat16)
    query_seq = queries.reshape(seq_count, LEN, heads_here, HD)
    key_seq = keyset.reshape(seq_count, LEN, heads_here, HD)
    value_seq = valset.reshape(seq_count, LEN, heads_here, HD)

    def attend_block(block_id):
        seq_id = block_id // block_count
        row_start = block_id % block_count * QB
        query_rows = lax.dynamic_slice_in_dim(
            lax.dynamic_index_in_dim(query_seq, seq_id, 0, False), row_start, QB, 0
        )
        key_rows = lax.dynamic_index_in_dim(key_seq, seq_id, 0, False)
        value_rows = lax.dynamic_index_in_dim(value_seq, seq_id, 0, False)
        logits = (
            jnp.einsum("qhd,khd->hqk", query_rows, key_rows, preferred_element_type=jnp.float32)
            * score_scale
        )
        row_max = jnp.max(logits, axis=2, keepdims=True)
        exponent = jnp.exp(logits - row_max)
        totals = jnp.sum(exponent, axis=2, keepdims=True)
        probs_low = (exponent / totals).astype(jnp.bfloat16)
        context_rows = jnp.einsum(
            "hqk,khd->qhd", probs_low, value_rows, preferred_element_type=jnp.float32
        )
        return (
            context_rows.reshape(QB, width).astype(jnp.bfloat16),
            (row_max + jnp.log(totals))[:, :, 0],
            jnp.max(row_max, axis=(1, 2)),
        )

    context_blocks, log_totals, block_peaks = lax.map(
        attend_block, jnp.arange(seq_count * block_count)
    )
    context = context_blocks.reshape(group_rows, width)
    logit_peak = lax.pmax(jnp.max(block_peaks, axis=0), "dp")
    attention = lax.psum_scatter(
        jnp.dot(context, out_full, preferred_element_type=jnp.float32).astype(jnp.bfloat16),
        "tensor",
        scatter_dimension=0,
        tiled=True,
    ).astype(jnp.float32) + out_bias.astype(jnp.float32)
    first_resid = tokens.astype(jnp.float32) + attention
    hidden, first_pull = jax.vjp(
        layer_norm, first_resid, first_gain.astype(jnp.float32), first_shift.astype(jnp.float32)
    )
    hidden_all = lax.all_gather(hidden.astype(jnp.bfloat16), "tensor", axis=0, tiled=True)
    upper = jnp.dot(hidden_all, up_full, preferred_element_type=jnp.float32) + up_bias.astype(
        jnp.float32
    )
    acted = jax.nn.gelu(upper, approximate=False).astype(jnp.bfloat16)
    branch = lax.psum_scatter(
        jnp.dot(acted, down_full, preferred_element_type=jnp.float32).astype(jnp.bfloat16),
        "tensor",
        scatter_dimension=0,
        tiled=True,
    ).astype(jnp.float32) + down_bias.astype(jnp.float32)
    normed, second_pull = jax.vjp(
        layer_norm,
        hidden + branch,
        second_gain.astype(jnp.float32),
        second_shift.astype(jnp.float32),
    )
    layer_out = normed.astype(jnp.bfloat16)
    grad_second, second_gain_grad, second_shift_grad = second_pull(cotangent.astype(jnp.float32))
    grad_branch = grad_second.astype(jnp.bfloat16)
    down_bias_grad = jnp.sum(grad_branch, axis=0, dtype=jnp.float32)
    branch_all = lax.all_gather(grad_branch, "tensor", axis=0, tiled=True)
    grad_acted = contract_cols(branch_all, down_full)
    down_weight_grad = contract_rows(acted, branch_all)
    grad_upper = (grad_acted * gelu_slope(upper)).astype(jnp.bfloat16)
    up_bias_grad = jnp.sum(grad_upper, axis=0, dtype=jnp.float32)
    up_weight_grad = contract_rows(hidden_all, grad_upper)
    grad_hidden = grad_second + lax.psum_scatter(
        contract_cols(grad_upper, up_full).astype(jnp.bfloat16),
        "tensor",
        scatter_dimension=0,
        tiled=True,
    ).astype(jnp.float32)
    grad_first, first_gain_grad, first_shift_grad = first_pull(grad_hidden)
    grad_attn = grad_first.astype(jnp.bfloat16)
    out_bias_grad = jnp.sum(grad_attn, axis=0, dtype=jnp.float32)
    attn_all = lax.all_gather(grad_attn, "tensor", axis=0, tiled=True)
    grad_context = contract_cols(attn_all, out_full).astype(jnp.bfloat16)
    out_weight_grad = contract_rows(context, attn_all)
    query_blocks = queries.reshape(seq_count, block_count, QB, heads_here, HD)
    grad_blocks = grad_context.reshape(seq_count, block_count, QB, heads_here, HD)
    log_blocks = log_totals.reshape(seq_count, block_count, heads_here, QB)

    def sequence_back(item):
        query_part, grad_part, log_part, key_rows, value_rows = item

        def block_back(carry, piece):
            key_acc, value_acc = carry
            query_rows, grad_rows, log_rows = piece
            logits = (
                jnp.einsum("qhd,khd->hqk", query_rows, key_rows, preferred_element_type=jnp.float32)
                * score_scale
            )
            probs = jnp.exp(logits - log_rows[:, :, None])
            probs_low = probs.astype(jnp.bfloat16)
            value_acc = value_acc + jnp.einsum(
                "hqk,qhd->khd", probs_low, grad_rows, preferred_element_type=jnp.float32
            )
            grad_probs = jnp.einsum(
                "qhd,khd->hqk", grad_rows, value_rows, preferred_element_type=jnp.float32
            )
            inner = jnp.sum(probs * grad_probs, axis=2, keepdims=True)
            grad_logits = (probs * (grad_probs - inner)).astype(jnp.bfloat16)
            grad_query = (
                jnp.einsum(
                    "hqk,khd->qhd", grad_logits, key_rows, preferred_element_type=jnp.float32
                )
                * score_scale
            )
            key_acc = (
                key_acc
                + jnp.einsum(
                    "hqk,qhd->khd", grad_logits, query_rows, preferred_element_type=jnp.float32
                )
                * score_scale
            )
            return ((key_acc, value_acc), grad_query.astype(jnp.bfloat16))

        empty = jnp.zeros((LEN, heads_here, HD), jnp.float32)
        (key_acc, value_acc), grad_query_rows = lax.scan(
            block_back, (empty, empty), (query_part, grad_part, log_part)
        )
        return (grad_query_rows, key_acc.astype(jnp.bfloat16), value_acc.astype(jnp.bfloat16))

    grad_queries_all, grad_keys_all, grad_values_all = lax.map(
        sequence_back, (query_blocks, grad_blocks, log_blocks, key_seq, value_seq)
    )
    grad_joint = jnp.concatenate(
        [
            grad_queries_all.reshape(group_rows, width),
            grad_keys_all.reshape(group_rows, width),
            grad_values_all.reshape(group_rows, width),
        ],
        axis=1,
    )
    joint_grad = contract_rows(gathered, grad_joint)
    query_weight_grad = joint_grad[:, :width]
    key_weight_grad = joint_grad[:, width : 2 * width]
    value_weight_grad = joint_grad[:, 2 * width :]
    query_bias_grad = jnp.sum(grad_joint[:, :width], axis=0, dtype=jnp.float32)
    value_bias_grad = jnp.sum(grad_joint[:, 2 * width :], axis=0, dtype=jnp.float32)
    tokens_grad = (
        grad_first
        + lax.psum_scatter(
            contract_cols(grad_joint, joint_weight).astype(jnp.bfloat16),
            "tensor",
            scatter_dimension=0,
            tiled=True,
        ).astype(jnp.float32)
    ).astype(jnp.bfloat16)
    (
        query_weight_grad,
        key_weight_grad,
        value_weight_grad,
        out_weight_grad,
        up_weight_grad,
        down_weight_grad,
    ) = (
        lax.psum_scatter(
            query_weight_grad.astype(jnp.bfloat16), "dp", scatter_dimension=0, tiled=True
        ).astype(jnp.float32),
        lax.psum_scatter(
            key_weight_grad.astype(jnp.bfloat16), "dp", scatter_dimension=0, tiled=True
        ).astype(jnp.float32),
        lax.psum_scatter(
            value_weight_grad.astype(jnp.bfloat16), "dp", scatter_dimension=0, tiled=True
        ).astype(jnp.float32),
        lax.psum_scatter(
            out_weight_grad.astype(jnp.bfloat16), "dp", scatter_dimension=1, tiled=True
        ).astype(jnp.float32),
        lax.psum_scatter(
            up_weight_grad.astype(jnp.bfloat16), "dp", scatter_dimension=0, tiled=True
        ).astype(jnp.float32),
        lax.psum_scatter(
            down_weight_grad.astype(jnp.bfloat16), "dp", scatter_dimension=1, tiled=True
        ).astype(jnp.float32),
    )
    tensor_place = lax.axis_index("tensor")
    model_width = out_bias.shape[0]
    query_spread = lax.dynamic_update_slice_in_dim(
        jnp.zeros((model_width,), jnp.float32), query_bias_grad, tensor_place * width, 0
    )
    value_spread = lax.dynamic_update_slice_in_dim(
        jnp.zeros((model_width,), jnp.float32), value_bias_grad, tensor_place * width, 0
    )
    up_spread = lax.dynamic_update_slice_in_dim(
        jnp.zeros((hidden_width * lax.axis_size("tensor"),), jnp.float32),
        up_bias_grad,
        tensor_place * hidden_width,
        0,
    )
    (
        query_spread,
        value_spread,
        up_spread,
        out_bias_grad,
        down_bias_grad,
        first_gain_grad,
        first_shift_grad,
        second_gain_grad,
        second_shift_grad,
    ) = lax.psum(
        (
            query_spread,
            value_spread,
            up_spread,
            out_bias_grad,
            down_bias_grad,
            first_gain_grad,
            first_shift_grad,
            second_gain_grad,
            second_shift_grad,
        ),
        ("dp", "tensor"),
    )
    query_bias_grad = lax.dynamic_slice_in_dim(query_spread, tensor_place * width, width, 0)
    value_bias_grad = lax.dynamic_slice_in_dim(value_spread, tensor_place * width, width, 0)
    up_bias_grad = lax.dynamic_slice_in_dim(up_spread, tensor_place * hidden_width, hidden_width, 0)
    factor = clip_limit / jnp.maximum(logit_peak, clip_limit)
    column_scale = jnp.repeat(jnp.sqrt(factor), HD)
    query_clipped = (query_weight.astype(jnp.float32) * column_scale).astype(jnp.bfloat16)
    query_bias_clipped = (query_bias.astype(jnp.float32) * column_scale).astype(jnp.bfloat16)
    key_clipped = (key_weight.astype(jnp.float32) * column_scale).astype(jnp.bfloat16)
    return (
        layer_out,
        tokens_grad,
        query_weight_grad,
        query_bias_grad,
        key_weight_grad,
        value_weight_grad,
        value_bias_grad,
        out_weight_grad,
        out_bias_grad,
        first_gain_grad,
        first_shift_grad,
        up_weight_grad,
        up_bias_grad,
        down_weight_grad,
        down_bias_grad,
        second_gain_grad,
        second_shift_grad,
        logit_peak,
        query_clipped,
        query_bias_clipped,
        key_clipped,
    )


LOG2E=1.4426950408889634
NT=(((1,),(1,)),((),()))
NN=(((1,),(0,)),((),()))
F32=jnp.float32
BF=jnp.bfloat16
MESH=pl.DeviceIdType.MESH
EPSILON=1e-5
NC=4


def dot(a,b,dims):
    return lax.dot_general(a,b,dims,preferred_element_type=jnp.float32)


def greet(partner):
    barrier=pltpu.get_barrier_semaphore()
    pl.semaphore_signal(barrier,inc=1,device_id=partner,device_id_type=MESH)
    pl.semaphore_wait(barrier,1)


def main_kernel(wq,wk,wv,wos,wu,wds,tok,cot_hbm,v_ob,v_g1,v_b1,v_db,v_g2,v_b2,v_ub,v_qb,v_vb,lim,
               lo_hbm,tg_hbm,fin,fin_head,go_hbm,qc_hbm,kc_hbm,smalls,dw,r1,r2,r3,x_hbm,wh_hbm,
               bias,vec,upb,gf,eb,er,lb,lr,sh,qkv,vt,kt,ctx,ctxo,lse,cl,wo,wup,wdn,xh,rst,hall,act,slp,ball,ga,dcs,dcall,part,pch,ctt,dqt,dl,dkv,sbuf,rbuf,tb,th,stage,
               lsem,losem,dsem,osem,ssem,rsem,rl,g1s,g1r,g2s,g2r,g3s,g3r,ts,tr,azs,azr,axs,axr,acs,acr,es,erc,ls,lrc,fl,fs):
    d=lax.axis_index("dp"); t=lax.axis_index("tensor")
    partner=(d,1-t)
    core=d%2; x_=(d//2)%2; z=d//4
    def dev(z_,xx,c_): return ((z_*2+xx)*2+c_,t)
    sib=dev(z,x_,1-core); xp=dev(z,1-x_,core); zp=[dev((z+k)%4,x_,core) for k in (1,2,3)]
    own,dm=tok.shape; cr=own//NC; cg=2*cr; rows_all=2*own; width=ctx.shape[1]; ff=wup.shape[2]; wide=wo.shape[2]; pairs=width//128
    def local(src,dst,i): return pltpu.make_async_copy(src,dst,lsem.at[i])
    def remote(src,dst,a,b,p): return pltpu.make_async_remote_copy(src,dst,a,b,device_id=p,device_id_type=MESH)
    cot_load=local(cot_hbm,cl,0)
    cot_load.start()
    barrier=pltpu.get_barrier_semaphore()
    n=3*width
    def row(v): return v[...].astype(F32).reshape(1,v.shape[0])
    sh[:,0:width]=wq[...]; sh[:,width:2*width]=wk[...]; sh[:,2*width:n]=wv[...]
    everyone=[partner,sib,xp]+zp
    for p in everyone: pl.semaphore_signal(barrier,inc=1,device_id=p,device_id_type=MESH)
    def chunk(c): return pl.ds(pl.multiple_of(c*cg,cg),cg)
    def rows(rank,c): return pl.ds(pl.multiple_of(c*cg+rank*cr,cr),cr)
    def half(rank): return pl.ds(pl.multiple_of(rank*cr,cr),cr)
    def loc(c): return pl.ds(pl.multiple_of(c*cr,cr),cr)
    def rs_copy(k,c):
        return pltpu.make_async_remote_copy(sbuf.at[k-1,loc(c)],rbuf.at[k-1,loc(c)],ssem.at[k,c],rsem.at[k,c],device_id=partner,device_id_type=MESH)
    def ag_copy(k,buf,c,rank):
        return pltpu.make_async_remote_copy(buf.at[rows(rank,c)],buf.at[rows(rank,c)],ssem.at[k,c],rsem.at[k,c],device_id=partner,device_id_type=MESH)
    def cols(rank): return pl.ds(pl.multiple_of(rank*width,128),width)
    def ctx_copy(c,rank):
        return pltpu.make_async_remote_copy(ctx.at[rows(1-rank,c)],ctxo.at[loc(c),cols(rank)],ssem.at[0,c],rsem.at[0,c],device_id=partner,device_id_type=MESH)
    def dctx_copy(c,rank):
        return pltpu.make_async_remote_copy(dcs.at[loc(c),cols(1-rank)],dcall.at[rows(rank,c)],ssem.at[5,c],rsem.at[5,c],device_id=partner,device_id_type=MESH)
    early=eb.at[0]
    early[...]=jnp.zeros((16,dm),F32)
    early[10:11]=jnp.full((1,dm),-jnp.inf,F32)
    lb[0]=jnp.zeros((8,dm),F32)
    def whole(w): return w[...].reshape(dm,w.shape[2])
    def strip(w,cs): return w[:,:,cs].reshape(dm,TF)
    dkv[...]=jnp.zeros_like(dkv)
    lane=lax.broadcasted_iota(jnp.int32,(1,128),1)
    scale=jnp.bfloat16(HD**-0.5); zero=jnp.bfloat16(0)
    q4=ff//2
    groups=[(act,0,0,width),(act,width,width,width),(act,2*width,2*width,width),(wo,0,n,wide),
            (wup,0,n+wide,q4),(wup,q4,n+wide+q4,q4),(wdn,0,n+wide+ff,q4),(wdn,q4,n+wide+ff+q4,q4)]
    def block(z_,xx): return (z_*2+xx)*2+core
    me=block(z,x_)
    def place(g,b):
        buf,c0,_,nc=groups[g]
        return buf.at[b,:,c0:c0+nc]
    def shard(g): return sh.at[:,groups[g][2]:groups[g][2]+groups[g][3]]
    up=dev(jnp.minimum(z+1,3),x_,core); down=dev(jnp.maximum(z-1,0),x_,core)
    def z_hop(g,way,j,b): return remote(shard(g) if j==1 else place(g,b),place(g,b),azs.at[g,way,j-1],azr.at[g,way,j-1],up if way==0 else down)
    def x_hop(g,zz,own_): return remote(shard(g) if own_ else place(g,block(zz,x_)),place(g,block(zz,x_)),axs.at[g,zz],axr.at[g,zz],xp)
    def x_land(g,zz): return remote(place(g,block(zz,1-x_)),place(g,block(zz,1-x_)),axs.at[g,zz],axr.at[g,zz],xp)
    def c_hop(g,xx,zz,b,own_): return remote(shard(g) if own_ else place(g,b),place(g,b),acs.at[g,4*xx+zz],acr.at[g,4*xx+zz],sib)
    def gather_start(g):
        buf,c0,s0,nc=groups[g]
        @pl.when(z<3)
        def _(): z_hop(g,0,1,me).start()
        @pl.when(z>0)
        def _(): z_hop(g,1,1,me).start()
        x_hop(g,z,True).start()
        c_hop(g,0,z,me,True).start()
        buf[me,:,c0:c0+nc]=sh[:,s0:s0+nc]
    def gather_z(g,j):
        for way in (0,1):
            here=(z>=j) if way==0 else (z+j<=3)
            zz=jnp.maximum(z-j,0) if way==0 else jnp.minimum(z+j,3)
            b=block(zz,x_)
            @pl.when(here)
            def _():
                z_hop(g,way,j,b).wait_recv()
                x_hop(g,zz,False).start()
                c_hop(g,0,zz,b,False).start()
            if j<3:
                @pl.when(here & ((z<3) if way==0 else (z>0)))
                def _(): z_hop(g,way,j+1,b).start()
    def gather_x(g):
        for zz in range(4):
            x_land(g,zz).wait_recv()
            c_hop(g,1,zz,block(zz,1-x_),False).start()
    def gather_done(g):
        for xx in (0,1):
            for zz in range(4):
                b=block(zz,x_)
                c_hop(g,xx,zz,b,False).wait_recv()
                c_hop(g,xx,zz,b,False).wait_send()
        for zz in range(4): x_land(g,zz).wait_send()
        for j in (1,2,3):
            @pl.when((z>=j-1) & (z<3))
            def _(): z_hop(g,0,j,me).wait_send()
            @pl.when((z+j-1<=3) & (z>0))
            def _(): z_hop(g,1,j,me).wait_send()
    own_copies=[local(tok.at[c*cr:(c+1)*cr],hall.at[rows(t,c)],1+c) for c in range(NC)]
    for c in own_copies: c.start()
    pl.semaphore_wait(barrier,len(everyone))
    gather_start(0); gather_start(1)
    def tok_copy(c): return remote(tok.at[loc(c)],hall.at[rows(t,c)],ts.at[c],tr.at[c],partner)
    def mine_o(rank): return sh.at[:,pl.ds(pl.multiple_of(n+rank*width,128),width)]
    o_swap=remote(mine_o(t),mine_o(t),ts.at[NC],tr.at[NC],partner)
    sh[:,pl.ds(pl.multiple_of(n+t*width,128),width)]=wos[...]
    o_swap.start()
    @pl.loop(0,NC)
    def _(c): tok_copy(c).start()
    sh[:,n+wide:n+wide+ff]=wu[...]
    sh[:,n+wide+ff:]=wds[...]
    for i,v in enumerate((v_ob,v_g1,v_b1,v_db,v_g2,v_b2)): vec[i:i+1]=row(v)
    upb[...]=row(v_ub)
    bias[...]=jnp.zeros_like(bias)
    bias[:,0:width]=row(v_qb); bias[:,2*width:]=row(v_vb)
    gather_z(0,1); gather_start(2)
    gather_z(1,1); gather_z(0,2)
    gather_z(2,1); o_swap.wait_recv(); gather_start(3)
    gather_z(1,2); gather_z(0,3); gather_z(2,2); gather_z(1,3)
    gather_x(0); gather_z(3,1); gather_z(2,3)
    gather_x(1); gather_z(3,2)
    gather_start(4)
    gather_x(2); gather_z(3,3); gather_z(4,1)
    for g in range(3): gather_done(g)
    for c in own_copies: c.wait()
    TF=512
    @pl.loop(0,NC)
    def _(c):
        tok_copy(c).wait_recv()
        @pl.loop(0,n//TF)
        def _(j):
            cs=pl.ds(pl.multiple_of(j*TF,TF),TF)
            qkv[chunk(c),cs]=(dot(hall[chunk(c)],strip(act,cs),NN)+bias[:,cs]).astype(BF)
        th[:,chunk(c)]=hall[chunk(c)].T
        @pl.when(c==0)
        def _(): gather_z(4,2)
        @pl.when(c==1)
        def _():
            gather_x(3); gather_z(4,3)
            gather_start(5)
        @pl.when(c==3)
        def _(): gather_done(3)
    x_out=local(th,x_hbm,5); w_out=local(act.at[:,:,0:n],wh_hbm,6)
    x_out.start(); w_out.start()
    ones=jnp.where(lax.broadcasted_iota(jnp.int32,(16,rows_all),0)==0,1.0,0.0).astype(BF)
    @pl.loop(0,pairs)
    def _(p):
        ck=pl.multiple_of(width+p*128,128); cv=pl.multiple_of(2*width+p*128,128)
        kt[p]=qkv[:,pl.ds(ck,128)].T
        v=qkv[:,pl.ds(cv,128)].T
        vt[2*p,0:64]=v[0:64]; vt[2*p,64:80]=ones
        vt[2*p+1,0:64]=v[64:128]; vt[2*p+1,64:80]=ones
    gather_z(5,1)
    def split(k,c):
        sbuf[k-1,loc(c)]=pch[half(1-t)].astype(BF)
        rs_copy(k,c).start()
        part[loc(c)]=pch[half(t)]
    def stats(v):
        cen=v-jnp.mean(v,axis=1,keepdims=True)
        r=lax.rsqrt(jnp.mean(cen*cen,axis=1,keepdims=True)+EPSILON)
        return cen*r,r
    def lo_copy(c): return pltpu.make_async_copy(cl.at[loc(c)],lo_hbm.at[loc(c)],losem.at[c])
    def own_tile(i,col): return pltpu.make_async_copy(stage.at[i%2,:,:,core],dw.at[:,:,core,:,pl.ds(col if isinstance(col,int) else pl.multiple_of(col,512),512)],osem.at[i%2])
    def pair_tile(i,g,off): return remote(stage.at[i%2,:,:,1-core],r1.at[g,:,:,:,pl.ds(off if isinstance(off,int) else pl.multiple_of(off,512),512)],g1s.at[i],g1r.at[i],sib)
    def wgrad(i,g,off,left,right_ref,rcol,ocol):
        if not isinstance(i,int) or 2<=i<8: own_tile(i-2,0).wait()
        if not isinstance(i,int) or i>=2: pair_tile(i-2,0,0).wait_send()
        @pl.loop(0,dm//256)
        def _(k):
            ms=pl.ds(pl.multiple_of(k*256,256),256)
            cs=pl.ds(rcol if isinstance(rcol,int) else pl.multiple_of(rcol,512),512)
            right=right_ref[:,cs] if len(right_ref.shape)==2 else strip(right_ref,cs)
            stage[i%2,k]=dot(left[ms],right,NN).astype(BF).reshape(2,2,64,512)
        own_tile(i,ocol).start()
        pair_tile(i,g,off).start()
    def stage_a(c):
        rs=chunk(c)
        @pl.loop(0,pairs//2)
        def _(pp):
            todo=[]
            for i in (0,1):
                p=2*pp+i
                cq=pl.ds(pl.multiple_of(p*128,128),128); ck=pl.ds(pl.multiple_of(width+p*128,128),128)
                for h in (0,1): todo.append((i,2*p+h,h,cq,ck,(lane<64) if h==0 else (lane>=64)))
            sts=[dot(qkv[:,ck],jnp.where(keep,qkv[rs,cq]*scale,zero),NT) for _,_,_,cq,ck,keep in todo]
            ms=[jnp.max(st,axis=0,keepdims=True) for st in sts]
            mcs=[v*LOG2E for v in ms]
            pts=[jnp.exp2(st*LOG2E-mc).astype(BF) for st,mc in zip(sts,mcs)]
            ots=[dot(vt[e[1]],pt,NN) for e,pt in zip(todo,pts)]
            for (i,hd,h,_,_,_),ot,mc in zip(todo,ots,mcs):
                tot=ot[64:65]
                ctt[i,h*64:(h+1)*64,:]=ot[0:64]*(1.0/tot)
                lse[pl.ds(hd,1),rs]=mc+jnp.log2(tot)
            tops=[jnp.max(v,axis=1,keepdims=True) for v in ms]
            for i in (0,1):
                cq=todo[2*i][3]
                early[10:11,cq]=jnp.maximum(early[10:11,cq],jnp.where(lane<64,tops[2*i],tops[2*i+1]))
                ctx[rs,cq]=ctt[i].T.astype(BF)
            step=c*(pairs//2)+pp
            @pl.when(step==0)
            def _():
                gather_z(5,2); gather_start(6)
            @pl.when(step==2)
            def _():
                gather_z(5,3); gather_z(6,1)
            @pl.when(step==3)
            def _():
                gather_x(4); gather_start(7)
            @pl.when(step==4)
            def _():
                gather_z(6,2)
            @pl.when(step==5)
            def _():
                gather_z(7,1)
            @pl.when(step==6)
            def _():
                gather_z(6,3); gather_z(7,2)
            @pl.when(step==7)
            def _():
                gather_x(5)
        ctx_copy(c,t).start()
        ctxo[loc(c),cols(t)]=ctx[rows(t,c)]
    def stage_b(c):
        ctx_copy(c,1-t).wait_recv()
        x,r=stats(hall[rows(t,c)].astype(F32)+dot(ctxo[loc(c)],whole(wo),NT)+vec[0:1])
        xh[loc(c)]=x
        rst[loc(c)]=jnp.broadcast_to(r,(cr,128))
        hall[rows(t,c)]=(x*vec[1:2]+vec[2:3]).astype(BF)
        ag_copy(3,hall,c,t).start()
    def stage_c(c):
        rs=chunk(c)
        ag_copy(3,hall,c,1-t).wait_recv()
        @pl.loop(0,ff//TF)
        def _(j):
            cs=pl.ds(pl.multiple_of(j*TF,TF),TF)
            u=dot(hall[rs],strip(wup,cs),NN)+upb[:,cs]
            cdf=0.5*(1.0+lax.erf(u*0.5**0.5))
            act[pl.ds(4*c,4),:,cs]=(u*cdf).astype(BF).reshape(4,64,TF)
            slp[rs,cs]=(cdf+u*jnp.exp(-0.5*u*u)*(0.5/math.pi)**0.5).astype(BF)
    def stage_c2(c):
        pch[...]=dot(act[pl.ds(4*c,4)].reshape(cg,ff),whole(wdn),NT)
        split(1,c)
    def stage_d(c):
        rs_copy(1,c).wait_recv()
        x,r=stats(xh[loc(c)]*vec[1:2]+vec[2:3]+part[loc(c)]+rbuf[0,loc(c)].astype(F32)+vec[3:4])
        dy=cl[loc(c)].astype(F32)
        cl[loc(c)]=(x*vec[4:5]+vec[5:6]).astype(BF)
        lo_copy(c).start()
        early[4:5]+=jnp.sum(dy*x,axis=0,keepdims=True)
        early[5:6]+=jnp.sum(dy,axis=0,keepdims=True)
        dx=dy*vec[4:5]
        g=r*(dx-jnp.mean(dx,axis=1,keepdims=True)-x*jnp.mean(dx*x,axis=1,keepdims=True))
        gf[loc(c)]=g
        gb=g.astype(BF)
        early[3:4]+=jnp.sum(gb.astype(F32),axis=0,keepdims=True)
        ball[rows(t,c)]=gb
        ag_copy(4,ball,c,t).start()
        tb[:,rows(t,c)]=gb.T
    def stage_e(c):
        rs=chunk(c)
        ag_copy(4,ball,c,1-t).wait_recv()
        @pl.loop(0,ff//TF)
        def _(j):
            cs=pl.ds(pl.multiple_of(j*TF,TF),TF)
            gu=(dot(ball[rs],strip(wdn,cs),NN)*slp[rs,cs].astype(F32)).astype(BF)
            slp[rs,cs]=gu
            row=pl.ds(8+j*TF//dm,1); cc=pl.ds(pl.multiple_of(j*TF%dm,TF),TF)
            early[row,cc]+=jnp.sum(gu.astype(F32),axis=0,keepdims=True)
        pch[...]=dot(slp[rs],whole(wup),NT)
        split(2,c)
        tb[:,rows(1-t,c)]=ball[rows(1-t,c)].T
        th[:,chunk(c)]=hall[chunk(c)].T
    def stage_f(c):
        rs_copy(2,c).wait_recv()
        dy=gf[loc(c)]+part[loc(c)]+rbuf[1,loc(c)].astype(F32)
        x=xh[loc(c)]; r=rst[loc(c)][:,0:1]
        early[1:2]+=jnp.sum(dy*x,axis=0,keepdims=True)
        early[2:3]+=jnp.sum(dy,axis=0,keepdims=True)
        dx=dy*vec[1:2]
        g=r*(dx-jnp.mean(dx,axis=1,keepdims=True)-x*jnp.mean(dx*x,axis=1,keepdims=True))
        gf[loc(c)]=g
        gb=g.astype(BF)
        early[0:1]+=jnp.sum(gb.astype(F32),axis=0,keepdims=True)
        ga[loc(c)]=gb
        ball[rows(t,c)]=gb
        dcs[loc(c)]=dot(gb,whole(wo),NN).astype(BF)
        dctx_copy(c,t).start()
        dcall[rows(t,c)]=dcs[loc(c),cols(t)]
    def stage_g(c):
        rs=chunk(c)
        dctx_copy(c,1-t).wait_recv()
        @pl.when(c==0)
        def _():
            for i in range(NC): ga_copy(i).start()
        @pl.loop(0,pairs)
        def _(p):
            cq=pl.ds(pl.multiple_of(p*128,128),128); ck=pl.ds(pl.multiple_of(width+p*128,128),128); cv=pl.ds(pl.multiple_of(2*width+p*128,128),128)
            prod=(ctx[rs,cq].astype(F32)*dcall[rs,cq].astype(F32)).T
            dl[0:1]=jnp.sum(prod[0:64],axis=0,keepdims=True)
            dl[1:2]=jnp.sum(prod[64:128],axis=0,keepdims=True)
            for h in (0,1):
                keep=(lane<64) if h==0 else (lane>=64)
                q=jnp.where(keep,qkv[rs,cq]*scale,zero)
                do=jnp.where(keep,dcall[rs,cq],zero)
                st=dot(qkv[:,ck],q,NT)
                pt=jnp.exp2(st*LOG2E-lse[pl.ds(2*p+h,1),rs])
                dpt=dot(qkv[:,cv],do,NT)
                ds=(pt*(dpt-dl[h:h+1])).astype(BF)
                dkv[1,:,cq]+=dot(pt.astype(BF),do,NN)
                dkv[0,:,cq]+=dot(ds,q,NN)
                dqt[h*64:(h+1)*64,:]=dot(kt[p,h*64:(h+1)*64,:],ds,NN)
            qkv[rs,cq]=(dqt[...].T*(HD**-0.5)).astype(BF)
            step=c*pairs+p
            @pl.when(step==0)
            def _():
                add3(0)
                add2(2)
                fetch2(3)
            @pl.when(step==1)
            def _():
                add2(3)
                ecopy(0).start()
            @pl.when(step==4)
            def _():
                eadd(0); ecopy(1).start()
            @pl.when(step==5)
            def _():
                s2(1).wait_send(); s2(2).start()
                fetch3(1)
            @pl.when(step==6)
            def _():
                eadd(1); ecopy(2).start()
            @pl.when(step==7)
            def _():
                sent3(0); add3(1)
            @pl.when(step==8)
            def _():
                eadd(2); ecopy(3).start()
            @pl.when(step==9)
            def _():
                fetchf(0)
            @pl.when(step==10)
            def _():
                finish(0)
                eadd(3); ecopy(4).start()
            @pl.when(step==11)
            def _():
                s2(2).wait_send(); s2(3).start()
                fetch3(2)
            @pl.when(step==12)
            def _():
                for i in range(NC): ga_copy(i).wait_recv()
                for i in range(NC): th[:,i*cg:(i+1)*cg]=ball[i*cg:(i+1)*cg].T
            @pl.when(step==13)
            def _():
                sent3(1); add3(2)
                wgrad(8,4,0,th,ctx,0,base[4])
            @pl.when(step==14)
            def _():
                x_in.start()
            @pl.when(step==15)
            def _():
                fetch2(4)
    def grad_down(c): wgrad(c,c//2,c%2*512,tb,act,c*512,width+ff+c*512)
    def grad_up(c): wgrad(4+c,2+c//2,c%2*512,th,slp,c*512,width+c*512)
    def ga_copy(c):
        return pltpu.make_async_remote_copy(ga.at[loc(c)],ball.at[rows(t,c)],ssem.at[7,c],rsem.at[7,c],device_id=partner,device_id_type=MESH)
    @pl.loop(0,NC)
    def _(c):
        stage_a(c)
        @pl.when(c>0)
        def _(): stage_b(c-1)
    cot_load.wait(); w_out.wait(); x_out.wait()
    gather_done(4); gather_done(5)
    gather_z(7,3)
    @pl.loop(0,NC-1)
    def _(c):
        stage_c(c)
        @pl.when(c==0)
        def _(): stage_b(NC-1)
    gather_x(6); gather_x(7)
    gather_done(6); gather_done(7)
    @pl.loop(0,NC)
    def _(c):
        stage_c2(c)
        @pl.when(c==1)
        def _(): stage_c(NC-1)
    @pl.loop(0,NC)
    def _(c): stage_d(c)
    @pl.loop(0,NC)
    def _(c): stage_e(c)
    piece=ff//2
    base=(width+ff,width+ff+piece,width,width+piece,0,width+2*ff,2*width+2*ff,3*width+2*ff)
    span=(piece,)*4+(width,)*4
    tiles=((0,1),(2,3),(4,5),(6,7),(8,),(9,),(10,),(11,))
    slots2=[wup.at[8:12,:,0:piece],wup.at[12:16,:,0:piece],wup.at[8:12,:,piece:],wup.at[12:16,:,piece:],wup.at[0:4,:,piece:],wup.at[4:8,:,piece:]]
    slots3=[wdn.at[12:16,:,0:piece],wdn.at[12:16,:,piece:],wdn.at[0:4,:,piece:],wdn.at[4:8,:,piece:],wdn.at[8:12,:,piece:]]
    sum2=[slots2[g%6] for g in range(8)]
    sum3=[slots3[g%5] for g in range(8)]
    def s2(g): return remote(sum2[g].at[:,:,0:span[g]],r2.at[g,:,:,0:span[g]],g2s.at[g],g2r.at[g],xp)
    def s3(g,k): return remote(sum3[g].at[(z+k)%4,:,0:span[g]],r3.at[g,3-k,:,0:span[g]],g3s.at[g,k-1],g3r.at[g,k-1],zp[k-1])
    def load2(g): return [pltpu.make_async_copy(dw.at[:,1-x_,core,:,base[g]:base[g]+span[g]],wup.at[0:4,:,0:span[g]],rl.at[0]),
                          pltpu.make_async_copy(r1.at[g,:,1-x_,:,0:span[g]],wup.at[4:8,:,0:span[g]],rl.at[1])]
    def load3(g): return [pltpu.make_async_copy(dw.at[:,x_,core,:,base[g]:base[g]+span[g]],wdn.at[0:4,:,0:span[g]],rl.at[2]),
                         pltpu.make_async_copy(r1.at[g,:,x_,:,0:span[g]],wdn.at[4:8,:,0:span[g]],rl.at[3]),
                         pltpu.make_async_copy(r2.at[g,:,:,0:span[g]],wdn.at[8:12,:,0:span[g]],rl.at[4])]
    def fetch2(g):
        for i in tiles[g]:
            if i>=6: own_tile(i,0).wait()
            pair_tile(i,g,0).wait_recv()
        for l in load2(g): l.start()
    def add2(g):
        for l in load2(g): l.wait()
        @pl.loop(0,4)
        def _(i): sum2[g][i,:,0:span[g]]=(wup[i,:,0:span[g]].astype(F32)+wup[4+i,:,0:span[g]].astype(F32)).astype(BF)
    def fetch3(g):
        s2(g).wait_recv()
        for l in load3(g): l.start()
    def add3(g):
        for l in load3(g): l.wait()
        @pl.loop(0,4)
        def _(i): sum3[g][i,:,0:span[g]]=(wdn[i,:,0:span[g]].astype(F32)+wdn[4+i,:,0:span[g]].astype(F32)+wdn[8+i,:,0:span[g]].astype(F32)).astype(BF)
        for k in (1,2,3): s3(g,k).start()
    def sent3(g):
        for k in (1,2,3): s3(g,k).wait_send()
    def fslot(g,i):
        r=64*(6*(g%2)+i)
        return tb.at[r:r+64,0:span[g]]
    def loadf(g): return [pltpu.make_async_copy(src,fslot(g,i),fl.at[g%2,i]) for i,src in enumerate(
        [dw.at[z,x_,core,:,base[g]:base[g]+span[g]],r1.at[g,z,x_,:,0:span[g]],r2.at[g,z,:,0:span[g]]]+[r3.at[g,k,:,0:span[g]] for k in range(3)])]
    def fetchf(g):
        for k in (1,2,3): s3(g,k).wait_recv()
        for l in loadf(g): l.start()
    def final(g):
        for l in loadf(g): l.wait()
        v=[fslot(g,i)[...].astype(F32) for i in range(6)]
        return v[0]+v[1]+v[2]+v[3]+v[4]+v[5]
    def fin_copy(g):
        return pltpu.make_async_copy(xh.at[64*g:64*g+64,0:span[g]],fin.at[g] if g<4 else go_hbm if g==4 else fin_head.at[g-5],fs.at[g])
    def finish(g):
        xh[64*g:64*g+64,0:span[g]]=final(g)
        fin_copy(g).start()
    zb=[dev(z+1-2*(z%2),x_,core),dev((z+2)%4,x_,core)]
    hops=[sib,xp,zb[0],zb[1],partner]
    def ecopy(i): return remote(eb.at[i],er.at[i],es.at[i],erc.at[i],hops[i])
    def eadd(i):
        ecopy(i).wait_recv()
        b=eb[i,8:16]; c=er[i,8:16]
        if i<4:
            r=lax.broadcasted_iota(jnp.int32,b.shape,0)
            b=jnp.where(r==2,jnp.maximum(b,c),b+c)
        eb[i+1,0:8]=eb[i,0:8]+er[i,0:8]; eb[i+1,8:16]=b
    def lcopy(i): return remote(lb.at[i],lr.at[i],ls.at[i],lrc.at[i],hops[i])
    def ladd(i):
        lcopy(i).wait_recv()
        lb[i+1]=lb[i]+lr[i]
    @pl.loop(0,NC)
    def _(c):
        ag_copy(3,hall,c,t).wait_send()
        ag_copy(4,ball,c,t).wait_send()
    x_in=pltpu.make_async_copy(x_hbm,th,dsem.at[0])
    for c in range(3): grad_down(c)
    grad_down(3)
    fetch2(0)
    wh_in=pltpu.make_async_copy(wh_hbm,act.at[:,:,0:n],dsem.at[1])
    wh_in.start()
    add2(0); s2(0).start()
    @pl.loop(0,NC)
    def _(c):
        stage_f(c)
        grad_up(c)
        @pl.when(c==1)
        def _(): fetch2(1)
        @pl.when(c==2)
        def _(): add2(1)
        @pl.when(c==3)
        def _():
            fetch2(2)
            s2(0).wait_send(); s2(1).start()
            fetch3(0)
    @pl.loop(0,NC)
    def _(c): stage_g(c)
    add2(4)
    s2(3).wait_send(); s2(4).start()
    fetch3(3)
    x_in.wait()
    wgrad(9,5,0,th,qkv,0,base[5])
    sent3(2); add3(3)
    fetchf(1)
    @pl.loop(0,pairs)
    def _(p):
        cq=pl.ds(pl.multiple_of(p*128,128),128); ck=pl.ds(pl.multiple_of(width+p*128,128),128); cv=pl.ds(pl.multiple_of(2*width+p*128,128),128)
        qkv[:,ck]=dkv[0,:,cq].astype(BF)
        qkv[:,cv]=dkv[1,:,cq].astype(BF)
    fetch2(5)
    def ycopy(c): return remote(sbuf.at[0,loc(c)],rbuf.at[0,loc(c)],ssem.at[6,c],rsem.at[6,c],partner)
    wh_in.wait()
    def token_grad(c):
        pch[...]=dot(qkv[chunk(c)],act[:,:,0:n].reshape(dm,n),NT)
        rs_copy(1,c).wait_send()
        sbuf[0,loc(c)]=pch[half(1-t)].astype(BF)
        ycopy(c).start()
        part[loc(c)]=pch[half(t)]
    @pl.loop(0,2)
    def _(c): token_grad(c)
    add2(5)
    s2(4).wait_send(); s2(5).start()
    wgrad(10,6,0,th,qkv,width,base[6])
    fetch3(4)
    wgrad(11,7,0,th,qkv,2*width,base[7])
    fetch2(6)
    @pl.loop(2,NC)
    def _(c): token_grad(c)
    add2(6)
    s2(5).wait_send(); s2(6).start()
    fetch2(7)
    sent3(3); add3(4)
    fetch3(5)
    lb[0,0:1,0:width]=jnp.sum(qkv[:,0:width].astype(F32),axis=0,keepdims=True)
    lb[0,0:1,width:2*width]=jnp.sum(qkv[:,2*width:].astype(F32),axis=0,keepdims=True)
    lcopy(0).start()
    finish(1)
    add2(7)
    eadd(4)
    sent3(4); add3(5)
    s2(6).wait_send(); s2(7).start()
    fetch3(6)
    ladd(0); lcopy(1).start()
    fetchf(2)
    smalls[...]=eb[5]
    pk=eb[4,10:11,0:width]
    head=lax.broadcasted_iota(jnp.int32,(1,width),1)//HD
    limit=jnp.zeros((1,width),F32)
    for h in range(width//HD): limit=jnp.where(head==h,lim[h],limit)
    sc=jnp.sqrt(limit/jnp.maximum(pk,limit))
    ctxo[0:64,0:width]=(wq[...].astype(F32)*sc).astype(BF)
    ctxo[64:128,0:width]=(wk[...].astype(F32)*sc).astype(BF)
    clips=[pltpu.make_async_copy(ctxo.at[0:64,0:width],qc_hbm,fs.at[8]),pltpu.make_async_copy(ctxo.at[64:128,0:width],kc_hbm,fs.at[9])]
    for c in clips: c.start()
    smalls[11:12,0:width]=row(v_qb)*sc
    finish(2)
    ladd(1); lcopy(2).start()
    fetchf(3)
    sent3(5); add3(6)
    fetch3(7)
    finish(3)
    fetchf(4)
    ladd(2); lcopy(3).start()
    @pl.loop(0,NC)
    def _(c): lo_copy(c).wait()
    finish(4)
    sent3(6); add3(7)
    fetchf(5)
    def tg_copy(c): return pltpu.make_async_copy(cl.at[loc(c)],tg_hbm.at[loc(c)],losem.at[c])
    @pl.loop(0,NC)
    def _(c):
        ycopy(c).wait_recv()
        cl[loc(c)]=(gf[loc(c)]+part[loc(c)]+rbuf[0,loc(c)].astype(F32)).astype(BF)
        tg_copy(c).start()
    ladd(3)
    smalls[12:13]=lb[4,0:1]
    finish(5)
    fetchf(6)
    finish(6)
    fetchf(7)
    finish(7)
    o_swap.wait_send()
    for g in range(8):
        fin_copy(g).wait()
    for i in (10,11): pair_tile(i,0,0).wait_send()
    s2(7).wait_send()
    sent3(7)
    for c in clips: c.wait()
    for i in range(5): ecopy(i).wait_send()
    for i in range(4): lcopy(i).wait_send()
    @pl.loop(0,NC)
    def _(c):
        tg_copy(c).wait()
        ctx_copy(c,t).wait_send(); dctx_copy(c,t).wait_send(); tok_copy(c).wait_send()
        rs_copy(2,c).wait_send(); ycopy(c).wait_send()
        ga_copy(c).wait_send()

def main_call(shards,tok,cot,vectors,lim,cid):
    V=pl.BlockSpec(memory_space=pltpu.VMEM); A=pl.BlockSpec(memory_space=pl.ANY)
    width=shards[0].shape[1]; ff=shards[4].shape[1]; own,dm=tok.shape; rows=2*own; n=3*width; cr=own//NC; wide=2*width; piece=ff//2
    S=jax.ShapeDtypeStruct; M=pltpu.VMEM; D=pltpu.SemaphoreType.DMA
    return pl.pallas_call(main_kernel,
      out_shape=(S((own,dm),BF),S((own,dm),BF),S((4,64,piece),F32),S((3,64,width),F32),S((64,width),F32),S((64,width),BF),S((64,width),BF),S((16,dm),F32),
        S((4,2,2,64,width+2*ff+n),BF),S((8,4,2,64,piece),BF),S((8,4,64,piece),BF),S((8,3,64,piece),BF),S((dm,rows),BF),S((16,64,n),BF)),
      in_specs=[V]*6+[A,A]+[V]*9+[pl.BlockSpec(memory_space=pltpu.SMEM)],out_specs=(A,)*7+(V,)+(A,)*6,
      scratch_shapes=[M((1,n),F32),M((8,dm),F32),M((1,ff),F32),M((own,dm),F32),M((6,16,dm),F32),M((5,16,dm),F32),M((5,8,dm),F32),M((4,8,dm),F32),
        M((64,n+wide+2*ff),BF),M((rows,n),BF),M((width//HD,80,rows),BF),M((width//128,128,rows),BF),M((rows,width),BF),M((own,wide),BF),M((width//HD,rows),F32),M((own,dm),BF),
        M((16,64,wide),BF),M((16,64,ff),BF),M((16,64,ff),BF),
        M((own,dm),F32),M((own,128),F32),
        M((rows,dm),BF),M((16,64,ff),BF),M((rows,ff),BF),M((rows,dm),BF),M((own,dm),BF),M((own,wide),BF),M((rows,width),BF),
        M((own,dm),F32),M((2*cr,dm),F32),M((2,128,2*cr),F32),M((128,2*cr),F32),M((8,2*cr),F32),M((2,rows,width),F32),
        M((2,own,dm),BF),M((2,own,dm),BF),
        M((dm,rows),BF),M((dm,rows),BF),M((2,4,2,2,64,512),BF),
        D((7,)),D((NC,)),D((2,)),D((2,)),D((8,NC)),D((8,NC)),D((5,)),D((12,)),D((12,)),D((8,)),D((8,)),D((8,3)),D((8,3)),
        D((NC+1,)),D((NC+1,)),D((8,2,3)),D((8,2,3)),D((8,4)),D((8,4)),D((8,8)),D((8,8)),
        D((5,)),D((5,)),D((4,)),D((4,)),D((2,6)),D((10,))],
      compiler_params=pltpu.CompilerParams(collective_id=cid,has_side_effects=True,vmem_limit_bytes=61*2**20),
      name="main")(*shards,tok,cot,*vectors,lim)

def finish_kernel(lo,tg,fin,fin_head,go,qc,kc,smalls,
                  lo_,tg_,gq_,gk_,gv_,go_,gu_,gd_,qc_,kc_,qb_,vb_,ob_,g1_,b1_,ub_,db_,g2_,b2_,pk_,qbc_,h_lo,h_tg,h_fin,h_head,h_go,h_qc,h_kc,isem,sem):
    piece=fin.shape[2]
    ins=[pltpu.make_async_copy(a,b,isem.at[i]) for i,(a,b) in enumerate(((lo,h_lo),(tg,h_tg),(fin,h_fin),(fin_head,h_head),(go,h_go),(qc,h_qc),(kc,h_kc)))]
    outs=[[(h_lo,lo_)],[(h_tg,tg_)],[(h_fin.at[0],gd_.at[:,0:piece]),(h_fin.at[1],gd_.at[:,piece:]),(h_fin.at[2],gu_.at[:,0:piece]),(h_fin.at[3],gu_.at[:,piece:])],
          [(h_head.at[0],gq_),(h_head.at[1],gk_),(h_head.at[2],gv_)],[(h_go,go_)],[(h_qc,qc_)],[(h_kc,kc_)]]
    for c in ins: c.start()
    width=qb_.shape[0]; dm=ob_.shape[0]
    def line(v): return v.reshape(v.shape[1])
    qb_[...]=line(smalls[12:13,0:width]); vb_[...]=line(smalls[12:13,width:2*width])
    for i,o in enumerate((ob_,g1_,b1_,db_,g2_,b2_)): o[...]=line(smalls[i:i+1])
    ub_[0:dm]=line(smalls[8:9]); ub_[dm:2*dm]=line(smalls[9:10])
    for h in range(pk_.shape[0]): pk_[h]=jnp.max(smalls[10:11,h*HD:(h+1)*HD])
    qbc_[...]=line(smalls[11:12,0:width]).astype(BF)
    moved=[]
    for a,group in zip(ins,outs):
        a.wait()
        for src,dst in group:
            c=pltpu.make_async_copy(src,dst,sem.at[len(moved)])
            c.start()
            moved.append(c)
    for c in moved: c.wait()

def finish_call(big,smalls,heads):
    V=pl.BlockSpec(memory_space=pltpu.VMEM); A=pl.BlockSpec(memory_space=pl.ANY); S=jax.ShapeDtypeStruct
    lo,tg,fin,fin_head,go,qc,kc=big
    width=go.shape[1]; piece=fin.shape[2]; ff=2*piece; dm=tg.shape[1]
    return pl.pallas_call(finish_kernel,
      out_shape=(S(lo.shape,BF),S(tg.shape,BF))+(S((64,width),F32),)*4+(S((64,ff),F32),)*2+(S((64,width),BF),)*2
        +tuple(S((k,),F32) for k in (width,width,dm,dm,dm,ff,dm,dm,dm,heads))+(S((width,),BF),),
      in_specs=[A]*7+[V],out_specs=(A,)*10+(V,)*9+(pl.BlockSpec(memory_space=pltpu.SMEM),V),
      scratch_shapes=[pltpu.VMEM(a.shape,a.dtype) for a in big]+[pltpu.SemaphoreType.DMA((7,)),pltpu.SemaphoreType.DMA((12,))],
      compiler_params=pltpu.CompilerParams(vmem_limit_bytes=61*2**20),name="finish")(*big,smalls)

def per_device_pair(tokens,query_weight,query_bias,key_weight,value_weight,value_bias,out_weight,out_bias,first_gain,first_shift,
    up_weight,up_bias,down_weight,down_bias,second_gain,second_shift,cotangent,clip_limit):
    shards=(query_weight,key_weight,value_weight,out_weight.T,up_weight,down_weight.T)
    vectors=(out_bias,first_gain,first_shift,down_bias,second_gain,second_shift,up_bias,query_bias,value_bias)
    res=main_call(shards,tokens,cotangent,vectors,clip_limit,1)
    lo,tg,gq,gk,gv,go,gu,gd,qc,kc,qb,vb,ob,g1,b1,ub,db,g2,b2,pk,qbc=finish_call(res[:7],res[7],clip_limit.shape[0])
    return (lo,tg,gq,qb,gk,gv,vb,go.T,ob,g1,b1,gu,ub,gd.T,db,g2,b2,pk,qc,qbc,kc)


def layer(*args):
    paired = lax.axis_size("dp") == 16 and lax.axis_size("tensor") == 2 and 2 * args[0].shape[0] == LEN
    return per_device_pair(*args) if paired else per_device(*args)


def solution(mesh):
    in_specs = (
        P(("dp", "tensor"), None),
        P("dp", "tensor"),
        P("tensor"),
        P("dp", "tensor"),
        P("dp", "tensor"),
        P("tensor"),
        P("tensor", "dp"),
        P(),
        P(),
        P(),
        P("dp", "tensor"),
        P("tensor"),
        P("tensor", "dp"),
        P(),
        P(),
        P(),
        P(("dp", "tensor"), None),
        P("tensor"),
    )
    out_specs = (
        P(("dp", "tensor"), None),
        P(("dp", "tensor"), None),
        P("dp", "tensor"),
        P("tensor"),
        P("dp", "tensor"),
        P("dp", "tensor"),
        P("tensor"),
        P("tensor", "dp"),
        P(),
        P(),
        P(),
        P("dp", "tensor"),
        P("tensor"),
        P("tensor", "dp"),
        P(),
        P(),
        P(),
        P("tensor"),
        P("dp", "tensor"),
        P("tensor"),
        P("dp", "tensor"),
    )
    return jax.shard_map(
        layer, mesh=mesh, in_specs=in_specs, out_specs=out_specs, check_vma=False
    )
```

```python
import functools
import math

import jax
import jax.numpy as jnp
from jax import lax
from jax.experimental import pallas as pl
from jax.experimental.pallas import tpu as pltpu
from jax.sharding import PartitionSpec as P

HD = 64
LEN = 1024
QB = 512


def layer_norm(values, gain, shift):
    center = values - jnp.mean(values, axis=-1, keepdims=True)
    spread = jnp.mean(center * center, axis=-1, keepdims=True)
    return center * lax.rsqrt(spread + EPSILON) * gain + shift


def gelu_slope(upper):
    normal_cdf = 0.5 * (1.0 + lax.erf(upper * 0.5**0.5))
    return normal_cdf + upper * jnp.exp(-0.5 * upper * upper) * (0.5 / math.pi) ** 0.5


def contract_rows(left, right):
    return lax.dot_general(
        left, right, (((0,), (0,)), ((), ())), preferred_element_type=jnp.float32
    )


def contract_cols(left, right):
    return lax.dot_general(
        left, right, (((1,), (1,)), ((), ())), preferred_element_type=jnp.float32
    )


def per_device(
    tokens,
    query_weight,
    query_bias,
    key_weight,
    value_weight,
    value_bias,
    out_weight,
    out_bias,
    first_gain,
    first_shift,
    up_weight,
    up_bias,
    down_weight,
    down_bias,
    second_gain,
    second_shift,
    cotangent,
    clip_limit,
):
    query_full, key_full, value_full, out_full, up_full, down_full = (
        lax.all_gather(query_weight, "dp", axis=0, tiled=True),
        lax.all_gather(key_weight, "dp", axis=0, tiled=True),
        lax.all_gather(value_weight, "dp", axis=0, tiled=True),
        lax.all_gather(out_weight, "dp", axis=1, tiled=True),
        lax.all_gather(up_weight, "dp", axis=0, tiled=True),
        lax.all_gather(down_weight, "dp", axis=1, tiled=True),
    )
    width = query_full.shape[1]
    hidden_width = up_full.shape[1]
    heads_here = width // HD
    score_scale = HD ** (-0.5)
    joint_weight = jnp.concatenate([query_full, key_full, value_full], axis=1)
    gathered = lax.all_gather(tokens, "tensor", axis=0, tiled=True)
    group_rows = gathered.shape[0]
    seq_count = group_rows // LEN
    block_count = LEN // QB
    projected = jnp.dot(gathered, joint_weight, preferred_element_type=jnp.float32)
    queries = (projected[:, :width] + query_bias.astype(jnp.float32)).astype(jnp.bfloat16)
    keyset = projected[:, width : 2 * width].astype(jnp.bfloat16)
    valset = (projected[:, 2 * width :] + value_bias.astype(jnp.float32)).astype(jnp.bfloat16)
    query_seq = queries.reshape(seq_count, LEN, heads_here, HD)
    key_seq = keyset.reshape(seq_count, LEN, heads_here, HD)
    value_seq = valset.reshape(seq_count, LEN, heads_here, HD)

    def attend_block(block_id):
        seq_id = block_id // block_count
        row_start = block_id % block_count * QB
        query_rows = lax.dynamic_slice_in_dim(
            lax.dynamic_index_in_dim(query_seq, seq_id, 0, False), row_start, QB, 0
        )
        key_rows = lax.dynamic_index_in_dim(key_seq, seq_id, 0, False)
        value_rows = lax.dynamic_index_in_dim(value_seq, seq_id, 0, False)
        logits = (
            jnp.einsum("qhd,khd->hqk", query_rows, key_rows, preferred_element_type=jnp.float32)
            * score_scale
        )
        row_max = jnp.max(logits, axis=2, keepdims=True)
        exponent = jnp.exp(logits - row_max)
        totals = jnp.sum(exponent, axis=2, keepdims=True)
        probs_low = (exponent / totals).astype(jnp.bfloat16)
        context_rows = jnp.einsum(
            "hqk,khd->qhd", probs_low, value_rows, preferred_element_type=jnp.float32
        )
        return (
            context_rows.reshape(QB, width).astype(jnp.bfloat16),
            (row_max + jnp.log(totals))[:, :, 0],
            jnp.max(row_max, axis=(1, 2)),
        )

    context_blocks, log_totals, block_peaks = lax.map(
        attend_block, jnp.arange(seq_count * block_count)
    )
    context = context_blocks.reshape(group_rows, width)
    logit_peak = lax.pmax(jnp.max(block_peaks, axis=0), "dp")
    attention = lax.psum_scatter(
        jnp.dot(context, out_full, preferred_element_type=jnp.float32).astype(jnp.bfloat16),
        "tensor",
        scatter_dimension=0,
        tiled=True,
    ).astype(jnp.float32) + out_bias.astype(jnp.float32)
    first_resid = tokens.astype(jnp.float32) + attention
    hidden, first_pull = jax.vjp(
        layer_norm, first_resid, first_gain.astype(jnp.float32), first_shift.astype(jnp.float32)
    )
    hidden_all = lax.all_gather(hidden.astype(jnp.bfloat16), "tensor", axis=0, tiled=True)
    upper = jnp.dot(hidden_all, up_full, preferred_element_type=jnp.float32) + up_bias.astype(
        jnp.float32
    )
    acted = jax.nn.gelu(upper, approximate=False).astype(jnp.bfloat16)
    branch = lax.psum_scatter(
        jnp.dot(acted, down_full, preferred_element_type=jnp.float32).astype(jnp.bfloat16),
        "tensor",
        scatter_dimension=0,
        tiled=True,
    ).astype(jnp.float32) + down_bias.astype(jnp.float32)
    normed, second_pull = jax.vjp(
        layer_norm,
        hidden + branch,
        second_gain.astype(jnp.float32),
        second_shift.astype(jnp.float32),
    )
    layer_out = normed.astype(jnp.bfloat16)
    grad_second, second_gain_grad, second_shift_grad = second_pull(cotangent.astype(jnp.float32))
    grad_branch = grad_second.astype(jnp.bfloat16)
    down_bias_grad = jnp.sum(grad_branch, axis=0, dtype=jnp.float32)
    branch_all = lax.all_gather(grad_branch, "tensor", axis=0, tiled=True)
    grad_acted = contract_cols(branch_all, down_full)
    down_weight_grad = contract_rows(acted, branch_all)
    grad_upper = (grad_acted * gelu_slope(upper)).astype(jnp.bfloat16)
    up_bias_grad = jnp.sum(grad_upper, axis=0, dtype=jnp.float32)
    up_weight_grad = contract_rows(hidden_all, grad_upper)
    grad_hidden = grad_second + lax.psum_scatter(
        contract_cols(grad_upper, up_full).astype(jnp.bfloat16),
        "tensor",
        scatter_dimension=0,
        tiled=True,
    ).astype(jnp.float32)
    grad_first, first_gain_grad, first_shift_grad = first_pull(grad_hidden)
    grad_attn = grad_first.astype(jnp.bfloat16)
    out_bias_grad = jnp.sum(grad_attn, axis=0, dtype=jnp.float32)
    attn_all = lax.all_gather(grad_attn, "tensor", axis=0, tiled=True)
    grad_context = contract_cols(attn_all, out_full).astype(jnp.bfloat16)
    out_weight_grad = contract_rows(context, attn_all)
    query_blocks = queries.reshape(seq_count, block_count, QB, heads_here, HD)
    grad_blocks = grad_context.reshape(seq_count, block_count, QB, heads_here, HD)
    log_blocks = log_totals.reshape(seq_count, block_count, heads_here, QB)

    def sequence_back(item):
        query_part, grad_part, log_part, key_rows, value_rows = item

        def block_back(carry, piece):
            key_acc, value_acc = carry
            query_rows, grad_rows, log_rows = piece
            logits = (
                jnp.einsum("qhd,khd->hqk", query_rows, key_rows, preferred_element_type=jnp.float32)
                * score_scale
            )
            probs = jnp.exp(logits - log_rows[:, :, None])
            probs_low = probs.astype(jnp.bfloat16)
            value_acc = value_acc + jnp.einsum(
                "hqk,qhd->khd", probs_low, grad_rows, preferred_element_type=jnp.float32
            )
            grad_probs = jnp.einsum(
                "qhd,khd->hqk", grad_rows, value_rows, preferred_element_type=jnp.float32
            )
            inner = jnp.sum(probs * grad_probs, axis=2, keepdims=True)
            grad_logits = (probs * (grad_probs - inner)).astype(jnp.bfloat16)
            grad_query = (
                jnp.einsum(
                    "hqk,khd->qhd", grad_logits, key_rows, preferred_element_type=jnp.float32
                )
                * score_scale
            )
            key_acc = (
                key_acc
                + jnp.einsum(
                    "hqk,qhd->khd", grad_logits, query_rows, preferred_element_type=jnp.float32
                )
                * score_scale
            )
            return ((key_acc, value_acc), grad_query.astype(jnp.bfloat16))

        empty = jnp.zeros((LEN, heads_here, HD), jnp.float32)
        (key_acc, value_acc), grad_query_rows = lax.scan(
            block_back, (empty, empty), (query_part, grad_part, log_part)
        )
        return (grad_query_rows, key_acc.astype(jnp.bfloat16), value_acc.astype(jnp.bfloat16))

    grad_queries_all, grad_keys_all, grad_values_all = lax.map(
        sequence_back, (query_blocks, grad_blocks, log_blocks, key_seq, value_seq)
    )
    grad_joint = jnp.concatenate(
        [
            grad_queries_all.reshape(group_rows, width),
            grad_keys_all.reshape(group_rows, width),
            grad_values_all.reshape(group_rows, width),
        ],
        axis=1,
    )
    joint_grad = contract_rows(gathered, grad_joint)
    query_weight_grad = joint_grad[:, :width]
    key_weight_grad = joint_grad[:, width : 2 * width]
    value_weight_grad = joint_grad[:, 2 * width :]
    query_bias_grad = jnp.sum(grad_joint[:, :width], axis=0, dtype=jnp.float32)
    value_bias_grad = jnp.sum(grad_joint[:, 2 * width :], axis=0, dtype=jnp.float32)
    tokens_grad = (
        grad_first
        + lax.psum_scatter(
            contract_cols(grad_joint, joint_weight).astype(jnp.bfloat16),
            "tensor",
            scatter_dimension=0,
            tiled=True,
        ).astype(jnp.float32)
    ).astype(jnp.bfloat16)
    (
        query_weight_grad,
        key_weight_grad,
        value_weight_grad,
        out_weight_grad,
        up_weight_grad,
        down_weight_grad,
    ) = (
        lax.psum_scatter(
            query_weight_grad.astype(jnp.bfloat16), "dp", scatter_dimension=0, tiled=True
        ).astype(jnp.float32),
        lax.psum_scatter(
            key_weight_grad.astype(jnp.bfloat16), "dp", scatter_dimension=0, tiled=True
        ).astype(jnp.float32),
        lax.psum_scatter(
            value_weight_grad.astype(jnp.bfloat16), "dp", scatter_dimension=0, tiled=True
        ).astype(jnp.float32),
        lax.psum_scatter(
            out_weight_grad.astype(jnp.bfloat16), "dp", scatter_dimension=1, tiled=True
        ).astype(jnp.float32),
        lax.psum_scatter(
            up_weight_grad.astype(jnp.bfloat16), "dp", scatter_dimension=0, tiled=True
        ).astype(jnp.float32),
        lax.psum_scatter(
            down_weight_grad.astype(jnp.bfloat16), "dp", scatter_dimension=1, tiled=True
        ).astype(jnp.float32),
    )
    tensor_place = lax.axis_index("tensor")
    model_width = out_bias.shape[0]
    query_spread = lax.dynamic_update_slice_in_dim(
        jnp.zeros((model_width,), jnp.float32), query_bias_grad, tensor_place * width, 0
    )
    value_spread = lax.dynamic_update_slice_in_dim(
        jnp.zeros((model_width,), jnp.float32), value_bias_grad, tensor_place * width, 0
    )
    up_spread = lax.dynamic_update_slice_in_dim(
        jnp.zeros((hidden_width * lax.axis_size("tensor"),), jnp.float32),
        up_bias_grad,
        tensor_place * hidden_width,
        0,
    )
    (
        query_spread,
        value_spread,
        up_spread,
        out_bias_grad,
        down_bias_grad,
        first_gain_grad,
        first_shift_grad,
        second_gain_grad,
        second_shift_grad,
    ) = lax.psum(
        (
            query_spread,
            value_spread,
            up_spread,
            out_bias_grad,
            down_bias_grad,
            first_gain_grad,
            first_shift_grad,
            second_gain_grad,
            second_shift_grad,
        ),
        ("dp", "tensor"),
    )
    query_bias_grad = lax.dynamic_slice_in_dim(query_spread, tensor_place * width, width, 0)
    value_bias_grad = lax.dynamic_slice_in_dim(value_spread, tensor_place * width, width, 0)
    up_bias_grad = lax.dynamic_slice_in_dim(up_spread, tensor_place * hidden_width, hidden_width, 0)
    factor = clip_limit / jnp.maximum(logit_peak, clip_limit)
    column_scale = jnp.repeat(jnp.sqrt(factor), HD)
    query_clipped = (query_weight.astype(jnp.float32) * column_scale).astype(jnp.bfloat16)
    query_bias_clipped = (query_bias.astype(jnp.float32) * column_scale).astype(jnp.bfloat16)
    key_clipped = (key_weight.astype(jnp.float32) * column_scale).astype(jnp.bfloat16)
    return (
        layer_out,
        tokens_grad,
        query_weight_grad,
        query_bias_grad,
        key_weight_grad,
        value_weight_grad,
        value_bias_grad,
        out_weight_grad,
        out_bias_grad,
        first_gain_grad,
        first_shift_grad,
        up_weight_grad,
        up_bias_grad,
        down_weight_grad,
        down_bias_grad,
        second_gain_grad,
        second_shift_grad,
        logit_peak,
        query_clipped,
        query_bias_clipped,
        key_clipped,
    )


LOG2E=1.4426950408889634
NT=(((1,),(1,)),((),()))
NN=(((1,),(0,)),((),()))
F32=jnp.float32
BF=jnp.bfloat16
MESH=pl.DeviceIdType.MESH
EPSILON=1e-5
NC=4


def dot(a,b,dims):
    return lax.dot_general(a,b,dims,preferred_element_type=jnp.float32)


def greet(partner):
    barrier=pltpu.get_barrier_semaphore()
    pl.semaphore_signal(barrier,inc=1,device_id=partner,device_id_type=MESH)
    pl.semaphore_wait(barrier,1)


def main_kernel(wq,wk,wv,wos,wu,wds,tok,cot_hbm,v_ob,v_g1,v_b1,v_db,v_g2,v_b2,v_ub,v_qb,v_vb,lim,
               lo_hbm,tg_hbm,fin,fin_head,go_hbm,qc_hbm,kc_hbm,smalls,dw,r1,r2,r3,x_hbm,wh_hbm,
               bias,vec,upb,gf,eb,er,lb,lr,sh,qkv,vt,kt,ctx,ctxo,lse,cl,wo,wup,wdn,xh,rst,hall,act,slp,ball,ga,dcs,dcall,part,pch,ctt,dqt,dl,dkv,sbuf,rbuf,tb,th,stage,
               lsem,losem,dsem,osem,ssem,rsem,rl,g1s,g1r,g2s,g2r,g3s,g3r,ts,tr,azs,azr,axs,axr,acs,acr,es,erc,ls,lrc,fl,fs):
    d=lax.axis_index("dp"); t=lax.axis_index("tensor")
    partner=(d,1-t)
    core=d%2; x_=(d//2)%2; z=d//4
    def dev(z_,xx,c_): return ((z_*2+xx)*2+c_,t)
    sib=dev(z,x_,1-core); xp=dev(z,1-x_,core); zp=[dev((z+k)%4,x_,core) for k in (1,2,3)]
    own,dm=tok.shape; cr=own//NC; cg=2*cr; rows_all=2*own; width=ctx.shape[1]; ff=wup.shape[2]; wide=wo.shape[2]; pairs=width//128
    def local(src,dst,i): return pltpu.make_async_copy(src,dst,lsem.at[i])
    def remote(src,dst,a,b,p): return pltpu.make_async_remote_copy(src,dst,a,b,device_id=p,device_id_type=MESH)
    cot_load=local(cot_hbm,cl,0)
    cot_load.start()
    barrier=pltpu.get_barrier_semaphore()
    n=3*width
    def row(v): return v[...].astype(F32).reshape(1,v.shape[0])
    sh[:,0:width]=wq[...]; sh[:,width:2*width]=wk[...]; sh[:,2*width:n]=wv[...]
    everyone=[partner,sib,xp]+zp
    for p in everyone: pl.semaphore_signal(barrier,inc=1,device_id=p,device_id_type=MESH)
    def chunk(c): return pl.ds(pl.multiple_of(c*cg,cg),cg)
    def rows(rank,c): return pl.ds(pl.multiple_of(c*cg+rank*cr,cr),cr)
    def half(rank): return pl.ds(pl.multiple_of(rank*cr,cr),cr)
    def loc(c): return pl.ds(pl.multiple_of(c*cr,cr),cr)
    def rs_copy(k,c):
        return pltpu.make_async_remote_copy(sbuf.at[k-1,loc(c)],rbuf.at[k-1,loc(c)],ssem.at[k,c],rsem.at[k,c],device_id=partner,device_id_type=MESH)
    def ag_copy(k,buf,c,rank):
        return pltpu.make_async_remote_copy(buf.at[rows(rank,c)],buf.at[rows(rank,c)],ssem.at[k,c],rsem.at[k,c],device_id=partner,device_id_type=MESH)
    def cols(rank): return pl.ds(pl.multiple_of(rank*width,128),width)
    def ctx_copy(c,rank):
        return pltpu.make_async_remote_copy(ctx.at[rows(1-rank,c)],ctxo.at[loc(c),cols(rank)],ssem.at[0,c],rsem.at[0,c],device_id=partner,device_id_type=MESH)
    def dctx_copy(c,rank):
        return pltpu.make_async_remote_copy(dcs.at[loc(c),cols(1-rank)],dcall.at[rows(rank,c)],ssem.at[5,c],rsem.at[5,c],device_id=partner,device_id_type=MESH)
    early=eb.at[0]
    early[...]=jnp.zeros((16,dm),F32)
    early[10:11]=jnp.full((1,dm),-jnp.inf,F32)
    lb[0]=jnp.zeros((8,dm),F32)
    def whole(w): return w[...].reshape(dm,w.shape[2])
    def strip(w,cs): return w[:,:,cs].reshape(dm,TF)
    dkv[...]=jnp.zeros_like(dkv)
    lane=lax.broadcasted_iota(jnp.int32,(1,128),1)
    scale=jnp.bfloat16(HD**-0.5); zero=jnp.bfloat16(0)
    q4=ff//2
    groups=[(act,0,0,width),(act,width,width,width),(act,2*width,2*width,width),(wo,0,n,wide),
            (wup,0,n+wide,q4),(wup,q4,n+wide+q4,q4),(wdn,0,n+wide+ff,q4),(wdn,q4,n+wide+ff+q4,q4)]
    def block(z_,xx): return (z_*2+xx)*2+core
    me=block(z,x_)
    def place(g,b):
        buf,c0,_,nc=groups[g]
        return buf.at[b,:,c0:c0+nc]
    def shard(g): return sh.at[:,groups[g][2]:groups[g][2]+groups[g][3]]
    up=dev(jnp.minimum(z+1,3),x_,core); down=dev(jnp.maximum(z-1,0),x_,core)
    def z_hop(g,way,j,b): return remote(shard(g) if j==1 else place(g,b),place(g,b),azs.at[g,way,j-1],azr.at[g,way,j-1],up if way==0 else down)
    def x_hop(g,zz,own_): return remote(shard(g) if own_ else place(g,block(zz,x_)),place(g,block(zz,x_)),axs.at[g,zz],axr.at[g,zz],xp)
    def x_land(g,zz): return remote(place(g,block(zz,1-x_)),place(g,block(zz,1-x_)),axs.at[g,zz],axr.at[g,zz],xp)
    def c_hop(g,xx,zz,b,own_): return remote(shard(g) if own_ else place(g,b),place(g,b),acs.at[g,4*xx+zz],acr.at[g,4*xx+zz],sib)
    def gather_start(g):
        buf,c0,s0,nc=groups[g]
        @pl.when(z<3)
        def _(): z_hop(g,0,1,me).start()
        @pl.when(z>0)
        def _(): z_hop(g,1,1,me).start()
        x_hop(g,z,True).start()
        c_hop(g,0,z,me,True).start()
        buf[me,:,c0:c0+nc]=sh[:,s0:s0+nc]
    def gather_z(g,j):
        for way in (0,1):
            here=(z>=j) if way==0 else (z+j<=3)
            zz=jnp.maximum(z-j,0) if way==0 else jnp.minimum(z+j,3)
            b=block(zz,x_)
            @pl.when(here)
            def _():
                z_hop(g,way,j,b).wait_recv()
                x_hop(g,zz,False).start()
                c_hop(g,0,zz,b,False).start()
            if j<3:
                @pl.when(here & ((z<3) if way==0 else (z>0)))
                def _(): z_hop(g,way,j+1,b).start()
    def gather_x(g):
        for zz in range(4):
            x_land(g,zz).wait_recv()
            c_hop(g,1,zz,block(zz,1-x_),False).start()
    def gather_done(g):
        for xx in (0,1):
            for zz in range(4):
                b=block(zz,x_)
                c_hop(g,xx,zz,b,False).wait_recv()
                c_hop(g,xx,zz,b,False).wait_send()
        for zz in range(4): x_land(g,zz).wait_send()
        for j in (1,2,3):
            @pl.when((z>=j-1) & (z<3))
            def _(): z_hop(g,0,j,me).wait_send()
            @pl.when((z+j-1<=3) & (z>0))
            def _(): z_hop(g,1,j,me).wait_send()
    own_copies=[local(tok.at[c*cr:(c+1)*cr],hall.at[rows(t,c)],1+c) for c in range(NC)]
    for c in own_copies: c.start()
    pl.semaphore_wait(barrier,len(everyone))
    gather_start(0); gather_start(1)
    def tok_copy(c): return remote(tok.at[loc(c)],hall.at[rows(t,c)],ts.at[c],tr.at[c],partner)
    def mine_o(rank): return sh.at[:,pl.ds(pl.multiple_of(n+rank*width,128),width)]
    o_swap=remote(mine_o(t),mine_o(t),ts.at[NC],tr.at[NC],partner)
    sh[:,pl.ds(pl.multiple_of(n+t*width,128),width)]=wos[...]
    o_swap.start()
    @pl.loop(0,NC)
    def _(c): tok_copy(c).start()
    sh[:,n+wide:n+wide+ff]=wu[...]
    sh[:,n+wide+ff:]=wds[...]
    for i,v in enumerate((v_ob,v_g1,v_b1,v_db,v_g2,v_b2)): vec[i:i+1]=row(v)
    upb[...]=row(v_ub)
    bias[...]=jnp.zeros_like(bias)
    bias[:,0:width]=row(v_qb); bias[:,2*width:]=row(v_vb)
    gather_start(2)
    gather_z(0,1)
    gather_z(1,1); gather_z(0,2)
    gather_z(2,1); o_swap.wait_recv(); gather_start(3)
    gather_z(1,2); gather_z(0,3)
    gather_start(4)
    gather_z(2,2); gather_z(1,3)
    gather_x(0); gather_z(3,1); gather_z(2,3)
    gather_x(1); gather_z(3,2); gather_z(4,1)
    gather_start(5)
    gather_x(2); gather_z(3,3); gather_z(4,2)
    for g in range(3): gather_done(g)
    for c in own_copies: c.wait()
    TF=512
    @pl.loop(0,NC)
    def _(c):
        tok_copy(c).wait_recv()
        @pl.loop(0,n//TF)
        def _(j):
            cs=pl.ds(pl.multiple_of(j*TF,TF),TF)
            qkv[chunk(c),cs]=(dot(hall[chunk(c)],strip(act,cs),NN)+bias[:,cs]).astype(BF)
        th[:,chunk(c)]=hall[chunk(c)].T
        @pl.when(c==0)
        def _(): gather_z(4,3)
        @pl.when(c==1)
        def _():
            gather_x(3); gather_z(5,1)
            gather_start(6)
        @pl.when(c==3)
        def _():
            gather_z(5,2); gather_done(3)
    x_out=local(th,x_hbm,5); w_out=local(act.at[:,:,0:n],wh_hbm,6)
    x_out.start(); w_out.start()
    ones=jnp.where(lax.broadcasted_iota(jnp.int32,(16,rows_all),0)==0,1.0,0.0).astype(BF)
    @pl.loop(0,pairs)
    def _(p):
        ck=pl.multiple_of(width+p*128,128); cv=pl.multiple_of(2*width+p*128,128)
        kt[p]=qkv[:,pl.ds(ck,128)].T
        v=qkv[:,pl.ds(cv,128)].T
        vt[2*p,0:64]=v[0:64]; vt[2*p,64:80]=ones
        vt[2*p+1,0:64]=v[64:128]; vt[2*p+1,64:80]=ones
    gather_z(6,1)
    def split(k,c):
        sbuf[k-1,loc(c)]=pch[half(1-t)].astype(BF)
        rs_copy(k,c).start()
        part[loc(c)]=pch[half(t)]
    def stats(v):
        cen=v-jnp.mean(v,axis=1,keepdims=True)
        r=lax.rsqrt(jnp.mean(cen*cen,axis=1,keepdims=True)+EPSILON)
        return cen*r,r
    def lo_copy(c): return pltpu.make_async_copy(cl.at[loc(c)],lo_hbm.at[loc(c)],losem.at[c])
    def own_tile(i,col): return pltpu.make_async_copy(stage.at[i%2,:,:,core],dw.at[:,:,core,:,pl.ds(col if isinstance(col,int) else pl.multiple_of(col,512),512)],osem.at[i%2])
    def pair_tile(i,g,off): return remote(stage.at[i%2,:,:,1-core],r1.at[g,:,:,:,pl.ds(off if isinstance(off,int) else pl.multiple_of(off,512),512)],g1s.at[i],g1r.at[i],sib)
    def wgrad(i,g,off,left,right_ref,rcol,ocol):
        if not isinstance(i,int) or 2<=i<8: own_tile(i-2,0).wait()
        if not isinstance(i,int) or i>=2: pair_tile(i-2,0,0).wait_send()
        @pl.loop(0,dm//256)
        def _(k):
            ms=pl.ds(pl.multiple_of(k*256,256),256)
            cs=pl.ds(rcol if isinstance(rcol,int) else pl.multiple_of(rcol,512),512)
            right=right_ref[:,cs] if len(right_ref.shape)==2 else strip(right_ref,cs)
            stage[i%2,k]=dot(left[ms],right,NN).astype(BF).reshape(2,2,64,512)
        own_tile(i,ocol).start()
        pair_tile(i,g,off).start()
    def stage_a(c):
        rs=chunk(c)
        @pl.loop(0,pairs//2)
        def _(pp):
            todo=[]
            for i in (0,1):
                p=2*pp+i
                cq=pl.ds(pl.multiple_of(p*128,128),128); ck=pl.ds(pl.multiple_of(width+p*128,128),128)
                for h in (0,1): todo.append((i,2*p+h,h,cq,ck,(lane<64) if h==0 else (lane>=64)))
            sts=[dot(qkv[:,ck],jnp.where(keep,qkv[rs,cq]*scale,zero),NT) for _,_,_,cq,ck,keep in todo]
            ms=[jnp.max(st,axis=0,keepdims=True) for st in sts]
            mcs=[v*LOG2E for v in ms]
            pts=[jnp.exp2(st*LOG2E-mc).astype(BF) for st,mc in zip(sts,mcs)]
            ots=[dot(vt[e[1]],pt,NN) for e,pt in zip(todo,pts)]
            for (i,hd,h,_,_,_),ot,mc in zip(todo,ots,mcs):
                tot=ot[64:65]
                ctt[i,h*64:(h+1)*64,:]=ot[0:64]*(1.0/tot)
                lse[pl.ds(hd,1),rs]=mc+jnp.log2(tot)
            tops=[jnp.max(v,axis=1,keepdims=True) for v in ms]
            for i in (0,1):
                cq=todo[2*i][3]
                early[10:11,cq]=jnp.maximum(early[10:11,cq],jnp.where(lane<64,tops[2*i],tops[2*i+1]))
                ctx[rs,cq]=ctt[i].T.astype(BF)
            step=c*(pairs//2)+pp
            @pl.when(step==0)
            def _():
                gather_z(5,3); gather_start(7)
            @pl.when(step==2)
            def _():
                gather_z(6,2)
            @pl.when(step==3)
            def _():
                gather_z(7,1); gather_x(4)
            @pl.when(step==4)
            def _():
                gather_z(6,3)
            @pl.when(step==5)
            def _():
                gather_z(7,2)
            @pl.when(step==7)
            def _():
                gather_z(7,3); gather_x(5)
        ctx_copy(c,t).start()
        ctxo[loc(c),cols(t)]=ctx[rows(t,c)]
    def stage_b(c):
        ctx_copy(c,1-t).wait_recv()
        x,r=stats(hall[rows(t,c)].astype(F32)+dot(ctxo[loc(c)],whole(wo),NT)+vec[0:1])
        xh[loc(c)]=x
        rst[loc(c)]=jnp.broadcast_to(r,(cr,128))
        hall[rows(t,c)]=(x*vec[1:2]+vec[2:3]).astype(BF)
        ag_copy(3,hall,c,t).start()
    def stage_c(c):
        rs=chunk(c)
        ag_copy(3,hall,c,1-t).wait_recv()
        @pl.loop(0,ff//TF)
        def _(j):
            cs=pl.ds(pl.multiple_of(j*TF,TF),TF)
            u=dot(hall[rs],strip(wup,cs),NN)+upb[:,cs]
            cdf=0.5*(1.0+lax.erf(u*0.5**0.5))
            act[pl.ds(4*c,4),:,cs]=(u*cdf).astype(BF).reshape(4,64,TF)
            slp[rs,cs]=(cdf+u*jnp.exp(-0.5*u*u)*(0.5/math.pi)**0.5).astype(BF)
    def stage_c2(c):
        pch[...]=dot(act[pl.ds(4*c,4)].reshape(cg,ff),whole(wdn),NT)
        split(1,c)
    def stage_d(c):
        rs_copy(1,c).wait_recv()
        x,r=stats(xh[loc(c)]*vec[1:2]+vec[2:3]+part[loc(c)]+rbuf[0,loc(c)].astype(F32)+vec[3:4])
        dy=cl[loc(c)].astype(F32)
        cl[loc(c)]=(x*vec[4:5]+vec[5:6]).astype(BF)
        lo_copy(c).start()
        early[4:5]+=jnp.sum(dy*x,axis=0,keepdims=True)
        early[5:6]+=jnp.sum(dy,axis=0,keepdims=True)
        dx=dy*vec[4:5]
        g=r*(dx-jnp.mean(dx,axis=1,keepdims=True)-x*jnp.mean(dx*x,axis=1,keepdims=True))
        gf[loc(c)]=g
        gb=g.astype(BF)
        early[3:4]+=jnp.sum(gb.astype(F32),axis=0,keepdims=True)
        ball[rows(t,c)]=gb
        ag_copy(4,ball,c,t).start()
        tb[:,rows(t,c)]=gb.T
    def stage_e(c):
        rs=chunk(c)
        ag_copy(4,ball,c,1-t).wait_recv()
        @pl.loop(0,ff//TF)
        def _(j):
            cs=pl.ds(pl.multiple_of(j*TF,TF),TF)
            gu=(dot(ball[rs],strip(wdn,cs),NN)*slp[rs,cs].astype(F32)).astype(BF)
            slp[rs,cs]=gu
            row=pl.ds(8+j*TF//dm,1); cc=pl.ds(pl.multiple_of(j*TF%dm,TF),TF)
            early[row,cc]+=jnp.sum(gu.astype(F32),axis=0,keepdims=True)
        pch[...]=dot(slp[rs],whole(wup),NT)
        split(2,c)
        tb[:,rows(1-t,c)]=ball[rows(1-t,c)].T
        th[:,chunk(c)]=hall[chunk(c)].T
    def stage_f(c):
        rs_copy(2,c).wait_recv()
        dy=gf[loc(c)]+part[loc(c)]+rbuf[1,loc(c)].astype(F32)
        x=xh[loc(c)]; r=rst[loc(c)][:,0:1]
        early[1:2]+=jnp.sum(dy*x,axis=0,keepdims=True)
        early[2:3]+=jnp.sum(dy,axis=0,keepdims=True)
        dx=dy*vec[1:2]
        g=r*(dx-jnp.mean(dx,axis=1,keepdims=True)-x*jnp.mean(dx*x,axis=1,keepdims=True))
        gf[loc(c)]=g
        gb=g.astype(BF)
        early[0:1]+=jnp.sum(gb.astype(F32),axis=0,keepdims=True)
        ga[loc(c)]=gb
        ball[rows(t,c)]=gb
        dcs[loc(c)]=dot(gb,whole(wo),NN).astype(BF)
        dctx_copy(c,t).start()
        dcall[rows(t,c)]=dcs[loc(c),cols(t)]
    def stage_g(c):
        rs=chunk(c)
        dctx_copy(c,1-t).wait_recv()
        @pl.when(c==0)
        def _():
            for i in range(NC): ga_copy(i).start()
        @pl.loop(0,pairs)
        def _(p):
            cq=pl.ds(pl.multiple_of(p*128,128),128); ck=pl.ds(pl.multiple_of(width+p*128,128),128); cv=pl.ds(pl.multiple_of(2*width+p*128,128),128)
            prod=(ctx[rs,cq].astype(F32)*dcall[rs,cq].astype(F32)).T
            dl[0:1]=jnp.sum(prod[0:64],axis=0,keepdims=True)
            dl[1:2]=jnp.sum(prod[64:128],axis=0,keepdims=True)
            for h in (0,1):
                keep=(lane<64) if h==0 else (lane>=64)
                q=jnp.where(keep,qkv[rs,cq]*scale,zero)
                do=jnp.where(keep,dcall[rs,cq],zero)
                st=dot(qkv[:,ck],q,NT)
                pt=jnp.exp2(st*LOG2E-lse[pl.ds(2*p+h,1),rs])
                dpt=dot(qkv[:,cv],do,NT)
                ds=(pt*(dpt-dl[h:h+1])).astype(BF)
                dkv[1,:,cq]+=dot(pt.astype(BF),do,NN)
                dkv[0,:,cq]+=dot(ds,q,NN)
                dqt[h*64:(h+1)*64,:]=dot(kt[p,h*64:(h+1)*64,:],ds,NN)
            qkv[rs,cq]=(dqt[...].T*(HD**-0.5)).astype(BF)
            step=c*pairs+p
            @pl.when(step==0)
            def _():
                add3(0)
                add2(2)
                fetch2(3)
            @pl.when(step==1)
            def _():
                add2(3)
                ecopy(0).start()
            @pl.when(step==4)
            def _():
                eadd(0); ecopy(1).start()
            @pl.when(step==5)
            def _():
                s2(1).wait_send(); s2(2).start()
                fetch3(1)
            @pl.when(step==6)
            def _():
                eadd(1); ecopy(2).start()
            @pl.when(step==7)
            def _():
                sent3(0); add3(1)
            @pl.when(step==8)
            def _():
                eadd(2); ecopy(3).start()
            @pl.when(step==9)
            def _():
                fetchf(0)
            @pl.when(step==10)
            def _():
                finish(0)
                eadd(3); ecopy(4).start()
            @pl.when(step==11)
            def _():
                s2(2).wait_send(); s2(3).start()
                fetch3(2)
            @pl.when(step==12)
            def _():
                for i in range(NC): ga_copy(i).wait_recv()
                for i in range(NC): th[:,i*cg:(i+1)*cg]=ball[i*cg:(i+1)*cg].T
            @pl.when(step==13)
            def _():
                sent3(1); add3(2)
                wgrad(8,4,0,th,ctx,0,base[4])
            @pl.when(step==14)
            def _():
                x_in.start()
            @pl.when(step==15)
            def _():
                fetch2(4)
    def grad_down(c): wgrad(c,c//2,c%2*512,tb,act,c*512,width+ff+c*512)
    def grad_up(c): wgrad(4+c,2+c//2,c%2*512,th,slp,c*512,width+c*512)
    def ga_copy(c):
        return pltpu.make_async_remote_copy(ga.at[loc(c)],ball.at[rows(t,c)],ssem.at[7,c],rsem.at[7,c],device_id=partner,device_id_type=MESH)
    @pl.loop(0,NC)
    def _(c):
        stage_a(c)
        @pl.when(c>0)
        def _(): stage_b(c-1)
    cot_load.wait(); w_out.wait(); x_out.wait()
    gather_done(4); gather_done(5)
    @pl.loop(0,NC-1)
    def _(c):
        stage_c(c)
        @pl.when(c==0)
        def _(): stage_b(NC-1)
    gather_x(6); gather_x(7)
    gather_done(6); gather_done(7)
    @pl.loop(0,NC)
    def _(c):
        stage_c2(c)
        @pl.when(c==1)
        def _(): stage_c(NC-1)
    @pl.loop(0,NC)
    def _(c): stage_d(c)
    @pl.loop(0,NC)
    def _(c): stage_e(c)
    piece=ff//2
    base=(width+ff,width+ff+piece,width,width+piece,0,width+2*ff,2*width+2*ff,3*width+2*ff)
    span=(piece,)*4+(width,)*4
    tiles=((0,1),(2,3),(4,5),(6,7),(8,),(9,),(10,),(11,))
    slots2=[wup.at[8:12,:,0:piece],wup.at[12:16,:,0:piece],wup.at[8:12,:,piece:],wup.at[12:16,:,piece:],wup.at[0:4,:,piece:],wup.at[4:8,:,piece:]]
    slots3=[wdn.at[12:16,:,0:piece],wdn.at[12:16,:,piece:],wdn.at[0:4,:,piece:],wdn.at[4:8,:,piece:],wdn.at[8:12,:,piece:]]
    sum2=[slots2[g%6] for g in range(8)]
    sum3=[slots3[g%5] for g in range(8)]
    def s2(g): return remote(sum2[g].at[:,:,0:span[g]],r2.at[g,:,:,0:span[g]],g2s.at[g],g2r.at[g],xp)
    def s3(g,k): return remote(sum3[g].at[(z+k)%4,:,0:span[g]],r3.at[g,3-k,:,0:span[g]],g3s.at[g,k-1],g3r.at[g,k-1],zp[k-1])
    def load2(g): return [pltpu.make_async_copy(dw.at[:,1-x_,core,:,base[g]:base[g]+span[g]],wup.at[0:4,:,0:span[g]],rl.at[0]),
                          pltpu.make_async_copy(r1.at[g,:,1-x_,:,0:span[g]],wup.at[4:8,:,0:span[g]],rl.at[1])]
    def load3(g): return [pltpu.make_async_copy(dw.at[:,x_,core,:,base[g]:base[g]+span[g]],wdn.at[0:4,:,0:span[g]],rl.at[2]),
                         pltpu.make_async_copy(r1.at[g,:,x_,:,0:span[g]],wdn.at[4:8,:,0:span[g]],rl.at[3]),
                         pltpu.make_async_copy(r2.at[g,:,:,0:span[g]],wdn.at[8:12,:,0:span[g]],rl.at[4])]
    def fetch2(g):
        for i in tiles[g]:
            if i>=6: own_tile(i,0).wait()
            pair_tile(i,g,0).wait_recv()
        for l in load2(g): l.start()
    def add2(g):
        for l in load2(g): l.wait()
        @pl.loop(0,4)
        def _(i): sum2[g][i,:,0:span[g]]=(wup[i,:,0:span[g]].astype(F32)+wup[4+i,:,0:span[g]].astype(F32)).astype(BF)
    def fetch3(g):
        s2(g).wait_recv()
        for l in load3(g): l.start()
    def add3(g):
        for l in load3(g): l.wait()
        @pl.loop(0,4)
        def _(i): sum3[g][i,:,0:span[g]]=(wdn[i,:,0:span[g]].astype(F32)+wdn[4+i,:,0:span[g]].astype(F32)+wdn[8+i,:,0:span[g]].astype(F32)).astype(BF)
        for k in (1,2,3): s3(g,k).start()
    def sent3(g):
        for k in (1,2,3): s3(g,k).wait_send()
    def fslot(g,i):
        r=64*(6*(g%2)+i)
        return tb.at[r:r+64,0:span[g]]
    def loadf(g): return [pltpu.make_async_copy(src,fslot(g,i),fl.at[g%2,i]) for i,src in enumerate(
        [dw.at[z,x_,core,:,base[g]:base[g]+span[g]],r1.at[g,z,x_,:,0:span[g]],r2.at[g,z,:,0:span[g]]]+[r3.at[g,k,:,0:span[g]] for k in range(3)])]
    def fetchf(g):
        for k in (1,2,3): s3(g,k).wait_recv()
        for l in loadf(g): l.start()
    def final(g):
        for l in loadf(g): l.wait()
        v=[fslot(g,i)[...].astype(F32) for i in range(6)]
        return v[0]+v[1]+v[2]+v[3]+v[4]+v[5]
    def fin_copy(g):
        return pltpu.make_async_copy(xh.at[64*g:64*g+64,0:span[g]],fin.at[g] if g<4 else go_hbm if g==4 else fin_head.at[g-5],fs.at[g])
    def finish(g):
        xh[64*g:64*g+64,0:span[g]]=final(g)
        fin_copy(g).start()
    zb=[dev(z+1-2*(z%2),x_,core),dev((z+2)%4,x_,core)]
    hops=[sib,xp,zb[0],zb[1],partner]
    def ecopy(i): return remote(eb.at[i],er.at[i],es.at[i],erc.at[i],hops[i])
    def eadd(i):
        ecopy(i).wait_recv()
        b=eb[i,8:16]; c=er[i,8:16]
        if i<4:
            r=lax.broadcasted_iota(jnp.int32,b.shape,0)
            b=jnp.where(r==2,jnp.maximum(b,c),b+c)
        eb[i+1,0:8]=eb[i,0:8]+er[i,0:8]; eb[i+1,8:16]=b
    def lcopy(i): return remote(lb.at[i],lr.at[i],ls.at[i],lrc.at[i],hops[i])
    def ladd(i):
        lcopy(i).wait_recv()
        lb[i+1]=lb[i]+lr[i]
    @pl.loop(0,NC)
    def _(c):
        ag_copy(3,hall,c,t).wait_send()
        ag_copy(4,ball,c,t).wait_send()
    x_in=pltpu.make_async_copy(x_hbm,th,dsem.at[0])
    for c in range(3): grad_down(c)
    grad_down(3)
    fetch2(0)
    wh_in=pltpu.make_async_copy(wh_hbm,act.at[:,:,0:n],dsem.at[1])
    wh_in.start()
    add2(0); s2(0).start()
    @pl.loop(0,NC)
    def _(c):
        stage_f(c)
        grad_up(c)
        @pl.when(c==1)
        def _(): fetch2(1)
        @pl.when(c==2)
        def _():
            add2(1)
            s2(0).wait_send(); s2(1).start()
        @pl.when(c==3)
        def _():
            fetch2(2)
            fetch3(0)
    @pl.loop(0,NC)
    def _(c): stage_g(c)
    add2(4)
    s2(3).wait_send(); s2(4).start()
    fetch3(3)
    x_in.wait()
    wgrad(9,5,0,th,qkv,0,base[5])
    sent3(2); add3(3)
    fetchf(1)
    @pl.loop(0,pairs)
    def _(p):
        cq=pl.ds(pl.multiple_of(p*128,128),128); ck=pl.ds(pl.multiple_of(width+p*128,128),128); cv=pl.ds(pl.multiple_of(2*width+p*128,128),128)
        qkv[:,ck]=dkv[0,:,cq].astype(BF)
        qkv[:,cv]=dkv[1,:,cq].astype(BF)
    fetch2(5)
    def ycopy(c): return remote(sbuf.at[0,loc(c)],rbuf.at[0,loc(c)],ssem.at[6,c],rsem.at[6,c],partner)
    wh_in.wait()
    def token_grad(c):
        pch[...]=dot(qkv[chunk(c)],act[:,:,0:n].reshape(dm,n),NT)
        rs_copy(1,c).wait_send()
        sbuf[0,loc(c)]=pch[half(1-t)].astype(BF)
        ycopy(c).start()
        part[loc(c)]=pch[half(t)]
    token_grad(0)
    add2(5)
    s2(4).wait_send(); s2(5).start()
    token_grad(1)
    wgrad(10,6,0,th,qkv,width,base[6])
    fetch3(4)
    wgrad(11,7,0,th,qkv,2*width,base[7])
    fetch2(6)
    @pl.loop(2,NC)
    def _(c): token_grad(c)
    add2(6)
    s2(5).wait_send(); s2(6).start()
    fetch2(7)
    sent3(3); add3(4)
    fetch3(5)
    lb[0,0:1,0:width]=jnp.sum(qkv[:,0:width].astype(F32),axis=0,keepdims=True)
    lb[0,0:1,width:2*width]=jnp.sum(qkv[:,2*width:].astype(F32),axis=0,keepdims=True)
    lcopy(0).start()
    finish(1)
    add2(7)
    eadd(4)
    sent3(4); add3(5)
    s2(6).wait_send(); s2(7).start()
    fetch3(6)
    ladd(0); lcopy(1).start()
    fetchf(2)
    smalls[...]=eb[5]
    pk=eb[4,10:11,0:width]
    head=lax.broadcasted_iota(jnp.int32,(1,width),1)//HD
    limit=jnp.zeros((1,width),F32)
    for h in range(width//HD): limit=jnp.where(head==h,lim[h],limit)
    sc=jnp.sqrt(limit/jnp.maximum(pk,limit))
    ctxo[0:64,0:width]=(wq[...].astype(F32)*sc).astype(BF)
    ctxo[64:128,0:width]=(wk[...].astype(F32)*sc).astype(BF)
    clips=[pltpu.make_async_copy(ctxo.at[0:64,0:width],qc_hbm,fs.at[8]),pltpu.make_async_copy(ctxo.at[64:128,0:width],kc_hbm,fs.at[9])]
    for c in clips: c.start()
    smalls[11:12,0:width]=row(v_qb)*sc
    finish(2)
    ladd(1); lcopy(2).start()
    fetchf(3)
    sent3(5); add3(6)
    fetch3(7)
    finish(3)
    fetchf(4)
    ladd(2); lcopy(3).start()
    @pl.loop(0,NC)
    def _(c): lo_copy(c).wait()
    finish(4)
    sent3(6); add3(7)
    fetchf(5)
    def tg_copy(c): return pltpu.make_async_copy(cl.at[loc(c)],tg_hbm.at[loc(c)],losem.at[c])
    @pl.loop(0,NC)
    def _(c):
        ycopy(c).wait_recv()
        cl[loc(c)]=(gf[loc(c)]+part[loc(c)]+rbuf[0,loc(c)].astype(F32)).astype(BF)
        tg_copy(c).start()
    ladd(3)
    smalls[12:13]=lb[4,0:1]
    finish(5)
    fetchf(6)
    finish(6)
    fetchf(7)
    finish(7)
    o_swap.wait_send()
    for g in range(8):
        fin_copy(g).wait()
    for i in (10,11): pair_tile(i,0,0).wait_send()
    s2(7).wait_send()
    sent3(7)
    for c in clips: c.wait()
    for i in range(5): ecopy(i).wait_send()
    for i in range(4): lcopy(i).wait_send()
    @pl.loop(0,NC)
    def _(c):
        tg_copy(c).wait()
        ctx_copy(c,t).wait_send(); dctx_copy(c,t).wait_send(); tok_copy(c).wait_send()
        rs_copy(2,c).wait_send(); ycopy(c).wait_send()
        ga_copy(c).wait_send()

def main_call(shards,tok,cot,vectors,lim,cid):
    V=pl.BlockSpec(memory_space=pltpu.VMEM); A=pl.BlockSpec(memory_space=pl.ANY)
    width=shards[0].shape[1]; ff=shards[4].shape[1]; own,dm=tok.shape; rows=2*own; n=3*width; cr=own//NC; wide=2*width; piece=ff//2
    S=jax.ShapeDtypeStruct; M=pltpu.VMEM; D=pltpu.SemaphoreType.DMA
    return pl.pallas_call(main_kernel,
      out_shape=(S((own,dm),BF),S((own,dm),BF),S((4,64,piece),F32),S((3,64,width),F32),S((64,width),F32),S((64,width),BF),S((64,width),BF),S((16,dm),F32),
        S((4,2,2,64,width+2*ff+n),BF),S((8,4,2,64,piece),BF),S((8,4,64,piece),BF),S((8,3,64,piece),BF),S((dm,rows),BF),S((16,64,n),BF)),
      in_specs=[V]*6+[A,A]+[V]*9+[pl.BlockSpec(memory_space=pltpu.SMEM)],out_specs=(A,)*7+(V,)+(A,)*6,
      scratch_shapes=[M((1,n),F32),M((8,dm),F32),M((1,ff),F32),M((own,dm),F32),M((6,16,dm),F32),M((5,16,dm),F32),M((5,8,dm),F32),M((4,8,dm),F32),
        M((64,n+wide+2*ff),BF),M((rows,n),BF),M((width//HD,80,rows),BF),M((width//128,128,rows),BF),M((rows,width),BF),M((own,wide),BF),M((width//HD,rows),F32),M((own,dm),BF),
        M((16,64,wide),BF),M((16,64,ff),BF),M((16,64,ff),BF),
        M((own,dm),F32),M((own,128),F32),
        M((rows,dm),BF),M((16,64,ff),BF),M((rows,ff),BF),M((rows,dm),BF),M((own,dm),BF),M((own,wide),BF),M((rows,width),BF),
        M((own,dm),F32),M((2*cr,dm),F32),M((2,128,2*cr),F32),M((128,2*cr),F32),M((8,2*cr),F32),M((2,rows,width),F32),
        M((2,own,dm),BF),M((2,own,dm),BF),
        M((dm,rows),BF),M((dm,rows),BF),M((2,4,2,2,64,512),BF),
        D((7,)),D((NC,)),D((2,)),D((2,)),D((8,NC)),D((8,NC)),D((5,)),D((12,)),D((12,)),D((8,)),D((8,)),D((8,3)),D((8,3)),
        D((NC+1,)),D((NC+1,)),D((8,2,3)),D((8,2,3)),D((8,4)),D((8,4)),D((8,8)),D((8,8)),
        D((5,)),D((5,)),D((4,)),D((4,)),D((2,6)),D((10,))],
      compiler_params=pltpu.CompilerParams(collective_id=cid,has_side_effects=True,vmem_limit_bytes=61*2**20),
      name="main")(*shards,tok,cot,*vectors,lim)

def finish_kernel(lo,tg,fin,fin_head,go,qc,kc,smalls,
                  lo_,tg_,gq_,gk_,gv_,go_,gu_,gd_,qc_,kc_,qb_,vb_,ob_,g1_,b1_,ub_,db_,g2_,b2_,pk_,qbc_,h_lo,h_tg,h_fin,h_head,h_go,h_qc,h_kc,isem,sem):
    piece=fin.shape[2]
    ins=[pltpu.make_async_copy(a,b,isem.at[i]) for i,(a,b) in enumerate(((lo,h_lo),(tg,h_tg),(fin,h_fin),(fin_head,h_head),(go,h_go),(qc,h_qc),(kc,h_kc)))]
    outs=[[(h_lo,lo_)],[(h_tg,tg_)],[(h_fin.at[0],gd_.at[:,0:piece]),(h_fin.at[1],gd_.at[:,piece:]),(h_fin.at[2],gu_.at[:,0:piece]),(h_fin.at[3],gu_.at[:,piece:])],
          [(h_head.at[0],gq_),(h_head.at[1],gk_),(h_head.at[2],gv_)],[(h_go,go_)],[(h_qc,qc_)],[(h_kc,kc_)]]
    for c in ins: c.start()
    width=qb_.shape[0]; dm=ob_.shape[0]
    def line(v): return v.reshape(v.shape[1])
    qb_[...]=line(smalls[12:13,0:width]); vb_[...]=line(smalls[12:13,width:2*width])
    for i,o in enumerate((ob_,g1_,b1_,db_,g2_,b2_)): o[...]=line(smalls[i:i+1])
    ub_[0:dm]=line(smalls[8:9]); ub_[dm:2*dm]=line(smalls[9:10])
    for h in range(pk_.shape[0]): pk_[h]=jnp.max(smalls[10:11,h*HD:(h+1)*HD])
    qbc_[...]=line(smalls[11:12,0:width]).astype(BF)
    moved=[]
    for a,group in zip(ins,outs):
        a.wait()
        for src,dst in group:
            c=pltpu.make_async_copy(src,dst,sem.at[len(moved)])
            c.start()
            moved.append(c)
    for c in moved: c.wait()

def finish_call(big,smalls,heads):
    V=pl.BlockSpec(memory_space=pltpu.VMEM); A=pl.BlockSpec(memory_space=pl.ANY); S=jax.ShapeDtypeStruct
    lo,tg,fin,fin_head,go,qc,kc=big
    width=go.shape[1]; piece=fin.shape[2]; ff=2*piece; dm=tg.shape[1]
    return pl.pallas_call(finish_kernel,
      out_shape=(S(lo.shape,BF),S(tg.shape,BF))+(S((64,width),F32),)*4+(S((64,ff),F32),)*2+(S((64,width),BF),)*2
        +tuple(S((k,),F32) for k in (width,width,dm,dm,dm,ff,dm,dm,dm,heads))+(S((width,),BF),),
      in_specs=[A]*7+[V],out_specs=(A,)*10+(V,)*9+(pl.BlockSpec(memory_space=pltpu.SMEM),V),
      scratch_shapes=[pltpu.VMEM(a.shape,a.dtype) for a in big]+[pltpu.SemaphoreType.DMA((7,)),pltpu.SemaphoreType.DMA((12,))],
      compiler_params=pltpu.CompilerParams(vmem_limit_bytes=61*2**20),name="finish")(*big,smalls)

def per_device_pair(tokens,query_weight,query_bias,key_weight,value_weight,value_bias,out_weight,out_bias,first_gain,first_shift,
    up_weight,up_bias,down_weight,down_bias,second_gain,second_shift,cotangent,clip_limit):
    shards=(query_weight,key_weight,value_weight,out_weight.T,up_weight,down_weight.T)
    vectors=(out_bias,first_gain,first_shift,down_bias,second_gain,second_shift,up_bias,query_bias,value_bias)
    res=main_call(shards,tokens,cotangent,vectors,clip_limit,1)
    lo,tg,gq,gk,gv,go,gu,gd,qc,kc,qb,vb,ob,g1,b1,ub,db,g2,b2,pk,qbc=finish_call(res[:7],res[7],clip_limit.shape[0])
    return (lo,tg,gq,qb,gk,gv,vb,go.T,ob,g1,b1,gu,ub,gd.T,db,g2,b2,pk,qc,qbc,kc)


def layer(*args):
    paired = lax.axis_size("dp") == 16 and lax.axis_size("tensor") == 2 and 2 * args[0].shape[0] == LEN
    return per_device_pair(*args) if paired else per_device(*args)


def solution(mesh):
    in_specs = (
        P(("dp", "tensor"), None),
        P("dp", "tensor"),
        P("tensor"),
        P("dp", "tensor"),
        P("dp", "tensor"),
        P("tensor"),
        P("tensor", "dp"),
        P(),
        P(),
        P(),
        P("dp", "tensor"),
        P("tensor"),
        P("tensor", "dp"),
        P(),
        P(),
        P(),
        P(("dp", "tensor"), None),
        P("tensor"),
    )
    out_specs = (
        P(("dp", "tensor"), None),
        P(("dp", "tensor"), None),
        P("dp", "tensor"),
        P("tensor"),
        P("dp", "tensor"),
        P("dp", "tensor"),
        P("tensor"),
        P("tensor", "dp"),
        P(),
        P(),
        P(),
        P("dp", "tensor"),
        P("tensor"),
        P("tensor", "dp"),
        P(),
        P(),
        P(),
        P("tensor"),
        P("dp", "tensor"),
        P("tensor"),
        P("dp", "tensor"),
    )
    return jax.shard_map(
        layer, mesh=mesh, in_specs=in_specs, out_specs=out_specs, check_vma=False
    )
```

```python
import functools
import math

import jax
import jax.numpy as jnp
from jax import lax
from jax.experimental import pallas as pl
from jax.experimental.pallas import tpu as pltpu
from jax.sharding import PartitionSpec as P

HD = 64
LEN = 1024
QB = 512


def layer_norm(values, gain, shift):
    center = values - jnp.mean(values, axis=-1, keepdims=True)
    spread = jnp.mean(center * center, axis=-1, keepdims=True)
    return center * lax.rsqrt(spread + EPSILON) * gain + shift


def gelu_slope(upper):
    normal_cdf = 0.5 * (1.0 + lax.erf(upper * 0.5**0.5))
    return normal_cdf + upper * jnp.exp(-0.5 * upper * upper) * (0.5 / math.pi) ** 0.5


def contract_rows(left, right):
    return lax.dot_general(
        left, right, (((0,), (0,)), ((), ())), preferred_element_type=jnp.float32
    )


def contract_cols(left, right):
    return lax.dot_general(
        left, right, (((1,), (1,)), ((), ())), preferred_element_type=jnp.float32
    )


def per_device(
    tokens,
    query_weight,
    query_bias,
    key_weight,
    value_weight,
    value_bias,
    out_weight,
    out_bias,
    first_gain,
    first_shift,
    up_weight,
    up_bias,
    down_weight,
    down_bias,
    second_gain,
    second_shift,
    cotangent,
    clip_limit,
):
    query_full, key_full, value_full, out_full, up_full, down_full = (
        lax.all_gather(query_weight, "dp", axis=0, tiled=True),
        lax.all_gather(key_weight, "dp", axis=0, tiled=True),
        lax.all_gather(value_weight, "dp", axis=0, tiled=True),
        lax.all_gather(out_weight, "dp", axis=1, tiled=True),
        lax.all_gather(up_weight, "dp", axis=0, tiled=True),
        lax.all_gather(down_weight, "dp", axis=1, tiled=True),
    )
    width = query_full.shape[1]
    hidden_width = up_full.shape[1]
    heads_here = width // HD
    score_scale = HD ** (-0.5)
    joint_weight = jnp.concatenate([query_full, key_full, value_full], axis=1)
    gathered = lax.all_gather(tokens, "tensor", axis=0, tiled=True)
    group_rows = gathered.shape[0]
    seq_count = group_rows // LEN
    block_count = LEN // QB
    projected = jnp.dot(gathered, joint_weight, preferred_element_type=jnp.float32)
    queries = (projected[:, :width] + query_bias.astype(jnp.float32)).astype(jnp.bfloat16)
    keyset = projected[:, width : 2 * width].astype(jnp.bfloat16)
    valset = (projected[:, 2 * width :] + value_bias.astype(jnp.float32)).astype(jnp.bfloat16)
    query_seq = queries.reshape(seq_count, LEN, heads_here, HD)
    key_seq = keyset.reshape(seq_count, LEN, heads_here, HD)
    value_seq = valset.reshape(seq_count, LEN, heads_here, HD)

    def attend_block(block_id):
        seq_id = block_id // block_count
        row_start = block_id % block_count * QB
        query_rows = lax.dynamic_slice_in_dim(
            lax.dynamic_index_in_dim(query_seq, seq_id, 0, False), row_start, QB, 0
        )
        key_rows = lax.dynamic_index_in_dim(key_seq, seq_id, 0, False)
        value_rows = lax.dynamic_index_in_dim(value_seq, seq_id, 0, False)
        logits = (
            jnp.einsum("qhd,khd->hqk", query_rows, key_rows, preferred_element_type=jnp.float32)
            * score_scale
        )
        row_max = jnp.max(logits, axis=2, keepdims=True)
        exponent = jnp.exp(logits - row_max)
        totals = jnp.sum(exponent, axis=2, keepdims=True)
        probs_low = (exponent / totals).astype(jnp.bfloat16)
        context_rows = jnp.einsum(
            "hqk,khd->qhd", probs_low, value_rows, preferred_element_type=jnp.float32
        )
        return (
            context_rows.reshape(QB, width).astype(jnp.bfloat16),
            (row_max + jnp.log(totals))[:, :, 0],
            jnp.max(row_max, axis=(1, 2)),
        )

    context_blocks, log_totals, block_peaks = lax.map(
        attend_block, jnp.arange(seq_count * block_count)
    )
    context = context_blocks.reshape(group_rows, width)
    logit_peak = lax.pmax(jnp.max(block_peaks, axis=0), "dp")
    attention = lax.psum_scatter(
        jnp.dot(context, out_full, preferred_element_type=jnp.float32).astype(jnp.bfloat16),
        "tensor",
        scatter_dimension=0,
        tiled=True,
    ).astype(jnp.float32) + out_bias.astype(jnp.float32)
    first_resid = tokens.astype(jnp.float32) + attention
    hidden, first_pull = jax.vjp(
        layer_norm, first_resid, first_gain.astype(jnp.float32), first_shift.astype(jnp.float32)
    )
    hidden_all = lax.all_gather(hidden.astype(jnp.bfloat16), "tensor", axis=0, tiled=True)
    upper = jnp.dot(hidden_all, up_full, preferred_element_type=jnp.float32) + up_bias.astype(
        jnp.float32
    )
    acted = jax.nn.gelu(upper, approximate=False).astype(jnp.bfloat16)
    branch = lax.psum_scatter(
        jnp.dot(acted, down_full, preferred_element_type=jnp.float32).astype(jnp.bfloat16),
        "tensor",
        scatter_dimension=0,
        tiled=True,
    ).astype(jnp.float32) + down_bias.astype(jnp.float32)
    normed, second_pull = jax.vjp(
        layer_norm,
        hidden + branch,
        second_gain.astype(jnp.float32),
        second_shift.astype(jnp.float32),
    )
    layer_out = normed.astype(jnp.bfloat16)
    grad_second, second_gain_grad, second_shift_grad = second_pull(cotangent.astype(jnp.float32))
    grad_branch = grad_second.astype(jnp.bfloat16)
    down_bias_grad = jnp.sum(grad_branch, axis=0, dtype=jnp.float32)
    branch_all = lax.all_gather(grad_branch, "tensor", axis=0, tiled=True)
    grad_acted = contract_cols(branch_all, down_full)
    down_weight_grad = contract_rows(acted, branch_all)
    grad_upper = (grad_acted * gelu_slope(upper)).astype(jnp.bfloat16)
    up_bias_grad = jnp.sum(grad_upper, axis=0, dtype=jnp.float32)
    up_weight_grad = contract_rows(hidden_all, grad_upper)
    grad_hidden = grad_second + lax.psum_scatter(
        contract_cols(grad_upper, up_full).astype(jnp.bfloat16),
        "tensor",
        scatter_dimension=0,
        tiled=True,
    ).astype(jnp.float32)
    grad_first, first_gain_grad, first_shift_grad = first_pull(grad_hidden)
    grad_attn = grad_first.astype(jnp.bfloat16)
    out_bias_grad = jnp.sum(grad_attn, axis=0, dtype=jnp.float32)
    attn_all = lax.all_gather(grad_attn, "tensor", axis=0, tiled=True)
    grad_context = contract_cols(attn_all, out_full).astype(jnp.bfloat16)
    out_weight_grad = contract_rows(context, attn_all)
    query_blocks = queries.reshape(seq_count, block_count, QB, heads_here, HD)
    grad_blocks = grad_context.reshape(seq_count, block_count, QB, heads_here, HD)
    log_blocks = log_totals.reshape(seq_count, block_count, heads_here, QB)

    def sequence_back(item):
        query_part, grad_part, log_part, key_rows, value_rows = item

        def block_back(carry, piece):
            key_acc, value_acc = carry
            query_rows, grad_rows, log_rows = piece
            logits = (
                jnp.einsum("qhd,khd->hqk", query_rows, key_rows, preferred_element_type=jnp.float32)
                * score_scale
            )
            probs = jnp.exp(logits - log_rows[:, :, None])
            probs_low = probs.astype(jnp.bfloat16)
            value_acc = value_acc + jnp.einsum(
                "hqk,qhd->khd", probs_low, grad_rows, preferred_element_type=jnp.float32
            )
            grad_probs = jnp.einsum(
                "qhd,khd->hqk", grad_rows, value_rows, preferred_element_type=jnp.float32
            )
            inner = jnp.sum(probs * grad_probs, axis=2, keepdims=True)
            grad_logits = (probs * (grad_probs - inner)).astype(jnp.bfloat16)
            grad_query = (
                jnp.einsum(
                    "hqk,khd->qhd", grad_logits, key_rows, preferred_element_type=jnp.float32
                )
                * score_scale
            )
            key_acc = (
                key_acc
                + jnp.einsum(
                    "hqk,qhd->khd", grad_logits, query_rows, preferred_element_type=jnp.float32
                )
                * score_scale
            )
            return ((key_acc, value_acc), grad_query.astype(jnp.bfloat16))

        empty = jnp.zeros((LEN, heads_here, HD), jnp.float32)
        (key_acc, value_acc), grad_query_rows = lax.scan(
            block_back, (empty, empty), (query_part, grad_part, log_part)
        )
        return (grad_query_rows, key_acc.astype(jnp.bfloat16), value_acc.astype(jnp.bfloat16))

    grad_queries_all, grad_keys_all, grad_values_all = lax.map(
        sequence_back, (query_blocks, grad_blocks, log_blocks, key_seq, value_seq)
    )
    grad_joint = jnp.concatenate(
        [
            grad_queries_all.reshape(group_rows, width),
            grad_keys_all.reshape(group_rows, width),
            grad_values_all.reshape(group_rows, width),
        ],
        axis=1,
    )
    joint_grad = contract_rows(gathered, grad_joint)
    query_weight_grad = joint_grad[:, :width]
    key_weight_grad = joint_grad[:, width : 2 * width]
    value_weight_grad = joint_grad[:, 2 * width :]
    query_bias_grad = jnp.sum(grad_joint[:, :width], axis=0, dtype=jnp.float32)
    value_bias_grad = jnp.sum(grad_joint[:, 2 * width :], axis=0, dtype=jnp.float32)
    tokens_grad = (
        grad_first
        + lax.psum_scatter(
            contract_cols(grad_joint, joint_weight).astype(jnp.bfloat16),
            "tensor",
            scatter_dimension=0,
            tiled=True,
        ).astype(jnp.float32)
    ).astype(jnp.bfloat16)
    (
        query_weight_grad,
        key_weight_grad,
        value_weight_grad,
        out_weight_grad,
        up_weight_grad,
        down_weight_grad,
    ) = (
        lax.psum_scatter(
            query_weight_grad.astype(jnp.bfloat16), "dp", scatter_dimension=0, tiled=True
        ).astype(jnp.float32),
        lax.psum_scatter(
            key_weight_grad.astype(jnp.bfloat16), "dp", scatter_dimension=0, tiled=True
        ).astype(jnp.float32),
        lax.psum_scatter(
            value_weight_grad.astype(jnp.bfloat16), "dp", scatter_dimension=0, tiled=True
        ).astype(jnp.float32),
        lax.psum_scatter(
            out_weight_grad.astype(jnp.bfloat16), "dp", scatter_dimension=1, tiled=True
        ).astype(jnp.float32),
        lax.psum_scatter(
            up_weight_grad.astype(jnp.bfloat16), "dp", scatter_dimension=0, tiled=True
        ).astype(jnp.float32),
        lax.psum_scatter(
            down_weight_grad.astype(jnp.bfloat16), "dp", scatter_dimension=1, tiled=True
        ).astype(jnp.float32),
    )
    tensor_place = lax.axis_index("tensor")
    model_width = out_bias.shape[0]
    query_spread = lax.dynamic_update_slice_in_dim(
        jnp.zeros((model_width,), jnp.float32), query_bias_grad, tensor_place * width, 0
    )
    value_spread = lax.dynamic_update_slice_in_dim(
        jnp.zeros((model_width,), jnp.float32), value_bias_grad, tensor_place * width, 0
    )
    up_spread = lax.dynamic_update_slice_in_dim(
        jnp.zeros((hidden_width * lax.axis_size("tensor"),), jnp.float32),
        up_bias_grad,
        tensor_place * hidden_width,
        0,
    )
    (
        query_spread,
        value_spread,
        up_spread,
        out_bias_grad,
        down_bias_grad,
        first_gain_grad,
        first_shift_grad,
        second_gain_grad,
        second_shift_grad,
    ) = lax.psum(
        (
            query_spread,
            value_spread,
            up_spread,
            out_bias_grad,
            down_bias_grad,
            first_gain_grad,
            first_shift_grad,
            second_gain_grad,
            second_shift_grad,
        ),
        ("dp", "tensor"),
    )
    query_bias_grad = lax.dynamic_slice_in_dim(query_spread, tensor_place * width, width, 0)
    value_bias_grad = lax.dynamic_slice_in_dim(value_spread, tensor_place * width, width, 0)
    up_bias_grad = lax.dynamic_slice_in_dim(up_spread, tensor_place * hidden_width, hidden_width, 0)
    factor = clip_limit / jnp.maximum(logit_peak, clip_limit)
    column_scale = jnp.repeat(jnp.sqrt(factor), HD)
    query_clipped = (query_weight.astype(jnp.float32) * column_scale).astype(jnp.bfloat16)
    query_bias_clipped = (query_bias.astype(jnp.float32) * column_scale).astype(jnp.bfloat16)
    key_clipped = (key_weight.astype(jnp.float32) * column_scale).astype(jnp.bfloat16)
    return (
        layer_out,
        tokens_grad,
        query_weight_grad,
        query_bias_grad,
        key_weight_grad,
        value_weight_grad,
        value_bias_grad,
        out_weight_grad,
        out_bias_grad,
        first_gain_grad,
        first_shift_grad,
        up_weight_grad,
        up_bias_grad,
        down_weight_grad,
        down_bias_grad,
        second_gain_grad,
        second_shift_grad,
        logit_peak,
        query_clipped,
        query_bias_clipped,
        key_clipped,
    )


LOG2E=1.4426950408889634
NT=(((1,),(1,)),((),()))
NN=(((1,),(0,)),((),()))
F32=jnp.float32
BF=jnp.bfloat16
MESH=pl.DeviceIdType.MESH
EPSILON=1e-5
NC=4


def dot(a,b,dims):
    return lax.dot_general(a,b,dims,preferred_element_type=jnp.float32)


def greet(partner):
    barrier=pltpu.get_barrier_semaphore()
    pl.semaphore_signal(barrier,inc=1,device_id=partner,device_id_type=MESH)
    pl.semaphore_wait(barrier,1)


def main_kernel(wq,wk,wv,wos,wu,wds,tok,cot_hbm,v_ob,v_g1,v_b1,v_db,v_g2,v_b2,v_ub,v_qb,v_vb,lim,
               lo_hbm,tg_hbm,fin,fin_head,go_hbm,qc_hbm,kc_hbm,smalls,dw,r1,r2,r3,x_hbm,wh_hbm,
               bias,vec,upb,gf,eb,er,lb,lr,sh,qkv,vt,kt,ctx,ctxo,lse,cl,wo,wup,wdn,xh,rst,hall,act,slp,ball,ga,dcs,dcall,part,pch,ctt,dqt,dl,dkv,sbuf,rbuf,tb,th,stage,
               lsem,losem,dsem,osem,ssem,rsem,rl,g1s,g1r,g2s,g2r,g3s,g3r,ts,tr,azs,azr,oys,oyr,ocs,ocr,axs,axr,acs,acr,es,erc,ls,lrc,fl,fs):
    d=lax.axis_index("dp"); t=lax.axis_index("tensor")
    partner=(d,1-t)
    core=d%2; x_=(d//2)%2; z=d//4
    def dev(z_,xx,c_): return ((z_*2+xx)*2+c_,t)
    sib=dev(z,x_,1-core); xp=dev(z,1-x_,core); zp=[dev((z+k)%4,x_,core) for k in (1,2,3)]
    own,dm=tok.shape; cr=own//NC; cg=2*cr; rows_all=2*own; width=ctx.shape[1]; ff=wup.shape[2]; wide=wo.shape[2]; pairs=width//128
    def local(src,dst,i): return pltpu.make_async_copy(src,dst,lsem.at[i])
    def remote(src,dst,a,b,p): return pltpu.make_async_remote_copy(src,dst,a,b,device_id=p,device_id_type=MESH)
    cot_load=local(cot_hbm,cl,0)
    cot_load.start()
    barrier=pltpu.get_barrier_semaphore()
    n=3*width
    def row(v): return v[...].astype(F32).reshape(1,v.shape[0])
    sh[:,0:width]=wq[...]; sh[:,width:2*width]=wk[...]; sh[:,2*width:n]=wv[...]
    everyone=[partner,sib,xp]+zp
    for p in everyone: pl.semaphore_signal(barrier,inc=1,device_id=p,device_id_type=MESH)
    def chunk(c): return pl.ds(pl.multiple_of(c*cg,cg),cg)
    def rows(rank,c): return pl.ds(pl.multiple_of(c*cg+rank*cr,cr),cr)
    def half(rank): return pl.ds(pl.multiple_of(rank*cr,cr),cr)
    def loc(c): return pl.ds(pl.multiple_of(c*cr,cr),cr)
    def rs_copy(k,c):
        return pltpu.make_async_remote_copy(sbuf.at[k-1,loc(c)],rbuf.at[k-1,loc(c)],ssem.at[k,c],rsem.at[k,c],device_id=partner,device_id_type=MESH)
    def ag_copy(k,buf,c,rank):
        return pltpu.make_async_remote_copy(buf.at[rows(rank,c)],buf.at[rows(rank,c)],ssem.at[k,c],rsem.at[k,c],device_id=partner,device_id_type=MESH)
    def cols(rank): return pl.ds(pl.multiple_of(rank*width,128),width)
    def ctx_copy(c,rank):
        return pltpu.make_async_remote_copy(ctx.at[rows(1-rank,c)],ctxo.at[loc(c),cols(rank)],ssem.at[0,c],rsem.at[0,c],device_id=partner,device_id_type=MESH)
    def dctx_copy(c,rank):
        return pltpu.make_async_remote_copy(dcs.at[loc(c),cols(1-rank)],dcall.at[rows(rank,c)],ssem.at[5,c],rsem.at[5,c],device_id=partner,device_id_type=MESH)
    early=eb.at[0]
    early[...]=jnp.zeros((16,dm),F32)
    early[10:11]=jnp.full((1,dm),-jnp.inf,F32)
    lb[0]=jnp.zeros((8,dm),F32)
    def whole(w): return w[...].reshape(dm,w.shape[2])
    def strip(w,cs): return w[:,:,cs].reshape(dm,TF)
    dkv[...]=jnp.zeros_like(dkv)
    lane=lax.broadcasted_iota(jnp.int32,(1,128),1)
    scale=jnp.bfloat16(HD**-0.5); zero=jnp.bfloat16(0)
    q4=ff//2
    groups=[(act,0,0,width),(act,width,width,width),(act,2*width,2*width,width),(wo,0,n,width),
            (wup,0,n+wide,q4),(wup,q4,n+wide+q4,q4),(wdn,0,n+wide+ff,q4),(wdn,q4,n+wide+ff+q4,q4)]
    def block(z_,xx): return (z_*2+xx)*2+core
    me=block(z,x_)
    def place(g,b):
        buf,c0,_,nc=groups[g]
        return buf.at[b,:,cols(t)] if g==3 else buf.at[b,:,c0:c0+nc]
    def shard(g): return sh.at[:,groups[g][2]:groups[g][2]+groups[g][3]]
    up=dev(jnp.minimum(z+1,3),x_,core); down=dev(jnp.maximum(z-1,0),x_,core)
    def z_hop(g,way,j,b): return remote(shard(g) if j==1 else place(g,b),place(g,b),azs.at[g,way,j-1],azr.at[g,way,j-1],up if way==0 else down)
    def x_hop(g,zz,own_): return remote(shard(g) if own_ else place(g,block(zz,x_)),place(g,block(zz,x_)),axs.at[g,zz],axr.at[g,zz],xp)
    def x_land(g,zz): return remote(place(g,block(zz,1-x_)),place(g,block(zz,1-x_)),axs.at[g,zz],axr.at[g,zz],xp)
    def c_hop(g,xx,zz,b,own_): return remote(shard(g) if own_ else place(g,b),place(g,b),acs.at[g,4*xx+zz],acr.at[g,4*xx+zz],sib)
    def gather_start(g):
        buf,c0,s0,nc=groups[g]
        @pl.when(z<3)
        def _(): z_hop(g,0,1,me).start()
        @pl.when(z>0)
        def _(): z_hop(g,1,1,me).start()
        x_hop(g,z,True).start()
        c_hop(g,0,z,me,True).start()
        buf[me,:,cols(t) if g==3 else slice(c0,c0+nc)]=sh[:,s0:s0+nc]
    def gather_z(g,j):
        for way in (0,1):
            here=(z>=j) if way==0 else (z+j<=3)
            zz=jnp.maximum(z-j,0) if way==0 else jnp.minimum(z+j,3)
            b=block(zz,x_)
            @pl.when(here)
            def _():
                z_hop(g,way,j,b).wait_recv()
                x_hop(g,zz,False).start()
                c_hop(g,0,zz,b,False).start()
            if j<3:
                @pl.when(here & ((z<3) if way==0 else (z>0)))
                def _(): z_hop(g,way,j+1,b).start()
    def gather_x(g):
        for zz in range(4):
            x_land(g,zz).wait_recv()
            c_hop(g,1,zz,block(zz,1-x_),False).start()
    def gather_done(g):
        for xx in (0,1):
            for zz in range(4):
                b=block(zz,x_)
                c_hop(g,xx,zz,b,False).wait_recv()
                c_hop(g,xx,zz,b,False).wait_send()
        for zz in range(4): x_land(g,zz).wait_send()
        for j in (1,2,3):
            @pl.when((z>=j-1) & (z<3))
            def _(): z_hop(g,0,j,me).wait_send()
            @pl.when((z+j-1<=3) & (z>0))
            def _(): z_hop(g,1,j,me).wait_send()
    own_copies=[local(tok.at[c*cr:(c+1)*cr],hall.at[rows(t,c)],1+c) for c in range(NC)]
    for c in own_copies: c.start()
    pl.semaphore_wait(barrier,len(everyone))
    gather_start(0); gather_start(1)
    def tok_copy(c): return remote(tok.at[loc(c)],hall.at[rows(t,c)],ts.at[c],tr.at[c],partner)
    def o_swap(k,rank): return remote(wo.at[2*k+core,:,cols(rank)],wo.at[2*k+core,:,cols(rank)],oys.at[k],oyr.at[k],partner)
    def o_core(k): return remote(wo.at[2*k+core,:,cols(1-t)],wo.at[2*k+core,:,cols(1-t)],ocs.at[k],ocr.at[k],sib)
    sh[:,n:n+width]=wos[...]
    @pl.loop(0,NC)
    def _(c): tok_copy(c).start()
    sh[:,n+wide:n+wide+ff]=wu[...]
    sh[:,n+wide+ff:]=wds[...]
    for i,v in enumerate((v_ob,v_g1,v_b1,v_db,v_g2,v_b2)): vec[i:i+1]=row(v)
    upb[...]=row(v_ub)
    bias[...]=jnp.zeros_like(bias)
    bias[:,0:width]=row(v_qb); bias[:,2*width:]=row(v_vb)
    gather_z(0,1); gather_start(2)
    gather_z(1,1); gather_z(0,2)
    gather_z(2,1); gather_start(3)
    gather_z(1,2); gather_z(0,3); gather_z(2,2); gather_z(1,3)
    gather_x(0); gather_z(3,1); gather_z(2,3)
    gather_x(1); gather_z(3,2)
    gather_start(4)
    gather_x(2); gather_z(3,3); gather_z(4,1)
    for g in range(3): gather_done(g)
    for c in own_copies: c.wait()
    TF=512
    @pl.loop(0,NC)
    def _(c):
        tok_copy(c).wait_recv()
        @pl.loop(0,n//TF)
        def _(j):
            cs=pl.ds(pl.multiple_of(j*TF,TF),TF)
            qkv[chunk(c),cs]=(dot(hall[chunk(c)],strip(act,cs),NN)+bias[:,cs]).astype(BF)
        th[:,chunk(c)]=hall[chunk(c)].T
        @pl.when(c==0)
        def _(): gather_z(4,2)
        @pl.when(c==1)
        def _():
            gather_x(3)
            for k in range(8): o_swap(k,t).start()
            gather_z(4,3)
            gather_start(5)
        @pl.when(c==3)
        def _(): gather_done(3)
    x_out=local(th,x_hbm,5); w_out=local(act.at[:,:,0:n],wh_hbm,6)
    x_out.start(); w_out.start()
    ones=jnp.where(lax.broadcasted_iota(jnp.int32,(16,rows_all),0)==0,1.0,0.0).astype(BF)
    @pl.loop(0,pairs)
    def _(p):
        ck=pl.multiple_of(width+p*128,128); cv=pl.multiple_of(2*width+p*128,128)
        kt[p]=qkv[:,pl.ds(ck,128)].T
        v=qkv[:,pl.ds(cv,128)].T
        vt[2*p,0:64]=v[0:64]; vt[2*p,64:80]=ones
        vt[2*p+1,0:64]=v[64:128]; vt[2*p+1,64:80]=ones
    gather_z(5,1)
    def split(k,c):
        sbuf[k-1,loc(c)]=pch[half(1-t)].astype(BF)
        rs_copy(k,c).start()
        part[loc(c)]=pch[half(t)]
    def stats(v):
        cen=v-jnp.mean(v,axis=1,keepdims=True)
        r=lax.rsqrt(jnp.mean(cen*cen,axis=1,keepdims=True)+EPSILON)
        return cen*r,r
    def lo_copy(c): return pltpu.make_async_copy(cl.at[loc(c)],lo_hbm.at[loc(c)],losem.at[c])
    def own_tile(i,col): return pltpu.make_async_copy(stage.at[i%2,:,:,core],dw.at[:,:,core,:,pl.ds(col if isinstance(col,int) else pl.multiple_of(col,512),512)],osem.at[i%2])
    def pair_tile(i,g,off): return remote(stage.at[i%2,:,:,1-core],r1.at[g,:,:,:,pl.ds(off if isinstance(off,int) else pl.multiple_of(off,512),512)],g1s.at[i],g1r.at[i],sib)
    def wgrad(i,g,off,left,right_ref,rcol,ocol):
        if not isinstance(i,int) or 2<=i<8: own_tile(i-2,0).wait()
        if not isinstance(i,int) or i>=2: pair_tile(i-2,0,0).wait_send()
        @pl.loop(0,dm//256)
        def _(k):
            ms=pl.ds(pl.multiple_of(k*256,256),256)
            cs=pl.ds(rcol if isinstance(rcol,int) else pl.multiple_of(rcol,512),512)
            right=right_ref[:,cs] if len(right_ref.shape)==2 else strip(right_ref,cs)
            stage[i%2,k]=dot(left[ms],right,NN).astype(BF).reshape(2,2,64,512)
        own_tile(i,ocol).start()
        pair_tile(i,g,off).start()
    def stage_a(c):
        rs=chunk(c)
        @pl.loop(0,pairs//2)
        def _(pp):
            todo=[]
            for i in (0,1):
                p=2*pp+i
                cq=pl.ds(pl.multiple_of(p*128,128),128); ck=pl.ds(pl.multiple_of(width+p*128,128),128)
                for h in (0,1): todo.append((i,2*p+h,h,cq,ck,(lane<64) if h==0 else (lane>=64)))
            sts=[dot(qkv[:,ck],jnp.where(keep,qkv[rs,cq]*scale,zero),NT) for _,_,_,cq,ck,keep in todo]
            ms=[jnp.max(st,axis=0,keepdims=True) for st in sts]
            mcs=[v*LOG2E for v in ms]
            pts=[jnp.exp2(st*LOG2E-mc).astype(BF) for st,mc in zip(sts,mcs)]
            ots=[dot(vt[e[1]],pt,NN) for e,pt in zip(todo,pts)]
            for (i,hd,h,_,_,_),ot,mc in zip(todo,ots,mcs):
                tot=ot[64:65]
                ctt[i,h*64:(h+1)*64,:]=ot[0:64]*(1.0/tot)
                lse[pl.ds(hd,1),rs]=mc+jnp.log2(tot)
            tops=[jnp.max(v,axis=1,keepdims=True) for v in ms]
            for i in (0,1):
                cq=todo[2*i][3]
                early[10:11,cq]=jnp.maximum(early[10:11,cq],jnp.where(lane<64,tops[2*i],tops[2*i+1]))
                ctx[rs,cq]=ctt[i].T.astype(BF)
            step=c*(pairs//2)+pp
            @pl.when(step==0)
            def _():
                gather_z(5,2); gather_start(6)
            @pl.when(step==2)
            def _():
                gather_z(5,3); gather_z(6,1)
            @pl.when(step==3)
            def _():
                gather_x(4); gather_start(7)
                for k in range(8):
                    o_swap(k,1-t).wait_recv()
                    o_core(k).start()
                for k in range(8): o_core(k).wait_recv()
            @pl.when(step==4)
            def _():
                gather_z(6,2)
            @pl.when(step==5)
            def _():
                gather_z(7,1)
            @pl.when(step==6)
            def _():
                gather_z(6,3); gather_z(7,2)
            @pl.when(step==7)
            def _():
                gather_x(5)
        ctx_copy(c,t).start()
        ctxo[loc(c),cols(t)]=ctx[rows(t,c)]
    def stage_b(c):
        ctx_copy(c,1-t).wait_recv()
        x,r=stats(hall[rows(t,c)].astype(F32)+dot(ctxo[loc(c)],whole(wo),NT)+vec[0:1])
        xh[loc(c)]=x
        rst[loc(c)]=jnp.broadcast_to(r,(cr,128))
        hall[rows(t,c)]=(x*vec[1:2]+vec[2:3]).astype(BF)
        ag_copy(3,hall,c,t).start()
    def stage_c(c):
        rs=chunk(c)
        ag_copy(3,hall,c,1-t).wait_recv()
        @pl.loop(0,ff//TF)
        def _(j):
            cs=pl.ds(pl.multiple_of(j*TF,TF),TF)
            u=dot(hall[rs],strip(wup,cs),NN)+upb[:,cs]
            cdf=0.5*(1.0+lax.erf(u*0.5**0.5))
            act[pl.ds(4*c,4),:,cs]=(u*cdf).astype(BF).reshape(4,64,TF)
            slp[rs,cs]=(cdf+u*jnp.exp(-0.5*u*u)*(0.5/math.pi)**0.5).astype(BF)
    def stage_c2(c):
        pch[...]=dot(act[pl.ds(4*c,4)].reshape(cg,ff),whole(wdn),NT)
        split(1,c)
    def stage_d(c):
        rs_copy(1,c).wait_recv()
        x,r=stats(xh[loc(c)]*vec[1:2]+vec[2:3]+part[loc(c)]+rbuf[0,loc(c)].astype(F32)+vec[3:4])
        dy=cl[loc(c)].astype(F32)
        cl[loc(c)]=(x*vec[4:5]+vec[5:6]).astype(BF)
        lo_copy(c).start()
        early[4:5]+=jnp.sum(dy*x,axis=0,keepdims=True)
        early[5:6]+=jnp.sum(dy,axis=0,keepdims=True)
        dx=dy*vec[4:5]
        g=r*(dx-jnp.mean(dx,axis=1,keepdims=True)-x*jnp.mean(dx*x,axis=1,keepdims=True))
        gf[loc(c)]=g
        gb=g.astype(BF)
        early[3:4]+=jnp.sum(gb.astype(F32),axis=0,keepdims=True)
        ball[rows(t,c)]=gb
        ag_copy(4,ball,c,t).start()
        tb[:,rows(t,c)]=gb.T
    def stage_e(c):
        rs=chunk(c)
        ag_copy(4,ball,c,1-t).wait_recv()
        @pl.loop(0,ff//TF)
        def _(j):
            cs=pl.ds(pl.multiple_of(j*TF,TF),TF)
            gu=(dot(ball[rs],strip(wdn,cs),NN)*slp[rs,cs].astype(F32)).astype(BF)
            slp[rs,cs]=gu
            row=pl.ds(8+j*TF//dm,1); cc=pl.ds(pl.multiple_of(j*TF%dm,TF),TF)
            early[row,cc]+=jnp.sum(gu.astype(F32),axis=0,keepdims=True)
        pch[...]=dot(slp[rs],whole(wup),NT)
        split(2,c)
        tb[:,rows(1-t,c)]=ball[rows(1-t,c)].T
        th[:,chunk(c)]=hall[chunk(c)].T
    def stage_f(c):
        rs_copy(2,c).wait_recv()
        dy=gf[loc(c)]+part[loc(c)]+rbuf[1,loc(c)].astype(F32)
        x=xh[loc(c)]; r=rst[loc(c)][:,0:1]
        early[1:2]+=jnp.sum(dy*x,axis=0,keepdims=True)
        early[2:3]+=jnp.sum(dy,axis=0,keepdims=True)
        dx=dy*vec[1:2]
        g=r*(dx-jnp.mean(dx,axis=1,keepdims=True)-x*jnp.mean(dx*x,axis=1,keepdims=True))
        gf[loc(c)]=g
        gb=g.astype(BF)
        early[0:1]+=jnp.sum(gb.astype(F32),axis=0,keepdims=True)
        ga[loc(c)]=gb
        ball[rows(t,c)]=gb
        dcs[loc(c)]=dot(gb,whole(wo),NN).astype(BF)
        dctx_copy(c,t).start()
        dcall[rows(t,c)]=dcs[loc(c),cols(t)]
    def stage_g(c):
        rs=chunk(c)
        dctx_copy(c,1-t).wait_recv()
        @pl.when(c==0)
        def _():
            for i in range(NC): ga_copy(i).start()
        @pl.loop(0,pairs)
        def _(p):
            cq=pl.ds(pl.multiple_of(p*128,128),128); ck=pl.ds(pl.multiple_of(width+p*128,128),128); cv=pl.ds(pl.multiple_of(2*width+p*128,128),128)
            prod=(ctx[rs,cq].astype(F32)*dcall[rs,cq].astype(F32)).T
            dl[0:1]=jnp.sum(prod[0:64],axis=0,keepdims=True)
            dl[1:2]=jnp.sum(prod[64:128],axis=0,keepdims=True)
            for h in (0,1):
                keep=(lane<64) if h==0 else (lane>=64)
                q=jnp.where(keep,qkv[rs,cq]*scale,zero)
                do=jnp.where(keep,dcall[rs,cq],zero)
                st=dot(qkv[:,ck],q,NT)
                pt=jnp.exp2(st*LOG2E-lse[pl.ds(2*p+h,1),rs])
                dpt=dot(qkv[:,cv],do,NT)
                ds=(pt*(dpt-dl[h:h+1])).astype(BF)
                dkv[1,:,cq]+=dot(pt.astype(BF),do,NN)
                dkv[0,:,cq]+=dot(ds,q,NN)
                dqt[h*64:(h+1)*64,:]=dot(kt[p,h*64:(h+1)*64,:],ds,NN)
            qkv[rs,cq]=(dqt[...].T*(HD**-0.5)).astype(BF)
            step=c*pairs+p
            @pl.when(step==0)
            def _():
                add3(0)
                add2(2)
                fetch2(3)
            @pl.when(step==1)
            def _():
                add2(3)
                ecopy(0).start()
            @pl.when(step==4)
            def _():
                eadd(0); ecopy(1).start()
            @pl.when(step==5)
            def _():
                s2(1).wait_send(); s2(2).start()
                fetch3(1)
            @pl.when(step==6)
            def _():
                eadd(1); ecopy(2).start()
            @pl.when(step==7)
            def _():
                sent3(0); add3(1)
            @pl.when(step==8)
            def _():
                eadd(2); ecopy(3).start()
            @pl.when(step==9)
            def _():
                fetchf(0)
            @pl.when(step==10)
            def _():
                finish(0)
                eadd(3); ecopy(4).start()
            @pl.when(step==11)
            def _():
                s2(2).wait_send(); s2(3).start()
                fetch3(2)
            @pl.when(step==12)
            def _():
                for i in range(NC): ga_copy(i).wait_recv()
                for i in range(NC): th[:,i*cg:(i+1)*cg]=ball[i*cg:(i+1)*cg].T
            @pl.when(step==13)
            def _():
                sent3(1); add3(2)
                wgrad(8,4,0,th,ctx,0,base[4])
            @pl.when(step==14)
            def _():
                x_in.start()
            @pl.when(step==15)
            def _():
                fetch2(4)
    def grad_down(c): wgrad(c,c//2,c%2*512,tb,act,c*512,width+ff+c*512)
    def grad_up(c): wgrad(4+c,2+c//2,c%2*512,th,slp,c*512,width+c*512)
    def ga_copy(c):
        return pltpu.make_async_remote_copy(ga.at[loc(c)],ball.at[rows(t,c)],ssem.at[7,c],rsem.at[7,c],device_id=partner,device_id_type=MESH)
    @pl.loop(0,NC)
    def _(c):
        stage_a(c)
        @pl.when(c>0)
        def _(): stage_b(c-1)
    cot_load.wait(); w_out.wait(); x_out.wait()
    gather_done(4); gather_done(5)
    gather_z(7,3)
    @pl.loop(0,NC-1)
    def _(c):
        stage_c(c)
        @pl.when(c==0)
        def _(): stage_b(NC-1)
    gather_x(6); gather_x(7)
    gather_done(6); gather_done(7)
    @pl.loop(0,NC)
    def _(c):
        stage_c2(c)
        @pl.when(c==1)
        def _(): stage_c(NC-1)
    @pl.loop(0,NC)
    def _(c): stage_d(c)
    @pl.loop(0,NC)
    def _(c): stage_e(c)
    piece=ff//2
    base=(width+ff,width+ff+piece,width,width+piece,0,width+2*ff,2*width+2*ff,3*width+2*ff)
    span=(piece,)*4+(width,)*4
    tiles=((0,1),(2,3),(4,5),(6,7),(8,),(9,),(10,),(11,))
    slots2=[wup.at[8:12,:,0:piece],wup.at[12:16,:,0:piece],wup.at[8:12,:,piece:],wup.at[12:16,:,piece:],wup.at[0:4,:,piece:],wup.at[4:8,:,piece:]]
    slots3=[wdn.at[12:16,:,0:piece],wdn.at[12:16,:,piece:],wdn.at[0:4,:,piece:],wdn.at[4:8,:,piece:],wdn.at[8:12,:,piece:]]
    sum2=[slots2[g%6] for g in range(8)]
    sum3=[slots3[g%5] for g in range(8)]
    def s2(g): return remote(sum2[g].at[:,:,0:span[g]],r2.at[g,:,:,0:span[g]],g2s.at[g],g2r.at[g],xp)
    def s3(g,k): return remote(sum3[g].at[(z+k)%4,:,0:span[g]],r3.at[g,3-k,:,0:span[g]],g3s.at[g,k-1],g3r.at[g,k-1],zp[k-1])
    def load2(g): return [pltpu.make_async_copy(dw.at[:,1-x_,core,:,base[g]:base[g]+span[g]],wup.at[0:4,:,0:span[g]],rl.at[0]),
                          pltpu.make_async_copy(r1.at[g,:,1-x_,:,0:span[g]],wup.at[4:8,:,0:span[g]],rl.at[1])]
    def load3(g): return [pltpu.make_async_copy(dw.at[:,x_,core,:,base[g]:base[g]+span[g]],wdn.at[0:4,:,0:span[g]],rl.at[2]),
                         pltpu.make_async_copy(r1.at[g,:,x_,:,0:span[g]],wdn.at[4:8,:,0:span[g]],rl.at[3]),
                         pltpu.make_async_copy(r2.at[g,:,:,0:span[g]],wdn.at[8:12,:,0:span[g]],rl.at[4])]
    def fetch2(g):
        for i in tiles[g]:
            if i>=6: own_tile(i,0).wait()
            pair_tile(i,g,0).wait_recv()
        for l in load2(g): l.start()
    def add2(g):
        for l in load2(g): l.wait()
        @pl.loop(0,4)
        def _(i): sum2[g][i,:,0:span[g]]=(wup[i,:,0:span[g]].astype(F32)+wup[4+i,:,0:span[g]].astype(F32)).astype(BF)
    def fetch3(g):
        s2(g).wait_recv()
        for l in load3(g): l.start()
    def add3(g):
        for l in load3(g): l.wait()
        @pl.loop(0,4)
        def _(i): sum3[g][i,:,0:span[g]]=(wdn[i,:,0:span[g]].astype(F32)+wdn[4+i,:,0:span[g]].astype(F32)+wdn[8+i,:,0:span[g]].astype(F32)).astype(BF)
        for k in (1,2,3): s3(g,k).start()
    def sent3(g):
        for k in (1,2,3): s3(g,k).wait_send()
    def fslot(g,i):
        r=64*(6*(g%2)+i)
        return tb.at[r:r+64,0:span[g]]
    def loadf(g): return [pltpu.make_async_copy(src,fslot(g,i),fl.at[g%2,i]) for i,src in enumerate(
        [dw.at[z,x_,core,:,base[g]:base[g]+span[g]],r1.at[g,z,x_,:,0:span[g]],r2.at[g,z,:,0:span[g]]]+[r3.at[g,k,:,0:span[g]] for k in range(3)])]
    def fetchf(g):
        for k in (1,2,3): s3(g,k).wait_recv()
        for l in loadf(g): l.start()
    def final(g):
        for l in loadf(g): l.wait()
        v=[fslot(g,i)[...].astype(F32) for i in range(6)]
        return v[0]+v[1]+v[2]+v[3]+v[4]+v[5]
    def fin_copy(g):
        return pltpu.make_async_copy(xh.at[64*g:64*g+64,0:span[g]],fin.at[g] if g<4 else go_hbm if g==4 else fin_head.at[g-5],fs.at[g])
    def finish(g):
        xh[64*g:64*g+64,0:span[g]]=final(g)
        fin_copy(g).start()
    zb=[dev(z+1-2*(z%2),x_,core),dev((z+2)%4,x_,core)]
    hops=[sib,xp,zb[0],zb[1],partner]
    def ecopy(i): return remote(eb.at[i],er.at[i],es.at[i],erc.at[i],hops[i])
    def eadd(i):
        ecopy(i).wait_recv()
        b=eb[i,8:16]; c=er[i,8:16]
        if i<4:
            r=lax.broadcasted_iota(jnp.int32,b.shape,0)
            b=jnp.where(r==2,jnp.maximum(b,c),b+c)
        eb[i+1,0:8]=eb[i,0:8]+er[i,0:8]; eb[i+1,8:16]=b
    def lcopy(i): return remote(lb.at[i],lr.at[i],ls.at[i],lrc.at[i],hops[i])
    def ladd(i):
        lcopy(i).wait_recv()
        lb[i+1]=lb[i]+lr[i]
    @pl.loop(0,NC)
    def _(c):
        ag_copy(3,hall,c,t).wait_send()
        ag_copy(4,ball,c,t).wait_send()
    x_in=pltpu.make_async_copy(x_hbm,th,dsem.at[0])
    for c in range(3): grad_down(c)
    grad_down(3)
    fetch2(0)
    wh_in=pltpu.make_async_copy(wh_hbm,act.at[:,:,0:n],dsem.at[1])
    wh_in.start()
    add2(0); s2(0).start()
    @pl.loop(0,NC)
    def _(c):
        stage_f(c)
        grad_up(c)
        @pl.when(c==1)
        def _(): fetch2(1)
        @pl.when(c==2)
        def _(): add2(1)
        @pl.when(c==3)
        def _():
            fetch2(2)
            s2(0).wait_send(); s2(1).start()
            fetch3(0)
    @pl.loop(0,NC)
    def _(c): stage_g(c)
    add2(4)
    s2(3).wait_send(); s2(4).start()
    fetch3(3)
    x_in.wait()
    wgrad(9,5,0,th,qkv,0,base[5])
    sent3(2); add3(3)
    fetchf(1)
    @pl.loop(0,pairs)
    def _(p):
        cq=pl.ds(pl.multiple_of(p*128,128),128); ck=pl.ds(pl.multiple_of(width+p*128,128),128); cv=pl.ds(pl.multiple_of(2*width+p*128,128),128)
        qkv[:,ck]=dkv[0,:,cq].astype(BF)
        qkv[:,cv]=dkv[1,:,cq].astype(BF)
    fetch2(5)
    def ycopy(c): return remote(sbuf.at[0,loc(c)],rbuf.at[0,loc(c)],ssem.at[6,c],rsem.at[6,c],partner)
    wh_in.wait()
    def token_grad(c):
        pch[...]=dot(qkv[chunk(c)],act[:,:,0:n].reshape(dm,n),NT)
        rs_copy(1,c).wait_send()
        sbuf[0,loc(c)]=pch[half(1-t)].astype(BF)
        ycopy(c).start()
        part[loc(c)]=pch[half(t)]
    @pl.loop(0,2)
    def _(c): token_grad(c)
    add2(5)
    s2(4).wait_send(); s2(5).start()
    wgrad(10,6,0,th,qkv,width,base[6])
    fetch3(4)
    wgrad(11,7,0,th,qkv,2*width,base[7])
    fetch2(6)
    @pl.loop(2,NC)
    def _(c): token_grad(c)
    add2(6)
    s2(5).wait_send(); s2(6).start()
    fetch2(7)
    sent3(3); add3(4)
    fetch3(5)
    lb[0,0:1,0:width]=jnp.sum(qkv[:,0:width].astype(F32),axis=0,keepdims=True)
    lb[0,0:1,width:2*width]=jnp.sum(qkv[:,2*width:].astype(F32),axis=0,keepdims=True)
    lcopy(0).start()
    finish(1)
    add2(7)
    eadd(4)
    sent3(4); add3(5)
    s2(6).wait_send(); s2(7).start()
    fetch3(6)
    ladd(0); lcopy(1).start()
    fetchf(2)
    smalls[...]=eb[5]
    pk=eb[4,10:11,0:width]
    head=lax.broadcasted_iota(jnp.int32,(1,width),1)//HD
    limit=jnp.zeros((1,width),F32)
    for h in range(width//HD): limit=jnp.where(head==h,lim[h],limit)
    sc=jnp.sqrt(limit/jnp.maximum(pk,limit))
    ctxo[0:64,0:width]=(wq[...].astype(F32)*sc).astype(BF)
    ctxo[64:128,0:width]=(wk[...].astype(F32)*sc).astype(BF)
    clips=[pltpu.make_async_copy(ctxo.at[0:64,0:width],qc_hbm,fs.at[8]),pltpu.make_async_copy(ctxo.at[64:128,0:width],kc_hbm,fs.at[9])]
    for c in clips: c.start()
    smalls[11:12,0:width]=row(v_qb)*sc
    finish(2)
    ladd(1); lcopy(2).start()
    fetchf(3)
    sent3(5); add3(6)
    fetch3(7)
    finish(3)
    fetchf(4)
    ladd(2); lcopy(3).start()
    @pl.loop(0,NC)
    def _(c): lo_copy(c).wait()
    finish(4)
    sent3(6); add3(7)
    fetchf(5)
    def tg_copy(c): return pltpu.make_async_copy(cl.at[loc(c)],tg_hbm.at[loc(c)],losem.at[c])
    @pl.loop(0,NC)
    def _(c):
        ycopy(c).wait_recv()
        cl[loc(c)]=(gf[loc(c)]+part[loc(c)]+rbuf[0,loc(c)].astype(F32)).astype(BF)
        tg_copy(c).start()
    ladd(3)
    smalls[12:13]=lb[4,0:1]
    finish(5)
    fetchf(6)
    finish(6)
    fetchf(7)
    finish(7)
    for k in range(8):
        o_swap(k,t).wait_send()
        o_core(k).wait_send()
    for g in range(8):
        fin_copy(g).wait()
    for i in (10,11): pair_tile(i,0,0).wait_send()
    s2(7).wait_send()
    sent3(7)
    for c in clips: c.wait()
    for i in range(5): ecopy(i).wait_send()
    for i in range(4): lcopy(i).wait_send()
    @pl.loop(0,NC)
    def _(c):
        tg_copy(c).wait()
        ctx_copy(c,t).wait_send(); dctx_copy(c,t).wait_send(); tok_copy(c).wait_send()
        rs_copy(2,c).wait_send(); ycopy(c).wait_send()
        ga_copy(c).wait_send()

def main_call(shards,tok,cot,vectors,lim,cid):
    V=pl.BlockSpec(memory_space=pltpu.VMEM); A=pl.BlockSpec(memory_space=pl.ANY)
    width=shards[0].shape[1]; ff=shards[4].shape[1]; own,dm=tok.shape; rows=2*own; n=3*width; cr=own//NC; wide=2*width; piece=ff//2
    S=jax.ShapeDtypeStruct; M=pltpu.VMEM; D=pltpu.SemaphoreType.DMA
    return pl.pallas_call(main_kernel,
      out_shape=(S((own,dm),BF),S((own,dm),BF),S((4,64,piece),F32),S((3,64,width),F32),S((64,width),F32),S((64,width),BF),S((64,width),BF),S((16,dm),F32),
        S((4,2,2,64,width+2*ff+n),BF),S((8,4,2,64,piece),BF),S((8,4,64,piece),BF),S((8,3,64,piece),BF),S((dm,rows),BF),S((16,64,n),BF)),
      in_specs=[V]*6+[A,A]+[V]*9+[pl.BlockSpec(memory_space=pltpu.SMEM)],out_specs=(A,)*7+(V,)+(A,)*6,
      scratch_shapes=[M((1,n),F32),M((8,dm),F32),M((1,ff),F32),M((own,dm),F32),M((6,16,dm),F32),M((5,16,dm),F32),M((5,8,dm),F32),M((4,8,dm),F32),
        M((64,n+wide+2*ff),BF),M((rows,n),BF),M((width//HD,80,rows),BF),M((width//128,128,rows),BF),M((rows,width),BF),M((own,wide),BF),M((width//HD,rows),F32),M((own,dm),BF),
        M((16,64,wide),BF),M((16,64,ff),BF),M((16,64,ff),BF),
        M((own,dm),F32),M((own,128),F32),
        M((rows,dm),BF),M((16,64,ff),BF),M((rows,ff),BF),M((rows,dm),BF),M((own,dm),BF),M((own,wide),BF),M((rows,width),BF),
        M((own,dm),F32),M((2*cr,dm),F32),M((2,128,2*cr),F32),M((128,2*cr),F32),M((8,2*cr),F32),M((2,rows,width),F32),
        M((2,own,dm),BF),M((2,own,dm),BF),
        M((dm,rows),BF),M((dm,rows),BF),M((2,4,2,2,64,512),BF),
        D((7,)),D((NC,)),D((2,)),D((2,)),D((8,NC)),D((8,NC)),D((5,)),D((12,)),D((12,)),D((8,)),D((8,)),D((8,3)),D((8,3)),
        D((NC+1,)),D((NC+1,)),D((8,2,3)),D((8,2,3)),D((8,)),D((8,)),D((8,)),D((8,)),D((8,4)),D((8,4)),D((8,8)),D((8,8)),
        D((5,)),D((5,)),D((4,)),D((4,)),D((2,6)),D((10,))],
      compiler_params=pltpu.CompilerParams(collective_id=cid,has_side_effects=True,vmem_limit_bytes=61*2**20),
      name="main")(*shards,tok,cot,*vectors,lim)

def finish_kernel(lo,tg,fin,fin_head,go,qc,kc,smalls,
                  lo_,tg_,gq_,gk_,gv_,go_,gu_,gd_,qc_,kc_,qb_,vb_,ob_,g1_,b1_,ub_,db_,g2_,b2_,pk_,qbc_,h_lo,h_tg,h_fin,h_head,h_go,h_qc,h_kc,isem,sem):
    piece=fin.shape[2]
    ins=[pltpu.make_async_copy(a,b,isem.at[i]) for i,(a,b) in enumerate(((lo,h_lo),(tg,h_tg),(fin,h_fin),(fin_head,h_head),(go,h_go),(qc,h_qc),(kc,h_kc)))]
    outs=[[(h_lo,lo_)],[(h_tg,tg_)],[(h_fin.at[0],gd_.at[:,0:piece]),(h_fin.at[1],gd_.at[:,piece:]),(h_fin.at[2],gu_.at[:,0:piece]),(h_fin.at[3],gu_.at[:,piece:])],
          [(h_head.at[0],gq_),(h_head.at[1],gk_),(h_head.at[2],gv_)],[(h_go,go_)],[(h_qc,qc_)],[(h_kc,kc_)]]
    for c in ins: c.start()
    width=qb_.shape[0]; dm=ob_.shape[0]
    def line(v): return v.reshape(v.shape[1])
    qb_[...]=line(smalls[12:13,0:width]); vb_[...]=line(smalls[12:13,width:2*width])
    for i,o in enumerate((ob_,g1_,b1_,db_,g2_,b2_)): o[...]=line(smalls[i:i+1])
    ub_[0:dm]=line(smalls[8:9]); ub_[dm:2*dm]=line(smalls[9:10])
    for h in range(pk_.shape[0]): pk_[h]=jnp.max(smalls[10:11,h*HD:(h+1)*HD])
    qbc_[...]=line(smalls[11:12,0:width]).astype(BF)
    moved=[]
    for a,group in zip(ins,outs):
        a.wait()
        for src,dst in group:
            c=pltpu.make_async_copy(src,dst,sem.at[len(moved)])
            c.start()
            moved.append(c)
    for c in moved: c.wait()

def finish_call(big,smalls,heads):
    V=pl.BlockSpec(memory_space=pltpu.VMEM); A=pl.BlockSpec(memory_space=pl.ANY); S=jax.ShapeDtypeStruct
    lo,tg,fin,fin_head,go,qc,kc=big
    width=go.shape[1]; piece=fin.shape[2]; ff=2*piece; dm=tg.shape[1]
    return pl.pallas_call(finish_kernel,
      out_shape=(S(lo.shape,BF),S(tg.shape,BF))+(S((64,width),F32),)*4+(S((64,ff),F32),)*2+(S((64,width),BF),)*2
        +tuple(S((k,),F32) for k in (width,width,dm,dm,dm,ff,dm,dm,dm,heads))+(S((width,),BF),),
      in_specs=[A]*7+[V],out_specs=(A,)*10+(V,)*9+(pl.BlockSpec(memory_space=pltpu.SMEM),V),
      scratch_shapes=[pltpu.VMEM(a.shape,a.dtype) for a in big]+[pltpu.SemaphoreType.DMA((7,)),pltpu.SemaphoreType.DMA((12,))],
      compiler_params=pltpu.CompilerParams(vmem_limit_bytes=61*2**20),name="finish")(*big,smalls)

def per_device_pair(tokens,query_weight,query_bias,key_weight,value_weight,value_bias,out_weight,out_bias,first_gain,first_shift,
    up_weight,up_bias,down_weight,down_bias,second_gain,second_shift,cotangent,clip_limit):
    shards=(query_weight,key_weight,value_weight,out_weight.T,up_weight,down_weight.T)
    vectors=(out_bias,first_gain,first_shift,down_bias,second_gain,second_shift,up_bias,query_bias,value_bias)
    res=main_call(shards,tokens,cotangent,vectors,clip_limit,1)
    lo,tg,gq,gk,gv,go,gu,gd,qc,kc,qb,vb,ob,g1,b1,ub,db,g2,b2,pk,qbc=finish_call(res[:7],res[7],clip_limit.shape[0])
    return (lo,tg,gq,qb,gk,gv,vb,go.T,ob,g1,b1,gu,ub,gd.T,db,g2,b2,pk,qc,qbc,kc)


def layer(*args):
    paired = lax.axis_size("dp") == 16 and lax.axis_size("tensor") == 2 and 2 * args[0].shape[0] == LEN
    return per_device_pair(*args) if paired else per_device(*args)


def solution(mesh):
    in_specs = (
        P(("dp", "tensor"), None),
        P("dp", "tensor"),
        P("tensor"),
        P("dp", "tensor"),
        P("dp", "tensor"),
        P("tensor"),
        P("tensor", "dp"),
        P(),
        P(),
        P(),
        P("dp", "tensor"),
        P("tensor"),
        P("tensor", "dp"),
        P(),
        P(),
        P(),
        P(("dp", "tensor"), None),
        P("tensor"),
    )
    out_specs = (
        P(("dp", "tensor"), None),
        P(("dp", "tensor"), None),
        P("dp", "tensor"),
        P("tensor"),
        P("dp", "tensor"),
        P("dp", "tensor"),
        P("tensor"),
        P("tensor", "dp"),
        P(),
        P(),
        P(),
        P("dp", "tensor"),
        P("tensor"),
        P("tensor", "dp"),
        P(),
        P(),
        P(),
        P("tensor"),
        P("dp", "tensor"),
        P("tensor"),
        P("dp", "tensor"),
    )
    return jax.shard_map(
        layer, mesh=mesh, in_specs=in_specs, out_specs=out_specs, check_vma=False
    )
```

```python
import functools
import math

import jax
import jax.numpy as jnp
from jax import lax
from jax.experimental import pallas as pl
from jax.experimental.pallas import tpu as pltpu
from jax.sharding import PartitionSpec as P

HD = 64
LEN = 1024
QB = 512


def layer_norm(values, gain, shift):
    center = values - jnp.mean(values, axis=-1, keepdims=True)
    spread = jnp.mean(center * center, axis=-1, keepdims=True)
    return center * lax.rsqrt(spread + EPSILON) * gain + shift


def gelu_slope(upper):
    normal_cdf = 0.5 * (1.0 + lax.erf(upper * 0.5**0.5))
    return normal_cdf + upper * jnp.exp(-0.5 * upper * upper) * (0.5 / math.pi) ** 0.5


def contract_rows(left, right):
    return lax.dot_general(
        left, right, (((0,), (0,)), ((), ())), preferred_element_type=jnp.float32
    )


def contract_cols(left, right):
    return lax.dot_general(
        left, right, (((1,), (1,)), ((), ())), preferred_element_type=jnp.float32
    )


def per_device(
    tokens,
    query_weight,
    query_bias,
    key_weight,
    value_weight,
    value_bias,
    out_weight,
    out_bias,
    first_gain,
    first_shift,
    up_weight,
    up_bias,
    down_weight,
    down_bias,
    second_gain,
    second_shift,
    cotangent,
    clip_limit,
):
    query_full, key_full, value_full, out_full, up_full, down_full = (
        lax.all_gather(query_weight, "dp", axis=0, tiled=True),
        lax.all_gather(key_weight, "dp", axis=0, tiled=True),
        lax.all_gather(value_weight, "dp", axis=0, tiled=True),
        lax.all_gather(out_weight, "dp", axis=1, tiled=True),
        lax.all_gather(up_weight, "dp", axis=0, tiled=True),
        lax.all_gather(down_weight, "dp", axis=1, tiled=True),
    )
    width = query_full.shape[1]
    hidden_width = up_full.shape[1]
    heads_here = width // HD
    score_scale = HD ** (-0.5)
    joint_weight = jnp.concatenate([query_full, key_full, value_full], axis=1)
    gathered = lax.all_gather(tokens, "tensor", axis=0, tiled=True)
    group_rows = gathered.shape[0]
    seq_count = group_rows // LEN
    block_count = LEN // QB
    projected = jnp.dot(gathered, joint_weight, preferred_element_type=jnp.float32)
    queries = (projected[:, :width] + query_bias.astype(jnp.float32)).astype(jnp.bfloat16)
    keyset = projected[:, width : 2 * width].astype(jnp.bfloat16)
    valset = (projected[:, 2 * width :] + value_bias.astype(jnp.float32)).astype(jnp.bfloat16)
    query_seq = queries.reshape(seq_count, LEN, heads_here, HD)
    key_seq = keyset.reshape(seq_count, LEN, heads_here, HD)
    value_seq = valset.reshape(seq_count, LEN, heads_here, HD)

    def attend_block(block_id):
        seq_id = block_id // block_count
        row_start = block_id % block_count * QB
        query_rows = lax.dynamic_slice_in_dim(
            lax.dynamic_index_in_dim(query_seq, seq_id, 0, False), row_start, QB, 0
        )
        key_rows = lax.dynamic_index_in_dim(key_seq, seq_id, 0, False)
        value_rows = lax.dynamic_index_in_dim(value_seq, seq_id, 0, False)
        logits = (
            jnp.einsum("qhd,khd->hqk", query_rows, key_rows, preferred_element_type=jnp.float32)
            * score_scale
        )
        row_max = jnp.max(logits, axis=2, keepdims=True)
        exponent = jnp.exp(logits - row_max)
        totals = jnp.sum(exponent, axis=2, keepdims=True)
        probs_low = (exponent / totals).astype(jnp.bfloat16)
        context_rows = jnp.einsum(
            "hqk,khd->qhd", probs_low, value_rows, preferred_element_type=jnp.float32
        )
        return (
            context_rows.reshape(QB, width).astype(jnp.bfloat16),
            (row_max + jnp.log(totals))[:, :, 0],
            jnp.max(row_max, axis=(1, 2)),
        )

    context_blocks, log_totals, block_peaks = lax.map(
        attend_block, jnp.arange(seq_count * block_count)
    )
    context = context_blocks.reshape(group_rows, width)
    logit_peak = lax.pmax(jnp.max(block_peaks, axis=0), "dp")
    attention = lax.psum_scatter(
        jnp.dot(context, out_full, preferred_element_type=jnp.float32).astype(jnp.bfloat16),
        "tensor",
        scatter_dimension=0,
        tiled=True,
    ).astype(jnp.float32) + out_bias.astype(jnp.float32)
    first_resid = tokens.astype(jnp.float32) + attention
    hidden, first_pull = jax.vjp(
        layer_norm, first_resid, first_gain.astype(jnp.float32), first_shift.astype(jnp.float32)
    )
    hidden_all = lax.all_gather(hidden.astype(jnp.bfloat16), "tensor", axis=0, tiled=True)
    upper = jnp.dot(hidden_all, up_full, preferred_element_type=jnp.float32) + up_bias.astype(
        jnp.float32
    )
    acted = jax.nn.gelu(upper, approximate=False).astype(jnp.bfloat16)
    branch = lax.psum_scatter(
        jnp.dot(acted, down_full, preferred_element_type=jnp.float32).astype(jnp.bfloat16),
        "tensor",
        scatter_dimension=0,
        tiled=True,
    ).astype(jnp.float32) + down_bias.astype(jnp.float32)
    normed, second_pull = jax.vjp(
        layer_norm,
        hidden + branch,
        second_gain.astype(jnp.float32),
        second_shift.astype(jnp.float32),
    )
    layer_out = normed.astype(jnp.bfloat16)
    grad_second, second_gain_grad, second_shift_grad = second_pull(cotangent.astype(jnp.float32))
    grad_branch = grad_second.astype(jnp.bfloat16)
    down_bias_grad = jnp.sum(grad_branch, axis=0, dtype=jnp.float32)
    branch_all = lax.all_gather(grad_branch, "tensor", axis=0, tiled=True)
    grad_acted = contract_cols(branch_all, down_full)
    down_weight_grad = contract_rows(acted, branch_all)
    grad_upper = (grad_acted * gelu_slope(upper)).astype(jnp.bfloat16)
    up_bias_grad = jnp.sum(grad_upper, axis=0, dtype=jnp.float32)
    up_weight_grad = contract_rows(hidden_all, grad_upper)
    grad_hidden = grad_second + lax.psum_scatter(
        contract_cols(grad_upper, up_full).astype(jnp.bfloat16),
        "tensor",
        scatter_dimension=0,
        tiled=True,
    ).astype(jnp.float32)
    grad_first, first_gain_grad, first_shift_grad = first_pull(grad_hidden)
    grad_attn = grad_first.astype(jnp.bfloat16)
    out_bias_grad = jnp.sum(grad_attn, axis=0, dtype=jnp.float32)
    attn_all = lax.all_gather(grad_attn, "tensor", axis=0, tiled=True)
    grad_context = contract_cols(attn_all, out_full).astype(jnp.bfloat16)
    out_weight_grad = contract_rows(context, attn_all)
    query_blocks = queries.reshape(seq_count, block_count, QB, heads_here, HD)
    grad_blocks = grad_context.reshape(seq_count, block_count, QB, heads_here, HD)
    log_blocks = log_totals.reshape(seq_count, block_count, heads_here, QB)

    def sequence_back(item):
        query_part, grad_part, log_part, key_rows, value_rows = item

        def block_back(carry, piece):
            key_acc, value_acc = carry
            query_rows, grad_rows, log_rows = piece
            logits = (
                jnp.einsum("qhd,khd->hqk", query_rows, key_rows, preferred_element_type=jnp.float32)
                * score_scale
            )
            probs = jnp.exp(logits - log_rows[:, :, None])
            probs_low = probs.astype(jnp.bfloat16)
            value_acc = value_acc + jnp.einsum(
                "hqk,qhd->khd", probs_low, grad_rows, preferred_element_type=jnp.float32
            )
            grad_probs = jnp.einsum(
                "qhd,khd->hqk", grad_rows, value_rows, preferred_element_type=jnp.float32
            )
            inner = jnp.sum(probs * grad_probs, axis=2, keepdims=True)
            grad_logits = (probs * (grad_probs - inner)).astype(jnp.bfloat16)
            grad_query = (
                jnp.einsum(
                    "hqk,khd->qhd", grad_logits, key_rows, preferred_element_type=jnp.float32
                )
                * score_scale
            )
            key_acc = (
                key_acc
                + jnp.einsum(
                    "hqk,qhd->khd", grad_logits, query_rows, preferred_element_type=jnp.float32
                )
                * score_scale
            )
            return ((key_acc, value_acc), grad_query.astype(jnp.bfloat16))

        empty = jnp.zeros((LEN, heads_here, HD), jnp.float32)
        (key_acc, value_acc), grad_query_rows = lax.scan(
            block_back, (empty, empty), (query_part, grad_part, log_part)
        )
        return (grad_query_rows, key_acc.astype(jnp.bfloat16), value_acc.astype(jnp.bfloat16))

    grad_queries_all, grad_keys_all, grad_values_all = lax.map(
        sequence_back, (query_blocks, grad_blocks, log_blocks, key_seq, value_seq)
    )
    grad_joint = jnp.concatenate(
        [
            grad_queries_all.reshape(group_rows, width),
            grad_keys_all.reshape(group_rows, width),
            grad_values_all.reshape(group_rows, width),
        ],
        axis=1,
    )
    joint_grad = contract_rows(gathered, grad_joint)
    query_weight_grad = joint_grad[:, :width]
    key_weight_grad = joint_grad[:, width : 2 * width]
    value_weight_grad = joint_grad[:, 2 * width :]
    query_bias_grad = jnp.sum(grad_joint[:, :width], axis=0, dtype=jnp.float32)
    value_bias_grad = jnp.sum(grad_joint[:, 2 * width :], axis=0, dtype=jnp.float32)
    tokens_grad = (
        grad_first
        + lax.psum_scatter(
            contract_cols(grad_joint, joint_weight).astype(jnp.bfloat16),
            "tensor",
            scatter_dimension=0,
            tiled=True,
        ).astype(jnp.float32)
    ).astype(jnp.bfloat16)
    (
        query_weight_grad,
        key_weight_grad,
        value_weight_grad,
        out_weight_grad,
        up_weight_grad,
        down_weight_grad,
    ) = (
        lax.psum_scatter(
            query_weight_grad.astype(jnp.bfloat16), "dp", scatter_dimension=0, tiled=True
        ).astype(jnp.float32),
        lax.psum_scatter(
            key_weight_grad.astype(jnp.bfloat16), "dp", scatter_dimension=0, tiled=True
        ).astype(jnp.float32),
        lax.psum_scatter(
            value_weight_grad.astype(jnp.bfloat16), "dp", scatter_dimension=0, tiled=True
        ).astype(jnp.float32),
        lax.psum_scatter(
            out_weight_grad.astype(jnp.bfloat16), "dp", scatter_dimension=1, tiled=True
        ).astype(jnp.float32),
        lax.psum_scatter(
            up_weight_grad.astype(jnp.bfloat16), "dp", scatter_dimension=0, tiled=True
        ).astype(jnp.float32),
        lax.psum_scatter(
            down_weight_grad.astype(jnp.bfloat16), "dp", scatter_dimension=1, tiled=True
        ).astype(jnp.float32),
    )
    tensor_place = lax.axis_index("tensor")
    model_width = out_bias.shape[0]
    query_spread = lax.dynamic_update_slice_in_dim(
        jnp.zeros((model_width,), jnp.float32), query_bias_grad, tensor_place * width, 0
    )
    value_spread = lax.dynamic_update_slice_in_dim(
        jnp.zeros((model_width,), jnp.float32), value_bias_grad, tensor_place * width, 0
    )
    up_spread = lax.dynamic_update_slice_in_dim(
        jnp.zeros((hidden_width * lax.axis_size("tensor"),), jnp.float32),
        up_bias_grad,
        tensor_place * hidden_width,
        0,
    )
    (
        query_spread,
        value_spread,
        up_spread,
        out_bias_grad,
        down_bias_grad,
        first_gain_grad,
        first_shift_grad,
        second_gain_grad,
        second_shift_grad,
    ) = lax.psum(
        (
            query_spread,
            value_spread,
            up_spread,
            out_bias_grad,
            down_bias_grad,
            first_gain_grad,
            first_shift_grad,
            second_gain_grad,
            second_shift_grad,
        ),
        ("dp", "tensor"),
    )
    query_bias_grad = lax.dynamic_slice_in_dim(query_spread, tensor_place * width, width, 0)
    value_bias_grad = lax.dynamic_slice_in_dim(value_spread, tensor_place * width, width, 0)
    up_bias_grad = lax.dynamic_slice_in_dim(up_spread, tensor_place * hidden_width, hidden_width, 0)
    factor = clip_limit / jnp.maximum(logit_peak, clip_limit)
    column_scale = jnp.repeat(jnp.sqrt(factor), HD)
    query_clipped = (query_weight.astype(jnp.float32) * column_scale).astype(jnp.bfloat16)
    query_bias_clipped = (query_bias.astype(jnp.float32) * column_scale).astype(jnp.bfloat16)
    key_clipped = (key_weight.astype(jnp.float32) * column_scale).astype(jnp.bfloat16)
    return (
        layer_out,
        tokens_grad,
        query_weight_grad,
        query_bias_grad,
        key_weight_grad,
        value_weight_grad,
        value_bias_grad,
        out_weight_grad,
        out_bias_grad,
        first_gain_grad,
        first_shift_grad,
        up_weight_grad,
        up_bias_grad,
        down_weight_grad,
        down_bias_grad,
        second_gain_grad,
        second_shift_grad,
        logit_peak,
        query_clipped,
        query_bias_clipped,
        key_clipped,
    )


LOG2E=1.4426950408889634
NT=(((1,),(1,)),((),()))
NN=(((1,),(0,)),((),()))
F32=jnp.float32
BF=jnp.bfloat16
MESH=pl.DeviceIdType.MESH
EPSILON=1e-5
NC=4


def dot(a,b,dims):
    return lax.dot_general(a,b,dims,preferred_element_type=jnp.float32)


def greet(partner):
    barrier=pltpu.get_barrier_semaphore()
    pl.semaphore_signal(barrier,inc=1,device_id=partner,device_id_type=MESH)
    pl.semaphore_wait(barrier,1)


def main_kernel(wq,wk,wv,wos,wu,wds,tok,cot_hbm,v_ob,v_g1,v_b1,v_db,v_g2,v_b2,v_ub,v_qb,v_vb,lim,
               lo_hbm,tg_hbm,fin,fin_head,go_hbm,qc_hbm,kc_hbm,smalls,dw,r1,r2,r3,x_hbm,wh_hbm,
               bias,vec,upb,gf,eb,er,lb,lr,sh,qkv,vt,kt,ctx,ctxo,lse,cl,wo,wup,wdn,xh,rst,hall,act,slp,ball,ga,dcs,dcall,part,pch,ctt,dqt,dl,dkv,sbuf,rbuf,tb,th,stage,
               lsem,losem,dsem,osem,ssem,rsem,rl,g1s,g1r,g2s,g2r,g3s,g3r,ts,tr,azs,azr,axs,axr,acs,acr,es,erc,ls,lrc,fl,fs):
    d=lax.axis_index("dp"); t=lax.axis_index("tensor")
    partner=(d,1-t)
    core=d%2; x_=(d//2)%2; z=d//4
    def dev(z_,xx,c_): return ((z_*2+xx)*2+c_,t)
    sib=dev(z,x_,1-core); xp=dev(z,1-x_,core); zp=[dev((z+k)%4,x_,core) for k in (1,2,3)]
    own,dm=tok.shape; cr=own//NC; cg=2*cr; rows_all=2*own; width=ctx.shape[1]; ff=wup.shape[2]; wide=wo.shape[2]; pairs=width//128
    def local(src,dst,i): return pltpu.make_async_copy(src,dst,lsem.at[i])
    def remote(src,dst,a,b,p): return pltpu.make_async_remote_copy(src,dst,a,b,device_id=p,device_id_type=MESH)
    cot_load=local(cot_hbm,cl,0)
    cot_load.start()
    barrier=pltpu.get_barrier_semaphore()
    n=3*width
    def row(v): return v[...].astype(F32).reshape(1,v.shape[0])
    sh[:,0:width]=wq[...]; sh[:,width:2*width]=wk[...]; sh[:,2*width:n]=wv[...]
    everyone=[partner,sib,xp]+zp
    for p in everyone: pl.semaphore_signal(barrier,inc=1,device_id=p,device_id_type=MESH)
    def chunk(c): return pl.ds(pl.multiple_of(c*cg,cg),cg)
    def rows(rank,c): return pl.ds(pl.multiple_of(c*cg+rank*cr,cr),cr)
    def half(rank): return pl.ds(pl.multiple_of(rank*cr,cr),cr)
    def loc(c): return pl.ds(pl.multiple_of(c*cr,cr),cr)
    def rs_copy(k,c):
        return pltpu.make_async_remote_copy(sbuf.at[k-1,loc(c)],rbuf.at[k-1,loc(c)],ssem.at[k,c],rsem.at[k,c],device_id=partner,device_id_type=MESH)
    def ag_copy(k,buf,c,rank):
        return pltpu.make_async_remote_copy(buf.at[rows(rank,c)],buf.at[rows(rank,c)],ssem.at[k,c],rsem.at[k,c],device_id=partner,device_id_type=MESH)
    def cols(rank): return pl.ds(pl.multiple_of(rank*width,128),width)
    def ctx_copy(c,rank):
        return pltpu.make_async_remote_copy(ctx.at[rows(1-rank,c)],ctxo.at[loc(c),cols(rank)],ssem.at[0,c],rsem.at[0,c],device_id=partner,device_id_type=MESH)
    def dctx_copy(c,rank):
        return pltpu.make_async_remote_copy(dcs.at[loc(c),cols(1-rank)],dcall.at[rows(rank,c)],ssem.at[5,c],rsem.at[5,c],device_id=partner,device_id_type=MESH)
    early=eb.at[0]
    early[...]=jnp.zeros((16,dm),F32)
    early[10:11]=jnp.full((1,dm),-jnp.inf,F32)
    lb[0]=jnp.zeros((8,dm),F32)
    def whole(w): return w[...].reshape(dm,w.shape[2])
    def strip(w,cs): return w[:,:,cs].reshape(dm,TF)
    dkv[...]=jnp.zeros_like(dkv)
    lane=lax.broadcasted_iota(jnp.int32,(1,128),1)
    scale=jnp.bfloat16(HD**-0.5); zero=jnp.bfloat16(0)
    q4=ff//2
    groups=[(act,0,0,width),(act,width,width,width),(act,2*width,2*width,width),(wo,0,n,wide),
            (wup,0,n+wide,q4),(wup,q4,n+wide+q4,q4),(wdn,0,n+wide+ff,q4),(wdn,q4,n+wide+ff+q4,q4)]
    def block(z_,xx): return (z_*2+xx)*2+core
    me=block(z,x_)
    def place(g,b):
        buf,c0,_,nc=groups[g]
        return buf.at[b,:,c0:c0+nc]
    def shard(g): return sh.at[:,groups[g][2]:groups[g][2]+groups[g][3]]
    up=dev(jnp.minimum(z+1,3),x_,core); down=dev(jnp.maximum(z-1,0),x_,core)
    def z_hop(g,way,j,b): return remote(shard(g) if j==1 else place(g,b),place(g,b),azs.at[g,way,j-1],azr.at[g,way,j-1],up if way==0 else down)
    def x_hop(g,zz,own_): return remote(shard(g) if own_ else place(g,block(zz,x_)),place(g,block(zz,x_)),axs.at[g,zz],axr.at[g,zz],xp)
    def x_land(g,zz): return remote(place(g,block(zz,1-x_)),place(g,block(zz,1-x_)),axs.at[g,zz],axr.at[g,zz],xp)
    def c_hop(g,xx,zz,b,own_): return remote(shard(g) if own_ else place(g,b),place(g,b),acs.at[g,4*xx+zz],acr.at[g,4*xx+zz],sib)
    def gather_start(g):
        buf,c0,s0,nc=groups[g]
        @pl.when(z<3)
        def _(): z_hop(g,0,1,me).start()
        @pl.when(z>0)
        def _(): z_hop(g,1,1,me).start()
        x_hop(g,z,True).start()
        c_hop(g,0,z,me,True).start()
        buf[me,:,c0:c0+nc]=sh[:,s0:s0+nc]
    def gather_z(g,j):
        for way in (0,1):
            here=(z>=j) if way==0 else (z+j<=3)
            zz=jnp.maximum(z-j,0) if way==0 else jnp.minimum(z+j,3)
            b=block(zz,x_)
            @pl.when(here)
            def _():
                z_hop(g,way,j,b).wait_recv()
                x_hop(g,zz,False).start()
                c_hop(g,0,zz,b,False).start()
            if j<3:
                @pl.when(here & ((z<3) if way==0 else (z>0)))
                def _(): z_hop(g,way,j+1,b).start()
    def gather_x(g):
        for zz in range(4):
            x_land(g,zz).wait_recv()
            c_hop(g,1,zz,block(zz,1-x_),False).start()
    def gather_done(g):
        for xx in (0,1):
            for zz in range(4):
                b=block(zz,x_)
                c_hop(g,xx,zz,b,False).wait_recv()
                c_hop(g,xx,zz,b,False).wait_send()
        for zz in range(4): x_land(g,zz).wait_send()
        for j in (1,2,3):
            @pl.when((z>=j-1) & (z<3))
            def _(): z_hop(g,0,j,me).wait_send()
            @pl.when((z+j-1<=3) & (z>0))
            def _(): z_hop(g,1,j,me).wait_send()
    own_copies=[local(tok.at[c*cr:(c+1)*cr],hall.at[rows(t,c)],1+c) for c in range(NC)]
    for c in own_copies: c.start()
    pl.semaphore_wait(barrier,len(everyone))
    gather_start(0); gather_start(1)
    def tok_copy(c): return remote(tok.at[loc(c)],hall.at[rows(t,c)],ts.at[c],tr.at[c],partner)
    def mine_o(rank): return sh.at[:,pl.ds(pl.multiple_of(n+rank*width,128),width)]
    o_swap=remote(mine_o(t),mine_o(t),ts.at[NC],tr.at[NC],partner)
    sh[:,pl.ds(pl.multiple_of(n+t*width,128),width)]=wos[...]
    o_swap.start()
    @pl.loop(0,NC)
    def _(c): tok_copy(c).start()
    sh[:,n+wide:n+wide+ff]=wu[...]
    sh[:,n+wide+ff:]=wds[...]
    for i,v in enumerate((v_ob,v_g1,v_b1,v_db,v_g2,v_b2)): vec[i:i+1]=row(v)
    upb[...]=row(v_ub)
    bias[...]=jnp.zeros_like(bias)
    bias[:,0:width]=row(v_qb); bias[:,2*width:]=row(v_vb)
    gather_z(0,1); gather_start(2)
    gather_z(1,1); gather_z(0,2)
    gather_z(2,1); o_swap.wait_recv(); gather_start(3)
    gather_z(1,2); gather_z(0,3); gather_z(2,2); gather_z(1,3)
    gather_x(0); gather_z(3,1); gather_z(2,3)
    gather_x(1); gather_z(3,2)
    gather_start(4)
    gather_x(2); gather_z(3,3); gather_z(4,1)
    for g in range(3): gather_done(g)
    for c in own_copies: c.wait()
    TF=512
    @pl.loop(0,NC)
    def _(c):
        tok_copy(c).wait_recv()
        @pl.loop(0,n//TF)
        def _(j):
            cs=pl.ds(pl.multiple_of(j*TF,TF),TF)
            qkv[chunk(c),cs]=(dot(hall[chunk(c)],strip(act,cs),NN)+bias[:,cs]).astype(BF)
        th[:,chunk(c)]=hall[chunk(c)].T
        @pl.when(c==0)
        def _(): gather_z(4,2)
        @pl.when(c==1)
        def _():
            gather_x(3); gather_z(4,3)
            gather_start(5)
        @pl.when(c==3)
        def _(): gather_done(3)
    x_out=local(th,x_hbm,5); w_out=local(act.at[:,:,0:n],wh_hbm,6)
    x_out.start(); w_out.start()
    ones=jnp.where(lax.broadcasted_iota(jnp.int32,(16,rows_all),0)==0,1.0,0.0).astype(BF)
    @pl.loop(0,pairs)
    def _(p):
        ck=pl.multiple_of(width+p*128,128); cv=pl.multiple_of(2*width+p*128,128)
        kt[p]=qkv[:,pl.ds(ck,128)].T
        v=qkv[:,pl.ds(cv,128)].T
        vt[2*p,0:64]=v[0:64]; vt[2*p,64:80]=ones
        vt[2*p+1,0:64]=v[64:128]; vt[2*p+1,64:80]=ones
    gather_z(5,1)
    def split(k,c):
        sbuf[k-1,loc(c)]=pch[half(1-t)].astype(BF)
        rs_copy(k,c).start()
        part[loc(c)]=pch[half(t)]
    def stats(v):
        cen=v-jnp.mean(v,axis=1,keepdims=True)
        r=lax.rsqrt(jnp.mean(cen*cen,axis=1,keepdims=True)+EPSILON)
        return cen*r,r
    def lo_copy(c): return pltpu.make_async_copy(cl.at[loc(c)],lo_hbm.at[loc(c)],losem.at[c])
    def own_tile(i,col): return pltpu.make_async_copy(stage.at[i%2,:,:,core],dw.at[:,:,core,:,pl.ds(col if isinstance(col,int) else pl.multiple_of(col,512),512)],osem.at[i%2])
    def pair_tile(i,g,off): return remote(stage.at[i%2,:,:,1-core],r1.at[g,:,:,:,pl.ds(off if isinstance(off,int) else pl.multiple_of(off,512),512)],g1s.at[i],g1r.at[i],sib)
    def wgrad(i,g,off,left,right_ref,rcol,ocol):
        if not isinstance(i,int) or 2<=i<8: own_tile(i-2,0).wait()
        if not isinstance(i,int) or i>=2: pair_tile(i-2,0,0).wait_send()
        @pl.loop(0,dm//256)
        def _(k):
            ms=pl.ds(pl.multiple_of(k*256,256),256)
            cs=pl.ds(rcol if isinstance(rcol,int) else pl.multiple_of(rcol,512),512)
            right=right_ref[:,cs] if len(right_ref.shape)==2 else strip(right_ref,cs)
            stage[i%2,k]=dot(left[ms],right,NN).astype(BF).reshape(2,2,64,512)
        own_tile(i,ocol).start()
        pair_tile(i,g,off).start()
    def stage_a(c):
        rs=chunk(c)
        @pl.loop(0,pairs//2)
        def _(pp):
            todo=[]
            for i in (0,1):
                p=2*pp+i
                cq=pl.ds(pl.multiple_of(p*128,128),128); ck=pl.ds(pl.multiple_of(width+p*128,128),128)
                for h in (0,1): todo.append((i,2*p+h,h,cq,ck,(lane<64) if h==0 else (lane>=64)))
            sts=[dot(qkv[:,ck],jnp.where(keep,qkv[rs,cq]*scale,zero),NT) for _,_,_,cq,ck,keep in todo]
            ms=[jnp.max(st,axis=0,keepdims=True) for st in sts]
            mcs=[v*LOG2E for v in ms]
            pts=[jnp.exp2(st*LOG2E-mc).astype(BF) for st,mc in zip(sts,mcs)]
            ots=[dot(vt[e[1]],pt,NN) for e,pt in zip(todo,pts)]
            for (i,hd,h,_,_,_),ot,mc in zip(todo,ots,mcs):
                tot=ot[64:65]
                ctt[i,h*64:(h+1)*64,:]=ot[0:64]*(1.0/tot)
                lse[pl.ds(hd,1),rs]=mc+jnp.log2(tot)
            tops=[jnp.max(v,axis=1,keepdims=True) for v in ms]
            for i in (0,1):
                cq=todo[2*i][3]
                early[10:11,cq]=jnp.maximum(early[10:11,cq],jnp.where(lane<64,tops[2*i],tops[2*i+1]))
                ctx[rs,cq]=ctt[i].T.astype(BF)
            step=c*(pairs//2)+pp
            @pl.when(step==2)
            def _():
                gather_z(5,2); gather_start(6)
            @pl.when(step==3)
            def _():
                gather_z(5,3)
            @pl.when(step==4)
            def _():
                gather_z(6,1); gather_start(7)
            @pl.when(step==6)
            def _():
                gather_z(6,2); gather_x(4)
            @pl.when(step==7)
            def _():
                gather_z(7,1)
        ctx_copy(c,t).start()
        ctxo[loc(c),cols(t)]=ctx[rows(t,c)]
    def stage_b(c):
        ctx_copy(c,1-t).wait_recv()
        x,r=stats(hall[rows(t,c)].astype(F32)+dot(ctxo[loc(c)],whole(wo),NT)+vec[0:1])
        xh[loc(c)]=x
        rst[loc(c)]=jnp.broadcast_to(r,(cr,128))
        hall[rows(t,c)]=(x*vec[1:2]+vec[2:3]).astype(BF)
        ag_copy(3,hall,c,t).start()
    def stage_c(c):
        rs=chunk(c)
        ag_copy(3,hall,c,1-t).wait_recv()
        @pl.loop(0,ff//TF)
        def _(j):
            cs=pl.ds(pl.multiple_of(j*TF,TF),TF)
            u=dot(hall[rs],strip(wup,cs),NN)+upb[:,cs]
            cdf=0.5*(1.0+lax.erf(u*0.5**0.5))
            act[pl.ds(4*c,4),:,cs]=(u*cdf).astype(BF).reshape(4,64,TF)
            slp[rs,cs]=(cdf+u*jnp.exp(-0.5*u*u)*(0.5/math.pi)**0.5).astype(BF)
    def stage_c2(c):
        pch[...]=dot(act[pl.ds(4*c,4)].reshape(cg,ff),whole(wdn),NT)
        split(1,c)
    def stage_d(c):
        rs_copy(1,c).wait_recv()
        x,r=stats(xh[loc(c)]*vec[1:2]+vec[2:3]+part[loc(c)]+rbuf[0,loc(c)].astype(F32)+vec[3:4])
        dy=cl[loc(c)].astype(F32)
        cl[loc(c)]=(x*vec[4:5]+vec[5:6]).astype(BF)
        lo_copy(c).start()
        early[4:5]+=jnp.sum(dy*x,axis=0,keepdims=True)
        early[5:6]+=jnp.sum(dy,axis=0,keepdims=True)
        dx=dy*vec[4:5]
        g=r*(dx-jnp.mean(dx,axis=1,keepdims=True)-x*jnp.mean(dx*x,axis=1,keepdims=True))
        gf[loc(c)]=g
        gb=g.astype(BF)
        early[3:4]+=jnp.sum(gb.astype(F32),axis=0,keepdims=True)
        ball[rows(t,c)]=gb
        ag_copy(4,ball,c,t).start()
        tb[:,rows(t,c)]=gb.T
    def stage_e(c):
        rs=chunk(c)
        ag_copy(4,ball,c,1-t).wait_recv()
        @pl.loop(0,ff//TF)
        def _(j):
            cs=pl.ds(pl.multiple_of(j*TF,TF),TF)
            gu=(dot(ball[rs],strip(wdn,cs),NN)*slp[rs,cs].astype(F32)).astype(BF)
            slp[rs,cs]=gu
            row=pl.ds(8+j*TF//dm,1); cc=pl.ds(pl.multiple_of(j*TF%dm,TF),TF)
            early[row,cc]+=jnp.sum(gu.astype(F32),axis=0,keepdims=True)
        pch[...]=dot(slp[rs],whole(wup),NT)
        split(2,c)
        tb[:,rows(1-t,c)]=ball[rows(1-t,c)].T
        th[:,chunk(c)]=hall[chunk(c)].T
    def stage_f(c):
        rs_copy(2,c).wait_recv()
        dy=gf[loc(c)]+part[loc(c)]+rbuf[1,loc(c)].astype(F32)
        x=xh[loc(c)]; r=rst[loc(c)][:,0:1]
        early[1:2]+=jnp.sum(dy*x,axis=0,keepdims=True)
        early[2:3]+=jnp.sum(dy,axis=0,keepdims=True)
        dx=dy*vec[1:2]
        g=r*(dx-jnp.mean(dx,axis=1,keepdims=True)-x*jnp.mean(dx*x,axis=1,keepdims=True))
        gf[loc(c)]=g
        gb=g.astype(BF)
        early[0:1]+=jnp.sum(gb.astype(F32),axis=0,keepdims=True)
        ga[loc(c)]=gb
        ball[rows(t,c)]=gb
        dcs[loc(c)]=dot(gb,whole(wo),NN).astype(BF)
        dctx_copy(c,t).start()
        dcall[rows(t,c)]=dcs[loc(c),cols(t)]
    def stage_g(c):
        rs=chunk(c)
        dctx_copy(c,1-t).wait_recv()
        @pl.when(c==0)
        def _():
            for i in range(NC): ga_copy(i).start()
        @pl.loop(0,pairs)
        def _(p):
            cq=pl.ds(pl.multiple_of(p*128,128),128); ck=pl.ds(pl.multiple_of(width+p*128,128),128); cv=pl.ds(pl.multiple_of(2*width+p*128,128),128)
            prod=(ctx[rs,cq].astype(F32)*dcall[rs,cq].astype(F32)).T
            dl[0:1]=jnp.sum(prod[0:64],axis=0,keepdims=True)
            dl[1:2]=jnp.sum(prod[64:128],axis=0,keepdims=True)
            for h in (0,1):
                keep=(lane<64) if h==0 else (lane>=64)
                q=jnp.where(keep,qkv[rs,cq]*scale,zero)
                do=jnp.where(keep,dcall[rs,cq],zero)
                st=dot(qkv[:,ck],q,NT)
                pt=jnp.exp2(st*LOG2E-lse[pl.ds(2*p+h,1),rs])
                dpt=dot(qkv[:,cv],do,NT)
                ds=(pt*(dpt-dl[h:h+1])).astype(BF)
                dkv[1,:,cq]+=dot(pt.astype(BF),do,NN)
                dkv[0,:,cq]+=dot(ds,q,NN)
                dqt[h*64:(h+1)*64,:]=dot(kt[p,h*64:(h+1)*64,:],ds,NN)
            qkv[rs,cq]=(dqt[...].T*(HD**-0.5)).astype(BF)
            step=c*pairs+p
            @pl.when(step==0)
            def _():
                add3(0)
                add2(2)
                fetch2(3)
            @pl.when(step==1)
            def _():
                add2(3)
                ecopy(0).start()
            @pl.when(step==4)
            def _():
                eadd(0); ecopy(1).start()
            @pl.when(step==5)
            def _():
                s2(1).wait_send(); s2(2).start()
                fetch3(1)
            @pl.when(step==6)
            def _():
                eadd(1); ecopy(2).start()
            @pl.when(step==7)
            def _():
                sent3(0); add3(1)
            @pl.when(step==8)
            def _():
                eadd(2); ecopy(3).start()
            @pl.when(step==9)
            def _():
                fetchf(0)
            @pl.when(step==10)
            def _():
                finish(0)
                eadd(3); ecopy(4).start()
            @pl.when(step==11)
            def _():
                s2(2).wait_send(); s2(3).start()
                fetch3(2)
            @pl.when(step==12)
            def _():
                for i in range(NC): ga_copy(i).wait_recv()
                for i in range(NC): th[:,i*cg:(i+1)*cg]=ball[i*cg:(i+1)*cg].T
            @pl.when(step==13)
            def _():
                sent3(1); add3(2)
                wgrad(8,4,0,th,ctx,0,base[4])
            @pl.when(step==14)
            def _():
                x_in.start()
            @pl.when(step==15)
            def _():
                fetch2(4)
    def grad_down(c): wgrad(c,c//2,c%2*512,tb,act,c*512,width+ff+c*512)
    def grad_up(c): wgrad(4+c,2+c//2,c%2*512,th,slp,c*512,width+c*512)
    def ga_copy(c):
        return pltpu.make_async_remote_copy(ga.at[loc(c)],ball.at[rows(t,c)],ssem.at[7,c],rsem.at[7,c],device_id=partner,device_id_type=MESH)
    @pl.loop(0,NC)
    def _(c):
        stage_a(c)
        @pl.when(c>0)
        def _(): stage_b(c-1)
    cot_load.wait(); w_out.wait(); x_out.wait()
    gather_z(6,3); gather_z(7,2)
    gather_x(5)
    gather_done(4); gather_done(5)
    @pl.loop(0,NC-1)
    def _(c):
        stage_c(c)
        @pl.when(c==0)
        def _():
            stage_b(NC-1)
            gather_z(7,3)
    gather_x(6); gather_x(7)
    gather_done(6); gather_done(7)
    @pl.loop(0,NC)
    def _(c):
        stage_c2(c)
        @pl.when(c==1)
        def _(): stage_c(NC-1)
    @pl.loop(0,NC)
    def _(c): stage_d(c)
    @pl.loop(0,NC)
    def _(c): stage_e(c)
    piece=ff//2
    base=(width+ff,width+ff+piece,width,width+piece,0,width+2*ff,2*width+2*ff,3*width+2*ff)
    span=(piece,)*4+(width,)*4
    tiles=((0,1),(2,3),(4,5),(6,7),(8,),(9,),(10,),(11,))
    slots2=[wup.at[8:12,:,0:piece],wup.at[12:16,:,0:piece],wup.at[8:12,:,piece:],wup.at[12:16,:,piece:],wup.at[0:4,:,piece:],wup.at[4:8,:,piece:]]
    slots3=[wdn.at[12:16,:,0:piece],wdn.at[12:16,:,piece:],wdn.at[0:4,:,piece:],wdn.at[4:8,:,piece:],wdn.at[8:12,:,piece:]]
    sum2=[slots2[g%6] for g in range(8)]
    sum3=[slots3[g%5] for g in range(8)]
    def s2(g): return remote(sum2[g].at[:,:,0:span[g]],r2.at[g,:,:,0:span[g]],g2s.at[g],g2r.at[g],xp)
    def s3(g,k): return remote(sum3[g].at[(z+k)%4,:,0:span[g]],r3.at[g,3-k,:,0:span[g]],g3s.at[g,k-1],g3r.at[g,k-1],zp[k-1])
    def load2(g): return [pltpu.make_async_copy(dw.at[:,1-x_,core,:,base[g]:base[g]+span[g]],wup.at[0:4,:,0:span[g]],rl.at[0]),
                          pltpu.make_async_copy(r1.at[g,:,1-x_,:,0:span[g]],wup.at[4:8,:,0:span[g]],rl.at[1])]
    def load3(g): return [pltpu.make_async_copy(dw.at[:,x_,core,:,base[g]:base[g]+span[g]],wdn.at[0:4,:,0:span[g]],rl.at[2]),
                         pltpu.make_async_copy(r1.at[g,:,x_,:,0:span[g]],wdn.at[4:8,:,0:span[g]],rl.at[3]),
                         pltpu.make_async_copy(r2.at[g,:,:,0:span[g]],wdn.at[8:12,:,0:span[g]],rl.at[4])]
    def fetch2(g):
        for i in tiles[g]:
            if i>=6: own_tile(i,0).wait()
            pair_tile(i,g,0).wait_recv()
        for l in load2(g): l.start()
    def add2(g):
        for l in load2(g): l.wait()
        @pl.loop(0,4)
        def _(i): sum2[g][i,:,0:span[g]]=(wup[i,:,0:span[g]].astype(F32)+wup[4+i,:,0:span[g]].astype(F32)).astype(BF)
    def fetch3(g):
        s2(g).wait_recv()
        for l in load3(g): l.start()
    def add3(g):
        for l in load3(g): l.wait()
        @pl.loop(0,4)
        def _(i): sum3[g][i,:,0:span[g]]=(wdn[i,:,0:span[g]].astype(F32)+wdn[4+i,:,0:span[g]].astype(F32)+wdn[8+i,:,0:span[g]].astype(F32)).astype(BF)
        for k in (1,2,3): s3(g,k).start()
    def sent3(g):
        for k in (1,2,3): s3(g,k).wait_send()
    def fslot(g,i):
        r=64*(6*(g%2)+i)
        return tb.at[r:r+64,0:span[g]]
    def loadf(g): return [pltpu.make_async_copy(src,fslot(g,i),fl.at[g%2,i]) for i,src in enumerate(
        [dw.at[z,x_,core,:,base[g]:base[g]+span[g]],r1.at[g,z,x_,:,0:span[g]],r2.at[g,z,:,0:span[g]]]+[r3.at[g,k,:,0:span[g]] for k in range(3)])]
    def fetchf(g):
        for k in (1,2,3): s3(g,k).wait_recv()
        for l in loadf(g): l.start()
    def final(g):
        for l in loadf(g): l.wait()
        v=[fslot(g,i)[...].astype(F32) for i in range(6)]
        return v[0]+v[1]+v[2]+v[3]+v[4]+v[5]
    def fin_copy(g):
        return pltpu.make_async_copy(xh.at[64*g:64*g+64,0:span[g]],fin.at[g] if g<4 else go_hbm if g==4 else fin_head.at[g-5],fs.at[g])
    def finish(g):
        xh[64*g:64*g+64,0:span[g]]=final(g)
        fin_copy(g).start()
    zb=[dev(z+1-2*(z%2),x_,core),dev((z+2)%4,x_,core)]
    hops=[sib,xp,zb[0],zb[1],partner]
    def ecopy(i): return remote(eb.at[i],er.at[i],es.at[i],erc.at[i],hops[i])
    def eadd(i):
        ecopy(i).wait_recv()
        b=eb[i,8:16]; c=er[i,8:16]
        if i<4:
            r=lax.broadcasted_iota(jnp.int32,b.shape,0)
            b=jnp.where(r==2,jnp.maximum(b,c),b+c)
        eb[i+1,0:8]=eb[i,0:8]+er[i,0:8]; eb[i+1,8:16]=b
    def lcopy(i): return remote(lb.at[i],lr.at[i],ls.at[i],lrc.at[i],hops[i])
    def ladd(i):
        lcopy(i).wait_recv()
        lb[i+1]=lb[i]+lr[i]
    @pl.loop(0,NC)
    def _(c):
        ag_copy(3,hall,c,t).wait_send()
        ag_copy(4,ball,c,t).wait_send()
    x_in=pltpu.make_async_copy(x_hbm,th,dsem.at[0])
    for c in range(3): grad_down(c)
    grad_down(3)
    fetch2(0)
    wh_in=pltpu.make_async_copy(wh_hbm,act.at[:,:,0:n],dsem.at[1])
    wh_in.start()
    add2(0); s2(0).start()
    @pl.loop(0,NC)
    def _(c):
        stage_f(c)
        grad_up(c)
        @pl.when(c==1)
        def _(): fetch2(1)
        @pl.when(c==2)
        def _(): add2(1)
        @pl.when(c==3)
        def _():
            fetch2(2)
            s2(0).wait_send(); s2(1).start()
            fetch3(0)
    @pl.loop(0,NC)
    def _(c): stage_g(c)
    add2(4)
    s2(3).wait_send(); s2(4).start()
    fetch3(3)
    x_in.wait()
    wgrad(9,5,0,th,qkv,0,base[5])
    sent3(2); add3(3)
    fetchf(1)
    @pl.loop(0,pairs)
    def _(p):
        cq=pl.ds(pl.multiple_of(p*128,128),128); ck=pl.ds(pl.multiple_of(width+p*128,128),128); cv=pl.ds(pl.multiple_of(2*width+p*128,128),128)
        qkv[:,ck]=dkv[0,:,cq].astype(BF)
        qkv[:,cv]=dkv[1,:,cq].astype(BF)
    fetch2(5)
    def ycopy(c): return remote(sbuf.at[0,loc(c)],rbuf.at[0,loc(c)],ssem.at[6,c],rsem.at[6,c],partner)
    wh_in.wait()
    def token_grad(c):
        pch[...]=dot(qkv[chunk(c)],act[:,:,0:n].reshape(dm,n),NT)
        rs_copy(1,c).wait_send()
        sbuf[0,loc(c)]=pch[half(1-t)].astype(BF)
        ycopy(c).start()
        part[loc(c)]=pch[half(t)]
    @pl.loop(0,2)
    def _(c): token_grad(c)
    add2(5)
    s2(4).wait_send(); s2(5).start()
    wgrad(10,6,0,th,qkv,width,base[6])
    fetch3(4)
    wgrad(11,7,0,th,qkv,2*width,base[7])
    fetch2(6)
    @pl.loop(2,NC)
    def _(c): token_grad(c)
    add2(6)
    s2(5).wait_send(); s2(6).start()
    fetch2(7)
    sent3(3); add3(4)
    fetch3(5)
    lb[0,0:1,0:width]=jnp.sum(qkv[:,0:width].astype(F32),axis=0,keepdims=True)
    lb[0,0:1,width:2*width]=jnp.sum(qkv[:,2*width:].astype(F32),axis=0,keepdims=True)
    lcopy(0).start()
    finish(1)
    add2(7)
    eadd(4)
    sent3(4); add3(5)
    s2(6).wait_send(); s2(7).start()
    fetch3(6)
    ladd(0); lcopy(1).start()
    fetchf(2)
    smalls[...]=eb[5]
    pk=eb[4,10:11,0:width]
    head=lax.broadcasted_iota(jnp.int32,(1,width),1)//HD
    limit=jnp.zeros((1,width),F32)
    for h in range(width//HD): limit=jnp.where(head==h,lim[h],limit)
    sc=jnp.sqrt(limit/jnp.maximum(pk,limit))
    ctxo[0:64,0:width]=(wq[...].astype(F32)*sc).astype(BF)
    ctxo[64:128,0:width]=(wk[...].astype(F32)*sc).astype(BF)
    clips=[pltpu.make_async_copy(ctxo.at[0:64,0:width],qc_hbm,fs.at[8]),pltpu.make_async_copy(ctxo.at[64:128,0:width],kc_hbm,fs.at[9])]
    for c in clips: c.start()
    smalls[11:12,0:width]=row(v_qb)*sc
    finish(2)
    ladd(1); lcopy(2).start()
    fetchf(3)
    sent3(5); add3(6)
    fetch3(7)
    finish(3)
    fetchf(4)
    ladd(2); lcopy(3).start()
    @pl.loop(0,NC)
    def _(c): lo_copy(c).wait()
    finish(4)
    sent3(6); add3(7)
    fetchf(5)
    def tg_copy(c): return pltpu.make_async_copy(cl.at[loc(c)],tg_hbm.at[loc(c)],losem.at[c])
    @pl.loop(0,NC)
    def _(c):
        ycopy(c).wait_recv()
        cl[loc(c)]=(gf[loc(c)]+part[loc(c)]+rbuf[0,loc(c)].astype(F32)).astype(BF)
        tg_copy(c).start()
    ladd(3)
    smalls[12:13]=lb[4,0:1]
    finish(5)
    fetchf(6)
    finish(6)
    fetchf(7)
    finish(7)
    o_swap.wait_send()
    for g in range(8):
        fin_copy(g).wait()
    for i in (10,11): pair_tile(i,0,0).wait_send()
    s2(7).wait_send()
    sent3(7)
    for c in clips: c.wait()
    for i in range(5): ecopy(i).wait_send()
    for i in range(4): lcopy(i).wait_send()
    @pl.loop(0,NC)
    def _(c):
        tg_copy(c).wait()
        ctx_copy(c,t).wait_send(); dctx_copy(c,t).wait_send(); tok_copy(c).wait_send()
        rs_copy(2,c).wait_send(); ycopy(c).wait_send()
        ga_copy(c).wait_send()

def main_call(shards,tok,cot,vectors,lim,cid):
    V=pl.BlockSpec(memory_space=pltpu.VMEM); A=pl.BlockSpec(memory_space=pl.ANY)
    width=shards[0].shape[1]; ff=shards[4].shape[1]; own,dm=tok.shape; rows=2*own; n=3*width; cr=own//NC; wide=2*width; piece=ff//2
    S=jax.ShapeDtypeStruct; M=pltpu.VMEM; D=pltpu.SemaphoreType.DMA
    return pl.pallas_call(main_kernel,
      out_shape=(S((own,dm),BF),S((own,dm),BF),S((4,64,piece),F32),S((3,64,width),F32),S((64,width),F32),S((64,width),BF),S((64,width),BF),S((16,dm),F32),
        S((4,2,2,64,width+2*ff+n),BF),S((8,4,2,64,piece),BF),S((8,4,64,piece),BF),S((8,3,64,piece),BF),S((dm,rows),BF),S((16,64,n),BF)),
      in_specs=[V]*6+[A,A]+[V]*9+[pl.BlockSpec(memory_space=pltpu.SMEM)],out_specs=(A,)*7+(V,)+(A,)*6,
      scratch_shapes=[M((1,n),F32),M((8,dm),F32),M((1,ff),F32),M((own,dm),F32),M((6,16,dm),F32),M((5,16,dm),F32),M((5,8,dm),F32),M((4,8,dm),F32),
        M((64,n+wide+2*ff),BF),M((rows,n),BF),M((width//HD,80,rows),BF),M((width//128,128,rows),BF),M((rows,width),BF),M((own,wide),BF),M((width//HD,rows),F32),M((own,dm),BF),
        M((16,64,wide),BF),M((16,64,ff),BF),M((16,64,ff),BF),
        M((own,dm),F32),M((own,128),F32),
        M((rows,dm),BF),M((16,64,ff),BF),M((rows,ff),BF),M((rows,dm),BF),M((own,dm),BF),M((own,wide),BF),M((rows,width),BF),
        M((own,dm),F32),M((2*cr,dm),F32),M((2,128,2*cr),F32),M((128,2*cr),F32),M((8,2*cr),F32),M((2,rows,width),F32),
        M((2,own,dm),BF),M((2,own,dm),BF),
        M((dm,rows),BF),M((dm,rows),BF),M((2,4,2,2,64,512),BF),
        D((7,)),D((NC,)),D((2,)),D((2,)),D((8,NC)),D((8,NC)),D((5,)),D((12,)),D((12,)),D((8,)),D((8,)),D((8,3)),D((8,3)),
        D((NC+1,)),D((NC+1,)),D((8,2,3)),D((8,2,3)),D((8,4)),D((8,4)),D((8,8)),D((8,8)),
        D((5,)),D((5,)),D((4,)),D((4,)),D((2,6)),D((10,))],
      compiler_params=pltpu.CompilerParams(collective_id=cid,has_side_effects=True,vmem_limit_bytes=61*2**20),
      name="main")(*shards,tok,cot,*vectors,lim)

def finish_kernel(lo,tg,fin,fin_head,go,qc,kc,smalls,
                  lo_,tg_,gq_,gk_,gv_,go_,gu_,gd_,qc_,kc_,qb_,vb_,ob_,g1_,b1_,ub_,db_,g2_,b2_,pk_,qbc_,h_lo,h_tg,h_fin,h_head,h_go,h_qc,h_kc,isem,sem):
    piece=fin.shape[2]
    ins=[pltpu.make_async_copy(a,b,isem.at[i]) for i,(a,b) in enumerate(((lo,h_lo),(tg,h_tg),(fin,h_fin),(fin_head,h_head),(go,h_go),(qc,h_qc),(kc,h_kc)))]
    outs=[[(h_lo,lo_)],[(h_tg,tg_)],[(h_fin.at[0],gd_.at[:,0:piece]),(h_fin.at[1],gd_.at[:,piece:]),(h_fin.at[2],gu_.at[:,0:piece]),(h_fin.at[3],gu_.at[:,piece:])],
          [(h_head.at[0],gq_),(h_head.at[1],gk_),(h_head.at[2],gv_)],[(h_go,go_)],[(h_qc,qc_)],[(h_kc,kc_)]]
    for c in ins: c.start()
    width=qb_.shape[0]; dm=ob_.shape[0]
    def line(v): return v.reshape(v.shape[1])
    qb_[...]=line(smalls[12:13,0:width]); vb_[...]=line(smalls[12:13,width:2*width])
    for i,o in enumerate((ob_,g1_,b1_,db_,g2_,b2_)): o[...]=line(smalls[i:i+1])
    ub_[0:dm]=line(smalls[8:9]); ub_[dm:2*dm]=line(smalls[9:10])
    for h in range(pk_.shape[0]): pk_[h]=jnp.max(smalls[10:11,h*HD:(h+1)*HD])
    qbc_[...]=line(smalls[11:12,0:width]).astype(BF)
    moved=[]
    for a,group in zip(ins,outs):
        a.wait()
        for src,dst in group:
            c=pltpu.make_async_copy(src,dst,sem.at[len(moved)])
            c.start()
            moved.append(c)
    for c in moved: c.wait()

def finish_call(big,smalls,heads):
    V=pl.BlockSpec(memory_space=pltpu.VMEM); A=pl.BlockSpec(memory_space=pl.ANY); S=jax.ShapeDtypeStruct
    lo,tg,fin,fin_head,go,qc,kc=big
    width=go.shape[1]; piece=fin.shape[2]; ff=2*piece; dm=tg.shape[1]
    return pl.pallas_call(finish_kernel,
      out_shape=(S(lo.shape,BF),S(tg.shape,BF))+(S((64,width),F32),)*4+(S((64,ff),F32),)*2+(S((64,width),BF),)*2
        +tuple(S((k,),F32) for k in (width,width,dm,dm,dm,ff,dm,dm,dm,heads))+(S((width,),BF),),
      in_specs=[A]*7+[V],out_specs=(A,)*10+(V,)*9+(pl.BlockSpec(memory_space=pltpu.SMEM),V),
      scratch_shapes=[pltpu.VMEM(a.shape,a.dtype) for a in big]+[pltpu.SemaphoreType.DMA((7,)),pltpu.SemaphoreType.DMA((12,))],
      compiler_params=pltpu.CompilerParams(vmem_limit_bytes=61*2**20),name="finish")(*big,smalls)

def per_device_pair(tokens,query_weight,query_bias,key_weight,value_weight,value_bias,out_weight,out_bias,first_gain,first_shift,
    up_weight,up_bias,down_weight,down_bias,second_gain,second_shift,cotangent,clip_limit):
    shards=(query_weight,key_weight,value_weight,out_weight.T,up_weight,down_weight.T)
    vectors=(out_bias,first_gain,first_shift,down_bias,second_gain,second_shift,up_bias,query_bias,value_bias)
    res=main_call(shards,tokens,cotangent,vectors,clip_limit,1)
    lo,tg,gq,gk,gv,go,gu,gd,qc,kc,qb,vb,ob,g1,b1,ub,db,g2,b2,pk,qbc=finish_call(res[:7],res[7],clip_limit.shape[0])
    return (lo,tg,gq,qb,gk,gv,vb,go.T,ob,g1,b1,gu,ub,gd.T,db,g2,b2,pk,qc,qbc,kc)


def layer(*args):
    paired = lax.axis_size("dp") == 16 and lax.axis_size("tensor") == 2 and 2 * args[0].shape[0] == LEN
    return per_device_pair(*args) if paired else per_device(*args)


def solution(mesh):
    in_specs = (
        P(("dp", "tensor"), None),
        P("dp", "tensor"),
        P("tensor"),
        P("dp", "tensor"),
        P("dp", "tensor"),
        P("tensor"),
        P("tensor", "dp"),
        P(),
        P(),
        P(),
        P("dp", "tensor"),
        P("tensor"),
        P("tensor", "dp"),
        P(),
        P(),
        P(),
        P(("dp", "tensor"), None),
        P("tensor"),
    )
    out_specs = (
        P(("dp", "tensor"), None),
        P(("dp", "tensor"), None),
        P("dp", "tensor"),
        P("tensor"),
        P("dp", "tensor"),
        P("dp", "tensor"),
        P("tensor"),
        P("tensor", "dp"),
        P(),
        P(),
        P(),
        P("dp", "tensor"),
        P("tensor"),
        P("tensor", "dp"),
        P(),
        P(),
        P(),
        P("tensor"),
        P("dp", "tensor"),
        P("tensor"),
        P("dp", "tensor"),
    )
    return jax.shard_map(
        layer, mesh=mesh, in_specs=in_specs, out_specs=out_specs, check_vma=False
    )
```

```python
import functools
import math

import jax
import jax.numpy as jnp
from jax import lax
from jax.experimental import pallas as pl
from jax.experimental.pallas import tpu as pltpu
from jax.sharding import PartitionSpec as P

HD = 64
LEN = 1024
QB = 512


def layer_norm(values, gain, shift):
    center = values - jnp.mean(values, axis=-1, keepdims=True)
    spread = jnp.mean(center * center, axis=-1, keepdims=True)
    return center * lax.rsqrt(spread + EPSILON) * gain + shift


def gelu_slope(upper):
    normal_cdf = 0.5 * (1.0 + lax.erf(upper * 0.5**0.5))
    return normal_cdf + upper * jnp.exp(-0.5 * upper * upper) * (0.5 / math.pi) ** 0.5


def contract_rows(left, right):
    return lax.dot_general(
        left, right, (((0,), (0,)), ((), ())), preferred_element_type=jnp.float32
    )


def contract_cols(left, right):
    return lax.dot_general(
        left, right, (((1,), (1,)), ((), ())), preferred_element_type=jnp.float32
    )


def per_device(
    tokens,
    query_weight,
    query_bias,
    key_weight,
    value_weight,
    value_bias,
    out_weight,
    out_bias,
    first_gain,
    first_shift,
    up_weight,
    up_bias,
    down_weight,
    down_bias,
    second_gain,
    second_shift,
    cotangent,
    clip_limit,
):
    query_full, key_full, value_full, out_full, up_full, down_full = (
        lax.all_gather(query_weight, "dp", axis=0, tiled=True),
        lax.all_gather(key_weight, "dp", axis=0, tiled=True),
        lax.all_gather(value_weight, "dp", axis=0, tiled=True),
        lax.all_gather(out_weight, "dp", axis=1, tiled=True),
        lax.all_gather(up_weight, "dp", axis=0, tiled=True),
        lax.all_gather(down_weight, "dp", axis=1, tiled=True),
    )
    width = query_full.shape[1]
    hidden_width = up_full.shape[1]
    heads_here = width // HD
    score_scale = HD ** (-0.5)
    joint_weight = jnp.concatenate([query_full, key_full, value_full], axis=1)
    gathered = lax.all_gather(tokens, "tensor", axis=0, tiled=True)
    group_rows = gathered.shape[0]
    seq_count = group_rows // LEN
    block_count = LEN // QB
    projected = jnp.dot(gathered, joint_weight, preferred_element_type=jnp.float32)
    queries = (projected[:, :width] + query_bias.astype(jnp.float32)).astype(jnp.bfloat16)
    keyset = projected[:, width : 2 * width].astype(jnp.bfloat16)
    valset = (projected[:, 2 * width :] + value_bias.astype(jnp.float32)).astype(jnp.bfloat16)
    query_seq = queries.reshape(seq_count, LEN, heads_here, HD)
    key_seq = keyset.reshape(seq_count, LEN, heads_here, HD)
    value_seq = valset.reshape(seq_count, LEN, heads_here, HD)

    def attend_block(block_id):
        seq_id = block_id // block_count
        row_start = block_id % block_count * QB
        query_rows = lax.dynamic_slice_in_dim(
            lax.dynamic_index_in_dim(query_seq, seq_id, 0, False), row_start, QB, 0
        )
        key_rows = lax.dynamic_index_in_dim(key_seq, seq_id, 0, False)
        value_rows = lax.dynamic_index_in_dim(value_seq, seq_id, 0, False)
        logits = (
            jnp.einsum("qhd,khd->hqk", query_rows, key_rows, preferred_element_type=jnp.float32)
            * score_scale
        )
        row_max = jnp.max(logits, axis=2, keepdims=True)
        exponent = jnp.exp(logits - row_max)
        totals = jnp.sum(exponent, axis=2, keepdims=True)
        probs_low = (exponent / totals).astype(jnp.bfloat16)
        context_rows = jnp.einsum(
            "hqk,khd->qhd", probs_low, value_rows, preferred_element_type=jnp.float32
        )
        return (
            context_rows.reshape(QB, width).astype(jnp.bfloat16),
            (row_max + jnp.log(totals))[:, :, 0],
            jnp.max(row_max, axis=(1, 2)),
        )

    context_blocks, log_totals, block_peaks = lax.map(
        attend_block, jnp.arange(seq_count * block_count)
    )
    context = context_blocks.reshape(group_rows, width)
    logit_peak = lax.pmax(jnp.max(block_peaks, axis=0), "dp")
    attention = lax.psum_scatter(
        jnp.dot(context, out_full, preferred_element_type=jnp.float32).astype(jnp.bfloat16),
        "tensor",
        scatter_dimension=0,
        tiled=True,
    ).astype(jnp.float32) + out_bias.astype(jnp.float32)
    first_resid = tokens.astype(jnp.float32) + attention
    hidden, first_pull = jax.vjp(
        layer_norm, first_resid, first_gain.astype(jnp.float32), first_shift.astype(jnp.float32)
    )
    hidden_all = lax.all_gather(hidden.astype(jnp.bfloat16), "tensor", axis=0, tiled=True)
    upper = jnp.dot(hidden_all, up_full, preferred_element_type=jnp.float32) + up_bias.astype(
        jnp.float32
    )
    acted = jax.nn.gelu(upper, approximate=False).astype(jnp.bfloat16)
    branch = lax.psum_scatter(
        jnp.dot(acted, down_full, preferred_element_type=jnp.float32).astype(jnp.bfloat16),
        "tensor",
        scatter_dimension=0,
        tiled=True,
    ).astype(jnp.float32) + down_bias.astype(jnp.float32)
    normed, second_pull = jax.vjp(
        layer_norm,
        hidden + branch,
        second_gain.astype(jnp.float32),
        second_shift.astype(jnp.float32),
    )
    layer_out = normed.astype(jnp.bfloat16)
    grad_second, second_gain_grad, second_shift_grad = second_pull(cotangent.astype(jnp.float32))
    grad_branch = grad_second.astype(jnp.bfloat16)
    down_bias_grad = jnp.sum(grad_branch, axis=0, dtype=jnp.float32)
    branch_all = lax.all_gather(grad_branch, "tensor", axis=0, tiled=True)
    grad_acted = contract_cols(branch_all, down_full)
    down_weight_grad = contract_rows(acted, branch_all)
    grad_upper = (grad_acted * gelu_slope(upper)).astype(jnp.bfloat16)
    up_bias_grad = jnp.sum(grad_upper, axis=0, dtype=jnp.float32)
    up_weight_grad = contract_rows(hidden_all, grad_upper)
    grad_hidden = grad_second + lax.psum_scatter(
        contract_cols(grad_upper, up_full).astype(jnp.bfloat16),
        "tensor",
        scatter_dimension=0,
        tiled=True,
    ).astype(jnp.float32)
    grad_first, first_gain_grad, first_shift_grad = first_pull(grad_hidden)
    grad_attn = grad_first.astype(jnp.bfloat16)
    out_bias_grad = jnp.sum(grad_attn, axis=0, dtype=jnp.float32)
    attn_all = lax.all_gather(grad_attn, "tensor", axis=0, tiled=True)
    grad_context = contract_cols(attn_all, out_full).astype(jnp.bfloat16)
    out_weight_grad = contract_rows(context, attn_all)
    query_blocks = queries.reshape(seq_count, block_count, QB, heads_here, HD)
    grad_blocks = grad_context.reshape(seq_count, block_count, QB, heads_here, HD)
    log_blocks = log_totals.reshape(seq_count, block_count, heads_here, QB)

    def sequence_back(item):
        query_part, grad_part, log_part, key_rows, value_rows = item

        def block_back(carry, piece):
            key_acc, value_acc = carry
            query_rows, grad_rows, log_rows = piece
            logits = (
                jnp.einsum("qhd,khd->hqk", query_rows, key_rows, preferred_element_type=jnp.float32)
                * score_scale
            )
            probs = jnp.exp(logits - log_rows[:, :, None])
            probs_low = probs.astype(jnp.bfloat16)
            value_acc = value_acc + jnp.einsum(
                "hqk,qhd->khd", probs_low, grad_rows, preferred_element_type=jnp.float32
            )
            grad_probs = jnp.einsum(
                "qhd,khd->hqk", grad_rows, value_rows, preferred_element_type=jnp.float32
            )
            inner = jnp.sum(probs * grad_probs, axis=2, keepdims=True)
            grad_logits = (probs * (grad_probs - inner)).astype(jnp.bfloat16)
            grad_query = (
                jnp.einsum(
                    "hqk,khd->qhd", grad_logits, key_rows, preferred_element_type=jnp.float32
                )
                * score_scale
            )
            key_acc = (
                key_acc
                + jnp.einsum(
                    "hqk,qhd->khd", grad_logits, query_rows, preferred_element_type=jnp.float32
                )
                * score_scale
            )
            return ((key_acc, value_acc), grad_query.astype(jnp.bfloat16))

        empty = jnp.zeros((LEN, heads_here, HD), jnp.float32)
        (key_acc, value_acc), grad_query_rows = lax.scan(
            block_back, (empty, empty), (query_part, grad_part, log_part)
        )
        return (grad_query_rows, key_acc.astype(jnp.bfloat16), value_acc.astype(jnp.bfloat16))

    grad_queries_all, grad_keys_all, grad_values_all = lax.map(
        sequence_back, (query_blocks, grad_blocks, log_blocks, key_seq, value_seq)
    )
    grad_joint = jnp.concatenate(
        [
            grad_queries_all.reshape(group_rows, width),
            grad_keys_all.reshape(group_rows, width),
            grad_values_all.reshape(group_rows, width),
        ],
        axis=1,
    )
    joint_grad = contract_rows(gathered, grad_joint)
    query_weight_grad = joint_grad[:, :width]
    key_weight_grad = joint_grad[:, width : 2 * width]
    value_weight_grad = joint_grad[:, 2 * width :]
    query_bias_grad = jnp.sum(grad_joint[:, :width], axis=0, dtype=jnp.float32)
    value_bias_grad = jnp.sum(grad_joint[:, 2 * width :], axis=0, dtype=jnp.float32)
    tokens_grad = (
        grad_first
        + lax.psum_scatter(
            contract_cols(grad_joint, joint_weight).astype(jnp.bfloat16),
            "tensor",
            scatter_dimension=0,
            tiled=True,
        ).astype(jnp.float32)
    ).astype(jnp.bfloat16)
    (
        query_weight_grad,
        key_weight_grad,
        value_weight_grad,
        out_weight_grad,
        up_weight_grad,
        down_weight_grad,
    ) = (
        lax.psum_scatter(
            query_weight_grad.astype(jnp.bfloat16), "dp", scatter_dimension=0, tiled=True
        ).astype(jnp.float32),
        lax.psum_scatter(
            key_weight_grad.astype(jnp.bfloat16), "dp", scatter_dimension=0, tiled=True
        ).astype(jnp.float32),
        lax.psum_scatter(
            value_weight_grad.astype(jnp.bfloat16), "dp", scatter_dimension=0, tiled=True
        ).astype(jnp.float32),
        lax.psum_scatter(
            out_weight_grad.astype(jnp.bfloat16), "dp", scatter_dimension=1, tiled=True
        ).astype(jnp.float32),
        lax.psum_scatter(
            up_weight_grad.astype(jnp.bfloat16), "dp", scatter_dimension=0, tiled=True
        ).astype(jnp.float32),
        lax.psum_scatter(
            down_weight_grad.astype(jnp.bfloat16), "dp", scatter_dimension=1, tiled=True
        ).astype(jnp.float32),
    )
    tensor_place = lax.axis_index("tensor")
    model_width = out_bias.shape[0]
    query_spread = lax.dynamic_update_slice_in_dim(
        jnp.zeros((model_width,), jnp.float32), query_bias_grad, tensor_place * width, 0
    )
    value_spread = lax.dynamic_update_slice_in_dim(
        jnp.zeros((model_width,), jnp.float32), value_bias_grad, tensor_place * width, 0
    )
    up_spread = lax.dynamic_update_slice_in_dim(
        jnp.zeros((hidden_width * lax.axis_size("tensor"),), jnp.float32),
        up_bias_grad,
        tensor_place * hidden_width,
        0,
    )
    (
        query_spread,
        value_spread,
        up_spread,
        out_bias_grad,
        down_bias_grad,
        first_gain_grad,
        first_shift_grad,
        second_gain_grad,
        second_shift_grad,
    ) = lax.psum(
        (
            query_spread,
            value_spread,
            up_spread,
            out_bias_grad,
            down_bias_grad,
            first_gain_grad,
            first_shift_grad,
            second_gain_grad,
            second_shift_grad,
        ),
        ("dp", "tensor"),
    )
    query_bias_grad = lax.dynamic_slice_in_dim(query_spread, tensor_place * width, width, 0)
    value_bias_grad = lax.dynamic_slice_in_dim(value_spread, tensor_place * width, width, 0)
    up_bias_grad = lax.dynamic_slice_in_dim(up_spread, tensor_place * hidden_width, hidden_width, 0)
    factor = clip_limit / jnp.maximum(logit_peak, clip_limit)
    column_scale = jnp.repeat(jnp.sqrt(factor), HD)
    query_clipped = (query_weight.astype(jnp.float32) * column_scale).astype(jnp.bfloat16)
    query_bias_clipped = (query_bias.astype(jnp.float32) * column_scale).astype(jnp.bfloat16)
    key_clipped = (key_weight.astype(jnp.float32) * column_scale).astype(jnp.bfloat16)
    return (
        layer_out,
        tokens_grad,
        query_weight_grad,
        query_bias_grad,
        key_weight_grad,
        value_weight_grad,
        value_bias_grad,
        out_weight_grad,
        out_bias_grad,
        first_gain_grad,
        first_shift_grad,
        up_weight_grad,
        up_bias_grad,
        down_weight_grad,
        down_bias_grad,
        second_gain_grad,
        second_shift_grad,
        logit_peak,
        query_clipped,
        query_bias_clipped,
        key_clipped,
    )


LOG2E=1.4426950408889634
NT=(((1,),(1,)),((),()))
NN=(((1,),(0,)),((),()))
F32=jnp.float32
BF=jnp.bfloat16
MESH=pl.DeviceIdType.MESH
EPSILON=1e-5
NC=4


def dot(a,b,dims):
    return lax.dot_general(a,b,dims,preferred_element_type=jnp.float32)


def greet(partner):
    barrier=pltpu.get_barrier_semaphore()
    pl.semaphore_signal(barrier,inc=1,device_id=partner,device_id_type=MESH)
    pl.semaphore_wait(barrier,1)


def main_kernel(wq,wk,wv,wos,wu,wds,tok,cot_hbm,v_ob,v_g1,v_b1,v_db,v_g2,v_b2,v_ub,v_qb,v_vb,lim,
               lo_hbm,tg_hbm,fin,fin_head,go_hbm,qc_hbm,kc_hbm,smalls,dw,r1,r2,r3,x_hbm,wh_hbm,
               bias,vec,upb,gf,eb,er,lb,lr,sh,qkv,vt,kt,ctx,ctxo,lse,cl,wo,wup,wdn,xh,rst,hall,act,slp,ball,ga,dcs,dcall,part,pch,ctt,dqt,dl,dkv,sbuf,rbuf,tb,th,stage,
               lsem,losem,dsem,osem,ssem,rsem,rl,g1s,g1r,g2s,g2r,g3s,g3r,ts,tr,azs,azr,axs,axr,acs,acr,es,erc,ls,lrc,fl,fs):
    d=lax.axis_index("dp"); t=lax.axis_index("tensor")
    partner=(d,1-t)
    core=d%2; x_=(d//2)%2; z=d//4
    def dev(z_,xx,c_): return ((z_*2+xx)*2+c_,t)
    sib=dev(z,x_,1-core); xp=dev(z,1-x_,core); zp=[dev((z+k)%4,x_,core) for k in (1,2,3)]
    own,dm=tok.shape; cr=own//NC; cg=2*cr; rows_all=2*own; width=ctx.shape[1]; ff=wup.shape[2]; wide=wo.shape[2]; pairs=width//128
    def local(src,dst,i): return pltpu.make_async_copy(src,dst,lsem.at[i])
    def remote(src,dst,a,b,p): return pltpu.make_async_remote_copy(src,dst,a,b,device_id=p,device_id_type=MESH)
    cot_load=local(cot_hbm,cl,0)
    cot_load.start()
    barrier=pltpu.get_barrier_semaphore()
    n=3*width
    def row(v): return v[...].astype(F32).reshape(1,v.shape[0])
    sh[:,0:width]=wq[...]; sh[:,width:2*width]=wk[...]; sh[:,2*width:n]=wv[...]
    everyone=[partner,sib,xp]+zp
    for p in everyone: pl.semaphore_signal(barrier,inc=1,device_id=p,device_id_type=MESH)
    def chunk(c): return pl.ds(pl.multiple_of(c*cg,cg),cg)
    def rows(rank,c): return pl.ds(pl.multiple_of(c*cg+rank*cr,cr),cr)
    def half(rank): return pl.ds(pl.multiple_of(rank*cr,cr),cr)
    def loc(c): return pl.ds(pl.multiple_of(c*cr,cr),cr)
    def rs_copy(k,c):
        return pltpu.make_async_remote_copy(sbuf.at[k-1,loc(c)],rbuf.at[k-1,loc(c)],ssem.at[k,c],rsem.at[k,c],device_id=partner,device_id_type=MESH)
    def ag_copy(k,buf,c,rank):
        return pltpu.make_async_remote_copy(buf.at[rows(rank,c)],buf.at[rows(rank,c)],ssem.at[k,c],rsem.at[k,c],device_id=partner,device_id_type=MESH)
    def cols(rank): return pl.ds(pl.multiple_of(rank*width,128),width)
    def ctx_copy(c,rank):
        return pltpu.make_async_remote_copy(ctx.at[rows(1-rank,c)],ctxo.at[loc(c),cols(rank)],ssem.at[0,c],rsem.at[0,c],device_id=partner,device_id_type=MESH)
    def dctx_copy(c,rank):
        return pltpu.make_async_remote_copy(dcs.at[loc(c),cols(1-rank)],dcall.at[rows(rank,c)],ssem.at[5,c],rsem.at[5,c],device_id=partner,device_id_type=MESH)
    early=eb.at[0]
    early[...]=jnp.zeros((16,dm),F32)
    early[10:11]=jnp.full((1,dm),-jnp.inf,F32)
    lb[0]=jnp.zeros((8,dm),F32)
    def whole(w): return w[...].reshape(dm,w.shape[2])
    def strip(w,cs): return w[:,:,cs].reshape(dm,TF)
    dkv[...]=jnp.zeros_like(dkv)
    lane=lax.broadcasted_iota(jnp.int32,(1,128),1)
    scale=jnp.bfloat16(HD**-0.5); zero=jnp.bfloat16(0)
    q4=ff//2
    groups=[(act,0,0,width),(act,width,width,width),(act,2*width,2*width,width),(wo,0,n,wide),
            (wup,0,n+wide,q4),(wup,q4,n+wide+q4,q4),(wdn,0,n+wide+ff,q4),(wdn,q4,n+wide+ff+q4,q4)]
    def block(z_,xx): return (z_*2+xx)*2+core
    me=block(z,x_)
    def place(g,b):
        buf,c0,_,nc=groups[g]
        return buf.at[b,:,c0:c0+nc]
    def shard(g): return sh.at[:,groups[g][2]:groups[g][2]+groups[g][3]]
    up=dev(jnp.minimum(z+1,3),x_,core); down=dev(jnp.maximum(z-1,0),x_,core)
    def z_hop(g,way,j,b): return remote(shard(g) if j==1 else place(g,b),place(g,b),azs.at[g,way,j-1],azr.at[g,way,j-1],up if way==0 else down)
    def x_hop(g,zz,own_): return remote(shard(g) if own_ else place(g,block(zz,x_)),place(g,block(zz,x_)),axs.at[g,zz],axr.at[g,zz],xp)
    def x_land(g,zz): return remote(place(g,block(zz,1-x_)),place(g,block(zz,1-x_)),axs.at[g,zz],axr.at[g,zz],xp)
    def c_hop(g,xx,zz,b,own_): return remote(shard(g) if own_ else place(g,b),place(g,b),acs.at[g,4*xx+zz],acr.at[g,4*xx+zz],sib)
    def gather_start(g):
        buf,c0,s0,nc=groups[g]
        @pl.when(z<3)
        def _(): z_hop(g,0,1,me).start()
        @pl.when(z>0)
        def _(): z_hop(g,1,1,me).start()
        x_hop(g,z,True).start()
        c_hop(g,0,z,me,True).start()
        buf[me,:,c0:c0+nc]=sh[:,s0:s0+nc]
    def gather_z(g,j):
        for way in (0,1):
            here=(z>=j) if way==0 else (z+j<=3)
            zz=jnp.maximum(z-j,0) if way==0 else jnp.minimum(z+j,3)
            b=block(zz,x_)
            @pl.when(here)
            def _():
                z_hop(g,way,j,b).wait_recv()
                x_hop(g,zz,False).start()
                c_hop(g,0,zz,b,False).start()
            if j<3:
                @pl.when(here & ((z<3) if way==0 else (z>0)))
                def _(): z_hop(g,way,j+1,b).start()
    def gather_x(g):
        for zz in range(4):
            x_land(g,zz).wait_recv()
            c_hop(g,1,zz,block(zz,1-x_),False).start()
    def gather_done(g):
        for xx in (0,1):
            for zz in range(4):
                b=block(zz,x_)
                c_hop(g,xx,zz,b,False).wait_recv()
                c_hop(g,xx,zz,b,False).wait_send()
        for zz in range(4): x_land(g,zz).wait_send()
        for j in (1,2,3):
            @pl.when((z>=j-1) & (z<3))
            def _(): z_hop(g,0,j,me).wait_send()
            @pl.when((z+j-1<=3) & (z>0))
            def _(): z_hop(g,1,j,me).wait_send()
    own_copies=[local(tok.at[c*cr:(c+1)*cr],hall.at[rows(t,c)],1+c) for c in range(NC)]
    for c in own_copies: c.start()
    pl.semaphore_wait(barrier,len(everyone))
    gather_start(0); gather_start(1)
    def tok_copy(c): return remote(tok.at[loc(c)],hall.at[rows(t,c)],ts.at[c],tr.at[c],partner)
    def mine_o(rank): return sh.at[:,pl.ds(pl.multiple_of(n+rank*width,128),width)]
    o_swap=remote(mine_o(t),mine_o(t),ts.at[NC],tr.at[NC],partner)
    sh[:,pl.ds(pl.multiple_of(n+t*width,128),width)]=wos[...]
    o_swap.start()
    @pl.loop(0,NC)
    def _(c): tok_copy(c).start()
    sh[:,n+wide:n+wide+ff]=wu[...]
    sh[:,n+wide+ff:]=wds[...]
    for i,v in enumerate((v_ob,v_g1,v_b1,v_db,v_g2,v_b2)): vec[i:i+1]=row(v)
    upb[...]=row(v_ub)
    bias[...]=jnp.zeros_like(bias)
    bias[:,0:width]=row(v_qb); bias[:,2*width:]=row(v_vb)
    gather_z(0,1); gather_start(2)
    gather_z(1,1); gather_z(0,2)
    gather_z(2,1); o_swap.wait_recv(); gather_start(3)
    gather_z(1,2); gather_z(0,3); gather_z(2,2); gather_z(1,3)
    gather_x(0); gather_z(3,1); gather_z(2,3)
    gather_x(1); gather_z(3,2)
    gather_start(4)
    gather_x(2); gather_z(3,3); gather_z(4,1)
    for g in range(3): gather_done(g)
    for c in own_copies: c.wait()
    TF=512
    @pl.loop(0,NC)
    def _(c):
        tok_copy(c).wait_recv()
        @pl.loop(0,n//TF)
        def _(j):
            cs=pl.ds(pl.multiple_of(j*TF,TF),TF)
            qkv[chunk(c),cs]=(dot(hall[chunk(c)],strip(act,cs),NN)+bias[:,cs]).astype(BF)
        th[:,chunk(c)]=hall[chunk(c)].T
        @pl.when(c==0)
        def _(): gather_z(4,2)
        @pl.when(c==1)
        def _():
            gather_x(3); gather_z(4,3)
            gather_start(5)
        @pl.when(c==3)
        def _(): gather_done(3)
    x_out=local(th,x_hbm,5); w_out=local(act.at[:,:,0:n],wh_hbm,6)
    x_out.start(); w_out.start()
    ones=jnp.where(lax.broadcasted_iota(jnp.int32,(16,rows_all),0)==0,1.0,0.0).astype(BF)
    @pl.loop(0,pairs)
    def _(p):
        ck=pl.multiple_of(width+p*128,128); cv=pl.multiple_of(2*width+p*128,128)
        kt[p]=qkv[:,pl.ds(ck,128)].T
        v=qkv[:,pl.ds(cv,128)].T
        vt[2*p,0:64]=v[0:64]; vt[2*p,64:80]=ones
        vt[2*p+1,0:64]=v[64:128]; vt[2*p+1,64:80]=ones
    gather_z(5,1)
    def split(k,c):
        sbuf[k-1,loc(c)]=pch[half(1-t)].astype(BF)
        rs_copy(k,c).start()
        part[loc(c)]=pch[half(t)]
    def stats(v):
        cen=v-jnp.mean(v,axis=1,keepdims=True)
        r=lax.rsqrt(jnp.mean(cen*cen,axis=1,keepdims=True)+EPSILON)
        return cen*r,r
    def lo_copy(c): return pltpu.make_async_copy(cl.at[loc(c)],lo_hbm.at[loc(c)],losem.at[c])
    def own_tile(i,col): return pltpu.make_async_copy(stage.at[i%2,:,:,core],dw.at[:,:,core,:,pl.ds(col if isinstance(col,int) else pl.multiple_of(col,512),512)],osem.at[i%2])
    def pair_tile(i,g,off): return remote(stage.at[i%2,:,:,1-core],r1.at[g,:,:,:,pl.ds(off if isinstance(off,int) else pl.multiple_of(off,512),512)],g1s.at[i],g1r.at[i],sib)
    def wgrad(i,g,off,left,right_ref,rcol,ocol):
        if not isinstance(i,int) or 2<=i<8: own_tile(i-2,0).wait()
        if not isinstance(i,int) or i>=2: pair_tile(i-2,0,0).wait_send()
        @pl.loop(0,dm//256)
        def _(k):
            ms=pl.ds(pl.multiple_of(k*256,256),256)
            cs=pl.ds(rcol if isinstance(rcol,int) else pl.multiple_of(rcol,512),512)
            right=right_ref[:,cs] if len(right_ref.shape)==2 else strip(right_ref,cs)
            stage[i%2,k]=dot(left[ms],right,NN).astype(BF).reshape(2,2,64,512)
        own_tile(i,ocol).start()
        pair_tile(i,g,off).start()
    def stage_a(c):
        rs=chunk(c)
        @pl.loop(0,pairs//2)
        def _(pp):
            todo=[]
            for i in (0,1):
                p=2*pp+i
                cq=pl.ds(pl.multiple_of(p*128,128),128); ck=pl.ds(pl.multiple_of(width+p*128,128),128)
                for h in (0,1): todo.append((i,2*p+h,h,cq,ck,(lane<64) if h==0 else (lane>=64)))
            sts=[dot(qkv[:,ck],jnp.where(keep,qkv[rs,cq]*scale,zero),NT) for _,_,_,cq,ck,keep in todo]
            ms=[jnp.max(st,axis=0,keepdims=True) for st in sts]
            mcs=[v*LOG2E for v in ms]
            pts=[jnp.exp2(st*LOG2E-mc).astype(BF) for st,mc in zip(sts,mcs)]
            ots=[dot(vt[e[1]],pt,NN) for e,pt in zip(todo,pts)]
            for (i,hd,h,_,_,_),ot,mc in zip(todo,ots,mcs):
                tot=ot[64:65]
                ctt[i,h*64:(h+1)*64,:]=ot[0:64]*(1.0/tot)
                lse[pl.ds(hd,1),rs]=mc+jnp.log2(tot)
            tops=[jnp.max(v,axis=1,keepdims=True) for v in ms]
            for i in (0,1):
                cq=todo[2*i][3]
                early[10:11,cq]=jnp.maximum(early[10:11,cq],jnp.where(lane<64,tops[2*i],tops[2*i+1]))
                ctx[rs,cq]=ctt[i].T.astype(BF)
            step=c*(pairs//2)+pp
            @pl.when(step==2)
            def _():
                gather_z(5,2); gather_start(6)
            @pl.when(step==3)
            def _():
                gather_z(5,3)
            @pl.when(step==4)
            def _():
                gather_z(6,1); gather_start(7)
            @pl.when(step==6)
            def _():
                gather_z(6,2); gather_x(4)
            @pl.when(step==7)
            def _():
                gather_z(7,1)
        ctx_copy(c,t).start()
        ctxo[loc(c),cols(t)]=ctx[rows(t,c)]
    def stage_b(c):
        ctx_copy(c,1-t).wait_recv()
        x,r=stats(hall[rows(t,c)].astype(F32)+dot(ctxo[loc(c)],whole(wo),NT)+vec[0:1])
        xh[loc(c)]=x
        rst[loc(c)]=jnp.broadcast_to(r,(cr,128))
        hall[rows(t,c)]=(x*vec[1:2]+vec[2:3]).astype(BF)
        ag_copy(3,hall,c,t).start()
    def stage_c(c):
        rs=chunk(c)
        ag_copy(3,hall,c,1-t).wait_recv()
        @pl.loop(0,ff//TF)
        def _(j):
            cs=pl.ds(pl.multiple_of(j*TF,TF),TF)
            u=dot(hall[rs],strip(wup,cs),NN)+upb[:,cs]
            cdf=0.5*(1.0+lax.erf(u*0.5**0.5))
            act[pl.ds(4*c,4),:,cs]=(u*cdf).astype(BF).reshape(4,64,TF)
            slp[rs,cs]=(cdf+u*jnp.exp(-0.5*u*u)*(0.5/math.pi)**0.5).astype(BF)
    def stage_c2(c):
        pch[...]=dot(act[pl.ds(4*c,4)].reshape(cg,ff),whole(wdn),NT)
        split(1,c)
    def stage_d(c):
        rs_copy(1,c).wait_recv()
        x,r=stats(xh[loc(c)]*vec[1:2]+vec[2:3]+part[loc(c)]+rbuf[0,loc(c)].astype(F32)+vec[3:4])
        dy=cl[loc(c)].astype(F32)
        cl[loc(c)]=(x*vec[4:5]+vec[5:6]).astype(BF)
        lo_copy(c).start()
        early[4:5]+=jnp.sum(dy*x,axis=0,keepdims=True)
        early[5:6]+=jnp.sum(dy,axis=0,keepdims=True)
        dx=dy*vec[4:5]
        g=r*(dx-jnp.mean(dx,axis=1,keepdims=True)-x*jnp.mean(dx*x,axis=1,keepdims=True))
        gf[loc(c)]=g
        gb=g.astype(BF)
        early[3:4]+=jnp.sum(gb.astype(F32),axis=0,keepdims=True)
        ball[rows(t,c)]=gb
        ag_copy(4,ball,c,t).start()
        tb[:,rows(t,c)]=gb.T
    def stage_e(c):
        rs=chunk(c)
        ag_copy(4,ball,c,1-t).wait_recv()
        @pl.loop(0,ff//TF)
        def _(j):
            cs=pl.ds(pl.multiple_of(j*TF,TF),TF)
            gu=(dot(ball[rs],strip(wdn,cs),NN)*slp[rs,cs].astype(F32)).astype(BF)
            slp[rs,cs]=gu
            row=pl.ds(8+j*TF//dm,1); cc=pl.ds(pl.multiple_of(j*TF%dm,TF),TF)
            early[row,cc]+=jnp.sum(gu.astype(F32),axis=0,keepdims=True)
        pch[...]=dot(slp[rs],whole(wup),NT)
        split(2,c)
        tb[:,rows(1-t,c)]=ball[rows(1-t,c)].T
        th[:,chunk(c)]=hall[chunk(c)].T
    def stage_f(c):
        rs_copy(2,c).wait_recv()
        dy=gf[loc(c)]+part[loc(c)]+rbuf[1,loc(c)].astype(F32)
        x=xh[loc(c)]; r=rst[loc(c)][:,0:1]
        early[1:2]+=jnp.sum(dy*x,axis=0,keepdims=True)
        early[2:3]+=jnp.sum(dy,axis=0,keepdims=True)
        dx=dy*vec[1:2]
        g=r*(dx-jnp.mean(dx,axis=1,keepdims=True)-x*jnp.mean(dx*x,axis=1,keepdims=True))
        gf[loc(c)]=g
        gb=g.astype(BF)
        early[0:1]+=jnp.sum(gb.astype(F32),axis=0,keepdims=True)
        ga[loc(c)]=gb
        ball[rows(t,c)]=gb
        dcs[loc(c)]=dot(gb,whole(wo),NN).astype(BF)
        dctx_copy(c,t).start()
        dcall[rows(t,c)]=dcs[loc(c),cols(t)]
    def stage_g(c):
        rs=chunk(c)
        dctx_copy(c,1-t).wait_recv()
        @pl.when(c==0)
        def _():
            for i in range(NC): ga_copy(i).start()
        @pl.loop(0,pairs)
        def _(p):
            cq=pl.ds(pl.multiple_of(p*128,128),128); ck=pl.ds(pl.multiple_of(width+p*128,128),128); cv=pl.ds(pl.multiple_of(2*width+p*128,128),128)
            prod=(ctx[rs,cq].astype(F32)*dcall[rs,cq].astype(F32)).T
            dl[0:1]=jnp.sum(prod[0:64],axis=0,keepdims=True)
            dl[1:2]=jnp.sum(prod[64:128],axis=0,keepdims=True)
            for h in (0,1):
                keep=(lane<64) if h==0 else (lane>=64)
                q=jnp.where(keep,qkv[rs,cq]*scale,zero)
                do=jnp.where(keep,dcall[rs,cq],zero)
                st=dot(qkv[:,ck],q,NT)
                pt=jnp.exp2(st*LOG2E-lse[pl.ds(2*p+h,1),rs])
                dpt=dot(qkv[:,cv],do,NT)
                ds=(pt*(dpt-dl[h:h+1])).astype(BF)
                dkv[1,:,cq]+=dot(pt.astype(BF),do,NN)
                dkv[0,:,cq]+=dot(ds,q,NN)
                dqt[h*64:(h+1)*64,:]=dot(kt[p,h*64:(h+1)*64,:],ds,NN)
            qkv[rs,cq]=(dqt[...].T*(HD**-0.5)).astype(BF)
            step=c*pairs+p
            @pl.when(step==0)
            def _():
                add3(0)
                add2(2)
                fetch2(3)
            @pl.when(step==1)
            def _():
                add2(3)
                ecopy(0).start()
            @pl.when(step==4)
            def _():
                eadd(0); ecopy(1).start()
            @pl.when(step==5)
            def _():
                s2(1).wait_send(); s2(2).start()
                fetch3(1)
            @pl.when(step==6)
            def _():
                eadd(1); ecopy(2).start()
            @pl.when(step==7)
            def _():
                sent3(0); add3(1)
            @pl.when(step==8)
            def _():
                eadd(2); ecopy(3).start()
            @pl.when(step==9)
            def _():
                fetchf(0)
            @pl.when(step==10)
            def _():
                finish(0)
                eadd(3); ecopy(4).start()
            @pl.when(step==11)
            def _():
                s2(2).wait_send(); s2(3).start()
                fetch3(2)
            @pl.when(step==12)
            def _():
                for i in range(NC): ga_copy(i).wait_recv()
                for i in range(NC): th[:,i*cg:(i+1)*cg]=ball[i*cg:(i+1)*cg].T
            @pl.when(step==13)
            def _():
                sent3(1); add3(2)
                wgrad(8,4,0,th,ctx,0,base[4])
            @pl.when(step==14)
            def _():
                x_in.start()
            @pl.when(step==15)
            def _():
                fetch2(4)
    def grad_down(c): wgrad(c,c//2,c%2*512,tb,act,c*512,width+ff+c*512)
    def grad_up(c): wgrad(4+c,2+c//2,c%2*512,th,slp,c*512,width+c*512)
    def ga_copy(c):
        return pltpu.make_async_remote_copy(ga.at[loc(c)],ball.at[rows(t,c)],ssem.at[7,c],rsem.at[7,c],device_id=partner,device_id_type=MESH)
    @pl.loop(0,NC)
    def _(c):
        stage_a(c)
        @pl.when(c>0)
        def _(): stage_b(c-1)
    cot_load.wait(); w_out.wait(); x_out.wait()
    gather_z(6,3); gather_z(7,2)
    gather_x(5)
    gather_done(4); gather_done(5)
    @pl.loop(0,NC-1)
    def _(c):
        stage_c(c)
        @pl.when(c==0)
        def _():
            stage_b(NC-1)
            gather_z(7,3)
    gather_x(6); gather_x(7)
    gather_done(6); gather_done(7)
    @pl.loop(0,NC)
    def _(c):
        stage_c2(c)
        @pl.when(c==1)
        def _(): stage_c(NC-1)
    @pl.loop(0,NC)
    def _(c): stage_d(c)
    @pl.loop(0,NC)
    def _(c): stage_e(c)
    piece=ff//2
    base=(width+ff,width+ff+piece,width,width+piece,0,width+2*ff,2*width+2*ff,3*width+2*ff)
    span=(piece,)*4+(width,)*4
    tiles=((0,1),(2,3),(4,5),(6,7),(8,),(9,),(10,),(11,))
    slots2=[wup.at[8:12,:,0:piece],wup.at[12:16,:,0:piece],wup.at[8:12,:,piece:],wup.at[12:16,:,piece:],wup.at[0:4,:,piece:],wup.at[4:8,:,piece:]]
    slots3=[wdn.at[12:16,:,0:piece],wdn.at[12:16,:,piece:],wdn.at[0:4,:,piece:],wdn.at[4:8,:,piece:],wdn.at[8:12,:,piece:]]
    sum2=[slots2[g%6] for g in range(8)]
    sum3=[slots3[g%5] for g in range(8)]
    def s2(g): return remote(sum2[g].at[:,:,0:span[g]],r2.at[g,:,:,0:span[g]],g2s.at[g],g2r.at[g],xp)
    def s3(g,k): return remote(sum3[g].at[(z+k)%4,:,0:span[g]],r3.at[g,3-k,:,0:span[g]],g3s.at[g,k-1],g3r.at[g,k-1],zp[k-1])
    def load2(g): return [pltpu.make_async_copy(dw.at[:,1-x_,core,:,base[g]:base[g]+span[g]],wup.at[0:4,:,0:span[g]],rl.at[0]),
                          pltpu.make_async_copy(r1.at[g,:,1-x_,:,0:span[g]],wup.at[4:8,:,0:span[g]],rl.at[1])]
    def load3(g): return [pltpu.make_async_copy(dw.at[:,x_,core,:,base[g]:base[g]+span[g]],wdn.at[0:4,:,0:span[g]],rl.at[2]),
                         pltpu.make_async_copy(r1.at[g,:,x_,:,0:span[g]],wdn.at[4:8,:,0:span[g]],rl.at[3]),
                         pltpu.make_async_copy(r2.at[g,:,:,0:span[g]],wdn.at[8:12,:,0:span[g]],rl.at[4])]
    def fetch2(g):
        for i in tiles[g]:
            if i>=6: own_tile(i,0).wait()
            pair_tile(i,g,0).wait_recv()
        for l in load2(g): l.start()
    def add2(g):
        for l in load2(g): l.wait()
        @pl.loop(0,4)
        def _(i): sum2[g][i,:,0:span[g]]=(wup[i,:,0:span[g]].astype(F32)+wup[4+i,:,0:span[g]].astype(F32)).astype(BF)
    def fetch3(g):
        s2(g).wait_recv()
        for l in load3(g): l.start()
    def add3(g):
        for l in load3(g): l.wait()
        @pl.loop(0,4)
        def _(i): sum3[g][i,:,0:span[g]]=(wdn[i,:,0:span[g]].astype(F32)+wdn[4+i,:,0:span[g]].astype(F32)+wdn[8+i,:,0:span[g]].astype(F32)).astype(BF)
        for k in (1,2,3): s3(g,k).start()
    def sent3(g):
        for k in (1,2,3): s3(g,k).wait_send()
    def fslot(g,i):
        r=64*(6*(g%2)+i)
        return tb.at[r:r+64,0:span[g]]
    def loadf(g): return [pltpu.make_async_copy(src,fslot(g,i),fl.at[g%2,i]) for i,src in enumerate(
        [dw.at[z,x_,core,:,base[g]:base[g]+span[g]],r1.at[g,z,x_,:,0:span[g]],r2.at[g,z,:,0:span[g]]]+[r3.at[g,k,:,0:span[g]] for k in range(3)])]
    def fetchf(g):
        for k in (1,2,3): s3(g,k).wait_recv()
        for l in loadf(g): l.start()
    def final(g):
        for l in loadf(g): l.wait()
        v=[fslot(g,i)[...].astype(F32) for i in range(6)]
        return v[0]+v[1]+v[2]+v[3]+v[4]+v[5]
    def fin_copy(g):
        return pltpu.make_async_copy(xh.at[64*g:64*g+64,0:span[g]],fin.at[g] if g<4 else go_hbm if g==4 else fin_head.at[g-5],fs.at[g])
    def finish(g):
        xh[64*g:64*g+64,0:span[g]]=final(g)
        fin_copy(g).start()
    zb=[dev(z+1-2*(z%2),x_,core),dev((z+2)%4,x_,core)]
    hops=[sib,xp,zb[0],zb[1],partner]
    def ecopy(i): return remote(eb.at[i],er.at[i],es.at[i],erc.at[i],hops[i])
    def eadd(i):
        ecopy(i).wait_recv()
        b=eb[i,8:16]; c=er[i,8:16]
        if i<4:
            r=lax.broadcasted_iota(jnp.int32,b.shape,0)
            b=jnp.where(r==2,jnp.maximum(b,c),b+c)
        eb[i+1,0:8]=eb[i,0:8]+er[i,0:8]; eb[i+1,8:16]=b
    def lcopy(i): return remote(lb.at[i],lr.at[i],ls.at[i],lrc.at[i],hops[i])
    def ladd(i):
        lcopy(i).wait_recv()
        lb[i+1]=lb[i]+lr[i]
    @pl.loop(0,NC)
    def _(c):
        ag_copy(3,hall,c,t).wait_send()
        ag_copy(4,ball,c,t).wait_send()
    x_in=pltpu.make_async_copy(x_hbm,th,dsem.at[0])
    for c in range(3): grad_down(c)
    grad_down(3)
    fetch2(0)
    wh_in=pltpu.make_async_copy(wh_hbm,act.at[:,:,0:n],dsem.at[1])
    wh_in.start()
    add2(0); s2(0).start()
    @pl.loop(0,NC)
    def _(c):
        stage_f(c)
        grad_up(c)
        @pl.when(c==1)
        def _(): fetch2(1)
        @pl.when(c==2)
        def _(): add2(1)
        @pl.when(c==3)
        def _():
            s2(0).wait_send(); s2(1).start()
            fetch2(2)
            fetch3(0)
    @pl.loop(0,NC)
    def _(c): stage_g(c)
    add2(4)
    s2(3).wait_send(); s2(4).start()
    fetch3(3)
    x_in.wait()
    wgrad(9,5,0,th,qkv,0,base[5])
    sent3(2); add3(3)
    fetchf(1)
    @pl.loop(0,pairs)
    def _(p):
        cq=pl.ds(pl.multiple_of(p*128,128),128); ck=pl.ds(pl.multiple_of(width+p*128,128),128); cv=pl.ds(pl.multiple_of(2*width+p*128,128),128)
        qkv[:,ck]=dkv[0,:,cq].astype(BF)
        qkv[:,cv]=dkv[1,:,cq].astype(BF)
    fetch2(5)
    def ycopy(c): return remote(sbuf.at[0,loc(c)],rbuf.at[0,loc(c)],ssem.at[6,c],rsem.at[6,c],partner)
    wh_in.wait()
    def token_grad(c):
        pch[...]=dot(qkv[chunk(c)],act[:,:,0:n].reshape(dm,n),NT)
        rs_copy(1,c).wait_send()
        sbuf[0,loc(c)]=pch[half(1-t)].astype(BF)
        ycopy(c).start()
        part[loc(c)]=pch[half(t)]
    token_grad(0)
    add2(5)
    s2(4).wait_send(); s2(5).start()
    token_grad(1)
    wgrad(10,6,0,th,qkv,width,base[6])
    fetch3(4)
    wgrad(11,7,0,th,qkv,2*width,base[7])
    fetch2(6)
    @pl.loop(2,NC)
    def _(c): token_grad(c)
    add2(6)
    s2(5).wait_send(); s2(6).start()
    fetch2(7)
    sent3(3); add3(4)
    fetch3(5)
    lb[0,0:1,0:width]=jnp.sum(qkv[:,0:width].astype(F32),axis=0,keepdims=True)
    lb[0,0:1,width:2*width]=jnp.sum(qkv[:,2*width:].astype(F32),axis=0,keepdims=True)
    lcopy(0).start()
    finish(1)
    add2(7)
    eadd(4)
    sent3(4); add3(5)
    s2(6).wait_send(); s2(7).start()
    fetch3(6)
    ladd(0); lcopy(1).start()
    fetchf(2)
    smalls[...]=eb[5]
    pk=eb[4,10:11,0:width]
    head=lax.broadcasted_iota(jnp.int32,(1,width),1)//HD
    limit=jnp.zeros((1,width),F32)
    for h in range(width//HD): limit=jnp.where(head==h,lim[h],limit)
    sc=jnp.sqrt(limit/jnp.maximum(pk,limit))
    ctxo[0:64,0:width]=(wq[...].astype(F32)*sc).astype(BF)
    ctxo[64:128,0:width]=(wk[...].astype(F32)*sc).astype(BF)
    clips=[pltpu.make_async_copy(ctxo.at[0:64,0:width],qc_hbm,fs.at[8]),pltpu.make_async_copy(ctxo.at[64:128,0:width],kc_hbm,fs.at[9])]
    for c in clips: c.start()
    smalls[11:12,0:width]=row(v_qb)*sc
    finish(2)
    ladd(1); lcopy(2).start()
    fetchf(3)
    sent3(5); add3(6)
    fetch3(7)
    finish(3)
    fetchf(4)
    ladd(2); lcopy(3).start()
    @pl.loop(0,NC)
    def _(c): lo_copy(c).wait()
    finish(4)
    sent3(6); add3(7)
    fetchf(5)
    def tg_copy(c): return pltpu.make_async_copy(cl.at[loc(c)],tg_hbm.at[loc(c)],losem.at[c])
    @pl.loop(0,NC)
    def _(c):
        ycopy(c).wait_recv()
        cl[loc(c)]=(gf[loc(c)]+part[loc(c)]+rbuf[0,loc(c)].astype(F32)).astype(BF)
        tg_copy(c).start()
    ladd(3)
    smalls[12:13]=lb[4,0:1]
    finish(5)
    fetchf(6)
    finish(6)
    fetchf(7)
    finish(7)
    o_swap.wait_send()
    for g in range(8):
        fin_copy(g).wait()
    for i in (10,11): pair_tile(i,0,0).wait_send()
    s2(7).wait_send()
    sent3(7)
    for c in clips: c.wait()
    for i in range(5): ecopy(i).wait_send()
    for i in range(4): lcopy(i).wait_send()
    @pl.loop(0,NC)
    def _(c):
        tg_copy(c).wait()
        ctx_copy(c,t).wait_send(); dctx_copy(c,t).wait_send(); tok_copy(c).wait_send()
        rs_copy(2,c).wait_send(); ycopy(c).wait_send()
        ga_copy(c).wait_send()

def main_call(shards,tok,cot,vectors,lim,cid):
    V=pl.BlockSpec(memory_space=pltpu.VMEM); A=pl.BlockSpec(memory_space=pl.ANY)
    width=shards[0].shape[1]; ff=shards[4].shape[1]; own,dm=tok.shape; rows=2*own; n=3*width; cr=own//NC; wide=2*width; piece=ff//2
    S=jax.ShapeDtypeStruct; M=pltpu.VMEM; D=pltpu.SemaphoreType.DMA
    return pl.pallas_call(main_kernel,
      out_shape=(S((own,dm),BF),S((own,dm),BF),S((4,64,piece),F32),S((3,64,width),F32),S((64,width),F32),S((64,width),BF),S((64,width),BF),S((16,dm),F32),
        S((4,2,2,64,width+2*ff+n),BF),S((8,4,2,64,piece),BF),S((8,4,64,piece),BF),S((8,3,64,piece),BF),S((dm,rows),BF),S((16,64,n),BF)),
      in_specs=[V]*6+[A,A]+[V]*9+[pl.BlockSpec(memory_space=pltpu.SMEM)],out_specs=(A,)*7+(V,)+(A,)*6,
      scratch_shapes=[M((1,n),F32),M((8,dm),F32),M((1,ff),F32),M((own,dm),F32),M((6,16,dm),F32),M((5,16,dm),F32),M((5,8,dm),F32),M((4,8,dm),F32),
        M((64,n+wide+2*ff),BF),M((rows,n),BF),M((width//HD,80,rows),BF),M((width//128,128,rows),BF),M((rows,width),BF),M((own,wide),BF),M((width//HD,rows),F32),M((own,dm),BF),
        M((16,64,wide),BF),M((16,64,ff),BF),M((16,64,ff),BF),
        M((own,dm),F32),M((own,128),F32),
        M((rows,dm),BF),M((16,64,ff),BF),M((rows,ff),BF),M((rows,dm),BF),M((own,dm),BF),M((own,wide),BF),M((rows,width),BF),
        M((own,dm),F32),M((2*cr,dm),F32),M((2,128,2*cr),F32),M((128,2*cr),F32),M((8,2*cr),F32),M((2,rows,width),F32),
        M((2,own,dm),BF),M((2,own,dm),BF),
        M((dm,rows),BF),M((dm,rows),BF),M((2,4,2,2,64,512),BF),
        D((7,)),D((NC,)),D((2,)),D((2,)),D((8,NC)),D((8,NC)),D((5,)),D((12,)),D((12,)),D((8,)),D((8,)),D((8,3)),D((8,3)),
        D((NC+1,)),D((NC+1,)),D((8,2,3)),D((8,2,3)),D((8,4)),D((8,4)),D((8,8)),D((8,8)),
        D((5,)),D((5,)),D((4,)),D((4,)),D((2,6)),D((10,))],
      compiler_params=pltpu.CompilerParams(collective_id=cid,has_side_effects=True,vmem_limit_bytes=61*2**20),
      name="main")(*shards,tok,cot,*vectors,lim)

def finish_kernel(lo,tg,fin,fin_head,go,qc,kc,smalls,
                  lo_,tg_,gq_,gk_,gv_,go_,gu_,gd_,qc_,kc_,qb_,vb_,ob_,g1_,b1_,ub_,db_,g2_,b2_,pk_,qbc_,h_lo,h_tg,h_fin,h_head,h_go,h_qc,h_kc,isem,sem):
    piece=fin.shape[2]
    ins=[pltpu.make_async_copy(a,b,isem.at[i]) for i,(a,b) in enumerate(((lo,h_lo),(tg,h_tg),(fin,h_fin),(fin_head,h_head),(go,h_go),(qc,h_qc),(kc,h_kc)))]
    outs=[[(h_lo,lo_)],[(h_tg,tg_)],[(h_fin.at[0],gd_.at[:,0:piece]),(h_fin.at[1],gd_.at[:,piece:]),(h_fin.at[2],gu_.at[:,0:piece]),(h_fin.at[3],gu_.at[:,piece:])],
          [(h_head.at[0],gq_),(h_head.at[1],gk_),(h_head.at[2],gv_)],[(h_go,go_)],[(h_qc,qc_)],[(h_kc,kc_)]]
    for c in ins: c.start()
    width=qb_.shape[0]; dm=ob_.shape[0]
    def line(v): return v.reshape(v.shape[1])
    qb_[...]=line(smalls[12:13,0:width]); vb_[...]=line(smalls[12:13,width:2*width])
    for i,o in enumerate((ob_,g1_,b1_,db_,g2_,b2_)): o[...]=line(smalls[i:i+1])
    ub_[0:dm]=line(smalls[8:9]); ub_[dm:2*dm]=line(smalls[9:10])
    for h in range(pk_.shape[0]): pk_[h]=jnp.max(smalls[10:11,h*HD:(h+1)*HD])
    qbc_[...]=line(smalls[11:12,0:width]).astype(BF)
    moved=[]
    for a,group in zip(ins,outs):
        a.wait()
        for src,dst in group:
            c=pltpu.make_async_copy(src,dst,sem.at[len(moved)])
            c.start()
            moved.append(c)
    for c in moved: c.wait()

def finish_call(big,smalls,heads):
    V=pl.BlockSpec(memory_space=pltpu.VMEM); A=pl.BlockSpec(memory_space=pl.ANY); S=jax.ShapeDtypeStruct
    lo,tg,fin,fin_head,go,qc,kc=big
    width=go.shape[1]; piece=fin.shape[2]; ff=2*piece; dm=tg.shape[1]
    return pl.pallas_call(finish_kernel,
      out_shape=(S(lo.shape,BF),S(tg.shape,BF))+(S((64,width),F32),)*4+(S((64,ff),F32),)*2+(S((64,width),BF),)*2
        +tuple(S((k,),F32) for k in (width,width,dm,dm,dm,ff,dm,dm,dm,heads))+(S((width,),BF),),
      in_specs=[A]*7+[V],out_specs=(A,)*10+(V,)*9+(pl.BlockSpec(memory_space=pltpu.SMEM),V),
      scratch_shapes=[pltpu.VMEM(a.shape,a.dtype) for a in big]+[pltpu.SemaphoreType.DMA((7,)),pltpu.SemaphoreType.DMA((12,))],
      compiler_params=pltpu.CompilerParams(vmem_limit_bytes=61*2**20),name="finish")(*big,smalls)

def per_device_pair(tokens,query_weight,query_bias,key_weight,value_weight,value_bias,out_weight,out_bias,first_gain,first_shift,
    up_weight,up_bias,down_weight,down_bias,second_gain,second_shift,cotangent,clip_limit):
    shards=(query_weight,key_weight,value_weight,out_weight.T,up_weight,down_weight.T)
    vectors=(out_bias,first_gain,first_shift,down_bias,second_gain,second_shift,up_bias,query_bias,value_bias)
    res=main_call(shards,tokens,cotangent,vectors,clip_limit,1)
    lo,tg,gq,gk,gv,go,gu,gd,qc,kc,qb,vb,ob,g1,b1,ub,db,g2,b2,pk,qbc=finish_call(res[:7],res[7],clip_limit.shape[0])
    return (lo,tg,gq,qb,gk,gv,vb,go.T,ob,g1,b1,gu,ub,gd.T,db,g2,b2,pk,qc,qbc,kc)


def layer(*args):
    paired = lax.axis_size("dp") == 16 and lax.axis_size("tensor") == 2 and 2 * args[0].shape[0] == LEN
    return per_device_pair(*args) if paired else per_device(*args)


def solution(mesh):
    in_specs = (
        P(("dp", "tensor"), None),
        P("dp", "tensor"),
        P("tensor"),
        P("dp", "tensor"),
        P("dp", "tensor"),
        P("tensor"),
        P("tensor", "dp"),
        P(),
        P(),
        P(),
        P("dp", "tensor"),
        P("tensor"),
        P("tensor", "dp"),
        P(),
        P(),
        P(),
        P(("dp", "tensor"), None),
        P("tensor"),
    )
    out_specs = (
        P(("dp", "tensor"), None),
        P(("dp", "tensor"), None),
        P("dp", "tensor"),
        P("tensor"),
        P("dp", "tensor"),
        P("dp", "tensor"),
        P("tensor"),
        P("tensor", "dp"),
        P(),
        P(),
        P(),
        P("dp", "tensor"),
        P("tensor"),
        P("tensor", "dp"),
        P(),
        P(),
        P(),
        P("tensor"),
        P("dp", "tensor"),
        P("tensor"),
        P("dp", "tensor"),
    )
    return jax.shard_map(
        layer, mesh=mesh, in_specs=in_specs, out_specs=out_specs, check_vma=False
    )
```
